32 devices in a mesh: dp: 2 (over y), seq: 4 (over x, core), ffn: 4 (over z).
Axes of the slice: x: 2, y: 2, z: 4, core: 2. Of those that a mesh axis runs over, the one named last changes fastest.
Arguments:
- tokens: bfloat16 [8, 4096, 768], P(('dp', 'ffn'), 'seq'), may hold values from -6 to 6
- w_query: bfloat16 [768, 768], P(('dp', 'seq', 'ffn')), may hold values from -0.21875 to 0.21875
- w_key: bfloat16 [768, 768], P(('dp', 'seq', 'ffn')), may hold values from -0.21875 to 0.21875
- w_value: bfloat16 [768, 768], P(('dp', 'seq', 'ffn')), may hold values from -0.21875 to 0.21875
- w_output: bfloat16 [768, 768], P(('dp', 'seq', 'ffn')), may hold values from -0.875 to 0.875
- b_query: bfloat16 [768], P(('dp', 'seq', 'ffn')), may hold values from -3 to 3
- b_value: bfloat16 [768], P(('dp', 'seq', 'ffn')), may hold values from -3 to 3
- b_output: bfloat16 [768], P(('dp', 'seq', 'ffn')), may hold values from -3 to 3
- w_up: bfloat16 [768, 3072], P(('dp', 'seq'), 'ffn'), may hold values from -0.21875 to 0.21875
- b_up: bfloat16 [3072], P('ffn'), may hold values from -3 to 3
- w_down: bfloat16 [768, 3072], P(('dp', 'seq'), 'ffn'), may hold values from -0.109375 to 0.109375
- b_down: bfloat16 [768], P(('dp', 'seq', 'ffn')), may hold values from -3 to 3
- gain_attn: bfloat16 [768], P(('dp', 'seq', 'ffn')), may hold values from 0.25 to 1.75
- shift_attn: bfloat16 [768], P(('dp', 'seq', 'ffn')), may hold values from -2 to 2
- gain_ffn: bfloat16 [768], P(('dp', 'seq', 'ffn')), may hold values from 0.25 to 1.75
- shift_ffn: bfloat16 [768], P(('dp', 'seq', 'ffn')), may hold values from -2 to 2
- segment_ids: int32 [8, 4096], P(('dp', 'ffn')), may hold values from 0 to 15, never falling along the last dimension, each value on 1 to 2048 neighbouring positions
- random_blocks: int32 [8, 12, 64, 3], P(('dp', 'ffn'), 'seq'), may hold values from 0 to 63, as said below
- global_blocks: int32 [8, 2], P(('dp', 'ffn')), may hold values from 0 to 63, as said below
- cotangent: bfloat16 [8, 4096, 768], P(('dp', 'ffn'), 'seq'), may hold values from -6 to 6
Outputs:
- output: bfloat16 [8, 4096, 768], P(('dp', 'ffn'), 'seq')
- grad_tokens: float32 [8, 4096, 768], P(('dp', 'ffn'), 'seq')
- grad_w_query: float32 [768, 768], P(('dp', 'seq', 'ffn'))
- grad_w_key: float32 [768, 768], P(('dp', 'seq', 'ffn'))
- grad_w_value: float32 [768, 768], P(('dp', 'seq', 'ffn'))
- grad_w_output: float32 [768, 768], P(('dp', 'seq', 'ffn'))
- grad_b_query: float32 [768], P(('dp', 'seq', 'ffn'))
- grad_b_value: float32 [768], P(('dp', 'seq', 'ffn'))
- grad_b_output: float32 [768], P(('dp', 'seq', 'ffn'))
- grad_w_up: float32 [768, 3072], P(('dp', 'seq'), 'ffn')
- grad_b_up: float32 [3072], P('ffn')
- grad_w_down: float32 [768, 3072], P(('dp', 'seq'), 'ffn')
- grad_b_down: float32 [768], P(('dp', 'seq', 'ffn'))
- grad_gain_attn: float32 [768], P(('dp', 'seq', 'ffn'))
- grad_shift_attn: float32 [768], P(('dp', 'seq', 'ffn'))
- grad_gain_ffn: float32 [768], P(('dp', 'seq', 'ffn'))
- grad_shift_ffn: float32 [768], P(('dp', 'seq', 'ffn'))
The draws below stay inside these ranges and needn't reach their ends.
Inputs may be any that keep to these rules, and one draw needn't show every extreme that they name: `segment_ids`: numbers never fall along a sequence; a document is the run of positions sharing one number. `random_blocks`: the 3 entries of one query block differ, and none is within one block of the query block or one of the sequence's global blocks. `global_blocks`: two different block numbers of the sequence; sequence 0 has the first and the last block.
All inputs are finite; a program needn't handle non-finite values.
Results may differ from the reference program's by a relative error of at most 0.014.
Values may be sent and summed in bfloat16 or wider, within the bound.
No kernel may reach another device: no remote copies, remote signals or barrier semaphores. Data moves between devices by JAX's collectives and lax.ppermute only.
A program may use at most 256 MiB of HBM per device.

```python
import math
import jax
import jax.numpy as jnp
import numpy as np
from jax import lax

D = 768
HEADS = 12
HEAD_DIM = 64
FF = 3072
BLOCK = 64
RANDOM = 3
LENGTH = 4096
NBLOCKS = 64
SEQS = 8


def pick_globals(key):
    noise = jax.random.randint(jax.random.fold_in(key, 11), (SEQS, NBLOCKS), 0, 1 << 20, dtype=jnp.int32)
    blocks = jnp.arange(NBLOCKS, dtype=jnp.int32)
    ranked = noise * NBLOCKS + blocks[None, :]
    first_seq = jnp.arange(SEQS, dtype=jnp.int32)[:, None] == 0
    ends = (blocks[None, :] == 0) | (blocks[None, :] == NBLOCKS - 1)
    ranked = ranked + jnp.where(first_seq & ends, (1 << 20) * NBLOCKS, 0).astype(jnp.int32)
    return lax.top_k(ranked, 2)[1].astype(jnp.int32)


def draw_global_blocks(key, part):
    return pick_globals(key)


def draw_random_blocks(key, part):
    global_ids = pick_globals(key)
    blocks = jnp.arange(NBLOCKS, dtype=jnp.int32)
    nearby = jnp.abs(blocks[:, None] - blocks[None, :]) <= 1
    is_global = jnp.any(blocks[None, :, None] == global_ids[:, None, :], axis=-1)
    banned = nearby[None, None, :, :] | is_global[:, None, None, :]
    noise = jax.random.randint(jax.random.fold_in(key, 23), (SEQS, HEADS, NBLOCKS, NBLOCKS), 0, 1 << 20, dtype=jnp.int32)
    ranked = jnp.where(banned, -1, noise * NBLOCKS + blocks[None, None, None, :])
    return lax.top_k(ranked, RANDOM)[1].astype(jnp.int32)


def levels(stream_key, extent, shards, low, top_value):
    loudness = 1.0
    for position, shards_of in shards:
        steps = jax.random.uniform(jax.random.fold_in(jax.random.fold_in(stream_key, 6), position), (shards_of,), jnp.float32, low / len(shards), top_value / len(shards))
        loudness = loudness * jnp.repeat(jnp.exp(steps), extent[position] // shards_of).reshape((-1,) + (1,) * (len(extent) - 1 - position))
    return loudness


def split_up(count, total, reach, skew):
    portions = [(1 << 20) // math.isqrt(rank ** skew) + 1 for rank in range(2, count + 1)]
    spare, given = total - reach - (count - 1), [1] * (count - 1)
    while spare > 0:
        free = [i for i in range(count - 1) if given[i] < reach]
        mass, remaining = sum([portions[i] for i in free]), spare
        for i in free:
            addition = min(reach - given[i], max(1, remaining * portions[i] // mass), spare)
            given[i] = given[i] + addition
            spare = spare - addition
    return np.array([reach] + given)


def ragged(stream_key, number_of, total, bound, lean):
    if number_of == 2:
        one = jax.random.randint(stream_key, (), max(1, total - bound), min(bound, total - 1) + 1)
        return jnp.stack([one, total - one])
    tallies = jnp.asarray(split_up(number_of, total, bound, lean), jnp.int32)
    couples = (number_of - 1) // 2
    source_of, sink = tallies[1:1 + 2 * couples:2], tallies[2:2 + 2 * couples:2]
    margin = jnp.minimum(source_of - 1, bound - sink)
    moved = jax.random.randint(jax.random.fold_in(stream_key, 1), (couples,), 0, 1 << 20) % (margin + 1)
    tallies = tallies.at[1:1 + 2 * couples:2].set(source_of - moved).at[2:2 + 2 * couples:2].set(sink + moved)
    return tallies[jax.random.permutation(jax.random.fold_in(stream_key, 2), number_of)]


def gaussian(own_key, shape, scale, bound, split=(), kind=jnp.bfloat16):
    array = scale * jax.random.normal(own_key, shape, jnp.float32)
    if split:
        array = array * levels(own_key, shape, split, -0.22, 0.18)
    return jnp.clip(array, -bound, bound).astype(kind)


def setup_inputs(seed: int = 0) -> dict:
    arg_keys = jax.random.split(jax.random.key(seed), 21)
    return {
        "tokens": gaussian(arg_keys[0], (SEQS, LENGTH, D), 1.0, 6.0, ((0, 8), (1, 4))),
        "w_query": gaussian(arg_keys[1], (D, D), D ** -0.5, 0.21875, ((0, 32),)),
        "w_key": gaussian(arg_keys[2], (D, D), D ** -0.5, 0.21875, ((0, 32),)),
        "w_value": gaussian(arg_keys[3], (D, D), D ** -0.5, 0.21875, ((0, 32),)),
        "w_output": gaussian(arg_keys[4], (D, D), (D // 16) ** -0.5, 0.875, ((0, 32),)),
        "b_query": gaussian(arg_keys[5], (D,), 0.5, 3.0, ((0, 32),)),
        "b_value": gaussian(arg_keys[6], (D,), 0.5, 3.0, ((0, 32),)),
        "b_output": gaussian(arg_keys[7], (D,), 0.5, 3.0, ((0, 32),)),
        "w_up": gaussian(arg_keys[8], (D, FF), D ** -0.5, 0.21875, ((0, 8), (1, 4))),
        "b_up": gaussian(arg_keys[9], (FF,), 0.5, 3.0, ((0, 4),)),
        "w_down": gaussian(arg_keys[10], (D, FF), FF ** -0.5, 0.109375, ((0, 8), (1, 4))),
        "b_down": gaussian(arg_keys[11], (D,), 0.5, 3.0, ((0, 32),)),
        "gain_attn": jnp.clip(1.0 + 0.15 * jax.random.normal(arg_keys[12], (D,), jnp.float32), 0.25, 1.75).astype(jnp.bfloat16),
        "shift_attn": gaussian(arg_keys[13], (D,), 0.3, 2.0, ((0, 32),)),
        "gain_ffn": jnp.clip(1.0 + 0.15 * jax.random.normal(arg_keys[14], (D,), jnp.float32), 0.25, 1.75).astype(jnp.bfloat16),
        "shift_ffn": gaussian(arg_keys[15], (D,), 0.3, 2.0, ((0, 32),)),
        "segment_ids": jax.vmap(lambda own: jnp.searchsorted(jnp.cumsum(ragged(own, max(4, LENGTH // 256), LENGTH, LENGTH // 2, 2)), jnp.arange(LENGTH), side="right"))(jax.random.split(arg_keys[16], SEQS)).reshape((SEQS, LENGTH)).astype(jnp.int32),
        "random_blocks": draw_random_blocks(jax.random.fold_in(arg_keys[20], 71), 0),
        "global_blocks": draw_global_blocks(jax.random.fold_in(arg_keys[20], 71), 0),
        "cotangent": gaussian(arg_keys[19], (SEQS, LENGTH, D), 1.0, 6.0, ((0, 8), (1, 4))),
    }


@jax.custom_vjp
def low(v):
    return lax.optimization_barrier(v.astype(jnp.bfloat16)).astype(jnp.float32)

@jax.custom_vjp
def low_back(v):
    return v

def low_keep(v):
    return (low(v), None)

def low_pass(kept, grad):
    return (grad,)

def back_keep(v):
    return (v, None)

def back_low(kept, grad):
    return (low(grad),)
low.defvjp(low_keep, low_pass)
low_back.defvjp(back_keep, back_low)
highest = lax.Precision.HIGHEST
neg_fill = -1e+30
norm_eps = 1e-12

def matmul(left_mat, right_mat):
    return jnp.dot(left_mat, right_mat, precision=highest)

def layer_norm(residual, gain, shift):
    center = residual - lax.optimization_barrier(jnp.mean(residual, axis=-1, keepdims=True))
    spread = lax.optimization_barrier(jnp.mean(center * center, axis=-1, keepdims=True))
    return center * lax.rsqrt(spread + norm_eps) * gain + shift

def masked_softmax(scores, allowed):
    masked = jnp.where(allowed, scores, neg_fill)
    row_peak = lax.optimization_barrier(jnp.max(masked, axis=-1, keepdims=True))
    exp_terms = jnp.where(allowed, jnp.exp(masked - row_peak), 0.0)
    return exp_terms / lax.optimization_barrier(jnp.sum(exp_terms, axis=-1, keepdims=True))

def block_tables(global_ids, nblocks):
    blocks = jnp.arange(nblocks, dtype=jnp.int32)
    nearby = blocks[:, None] + jnp.arange(-1, 2, dtype=jnp.int32)[None, :]
    inside = (nearby >= 0) & (nearby < nblocks)
    nearby = jnp.clip(nearby, 0, nblocks - 1).astype(jnp.int32)
    hits_glob = jnp.any(nearby[:, :, None] == global_ids[None, None, :], axis=-1)
    return (nearby, inside & jnp.logical_not(hits_glob))

def key_table(nearby, near_ok, rand_head, global_ids):
    nblocks = nearby.shape[0]
    key_index = jnp.concatenate([nearby, rand_head.astype(jnp.int32), jnp.broadcast_to(global_ids[None, :], (nblocks, global_ids.shape[0])).astype(jnp.int32)], axis=1)
    usable = jnp.concatenate([near_ok, jnp.ones((nblocks, rand_head.shape[1] + global_ids.shape[0]), dtype=jnp.bool_)], axis=1)
    return (key_index, usable)

def attend_sequence(query, key_rows, value_rows, seq_ids, rand_seq, global_ids):
    score_scale = HEAD_DIM ** (-0.5)

    def to_blocks(array_in):
        return array_in.reshape(NBLOCKS, BLOCK, HEADS, HEAD_DIM).transpose(2, 0, 1, 3)
    seg_blocks = seq_ids.reshape(NBLOCKS, BLOCK)
    nearby, near_ok = block_tables(global_ids, NBLOCKS)

    def one_head(operands):
        query_blk, key_blk, value_blk, rand_head = operands
        key_index, usable = key_table(nearby, near_ok, rand_head, global_ids)
        key_sel = key_blk[key_index].reshape(NBLOCKS, -1, HEAD_DIM)
        value_sel = value_blk[key_index].reshape(NBLOCKS, -1, HEAD_DIM)
        seg_sel = seg_blocks[key_index].reshape(NBLOCKS, -1)
        usable_keys = jnp.repeat(usable, BLOCK, axis=1)
        allowed = usable_keys[:, None, :] & (seg_blocks[:, :, None] == seg_sel[:, None, :])
        scores = low_back(jnp.einsum('nqd,nkd->nqk', query_blk, key_sel, precision=highest) * score_scale)
        weights_sparse = masked_softmax(scores, allowed)
        context = jnp.einsum('nqk,nkd->nqd', low(weights_sparse), value_sel, precision=highest)
        query_glob = query_blk[global_ids]
        key_flat = key_blk.reshape(-1, HEAD_DIM)
        value_flat = value_blk.reshape(-1, HEAD_DIM)
        allowed_glob = seg_blocks[global_ids][:, :, None] == seq_ids[None, None, :]
        scores_glob = low_back(jnp.einsum('gqd,kd->gqk', query_glob, key_flat, precision=highest) * score_scale)
        weights_glob = masked_softmax(scores_glob, allowed_glob)
        context_glob = jnp.einsum('gqk,kd->gqd', low(weights_glob), value_flat, precision=highest)
        return context.at[global_ids].set(context_glob)
    contexts = lax.map(jax.checkpoint(one_head), (to_blocks(query), to_blocks(key_rows), to_blocks(value_rows), rand_seq))
    return contexts.transpose(1, 2, 0, 3).reshape(LENGTH, D)

def layer(params, tokens_seq, seq_ids, rand_seq, global_ids):
    w_query, w_key, w_value, w_output, b_query, b_value, b_output, w_up, b_up, w_down, b_down, gain_attn, shift_attn, gain_ffn, shift_ffn = params
    query = low(low_back(matmul(tokens_seq, w_query) + b_query))
    key_rows = low(low_back(matmul(tokens_seq, w_key)))
    value_rows = low(low_back(matmul(tokens_seq, w_value) + b_value))
    context = low(low_back(attend_sequence(query, key_rows, value_rows, seq_ids, rand_seq, global_ids)))
    branch = low_back(matmul(context, w_output) + b_output)
    resid_one = tokens_seq + branch
    normed_one = layer_norm(resid_one, gain_attn, shift_attn)
    normed_low = low(normed_one)
    pre_act = low_back(matmul(normed_low, w_up) + b_up)
    hidden = low(jax.nn.gelu(pre_act, approximate=False))
    ffn_out = low_back(lax.dot_general(hidden, w_down, (((1,), (1,)), ((), ())), precision=highest) + b_down)
    resid_two = normed_one + ffn_out
    return layer_norm(resid_two, gain_ffn, shift_ffn)

def reference(tokens, w_query, w_key, w_value, w_output, b_query, b_value, b_output, w_up, b_up, w_down, b_down, gain_attn, shift_attn, gain_ffn, shift_ffn, segment_ids, random_blocks, global_blocks, cotangent):
    params = (w_query.astype(jnp.float32), w_key.astype(jnp.float32), w_value.astype(jnp.float32), w_output.astype(jnp.float32), b_query.astype(jnp.float32), b_value.astype(jnp.float32), b_output.astype(jnp.float32), w_up.astype(jnp.float32), b_up.astype(jnp.float32), w_down.astype(jnp.float32), b_down.astype(jnp.float32), gain_attn.astype(jnp.float32), shift_attn.astype(jnp.float32), gain_ffn.astype(jnp.float32), shift_ffn.astype(jnp.float32))
    tokens_wide = tokens.astype(jnp.float32)
    cot_wide = cotangent.astype(jnp.float32)

    def whole(param_set, tokens_in):

        def per_sequence(operands):
            tok_seq, seq_ids, rand_seq, global_ids = operands
            return layer(param_set, tok_seq, seq_ids, rand_seq, global_ids)
        return lax.map(jax.checkpoint(per_sequence), (tokens_in, segment_ids, random_blocks, global_blocks))
    output, backward = jax.vjp(whole, params, tokens_wide)
    grad_params, grad_tokens = backward(cot_wide)
    return (output.astype(jnp.bfloat16), grad_tokens, grad_params[0], grad_params[1], grad_params[2], grad_params[3], grad_params[4], grad_params[5], grad_params[6], grad_params[7], grad_params[8], grad_params[9], grad_params[10], grad_params[11], grad_params[12], grad_params[13], grad_params[14])
```

```python
import functools
import jax
import jax.numpy as jnp
from jax import lax
from jax.experimental import pallas as pl
from jax.sharding import PartitionSpec as P
from jax.experimental.pallas import tpu as pltpu

HEAD_DIM = 64
BLOCK = 64
PAIR = 2 * BLOCK
MASKED = -1e30
bf16 = jnp.bfloat16
f32 = jnp.float32


def dot_nn(a, b):
    return lax.dot_general(a, b, (((1,), (0,)), ((), ())), preferred_element_type=f32)


def dot_nt(a, b):
    return lax.dot_general(a, b, (((1,), (1,)), ((), ())), preferred_element_type=f32)


def dot_tn(a, b):
    return lax.dot_general(a, b, (((0,), (0,)), ((), ())), preferred_element_type=f32)


def pair_table(rand_local, global_ids, flip, nblocks):
    heads = rand_local.shape[0]
    null = nblocks
    first = (2 * jnp.arange(nblocks // 2, dtype=jnp.int32)) ^ flip

    def near(block):
        bad = (block < 0) | (block >= nblocks) | (block == global_ids[0]) | (block == global_ids[1])
        return jnp.where(bad, null, block ^ flip)

    rand_first = rand_local[:, first, :] ^ flip
    rand_second = rand_local[:, first + 1, :] ^ flip
    nears = jnp.stack([near(first), near(first + 1), near(first - 1), near(first + 2)], axis=1)
    nears = jnp.broadcast_to(nears[None], (heads,) + nears.shape)
    return jnp.concatenate(
        [nears[:, :, 0:3], rand_first, nears[:, :, 3:4], rand_second], axis=2
    ).astype(jnp.int32).reshape(-1)


def slots(tab_ref, gl_ref, head, pair, npairs):
    at = (head * npairs + pair) * 10
    got = [pl.multiple_of(tab_ref[at + j] * BLOCK, BLOCK) for j in range(10)]
    glob = [pl.multiple_of(gl_ref[j] * BLOCK, BLOCK) for j in range(2)]
    return got[0:2] + glob, got[2:6], got[6:10]


def stack_rows(ref, offsets, lanes):
    return jnp.concatenate([ref[pl.ds(o, BLOCK), lanes] for o in offsets], axis=0)


def lane_halves(width, dtype):
    lane = lax.broadcasted_iota(jnp.int32, (1, width), 1) % PAIR
    first = (lane < BLOCK).astype(dtype)
    second = (lane >= BLOCK).astype(dtype)
    return first, second


def fill_kv(kv_refs, k_sc, v_sc, heads):
    rows = kv_refs[0].shape[0]
    kw = heads * PAIR
    for c, ref in enumerate(kv_refs):
        k_sc[pl.ds(c * rows, rows), :] = ref[:, 0:kw]
        v_sc[pl.ds(c * rows, rows), :] = ref[:, kw:]
    last = len(kv_refs) * rows
    lane = lax.broadcasted_iota(jnp.int32, (BLOCK, kw), 1) % PAIR
    k_sc[pl.ds(last, BLOCK), :] = (lane == BLOCK + 16).astype(f32).astype(bf16)
    v_sc[pl.ds(last, BLOCK), :] = jnp.zeros((BLOCK, v_sc.shape[1]), bf16)


def global_columns(src_ref, rows, gl_ref):
    lane = lax.broadcasted_iota(jnp.int32, (1, PAIR), 1)
    parts = []
    for g in range(2):
        block = gl_ref[g]
        at = pl.multiple_of((block // 2) * PAIR, PAIR)
        both = src_ref[rows, pl.ds(at, PAIR)].astype(f32)
        moved = pltpu.roll(both, BLOCK, 1)
        parts.append(jnp.where(block % 2 == g, both, moved))
    return jnp.where(lane < BLOCK, parts[0], parts[1])


def put_global_columns(dst_ref, rows, gl_ref, value, per_chunk):
    lane = lax.broadcasted_iota(jnp.int32, (1, PAIR), 1)
    moved = pltpu.roll(value, BLOCK, 1)
    for g in range(2):
        block = gl_ref[g]
        pair = block // 2
        half = block % 2
        chunk = pair // per_chunk
        at = pl.multiple_of((pair % per_chunk) * PAIR, PAIR)
        src = jnp.where(half == g, value, moved)
        old = dst_ref[chunk, rows, pl.ds(at, PAIR)].astype(f32)
        new = jnp.where((lane >= BLOCK) == (half == 1), src, old)
        dst_ref[chunk, rows, pl.ds(at, PAIR)] = new.astype(dst_ref.dtype)


def forward_kernel(heads, chunks, tab_ref, gl_ref, *refs):
    kv_refs, q_refs = refs[0:chunks], refs[chunks : 2 * chunks]
    out_ref, lse_ref, lseg_ref, k_sc, v_sc, q_sc, s_sc = refs[2 * chunks :]
    rows = kv_refs[0].shape[0]
    length = rows * chunks
    npairs = length // PAIR
    per_chunk = npairs // chunks
    fill_kv(kv_refs, k_sc, v_sc, heads)
    for c in range(chunks):
        q_sc[:, c * rows : (c + 1) * rows] = q_refs[c][...]
    first, second = lane_halves(PAIR, bf16)
    lane = lax.broadcasted_iota(jnp.int32, (1, PAIR), 1)

    @pl.loop(0, npairs)
    def _(pair):
        chunk = pair // per_chunk
        local = pl.multiple_of((pair % per_chunk) * PAIR, PAIR)
        at = pl.multiple_of(pair * PAIR, PAIR)
        for h in range(heads):
            shared, mine, other = slots(tab_ref, gl_ref, h, pair, npairs)
            kl = slice(h * PAIR, (h + 1) * PAIR)
            vl = slice((h // 2) * PAIR, (h // 2 + 1) * PAIR)
            off = BLOCK * (h % 2)
            q = q_sc[kl, pl.ds(at, PAIR)]
            s_sh = dot_nn(stack_rows(k_sc, shared, kl), q)
            k_pr = jnp.concatenate([stack_rows(k_sc, mine, kl), stack_rows(k_sc, other, kl)], axis=1)
            s_pr = dot_nn(k_pr, jnp.concatenate([q * first, q * second], axis=0))
            peak = jnp.maximum(jnp.max(s_sh, axis=0, keepdims=True), jnp.max(s_pr, axis=0, keepdims=True))
            e_sh = jnp.exp(s_sh - peak)
            e_pr = jnp.exp(s_pr - peak)
            total = jnp.sum(e_sh, axis=0, keepdims=True) + jnp.sum(e_pr, axis=0, keepdims=True)
            inv = 1.0 / total
            p_sh = (e_sh * inv).astype(bf16)
            p_pr = (e_pr * inv).astype(bf16)
            v_pr = jnp.concatenate([stack_rows(v_sc, mine, vl), stack_rows(v_sc, other, vl)], axis=1)
            o_sh = dot_tn(stack_rows(v_sc, shared, vl), p_sh)
            o_pr = dot_tn(v_pr, p_pr)
            ctx = o_sh[off : off + BLOCK] + jnp.where(
                lane < BLOCK, o_pr[off : off + BLOCK], o_pr[PAIR + off : PAIR + off + BLOCK]
            )
            out_ref[chunk, h * BLOCK : (h + 1) * BLOCK, pl.ds(local, PAIR)] = ctx.astype(bf16)
            lse_ref[h, pl.ds(pair, 1), :] = peak + jnp.log(total)

    step = 512
    for h in range(heads):
        kl = slice(h * PAIR, (h + 1) * PAIR)
        vl = slice((h // 2) * PAIR, (h // 2 + 1) * PAIR)
        off = BLOCK * (h % 2)
        q = global_columns(q_sc, kl, gl_ref).astype(bf16)

        def score(c, peak):
            at = pl.multiple_of(c * step, step)
            s = dot_nn(k_sc[pl.ds(at, step), kl], q)
            s_sc[pl.ds(at, step), :] = s
            return jnp.maximum(peak, jnp.max(s, axis=0, keepdims=True))

        peak = lax.fori_loop(0, length // step, score, jnp.full((1, PAIR), MASKED, f32))

        def gather(c, carry):
            total, ctx = carry
            at = pl.multiple_of(c * step, step)
            e = jnp.exp(s_sc[pl.ds(at, step), :] - peak)
            ctx = ctx + dot_tn(v_sc[pl.ds(at, step), vl], e.astype(bf16))
            return total + jnp.sum(e, axis=0, keepdims=True), ctx

        total, ctx = lax.fori_loop(
            0, length // step, gather, (jnp.zeros((1, PAIR), f32), jnp.zeros((PAIR, PAIR), f32))
        )
        ctx = ctx[off : off + BLOCK] * (1.0 / total)
        put_global_columns(out_ref, slice(h * BLOCK, (h + 1) * BLOCK), gl_ref, ctx, per_chunk)
        lseg_ref[h : h + 1, :] = peak + jnp.log(total)


def attention_forward(tab, gl, kv, q):
    chunks = len(kv)
    rows = kv[0].shape[0]
    heads = q[0].shape[0] // PAIR
    vw = kv[0].shape[1] - heads * PAIR
    length = rows * chunks
    whole = lambda: pl.BlockSpec(memory_space=pltpu.VMEM)
    return pl.pallas_call(
        functools.partial(forward_kernel, heads, chunks),
        out_shape=(
            jax.ShapeDtypeStruct((chunks, heads * HEAD_DIM, rows), bf16),
            jax.ShapeDtypeStruct((heads, length // PAIR, PAIR), f32),
            jax.ShapeDtypeStruct((heads, PAIR), f32),
        ),
        in_specs=[pl.BlockSpec(memory_space=pltpu.SMEM)] * 2 + [whole()] * (2 * chunks),
        out_specs=(whole(), whole(), whole()),
        scratch_shapes=[
            pltpu.VMEM((length + BLOCK, heads * PAIR), bf16),
            pltpu.VMEM((length + BLOCK, vw), bf16),
            pltpu.VMEM((heads * PAIR, length), bf16),
            pltpu.VMEM((length, PAIR), f32),
        ],
        compiler_params=pltpu.CompilerParams(vmem_limit_bytes=56 << 20),
        cost_estimate=pl.CostEstimate(flops=8_000_000_000, bytes_accessed=12_000_000, transcendentals=8_000_000),
        name="attention_forward",
    )(tab, gl, *kv, *q)


def backward_kernel(heads, chunks, tab_ref, gl_ref, *refs):
    kv_refs, q_refs, do_refs = refs[0:chunks], refs[chunks : 2 * chunks], refs[2 * chunks : 3 * chunks]
    lse_ref, lseg_ref, dq_ref, dkv_ref, k_sc, v_sc, q_sc, do_sc, acc, p_sc, d_sc, dqg_sc = refs[3 * chunks :]
    rows = kv_refs[0].shape[0]
    length = rows * chunks
    npairs = length // PAIR
    per_chunk = npairs // chunks
    fill_kv(kv_refs, k_sc, v_sc, heads)
    for c in range(chunks):
        q_sc[:, c * rows : (c + 1) * rows] = q_refs[c][...]
        do_sc[:, c * rows : (c + 1) * rows] = do_refs[c][...]
    first, second = lane_halves(PAIR, bf16)
    first2, second2 = lane_halves(2 * PAIR, bf16)
    ffirst, fsecond = lane_halves(PAIR, f32)
    lane = lax.broadcasted_iota(jnp.int32, (1, PAIR), 1)
    zeros = jnp.zeros((BLOCK, PAIR), bf16)

    def value_rows(do, h):
        return jnp.concatenate([do, zeros] if h % 2 == 0 else [zeros, do], axis=0)

    def sources(q, do):
        top = jnp.concatenate([q[0:BLOCK], zeros], axis=1)
        return jnp.concatenate([top, jnp.concatenate([zeros, do], axis=1)], axis=0)

    step = 512
    for h in range(heads):
        kl = slice(h * PAIR, (h + 1) * PAIR)
        vl = slice((h // 2) * PAIR, (h // 2 + 1) * PAIR)
        q = global_columns(q_sc, kl, gl_ref).astype(bf16)
        do = global_columns(do_sc, slice(h * BLOCK, (h + 1) * BLOCK), gl_ref).astype(bf16)
        do_v = value_rows(do, h)
        lse = lseg_ref[h : h + 1, :]
        src = sources(q, do)

        def weigh(c, delta):
            at = pl.multiple_of(c * step, step)
            p = jnp.exp(dot_nn(k_sc[pl.ds(at, step), kl], q) - lse)
            dp = dot_nn(v_sc[pl.ds(at, step), vl], do_v)
            p_sc[pl.ds(at, step), :] = p
            d_sc[pl.ds(at, step), :] = dp
            return delta + jnp.sum(p * dp, axis=0, keepdims=True)

        delta = lax.fori_loop(0, length // step, weigh, jnp.zeros((1, PAIR), f32))

        def spread(c, dq):
            at = pl.multiple_of(c * step, step)
            p = p_sc[pl.ds(at, step), :]
            ds = (p * (d_sc[pl.ds(at, step), :] - delta)).astype(bf16)
            both = jnp.concatenate([ds, p.astype(bf16)], axis=1)
            acc[h, pl.ds(at, step), :] = dot_nt(both, src)
            return dq + dot_tn(k_sc[pl.ds(at, step), kl], ds)

        dq = lax.fori_loop(0, length // step, spread, jnp.zeros((PAIR, PAIR), f32))
        dqg_sc[h] = dq[0:BLOCK] * (HEAD_DIM ** -0.5)
        acc[h, pl.ds(length, BLOCK), :] = jnp.zeros((BLOCK, PAIR), f32)

    @pl.loop(0, npairs)
    def _(pair):
        chunk = pair // per_chunk
        local = pl.multiple_of((pair % per_chunk) * PAIR, PAIR)
        at = pl.multiple_of(pair * PAIR, PAIR)
        hit_first = (gl_ref[0] == 2 * pair) | (gl_ref[1] == 2 * pair)
        hit_second = (gl_ref[0] == 2 * pair + 1) | (gl_ref[1] == 2 * pair + 1)
        shut = ffirst * jnp.where(hit_first, -MASKED, 0.0) + fsecond * jnp.where(hit_second, -MASKED, 0.0)
        for h in range(heads):
            shared, mine, other = slots(tab_ref, gl_ref, h, pair, npairs)
            kl = slice(h * PAIR, (h + 1) * PAIR)
            vl = slice((h // 2) * PAIR, (h // 2 + 1) * PAIR)
            q = q_sc[kl, pl.ds(at, PAIR)]
            do = do_sc[h * BLOCK : (h + 1) * BLOCK, pl.ds(at, PAIR)]
            do_v = value_rows(do, h)
            lse = lse_ref[h, pl.ds(pair, 1), :] + shut
            k_sh = stack_rows(k_sc, shared, kl)
            k_pr = jnp.concatenate([stack_rows(k_sc, mine, kl), stack_rows(k_sc, other, kl)], axis=1)
            p_sh = jnp.exp(dot_nn(k_sh, q) - lse)
            p_pr = jnp.exp(dot_nn(k_pr, jnp.concatenate([q * first, q * second], axis=0)) - lse)
            d_sh = dot_nn(stack_rows(v_sc, shared, vl), do_v)
            v_pr = jnp.concatenate([stack_rows(v_sc, mine, vl), stack_rows(v_sc, other, vl)], axis=1)
            d_pr = dot_nn(v_pr, jnp.concatenate([do_v * first, do_v * second], axis=0))
            delta = jnp.sum(p_sh * d_sh, axis=0, keepdims=True) + jnp.sum(p_pr * d_pr, axis=0, keepdims=True)
            ds_sh = (p_sh * (d_sh - delta)).astype(bf16)
            ds_pr = (p_pr * (d_pr - delta)).astype(bf16)
            src = sources(q, do)
            g_sh = dot_nt(jnp.concatenate([ds_sh, p_sh.astype(bf16)], axis=1), src)
            src2 = jnp.concatenate([src * first2, src * second2], axis=0)
            g_pr = dot_nt(jnp.concatenate([ds_pr, p_pr.astype(bf16)], axis=1), src2)
            for j, o in enumerate(shared):
                acc[h, pl.ds(o, BLOCK), :] += g_sh[j * BLOCK : (j + 1) * BLOCK]
            for j, o in enumerate(mine):
                acc[h, pl.ds(o, BLOCK), :] += g_pr[j * BLOCK : (j + 1) * BLOCK, 0:PAIR]
            for j, o in enumerate(other):
                acc[h, pl.ds(o, BLOCK), :] += g_pr[j * BLOCK : (j + 1) * BLOCK, PAIR:]
            t_sh = dot_tn(k_sh, ds_sh)
            t_pr = dot_tn(k_pr, ds_pr)
            dq = t_sh[0:BLOCK] + jnp.where(lane < BLOCK, t_pr[0:BLOCK], t_pr[PAIR : PAIR + BLOCK])
            dq_ref[chunk, h * BLOCK : (h + 1) * BLOCK, pl.ds(local, PAIR)] = (dq * (HEAD_DIM ** -0.5)).astype(bf16)

    for h in range(heads):
        put_global_columns(dq_ref, slice(h * BLOCK, (h + 1) * BLOCK), gl_ref, dqg_sc[h], per_chunk)
        for c in range(chunks):
            dkv_ref[c, :, h * PAIR : (h + 1) * PAIR] = acc[h, pl.ds(c * rows, rows), :].astype(bf16)


def attention_backward(tab, gl, kv, q, do, lse, lseg):
    chunks = len(kv)
    rows = kv[0].shape[0]
    heads = q[0].shape[0] // PAIR
    vw = kv[0].shape[1] - heads * PAIR
    length = rows * chunks
    whole = lambda: pl.BlockSpec(memory_space=pltpu.VMEM)
    return pl.pallas_call(
        functools.partial(backward_kernel, heads, chunks),
        out_shape=(
            jax.ShapeDtypeStruct((chunks, heads * HEAD_DIM, rows), bf16),
            jax.ShapeDtypeStruct((chunks, rows, heads * PAIR), bf16),
        ),
        in_specs=[pl.BlockSpec(memory_space=pltpu.SMEM)] * 2 + [whole()] * (3 * chunks + 2),
        out_specs=(whole(), whole()),
        scratch_shapes=[
            pltpu.VMEM((length + BLOCK, heads * PAIR), bf16),
            pltpu.VMEM((length + BLOCK, vw), bf16),
            pltpu.VMEM((heads * PAIR, length), bf16),
            pltpu.VMEM((heads * HEAD_DIM, length), bf16),
            pltpu.VMEM((heads, length + BLOCK, PAIR), f32),
            pltpu.VMEM((length, PAIR), f32),
            pltpu.VMEM((length, PAIR), f32),
            pltpu.VMEM((heads, BLOCK, PAIR), f32),
        ],
        compiler_params=pltpu.CompilerParams(vmem_limit_bytes=60 << 20),
        cost_estimate=pl.CostEstimate(flops=25_000_000_000, bytes_accessed=20_000_000, transcendentals=8_000_000),
        name="attention_backward",
    )(tab, gl, *kv, *q, *do, lse, lseg)


def project(chunks_x, segs, w_q, w_kv, b_q, b_v, heads):
    kv_all, q_all = [], []
    kw = heads * PAIR
    for x, seg in zip(chunks_x, segs):
        y = jnp.dot(x, w_kv, preferred_element_type=f32) + b_v
        col = jnp.arange(y.shape[1], dtype=jnp.int32)[None, :]
        spot = col % PAIR - BLOCK
        mark = ((col < kw) & (spot == seg[:, None])).astype(f32)
        kv_all.append((y + mark).astype(bf16))
        z = lax.dot_general(w_q, x, (((0,), (1,)), ((), ())), preferred_element_type=f32) + b_q[:, None]
        row = jnp.arange(z.shape[0], dtype=jnp.int32)[:, None] % PAIR - BLOCK
        barred = (row >= 0) & (row <= 16) & (row != seg[None, :])
        q_all.append(jnp.where(barred, MASKED, z.astype(bf16).astype(f32) * HEAD_DIM ** -0.5).astype(bf16))
    return kv_all, q_all


norm_eps = 1e-12
ALL = ("dp", "seq", "ffn")


def layer_norm(residual, gain, shift):
    center = residual - jnp.mean(residual, axis=-1, keepdims=True)
    spread = jnp.mean(center * center, axis=-1, keepdims=True)
    return center * lax.rsqrt(spread + norm_eps) * gain + shift


def gelu_exact(values):
    return jax.nn.gelu(values, approximate=False)


def flip_send(array, axis, bits):
    count = lax.axis_size(axis)
    return lax.ppermute(array, axis, [(i, i ^ bits) for i in range(count)])


def shards(
    tokens, w_query, w_key, w_value, w_output, b_query, b_value, b_output, w_up, b_up, w_down, b_down,
    gain_attn, shift_attn, gain_ffn, shift_ffn, segment_ids, random_blocks, global_blocks, cotangent,
):
    seq_n, dp_n, ffn_n = lax.axis_size("seq"), lax.axis_size("dp"), lax.axis_size("ffn")
    me = lax.axis_index("seq")
    own, width = w_query.shape
    group = width // seq_n
    heads = group // HEAD_DIM
    features = tokens[0]
    rows = features.shape[0]

    near = [features] + [None] * (seq_n - 1)
    for k in range(1, seq_n):
        bit = k & -k
        near[k] = flip_send(features if bit == k else near[k ^ bit], "seq", bit)

    def by_group(w):
        return w.reshape(own, seq_n, group).transpose(1, 0, 2)

    note = jnp.pad(jnp.stack([b_query, b_value]), ((0, 0), (0, 3 * group - own)))
    pack = jnp.concatenate([by_group(w_query), by_group(w_key), by_group(w_value)], axis=2)
    pack = jnp.concatenate([pack, jnp.broadcast_to(note[None], (seq_n,) + note.shape)], axis=1)
    pack = lax.all_to_all(pack, "seq", split_axis=0, concat_axis=0, tiled=True)
    pack = lax.all_gather(pack, ("dp", "ffn"), axis=0, tiled=False).reshape(
        dp_n, ffn_n, seq_n, own + 2, 3 * group
    ).transpose(0, 2, 1, 3, 4)
    w_own = pack[:, :, :, :own].reshape(width, 3 * group)
    biases = lax.dynamic_slice(
        pack[:, :, :, own:, :own].transpose(3, 0, 1, 2, 4).reshape(2, width), (0, me * group), (2, group)
    ).astype(f32)
    w_q, w_k, w_v = w_own[:, :group], w_own[:, group : 2 * group], w_own[:, 2 * group :]

    def padded(w):
        lead = w.shape[:-1]
        return jnp.pad(w.reshape(lead + (heads, HEAD_DIM)), ((0, 0),) * len(lead) + ((0, 0), (0, HEAD_DIM))).reshape(
            lead + (heads * PAIR,)
        )

    spare = -group % PAIR
    w_kv = jnp.concatenate([padded(w_k), w_v, jnp.zeros((width, spare), bf16)], axis=1)
    b_kv = jnp.concatenate([jnp.zeros((heads * PAIR,), f32), biases[1], jnp.zeros((spare,), f32)])
    seg = segment_ids[0].reshape(seq_n, rows)
    segs = [lax.dynamic_index_in_dim(seg, me ^ k, keepdims=False) for k in range(seq_n)]
    kv, q = project(near, segs, padded(w_q), w_kv, padded(biases[0]), b_kv, heads)

    vectors = jnp.stack([b_output, b_down, gain_attn, shift_attn, gain_ffn, shift_ffn])
    vectors = jnp.pad(vectors, ((0, 0), (0, width - own)))
    rest = jnp.concatenate([w_up, w_down, w_output, b_up[None], vectors], axis=0)
    up_rows = w_up.shape[0]
    rest = lax.all_gather(rest, ALL, axis=0, tiled=False).reshape(dp_n * seq_n, ffn_n, rest.shape[0], width)
    up_blocks = rest[:, :, :up_rows].transpose(1, 0, 2, 3).reshape(ffn_n, width, -1)
    down_blocks = rest[:, :, up_rows : 2 * up_rows].transpose(1, 0, 2, 3).reshape(ffn_n, width, -1)
    at = 2 * up_rows
    output_full = rest[:, :, at : at + own].reshape(width, width)
    bias_up = rest[0, :, at + own].astype(f32)
    vecs = rest[:, :, at + own + 1 :, :own].transpose(2, 0, 1, 3).reshape(6, width).astype(f32)
    bias_output, bias_down, gain_one, shift_one, gain_two, shift_two = [vecs[i] for i in range(6)]

    nblocks = seq_n * rows // BLOCK
    flip = me.astype(jnp.int32) * (nblocks // seq_n)
    tab = pair_table(random_blocks[0], global_blocks[0], flip, nblocks)
    gl = global_blocks[0] ^ flip
    ctx, lse, lseg = attention_forward(tab, gl, kv, q)
    ctx_parts = [ctx[0]] + [flip_send(ctx[k], "seq", k) for k in range(1, seq_n)]
    ctx_tok = jnp.concatenate(ctx_parts, axis=0)
    relative = jnp.arange(seq_n) ^ me
    w_o = output_full.reshape(seq_n, group, width)[relative].reshape(width, width)

    branch = dot_tn(ctx_tok, w_o) + bias_output
    resid_one = features.astype(f32) + branch
    normed_one = layer_norm(resid_one, gain_one, shift_one)
    normed_low = normed_one.astype(bf16)
    pre_act = [dot_nn(normed_low, up_blocks[f]) + bias_up[f] for f in range(ffn_n)]
    hidden = [gelu_exact(p).astype(bf16) for p in pre_act]
    ffn_sum = sum(dot_nt(hidden[f], down_blocks[f]) for f in range(ffn_n))
    resid_two = normed_one + ffn_sum + bias_down
    normed_two = layer_norm(resid_two, gain_two, shift_two)
    grad_resid_two, grad_gain_two, grad_shift_two = jax.vjp(layer_norm, resid_two, gain_two, shift_two)[1](
        cotangent[0].astype(f32)
    )
    grad_ffn = grad_resid_two.astype(bf16)
    grad_bias_down = jnp.sum(grad_ffn.astype(f32), axis=0)
    grad_pre = [
        jax.vjp(gelu_exact, pre_act[f])[1](dot_nn(grad_ffn, down_blocks[f]))[0].astype(bf16) for f in range(ffn_n)
    ]
    grad_normed = sum(dot_nt(grad_pre[f], up_blocks[f]) for f in range(ffn_n))
    grad_resid_one, grad_gain_one, grad_shift_one = jax.vjp(layer_norm, resid_one, gain_one, shift_one)[1](
        grad_resid_two + grad_normed
    )
    grad_branch = grad_resid_one.astype(bf16)
    grad_bias_output = jnp.sum(grad_branch.astype(f32), axis=0)
    grad_ctx = dot_nt(w_o, grad_branch).astype(bf16).reshape(seq_n, group, rows)
    do = [grad_ctx[0]] + [flip_send(grad_ctx[k], "seq", k) for k in range(1, seq_n)]

    grad_down = jnp.stack([dot_tn(grad_ffn, hidden[f]).astype(bf16) for f in range(ffn_n)])
    grad_up = jnp.stack([dot_tn(normed_low, grad_pre[f]).astype(bf16) for f in range(ffn_n)])
    grad_bias_up = jnp.stack([jnp.sum(g.astype(f32), axis=0) for g in grad_pre])
    grad_out = dot_nn(ctx_tok, grad_branch).astype(bf16).reshape(seq_n, group, width)[relative].reshape(width, width)
    outer = dp_n * seq_n

    def placed(g):
        return g.reshape(ffn_n, outer, up_rows, width).transpose(1, 0, 2, 3)

    vec_grads = jnp.stack(
        [grad_bias_output, grad_bias_down, grad_gain_one, grad_shift_one, grad_gain_two, grad_shift_two]
    ).astype(bf16)
    vec_grads = vec_grads.reshape(6, outer, ffn_n, own).transpose(1, 2, 0, 3)
    vec_grads = jnp.pad(vec_grads, ((0, 0), (0, 0), (0, 0), (0, width - own)))
    sums = jnp.concatenate(
        [
            placed(grad_up),
            placed(grad_down),
            grad_out.reshape(outer, ffn_n, own, width),
            jnp.broadcast_to(grad_bias_up.astype(bf16)[None, :, None], (outer, ffn_n, 1, width)),
            vec_grads,
        ],
        axis=2,
    )
    sums = jnp.pad(sums, ((0, 0), (0, 0), (0, -sums.shape[2] % 32), (0, 0)))
    per = sums.shape[2]
    sums = lax.psum_scatter(
        sums.reshape(outer * ffn_n * per, width), ALL, scatter_dimension=0, tiled=True
    ).astype(f32)
    out_up, out_down, out_output = sums[:up_rows], sums[up_rows:at], sums[at : at + own]
    out_bias_up = sums[at + own]
    out_vecs = sums[at + own + 1 : at + own + 7, :own]

    dq, dkv = attention_backward(tab, gl, kv, q, do, lse, lseg)
    w_kv_pairs = jnp.concatenate(
        [w_k.reshape(width, heads, HEAD_DIM), w_v.reshape(width, heads, HEAD_DIM)], axis=2
    ).reshape(width, heads * PAIR)
    part = [
        lax.dot_general(dq[k], w_q, (((0,), (1,)), ((), ())), preferred_element_type=f32) + dot_nt(dkv[k], w_kv_pairs)
        for k in range(seq_n)
    ]
    bit = 1
    while bit < seq_n:
        for k in range(seq_n):
            if k & -k == bit and k != bit:
                part[k ^ bit] = part[k ^ bit] + flip_send(part[k].astype(bf16), "seq", bit).astype(f32)
        bit *= 2
    grad_features = grad_resid_one + part[0]
    bit = 1
    while bit < seq_n:
        grad_features = grad_features + flip_send(part[bit].astype(bf16), "seq", bit).astype(f32)
        bit *= 2

    grad_q = sum(
        lax.dot_general(near[k], dq[k], (((0,), (1,)), ((), ())), preferred_element_type=f32) for k in range(seq_n)
    )
    grad_kv = sum(dot_tn(near[k], dkv[k]) for k in range(seq_n)).reshape(width, heads, 2, HEAD_DIM)
    grad_w = jnp.concatenate(
        [grad_q, grad_kv[:, :, 0].reshape(width, group), grad_kv[:, :, 1].reshape(width, group)], axis=1
    )
    sum_q = jnp.sum(dq.astype(f32), axis=(0, 2))
    sum_v = jnp.sum(dkv.astype(f32), axis=(0, 1)).reshape(heads, 2, HEAD_DIM)[:, 1].reshape(group)
    sum_b = lax.dynamic_update_slice(jnp.zeros((2, width), f32), jnp.stack([sum_q, sum_v]), (0, me * group))
    sum_b = sum_b.reshape(2, dp_n, seq_n, ffn_n, own).transpose(1, 3, 2, 0, 4)
    sum_b = jnp.pad(sum_b, ((0, 0),) * 4 + ((0, 3 * group - own),))
    grad_w = grad_w.reshape(dp_n, seq_n, ffn_n, own, 3 * group).transpose(0, 2, 1, 3, 4)
    grad_w = jnp.concatenate([grad_w, sum_b], axis=3).astype(bf16)
    grad_w = jnp.pad(grad_w, ((0, 0),) * 3 + ((0, -(own + 2) % 32), (0, 0)))
    per = grad_w.shape[3]
    grad_w = lax.psum_scatter(
        grad_w.reshape(dp_n * ffn_n * seq_n * per, 3 * group), ("dp", "ffn"), scatter_dimension=0, tiled=True
    ).reshape(seq_n, per, 3 * group)
    grad_w = lax.all_to_all(grad_w, "seq", split_axis=0, concat_axis=0, tiled=True).astype(f32)
    out_qkv = [
        grad_w[:, :own, i * group : (i + 1) * group].transpose(1, 0, 2).reshape(own, width) for i in range(3)
    ]
    out_b = jnp.sum(grad_w[:, own : own + 2, :own], axis=0)
    return (
        normed_two.astype(bf16)[None],
        grad_features[None],
        out_qkv[0],
        out_qkv[1],
        out_qkv[2],
        out_output,
        out_b[0],
        out_b[1],
        out_vecs[0],
        out_up,
        out_bias_up,
        out_down,
        out_vecs[1],
        out_vecs[2],
        out_vecs[3],
        out_vecs[4],
        out_vecs[5],
    )


def solution(mesh):
    return jax.shard_map(
        shards,
        mesh=mesh,
        in_specs=(
            P(("dp", "ffn"), "seq", None),
            P(("dp", "seq", "ffn"), None),
            P(("dp", "seq", "ffn"), None),
            P(("dp", "seq", "ffn"), None),
            P(("dp", "seq", "ffn"), None),
            P(("dp", "seq", "ffn")),
            P(("dp", "seq", "ffn")),
            P(("dp", "seq", "ffn")),
            P(("dp", "seq"), "ffn"),
            P("ffn"),
            P(("dp", "seq"), "ffn"),
            P(("dp", "seq", "ffn")),
            P(("dp", "seq", "ffn")),
            P(("dp", "seq", "ffn")),
            P(("dp", "seq", "ffn")),
            P(("dp", "seq", "ffn")),
            P(("dp", "ffn"), None),
            P(("dp", "ffn"), "seq", None, None),
            P(("dp", "ffn"), None),
            P(("dp", "ffn"), "seq", None),
        ),
        out_specs=(
            P(("dp", "ffn"), "seq", None),
            P(("dp", "ffn"), "seq", None),
            P(("dp", "seq", "ffn"), None),
            P(("dp", "seq", "ffn"), None),
            P(("dp", "seq", "ffn"), None),
            P(("dp", "seq", "ffn"), None),
            P(("dp", "seq", "ffn")),
            P(("dp", "seq", "ffn")),
            P(("dp", "seq", "ffn")),
            P(("dp", "seq"), "ffn"),
            P("ffn"),
            P(("dp", "seq"), "ffn"),
            P(("dp", "seq", "ffn")),
            P(("dp", "seq", "ffn")),
            P(("dp", "seq", "ffn")),
            P(("dp", "seq", "ffn")),
            P(("dp", "seq", "ffn")),
        ),
        check_vma=False,
    )
```

```python
import functools
import jax
import jax.numpy as jnp
from jax import lax
from jax.experimental import pallas as pl
from jax.sharding import PartitionSpec as P
from jax.experimental.pallas import tpu as pltpu

HEAD_DIM = 64
BLOCK = 64
PAIR = 2 * BLOCK
MASKED = -1e30
bf16 = jnp.bfloat16
f32 = jnp.float32


def dot_nn(a, b):
    return lax.dot_general(a, b, (((1,), (0,)), ((), ())), preferred_element_type=f32)


def dot_nt(a, b):
    return lax.dot_general(a, b, (((1,), (1,)), ((), ())), preferred_element_type=f32)


def dot_tn(a, b):
    return lax.dot_general(a, b, (((0,), (0,)), ((), ())), preferred_element_type=f32)


def pair_table(rand_local, global_ids, flip, nblocks):
    heads = rand_local.shape[0]
    null = nblocks
    first = (2 * jnp.arange(nblocks // 2, dtype=jnp.int32)) ^ flip

    def near(block):
        bad = (block < 0) | (block >= nblocks) | (block == global_ids[0]) | (block == global_ids[1])
        return jnp.where(bad, null, block ^ flip)

    rand_first = rand_local[:, first, :] ^ flip
    rand_second = rand_local[:, first + 1, :] ^ flip
    nears = jnp.stack([near(first), near(first + 1), near(first - 1), near(first + 2)], axis=1)
    nears = jnp.broadcast_to(nears[None], (heads,) + nears.shape)
    return jnp.concatenate(
        [nears[:, :, 0:3], rand_first, nears[:, :, 3:4], rand_second], axis=2
    ).astype(jnp.int32).reshape(-1)


def slots(tab_ref, gl_ref, head, pair, npairs):
    at = (head * npairs + pair) * 10
    got = [pl.multiple_of(tab_ref[at + j] * BLOCK, BLOCK) for j in range(10)]
    glob = [pl.multiple_of(gl_ref[j] * BLOCK, BLOCK) for j in range(2)]
    return got[0:2] + glob, got[2:6], got[6:10]


def stack_rows(ref, offsets, lanes):
    return jnp.concatenate([ref[pl.ds(o, BLOCK), lanes] for o in offsets], axis=0)


def lane_halves(width, dtype):
    lane = lax.broadcasted_iota(jnp.int32, (1, width), 1) % PAIR
    first = (lane < BLOCK).astype(dtype)
    second = (lane >= BLOCK).astype(dtype)
    return first, second


VALUE_GROUP = (0, 0, 1)
VALUE_ROW = (0, BLOCK, BLOCK)


def key_lanes(h):
    return slice(h * PAIR, (h + 1) * PAIR)


def value_lanes(h):
    return slice(VALUE_GROUP[h] * PAIR, (VALUE_GROUP[h] + 1) * PAIR)


def query_columns(q_ref, mask_ref, h, at):
    return jnp.concatenate([q_ref[h * BLOCK : (h + 1) * BLOCK, pl.ds(at, PAIR)], mask_ref[:, pl.ds(at, PAIR)]], axis=0)


def global_queries(q_ref, mask_ref, h, gl_ref):
    return jnp.concatenate(
        [
            global_columns(q_ref, slice(h * BLOCK, (h + 1) * BLOCK), gl_ref),
            global_columns(mask_ref, slice(0, BLOCK), gl_ref),
        ],
        axis=0,
    ).astype(bf16)


def global_columns(src_ref, rows, gl_ref):
    lane = lax.broadcasted_iota(jnp.int32, (1, PAIR), 1)
    parts = []
    for g in range(2):
        block = gl_ref[g]
        at = pl.multiple_of((block // 2) * PAIR, PAIR)
        both = src_ref[rows, pl.ds(at, PAIR)].astype(f32)
        moved = pltpu.roll(both, BLOCK, 1)
        parts.append(jnp.where(block % 2 == g, both, moved))
    return jnp.where(lane < BLOCK, parts[0], parts[1])


def put_global_columns(dst_ref, rows, gl_ref, value, per_chunk):
    lane = lax.broadcasted_iota(jnp.int32, (1, PAIR), 1)
    moved = pltpu.roll(value, BLOCK, 1)
    for g in range(2):
        block = gl_ref[g]
        pair = block // 2
        half = block % 2
        chunk = pair // per_chunk
        at = pl.multiple_of((pair % per_chunk) * PAIR, PAIR)
        src = jnp.where(half == g, value, moved)
        old = dst_ref[chunk, rows, pl.ds(at, PAIR)].astype(f32)
        new = jnp.where((lane >= BLOCK) == (half == 1), src, old)
        dst_ref[chunk, rows, pl.ds(at, PAIR)] = new.astype(dst_ref.dtype)


def project_rows(x, seg, wkv_ref, bkv_ref, wq_ref, bq_ref, k_ref, v_ref, q_ref, mask_ref, at):
    n = x.shape[0]
    y = dot_nn(x, wkv_ref[...]) + bkv_ref[...]
    spot = lax.broadcasted_iota(jnp.int32, (PAIR, n), 0) - BLOCK
    mark = jnp.transpose((spot == seg).astype(f32), (1, 0))
    lane = lax.broadcasted_iota(jnp.int32, (1, PAIR), 1)
    rows = pl.ds(at, n)
    k_ref[rows, 0:PAIR] = (y[:, 0:PAIR] + mark).astype(bf16)
    k_ref[rows, PAIR : 2 * PAIR] = (y[:, PAIR : 2 * PAIR] + mark).astype(bf16)
    both = y[:, 2 * PAIR : 3 * PAIR]
    k_ref[rows, 2 * PAIR : 3 * PAIR] = jnp.where(lane < BLOCK, both, mark).astype(bf16)
    v_ref[rows, 0:PAIR] = y[:, 3 * PAIR : 4 * PAIR].astype(bf16)
    v_ref[rows, PAIR : 2 * PAIR] = both.astype(bf16)
    z = (dot_nt(wq_ref[...], x) + bq_ref[...]).astype(bf16)
    q_ref[:, rows] = (z.astype(f32) * HEAD_DIM ** -0.5).astype(bf16)
    row = lax.broadcasted_iota(jnp.int32, (BLOCK, n), 0)
    mask_ref[:, rows] = jnp.where((row <= 16) & (row != seg), MASKED, 0.0).astype(bf16)


def forward_kernel(heads, chunks, tab_ref, gl_ref, *refs):
    x_refs = refs[0:chunks]
    (seg_ref, wkv_ref, bkv_ref, wq_ref, bq_ref, out_ref, lse_ref, lseg_ref, k_sc, v_sc, q_sc, mask_sc, s_sc) = refs[chunks:]
    rows = x_refs[0].shape[0]
    length = rows * chunks
    npairs = length // PAIR
    per_chunk = npairs // chunks
    tile = 256
    for c in range(chunks):

        @pl.loop(0, rows // tile)
        def _(t):
            at = pl.multiple_of(t * tile, tile)
            project_rows(
                x_refs[c][pl.ds(at, tile), :], seg_ref[c : c + 1, pl.ds(at, tile)], wkv_ref, bkv_ref, wq_ref, bq_ref,
                k_sc, v_sc, q_sc, mask_sc, pl.multiple_of(c * rows + t * tile, tile),
            )

    null_lane = lax.broadcasted_iota(jnp.int32, (BLOCK, heads * PAIR), 1) % PAIR
    k_sc[pl.ds(length, BLOCK), :] = (null_lane == BLOCK + 16).astype(f32).astype(bf16)
    v_sc[pl.ds(length, BLOCK), :] = jnp.zeros((BLOCK, 2 * PAIR), bf16)
    first, second = lane_halves(PAIR, bf16)
    lane = lax.broadcasted_iota(jnp.int32, (1, PAIR), 1)

    @pl.loop(0, npairs)
    def _(pair):
        chunk = pair // per_chunk
        local = pl.multiple_of((pair % per_chunk) * PAIR, PAIR)
        at = pl.multiple_of(pair * PAIR, PAIR)
        for h in range(heads):
            shared, mine, other = slots(tab_ref, gl_ref, h, pair, npairs)
            kl, vl, off = key_lanes(h), value_lanes(h), VALUE_ROW[h]
            q = query_columns(q_sc, mask_sc, h, at)
            s_sh = dot_nn(stack_rows(k_sc, shared, kl), q)
            k_pr = jnp.concatenate([stack_rows(k_sc, mine, kl), stack_rows(k_sc, other, kl)], axis=1)
            s_pr = dot_nn(k_pr, jnp.concatenate([q * first, q * second], axis=0))
            peak = jnp.maximum(jnp.max(s_sh, axis=0, keepdims=True), jnp.max(s_pr, axis=0, keepdims=True))
            e_sh = jnp.exp(s_sh - peak)
            e_pr = jnp.exp(s_pr - peak)
            total = jnp.sum(e_sh, axis=0, keepdims=True) + jnp.sum(e_pr, axis=0, keepdims=True)
            inv = 1.0 / total
            p_sh = (e_sh * inv).astype(bf16)
            p_pr = (e_pr * inv).astype(bf16)
            v_pr = jnp.concatenate([stack_rows(v_sc, mine, vl), stack_rows(v_sc, other, vl)], axis=1)
            o_sh = dot_tn(stack_rows(v_sc, shared, vl), p_sh)
            o_pr = dot_tn(v_pr, p_pr)
            ctx = o_sh[off : off + BLOCK] + jnp.where(
                lane < BLOCK, o_pr[off : off + BLOCK], o_pr[PAIR + off : PAIR + off + BLOCK]
            )
            out_ref[chunk, h * BLOCK : (h + 1) * BLOCK, pl.ds(local, PAIR)] = ctx.astype(bf16)
            lse_ref[h, pl.ds(pair, 1), :] = peak + jnp.log(total)

    step = 512
    for h in range(heads):
        kl, vl, off = key_lanes(h), value_lanes(h), VALUE_ROW[h]
        q = global_queries(q_sc, mask_sc, h, gl_ref)

        def score(c, peak):
            at = pl.multiple_of(c * step, step)
            s = dot_nn(k_sc[pl.ds(at, step), kl], q)
            s_sc[pl.ds(at, step), :] = s
            return jnp.maximum(peak, jnp.max(s, axis=0, keepdims=True))

        peak = lax.fori_loop(0, length // step, score, jnp.full((1, PAIR), MASKED, f32))

        def gather(c, carry):
            total, ctx = carry
            at = pl.multiple_of(c * step, step)
            e = jnp.exp(s_sc[pl.ds(at, step), :] - peak)
            ctx = ctx + dot_tn(v_sc[pl.ds(at, step), vl], e.astype(bf16))
            return total + jnp.sum(e, axis=0, keepdims=True), ctx

        total, ctx = lax.fori_loop(
            0, length // step, gather, (jnp.zeros((1, PAIR), f32), jnp.zeros((PAIR, PAIR), f32))
        )
        ctx = ctx[off : off + BLOCK] * (1.0 / total)
        put_global_columns(out_ref, slice(h * BLOCK, (h + 1) * BLOCK), gl_ref, ctx, per_chunk)
        lseg_ref[h : h + 1, :] = peak + jnp.log(total)


def attention_forward(tab, gl, x, seg, w_kv, b_kv, w_q, b_q):
    chunks = len(x)
    rows = x[0].shape[0]
    length = rows * chunks
    heads = w_q.shape[0] // HEAD_DIM
    whole = lambda: pl.BlockSpec(memory_space=pltpu.VMEM)
    return pl.pallas_call(
        functools.partial(forward_kernel, heads, chunks),
        out_shape=(
            jax.ShapeDtypeStruct((chunks, heads * HEAD_DIM, rows), bf16),
            jax.ShapeDtypeStruct((heads, length // PAIR, PAIR), f32),
            jax.ShapeDtypeStruct((heads, PAIR), f32),
            jax.ShapeDtypeStruct((length + BLOCK, heads * PAIR), bf16),
            jax.ShapeDtypeStruct((length + BLOCK, 2 * PAIR), bf16),
            jax.ShapeDtypeStruct((heads * HEAD_DIM, length), bf16),
            jax.ShapeDtypeStruct((BLOCK, length), bf16),
        ),
        in_specs=[pl.BlockSpec(memory_space=pltpu.SMEM)] * 2 + [whole() for _ in range(chunks + 5)],
        out_specs=tuple(whole() for _ in range(7)),
        scratch_shapes=[pltpu.VMEM((length, PAIR), f32)],
        compiler_params=pltpu.CompilerParams(vmem_limit_bytes=56 << 20),
        cost_estimate=pl.CostEstimate(flops=12_000_000_000, bytes_accessed=16_000_000, transcendentals=8_000_000),
        name="attention_forward",
    )(tab, gl, *x, seg, w_kv, b_kv, w_q, b_q)


def backward_kernel(heads, chunks, tab_ref, gl_ref, *refs):
    do_refs = refs[:chunks]
    (k_sc, v_sc, q_sc, mask_sc, lse_ref, lseg_ref, wq_ref, wkv_ref, dq_ref, dkv_ref, first_ref, part_ref,
     do_sc, acc, p_sc, d_sc, dqg_sc) = refs[chunks:]
    rows = do_refs[0].shape[1]
    length = rows * chunks
    npairs = length // PAIR
    per_chunk = npairs // chunks
    for c in range(chunks):
        do_sc[:, c * rows : (c + 1) * rows] = do_refs[c][...]
    first, second = lane_halves(PAIR, bf16)
    first2, second2 = lane_halves(2 * PAIR, bf16)
    ffirst, fsecond = lane_halves(PAIR, f32)
    lane = lax.broadcasted_iota(jnp.int32, (1, PAIR), 1)
    zeros = jnp.zeros((BLOCK, PAIR), bf16)

    def value_rows(do, h):
        return jnp.concatenate([zeros, do] if VALUE_ROW[h] else [do, zeros], axis=0)

    def sources(q, do):
        top = jnp.concatenate([q[0:BLOCK], zeros], axis=1)
        return jnp.concatenate([top, jnp.concatenate([zeros, do], axis=1)], axis=0)

    step = 512
    for h in range(heads):
        kl, vl = key_lanes(h), value_lanes(h)
        q = global_queries(q_sc, mask_sc, h, gl_ref)
        do = global_columns(do_sc, slice(h * BLOCK, (h + 1) * BLOCK), gl_ref).astype(bf16)
        do_v = value_rows(do, h)
        lse = lseg_ref[h : h + 1, :]
        src = sources(q, do)

        def weigh(c, delta):
            at = pl.multiple_of(c * step, step)
            p = jnp.exp(dot_nn(k_sc[pl.ds(at, step), kl], q) - lse)
            dp = dot_nn(v_sc[pl.ds(at, step), vl], do_v)
            p_sc[pl.ds(at, step), :] = p
            d_sc[pl.ds(at, step), :] = dp
            return delta + jnp.sum(p * dp, axis=0, keepdims=True)

        delta = lax.fori_loop(0, length // step, weigh, jnp.zeros((1, PAIR), f32))

        def spread(c, dq):
            at = pl.multiple_of(c * step, step)
            p = p_sc[pl.ds(at, step), :]
            ds = (p * (d_sc[pl.ds(at, step), :] - delta)).astype(bf16)
            both = jnp.concatenate([ds, p.astype(bf16)], axis=1)
            acc[h, pl.ds(at, step), :] = dot_nt(both, src)
            return dq + dot_tn(k_sc[pl.ds(at, step), kl], ds)

        dq = lax.fori_loop(0, length // step, spread, jnp.zeros((PAIR, PAIR), f32))
        dqg_sc[h] = dq[0:BLOCK] * (HEAD_DIM ** -0.5)
        acc[h, pl.ds(length, BLOCK), :] = jnp.zeros((BLOCK, PAIR), f32)

    @pl.loop(0, npairs)
    def _(pair):
        chunk = pair // per_chunk
        local = pl.multiple_of((pair % per_chunk) * PAIR, PAIR)
        at = pl.multiple_of(pair * PAIR, PAIR)
        hit_first = (gl_ref[0] == 2 * pair) | (gl_ref[1] == 2 * pair)
        hit_second = (gl_ref[0] == 2 * pair + 1) | (gl_ref[1] == 2 * pair + 1)
        shut = ffirst * jnp.where(hit_first, -MASKED, 0.0) + fsecond * jnp.where(hit_second, -MASKED, 0.0)
        for h in range(heads):
            shared, mine, other = slots(tab_ref, gl_ref, h, pair, npairs)
            kl, vl = key_lanes(h), value_lanes(h)
            q = query_columns(q_sc, mask_sc, h, at)
            do = do_sc[h * BLOCK : (h + 1) * BLOCK, pl.ds(at, PAIR)]
            do_v = value_rows(do, h)
            lse = lse_ref[h, pl.ds(pair, 1), :] + shut
            k_sh = stack_rows(k_sc, shared, kl)
            k_pr = jnp.concatenate([stack_rows(k_sc, mine, kl), stack_rows(k_sc, other, kl)], axis=1)
            p_sh = jnp.exp(dot_nn(k_sh, q) - lse)
            p_pr = jnp.exp(dot_nn(k_pr, jnp.concatenate([q * first, q * second], axis=0)) - lse)
            d_sh = dot_nn(stack_rows(v_sc, shared, vl), do_v)
            v_pr = jnp.concatenate([stack_rows(v_sc, mine, vl), stack_rows(v_sc, other, vl)], axis=1)
            d_pr = dot_nn(v_pr, jnp.concatenate([do_v * first, do_v * second], axis=0))
            delta = jnp.sum(p_sh * d_sh, axis=0, keepdims=True) + jnp.sum(p_pr * d_pr, axis=0, keepdims=True)
            ds_sh = (p_sh * (d_sh - delta)).astype(bf16)
            ds_pr = (p_pr * (d_pr - delta)).astype(bf16)
            src = sources(q, do)
            g_sh = dot_nt(jnp.concatenate([ds_sh, p_sh.astype(bf16)], axis=1), src)
            src2 = jnp.concatenate([src * first2, src * second2], axis=0)
            g_pr = dot_nt(jnp.concatenate([ds_pr, p_pr.astype(bf16)], axis=1), src2)
            for j, o in enumerate(shared):
                acc[h, pl.ds(o, BLOCK), :] += g_sh[j * BLOCK : (j + 1) * BLOCK]
            for j, o in enumerate(mine):
                acc[h, pl.ds(o, BLOCK), :] += g_pr[j * BLOCK : (j + 1) * BLOCK, 0:PAIR]
            for j, o in enumerate(other):
                acc[h, pl.ds(o, BLOCK), :] += g_pr[j * BLOCK : (j + 1) * BLOCK, PAIR:]
            t_sh = dot_tn(k_sh, ds_sh)
            t_pr = dot_tn(k_pr, ds_pr)
            dq = t_sh[0:BLOCK] + jnp.where(lane < BLOCK, t_pr[0:BLOCK], t_pr[PAIR : PAIR + BLOCK])
            dq_ref[chunk, h * BLOCK : (h + 1) * BLOCK, pl.ds(local, PAIR)] = (dq * (HEAD_DIM ** -0.5)).astype(bf16)

    for h in range(heads):
        put_global_columns(dq_ref, slice(h * BLOCK, (h + 1) * BLOCK), gl_ref, dqg_sc[h], per_chunk)
        for c in range(chunks):
            dkv_ref[c, :, h * PAIR : (h + 1) * PAIR] = acc[h, pl.ds(c * rows, rows), :].astype(bf16)
    tile = 256
    for c in range(chunks):

        @pl.loop(0, rows // tile)
        def _(t):
            at = pl.multiple_of(t * tile, tile)
            got = dot_tn(dq_ref[c, :, pl.ds(at, tile)], wq_ref[...]) + dot_nn(dkv_ref[c, pl.ds(at, tile), :], wkv_ref[...])
            if c == 0:
                first_ref[pl.ds(at, tile), :] = got
            else:
                part_ref[c - 1, pl.ds(at, tile), :] = got.astype(bf16)


def attention_backward(tab, gl, do, k, v, q, mask, lse, lseg, w_q, w_kv):
    chunks = len(do)
    group, rows = do[0].shape
    heads = group // HEAD_DIM
    width = w_q.shape[1]
    length = rows * chunks
    whole = lambda: pl.BlockSpec(memory_space=pltpu.VMEM)
    return pl.pallas_call(
        functools.partial(backward_kernel, heads, chunks),
        out_shape=(
            jax.ShapeDtypeStruct((chunks, group, rows), bf16),
            jax.ShapeDtypeStruct((chunks, rows, heads * PAIR), bf16),
            jax.ShapeDtypeStruct((rows, width), f32),
            jax.ShapeDtypeStruct((chunks - 1, rows, width), bf16),
        ),
        in_specs=[pl.BlockSpec(memory_space=pltpu.SMEM)] * 2 + [whole() for _ in range(chunks + 8)],
        out_specs=tuple(whole() for _ in range(4)),
        scratch_shapes=[
            pltpu.VMEM((group, length), bf16),
            pltpu.VMEM((heads, length + BLOCK, PAIR), f32),
            pltpu.VMEM((length, PAIR), f32),
            pltpu.VMEM((length, PAIR), f32),
            pltpu.VMEM((heads, BLOCK, PAIR), f32),
        ],
        compiler_params=pltpu.CompilerParams(vmem_limit_bytes=60 << 20),
        cost_estimate=pl.CostEstimate(flops=30_000_000_000, bytes_accessed=24_000_000, transcendentals=8_000_000),
        name="attention_backward",
    )(tab, gl, *do, k, v, q, mask, lse, lseg, w_q, w_kv)


def weights_kernel(chunks, *refs):
    x_refs = refs[:chunks]
    dq_ref, dkv_ref, gw_ref, sq_ref, skv_ref, acc = refs[chunks:]
    group = dq_ref.shape[1]
    total_q = jnp.zeros((group, 1), f32)
    total_kv = jnp.zeros((1, dkv_ref.shape[2]), f32)
    for c in range(chunks):
        x = x_refs[c][...]
        got_q = dot_nn(dq_ref[c], x)
        got_kv = dot_tn(dkv_ref[c], x)
        if c == 0:
            acc[0:group, :] = got_q
            acc[group:, :] = got_kv
        else:
            acc[0:group, :] += got_q
            acc[group:, :] += got_kv
        total_q = total_q + jnp.sum(dq_ref[c].astype(f32), axis=1, keepdims=True)
        total_kv = total_kv + jnp.sum(dkv_ref[c].astype(f32), axis=0, keepdims=True)
    gw_ref[...] = jnp.transpose(acc[...], (1, 0)).astype(bf16)
    sq_ref[...] = total_q
    skv_ref[...] = total_kv


def projection_gradients(x, dq, dkv):
    chunks, group, rows = dq.shape
    width = x[0].shape[1]
    lanes = dkv.shape[2]
    whole = lambda: pl.BlockSpec(memory_space=pltpu.VMEM)
    return pl.pallas_call(
        functools.partial(weights_kernel, chunks),
        out_shape=(
            jax.ShapeDtypeStruct((width, group + lanes), bf16),
            jax.ShapeDtypeStruct((group, 1), f32),
            jax.ShapeDtypeStruct((1, lanes), f32),
        ),
        in_specs=[whole() for _ in range(chunks + 2)],
        out_specs=tuple(whole() for _ in range(3)),
        scratch_shapes=[pltpu.VMEM((group + lanes, width), f32)],
        compiler_params=pltpu.CompilerParams(vmem_limit_bytes=40 << 20),
        cost_estimate=pl.CostEstimate(flops=4_000_000_000, bytes_accessed=12_000_000, transcendentals=0),
        name="projection_gradients",
    )(*x, dq, dkv)


NORM_EPS = 1e-12


def transposed(value):
    return jnp.transpose(value.astype(f32), (1, 0)).astype(bf16)


def unit_rows(value):
    center = value - jnp.mean(value, axis=-1, keepdims=True)
    scale = lax.rsqrt(jnp.mean(center * center, axis=-1, keepdims=True) + NORM_EPS)
    return center * scale, scale


def unit_rows_back(grad, unit, scale):
    return scale * (
        grad - jnp.mean(grad, axis=-1, keepdims=True) - unit * jnp.mean(grad * unit, axis=-1, keepdims=True)
    )


def rows_kernel(parts, blocks, up_rows, me_ref, *refs):
    ctx_refs = refs[:parts]
    (x_ref, cot_ref, rest_ref, wo_ref, vec_ref, bup_ref, out_ref, resid_ref, hid_ref, pre_ref, nlt_ref, gft_ref,
     gb_ref, do_ref, sums_ref, gbup_ref, slope_sc) = refs[parts:]
    group = ctx_refs[0].shape[0]
    width = x_ref.shape[1]

    def up(f):
        return rest_ref[:, f, 0:up_rows, :].reshape(width, rest_ref.shape[3])

    def down(f):
        return rest_ref[:, f, up_rows : 2 * up_rows, :].reshape(width, rest_ref.shape[3])

    def own_rows(k):
        return pl.ds(pl.multiple_of((me_ref[0] ^ k) * group, group), group)

    @pl.when(pl.program_id(0) == 0)
    def _():
        sums_ref[...] = jnp.zeros_like(sums_ref)
        gbup_ref[...] = jnp.zeros_like(gbup_ref)

    ctx = jnp.concatenate([r[...] for r in ctx_refs], axis=0)
    w_o = jnp.concatenate([wo_ref[own_rows(k), :] for k in range(parts)], axis=0)
    resid_one = x_ref[...].astype(f32) + (dot_tn(ctx, w_o) + vec_ref[0:1, :])
    unit_one, scale_one = unit_rows(resid_one)
    normed_one = unit_one * vec_ref[2:3, :] + vec_ref[3:4, :]
    low = normed_one.astype(bf16)
    nlt_ref[...] = transposed(normed_one)
    total = normed_one + vec_ref[1:2, :]
    pre = dot_nn(low, up(0)) + bup_ref[0:1, :]
    for f in range(blocks):
        later = dot_nn(low, up(f + 1)) + bup_ref[f + 1 : f + 2, :] if f + 1 < blocks else None
        phi = 0.5 + 0.5 * lax.erf(pre * (0.5 ** 0.5))
        slope_sc[f] = phi + pre * (jnp.exp(-0.5 * pre * pre) * 0.3989422804014327)
        hid = (pre * phi).astype(bf16)
        hid_ref[f] = hid
        total = total + dot_nt(hid, down(f))
        pre = later
    unit_two, scale_two = unit_rows(total)
    out_ref[...] = (unit_two * vec_ref[4:5, :] + vec_ref[5:6, :]).astype(bf16)
    cot = cot_ref[...].astype(f32)
    grad_two = unit_rows_back(cot * vec_ref[4:5, :], unit_two, scale_two)
    grad_ffn = grad_two.astype(bf16)
    gft_ref[...] = transposed(grad_two)
    grad_normed = grad_two
    back = dot_nn(grad_ffn, down(0))
    for f in range(blocks):
        later = dot_nn(grad_ffn, down(f + 1)) if f + 1 < blocks else None
        grad_pre = (back * slope_sc[f]).astype(bf16)
        pre_ref[f] = grad_pre
        gbup_ref[f : f + 1, :] += jnp.sum(grad_pre.astype(f32), axis=0, keepdims=True)
        grad_normed = grad_normed + dot_nt(grad_pre, up(f))
        back = later
    resid = unit_rows_back(grad_normed * vec_ref[2:3, :], unit_one, scale_one)
    resid_ref[...] = resid
    branch = resid.astype(bf16)
    gb_ref[...] = branch
    do = dot_nt(w_o, branch).astype(bf16)
    for k in range(parts):
        do_ref[k] = do[k * group : (k + 1) * group]
    for row, value in enumerate(
        (branch.astype(f32), grad_ffn.astype(f32), grad_normed * unit_one, grad_normed, cot * unit_two, cot)
    ):
        sums_ref[row : row + 1, :] += jnp.sum(value, axis=0, keepdims=True)


def rows_chain(me, ctx_parts, x, cot, rest, up_rows, w_o, vecs, bias_up):
    parts = len(ctx_parts)
    group, rows = ctx_parts[0].shape
    width = x.shape[1]
    outer, blocks, per, hidden = rest.shape
    tile = 256
    once = lambda shape: pl.BlockSpec(shape, lambda i: (0,) * len(shape), pipeline_mode=pl.Buffered(1))
    tall = pl.BlockSpec((tile, width), lambda i: (i, 0))
    wide = pl.BlockSpec((width, tile), lambda i: (0, i))
    cube = pl.BlockSpec((blocks, tile, hidden), lambda i: (0, i, 0))
    return pl.pallas_call(
        functools.partial(rows_kernel, parts, blocks, up_rows),
        grid=(rows // tile,),
        out_shape=(
            jax.ShapeDtypeStruct((rows, width), bf16),
            jax.ShapeDtypeStruct((rows, width), f32),
            jax.ShapeDtypeStruct((blocks, rows, hidden), bf16),
            jax.ShapeDtypeStruct((blocks, rows, hidden), bf16),
            jax.ShapeDtypeStruct((width, rows), bf16),
            jax.ShapeDtypeStruct((width, rows), bf16),
            jax.ShapeDtypeStruct((rows, width), bf16),
            jax.ShapeDtypeStruct((parts, group, rows), bf16),
            jax.ShapeDtypeStruct((8, width), f32),
            jax.ShapeDtypeStruct((8, hidden), f32),
        ),
        in_specs=[pl.BlockSpec(memory_space=pltpu.SMEM)]
        + [pl.BlockSpec((group, tile), lambda i: (0, i))] * parts
        + [tall, tall, once(rest.shape), once(w_o.shape), once(vecs.shape), once(bias_up.shape)],
        out_specs=(
            tall, tall, cube, cube, wide, wide, tall, pl.BlockSpec((parts, group, tile), lambda i: (0, 0, i)),
            pl.BlockSpec((8, width), lambda i: (0, 0)), pl.BlockSpec((8, hidden), lambda i: (0, 0)),
        ),
        scratch_shapes=[pltpu.VMEM((blocks, tile, hidden), f32)],
        compiler_params=pltpu.CompilerParams(vmem_limit_bytes=60 << 20),
        cost_estimate=pl.CostEstimate(flops=22_000_000_000, bytes_accessed=40_000_000, transcendentals=6_000_000),
        name="rows_chain",
    )(me, *ctx_parts, x, cot, rest, w_o, vecs, bias_up)


def outer_kernel(up_rows, small_rows, nlt_ref, gft_ref, pre_ref, hid_ref, small_ref, out_ref):
    slabs, hidden = out_ref.shape[0], out_ref.shape[3]
    up = dot_nn(nlt_ref[...], pre_ref[0]).astype(bf16)
    out_ref[:, 0, 0:up_rows, :] = up.reshape(slabs, up_rows, hidden)
    down = dot_nn(gft_ref[...], hid_ref[0]).astype(bf16)
    out_ref[:, 0, up_rows : 2 * up_rows, :] = down.reshape(slabs, up_rows, hidden)
    if small_rows:
        out_ref[:, 0, 2 * up_rows :, :] = small_ref[:, 0]


def outer_products(nlt, gft, pre, hid, small, slabs, up_rows):
    blocks, rows, hidden = pre.shape
    width = nlt.shape[0]
    small_rows = small.shape[2] if slabs == small.shape[0] else 0
    per = 2 * up_rows + small_rows
    once = lambda shape: pl.BlockSpec(shape, lambda i: (0,) * len(shape), pipeline_mode=pl.Buffered(1))
    return pl.pallas_call(
        functools.partial(outer_kernel, up_rows, small_rows),
        grid=(blocks,),
        out_shape=jax.ShapeDtypeStruct((slabs, blocks, per, hidden), bf16),
        in_specs=[
            once(nlt.shape),
            once(gft.shape),
            pl.BlockSpec((1, rows, hidden), lambda i: (i, 0, 0)),
            pl.BlockSpec((1, rows, hidden), lambda i: (i, 0, 0)),
            pl.BlockSpec((small.shape[0], 1) + small.shape[2:], lambda i: (0, i, 0, 0)),
        ],
        out_specs=pl.BlockSpec((slabs, 1, per, hidden), lambda i: (0, i, 0, 0)),
        compiler_params=pltpu.CompilerParams(vmem_limit_bytes=48 << 20),
        cost_estimate=pl.CostEstimate(flops=10_000_000_000, bytes_accessed=28_000_000, transcendentals=0),
        name="outer_products",
    )(nlt, gft, pre, hid, small)


ALL = ("dp", "seq", "ffn")


def flip_send(array, axis, bits):
    count = lax.axis_size(axis)
    return lax.ppermute(array, axis, [(i, i ^ bits) for i in range(count)])


def bits_of(axis):
    return lax.axis_size(axis).bit_length() - 1


def gather_doubling(array, axis):
    index = lax.axis_index(axis)
    size = lax.axis_size(axis)
    shape = array.shape
    bits = bits_of(axis)
    for place, bit in enumerate(reversed(range(bits))):
        other = flip_send(array, axis, 1 << bit)
        mine_second = ((index >> bit) & 1) == 1
        array = jnp.where(mine_second, jnp.stack([other, array], axis=place), jnp.stack([array, other], axis=place))
    return array.reshape((size,) + shape)


def scatter_halving(array, axis, dim):
    index = lax.axis_index(axis)
    for bit in range(bits_of(axis)):
        shape = array.shape
        array = array.reshape(shape[:dim] + (shape[dim] // 2, 2) + shape[dim + 1 :])
        mine = (index >> bit) & 1
        keep = lax.dynamic_index_in_dim(array, mine, dim + 1, keepdims=False)
        send = lax.dynamic_index_in_dim(array, 1 - mine, dim + 1, keepdims=False)
        array = keep + flip_send(send, axis, 1 << bit)
    return array.reshape(array.shape[:dim] + array.shape[dim + 1 :])


def shards(
    tokens, w_query, w_key, w_value, w_output, b_query, b_value, b_output, w_up, b_up, w_down, b_down,
    gain_attn, shift_attn, gain_ffn, shift_ffn, segment_ids, random_blocks, global_blocks, cotangent,
):
    seq_n, dp_n, ffn_n = lax.axis_size("seq"), lax.axis_size("dp"), lax.axis_size("ffn")
    outer = dp_n * seq_n
    me = lax.axis_index("seq")
    own, width = w_query.shape
    group = width // seq_n
    heads = group // HEAD_DIM
    features = tokens[0]
    rows = features.shape[0]
    relative = [me ^ k for k in range(seq_n)]

    def by_group(w):
        return w.reshape(own, seq_n, group).transpose(1, 0, 2)

    note = jnp.pad(jnp.stack([b_query, b_value]), ((0, 0), (0, 3 * group - own)))
    pack = jnp.concatenate([by_group(w_query), by_group(w_key), by_group(w_value)], axis=2)
    pack = jnp.concatenate([pack, jnp.broadcast_to(note[None], (seq_n,) + note.shape)], axis=1)
    got = [lax.dynamic_index_in_dim(pack, relative[k], keepdims=False) for k in range(seq_n)]
    got = [got[0]] + [flip_send(got[k], "seq", k) for k in range(1, seq_n)]
    got, features = lax.optimization_barrier((got, features))

    near = [features] + [None] * (seq_n - 1)
    for k in sorted(range(1, seq_n), key=lambda k: (k & (k - 1), -k)):
        bit = k & -k
        near[k] = flip_send(features if bit == k else near[k ^ bit], "seq", bit)

    pack = gather_doubling(gather_doubling(jnp.stack(got), "ffn"), "dp")
    order = jnp.stack(relative)
    pack = pack[:, :, order].transpose(0, 2, 1, 3, 4)
    w_own = pack[:, :, :, :own].reshape(width, 3 * group)
    biases = lax.dynamic_slice(
        pack[:, :, :, own:, :own].transpose(3, 0, 1, 2, 4).reshape(2, width), (0, me * group), (2, group)
    ).astype(f32)
    blank = jnp.zeros((width, HEAD_DIM), bf16)
    part_of = lambda i, h: w_own[:, i * group + h * HEAD_DIM : i * group + (h + 1) * HEAD_DIM]
    w_kv = jnp.concatenate(
        [part_of(1, 0), blank, part_of(1, 1), blank, part_of(1, 2), part_of(2, 2), part_of(2, 0), part_of(2, 1)], axis=1
    )
    b_value_own = biases[1].reshape(heads, HEAD_DIM)
    b_kv = jnp.concatenate([jnp.zeros((5 * HEAD_DIM,), f32), b_value_own[2], b_value_own[0], b_value_own[1]])[None]
    w_q_t = w_own[:, :group].T
    w_kv_t = jnp.concatenate([part_of(i, h) for h in range(heads) for i in (1, 2)], axis=1).T
    seg = segment_ids[0].reshape(seq_n, rows)[order]

    vectors = jnp.stack([b_output, b_down, gain_attn, shift_attn, gain_ffn, shift_ffn])
    vectors = jnp.pad(vectors, ((0, 0), (0, width - own)))
    rest = jnp.concatenate([w_up, w_down, w_output, b_up[None], vectors], axis=0)
    up_rows = w_up.shape[0]
    rest = lax.all_gather(rest, ALL, axis=0, tiled=False).reshape(outer, ffn_n, rest.shape[0], width)
    at = 2 * up_rows
    w_o = rest[:, :, at : at + own].reshape(width, width)
    bias_up = rest[0, :, at + own].astype(f32)
    vecs = rest[:, :, at + own + 1 :, :own].transpose(2, 0, 1, 3).reshape(6, width).astype(f32)
    direct = up_rows % 16 == 0
    if not direct:
        rest = rest[:, :, :at].reshape(outer, ffn_n, 2, up_rows, width).transpose(1, 2, 0, 3, 4)
        rest = rest.reshape(1, ffn_n, 2 * outer * up_rows, width)
    slabs, slab_rows = (outer, up_rows) if direct else (1, outer * up_rows)

    nblocks = seq_n * rows // BLOCK
    flip = me.astype(jnp.int32) * (nblocks // seq_n)
    tab = pair_table(random_blocks[0], global_blocks[0], flip, nblocks)
    gl = global_blocks[0] ^ flip
    ctx, lse, lseg, k_all, v_all, q_all, mask_all = attention_forward(
        tab, gl, near, seg, w_kv, b_kv, w_q_t, biases[0][:, None]
    )
    ctx_parts = [ctx[0]] + [flip_send(ctx[k], "seq", k) for k in range(1, seq_n)]

    (out, grad_resid_one, hidden, grad_pre, normed_t, grad_ffn_t, grad_branch, grad_ctx, sums, grad_bias_up) = rows_chain(
        me.astype(jnp.int32)[None], ctx_parts, features, cotangent[0], rest, slab_rows, w_o,
        jnp.pad(vecs, ((0, 2), (0, 0))), bias_up,
    )
    do = [grad_ctx[0]] + [flip_send(grad_ctx[k], "seq", k) for k in range(1, seq_n)]

    grad_out = dot_nn(jnp.concatenate(ctx_parts, axis=0), grad_branch).astype(bf16)
    grad_out = grad_out.reshape(seq_n, group, width)[order].reshape(outer, ffn_n, own, width)
    vec_grads = sums[:6].astype(bf16).reshape(6, outer, ffn_n, own).transpose(1, 2, 0, 3)
    vec_grads = jnp.pad(vec_grads, ((0, 0), (0, 0), (0, 25 - own), (0, width - own)))
    small = jnp.concatenate(
        [
            grad_out,
            jnp.broadcast_to(grad_bias_up[None, :ffn_n, None].astype(bf16), (outer, ffn_n, 1, width)),
            vec_grads,
        ],
        axis=2,
    )
    payload = outer_products(normed_t, grad_ffn_t, grad_pre, hidden, small, slabs, slab_rows)
    if not direct:
        payload = payload.reshape(ffn_n, 2, outer, up_rows, width).transpose(2, 0, 1, 3, 4)
        payload = jnp.concatenate([payload.reshape(outer, ffn_n, at, width), small], axis=2)
        payload = jnp.pad(payload, ((0, 0), (0, 0), (0, -payload.shape[2] % 32), (0, 0)))
    payload, do = lax.optimization_barrier((payload, do))
    per = payload.shape[2]
    total = lax.psum_scatter(payload.reshape(-1, width), ALL, scatter_dimension=0, tiled=True).astype(f32)
    out_up, out_down, out_output = total[:up_rows], total[up_rows:at], total[at : at + own]
    out_bias_up = total[at + own]
    out_vecs = total[at + own + 1 : at + own + 7, :own]

    dq, dkv, part_first, parts = attention_backward(
        tab, gl, do, k_all, v_all, q_all, mask_all, lse, lseg, w_q_t, w_kv_t
    )
    part = [None] + [parts[k - 1] for k in range(1, seq_n)]
    grad_features = grad_resid_one + part_first
    bit = 1
    while bit < seq_n:
        for k in range(seq_n):
            if k & -k == bit and k != bit:
                came = flip_send(part[k], "seq", bit).astype(f32)
                part[k ^ bit] = (part[k ^ bit].astype(f32) + came).astype(bf16)
        bit *= 2
    bit = seq_n // 2
    while bit:
        grad_features = grad_features + flip_send(part[bit], "seq", bit).astype(f32)
        bit //= 2

    grad_w, sum_q, sum_kv = projection_gradients(near, dq, dkv)
    sum_v = sum_kv.reshape(heads, 2, HEAD_DIM)[:, 1].reshape(group)
    sum_b = lax.dynamic_update_slice(jnp.zeros((2, width), f32), jnp.stack([sum_q[:, 0], sum_v]), (0, me * group))
    sum_b = sum_b.astype(bf16).reshape(2, dp_n, seq_n, ffn_n, own).transpose(1, 2, 3, 0, 4)
    sum_b = jnp.pad(sum_b, ((0, 0),) * 3 + ((0, 30 - own), (0, 3 * group - own)))
    grad_w = jnp.concatenate([grad_w.reshape(dp_n, seq_n, ffn_n, own, 3 * group), sum_b], axis=3)
    grad_w = scatter_halving(scatter_halving(grad_w, "dp", 0), "ffn", 1)
    sent = [lax.dynamic_index_in_dim(grad_w, relative[k], keepdims=False) for k in range(seq_n)]
    sent = [sent[0]] + [flip_send(sent[k], "seq", k) for k in range(1, seq_n)]
    grad_w = jnp.stack(sent)[order].astype(f32)
    out_query = grad_w[:, :own, :group].transpose(1, 0, 2).reshape(own, width)
    pairs = grad_w[:, :own, group:].reshape(seq_n, own, heads, 2, HEAD_DIM).transpose(3, 1, 0, 2, 4)
    out_key, out_value = pairs[0].reshape(own, width), pairs[1].reshape(own, width)
    out_b = jnp.sum(grad_w[:, own : own + 2, :own], axis=0)
    return (
        out[None],
        grad_features[None],
        out_query,
        out_key,
        out_value,
        out_output,
        out_b[0],
        out_b[1],
        out_vecs[0],
        out_up,
        out_bias_up,
        out_down,
        out_vecs[1],
        out_vecs[2],
        out_vecs[3],
        out_vecs[4],
        out_vecs[5],
    )


def solution(mesh):
    return jax.shard_map(
        shards,
        mesh=mesh,
        in_specs=(
            P(("dp", "ffn"), "seq", None),
            P(("dp", "seq", "ffn"), None),
            P(("dp", "seq", "ffn"), None),
            P(("dp", "seq", "ffn"), None),
            P(("dp", "seq", "ffn"), None),
            P(("dp", "seq", "ffn")),
            P(("dp", "seq", "ffn")),
            P(("dp", "seq", "ffn")),
            P(("dp", "seq"), "ffn"),
            P("ffn"),
            P(("dp", "seq"), "ffn"),
            P(("dp", "seq", "ffn")),
            P(("dp", "seq", "ffn")),
            P(("dp", "seq", "ffn")),
            P(("dp", "seq", "ffn")),
            P(("dp", "seq", "ffn")),
            P(("dp", "ffn"), None),
            P(("dp", "ffn"), "seq", None, None),
            P(("dp", "ffn"), None),
            P(("dp", "ffn"), "seq", None),
        ),
        out_specs=(
            P(("dp", "ffn"), "seq", None),
            P(("dp", "ffn"), "seq", None),
            P(("dp", "seq", "ffn"), None),
            P(("dp", "seq", "ffn"), None),
            P(("dp", "seq", "ffn"), None),
            P(("dp", "seq", "ffn"), None),
            P(("dp", "seq", "ffn")),
            P(("dp", "seq", "ffn")),
            P(("dp", "seq", "ffn")),
            P(("dp", "seq"), "ffn"),
            P("ffn"),
            P(("dp", "seq"), "ffn"),
            P(("dp", "seq", "ffn")),
            P(("dp", "seq", "ffn")),
            P(("dp", "seq", "ffn")),
            P(("dp", "seq", "ffn")),
            P(("dp", "seq", "ffn")),
        ),
        check_vma=False,
    )
```

```python
import functools
import jax
import jax.numpy as jnp
from jax import lax
from jax.experimental import pallas as pl
from jax.sharding import PartitionSpec as P
from jax.experimental.pallas import tpu as pltpu

HEAD_DIM = 64
BLOCK = 64
PAIR = 2 * BLOCK
MASKED = -1e30
bf16 = jnp.bfloat16
f32 = jnp.float32


def dot_nn(a, b):
    return lax.dot_general(a, b, (((1,), (0,)), ((), ())), preferred_element_type=f32)


def dot_nt(a, b):
    return lax.dot_general(a, b, (((1,), (1,)), ((), ())), preferred_element_type=f32)


def dot_tn(a, b):
    return lax.dot_general(a, b, (((0,), (0,)), ((), ())), preferred_element_type=f32)


def pair_table(rand_local, global_ids, flip, nblocks):
    heads = rand_local.shape[0]
    null = nblocks
    first = (2 * jnp.arange(nblocks // 2, dtype=jnp.int32)) ^ flip

    def near(block):
        bad = (block < 0) | (block >= nblocks) | (block == global_ids[0]) | (block == global_ids[1])
        return jnp.where(bad, null, block ^ flip)

    rand_first = rand_local[:, first, :] ^ flip
    rand_second = rand_local[:, first + 1, :] ^ flip
    nears = jnp.stack([near(first), near(first + 1), near(first - 1), near(first + 2)], axis=1)
    nears = jnp.broadcast_to(nears[None], (heads,) + nears.shape)
    return jnp.concatenate(
        [nears[:, :, 0:3], rand_first, nears[:, :, 3:4], rand_second], axis=2
    ).astype(jnp.int32).reshape(-1)


def slots(tab_ref, gl_ref, head, pair, npairs):
    at = (head * npairs + pair) * 10
    got = [pl.multiple_of(tab_ref[at + j] * BLOCK, BLOCK) for j in range(10)]
    glob = [pl.multiple_of(gl_ref[j] * BLOCK, BLOCK) for j in range(2)]
    return got[0:2] + glob, got[2:6], got[6:10]


def stack_rows(ref, offsets, lanes):
    return jnp.concatenate([ref[pl.ds(o, BLOCK), lanes] for o in offsets], axis=0)


def lane_halves(width, dtype):
    lane = lax.broadcasted_iota(jnp.int32, (1, width), 1) % PAIR
    first = (lane < BLOCK).astype(dtype)
    second = (lane >= BLOCK).astype(dtype)
    return first, second


UNROLL = 4


def head_lanes(h):
    return slice(h * PAIR, (h + 1) * PAIR)


def query_columns(q_ref, mask_ref, h, at):
    return jnp.concatenate([q_ref[h * BLOCK : (h + 1) * BLOCK, pl.ds(at, PAIR)], mask_ref[:, pl.ds(at, PAIR)]], axis=0)


def global_queries(q_ref, mask_ref, h, gl_ref):
    return jnp.concatenate(
        [
            global_columns(q_ref, slice(h * BLOCK, (h + 1) * BLOCK), gl_ref),
            global_columns(mask_ref, slice(0, BLOCK), gl_ref),
        ],
        axis=0,
    ).astype(bf16)


def global_columns(src_ref, rows, gl_ref):
    lane = lax.broadcasted_iota(jnp.int32, (1, PAIR), 1)
    parts = []
    for g in range(2):
        block = gl_ref[g]
        at = pl.multiple_of((block // 2) * PAIR, PAIR)
        both = src_ref[rows, pl.ds(at, PAIR)].astype(f32)
        moved = pltpu.roll(both, BLOCK, 1)
        parts.append(jnp.where(block % 2 == g, both, moved))
    return jnp.where(lane < BLOCK, parts[0], parts[1])


def put_global_columns(dst_ref, rows, gl_ref, value, per_chunk):
    lane = lax.broadcasted_iota(jnp.int32, (1, PAIR), 1)
    moved = pltpu.roll(value, BLOCK, 1)
    for g in range(2):
        block = gl_ref[g]
        pair = block // 2
        half = block % 2
        chunk = pair // per_chunk
        at = pl.multiple_of((pair % per_chunk) * PAIR, PAIR)
        src = jnp.where(half == g, value, moved)
        old = dst_ref[chunk, rows, pl.ds(at, PAIR)].astype(f32)
        new = jnp.where((lane >= BLOCK) == (half == 1), src, old)
        dst_ref[chunk, rows, pl.ds(at, PAIR)] = new.astype(dst_ref.dtype)


def project_rows(x, seg, w_ref, wq, bkv_ref, bq_ref, k_ref, v_ref, q_ref, mask_ref, at):
    n = x.shape[0]
    lanes = v_ref.shape[1]
    y = dot_nn(x, w_ref[:, 0:lanes]) + bkv_ref[...]
    spot = lax.broadcasted_iota(jnp.int32, (PAIR, n), 0) - BLOCK
    mark = jnp.transpose((spot == seg).astype(f32), (1, 0))
    lane = lax.broadcasted_iota(jnp.int32, (1, PAIR), 1)
    rows = pl.ds(at, n)
    v_ref[rows, :] = y.astype(bf16)
    for h in range(lanes // PAIR):
        k_ref[rows, head_lanes(h)] = jnp.where(lane < BLOCK, y[:, head_lanes(h)], mark).astype(bf16)
    z = (dot_nt(wq, x) + bq_ref[...]).astype(bf16)
    q_ref[:, rows] = (z.astype(f32) * HEAD_DIM ** -0.5).astype(bf16)
    row = lax.broadcasted_iota(jnp.int32, (BLOCK, n), 0)
    mask_ref[:, rows] = jnp.where((row <= 16) & (row != seg), MASKED, 0.0).astype(bf16)


def query_weights(w_ref, heads):
    at = heads * PAIR
    cols = w_ref[:, at : at + 2 * PAIR].astype(f32)
    return jnp.transpose(cols, (1, 0))[0 : heads * HEAD_DIM].astype(bf16)


def forward_kernel(heads, chunks, tab_ref, gl_ref, *refs):
    x_refs = refs[0:chunks]
    seg_ref, w_ref, bkv_ref, bq_ref = refs[chunks : chunks + 4]
    out_refs = refs[chunks + 4 : 2 * chunks + 4]
    lse_ref, lseg_ref, k_sc, v_sc, q_sc, mask_sc, s_sc, out_ref = refs[2 * chunks + 4 :]
    rows = x_refs[0].shape[0]
    length = rows * chunks
    npairs = length // PAIR
    per_chunk = npairs // chunks
    tile = 256
    wq = query_weights(w_ref, heads)
    for c in range(chunks):

        @pl.loop(0, rows // tile)
        def _(t):
            at = pl.multiple_of(t * tile, tile)
            project_rows(
                x_refs[c][pl.ds(at, tile), :], seg_ref[c : c + 1, pl.ds(at, tile)], w_ref, wq, bkv_ref, bq_ref,
                k_sc, v_sc, q_sc, mask_sc, pl.multiple_of(c * rows + t * tile, tile),
            )

    null_lane = lax.broadcasted_iota(jnp.int32, (BLOCK, heads * PAIR), 1) % PAIR
    k_sc[pl.ds(length, BLOCK), :] = (null_lane == BLOCK + 16).astype(f32).astype(bf16)
    v_sc[pl.ds(length, BLOCK), :] = jnp.zeros((BLOCK, heads * PAIR), bf16)
    first, second = lane_halves(PAIR, bf16)
    lane = lax.broadcasted_iota(jnp.int32, (1, PAIR), 1)

    def one_pair(pair):
        chunk = pair // per_chunk
        local = pl.multiple_of((pair % per_chunk) * PAIR, PAIR)
        at = pl.multiple_of(pair * PAIR, PAIR)
        for h in range(heads):
            shared, mine, other = slots(tab_ref, gl_ref, h, pair, npairs)
            kl = head_lanes(h)
            q = query_columns(q_sc, mask_sc, h, at)
            s_sh = dot_nn(stack_rows(k_sc, shared, kl), q)
            k_pr = jnp.concatenate([stack_rows(k_sc, mine, kl), stack_rows(k_sc, other, kl)], axis=1)
            s_pr = dot_nn(k_pr, jnp.concatenate([q * first, q * second], axis=0))
            peak = jnp.maximum(jnp.max(s_sh, axis=0, keepdims=True), jnp.max(s_pr, axis=0, keepdims=True))
            e_sh = jnp.exp(s_sh - peak)
            e_pr = jnp.exp(s_pr - peak)
            total = jnp.sum(e_sh, axis=0, keepdims=True) + jnp.sum(e_pr, axis=0, keepdims=True)
            inv = 1.0 / total
            p_sh = (e_sh * inv).astype(bf16)
            p_pr = (e_pr * inv).astype(bf16)
            v_pr = jnp.concatenate([stack_rows(v_sc, mine, kl), stack_rows(v_sc, other, kl)], axis=1)
            o_sh = dot_tn(stack_rows(v_sc, shared, kl), p_sh)
            o_pr = dot_tn(v_pr, p_pr)
            ctx = o_sh[BLOCK:PAIR] + jnp.where(lane < BLOCK, o_pr[BLOCK:PAIR], o_pr[PAIR + BLOCK : 2 * PAIR])
            out_ref[chunk, h * BLOCK : (h + 1) * BLOCK, pl.ds(local, PAIR)] = ctx.astype(bf16)
            lse_ref[h, pl.ds(pair, 1), :] = peak + jnp.log(total)

    @pl.loop(0, npairs // UNROLL)
    def _(some):
        for i in range(UNROLL):
            one_pair(UNROLL * some + i)

    step = 512
    queries = [global_queries(q_sc, mask_sc, h, gl_ref) for h in range(heads)]

    def score(c, peaks):
        at = pl.multiple_of(c * step, step)
        new = []
        for h in range(heads):
            got = dot_nn(k_sc[pl.ds(at, step), head_lanes(h)], queries[h])
            s_sc[h, pl.ds(at, step), :] = got
            new.append(jnp.maximum(peaks[h], jnp.max(got, axis=0, keepdims=True)))
        return tuple(new)

    peaks = lax.fori_loop(0, length // step, score, (jnp.full((1, PAIR), MASKED, f32),) * heads)

    def gather(c, carry):
        at = pl.multiple_of(c * step, step)
        new = []
        for h in range(heads):
            total, ctx = carry[h]
            e = jnp.exp(s_sc[h, pl.ds(at, step), :] - peaks[h])
            ctx = ctx + dot_tn(v_sc[pl.ds(at, step), head_lanes(h)], e.astype(bf16))
            new.append((total + jnp.sum(e, axis=0, keepdims=True), ctx))
        return tuple(new)

    start = (jnp.zeros((1, PAIR), f32), jnp.zeros((PAIR, PAIR), f32))
    sums = lax.fori_loop(0, length // step, gather, (start,) * heads)
    for h in range(heads):
        total, ctx = sums[h]
        ctx = ctx[BLOCK:PAIR] * (1.0 / total)
        put_global_columns(out_ref, slice(h * BLOCK, (h + 1) * BLOCK), gl_ref, ctx, per_chunk)
        lseg_ref[h : h + 1, :] = peaks[h] + jnp.log(total)
    for c in range(chunks):
        out_refs[c][...] = out_ref[c]


def attention_forward(tab, gl, x, seg, w, b_kv, b_q):
    chunks = len(x)
    rows = x[0].shape[0]
    length = rows * chunks
    heads = b_q.shape[0] // HEAD_DIM
    whole = lambda: pl.BlockSpec(memory_space=pltpu.VMEM)
    got = pl.pallas_call(
        functools.partial(forward_kernel, heads, chunks),
        out_shape=(jax.ShapeDtypeStruct((heads * HEAD_DIM, rows), bf16),) * chunks
        + (
            jax.ShapeDtypeStruct((heads, length // PAIR, PAIR), f32),
            jax.ShapeDtypeStruct((heads, PAIR), f32),
            jax.ShapeDtypeStruct((length + BLOCK, heads * PAIR), bf16),
            jax.ShapeDtypeStruct((length + BLOCK, heads * PAIR), bf16),
            jax.ShapeDtypeStruct((heads * HEAD_DIM, length), bf16),
            jax.ShapeDtypeStruct((BLOCK, length), bf16),
        ),
        in_specs=[pl.BlockSpec(memory_space=pltpu.SMEM)] * 2 + [whole() for _ in range(chunks + 4)],
        out_specs=tuple(whole() for _ in range(chunks + 6)),
        scratch_shapes=[
            pltpu.VMEM((heads, length, PAIR), f32),
            pltpu.VMEM((chunks, heads * HEAD_DIM, rows), bf16),
        ],
        compiler_params=pltpu.CompilerParams(vmem_limit_bytes=56 << 20),
        cost_estimate=pl.CostEstimate(flops=12_000_000_000, bytes_accessed=16_000_000, transcendentals=8_000_000),
        name="attention_forward",
    )(tab, gl, *x, seg, w, b_kv, b_q)
    return got[:chunks], got[chunks:]


def backward_kernel(heads, chunks, tab_ref, gl_ref, *refs):
    do_refs = refs[:chunks]
    (k_sc, v_sc, q_sc, mask_sc, lse_ref, lseg_ref, w_ref, dq_ref, dkv_ref, first_ref) = refs[chunks : chunks + 10]
    part_refs = refs[chunks + 10 : 2 * chunks + 9]
    do_sc, acc, p_sc, d_sc, dqg_sc = refs[2 * chunks + 9 :]
    rows = do_refs[0].shape[1]
    length = rows * chunks
    npairs = length // PAIR
    per_chunk = npairs // chunks
    for c in range(chunks):
        do_sc[:, c * rows : (c + 1) * rows] = do_refs[c][...]
    first, second = lane_halves(PAIR, bf16)
    first2, second2 = lane_halves(2 * PAIR, bf16)
    ffirst, fsecond = lane_halves(PAIR, f32)
    lane = lax.broadcasted_iota(jnp.int32, (1, PAIR), 1)
    zeros = jnp.zeros((BLOCK, PAIR), bf16)

    def value_rows(do):
        return jnp.concatenate([zeros, do], axis=0)

    def sources(q, do):
        top = jnp.concatenate([q[0:BLOCK], zeros], axis=1)
        return jnp.concatenate([top, jnp.concatenate([zeros, do], axis=1)], axis=0)

    step = 512
    queries = [global_queries(q_sc, mask_sc, h, gl_ref) for h in range(heads)]
    grads = [global_columns(do_sc, slice(h * BLOCK, (h + 1) * BLOCK), gl_ref).astype(bf16) for h in range(heads)]

    def weigh(c, deltas):
        at = pl.multiple_of(c * step, step)
        new = []
        for h in range(heads):
            p = jnp.exp(dot_nn(k_sc[pl.ds(at, step), head_lanes(h)], queries[h]) - lseg_ref[h : h + 1, :])
            dp = dot_nn(v_sc[pl.ds(at, step), head_lanes(h)], value_rows(grads[h]))
            p_sc[h, pl.ds(at, step), :] = p
            d_sc[h, pl.ds(at, step), :] = dp
            new.append(deltas[h] + jnp.sum(p * dp, axis=0, keepdims=True))
        return tuple(new)

    deltas = lax.fori_loop(0, length // step, weigh, (jnp.zeros((1, PAIR), f32),) * heads)

    def spread(c, dqs):
        at = pl.multiple_of(c * step, step)
        new = []
        for h in range(heads):
            p = p_sc[h, pl.ds(at, step), :]
            ds = (p * (d_sc[h, pl.ds(at, step), :] - deltas[h])).astype(bf16)
            both = jnp.concatenate([ds, p.astype(bf16)], axis=1)
            acc[h, pl.ds(at, step), :] = dot_nt(both, sources(queries[h], grads[h]))
            new.append(dqs[h] + dot_tn(k_sc[pl.ds(at, step), head_lanes(h)], ds))
        return tuple(new)

    dqs = lax.fori_loop(0, length // step, spread, (jnp.zeros((PAIR, PAIR), f32),) * heads)
    for h in range(heads):
        dqg_sc[h] = dqs[h][0:BLOCK] * (HEAD_DIM ** -0.5)
        acc[h, pl.ds(length, BLOCK), :] = jnp.zeros((BLOCK, PAIR), f32)

    def one_pair(pair):
        chunk = pair // per_chunk
        local = pl.multiple_of((pair % per_chunk) * PAIR, PAIR)
        at = pl.multiple_of(pair * PAIR, PAIR)
        hit_first = (gl_ref[0] == 2 * pair) | (gl_ref[1] == 2 * pair)
        hit_second = (gl_ref[0] == 2 * pair + 1) | (gl_ref[1] == 2 * pair + 1)
        shut = ffirst * jnp.where(hit_first, -MASKED, 0.0) + fsecond * jnp.where(hit_second, -MASKED, 0.0)
        for h in range(heads):
            shared, mine, other = slots(tab_ref, gl_ref, h, pair, npairs)
            kl = head_lanes(h)
            q = query_columns(q_sc, mask_sc, h, at)
            do = do_sc[h * BLOCK : (h + 1) * BLOCK, pl.ds(at, PAIR)]
            do_v = value_rows(do)
            lse = lse_ref[h, pl.ds(pair, 1), :] + shut
            k_sh = stack_rows(k_sc, shared, kl)
            k_pr = jnp.concatenate([stack_rows(k_sc, mine, kl), stack_rows(k_sc, other, kl)], axis=1)
            p_sh = jnp.exp(dot_nn(k_sh, q) - lse)
            p_pr = jnp.exp(dot_nn(k_pr, jnp.concatenate([q * first, q * second], axis=0)) - lse)
            d_sh = dot_nn(stack_rows(v_sc, shared, kl), do_v)
            v_pr = jnp.concatenate([stack_rows(v_sc, mine, kl), stack_rows(v_sc, other, kl)], axis=1)
            d_pr = dot_nn(v_pr, jnp.concatenate([do_v * first, do_v * second], axis=0))
            delta = jnp.sum(p_sh * d_sh, axis=0, keepdims=True) + jnp.sum(p_pr * d_pr, axis=0, keepdims=True)
            ds_sh = (p_sh * (d_sh - delta)).astype(bf16)
            ds_pr = (p_pr * (d_pr - delta)).astype(bf16)
            src = sources(q, do)
            g_sh = dot_nt(jnp.concatenate([ds_sh, p_sh.astype(bf16)], axis=1), src)
            src2 = jnp.concatenate([src * first2, src * second2], axis=0)
            g_pr = dot_nt(jnp.concatenate([ds_pr, p_pr.astype(bf16)], axis=1), src2)
            for j, o in enumerate(shared):
                acc[h, pl.ds(o, BLOCK), :] += g_sh[j * BLOCK : (j + 1) * BLOCK]
            for j, o in enumerate(mine):
                acc[h, pl.ds(o, BLOCK), :] += g_pr[j * BLOCK : (j + 1) * BLOCK, 0:PAIR]
            for j, o in enumerate(other):
                acc[h, pl.ds(o, BLOCK), :] += g_pr[j * BLOCK : (j + 1) * BLOCK, PAIR:]
            t_sh = dot_tn(k_sh, ds_sh)
            t_pr = dot_tn(k_pr, ds_pr)
            dq = t_sh[0:BLOCK] + jnp.where(lane < BLOCK, t_pr[0:BLOCK], t_pr[PAIR : PAIR + BLOCK])
            dq_ref[chunk, h * BLOCK : (h + 1) * BLOCK, pl.ds(local, PAIR)] = (dq * (HEAD_DIM ** -0.5)).astype(bf16)

    @pl.loop(0, npairs // UNROLL)
    def _(some):
        for i in range(UNROLL):
            one_pair(UNROLL * some + i)

    for h in range(heads):
        put_global_columns(dq_ref, slice(h * BLOCK, (h + 1) * BLOCK), gl_ref, dqg_sc[h], per_chunk)
        for c in range(chunks):
            dkv_ref[c, :, h * PAIR : (h + 1) * PAIR] = acc[h, pl.ds(c * rows, rows), :].astype(bf16)
    tile = 256
    wq = query_weights(w_ref, heads)
    for c in range(chunks):

        @pl.loop(0, rows // tile)
        def _(t):
            at = pl.multiple_of(t * tile, tile)
            got = dot_tn(dq_ref[c, :, pl.ds(at, tile)], wq)
            got = got + dot_nt(dkv_ref[c, pl.ds(at, tile), :], w_ref[:, 0 : heads * PAIR])
            if c == 0:
                first_ref[pl.ds(at, tile), :] = got
            else:
                part_refs[c - 1][pl.ds(at, tile), :] = got.astype(bf16)


def attention_backward(tab, gl, do, k, v, q, mask, lse, lseg, w):
    chunks = len(do)
    group, rows = do[0].shape
    heads = group // HEAD_DIM
    width = w.shape[0]
    length = rows * chunks
    whole = lambda: pl.BlockSpec(memory_space=pltpu.VMEM)
    return pl.pallas_call(
        functools.partial(backward_kernel, heads, chunks),
        out_shape=(
            jax.ShapeDtypeStruct((chunks, group, rows), bf16),
            jax.ShapeDtypeStruct((chunks, rows, heads * PAIR), bf16),
            jax.ShapeDtypeStruct((rows, width), f32),
        )
        + (jax.ShapeDtypeStruct((rows, width), bf16),) * (chunks - 1),
        in_specs=[pl.BlockSpec(memory_space=pltpu.SMEM)] * 2 + [whole() for _ in range(chunks + 7)],
        out_specs=tuple(whole() for _ in range(chunks + 2)),
        scratch_shapes=[
            pltpu.VMEM((group, length), bf16),
            pltpu.VMEM((heads, length + BLOCK, PAIR), f32),
            pltpu.VMEM((heads, length, PAIR), f32),
            pltpu.VMEM((heads, length, PAIR), f32),
            pltpu.VMEM((heads, BLOCK, PAIR), f32),
        ],
        compiler_params=pltpu.CompilerParams(vmem_limit_bytes=60 << 20),
        cost_estimate=pl.CostEstimate(flops=30_000_000_000, bytes_accessed=24_000_000, transcendentals=8_000_000),
        name="attention_backward",
    )(tab, gl, *do, k, v, q, mask, lse, lseg, w)


def round_up(value, to):
    return -(-value // to) * to


def half_columns(ref, index, place):
    at = index // 2 * PAIR
    both = ref[:, at : at + PAIR].astype(f32)
    return both if index % 2 == place else pltpu.roll(both, BLOCK, 1)


def two_halves(first, second):
    lane = lax.broadcasted_iota(jnp.int32, (1, PAIR), 1)
    return jnp.where(lane < BLOCK, first, second)


def pack_kernel(seq_n, wq_ref, wk_ref, wv_ref, wo_ref, up_ref, down_ref, bup_ref, vec_ref, pack_ref, rest_ref):
    own, width = wq_ref.shape
    heads = width // HEAD_DIM // seq_n
    blocks, inner = pack_ref.shape[0], pack_ref.shape[2]
    for s in range(seq_n):
        pieces = [
            two_halves(half_columns(wk_ref, s * heads + h, 0), half_columns(wv_ref, s * heads + h, 1))
            for h in range(heads)
        ]
        for h in range(0, heads, 2):
            second = half_columns(wq_ref, s * heads + h + 1, 1) if h + 1 < heads else jnp.zeros((own, PAIR), f32)
            pieces.append(two_halves(half_columns(wq_ref, s * heads + h, 0), second))
        piece = jnp.concatenate(pieces, axis=1).astype(bf16)
        notes = jnp.concatenate([vec_ref[...], jnp.zeros((8, piece.shape[1] - width), bf16)], axis=1) if (
            piece.shape[1] > width
        ) else vec_ref[:, 0 : piece.shape[1]]
        for b in range(blocks):
            for i in range(inner):
                pack_ref[b, s, i, 0:own, :] = piece
                pack_ref[b, s, i, own : own + 8, :] = notes
    u = up_ref.shape[0]
    rest_ref[0:u, :] = up_ref[...]
    rest_ref[u : 2 * u, :] = down_ref[...]
    rest_ref[2 * u : 2 * u + own, :] = wo_ref[...]
    row = lax.broadcasted_iota(jnp.int32, (8, 1), 0)
    block = jnp.where(row == 7, bup_ref[...].astype(f32), vec_ref[...].astype(f32))
    rest_ref[2 * u + own : 2 * u + own + 8, :] = block.astype(bf16)


def packed_weights(w_q, w_k, w_v, w_o, w_up, w_down, b_up, vec, dp_n, seq_n, ffn_n):
    own, width = w_q.shape
    heads = width // HEAD_DIM // seq_n
    lanes = heads * PAIR + round_up(heads * HEAD_DIM, PAIR)
    u = w_up.shape[0]
    if own % 8 or u % 16:
        group = heads * HEAD_DIM
        cols = lambda w: w.reshape(own, seq_n, heads, HEAD_DIM).transpose(1, 0, 2, 3)
        kv = jnp.stack([cols(w_k), cols(w_v)], axis=3).reshape(seq_n, own, 2 * group)
        piece = jnp.concatenate([kv, cols(w_q).reshape(seq_n, own, group)], axis=2)
        piece = jnp.pad(piece, ((0, 0), (0, round_up(own, 8) - own), (0, lanes - 3 * group)))
        notes = jnp.broadcast_to(vec[None, :, :lanes], (seq_n, 8, lanes))
        piece = jnp.concatenate([piece, notes], axis=1)
        pack = jnp.broadcast_to(piece[None, :, None], (dp_n, seq_n, ffn_n) + piece.shape[1:])
        w_o = jnp.pad(w_o, ((0, round_up(own, 8) - own), (0, 0)))
        return pack, jnp.concatenate([w_up, w_down, w_o, vec[:7], b_up], axis=0)
    whole = lambda: pl.BlockSpec(memory_space=pltpu.VMEM)
    return pl.pallas_call(
        functools.partial(pack_kernel, seq_n),
        out_shape=(
            jax.ShapeDtypeStruct((dp_n, seq_n, ffn_n, own + 8, lanes), bf16),
            jax.ShapeDtypeStruct((2 * u + own + 8, width), bf16),
        ),
        in_specs=[whole() for _ in range(8)],
        out_specs=(whole(), whole()),
        name="packed_weights",
    )(w_q, w_k, w_v, w_o, w_up, w_down, b_up, vec)


def weights_kernel(chunks, direct, *refs):
    x_refs = refs[:chunks]
    dq_ref, dkv_ref, out_ref, sums_ref, acc = refs[chunks:]
    group, rows = dq_ref.shape[1], dq_ref.shape[2]
    lanes = dkv_ref.shape[2]
    ones = jnp.ones((8, rows), bf16)
    sum_q = jnp.zeros((8, group), f32)
    sum_kv = jnp.zeros((8, lanes), f32)
    acc[lanes + group :, :] = jnp.zeros((acc.shape[0] - lanes - group, acc.shape[1]), f32)
    for c in range(chunks):
        x = x_refs[c][...]
        got_kv = dot_tn(dkv_ref[c], x)
        got_q = dot_nn(dq_ref[c], x)
        if c == 0:
            acc[0:lanes, :] = got_kv
            acc[lanes : lanes + group, :] = got_q
        else:
            acc[0:lanes, :] += got_kv
            acc[lanes : lanes + group, :] += got_q
        sum_q = sum_q + dot_nt(ones, dq_ref[c])
        sum_kv = sum_kv + dot_nn(ones, dkv_ref[c])
    grad = jnp.transpose(acc[...], (1, 0))
    blank = jnp.zeros((8, acc.shape[0] - lanes - group), f32)
    sums = jnp.concatenate([sum_kv, sum_q, blank], axis=1)
    sums_ref[...] = sums
    if direct:
        blocks, per, _ = out_ref.shape
        own = per - 8
        grad = grad.astype(f32).reshape(blocks, own, acc.shape[0])
        for b in range(blocks):
            out_ref[b, 0:own, :] = grad[b].astype(bf16)
            out_ref[b, own:, :] = sums.astype(bf16)
    else:
        out_ref[...] = grad.astype(bf16)


def projection_gradients(x, dq, dkv, own, devices):
    chunks, group, rows = dq.shape
    width = x[0].shape[1]
    lanes = dkv.shape[2]
    full = lanes + round_up(group, PAIR)
    direct = own % 8 == 0
    whole = lambda: pl.BlockSpec(memory_space=pltpu.VMEM)
    out, sums = pl.pallas_call(
        functools.partial(weights_kernel, chunks, direct),
        out_shape=(
            jax.ShapeDtypeStruct((devices, own + 8, full) if direct else (width, full), bf16),
            jax.ShapeDtypeStruct((8, full), f32),
        ),
        in_specs=[whole() for _ in range(chunks + 2)],
        out_specs=(whole(), whole()),
        scratch_shapes=[pltpu.VMEM((full, width), f32)],
        compiler_params=pltpu.CompilerParams(vmem_limit_bytes=40 << 20),
        cost_estimate=pl.CostEstimate(flops=4_000_000_000, bytes_accessed=12_000_000, transcendentals=0),
        name="projection_gradients",
    )(*x, dq, dkv)
    if not direct:
        out = jnp.pad(out.reshape(devices, own, full), ((0, 0), (0, round_up(own, 8) - own), (0, 0)))
        out = jnp.concatenate([out, jnp.broadcast_to(sums[None].astype(bf16), (devices, 8, full))], axis=1)
    return out


def unpack_kernel(own, got_ref, q_ref, k_ref, v_ref, sums_ref, tot):
    dp_n, seq_n, ffn_n, per, full = got_ref.shape
    width = q_ref.shape[1]
    heads = width // HEAD_DIM // seq_n
    for s in range(seq_n):
        total = jnp.zeros((per, full), f32)
        for d in range(dp_n):
            for f in range(ffn_n):
                total = total + got_ref[d, s, f].astype(f32)
        tot[s] = total
        sums_ref[s : s + 1, :] = total[per - 8 : per - 7, :]
    for w in range(width // PAIR):
        spots = [((2 * w + i) // heads, (2 * w + i) % heads) for i in range(2)]
        cols = slice(w * PAIR, (w + 1) * PAIR)
        for ref, where in (
            (k_ref, lambda h: 2 * h),
            (v_ref, lambda h: 2 * h + 1),
            (q_ref, lambda h: 2 * heads + h),
        ):
            both = [half_columns(tot.at[g], where(h), i) for i, (g, h) in enumerate(spots)]
            ref[:, cols] = two_halves(*both)[0:own]


def unpacked_gradients(got, own, width):
    dp_n, seq_n, ffn_n, per, full = got.shape
    whole = lambda: pl.BlockSpec(memory_space=pltpu.VMEM)
    return pl.pallas_call(
        functools.partial(unpack_kernel, own),
        out_shape=(jax.ShapeDtypeStruct((own, width), f32),) * 3 + (jax.ShapeDtypeStruct((seq_n, full), f32),),
        in_specs=[whole()],
        out_specs=tuple(whole() for _ in range(4)),
        scratch_shapes=[pltpu.VMEM((seq_n, per, full), f32)],
        compiler_params=pltpu.CompilerParams(vmem_limit_bytes=32 << 20),
        name="unpacked_gradients",
    )(got)


NORM_EPS = 1e-12


def transposed(value):
    return jnp.transpose(value.astype(f32), (1, 0)).astype(bf16)


def unit_rows(value):
    center = value - jnp.mean(value, axis=-1, keepdims=True)
    scale = lax.rsqrt(jnp.mean(center * center, axis=-1, keepdims=True) + NORM_EPS)
    return center * scale, scale


def unit_rows_back(grad, unit, scale):
    return scale * (
        grad - jnp.mean(grad, axis=-1, keepdims=True) - unit * jnp.mean(grad * unit, axis=-1, keepdims=True)
    )


def rows_kernel(parts, blocks, up_rows, me_ref, *refs):
    ctx_refs = refs[:parts]
    (x_ref, cot_ref, rest_ref, wo_ref, vec_ref, bup_ref, out_ref, resid_ref, hid_ref, pre_ref, nlt_ref, gft_ref,
     gb_ref) = refs[parts : parts + 13]
    do_refs = refs[parts + 13 : 2 * parts + 13]
    sums_ref, gbup_ref, slope_sc = refs[2 * parts + 13 :]
    group = ctx_refs[0].shape[0]
    width = x_ref.shape[1]

    def up(f):
        return rest_ref[:, f, 0:up_rows, :].reshape(width, rest_ref.shape[3])

    def down(f):
        return rest_ref[:, f, up_rows : 2 * up_rows, :].reshape(width, rest_ref.shape[3])

    def own_rows(k):
        return pl.ds(pl.multiple_of((me_ref[0] ^ k) * group, group), group)

    @pl.when(pl.program_id(0) == 0)
    def _():
        sums_ref[...] = jnp.zeros_like(sums_ref)
        gbup_ref[...] = jnp.zeros_like(gbup_ref)

    ctx = jnp.concatenate([r[...] for r in ctx_refs], axis=0)
    w_o = jnp.concatenate([wo_ref[own_rows(k), :] for k in range(parts)], axis=0)
    resid_one = x_ref[...].astype(f32) + (dot_tn(ctx, w_o) + vec_ref[0:1, :])
    unit_one, scale_one = unit_rows(resid_one)
    normed_one = unit_one * vec_ref[2:3, :] + vec_ref[3:4, :]
    low = normed_one.astype(bf16)
    nlt_ref[...] = transposed(normed_one)
    total = normed_one + vec_ref[1:2, :]
    pre = dot_nn(low, up(0)) + bup_ref[0:1, :]
    for f in range(blocks):
        later = dot_nn(low, up(f + 1)) + bup_ref[f + 1 : f + 2, :] if f + 1 < blocks else None
        phi = 0.5 + 0.5 * lax.erf(pre * (0.5 ** 0.5))
        slope_sc[f] = phi + pre * (jnp.exp(-0.5 * pre * pre) * 0.3989422804014327)
        hid = (pre * phi).astype(bf16)
        hid_ref[f] = hid
        total = total + dot_nt(hid, down(f))
        pre = later
    unit_two, scale_two = unit_rows(total)
    out_ref[...] = (unit_two * vec_ref[4:5, :] + vec_ref[5:6, :]).astype(bf16)
    cot = cot_ref[...].astype(f32)
    grad_two = unit_rows_back(cot * vec_ref[4:5, :], unit_two, scale_two)
    grad_ffn = grad_two.astype(bf16)
    gft_ref[...] = transposed(grad_two)
    grad_normed = grad_two
    back = dot_nn(grad_ffn, down(0))
    for f in range(blocks):
        later = dot_nn(grad_ffn, down(f + 1)) if f + 1 < blocks else None
        grad_pre = (back * slope_sc[f]).astype(bf16)
        pre_ref[f] = grad_pre
        gbup_ref[f : f + 1, :] += jnp.sum(grad_pre.astype(f32), axis=0, keepdims=True)
        grad_normed = grad_normed + dot_nt(grad_pre, up(f))
        back = later
    resid = unit_rows_back(grad_normed * vec_ref[2:3, :], unit_one, scale_one)
    resid_ref[...] = resid
    branch = resid.astype(bf16)
    gb_ref[...] = branch
    do = dot_nt(w_o, branch).astype(bf16)
    for k in range(parts):
        do_refs[k][...] = do[k * group : (k + 1) * group]
    for row, value in enumerate(
        (branch.astype(f32), grad_ffn.astype(f32), grad_normed * unit_one, grad_normed, cot * unit_two, cot)
    ):
        sums_ref[row : row + 1, :] += jnp.sum(value, axis=0, keepdims=True)


def rows_chain(me, ctx_parts, x, cot, rest, up_rows, w_o, vecs, bias_up):
    parts = len(ctx_parts)
    group, rows = ctx_parts[0].shape
    width = x.shape[1]
    outer, blocks, per, hidden = rest.shape
    tile = 256
    once = lambda shape: pl.BlockSpec(shape, lambda i: (0,) * len(shape), pipeline_mode=pl.Buffered(1))
    tall = pl.BlockSpec((tile, width), lambda i: (i, 0))
    wide = pl.BlockSpec((width, tile), lambda i: (0, i))
    cube = pl.BlockSpec((blocks, tile, hidden), lambda i: (0, i, 0))
    return pl.pallas_call(
        functools.partial(rows_kernel, parts, blocks, up_rows),
        grid=(rows // tile,),
        out_shape=(
            jax.ShapeDtypeStruct((rows, width), bf16),
            jax.ShapeDtypeStruct((rows, width), f32),
            jax.ShapeDtypeStruct((blocks, rows, hidden), bf16),
            jax.ShapeDtypeStruct((blocks, rows, hidden), bf16),
            jax.ShapeDtypeStruct((width, rows), bf16),
            jax.ShapeDtypeStruct((width, rows), bf16),
            jax.ShapeDtypeStruct((rows, width), bf16),
        )
        + (jax.ShapeDtypeStruct((group, rows), bf16),) * parts
        + (jax.ShapeDtypeStruct((8, width), f32), jax.ShapeDtypeStruct((8, hidden), f32)),
        in_specs=[pl.BlockSpec(memory_space=pltpu.SMEM)]
        + [pl.BlockSpec((group, tile), lambda i: (0, i))] * parts
        + [tall, tall, once(rest.shape), once(w_o.shape), once(vecs.shape), once(bias_up.shape)],
        out_specs=(
            tall, tall, cube, cube, wide, wide, tall,
        )
        + (pl.BlockSpec((group, tile), lambda i: (0, i)),) * parts
        + (pl.BlockSpec((8, width), lambda i: (0, 0)), pl.BlockSpec((8, hidden), lambda i: (0, 0))),
        scratch_shapes=[pltpu.VMEM((blocks, tile, hidden), f32)],
        compiler_params=pltpu.CompilerParams(vmem_limit_bytes=60 << 20),
        cost_estimate=pl.CostEstimate(flops=22_000_000_000, bytes_accessed=40_000_000, transcendentals=6_000_000),
        name="rows_chain",
    )(me, *ctx_parts, x, cot, rest, w_o, vecs, bias_up)


def outer_kernel(parts, up_rows, own, me_ref, *refs):
    ctx_refs = refs[:parts]
    nlt_ref, gft_ref, gb_ref, pre_ref, hid_ref, small_ref, out_ref, wo_sc = refs[parts:]
    slabs, hidden = out_ref.shape[0], out_ref.shape[3]
    group = ctx_refs[0].shape[0]
    f = pl.program_id(0)
    up = dot_nn(nlt_ref[...], pre_ref[0]).astype(bf16)
    out_ref[:, 0, 0:up_rows, :] = up.reshape(slabs, up_rows, hidden)
    down = dot_nn(gft_ref[...], hid_ref[0]).astype(bf16)
    out_ref[:, 0, up_rows : 2 * up_rows, :] = down.reshape(slabs, up_rows, hidden)
    if not own:
        return

    @pl.when(f == 0)
    def _():
        for k in range(parts):
            wo_sc[k] = dot_nn(ctx_refs[k][...], gb_ref[...])

    share = slabs // parts
    stride = group // share
    for k in range(parts):
        for j in range(share):
            rows = pl.ds(pl.multiple_of(j * stride + f * own, 8), own)
            out_ref[(me_ref[0] ^ k) * share + j, 0, 2 * up_rows : 2 * up_rows + own, :] = wo_sc[k, rows, :].astype(bf16)
    out_ref[:, 0, 2 * up_rows + own :, :] = small_ref[:, 0]


def outer_products(me, ctx_parts, nlt, gft, gb, pre, hid, small, slabs, up_rows, own):
    blocks, rows, hidden = pre.shape
    parts = len(ctx_parts)
    group = ctx_parts[0].shape[0]
    per = 2 * up_rows + (own + 8 if own else 0)
    once = lambda shape: pl.BlockSpec(shape, lambda i: (0,) * len(shape), pipeline_mode=pl.Buffered(1))
    return pl.pallas_call(
        functools.partial(outer_kernel, parts, up_rows, own),
        grid=(blocks,),
        out_shape=jax.ShapeDtypeStruct((slabs, blocks, per, hidden), bf16),
        in_specs=[pl.BlockSpec(memory_space=pltpu.SMEM)]
        + [once(c.shape) for c in ctx_parts]
        + [
            once(nlt.shape),
            once(gft.shape),
            once(gb.shape),
            pl.BlockSpec((1, rows, hidden), lambda i: (i, 0, 0)),
            pl.BlockSpec((1, rows, hidden), lambda i: (i, 0, 0)),
            pl.BlockSpec((small.shape[0], 1) + small.shape[2:], lambda i: (0, i, 0, 0)),
        ],
        out_specs=pl.BlockSpec((slabs, 1, per, hidden), lambda i: (0, i, 0, 0)),
        scratch_shapes=[pltpu.VMEM((parts, group, gb.shape[1]), f32)],
        compiler_params=pltpu.CompilerParams(vmem_limit_bytes=48 << 20),
        cost_estimate=pl.CostEstimate(flops=11_000_000_000, bytes_accessed=28_000_000, transcendentals=0),
        name="outer_products",
    )(me, *ctx_parts, nlt, gft, gb, pre, hid, small)


ALL = ("dp", "seq", "ffn")


def flip_send(array, axis, bits):
    count = lax.axis_size(axis)
    return lax.ppermute(array, axis, [(i, i ^ bits) for i in range(count)])


def shards(
    tokens, w_query, w_key, w_value, w_output, b_query, b_value, b_output, w_up, b_up, w_down, b_down,
    gain_attn, shift_attn, gain_ffn, shift_ffn, segment_ids, random_blocks, global_blocks, cotangent,
):
    seq_n, dp_n, ffn_n = lax.axis_size("seq"), lax.axis_size("dp"), lax.axis_size("ffn")
    outer, devices = dp_n * seq_n, dp_n * seq_n * ffn_n
    me = lax.axis_index("seq")
    here = (lax.axis_index("dp") * seq_n + me) * ffn_n + lax.axis_index("ffn")
    own, width = w_query.shape
    own_pad = round_up(own, 8)
    group = width // seq_n
    heads = group // HEAD_DIM
    features = tokens[0]
    rows = features.shape[0]
    order = jnp.stack([me ^ k for k in range(seq_n)])
    me_ref = me.astype(jnp.int32)[None]

    near = [features] + [None] * (seq_n - 1)
    for k in sorted(range(1, seq_n), key=lambda k: (k & (k - 1), -k)):
        bit = k & -k
        near[k] = flip_send(features if bit == k else near[k ^ bit], "seq", bit)

    vec = jnp.stack([b_output, b_down, gain_attn, shift_attn, gain_ffn, shift_ffn, b_query, b_value])
    vec = jnp.pad(vec, ((0, 0), (0, width - own)))
    pack, rest = packed_weights(
        w_query, w_key, w_value, w_output, w_up, w_down, b_up[None], vec, dp_n, seq_n, ffn_n
    )
    lanes = pack.shape[4]
    pack = lax.all_to_all(
        pack.reshape(devices, own_pad + 8, lanes), ALL, split_axis=0, concat_axis=0, tiled=True
    )
    rest = lax.all_gather(rest, ALL, axis=0, tiled=False)
    w_own = pack[:, :own].reshape(width, lanes)
    share = devices // seq_n
    biases = lax.dynamic_slice(pack, (share * me, own_pad + 6, 0), (share, 2, own))
    biases = biases.transpose(1, 0, 2).reshape(2, group).astype(f32)
    by_head = biases[1].reshape(heads, 1, HEAD_DIM)
    b_kv = jnp.concatenate([jnp.zeros_like(by_head), by_head], axis=1).reshape(1, heads * PAIR)
    seg = segment_ids[0].reshape(seq_n, rows)[order]

    nblocks = seq_n * rows // BLOCK
    flip = me.astype(jnp.int32) * (nblocks // seq_n)
    tab = pair_table(random_blocks[0], global_blocks[0], flip, nblocks)
    gl = global_blocks[0] ^ flip
    ctx, (lse, lseg, k_all, v_all, q_all, mask_all) = attention_forward(
        tab, gl, near, seg, w_own, b_kv, biases[0][:, None]
    )
    ctx_parts = [ctx[0]] + [flip_send(ctx[k], "seq", k) for k in range(1, seq_n)]

    up_rows = w_up.shape[0]
    at = 2 * up_rows
    rest = rest.reshape(outer, ffn_n, rest.shape[1], width)
    w_o = rest[:, :, at : at + own].reshape(width, width)
    bias_up = rest[0, :, at + own_pad + 7].astype(f32)
    vecs = rest[:, :, at + own_pad :, :own].transpose(2, 0, 1, 3).reshape(8, width).astype(f32)
    direct = up_rows % 16 == 0 and own % 8 == 0 and outer % seq_n == 0 and (outer // seq_n) * ffn_n * own == group
    if not direct:
        rest = rest[:, :, :at].reshape(outer, ffn_n, 2, up_rows, width).transpose(1, 2, 0, 3, 4)
        rest = rest.reshape(1, ffn_n, 2 * outer * up_rows, width)
    slabs, slab_rows = (outer, up_rows) if direct else (1, outer * up_rows)

    got = rows_chain(me_ref, ctx_parts, features, cotangent[0], rest, slab_rows, w_o, vecs, bias_up)
    out, grad_resid_one, hidden, grad_pre, normed_t, grad_ffn_t, grad_branch = got[:7]
    grad_ctx, (sums, grad_bias_up) = got[7 : 7 + seq_n], got[7 + seq_n :]
    do = [grad_ctx[0]] + [flip_send(grad_ctx[k], "seq", k) for k in range(1, seq_n)]

    vec_grads = sums[:6].astype(bf16).reshape(6, outer, ffn_n, own).transpose(1, 2, 0, 3)
    vec_grads = jnp.pad(vec_grads, ((0, 0), (0, 0), (0, 1), (0, width - own)))
    top = jnp.broadcast_to(grad_bias_up[None, :ffn_n, None].astype(bf16), (outer, ffn_n, 1, width))
    small = jnp.concatenate([top, vec_grads], axis=2)
    payload = outer_products(
        me_ref, ctx_parts, normed_t, grad_ffn_t, grad_branch, grad_pre, hidden, small, slabs, slab_rows,
        own if direct else 0,
    )
    if not direct:
        grad_out = dot_nn(jnp.concatenate(ctx_parts, axis=0), grad_branch).astype(bf16)
        grad_out = grad_out.reshape(seq_n, group, width)[order].reshape(outer, ffn_n, own, width)
        payload = payload.reshape(ffn_n, 2, outer, up_rows, width).transpose(2, 0, 1, 3, 4)
        payload = jnp.concatenate([payload.reshape(outer, ffn_n, at, width), grad_out, small], axis=2)
        payload = jnp.pad(payload, ((0, 0), (0, 0), (0, -payload.shape[2] % 32), (0, 0)))
    payload, do = lax.optimization_barrier((payload, do))
    total = lax.psum_scatter(payload.reshape(-1, width), ALL, scatter_dimension=0, tiled=True)
    total = total.astype(f32)
    out_up, out_down, out_output = total[:up_rows], total[up_rows:at], total[at : at + own]
    out_bias_up = total[at + own]
    out_vecs = total[at + own + 1 : at + own + 7, :own]

    got = attention_backward(tab, gl, do, k_all, v_all, q_all, mask_all, lse, lseg, w_own)
    dq, dkv, part_first = got[:3]
    part = [None] + list(got[3:])
    grad_features = grad_resid_one + part_first
    bit = 1
    while bit < seq_n:
        for k in range(seq_n):
            if k & -k == bit and k != bit:
                came = flip_send(part[k], "seq", bit).astype(f32)
                part[k ^ bit] = (part[k ^ bit].astype(f32) + came).astype(bf16)
        bit *= 2
    grad_w = projection_gradients(near, dq, dkv, own, devices)
    grad_w, part = lax.optimization_barrier((grad_w, part[1:]))
    part = [None] + part
    bit = seq_n // 2
    while bit:
        grad_features = grad_features + flip_send(part[bit], "seq", bit).astype(f32)
        bit //= 2
    grad_w = lax.all_to_all(grad_w, ALL, split_axis=0, concat_axis=0, tiled=True)
    out_query, out_key, out_value, col_sums = unpacked_gradients(
        grad_w.reshape(dp_n, seq_n, ffn_n, own_pad + 8, lanes), own, width
    )
    row = lax.dynamic_index_in_dim(col_sums, here // share, keepdims=False)
    row = jnp.stack([row[heads * PAIR : heads * PAIR + group], row[: heads * PAIR].reshape(heads, 2, HEAD_DIM)[:, 1].reshape(group)])
    out_b = lax.dynamic_slice(row, (0, here % share * own), (2, own))
    return (
        out[None],
        grad_features[None],
        out_query,
        out_key,
        out_value,
        out_output,
        out_b[0],
        out_b[1],
        out_vecs[0],
        out_up,
        out_bias_up,
        out_down,
        out_vecs[1],
        out_vecs[2],
        out_vecs[3],
        out_vecs[4],
        out_vecs[5],
    )


def solution(mesh):
    return jax.shard_map(
        shards,
        mesh=mesh,
        in_specs=(
            P(("dp", "ffn"), "seq", None),
            P(("dp", "seq", "ffn"), None),
            P(("dp", "seq", "ffn"), None),
            P(("dp", "seq", "ffn"), None),
            P(("dp", "seq", "ffn"), None),
            P(("dp", "seq", "ffn")),
            P(("dp", "seq", "ffn")),
            P(("dp", "seq", "ffn")),
            P(("dp", "seq"), "ffn"),
            P("ffn"),
            P(("dp", "seq"), "ffn"),
            P(("dp", "seq", "ffn")),
            P(("dp", "seq", "ffn")),
            P(("dp", "seq", "ffn")),
            P(("dp", "seq", "ffn")),
            P(("dp", "seq", "ffn")),
            P(("dp", "ffn"), None),
            P(("dp", "ffn"), "seq", None, None),
            P(("dp", "ffn"), None),
            P(("dp", "ffn"), "seq", None),
        ),
        out_specs=(
            P(("dp", "ffn"), "seq", None),
            P(("dp", "ffn"), "seq", None),
            P(("dp", "seq", "ffn"), None),
            P(("dp", "seq", "ffn"), None),
            P(("dp", "seq", "ffn"), None),
            P(("dp", "seq", "ffn"), None),
            P(("dp", "seq", "ffn")),
            P(("dp", "seq", "ffn")),
            P(("dp", "seq", "ffn")),
            P(("dp", "seq"), "ffn"),
            P("ffn"),
            P(("dp", "seq"), "ffn"),
            P(("dp", "seq", "ffn")),
            P(("dp", "seq", "ffn")),
            P(("dp", "seq", "ffn")),
            P(("dp", "seq", "ffn")),
            P(("dp", "seq", "ffn")),
        ),
        check_vma=False,
    )
```

```python
import functools
import jax
import jax.numpy as jnp
from jax import lax
from jax.experimental import pallas as pl
from jax.sharding import PartitionSpec as P
from jax.experimental.pallas import tpu as pltpu

HEAD_DIM = 64
BLOCK = 64
PAIR = 2 * BLOCK
MASKED = -1e30
bf16 = jnp.bfloat16
f32 = jnp.float32


def dot_nn(a, b):
    return lax.dot_general(a, b, (((1,), (0,)), ((), ())), preferred_element_type=f32)


def dot_nt(a, b):
    return lax.dot_general(a, b, (((1,), (1,)), ((), ())), preferred_element_type=f32)


def dot_tn(a, b):
    return lax.dot_general(a, b, (((0,), (0,)), ((), ())), preferred_element_type=f32)


def pair_table(rand_local, global_ids, flip, nblocks):
    heads = rand_local.shape[0]
    null = nblocks
    first = (2 * jnp.arange(nblocks // 2, dtype=jnp.int32)) ^ flip

    def near(block):
        bad = (block < 0) | (block >= nblocks) | (block == global_ids[0]) | (block == global_ids[1])
        return jnp.where(bad, null, block ^ flip)

    rand_first = rand_local[:, first, :] ^ flip
    rand_second = rand_local[:, first + 1, :] ^ flip
    nears = jnp.stack([near(first), near(first + 1), near(first - 1), near(first + 2)], axis=1)
    nears = jnp.broadcast_to(nears[None], (heads,) + nears.shape)
    return jnp.concatenate(
        [nears[:, :, 0:3], rand_first, nears[:, :, 3:4], rand_second], axis=2
    ).astype(jnp.int32).reshape(-1)


def slots(tab_ref, gl_ref, head, pair, npairs):
    at = (head * npairs + pair) * 10
    got = [pl.multiple_of(tab_ref[at + j] * BLOCK, BLOCK) for j in range(10)]
    glob = [pl.multiple_of(gl_ref[j] * BLOCK, BLOCK) for j in range(2)]
    return got[0:2] + glob, got[2:6], got[6:10]


def stack_rows(ref, offsets, lanes):
    return jnp.concatenate([ref[pl.ds(o, BLOCK), lanes] for o in offsets], axis=0)


def lane_halves(width, dtype):
    lane = lax.broadcasted_iota(jnp.int32, (1, width), 1) % PAIR
    first = (lane < BLOCK).astype(dtype)
    second = (lane >= BLOCK).astype(dtype)
    return first, second


UNROLL = 4
BACK_UNROLL = 8
VMEM_BYTES = 62 << 20


def head_lanes(h):
    return slice(h * PAIR, (h + 1) * PAIR)


def query_columns(q_ref, mask_ref, h, at):
    return jnp.concatenate([q_ref[h * BLOCK : (h + 1) * BLOCK, pl.ds(at, PAIR)], mask_ref[:, pl.ds(at, PAIR)]], axis=0)


def global_queries(q_ref, mask_ref, h, gl_ref):
    return jnp.concatenate(
        [
            global_columns(q_ref, slice(h * BLOCK, (h + 1) * BLOCK), gl_ref),
            global_columns(mask_ref, slice(0, BLOCK), gl_ref),
        ],
        axis=0,
    ).astype(bf16)


def global_columns(src_ref, rows, gl_ref):
    lane = lax.broadcasted_iota(jnp.int32, (1, PAIR), 1)
    parts = []
    for g in range(2):
        block = gl_ref[g]
        at = pl.multiple_of((block // 2) * PAIR, PAIR)
        both = src_ref[rows, pl.ds(at, PAIR)].astype(f32)
        moved = pltpu.roll(both, BLOCK, 1)
        parts.append(jnp.where(block % 2 == g, both, moved))
    return jnp.where(lane < BLOCK, parts[0], parts[1])


def put_global_columns(dst_ref, rows, gl_ref, value, per_chunk):
    lane = lax.broadcasted_iota(jnp.int32, (1, PAIR), 1)
    moved = pltpu.roll(value, BLOCK, 1)
    for g in range(2):
        block = gl_ref[g]
        pair = block // 2
        half = block % 2
        chunk = pair // per_chunk
        at = pl.multiple_of((pair % per_chunk) * PAIR, PAIR)
        src = jnp.where(half == g, value, moved)
        old = dst_ref[chunk, rows, pl.ds(at, PAIR)].astype(f32)
        new = jnp.where((lane >= BLOCK) == (half == 1), src, old)
        dst_ref[chunk, rows, pl.ds(at, PAIR)] = new.astype(dst_ref.dtype)


def project_rows(x, seg, w_ref, wq, bkv_ref, bq_ref, k_ref, v_ref, q_ref, mask_ref, at):
    n = x.shape[0]
    lanes = v_ref.shape[1]
    y = dot_nn(x, w_ref[:, 0:lanes]) + bkv_ref[...]
    spot = lax.broadcasted_iota(jnp.int32, (PAIR, n), 0) - BLOCK
    mark = jnp.transpose((spot == seg).astype(f32), (1, 0))
    lane = lax.broadcasted_iota(jnp.int32, (1, PAIR), 1)
    rows = pl.ds(at, n)
    v_ref[rows, :] = y.astype(bf16)
    for h in range(lanes // PAIR):
        k_ref[rows, head_lanes(h)] = jnp.where(lane < BLOCK, y[:, head_lanes(h)], mark).astype(bf16)
    z = (dot_nt(wq, x) + bq_ref[...]).astype(bf16)
    q_ref[:, rows] = (z.astype(f32) * HEAD_DIM ** -0.5).astype(bf16)
    row = lax.broadcasted_iota(jnp.int32, (BLOCK, n), 0)
    mask_ref[:, rows] = jnp.where((row <= 16) & (row != seg), MASKED, 0.0).astype(bf16)


def query_weights(w_ref, heads):
    at = heads * PAIR
    cols = w_ref[:, at : at + 2 * PAIR].astype(f32)
    return jnp.transpose(cols, (1, 0))[0 : heads * HEAD_DIM].astype(bf16)


def forward_kernel(heads, chunks, tab_ref, gl_ref, *refs):
    x_refs = refs[0:chunks]
    seg_ref, w_ref, bkv_ref, bq_ref = refs[chunks : chunks + 4]
    out_refs = refs[chunks + 4 : 2 * chunks + 4]
    lse_ref, lseg_ref, k_sc, v_sc, q_sc, mask_sc, s_sc, out_ref = refs[2 * chunks + 4 :]
    rows = x_refs[0].shape[0]
    length = rows * chunks
    npairs = length // PAIR
    per_chunk = npairs // chunks
    tile = 256
    wq = query_weights(w_ref, heads)
    for c in range(chunks):

        @pl.loop(0, rows // tile)
        def _(t):
            at = pl.multiple_of(t * tile, tile)
            project_rows(
                x_refs[c][pl.ds(at, tile), :], seg_ref[c : c + 1, pl.ds(at, tile)], w_ref, wq, bkv_ref, bq_ref,
                k_sc, v_sc, q_sc, mask_sc, pl.multiple_of(c * rows + t * tile, tile),
            )

    null_lane = lax.broadcasted_iota(jnp.int32, (BLOCK, heads * PAIR), 1) % PAIR
    k_sc[pl.ds(length, BLOCK), :] = (null_lane == BLOCK + 16).astype(f32).astype(bf16)
    v_sc[pl.ds(length, BLOCK), :] = jnp.zeros((BLOCK, heads * PAIR), bf16)
    first, second = lane_halves(PAIR, bf16)
    lane = lax.broadcasted_iota(jnp.int32, (1, PAIR), 1)

    def one_pair(pair):
        chunk = pair // per_chunk
        local = pl.multiple_of((pair % per_chunk) * PAIR, PAIR)
        at = pl.multiple_of(pair * PAIR, PAIR)
        for h in range(heads):
            shared, mine, other = slots(tab_ref, gl_ref, h, pair, npairs)
            kl = head_lanes(h)
            q = query_columns(q_sc, mask_sc, h, at)
            s_sh = dot_nn(stack_rows(k_sc, shared, kl), q)
            k_pr = jnp.concatenate([stack_rows(k_sc, mine, kl), stack_rows(k_sc, other, kl)], axis=1)
            s_pr = dot_nn(k_pr, jnp.concatenate([q * first, q * second], axis=0))
            peak = jnp.maximum(jnp.max(s_sh, axis=0, keepdims=True), jnp.max(s_pr, axis=0, keepdims=True))
            e_sh = jnp.exp(s_sh - peak)
            e_pr = jnp.exp(s_pr - peak)
            total = jnp.sum(e_sh, axis=0, keepdims=True) + jnp.sum(e_pr, axis=0, keepdims=True)
            inv = 1.0 / total
            p_sh = (e_sh * inv).astype(bf16)
            p_pr = (e_pr * inv).astype(bf16)
            v_pr = jnp.concatenate([stack_rows(v_sc, mine, kl), stack_rows(v_sc, other, kl)], axis=1)
            o_sh = dot_tn(stack_rows(v_sc, shared, kl), p_sh)
            o_pr = dot_tn(v_pr, p_pr)
            ctx = o_sh[BLOCK:PAIR] + jnp.where(lane < BLOCK, o_pr[BLOCK:PAIR], o_pr[PAIR + BLOCK : 2 * PAIR])
            out_ref[chunk, h * BLOCK : (h + 1) * BLOCK, pl.ds(local, PAIR)] = ctx.astype(bf16)
            lse_ref[h, pl.ds(pair, 1), :] = peak + jnp.log(total)

    @pl.loop(0, npairs // UNROLL)
    def _(some):
        for i in range(UNROLL):
            one_pair(UNROLL * some + i)

    step = 512
    queries = [global_queries(q_sc, mask_sc, h, gl_ref) for h in range(heads)]

    def score(c, peaks):
        at = pl.multiple_of(c * step, step)
        new = []
        for h in range(heads):
            got = dot_nn(k_sc[pl.ds(at, step), head_lanes(h)], queries[h])
            s_sc[h, pl.ds(at, step), :] = got
            new.append(jnp.maximum(peaks[h], jnp.max(got, axis=0, keepdims=True)))
        return tuple(new)

    peaks = lax.fori_loop(0, length // step, score, (jnp.full((1, PAIR), MASKED, f32),) * heads)

    def gather(c, carry):
        at = pl.multiple_of(c * step, step)
        new = []
        for h in range(heads):
            total, ctx = carry[h]
            e = jnp.exp(s_sc[h, pl.ds(at, step), :] - peaks[h])
            ctx = ctx + dot_tn(v_sc[pl.ds(at, step), head_lanes(h)], e.astype(bf16))
            new.append((total + jnp.sum(e, axis=0, keepdims=True), ctx))
        return tuple(new)

    start = (jnp.zeros((1, PAIR), f32), jnp.zeros((PAIR, PAIR), f32))
    sums = lax.fori_loop(0, length // step, gather, (start,) * heads)
    for h in range(heads):
        total, ctx = sums[h]
        ctx = ctx[BLOCK:PAIR] * (1.0 / total)
        put_global_columns(out_ref, slice(h * BLOCK, (h + 1) * BLOCK), gl_ref, ctx, per_chunk)
        lseg_ref[h : h + 1, :] = peaks[h] + jnp.log(total)
    for c in range(chunks):
        out_refs[c][...] = out_ref[c]


def attention_forward(tab, gl, x, seg, w, b_kv, b_q):
    chunks = len(x)
    rows = x[0].shape[0]
    length = rows * chunks
    heads = b_q.shape[0] // HEAD_DIM
    whole = lambda: pl.BlockSpec(memory_space=pltpu.VMEM)
    got = pl.pallas_call(
        functools.partial(forward_kernel, heads, chunks),
        out_shape=(jax.ShapeDtypeStruct((heads * HEAD_DIM, rows), bf16),) * chunks
        + (
            jax.ShapeDtypeStruct((heads, length // PAIR, PAIR), f32),
            jax.ShapeDtypeStruct((heads, PAIR), f32),
            jax.ShapeDtypeStruct((length + BLOCK, heads * PAIR), bf16),
            jax.ShapeDtypeStruct((length + BLOCK, heads * PAIR), bf16),
            jax.ShapeDtypeStruct((heads * HEAD_DIM, length), bf16),
            jax.ShapeDtypeStruct((BLOCK, length), bf16),
        ),
        in_specs=[pl.BlockSpec(memory_space=pltpu.SMEM)] * 2 + [whole() for _ in range(chunks + 4)],
        out_specs=tuple(whole() for _ in range(chunks + 6)),
        scratch_shapes=[
            pltpu.VMEM((heads, length, PAIR), f32),
            pltpu.VMEM((chunks, heads * HEAD_DIM, rows), bf16),
        ],
        compiler_params=pltpu.CompilerParams(vmem_limit_bytes=VMEM_BYTES),
        cost_estimate=pl.CostEstimate(flops=12_000_000_000, bytes_accessed=16_000_000, transcendentals=8_000_000),
        name="attention_forward",
    )(tab, gl, *x, seg, w, b_kv, b_q)
    return got[:chunks], got[chunks:]


def backward_kernel(h, chunks, tab_ref, gl_ref, *refs):
    do_refs = refs[:chunks]
    (k_ref, kv_ref, q_ref, mask_ref, seg_ref, lse_ref, lseg_ref, dq_ref, dkv_ref,
     do_sc, acc, p_sc, d_sc, seg_sc, line_sc) = refs[chunks:]
    rows = do_refs[0].shape[1]
    length = rows * chunks
    npairs = length // PAIR
    per_chunk = npairs // chunks
    scale = HEAD_DIM ** -0.5
    for c in range(chunks):
        do_sc[:, c * rows : (c + 1) * rows] = do_refs[c][...]

        @pl.loop(0, per_chunk)
        def _(t):
            at = pl.multiple_of(t * PAIR, PAIR)
            line = seg_ref[c : c + 1, pl.ds(at, PAIR)].astype(f32)
            line_sc[c * per_chunk + t] = line
            to = pl.multiple_of(c * rows + t * PAIR, PAIR)
            seg_sc[pl.ds(to, PAIR), :] = jnp.transpose(jnp.broadcast_to(line, (PAIR, PAIR)), (1, 0))

    seg_sc[pl.ds(length, BLOCK), :] = jnp.full((BLOCK, PAIR), -1.0, f32)
    acc[pl.ds(length, BLOCK), :] = jnp.zeros((BLOCK, PAIR), f32)
    first2, second2 = lane_halves(2 * PAIR, bf16)
    ffirst, fsecond = lane_halves(PAIR, f32)
    lane = lax.broadcasted_iota(jnp.int32, (1, PAIR), 1)
    line = lax.broadcasted_iota(jnp.int32, (PAIR, 1), 0)
    zeros = jnp.zeros((BLOCK, PAIR), bf16)
    blank = jnp.zeros((PAIR, PAIR), bf16)
    every = slice(0, PAIR)

    def joint(q, mask, do):
        left = jnp.concatenate([q, mask, blank], axis=0)
        right = jnp.concatenate([blank, zeros, do], axis=0)
        return jnp.concatenate([left, right], axis=1)

    def sources(q, do):
        top = jnp.concatenate([q, zeros], axis=1)
        return jnp.concatenate([top, jnp.concatenate([zeros, do], axis=1)], axis=0)

    step = 512
    all_rows = slice(0, BLOCK)
    q_glob = global_columns(q_ref, all_rows, gl_ref).astype(bf16)
    mask_glob = global_columns(mask_ref, all_rows, gl_ref).astype(bf16)
    do_glob = global_columns(do_sc, all_rows, gl_ref).astype(bf16)
    right_glob = joint(q_glob, mask_glob, do_glob)
    src_glob = sources(q_glob, do_glob)
    lse_glob = lseg_ref[h : h + 1, :]

    def weigh(c, delta):
        at = pl.multiple_of(c * step, step)
        both = dot_nn(jnp.concatenate([k_ref[pl.ds(at, step), :], kv_ref[pl.ds(at, step), :]], axis=1), right_glob)
        p = jnp.exp(both[:, 0:PAIR] - lse_glob)
        dp = both[:, PAIR:]
        p_sc[pl.ds(at, step), :] = p
        d_sc[pl.ds(at, step), :] = dp
        return delta + jnp.sum(p * dp, axis=0, keepdims=True)

    delta_glob = lax.fori_loop(0, length // step, weigh, jnp.zeros((1, PAIR), f32), unroll=4)

    def spread(c, dq):
        at = pl.multiple_of(c * step, step)
        p = p_sc[pl.ds(at, step), :]
        ds = (p * (d_sc[pl.ds(at, step), :] - delta_glob)).astype(bf16)
        acc[pl.ds(at, step), :] = dot_nt(jnp.concatenate([ds, p.astype(bf16)], axis=1), src_glob)
        return dq + dot_tn(k_ref[pl.ds(at, step), :], ds)

    dq_glob = lax.fori_loop(0, length // step, spread, jnp.zeros((PAIR, PAIR), f32), unroll=4)

    def one_pair(pair):
        chunk = pair // per_chunk
        local = pl.multiple_of((pair % per_chunk) * PAIR, PAIR)
        at = pl.multiple_of(pair * PAIR, PAIR)
        hit_first = (gl_ref[0] == 2 * pair) | (gl_ref[1] == 2 * pair)
        hit_second = (gl_ref[0] == 2 * pair + 1) | (gl_ref[1] == 2 * pair + 1)
        shut = ffirst * jnp.where(hit_first, -MASKED, 0.0) + fsecond * jnp.where(hit_second, -MASKED, 0.0)
        shared, mine, other = slots(tab_ref, gl_ref, h, pair, npairs)
        q = q_ref[:, pl.ds(at, PAIR)]
        do = do_sc[:, pl.ds(at, PAIR)]
        lse = lse_ref[0, pl.ds(pair, 1), :] + shut
        src = sources(q, do)
        src2 = jnp.concatenate([src * first2, src * second2], axis=0)
        k_sh = stack_rows(k_ref, shared, every)
        two_sh = dot_nn(
            jnp.concatenate([k_sh, stack_rows(kv_ref, shared, every)], axis=1),
            joint(q, mask_ref[:, pl.ds(at, PAIR)], do),
        )
        kv_pr = jnp.concatenate([stack_rows(kv_ref, mine, every), stack_rows(kv_ref, other, every)], axis=1)
        two_pr = dot_nn(kv_pr, src2)
        seg_pr = jnp.where(lane < BLOCK, stack_rows(seg_sc, mine, every), stack_rows(seg_sc, other, every))
        agree = seg_pr == line_sc[pair]
        p_sh = jnp.exp(two_sh[:, 0:PAIR] - lse)
        p_pr = jnp.where(agree, jnp.exp(two_pr[:, 0:PAIR] - lse), 0.0)
        d_sh, d_pr = two_sh[:, PAIR:], two_pr[:, PAIR:]
        delta = jnp.sum(p_sh * d_sh, axis=0, keepdims=True) + jnp.sum(p_pr * d_pr, axis=0, keepdims=True)
        ds_sh = (p_sh * (d_sh - delta)).astype(bf16)
        ds_pr = (p_pr * (d_pr - delta)).astype(bf16)
        g_sh = dot_nt(jnp.concatenate([ds_sh, p_sh.astype(bf16)], axis=1), src)
        g_pr = dot_nt(jnp.concatenate([ds_pr, p_pr.astype(bf16)], axis=1), src2)
        for j, o in enumerate(shared):
            acc[pl.ds(o, BLOCK), :] += g_sh[j * BLOCK : (j + 1) * BLOCK]
        for j, o in enumerate(mine):
            acc[pl.ds(o, BLOCK), :] += g_pr[j * BLOCK : (j + 1) * BLOCK, 0:PAIR]
        for j, o in enumerate(other):
            acc[pl.ds(o, BLOCK), :] += g_pr[j * BLOCK : (j + 1) * BLOCK, PAIR:]
        t_pr = dot_tn(ds_pr, kv_pr)
        dq = dot_tn(ds_sh, k_sh) + jnp.where(line < BLOCK, t_pr[:, 0:PAIR], t_pr[:, PAIR:])
        dq = jnp.transpose(dq, (1, 0))[0:BLOCK]
        dq_ref[chunk, :, pl.ds(local, PAIR)] = (dq * scale).astype(bf16)

    @pl.loop(0, npairs // BACK_UNROLL)
    def _(some):
        for i in range(BACK_UNROLL):
            one_pair(BACK_UNROLL * some + i)

    put_global_columns(dq_ref, all_rows, gl_ref, dq_glob[0:BLOCK] * scale, per_chunk)
    for c in range(chunks):
        dkv_ref[c] = acc[pl.ds(c * rows, rows), :].astype(bf16)


def attention_backward(h, tab, gl, do, k, kv, q, mask, seg, lse, lseg):
    chunks = len(do)
    rows = do[0].shape[1]
    length = rows * chunks
    one = pl.Buffered(1)
    lanes = pl.BlockSpec((length + BLOCK, PAIR), lambda i: (0, h), pipeline_mode=one)
    whole = lambda: pl.BlockSpec(memory_space=pltpu.VMEM)
    return pl.pallas_call(
        functools.partial(backward_kernel, h, chunks),
        grid=(1,),
        out_shape=(
            jax.ShapeDtypeStruct((chunks, HEAD_DIM, rows), bf16),
            jax.ShapeDtypeStruct((chunks, rows, PAIR), bf16),
        ),
        in_specs=[pl.BlockSpec(memory_space=pltpu.SMEM)] * 2
        + [pl.BlockSpec((HEAD_DIM, rows), lambda i: (h, 0), pipeline_mode=one) for _ in range(chunks)]
        + [
            lanes,
            lanes,
            pl.BlockSpec((HEAD_DIM, length), lambda i: (h, 0), pipeline_mode=one),
            whole(),
            whole(),
            pl.BlockSpec((1,) + lse.shape[1:], lambda i: (h, 0, 0), pipeline_mode=one),
            whole(),
        ],
        out_specs=(whole(), whole()),
        scratch_shapes=[
            pltpu.VMEM((HEAD_DIM, length), bf16),
            pltpu.VMEM((length + BLOCK, PAIR), f32),
            pltpu.VMEM((length, PAIR), f32),
            pltpu.VMEM((length, PAIR), f32),
            pltpu.VMEM((length + BLOCK, PAIR), f32),
            pltpu.VMEM((length // PAIR, 1, PAIR), f32),
        ],
        compiler_params=pltpu.CompilerParams(vmem_limit_bytes=VMEM_BYTES),
        cost_estimate=pl.CostEstimate(flops=9_000_000_000, bytes_accessed=6_000_000, transcendentals=3_000_000),
        name="attention_backward",
    )(tab, gl, *do, k, kv, q, mask, seg, lse, lseg)


def spread_kernel(heads, chunks, *refs):
    dq_refs, dkv_refs = refs[:heads], refs[heads : 2 * heads]
    w_ref, resid_ref = refs[2 * heads : 2 * heads + 2]
    out_refs = refs[2 * heads + 2 : -1]
    wq_sc = refs[-1]

    @pl.when(pl.program_id(0) == 0)
    def _():
        wq_sc[...] = query_weights(w_ref, heads)

    for c in range(chunks):
        dq = jnp.concatenate([r[c] for r in dq_refs], axis=0)
        dkv = jnp.concatenate([r[c] for r in dkv_refs], axis=1)
        got = dot_tn(dq, wq_sc[...]) + dot_nt(dkv, w_ref[:, 0 : heads * PAIR])
        if c == 0:
            out_refs[c][...] = resid_ref[...] + got
        else:
            out_refs[c][...] = got.astype(bf16)


def token_gradients(dq, dkv, w, resid):
    heads = len(dq)
    chunks, dim, rows = dq[0].shape
    width = w.shape[0]
    tile = 256
    tall = pl.BlockSpec((tile, width), lambda i: (i, 0))
    return pl.pallas_call(
        functools.partial(spread_kernel, heads, chunks),
        grid=(rows // tile,),
        out_shape=(jax.ShapeDtypeStruct((rows, width), f32),)
        + (jax.ShapeDtypeStruct((rows, width), bf16),) * (chunks - 1),
        in_specs=[pl.BlockSpec((chunks, dim, tile), lambda i: (0, 0, i)) for _ in range(heads)]
        + [pl.BlockSpec((chunks, tile, PAIR), lambda i: (0, i, 0)) for _ in range(heads)]
        + [pl.BlockSpec(w.shape, lambda i: (0, 0), pipeline_mode=pl.Buffered(1)), tall],
        out_specs=(tall,) * chunks,
        scratch_shapes=[pltpu.VMEM((heads * dim, width), bf16)],
        compiler_params=pltpu.CompilerParams(vmem_limit_bytes=VMEM_BYTES),
        cost_estimate=pl.CostEstimate(flops=4_000_000_000, bytes_accessed=14_000_000, transcendentals=0),
        name="token_gradients",
    )(*dq, *dkv, w, resid)


def round_up(value, to):
    return -(-value // to) * to


def half_columns(ref, index, place):
    at = index // 2 * PAIR
    both = ref[:, at : at + PAIR].astype(f32)
    return both if index % 2 == place else pltpu.roll(both, BLOCK, 1)


def two_halves(first, second):
    lane = lax.broadcasted_iota(jnp.int32, (1, PAIR), 1)
    return jnp.where(lane < BLOCK, first, second)


def pack_kernel(seq_n, wq_ref, wk_ref, wv_ref, wo_ref, up_ref, down_ref, bup_ref, vec_ref, pack_ref, rest_ref):
    own, width = wq_ref.shape
    heads = width // HEAD_DIM // seq_n
    blocks, inner = pack_ref.shape[0], pack_ref.shape[2]
    for s in range(seq_n):
        pieces = [
            two_halves(half_columns(wk_ref, s * heads + h, 0), half_columns(wv_ref, s * heads + h, 1))
            for h in range(heads)
        ]
        for h in range(0, heads, 2):
            second = half_columns(wq_ref, s * heads + h + 1, 1) if h + 1 < heads else jnp.zeros((own, PAIR), f32)
            pieces.append(two_halves(half_columns(wq_ref, s * heads + h, 0), second))
        piece = jnp.concatenate(pieces, axis=1).astype(bf16)
        notes = jnp.concatenate([vec_ref[...], jnp.zeros((8, piece.shape[1] - width), bf16)], axis=1) if (
            piece.shape[1] > width
        ) else vec_ref[:, 0 : piece.shape[1]]
        for b in range(blocks):
            for i in range(inner):
                pack_ref[b, s, i, 0:own, :] = piece
                pack_ref[b, s, i, own : own + 8, :] = notes
    u = up_ref.shape[0]
    rest_ref[0:u, :] = up_ref[...]
    rest_ref[u : 2 * u, :] = down_ref[...]
    rest_ref[2 * u : 2 * u + own, :] = wo_ref[...]
    row = lax.broadcasted_iota(jnp.int32, (8, 1), 0)
    block = jnp.where(row == 7, bup_ref[...].astype(f32), vec_ref[...].astype(f32))
    rest_ref[2 * u + own : 2 * u + own + 8, :] = block.astype(bf16)


def packed_weights(w_q, w_k, w_v, w_o, w_up, w_down, b_up, vec, dp_n, seq_n, ffn_n):
    own, width = w_q.shape
    heads = width // HEAD_DIM // seq_n
    lanes = heads * PAIR + round_up(heads * HEAD_DIM, PAIR)
    u = w_up.shape[0]
    if own % 8 or u % 16:
        group = heads * HEAD_DIM
        cols = lambda w: w.reshape(own, seq_n, heads, HEAD_DIM).transpose(1, 0, 2, 3)
        kv = jnp.stack([cols(w_k), cols(w_v)], axis=3).reshape(seq_n, own, 2 * group)
        piece = jnp.concatenate([kv, cols(w_q).reshape(seq_n, own, group)], axis=2)
        piece = jnp.pad(piece, ((0, 0), (0, round_up(own, 8) - own), (0, lanes - 3 * group)))
        notes = jnp.broadcast_to(vec[None, :, :lanes], (seq_n, 8, lanes))
        piece = jnp.concatenate([piece, notes], axis=1)
        pack = jnp.broadcast_to(piece[None, :, None], (dp_n, seq_n, ffn_n) + piece.shape[1:])
        w_o = jnp.pad(w_o, ((0, round_up(own, 8) - own), (0, 0)))
        return pack, jnp.concatenate([w_up, w_down, w_o, vec[:7], b_up], axis=0)
    whole = lambda: pl.BlockSpec(memory_space=pltpu.VMEM)
    return pl.pallas_call(
        functools.partial(pack_kernel, seq_n),
        out_shape=(
            jax.ShapeDtypeStruct((dp_n, seq_n, ffn_n, own + 8, lanes), bf16),
            jax.ShapeDtypeStruct((2 * u + own + 8, width), bf16),
        ),
        in_specs=[whole() for _ in range(8)],
        out_specs=(whole(), whole()),
        name="packed_weights",
    )(w_q, w_k, w_v, w_o, w_up, w_down, b_up, vec)


def weights_kernel(heads, chunks, direct, *refs):
    x_refs = refs[:chunks]
    dq_refs, dkv_refs = refs[chunks : chunks + heads], refs[chunks + heads : chunks + 2 * heads]
    out_ref, sums_ref, acc = refs[chunks + 2 * heads :]
    rows = x_refs[0].shape[0]
    lanes = heads * PAIR
    group = heads * HEAD_DIM
    ones = jnp.ones((8, rows), bf16)
    sum_q = jnp.zeros((8, group), f32)
    sum_kv = jnp.zeros((8, lanes), f32)
    acc[lanes + group :, :] = jnp.zeros((acc.shape[0] - lanes - group, acc.shape[1]), f32)
    for c in range(chunks):
        x = x_refs[c][...]
        dq = jnp.concatenate([r[c] for r in dq_refs], axis=0)
        dkv = jnp.concatenate([r[c] for r in dkv_refs], axis=1)
        got_kv = dot_tn(dkv, x)
        got_q = dot_nn(dq, x)
        if c == 0:
            acc[0:lanes, :] = got_kv
            acc[lanes : lanes + group, :] = got_q
        else:
            acc[0:lanes, :] += got_kv
            acc[lanes : lanes + group, :] += got_q
        sum_q = sum_q + dot_nt(ones, dq)
        sum_kv = sum_kv + dot_nn(ones, dkv)
    grad = jnp.transpose(acc[...], (1, 0))
    blank = jnp.zeros((8, acc.shape[0] - lanes - group), f32)
    sums = jnp.concatenate([sum_kv, sum_q, blank], axis=1)
    sums_ref[...] = sums
    if direct:
        blocks, per, _ = out_ref.shape
        own = per - 8
        grad = grad.reshape(blocks, own, acc.shape[0])
        for b in range(blocks):
            out_ref[b, 0:own, :] = grad[b].astype(bf16)
            out_ref[b, own:, :] = sums.astype(bf16)
    else:
        out_ref[...] = grad.astype(bf16)


def projection_gradients(x, dq, dkv, own, devices):
    heads = len(dq)
    chunks, dim, rows = dq[0].shape
    width = x[0].shape[1]
    full = heads * PAIR + round_up(heads * dim, PAIR)
    direct = own % 8 == 0
    whole = lambda: pl.BlockSpec(memory_space=pltpu.VMEM)
    out, sums = pl.pallas_call(
        functools.partial(weights_kernel, heads, chunks, direct),
        out_shape=(
            jax.ShapeDtypeStruct((devices, own + 8, full) if direct else (width, full), bf16),
            jax.ShapeDtypeStruct((8, full), f32),
        ),
        in_specs=[whole() for _ in range(chunks + 2 * heads)],
        out_specs=(whole(), whole()),
        scratch_shapes=[pltpu.VMEM((full, width), f32)],
        compiler_params=pltpu.CompilerParams(vmem_limit_bytes=VMEM_BYTES),
        cost_estimate=pl.CostEstimate(flops=4_000_000_000, bytes_accessed=12_000_000, transcendentals=0),
        name="projection_gradients",
    )(*x, *dq, *dkv)
    if not direct:
        out = jnp.pad(out.reshape(devices, own, full), ((0, 0), (0, round_up(own, 8) - own), (0, 0)))
        out = jnp.concatenate([out, jnp.broadcast_to(sums[None].astype(bf16), (devices, 8, full))], axis=1)
    return out


def unpack_kernel(own, got_ref, q_ref, k_ref, v_ref, sums_ref, tot):
    dp_n, seq_n, ffn_n, per, full = got_ref.shape
    width = q_ref.shape[1]
    heads = width // HEAD_DIM // seq_n
    for s in range(seq_n):
        total = jnp.zeros((per, full), f32)
        for d in range(dp_n):
            for f in range(ffn_n):
                total = total + got_ref[d, s, f].astype(f32)
        tot[s] = total
        sums_ref[s : s + 1, :] = total[per - 8 : per - 7, :]
    for w in range(width // PAIR):
        spots = [((2 * w + i) // heads, (2 * w + i) % heads) for i in range(2)]
        cols = slice(w * PAIR, (w + 1) * PAIR)
        for ref, where in (
            (k_ref, lambda h: 2 * h),
            (v_ref, lambda h: 2 * h + 1),
            (q_ref, lambda h: 2 * heads + h),
        ):
            both = [half_columns(tot.at[g], where(h), i) for i, (g, h) in enumerate(spots)]
            ref[:, cols] = two_halves(*both)[0:own]


def unpacked_gradients(got, own, width):
    dp_n, seq_n, ffn_n, per, full = got.shape
    whole = lambda: pl.BlockSpec(memory_space=pltpu.VMEM)
    return pl.pallas_call(
        functools.partial(unpack_kernel, own),
        out_shape=(jax.ShapeDtypeStruct((own, width), f32),) * 3 + (jax.ShapeDtypeStruct((seq_n, full), f32),),
        in_specs=[whole()],
        out_specs=tuple(whole() for _ in range(4)),
        scratch_shapes=[pltpu.VMEM((seq_n, per, full), f32)],
        compiler_params=pltpu.CompilerParams(vmem_limit_bytes=VMEM_BYTES),
        name="unpacked_gradients",
    )(got)


NORM_EPS = 1e-12


def transposed(value):
    return jnp.transpose(value.astype(f32), (1, 0)).astype(bf16)


def unit_rows(value):
    center = value - jnp.mean(value, axis=-1, keepdims=True)
    scale = lax.rsqrt(jnp.mean(center * center, axis=-1, keepdims=True) + NORM_EPS)
    return center * scale, scale


def unit_rows_back(grad, unit, scale):
    return scale * (
        grad - jnp.mean(grad, axis=-1, keepdims=True) - unit * jnp.mean(grad * unit, axis=-1, keepdims=True)
    )


def rows_kernel(parts, blocks, up_rows, me_ref, *refs):
    ctx_refs = refs[:parts]
    (x_ref, cot_ref, rest_ref, wo_ref, vec_ref, bup_ref, out_ref, resid_ref, hid_ref, pre_ref, nlt_ref, gft_ref,
     gb_ref) = refs[parts : parts + 13]
    do_refs = refs[parts + 13 : 2 * parts + 13]
    sums_ref, gbup_ref, slope_sc = refs[2 * parts + 13 :]
    group = ctx_refs[0].shape[0]
    width = x_ref.shape[1]

    def up(f):
        return rest_ref[:, f, 0:up_rows, :].reshape(width, rest_ref.shape[3])

    def down(f):
        return rest_ref[:, f, up_rows : 2 * up_rows, :].reshape(width, rest_ref.shape[3])

    def own_rows(k):
        return pl.ds(pl.multiple_of((me_ref[0] ^ k) * group, group), group)

    @pl.when(pl.program_id(0) == 0)
    def _():
        sums_ref[...] = jnp.zeros_like(sums_ref)
        gbup_ref[...] = jnp.zeros_like(gbup_ref)

    ctx = jnp.concatenate([r[...] for r in ctx_refs], axis=0)
    w_o = jnp.concatenate([wo_ref[own_rows(k), :] for k in range(parts)], axis=0)
    resid_one = x_ref[...].astype(f32) + (dot_tn(ctx, w_o) + vec_ref[0:1, :])
    unit_one, scale_one = unit_rows(resid_one)
    normed_one = unit_one * vec_ref[2:3, :] + vec_ref[3:4, :]
    low = normed_one.astype(bf16)
    nlt_ref[...] = transposed(normed_one)
    total = normed_one + vec_ref[1:2, :]
    pre = dot_nn(low, up(0)) + bup_ref[0:1, :]
    for f in range(blocks):
        later = dot_nn(low, up(f + 1)) + bup_ref[f + 1 : f + 2, :] if f + 1 < blocks else None
        phi = 0.5 + 0.5 * lax.erf(pre * (0.5 ** 0.5))
        slope_sc[f] = phi + pre * (jnp.exp(-0.5 * pre * pre) * 0.3989422804014327)
        hid = (pre * phi).astype(bf16)
        hid_ref[f] = hid
        total = total + dot_nt(hid, down(f))
        pre = later
    unit_two, scale_two = unit_rows(total)
    out_ref[...] = (unit_two * vec_ref[4:5, :] + vec_ref[5:6, :]).astype(bf16)
    cot = cot_ref[...].astype(f32)
    grad_two = unit_rows_back(cot * vec_ref[4:5, :], unit_two, scale_two)
    grad_ffn = grad_two.astype(bf16)
    gft_ref[...] = transposed(grad_two)
    grad_normed = grad_two
    back = dot_nn(grad_ffn, down(0))
    for f in range(blocks):
        later = dot_nn(grad_ffn, down(f + 1)) if f + 1 < blocks else None
        grad_pre = (back * slope_sc[f]).astype(bf16)
        pre_ref[f] = grad_pre
        gbup_ref[f : f + 1, :] += jnp.sum(grad_pre.astype(f32), axis=0, keepdims=True)
        grad_normed = grad_normed + dot_nt(grad_pre, up(f))
        back = later
    resid = unit_rows_back(grad_normed * vec_ref[2:3, :], unit_one, scale_one)
    resid_ref[...] = resid
    branch = resid.astype(bf16)
    gb_ref[...] = branch
    do = dot_nt(w_o, branch).astype(bf16)
    for k in range(parts):
        do_refs[k][...] = do[k * group : (k + 1) * group]
    for row, value in enumerate(
        (branch.astype(f32), grad_ffn.astype(f32), grad_normed * unit_one, grad_normed, cot * unit_two, cot)
    ):
        sums_ref[row : row + 1, :] += jnp.sum(value, axis=0, keepdims=True)


def rows_chain(me, ctx_parts, x, cot, rest, up_rows, w_o, vecs, bias_up):
    parts = len(ctx_parts)
    group, rows = ctx_parts[0].shape
    width = x.shape[1]
    outer, blocks, per, hidden = rest.shape
    tile = 256
    once = lambda shape: pl.BlockSpec(shape, lambda i: (0,) * len(shape), pipeline_mode=pl.Buffered(1))
    tall = pl.BlockSpec((tile, width), lambda i: (i, 0))
    wide = pl.BlockSpec((width, tile), lambda i: (0, i))
    cube = pl.BlockSpec((blocks, tile, hidden), lambda i: (0, i, 0))
    return pl.pallas_call(
        functools.partial(rows_kernel, parts, blocks, up_rows),
        grid=(rows // tile,),
        out_shape=(
            jax.ShapeDtypeStruct((rows, width), bf16),
            jax.ShapeDtypeStruct((rows, width), f32),
            jax.ShapeDtypeStruct((blocks, rows, hidden), bf16),
            jax.ShapeDtypeStruct((blocks, rows, hidden), bf16),
            jax.ShapeDtypeStruct((width, rows), bf16),
            jax.ShapeDtypeStruct((width, rows), bf16),
            jax.ShapeDtypeStruct((rows, width), bf16),
        )
        + (jax.ShapeDtypeStruct((group, rows), bf16),) * parts
        + (jax.ShapeDtypeStruct((8, width), f32), jax.ShapeDtypeStruct((8, hidden), f32)),
        in_specs=[pl.BlockSpec(memory_space=pltpu.SMEM)]
        + [pl.BlockSpec((group, tile), lambda i: (0, i))] * parts
        + [tall, tall, once(rest.shape), once(w_o.shape), once(vecs.shape), once(bias_up.shape)],
        out_specs=(
            tall, tall, cube, cube, wide, wide, tall,
        )
        + (pl.BlockSpec((group, tile), lambda i: (0, i)),) * parts
        + (pl.BlockSpec((8, width), lambda i: (0, 0)), pl.BlockSpec((8, hidden), lambda i: (0, 0))),
        scratch_shapes=[pltpu.VMEM((blocks, tile, hidden), f32)],
        compiler_params=pltpu.CompilerParams(vmem_limit_bytes=VMEM_BYTES),
        cost_estimate=pl.CostEstimate(flops=22_000_000_000, bytes_accessed=40_000_000, transcendentals=6_000_000),
        name="rows_chain",
    )(me, *ctx_parts, x, cot, rest, w_o, vecs, bias_up)


def outer_kernel(parts, up_rows, own, me_ref, *refs):
    ctx_refs = refs[:parts]
    nlt_ref, gft_ref, gb_ref, pre_ref, hid_ref, small_ref, out_ref, wo_sc = refs[parts:]
    slabs, hidden = out_ref.shape[0], out_ref.shape[3]
    group = ctx_refs[0].shape[0]
    f = pl.program_id(0)
    up = dot_nn(nlt_ref[...], pre_ref[0]).astype(bf16)
    out_ref[:, 0, 0:up_rows, :] = up.reshape(slabs, up_rows, hidden)
    down = dot_nn(gft_ref[...], hid_ref[0]).astype(bf16)
    out_ref[:, 0, up_rows : 2 * up_rows, :] = down.reshape(slabs, up_rows, hidden)
    if not own:
        return

    @pl.when(f == 0)
    def _():
        for k in range(parts):
            wo_sc[k] = dot_nn(ctx_refs[k][...], gb_ref[...])

    share = slabs // parts
    stride = group // share
    for k in range(parts):
        for j in range(share):
            rows = pl.ds(pl.multiple_of(j * stride + f * own, 8), own)
            out_ref[(me_ref[0] ^ k) * share + j, 0, 2 * up_rows : 2 * up_rows + own, :] = wo_sc[k, rows, :].astype(bf16)
    out_ref[:, 0, 2 * up_rows + own :, :] = small_ref[:, 0]


def outer_products(me, ctx_parts, nlt, gft, gb, pre, hid, small, slabs, up_rows, own):
    blocks, rows, hidden = pre.shape
    parts = len(ctx_parts)
    group = ctx_parts[0].shape[0]
    per = 2 * up_rows + (own + 8 if own else 0)
    once = lambda shape: pl.BlockSpec(shape, lambda i: (0,) * len(shape), pipeline_mode=pl.Buffered(1))
    return pl.pallas_call(
        functools.partial(outer_kernel, parts, up_rows, own),
        grid=(blocks,),
        out_shape=jax.ShapeDtypeStruct((slabs, blocks, per, hidden), bf16),
        in_specs=[pl.BlockSpec(memory_space=pltpu.SMEM)]
        + [once(c.shape) for c in ctx_parts]
        + [
            once(nlt.shape),
            once(gft.shape),
            once(gb.shape),
            pl.BlockSpec((1, rows, hidden), lambda i: (i, 0, 0)),
            pl.BlockSpec((1, rows, hidden), lambda i: (i, 0, 0)),
            pl.BlockSpec((small.shape[0], 1) + small.shape[2:], lambda i: (0, i, 0, 0)),
        ],
        out_specs=pl.BlockSpec((slabs, 1, per, hidden), lambda i: (0, i, 0, 0)),
        scratch_shapes=[pltpu.VMEM((parts, group, gb.shape[1]), f32)],
        compiler_params=pltpu.CompilerParams(vmem_limit_bytes=VMEM_BYTES),
        cost_estimate=pl.CostEstimate(flops=11_000_000_000, bytes_accessed=28_000_000, transcendentals=0),
        name="outer_products",
    )(me, *ctx_parts, nlt, gft, gb, pre, hid, small)


SPLITS = ((0, 64), (64, 112), (112, 160))
RING = 160


def outer_split_kernel(parts, up_rows, own, here_ref, *refs):
    ctx_refs = refs[:parts]
    nlt_ref, gft_ref, gb_ref, pre_ref, hid_ref, small_ref = refs[parts : parts + 6]
    keep_refs, send_refs = refs[parts + 6 : parts + 9], refs[parts + 9 : parts + 12]
    rest_ref, block_sc, wo_sc = refs[parts + 12 :]
    slabs, hidden = block_sc.shape[0], block_sc.shape[2]
    group = ctx_refs[0].shape[0]
    f = pl.program_id(0)
    below = RING - up_rows
    up = dot_nn(nlt_ref[...], pre_ref[0]).astype(bf16)
    block_sc[:, 0:up_rows, :] = up.reshape(slabs, up_rows, hidden)
    down = dot_nn(gft_ref[...], hid_ref[0]).astype(bf16).reshape(slabs, up_rows, hidden)
    block_sc[:, up_rows:RING, :] = down[:, 0:below]
    rest_ref[:, 0, 0 : up_rows - below, :] = down[:, below:]

    @pl.when(f == 0)
    def _():
        for k in range(parts):
            wo_sc[k] = dot_nn(ctx_refs[k][...], gb_ref[...])

    share = slabs // parts
    stride = group // share
    at = up_rows - below
    me = here_ref[0]
    for k in range(parts):
        for j in range(share):
            rows = pl.ds(pl.multiple_of(j * stride + f * own, 8), own)
            rest_ref[(me ^ k) * share + j, 0, at : at + own, :] = wo_sc[k, rows, :].astype(bf16)
    rest_ref[:, 0, at + own :, :] = small_ref[:, 0]
    core = me % 2
    for y in range(2):
        for x in range(2):
            for kind, outs in ((0, keep_refs), (1, send_refs)):
                slab = y * 4 + x * 2 + (core ^ kind)
                for i, (low, high) in enumerate(SPLITS):
                    spot = ((x, y, 0, 0), (y, 0, 0, x), (0, 0, x, y))[i]
                    outs[i][spot] = block_sc[slab, low:high, :]


def outer_split(here, ctx_parts, nlt, gft, gb, pre, hid, small, slabs, up_rows, own):
    blocks, rows, hidden = pre.shape
    parts = len(ctx_parts)
    group = ctx_parts[0].shape[0]
    rest_rows = 2 * up_rows - RING + own + 8
    once = lambda shape: pl.BlockSpec(shape, lambda i: (0,) * len(shape), pipeline_mode=pl.Buffered(1))
    tall = [high - low for low, high in SPLITS]
    specs = [
        pl.BlockSpec((2, 2, 1, 1, tall[0], hidden), lambda i: (0, 0, i % 2, i // 2, 0, 0)),
        pl.BlockSpec((2, 1, 1, 2, tall[1], hidden), lambda i: (0, i % 2, i // 2, 0, 0, 0)),
        pl.BlockSpec((1, 1, 2, 2, tall[2], hidden), lambda i: (i % 2, i // 2, 0, 0, 0, 0)),
    ]
    shapes = [jax.ShapeDtypeStruct((2, 2, 2, 2, t, hidden), bf16) for t in tall]
    got = pl.pallas_call(
        functools.partial(outer_split_kernel, parts, up_rows, own),
        grid=(blocks,),
        out_shape=tuple(shapes + shapes + [jax.ShapeDtypeStruct((slabs, blocks, rest_rows, hidden), bf16)]),
        in_specs=[pl.BlockSpec(memory_space=pltpu.SMEM)]
        + [once(c.shape) for c in ctx_parts]
        + [
            once(nlt.shape),
            once(gft.shape),
            once(gb.shape),
            pl.BlockSpec((1, rows, hidden), lambda i: (i, 0, 0)),
            pl.BlockSpec((1, rows, hidden), lambda i: (i, 0, 0)),
            pl.BlockSpec((small.shape[0], 1) + small.shape[2:], lambda i: (0, i, 0, 0)),
        ],
        out_specs=tuple(specs + specs + [pl.BlockSpec((slabs, 1, rest_rows, hidden), lambda i: (0, i, 0, 0))]),
        scratch_shapes=[pltpu.VMEM((slabs, RING, hidden), bf16), pltpu.VMEM((parts, group, gb.shape[1]), f32)],
        compiler_params=pltpu.CompilerParams(vmem_limit_bytes=VMEM_BYTES),
        cost_estimate=pl.CostEstimate(flops=11_000_000_000, bytes_accessed=28_000_000, transcendentals=0),
        name="outer_split",
    )(here, *ctx_parts, nlt, gft, gb, pre, hid, small)
    return got[0:3], got[3:6], got[6]


def merge_kernel(bits_ref, *refs):
    for i in range(3):
        mine = bits_ref[i]
        for kind in range(2):
            half = mine ^ kind
            total = refs[i][half].astype(f32) + refs[3 + i][half].astype(f32)
            refs[6 + 3 * kind + i][...] = total.astype(bf16)


def merged(bits, keep, came):
    flat = [a.reshape((2, -1, a.shape[-1])) for a in list(keep) + list(came)]
    steps = flat[0].shape[1] * 2 // (2 * SPLITS[0][1])
    steps = 4 if steps >= 4 else steps
    ins, outs, shapes = [], [], []
    for a in flat:
        part = a.shape[1] // steps
        ins.append(pl.BlockSpec((2, part, a.shape[2]), lambda i: (0, i, 0)))
    for a in flat:
        outs.append(pl.BlockSpec((a.shape[1] // steps, a.shape[2]), lambda i: (i, 0)))
        shapes.append(jax.ShapeDtypeStruct(a.shape[1:], bf16))
    got = pl.pallas_call(
        merge_kernel,
        grid=(steps,),
        out_shape=tuple(shapes),
        in_specs=[pl.BlockSpec(memory_space=pltpu.SMEM)] + ins,
        out_specs=tuple(outs),
        compiler_params=pltpu.CompilerParams(vmem_limit_bytes=VMEM_BYTES),
        name="merged",
    )(bits, *flat)
    return got[0:3], got[3:6]


def finish_kernel(up_rows, own, *refs):
    total = [refs[i][...].astype(f32) + refs[3 + i][...].astype(f32) for i in range(3)]
    rest_ref, up_ref, down_ref, wo_ref, small_ref = refs[6:]
    first, second, third = [high - low for low, high in SPLITS]
    split = up_rows - first
    rest = rest_ref[...].astype(f32)
    up_ref[0:first, :] = total[0]
    up_ref[first:, :] = total[1][0:split]
    down_ref[0 : second - split, :] = total[1][split:]
    down_ref[second - split : RING - up_rows, :] = total[2]
    at = 2 * up_rows - RING
    down_ref[RING - up_rows :, :] = rest[0:at]
    wo_ref[...] = rest[at : at + own]
    small_ref[...] = rest[at + own :]


def finished(keep, came, rest, up_rows, own):
    hidden = rest.shape[1]
    whole = lambda: pl.BlockSpec(memory_space=pltpu.VMEM)
    return pl.pallas_call(
        functools.partial(finish_kernel, up_rows, own),
        out_shape=tuple(jax.ShapeDtypeStruct((r, hidden), f32) for r in (up_rows, up_rows, own, 8)),
        in_specs=[whole() for _ in range(7)],
        out_specs=tuple(whole() for _ in range(4)),
        name="finished",
    )(*keep, *came, rest)


ALL = ("dp", "seq", "ffn")


def flip_send(array, axis, bits):
    count = lax.axis_size(axis)
    return lax.ppermute(array, axis, [(i, i ^ bits) for i in range(count)])


def shards(
    tokens, w_query, w_key, w_value, w_output, b_query, b_value, b_output, w_up, b_up, w_down, b_down,
    gain_attn, shift_attn, gain_ffn, shift_ffn, segment_ids, random_blocks, global_blocks, cotangent,
):
    seq_n, dp_n, ffn_n = lax.axis_size("seq"), lax.axis_size("dp"), lax.axis_size("ffn")
    outer, devices = dp_n * seq_n, dp_n * seq_n * ffn_n
    me = lax.axis_index("seq")
    here = (lax.axis_index("dp") * seq_n + me) * ffn_n + lax.axis_index("ffn")
    own, width = w_query.shape
    own_pad = round_up(own, 8)
    group = width // seq_n
    heads = group // HEAD_DIM
    features = tokens[0]
    rows = features.shape[0]
    order = jnp.stack([me ^ k for k in range(seq_n)])
    me_ref = me.astype(jnp.int32)[None]

    near = [features] + [None] * (seq_n - 1)
    for k in sorted(range(1, seq_n), key=lambda k: (k & (k - 1), -k)):
        bit = k & -k
        near[k] = flip_send(features if bit == k else near[k ^ bit], "seq", bit)

    vec = jnp.stack([b_output, b_down, gain_attn, shift_attn, gain_ffn, shift_ffn, b_query, b_value])
    vec = jnp.pad(vec, ((0, 0), (0, width - own)))
    seg = segment_ids[0].reshape(seq_n, rows)[order]
    nblocks = seq_n * rows // BLOCK
    flip = me.astype(jnp.int32) * (nblocks // seq_n)
    tab = pair_table(random_blocks[0], global_blocks[0], flip, nblocks)
    gl = global_blocks[0] ^ flip
    pack, rest = packed_weights(
        w_query, w_key, w_value, w_output, w_up, w_down, b_up[None], vec, dp_n, seq_n, ffn_n
    )
    lanes = pack.shape[4]
    pack, seg, tab, gl = lax.optimization_barrier((pack, seg, tab, gl))
    pack = lax.all_to_all(
        pack.reshape(devices, own_pad + 8, lanes), ALL, split_axis=0, concat_axis=0, tiled=True
    )
    rest = lax.all_gather(rest, ALL, axis=0, tiled=False)
    w_own = pack[:, :own].reshape(width, lanes)
    share = devices // seq_n
    biases = lax.dynamic_slice(pack, (share * me, own_pad + 6, 0), (share, 2, own))
    biases = biases.transpose(1, 0, 2).reshape(2, group).astype(f32)
    by_head = biases[1].reshape(heads, 1, HEAD_DIM)
    b_kv = jnp.concatenate([jnp.zeros_like(by_head), by_head], axis=1).reshape(1, heads * PAIR)

    ctx, (lse, lseg, k_all, v_all, q_all, mask_all) = attention_forward(
        tab, gl, near, seg, w_own, b_kv, biases[0][:, None]
    )
    ctx_parts = [ctx[0]] + [flip_send(ctx[k], "seq", k) for k in range(1, seq_n)]

    up_rows = w_up.shape[0]
    at = 2 * up_rows
    rest = rest.reshape(outer, ffn_n, rest.shape[1], width)
    w_o = rest[:, :, at : at + own].reshape(width, width)
    bias_up = rest[0, :, at + own_pad + 7].astype(f32)
    vecs = rest[:, :, at + own_pad :, :own].transpose(2, 0, 1, 3).reshape(8, width).astype(f32)
    direct = up_rows % 16 == 0 and own % 8 == 0 and outer % seq_n == 0 and (outer // seq_n) * ffn_n * own == group
    if not direct:
        rest = rest[:, :, :at].reshape(outer, ffn_n, 2, up_rows, width).transpose(1, 2, 0, 3, 4)
        rest = rest.reshape(1, ffn_n, 2 * outer * up_rows, width)
    slabs, slab_rows = (outer, up_rows) if direct else (1, outer * up_rows)

    got = rows_chain(me_ref, ctx_parts, features, cotangent[0], rest, slab_rows, w_o, vecs, bias_up)
    out, grad_resid_one, hidden, grad_pre, normed_t, grad_ffn_t, grad_branch = got[:7]
    grad_ctx, (sums, grad_bias_up) = got[7 : 7 + seq_n], got[7 + seq_n :]
    do = [grad_ctx[0]] + [flip_send(grad_ctx[k], "seq", k) for k in range(1, seq_n)]

    vec_grads = sums[:6].astype(bf16).reshape(6, outer, ffn_n, own).transpose(1, 2, 0, 3)
    vec_grads = jnp.pad(vec_grads, ((0, 0), (0, 0), (0, 1), (0, width - own)))
    top = jnp.broadcast_to(grad_bias_up[None, :ffn_n, None].astype(bf16), (outer, ffn_n, 1, width))
    small = jnp.concatenate([top, vec_grads], axis=2)
    chained = direct and (dp_n, seq_n, ffn_n) == (2, 4, 4) and up_rows == 96
    args = (tab, gl, k_all, v_all, q_all, mask_all, seg, lse, lseg)
    back = lambda h, do: attention_backward(h, *args[:2], do, *args[2:])
    if chained:
        place = jnp.stack([me, lax.axis_index("dp"), lax.axis_index("ffn")]).astype(jnp.int32)
        x_bit, y_bit, low_bit, high_bit = place[0] // 2, place[1], place[2] % 2, place[2] // 2
        cross = {"x": ("seq", 2), "y": ("dp", 1), "low": ("ffn", 1), "high": ("ffn", 2)}
        bit = {"x": x_bit, "y": y_bit, "low": low_bit, "high": high_bit}
        orders = (("x", "y", "low", "high"), ("y", "low", "high", "x"), ("low", "high", "x", "y"))
        keep, send, ring = outer_split(
            place, ctx_parts, normed_t, grad_ffn_t, grad_branch, grad_pre, hidden, small, slabs, slab_rows, own
        )
        keep, send, ring, do = lax.optimization_barrier((keep, send, ring, do))
        total = lax.psum_scatter(ring.reshape(-1, width), ALL, scatter_dimension=0, tiled=True)
        came = [flip_send(a, "seq", 1) for a in send]
        dq, dkv = [], []
        for step in range(heads):
            got = back(step, do)
            dq.append(got[0])
            dkv.append(got[1])
            came, dq[step] = lax.optimization_barrier((came, dq[step]))
            keep, send = merged(jnp.stack([bit[o[step]] for o in orders]), keep, came)
            send, do, dq = lax.optimization_barrier((send, do, dq))
            dq = list(dq)
            came = [flip_send(a, *cross[o[step]]) for a, o in zip(send, orders)]
    else:
        payload = outer_products(
            me_ref, ctx_parts, normed_t, grad_ffn_t, grad_branch, grad_pre, hidden, small, slabs, slab_rows,
            own if direct else 0,
        )
        if not direct:
            grad_out = dot_nn(jnp.concatenate(ctx_parts, axis=0), grad_branch).astype(bf16)
            grad_out = grad_out.reshape(seq_n, group, width)[order].reshape(outer, ffn_n, own, width)
            payload = payload.reshape(ffn_n, 2, outer, up_rows, width).transpose(2, 0, 1, 3, 4)
            payload = jnp.concatenate([payload.reshape(outer, ffn_n, at, width), grad_out, small], axis=2)
            payload = jnp.pad(payload, ((0, 0), (0, 0), (0, -payload.shape[2] % 32), (0, 0)))
        payload, do = lax.optimization_barrier((payload, do))
        total = lax.psum_scatter(payload.reshape(-1, width), ALL, scatter_dimension=0, tiled=True)
        total = total.astype(f32)
        out_up, out_down, out_output = total[:up_rows], total[up_rows:at], total[at : at + own]
        notes = total[at + own : at + own + 8]
        dq, dkv = zip(*[back(h, do) for h in range(heads)])

    got = token_gradients(dq, dkv, w_own, grad_resid_one)
    grad_features = got[0]
    part = [None] + list(got[1:])
    near_bit = 1
    while near_bit < seq_n:
        for k in range(seq_n):
            if k & -k == near_bit and k != near_bit:
                more = flip_send(part[k], "seq", near_bit).astype(f32)
                part[k ^ near_bit] = (part[k ^ near_bit].astype(f32) + more).astype(bf16)
        near_bit *= 2
    grad_w = projection_gradients(near, dq, dkv, own, devices)
    grad_w, part = lax.optimization_barrier((grad_w, part[1:]))
    part = [None] + part
    if chained:
        came, grad_w = lax.optimization_barrier((came, grad_w))
        keep, send = merged(jnp.stack([bit[o[heads]] for o in orders]), keep, came)
        came = [flip_send(a, *cross[o[heads]]) for a, o in zip(send, orders)]
        out_up, out_down, out_output, notes = finished(keep, came, total, up_rows, own)
    out_bias_up = notes[0]
    out_vecs = notes[1:7, :own]
    near_bit = seq_n // 2
    while near_bit:
        grad_features = grad_features + flip_send(part[near_bit], "seq", near_bit).astype(f32)
        near_bit //= 2
    grad_w = lax.all_to_all(grad_w, ALL, split_axis=0, concat_axis=0, tiled=True)
    out_query, out_key, out_value, col_sums = unpacked_gradients(
        grad_w.reshape(dp_n, seq_n, ffn_n, own_pad + 8, lanes), own, width
    )
    row = lax.dynamic_index_in_dim(col_sums, here // share, keepdims=False)
    row = jnp.stack([row[heads * PAIR : heads * PAIR + group], row[: heads * PAIR].reshape(heads, 2, HEAD_DIM)[:, 1].reshape(group)])
    out_b = lax.dynamic_slice(row, (0, here % share * own), (2, own))
    return (
        out[None],
        grad_features[None],
        out_query,
        out_key,
        out_value,
        out_output,
        out_b[0],
        out_b[1],
        out_vecs[0],
        out_up,
        out_bias_up,
        out_down,
        out_vecs[1],
        out_vecs[2],
        out_vecs[3],
        out_vecs[4],
        out_vecs[5],
    )


def solution(mesh):
    return jax.shard_map(
        shards,
        mesh=mesh,
        in_specs=(
            P(("dp", "ffn"), "seq", None),
            P(("dp", "seq", "ffn"), None),
            P(("dp", "seq", "ffn"), None),
            P(("dp", "seq", "ffn"), None),
            P(("dp", "seq", "ffn"), None),
            P(("dp", "seq", "ffn")),
            P(("dp", "seq", "ffn")),
            P(("dp", "seq", "ffn")),
            P(("dp", "seq"), "ffn"),
            P("ffn"),
            P(("dp", "seq"), "ffn"),
            P(("dp", "seq", "ffn")),
            P(("dp", "seq", "ffn")),
            P(("dp", "seq", "ffn")),
            P(("dp", "seq", "ffn")),
            P(("dp", "seq", "ffn")),
            P(("dp", "ffn"), None),
            P(("dp", "ffn"), "seq", None, None),
            P(("dp", "ffn"), None),
            P(("dp", "ffn"), "seq", None),
        ),
        out_specs=(
            P(("dp", "ffn"), "seq", None),
            P(("dp", "ffn"), "seq", None),
            P(("dp", "seq", "ffn"), None),
            P(("dp", "seq", "ffn"), None),
            P(("dp", "seq", "ffn"), None),
            P(("dp", "seq", "ffn"), None),
            P(("dp", "seq", "ffn")),
            P(("dp", "seq", "ffn")),
            P(("dp", "seq", "ffn")),
            P(("dp", "seq"), "ffn"),
            P("ffn"),
            P(("dp", "seq"), "ffn"),
            P(("dp", "seq", "ffn")),
            P(("dp", "seq", "ffn")),
            P(("dp", "seq", "ffn")),
            P(("dp", "seq", "ffn")),
            P(("dp", "seq", "ffn")),
        ),
        check_vma=False,
    )
```

```python
import functools
import jax
import jax.numpy as jnp
from jax import lax
from jax.experimental import pallas as pl
from jax.sharding import PartitionSpec as P
from jax.experimental.pallas import tpu as pltpu

HEAD_DIM = 64
BLOCK = 64
PAIR = 2 * BLOCK
MASKED = -1e30
bf16 = jnp.bfloat16
f32 = jnp.float32


def dot_nn(a, b):
    return lax.dot_general(a, b, (((1,), (0,)), ((), ())), preferred_element_type=f32)


def dot_nt(a, b):
    return lax.dot_general(a, b, (((1,), (1,)), ((), ())), preferred_element_type=f32)


def dot_tn(a, b):
    return lax.dot_general(a, b, (((0,), (0,)), ((), ())), preferred_element_type=f32)


def pair_table(rand_local, global_ids, flip, nblocks):
    heads = rand_local.shape[0]
    null = nblocks
    first = (2 * jnp.arange(nblocks // 2, dtype=jnp.int32)) ^ flip

    def near(block):
        bad = (block < 0) | (block >= nblocks) | (block == global_ids[0]) | (block == global_ids[1])
        return jnp.where(bad, null, block ^ flip)

    rand_first = rand_local[:, first, :] ^ flip
    rand_second = rand_local[:, first + 1, :] ^ flip
    nears = jnp.stack([near(first), near(first + 1), near(first - 1), near(first + 2)], axis=1)
    nears = jnp.broadcast_to(nears[None], (heads,) + nears.shape)
    return jnp.concatenate(
        [nears[:, :, 0:3], rand_first, nears[:, :, 3:4], rand_second], axis=2
    ).astype(jnp.int32).reshape(-1)


def slots(tab_ref, gl_ref, head, pair, npairs):
    at = (head * npairs + pair) * 10
    got = [pl.multiple_of(tab_ref[at + j] * BLOCK, BLOCK) for j in range(10)]
    glob = [pl.multiple_of(gl_ref[j] * BLOCK, BLOCK) for j in range(2)]
    return got[0:2] + glob, got[2:6], got[6:10]


def stack_rows(ref, offsets, lanes):
    return jnp.concatenate([ref[pl.ds(o, BLOCK), lanes] for o in offsets], axis=0)


def lane_halves(width, dtype):
    lane = lax.broadcasted_iota(jnp.int32, (1, width), 1) % PAIR
    first = (lane < BLOCK).astype(dtype)
    second = (lane >= BLOCK).astype(dtype)
    return first, second


UNROLL = 4
BACK_UNROLL = 4
APART = 64
VMEM_BYTES = 62 << 20


def head_lanes(h):
    return slice(h * PAIR, (h + 1) * PAIR)


def query_columns(q_ref, mask_ref, h, at):
    return jnp.concatenate([q_ref[h * BLOCK : (h + 1) * BLOCK, pl.ds(at, PAIR)], mask_ref[:, pl.ds(at, PAIR)]], axis=0)


def global_queries(q_ref, mask_ref, h, gl_ref):
    return jnp.concatenate(
        [
            global_columns(q_ref, slice(h * BLOCK, (h + 1) * BLOCK), gl_ref),
            global_columns(mask_ref, slice(0, BLOCK), gl_ref),
        ],
        axis=0,
    ).astype(bf16)


def global_columns(src_ref, rows, gl_ref):
    lane = lax.broadcasted_iota(jnp.int32, (1, PAIR), 1)
    parts = []
    for g in range(2):
        block = gl_ref[g]
        at = pl.multiple_of((block // 2) * PAIR, PAIR)
        both = src_ref[rows, pl.ds(at, PAIR)].astype(f32)
        moved = pltpu.roll(both, BLOCK, 1)
        parts.append(jnp.where(block % 2 == g, both, moved))
    return jnp.where(lane < BLOCK, parts[0], parts[1])


def put_global_columns(dst_ref, rows, gl_ref, value, per_chunk):
    lane = lax.broadcasted_iota(jnp.int32, (1, PAIR), 1)
    moved = pltpu.roll(value, BLOCK, 1)
    for g in range(2):
        block = gl_ref[g]
        pair = block // 2
        half = block % 2
        chunk = pair // per_chunk
        at = pl.multiple_of((pair % per_chunk) * PAIR, PAIR)
        src = jnp.where(half == g, value, moved)
        old = dst_ref[chunk, rows, pl.ds(at, PAIR)].astype(f32)
        new = jnp.where((lane >= BLOCK) == (half == 1), src, old)
        dst_ref[chunk, rows, pl.ds(at, PAIR)] = new.astype(dst_ref.dtype)


def project_rows(x, seg, w_ref, wq, bkv_ref, bq_ref, k_ref, v_ref, q_ref, mask_ref, at):
    n = x.shape[0]
    lanes = v_ref.shape[1]
    y = dot_nn(x, w_ref[:, 0:lanes]) + bkv_ref[...]
    spot = lax.broadcasted_iota(jnp.int32, (PAIR, n), 0) - BLOCK
    mark = jnp.transpose((spot == seg).astype(f32), (1, 0))
    lane = lax.broadcasted_iota(jnp.int32, (1, PAIR), 1)
    rows = pl.ds(at, n)
    v_ref[rows, :] = y.astype(bf16)
    for h in range(lanes // PAIR):
        k_ref[rows, head_lanes(h)] = jnp.where(lane < BLOCK, y[:, head_lanes(h)], mark).astype(bf16)
    z = (dot_nt(wq, x) + bq_ref[...]).astype(bf16)
    q_ref[:, rows] = (z.astype(f32) * HEAD_DIM ** -0.5).astype(bf16)
    row = lax.broadcasted_iota(jnp.int32, (BLOCK, n), 0)
    mask_ref[:, rows] = jnp.where((row <= 16) & (row != seg), MASKED, 0.0).astype(bf16)


def query_weights(w_ref, heads):
    at = heads * PAIR
    cols = w_ref[:, at : at + 2 * PAIR].astype(f32)
    return jnp.transpose(cols, (1, 0))[0 : heads * HEAD_DIM].astype(bf16)


def forward_kernel(heads, chunks, tab_ref, gl_ref, *refs):
    x_refs = refs[0:chunks]
    seg_ref, w_ref, bkv_ref, bq_ref = refs[chunks : chunks + 4]
    out_refs = refs[chunks + 4 : 2 * chunks + 4]
    lse_ref, lseg_ref, k_sc, v_sc, q_sc, mask_sc, s_sc, out_ref = refs[2 * chunks + 4 :]
    rows = x_refs[0].shape[0]
    length = rows * chunks
    npairs = length // PAIR
    per_chunk = npairs // chunks
    tile = 256
    wq = query_weights(w_ref, heads)
    for c in range(chunks):

        @pl.loop(0, rows // tile)
        def _(t):
            at = pl.multiple_of(t * tile, tile)
            project_rows(
                x_refs[c][pl.ds(at, tile), :], seg_ref[c : c + 1, pl.ds(at, tile)], w_ref, wq, bkv_ref, bq_ref,
                k_sc, v_sc, q_sc, mask_sc, pl.multiple_of(c * rows + t * tile, tile),
            )

    null_lane = lax.broadcasted_iota(jnp.int32, (BLOCK, heads * PAIR), 1) % PAIR
    k_sc[pl.ds(length, BLOCK), :] = (null_lane == BLOCK + 16).astype(f32).astype(bf16)
    v_sc[pl.ds(length, BLOCK), :] = jnp.zeros((BLOCK, heads * PAIR), bf16)
    first, second = lane_halves(PAIR, bf16)
    lane = lax.broadcasted_iota(jnp.int32, (1, PAIR), 1)

    def one_pair(pair):
        chunk = pair // per_chunk
        local = pl.multiple_of((pair % per_chunk) * PAIR, PAIR)
        at = pl.multiple_of(pair * PAIR, PAIR)
        for h in range(heads):
            shared, mine, other = slots(tab_ref, gl_ref, h, pair, npairs)
            kl = head_lanes(h)
            q = query_columns(q_sc, mask_sc, h, at)
            s_sh = dot_nn(stack_rows(k_sc, shared, kl), q)
            k_pr = jnp.concatenate([stack_rows(k_sc, mine, kl), stack_rows(k_sc, other, kl)], axis=1)
            s_pr = dot_nn(k_pr, jnp.concatenate([q * first, q * second], axis=0))
            peak = jnp.maximum(jnp.max(s_sh, axis=0, keepdims=True), jnp.max(s_pr, axis=0, keepdims=True))
            e_sh = jnp.exp(s_sh - peak)
            e_pr = jnp.exp(s_pr - peak)
            total = jnp.sum(e_sh, axis=0, keepdims=True) + jnp.sum(e_pr, axis=0, keepdims=True)
            inv = 1.0 / total
            p_sh = (e_sh * inv).astype(bf16)
            p_pr = (e_pr * inv).astype(bf16)
            v_pr = jnp.concatenate([stack_rows(v_sc, mine, kl), stack_rows(v_sc, other, kl)], axis=1)
            o_sh = dot_tn(stack_rows(v_sc, shared, kl), p_sh)
            o_pr = dot_tn(v_pr, p_pr)
            ctx = o_sh[BLOCK:PAIR] + jnp.where(lane < BLOCK, o_pr[BLOCK:PAIR], o_pr[PAIR + BLOCK : 2 * PAIR])
            out_ref[chunk, h * BLOCK : (h + 1) * BLOCK, pl.ds(local, PAIR)] = ctx.astype(bf16)
            lse_ref[h, pl.ds(pair, 1), :] = peak + jnp.log(total)

    @pl.loop(0, npairs // UNROLL)
    def _(some):
        for i in range(UNROLL):
            one_pair(UNROLL * some + i)

    step = 512
    queries = [global_queries(q_sc, mask_sc, h, gl_ref) for h in range(heads)]

    def score(c, peaks):
        at = pl.multiple_of(c * step, step)
        new = []
        for h in range(heads):
            got = dot_nn(k_sc[pl.ds(at, step), head_lanes(h)], queries[h])
            s_sc[h, pl.ds(at, step), :] = got
            new.append(jnp.maximum(peaks[h], jnp.max(got, axis=0, keepdims=True)))
        return tuple(new)

    peaks = lax.fori_loop(0, length // step, score, (jnp.full((1, PAIR), MASKED, f32),) * heads)

    def gather(c, carry):
        at = pl.multiple_of(c * step, step)
        new = []
        for h in range(heads):
            total, ctx = carry[h]
            e = jnp.exp(s_sc[h, pl.ds(at, step), :] - peaks[h])
            ctx = ctx + dot_tn(v_sc[pl.ds(at, step), head_lanes(h)], e.astype(bf16))
            new.append((total + jnp.sum(e, axis=0, keepdims=True), ctx))
        return tuple(new)

    start = (jnp.zeros((1, PAIR), f32), jnp.zeros((PAIR, PAIR), f32))
    sums = lax.fori_loop(0, length // step, gather, (start,) * heads)
    for h in range(heads):
        total, ctx = sums[h]
        ctx = ctx[BLOCK:PAIR] * (1.0 / total)
        put_global_columns(out_ref, slice(h * BLOCK, (h + 1) * BLOCK), gl_ref, ctx, per_chunk)
        lseg_ref[h : h + 1, :] = peaks[h] + jnp.log(total)
    for c in range(chunks):
        out_refs[c][...] = out_ref[c]


def attention_forward(tab, gl, x, seg, w, b_kv, b_q):
    chunks = len(x)
    rows = x[0].shape[0]
    length = rows * chunks
    heads = b_q.shape[0] // HEAD_DIM
    whole = lambda: pl.BlockSpec(memory_space=pltpu.VMEM)
    got = pl.pallas_call(
        functools.partial(forward_kernel, heads, chunks),
        out_shape=(jax.ShapeDtypeStruct((heads * HEAD_DIM, rows), bf16),) * chunks
        + (
            jax.ShapeDtypeStruct((heads, length // PAIR, PAIR), f32),
            jax.ShapeDtypeStruct((heads, PAIR), f32),
            jax.ShapeDtypeStruct((length + BLOCK, heads * PAIR), bf16),
            jax.ShapeDtypeStruct((length + BLOCK, heads * PAIR), bf16),
            jax.ShapeDtypeStruct((heads * HEAD_DIM, length), bf16),
            jax.ShapeDtypeStruct((BLOCK, length), bf16),
        ),
        in_specs=[pl.BlockSpec(memory_space=pltpu.SMEM)] * 2 + [whole() for _ in range(chunks + 4)],
        out_specs=tuple(whole() for _ in range(chunks + 6)),
        scratch_shapes=[
            pltpu.VMEM((heads, length, PAIR), f32),
            pltpu.VMEM((chunks, heads * HEAD_DIM, rows), bf16),
        ],
        compiler_params=pltpu.CompilerParams(vmem_limit_bytes=VMEM_BYTES),
        cost_estimate=pl.CostEstimate(flops=12_000_000_000, bytes_accessed=16_000_000, transcendentals=8_000_000),
        name="attention_forward",
    )(tab, gl, *x, seg, w, b_kv, b_q)
    return got[:chunks], got[chunks:]


def backward_kernel(heads, chunks, tab_ref, gl_ref, *refs):
    do_refs = refs[:chunks]
    (k_ref, kv_ref, q_ref, mask_ref, seg_ref, lse_ref, lseg_ref, w_ref, resid_ref, dq_ref, dkv_ref, first_ref) = refs[
        chunks : chunks + 12
    ]
    part_refs = refs[chunks + 12 : 2 * chunks + 11]
    do_sc, acc, p_sc, d_sc, seg_sc, line_sc = refs[2 * chunks + 11 :]
    rows = do_refs[0].shape[1]
    length = rows * chunks
    npairs = length // PAIR
    per_chunk = npairs // chunks
    scale = HEAD_DIM ** -0.5
    for c in range(chunks):
        do_sc[:, c * rows : (c + 1) * rows] = do_refs[c][...]
        for t in range(per_chunk):
            line = seg_ref[c : c + 1, t * PAIR : (t + 1) * PAIR].astype(f32)
            line_sc[c * per_chunk + t] = line
            to = c * rows + t * PAIR
            seg_sc[to : to + PAIR, :] = jnp.transpose(jnp.broadcast_to(line, (PAIR, PAIR)), (1, 0))
    seg_sc[length : length + BLOCK, :] = jnp.full((BLOCK, PAIR), -1.0, f32)
    first2, second2 = lane_halves(2 * PAIR, bf16)
    ffirst, fsecond = lane_halves(PAIR, f32)
    lane = lax.broadcasted_iota(jnp.int32, (1, PAIR), 1)
    line_row = lax.broadcasted_iota(jnp.int32, (PAIR, 1), 0)
    zeros = jnp.zeros((BLOCK, PAIR), bf16)
    blank = jnp.zeros((PAIR, PAIR), bf16)

    def head_rows(h):
        return slice(h * BLOCK, (h + 1) * BLOCK)

    def joint(q, mask, do):
        left = jnp.concatenate([q, mask, blank], axis=0)
        right = jnp.concatenate([blank, zeros, do], axis=0)
        return jnp.concatenate([left, right], axis=1)

    def sources(q, do):
        top = jnp.concatenate([q, zeros], axis=1)
        return jnp.concatenate([top, jnp.concatenate([zeros, do], axis=1)], axis=0)

    step = 512
    mask_glob = global_columns(mask_ref, slice(0, BLOCK), gl_ref).astype(bf16)
    q_glob = [global_columns(q_ref, head_rows(h), gl_ref).astype(bf16) for h in range(heads)]
    do_glob = [global_columns(do_sc, head_rows(h), gl_ref).astype(bf16) for h in range(heads)]

    def weigh(c, deltas):
        at = pl.multiple_of(c * step, step)
        new = []
        for h in range(heads):
            left = jnp.concatenate([k_ref[pl.ds(at, step), head_lanes(h)], kv_ref[pl.ds(at, step), head_lanes(h)]], axis=1)
            both = dot_nn(left, joint(q_glob[h], mask_glob, do_glob[h]))
            p = jnp.exp(both[:, 0:PAIR] - lseg_ref[h : h + 1, :])
            dp = both[:, PAIR:]
            p_sc[h, pl.ds(at, step), :] = p
            d_sc[h, pl.ds(at, step), :] = dp
            new.append(deltas[h] + jnp.sum(p * dp, axis=0, keepdims=True))
        return tuple(new)

    deltas = lax.fori_loop(0, length // step, weigh, (jnp.zeros((1, PAIR), f32),) * heads)

    def spread(c, dqs):
        at = pl.multiple_of(c * step, step)
        new = []
        for h in range(heads):
            p = p_sc[h, pl.ds(at, step), :]
            ds = (p * (d_sc[h, pl.ds(at, step), :] - deltas[h])).astype(bf16)
            both = jnp.concatenate([ds, p.astype(bf16)], axis=1)
            acc[h, pl.ds(at, step), :] = dot_nt(both, sources(q_glob[h], do_glob[h]))
            new.append(dqs[h] + dot_tn(k_ref[pl.ds(at, step), head_lanes(h)], ds))
        return tuple(new)

    dqs = lax.fori_loop(0, length // step, spread, (jnp.zeros((PAIR, PAIR), f32),) * heads)
    for h in range(heads):
        acc[h, pl.ds(length, BLOCK), :] = jnp.zeros((BLOCK, PAIR), f32)

    def one_pair(pair):
        chunk = pair // per_chunk
        local = pl.multiple_of((pair % per_chunk) * PAIR, PAIR)
        at = pl.multiple_of(pair * PAIR, PAIR)
        hit_first = (gl_ref[0] == 2 * pair) | (gl_ref[1] == 2 * pair)
        hit_second = (gl_ref[0] == 2 * pair + 1) | (gl_ref[1] == 2 * pair + 1)
        shut = ffirst * jnp.where(hit_first, -MASKED, 0.0) + fsecond * jnp.where(hit_second, -MASKED, 0.0)
        every = slice(0, PAIR)
        for h in range(heads):
            kl = head_lanes(h)
            shared, mine, other = slots(tab_ref, gl_ref, h, pair, npairs)
            q = q_ref[head_rows(h), pl.ds(at, PAIR)]
            do = do_sc[head_rows(h), pl.ds(at, PAIR)]
            lse = lse_ref[h, pl.ds(pair, 1), :] + shut
            src = sources(q, do)
            src2 = jnp.concatenate([src * first2, src * second2], axis=0)
            k_sh = stack_rows(k_ref, shared, kl)
            two_sh = dot_nn(
                jnp.concatenate([k_sh, stack_rows(kv_ref, shared, kl)], axis=1),
                joint(q, mask_ref[:, pl.ds(at, PAIR)], do),
            )
            kv_pr = jnp.concatenate([stack_rows(kv_ref, mine, kl), stack_rows(kv_ref, other, kl)], axis=1)
            two_pr = dot_nn(kv_pr, src2)
            seg_pr = jnp.where(lane < BLOCK, stack_rows(seg_sc, mine, every), stack_rows(seg_sc, other, every))
            agree = seg_pr == line_sc[pair]
            p_sh = jnp.exp(two_sh[:, 0:PAIR] - lse)
            p_pr = jnp.where(agree, jnp.exp(two_pr[:, 0:PAIR] - lse), 0.0)
            d_sh, d_pr = two_sh[:, PAIR:], two_pr[:, PAIR:]
            delta = jnp.sum(p_sh * d_sh, axis=0, keepdims=True) + jnp.sum(p_pr * d_pr, axis=0, keepdims=True)
            ds_sh = (p_sh * (d_sh - delta)).astype(bf16)
            ds_pr = (p_pr * (d_pr - delta)).astype(bf16)
            g_sh = dot_nt(jnp.concatenate([ds_sh, p_sh.astype(bf16)], axis=1), src)
            g_pr = dot_nt(jnp.concatenate([ds_pr, p_pr.astype(bf16)], axis=1), src2)
            for j, o in enumerate(shared):
                acc[h, pl.ds(o, BLOCK), :] += g_sh[j * BLOCK : (j + 1) * BLOCK]
            for j, o in enumerate(mine):
                acc[h, pl.ds(o, BLOCK), :] += g_pr[j * BLOCK : (j + 1) * BLOCK, 0:PAIR]
            for j, o in enumerate(other):
                acc[h, pl.ds(o, BLOCK), :] += g_pr[j * BLOCK : (j + 1) * BLOCK, PAIR:]
            t_pr = dot_tn(ds_pr, kv_pr)
            dq = dot_tn(ds_sh, k_sh) + jnp.where(line_row < BLOCK, t_pr[:, 0:PAIR], t_pr[:, PAIR:])
            dq = jnp.transpose(dq, (1, 0))[0:BLOCK]
            dq_ref[chunk, head_rows(h), pl.ds(local, PAIR)] = (dq * scale).astype(bf16)

    @pl.loop(0, npairs // BACK_UNROLL)
    def _(some):
        for i in range(BACK_UNROLL):
            one_pair(BACK_UNROLL * some + i)

    for h in range(heads):
        put_global_columns(dq_ref, head_rows(h), gl_ref, dqs[h][0:BLOCK] * scale, per_chunk)
        for c in range(chunks):
            dkv_ref[c, :, head_lanes(h)] = acc[h, pl.ds(c * rows, rows), :].astype(bf16)
    tile = 256
    wq = query_weights(w_ref, heads)
    for c in range(chunks):

        @pl.loop(0, rows // tile)
        def _(t):
            at = pl.multiple_of(t * tile, tile)
            got = dot_tn(dq_ref[c, :, pl.ds(at, tile)], wq)
            got = got + dot_nt(dkv_ref[c, pl.ds(at, tile), :], w_ref[:, 0 : heads * PAIR])
            if c == 0:
                first_ref[pl.ds(at, tile), :] = resid_ref[pl.ds(at, tile), :] + got
            else:
                part_refs[c - 1][pl.ds(at, tile), :] = got.astype(bf16)


def attention_backward(tab, gl, do, k, kv, q, mask, seg, lse, lseg, w, resid):
    chunks = len(do)
    group, rows = do[0].shape
    heads = group // HEAD_DIM
    width = w.shape[0]
    length = rows * chunks
    whole = lambda: pl.BlockSpec(memory_space=pltpu.VMEM)
    return pl.pallas_call(
        functools.partial(backward_kernel, heads, chunks),
        out_shape=(
            jax.ShapeDtypeStruct((chunks, group, rows), bf16),
            jax.ShapeDtypeStruct((chunks, rows, heads * PAIR), bf16),
            jax.ShapeDtypeStruct((rows, width), f32),
        )
        + (jax.ShapeDtypeStruct((rows, width), bf16),) * (chunks - 1),
        in_specs=[pl.BlockSpec(memory_space=pltpu.SMEM)] * 2 + [whole() for _ in range(chunks + 9)],
        out_specs=tuple(whole() for _ in range(chunks + 2)),
        scratch_shapes=[
            pltpu.VMEM((group, length), bf16),
            pltpu.VMEM((heads, length + BLOCK, PAIR), f32),
            pltpu.VMEM((heads, length, PAIR), f32),
            pltpu.VMEM((heads, length, PAIR), f32),
            pltpu.VMEM((length + BLOCK, PAIR), f32),
            pltpu.VMEM((length // PAIR, 1, PAIR), f32),
        ],
        compiler_params=pltpu.CompilerParams(vmem_limit_bytes=VMEM_BYTES),
        cost_estimate=pl.CostEstimate(flops=30_000_000_000, bytes_accessed=24_000_000, transcendentals=8_000_000),
        name="attention_backward",
    )(tab, gl, *do, k, kv, q, mask, seg, lse, lseg, w, resid)


def round_up(value, to):
    return -(-value // to) * to


def half_columns(ref, index, place):
    at = index // 2 * PAIR
    both = ref[:, at : at + PAIR].astype(f32)
    return both if index % 2 == place else pltpu.roll(both, BLOCK, 1)


def two_halves(first, second):
    lane = lax.broadcasted_iota(jnp.int32, (1, PAIR), 1)
    return jnp.where(lane < BLOCK, first, second)


def pack_kernel(seq_n, wq_ref, wk_ref, wv_ref, wo_ref, up_ref, down_ref, bup_ref, vec_ref, pack_ref, rest_ref):
    own, width = wq_ref.shape
    heads = width // HEAD_DIM // seq_n
    blocks, inner = pack_ref.shape[0], pack_ref.shape[2]
    for s in range(seq_n):
        pieces = [
            two_halves(half_columns(wk_ref, s * heads + h, 0), half_columns(wv_ref, s * heads + h, 1))
            for h in range(heads)
        ]
        for h in range(0, heads, 2):
            second = half_columns(wq_ref, s * heads + h + 1, 1) if h + 1 < heads else jnp.zeros((own, PAIR), f32)
            pieces.append(two_halves(half_columns(wq_ref, s * heads + h, 0), second))
        piece = jnp.concatenate(pieces, axis=1).astype(bf16)
        notes = jnp.concatenate([vec_ref[...], jnp.zeros((8, piece.shape[1] - width), bf16)], axis=1) if (
            piece.shape[1] > width
        ) else vec_ref[:, 0 : piece.shape[1]]
        for b in range(blocks):
            for i in range(inner):
                pack_ref[b, s, i, 0:own, :] = piece
                pack_ref[b, s, i, own : own + 8, :] = notes
    u = up_ref.shape[0]
    rest_ref[0:u, :] = up_ref[...]
    rest_ref[u : 2 * u, :] = down_ref[...]
    rest_ref[2 * u : 2 * u + own, :] = wo_ref[...]
    row = lax.broadcasted_iota(jnp.int32, (8, 1), 0)
    block = jnp.where(row == 7, bup_ref[...].astype(f32), vec_ref[...].astype(f32))
    rest_ref[2 * u + own : 2 * u + own + 8, :] = block.astype(bf16)


def packed_weights(w_q, w_k, w_v, w_o, w_up, w_down, b_up, vec, dp_n, seq_n, ffn_n):
    own, width = w_q.shape
    heads = width // HEAD_DIM // seq_n
    lanes = heads * PAIR + round_up(heads * HEAD_DIM, PAIR)
    u = w_up.shape[0]
    if own % 8 or u % 16:
        group = heads * HEAD_DIM
        cols = lambda w: w.reshape(own, seq_n, heads, HEAD_DIM).transpose(1, 0, 2, 3)
        kv = jnp.stack([cols(w_k), cols(w_v)], axis=3).reshape(seq_n, own, 2 * group)
        piece = jnp.concatenate([kv, cols(w_q).reshape(seq_n, own, group)], axis=2)
        piece = jnp.pad(piece, ((0, 0), (0, round_up(own, 8) - own), (0, lanes - 3 * group)))
        notes = jnp.broadcast_to(vec[None, :, :lanes], (seq_n, 8, lanes))
        piece = jnp.concatenate([piece, notes], axis=1)
        pack = jnp.broadcast_to(piece[None, :, None], (dp_n, seq_n, ffn_n) + piece.shape[1:])
        w_o = jnp.pad(w_o, ((0, round_up(own, 8) - own), (0, 0)))
        return pack, jnp.concatenate([w_up, w_down, w_o, vec[:7], b_up], axis=0)
    whole = lambda: pl.BlockSpec(memory_space=pltpu.VMEM)
    return pl.pallas_call(
        functools.partial(pack_kernel, seq_n),
        out_shape=(
            jax.ShapeDtypeStruct((dp_n, seq_n, ffn_n, own + 8, lanes), bf16),
            jax.ShapeDtypeStruct((2 * u + own + 8, width), bf16),
        ),
        in_specs=[whole() for _ in range(8)],
        out_specs=(whole(), whole()),
        name="packed_weights",
    )(w_q, w_k, w_v, w_o, w_up, w_down, b_up, vec)


def weights_kernel(chunks, direct, *refs):
    x_refs = refs[:chunks]
    dq_ref, dkv_ref, out_ref, sums_ref, acc = refs[chunks:]
    group, rows = dq_ref.shape[1], dq_ref.shape[2]
    lanes = dkv_ref.shape[2]
    ones = jnp.ones((8, rows), bf16)
    sum_q = jnp.zeros((8, group), f32)
    sum_kv = jnp.zeros((8, lanes), f32)
    acc[lanes + group :, :] = jnp.zeros((acc.shape[0] - lanes - group, acc.shape[1]), f32)
    for c in range(chunks):
        x = x_refs[c][...]
        got_kv = dot_tn(dkv_ref[c], x)
        got_q = dot_nn(dq_ref[c], x)
        if c == 0:
            acc[0:lanes, :] = got_kv
            acc[lanes : lanes + group, :] = got_q
        else:
            acc[0:lanes, :] += got_kv
            acc[lanes : lanes + group, :] += got_q
        sum_q = sum_q + dot_nt(ones, dq_ref[c])
        sum_kv = sum_kv + dot_nn(ones, dkv_ref[c])
    grad = jnp.transpose(acc[...], (1, 0))
    blank = jnp.zeros((8, acc.shape[0] - lanes - group), f32)
    sums = jnp.concatenate([sum_kv, sum_q, blank], axis=1)
    sums_ref[...] = sums
    if direct:
        blocks, per, _ = out_ref.shape
        own = per - 8
        grad = grad.astype(f32).reshape(blocks, own, acc.shape[0])
        for b in range(blocks):
            out_ref[b, 0:own, :] = grad[b].astype(bf16)
            out_ref[b, own:, :] = sums.astype(bf16)
    else:
        out_ref[...] = grad.astype(bf16)


def projection_gradients(x, dq, dkv, own, devices):
    chunks, group, rows = dq.shape
    width = x[0].shape[1]
    lanes = dkv.shape[2]
    full = lanes + round_up(group, PAIR)
    direct = own % 8 == 0
    whole = lambda: pl.BlockSpec(memory_space=pltpu.VMEM)
    out, sums = pl.pallas_call(
        functools.partial(weights_kernel, chunks, direct),
        out_shape=(
            jax.ShapeDtypeStruct((devices, own + 8, full) if direct else (width, full), bf16),
            jax.ShapeDtypeStruct((8, full), f32),
        ),
        in_specs=[whole() for _ in range(chunks + 2)],
        out_specs=(whole(), whole()),
        scratch_shapes=[pltpu.VMEM((full, width), f32)],
        compiler_params=pltpu.CompilerParams(vmem_limit_bytes=VMEM_BYTES),
        cost_estimate=pl.CostEstimate(flops=4_000_000_000, bytes_accessed=12_000_000, transcendentals=0),
        name="projection_gradients",
    )(*x, dq, dkv)
    if not direct:
        out = jnp.pad(out.reshape(devices, own, full), ((0, 0), (0, round_up(own, 8) - own), (0, 0)))
        out = jnp.concatenate([out, jnp.broadcast_to(sums[None].astype(bf16), (devices, 8, full))], axis=1)
    return out


def unpack_kernel(own, got_ref, q_ref, k_ref, v_ref, sums_ref, tot):
    dp_n, seq_n, ffn_n, per, full = got_ref.shape
    width = q_ref.shape[1]
    heads = width // HEAD_DIM // seq_n
    for s in range(seq_n):
        total = jnp.zeros((per, full), f32)
        for d in range(dp_n):
            for f in range(ffn_n):
                total = total + got_ref[d, s, f].astype(f32)
        tot[s] = total
        sums_ref[s : s + 1, :] = total[per - 8 : per - 7, :]
    for w in range(width // PAIR):
        spots = [((2 * w + i) // heads, (2 * w + i) % heads) for i in range(2)]
        cols = slice(w * PAIR, (w + 1) * PAIR)
        for ref, where in (
            (k_ref, lambda h: 2 * h),
            (v_ref, lambda h: 2 * h + 1),
            (q_ref, lambda h: 2 * heads + h),
        ):
            both = [half_columns(tot.at[g], where(h), i) for i, (g, h) in enumerate(spots)]
            ref[:, cols] = two_halves(*both)[0:own]


def unpacked_gradients(got, own, width):
    dp_n, seq_n, ffn_n, per, full = got.shape
    whole = lambda: pl.BlockSpec(memory_space=pltpu.VMEM)
    return pl.pallas_call(
        functools.partial(unpack_kernel, own),
        out_shape=(jax.ShapeDtypeStruct((own, width), f32),) * 3 + (jax.ShapeDtypeStruct((seq_n, full), f32),),
        in_specs=[whole()],
        out_specs=tuple(whole() for _ in range(4)),
        scratch_shapes=[pltpu.VMEM((seq_n, per, full), f32)],
        compiler_params=pltpu.CompilerParams(vmem_limit_bytes=VMEM_BYTES),
        name="unpacked_gradients",
    )(got)


NORM_EPS = 1e-12


def transposed(value):
    return jnp.transpose(value.astype(f32), (1, 0)).astype(bf16)


def unit_rows(value):
    center = value - jnp.mean(value, axis=-1, keepdims=True)
    scale = lax.rsqrt(jnp.mean(center * center, axis=-1, keepdims=True) + NORM_EPS)
    return center * scale, scale


def unit_rows_back(grad, unit, scale):
    return scale * (
        grad - jnp.mean(grad, axis=-1, keepdims=True) - unit * jnp.mean(grad * unit, axis=-1, keepdims=True)
    )


def rows_kernel(parts, blocks, up_rows, me_ref, *refs):
    ctx_refs = refs[:parts]
    (x_ref, cot_ref, rest_ref, wo_ref, vec_ref, bup_ref, out_ref, resid_ref, hid_ref, pre_ref, nlt_ref, gft_ref,
     gb_ref) = refs[parts : parts + 13]
    do_refs = refs[parts + 13 : 2 * parts + 13]
    sums_ref, gbup_ref, slope_sc = refs[2 * parts + 13 :]
    group = ctx_refs[0].shape[0]
    width = x_ref.shape[1]

    def up(f):
        return rest_ref[:, f, 0:up_rows, :].reshape(width, rest_ref.shape[3])

    def down(f):
        return rest_ref[:, f, up_rows : 2 * up_rows, :].reshape(width, rest_ref.shape[3])

    def own_rows(k):
        return pl.ds(pl.multiple_of((me_ref[0] ^ k) * group, group), group)

    @pl.when(pl.program_id(0) == 0)
    def _():
        sums_ref[...] = jnp.zeros_like(sums_ref)
        gbup_ref[...] = jnp.zeros_like(gbup_ref)

    ctx = jnp.concatenate([r[...] for r in ctx_refs], axis=0)
    w_o = jnp.concatenate([wo_ref[own_rows(k), :] for k in range(parts)], axis=0)
    resid_one = x_ref[...].astype(f32) + (dot_tn(ctx, w_o) + vec_ref[0:1, :])
    unit_one, scale_one = unit_rows(resid_one)
    normed_one = unit_one * vec_ref[2:3, :] + vec_ref[3:4, :]
    low = normed_one.astype(bf16)
    nlt_ref[...] = transposed(normed_one)
    total = normed_one + vec_ref[1:2, :]
    pre = dot_nn(low, up(0)) + bup_ref[0:1, :]
    for f in range(blocks):
        later = dot_nn(low, up(f + 1)) + bup_ref[f + 1 : f + 2, :] if f + 1 < blocks else None
        phi = 0.5 + 0.5 * lax.erf(pre * (0.5 ** 0.5))
        slope_sc[f] = phi + pre * (jnp.exp(-0.5 * pre * pre) * 0.3989422804014327)
        hid = (pre * phi).astype(bf16)
        hid_ref[f] = hid
        total = total + dot_nt(hid, down(f))
        pre = later
    unit_two, scale_two = unit_rows(total)
    out_ref[...] = (unit_two * vec_ref[4:5, :] + vec_ref[5:6, :]).astype(bf16)
    cot = cot_ref[...].astype(f32)
    grad_two = unit_rows_back(cot * vec_ref[4:5, :], unit_two, scale_two)
    grad_ffn = grad_two.astype(bf16)
    gft_ref[...] = transposed(grad_two)
    grad_normed = grad_two
    back = dot_nn(grad_ffn, down(0))
    for f in range(blocks):
        later = dot_nn(grad_ffn, down(f + 1)) if f + 1 < blocks else None
        grad_pre = (back * slope_sc[f]).astype(bf16)
        pre_ref[f] = grad_pre
        gbup_ref[f : f + 1, :] += jnp.sum(grad_pre.astype(f32), axis=0, keepdims=True)
        grad_normed = grad_normed + dot_nt(grad_pre, up(f))
        back = later
    resid = unit_rows_back(grad_normed * vec_ref[2:3, :], unit_one, scale_one)
    resid_ref[...] = resid
    branch = resid.astype(bf16)
    gb_ref[...] = branch
    do = dot_nt(w_o, branch).astype(bf16)
    for k in range(parts):
        do_refs[k][...] = do[k * group : (k + 1) * group]
    for row, value in enumerate(
        (branch.astype(f32), grad_ffn.astype(f32), grad_normed * unit_one, grad_normed, cot * unit_two, cot)
    ):
        sums_ref[row : row + 1, :] += jnp.sum(value, axis=0, keepdims=True)


def rows_chain(me, ctx_parts, x, cot, rest, up_rows, w_o, vecs, bias_up):
    parts = len(ctx_parts)
    group, rows = ctx_parts[0].shape
    width = x.shape[1]
    outer, blocks, per, hidden = rest.shape
    tile = 256
    once = lambda shape: pl.BlockSpec(shape, lambda i: (0,) * len(shape), pipeline_mode=pl.Buffered(1))
    tall = pl.BlockSpec((tile, width), lambda i: (i, 0))
    wide = pl.BlockSpec((width, tile), lambda i: (0, i))
    cube = pl.BlockSpec((blocks, tile, hidden), lambda i: (0, i, 0))
    return pl.pallas_call(
        functools.partial(rows_kernel, parts, blocks, up_rows),
        grid=(rows // tile,),
        out_shape=(
            jax.ShapeDtypeStruct((rows, width), bf16),
            jax.ShapeDtypeStruct((rows, width), f32),
            jax.ShapeDtypeStruct((blocks, rows, hidden), bf16),
            jax.ShapeDtypeStruct((blocks, rows, hidden), bf16),
            jax.ShapeDtypeStruct((width, rows), bf16),
            jax.ShapeDtypeStruct((width, rows), bf16),
            jax.ShapeDtypeStruct((rows, width), bf16),
        )
        + (jax.ShapeDtypeStruct((group, rows), bf16),) * parts
        + (jax.ShapeDtypeStruct((8, width), f32), jax.ShapeDtypeStruct((8, hidden), f32)),
        in_specs=[pl.BlockSpec(memory_space=pltpu.SMEM)]
        + [pl.BlockSpec((group, tile), lambda i: (0, i))] * parts
        + [tall, tall, once(rest.shape), once(w_o.shape), once(vecs.shape), once(bias_up.shape)],
        out_specs=(
            tall, tall, cube, cube, wide, wide, tall,
        )
        + (pl.BlockSpec((group, tile), lambda i: (0, i)),) * parts
        + (pl.BlockSpec((8, width), lambda i: (0, 0)), pl.BlockSpec((8, hidden), lambda i: (0, 0))),
        scratch_shapes=[pltpu.VMEM((blocks, tile, hidden), f32)],
        compiler_params=pltpu.CompilerParams(vmem_limit_bytes=VMEM_BYTES),
        cost_estimate=pl.CostEstimate(flops=22_000_000_000, bytes_accessed=40_000_000, transcendentals=6_000_000),
        name="rows_chain",
    )(me, *ctx_parts, x, cot, rest, w_o, vecs, bias_up)


def outer_kernel(parts, up_rows, own, apart, me_ref, *refs):
    ctx_refs = refs[:parts]
    nlt_ref, gft_ref, gb_ref, pre_ref, hid_ref, small_ref, out_ref = refs[parts : parts + 7]
    wo_sc = refs[-1]
    slabs, hidden = out_ref.shape[0], out_ref.shape[3]
    group = ctx_refs[0].shape[0]
    f = pl.program_id(0)
    up = dot_nn(nlt_ref[...], pre_ref[0]).astype(bf16).reshape(slabs, up_rows, hidden)
    if apart:
        refs[parts + 7][:, 0, :, :] = up[:, 0:apart]
    out_ref[:, 0, 0 : up_rows - apart, :] = up[:, apart:]
    at = up_rows - apart
    down = dot_nn(gft_ref[...], hid_ref[0]).astype(bf16)
    out_ref[:, 0, at : at + up_rows, :] = down.reshape(slabs, up_rows, hidden)
    at += up_rows
    if not own:
        return

    @pl.when(f == 0)
    def _():
        for k in range(parts):
            wo_sc[k] = dot_nn(ctx_refs[k][...], gb_ref[...])

    share = slabs // parts
    stride = group // share
    for k in range(parts):
        for j in range(share):
            rows = pl.ds(pl.multiple_of(j * stride + f * own, 8), own)
            out_ref[(me_ref[0] ^ k) * share + j, 0, at : at + own, :] = wo_sc[k, rows, :].astype(bf16)
    out_ref[:, 0, at + own :, :] = small_ref[:, 0]


def outer_products(me, ctx_parts, nlt, gft, gb, pre, hid, small, slabs, up_rows, own, apart):
    blocks, rows, hidden = pre.shape
    parts = len(ctx_parts)
    group = ctx_parts[0].shape[0]
    per = 2 * up_rows - apart + (own + 8 if own else 0)
    sizes = (per, apart) if apart else (per,)
    once = lambda shape: pl.BlockSpec(shape, lambda i: (0,) * len(shape), pipeline_mode=pl.Buffered(1))
    return pl.pallas_call(
        functools.partial(outer_kernel, parts, up_rows, own, apart),
        grid=(blocks,),
        out_shape=tuple(jax.ShapeDtypeStruct((slabs, blocks, r, hidden), bf16) for r in sizes),
        in_specs=[pl.BlockSpec(memory_space=pltpu.SMEM)]
        + [once(c.shape) for c in ctx_parts]
        + [
            once(nlt.shape),
            once(gft.shape),
            once(gb.shape),
            pl.BlockSpec((1, rows, hidden), lambda i: (i, 0, 0)),
            pl.BlockSpec((1, rows, hidden), lambda i: (i, 0, 0)),
            pl.BlockSpec((small.shape[0], 1) + small.shape[2:], lambda i: (0, i, 0, 0)),
        ],
        out_specs=tuple(pl.BlockSpec((slabs, 1, r, hidden), lambda i: (0, i, 0, 0)) for r in sizes),
        scratch_shapes=[pltpu.VMEM((parts, group, gb.shape[1]), f32)],
        compiler_params=pltpu.CompilerParams(vmem_limit_bytes=VMEM_BYTES),
        cost_estimate=pl.CostEstimate(flops=11_000_000_000, bytes_accessed=28_000_000, transcendentals=0),
        name="outer_products",
    )(me, *ctx_parts, nlt, gft, gb, pre, hid, small)


def finish_kernel(up_rows, own, apart_ref, total_ref, up_ref, down_ref, wo_ref, small_ref):
    apart = apart_ref.shape[1]
    total = jnp.zeros(apart_ref.shape[1:], f32)
    for d in range(apart_ref.shape[0]):
        total = total + apart_ref[d].astype(f32)
    up_ref[0:apart, :] = total
    rest = total_ref[...].astype(f32)
    at = up_rows - apart
    up_ref[apart:, :] = rest[0:at]
    down_ref[...] = rest[at : at + up_rows]
    at += up_rows
    wo_ref[...] = rest[at : at + own]
    small_ref[...] = rest[at + own : at + own + 8]


def finished(apart, total, up_rows, own):
    hidden = total.shape[1]
    whole = lambda: pl.BlockSpec(memory_space=pltpu.VMEM)
    return pl.pallas_call(
        functools.partial(finish_kernel, up_rows, own),
        out_shape=tuple(jax.ShapeDtypeStruct((r, hidden), f32) for r in (up_rows, up_rows, own, 8)),
        in_specs=[whole(), whole()],
        out_specs=tuple(whole() for _ in range(4)),
        name="finished",
    )(apart, total)


ALL = ("dp", "seq", "ffn")


def flip_send(array, axis, bits):
    count = lax.axis_size(axis)
    return lax.ppermute(array, axis, [(i, i ^ bits) for i in range(count)])


def shards(
    tokens, w_query, w_key, w_value, w_output, b_query, b_value, b_output, w_up, b_up, w_down, b_down,
    gain_attn, shift_attn, gain_ffn, shift_ffn, segment_ids, random_blocks, global_blocks, cotangent,
):
    seq_n, dp_n, ffn_n = lax.axis_size("seq"), lax.axis_size("dp"), lax.axis_size("ffn")
    outer, devices = dp_n * seq_n, dp_n * seq_n * ffn_n
    me = lax.axis_index("seq")
    here = (lax.axis_index("dp") * seq_n + me) * ffn_n + lax.axis_index("ffn")
    own, width = w_query.shape
    own_pad = round_up(own, 8)
    group = width // seq_n
    heads = group // HEAD_DIM
    features = tokens[0]
    rows = features.shape[0]
    order = jnp.stack([me ^ k for k in range(seq_n)])
    me_ref = me.astype(jnp.int32)[None]

    near = [features] + [None] * (seq_n - 1)
    for k in sorted(range(1, seq_n), key=lambda k: (k & (k - 1), -k)):
        bit = k & -k
        near[k] = flip_send(features if bit == k else near[k ^ bit], "seq", bit)

    vec = jnp.stack([b_output, b_down, gain_attn, shift_attn, gain_ffn, shift_ffn, b_query, b_value])
    vec = jnp.pad(vec, ((0, 0), (0, width - own)))
    seg = segment_ids[0].reshape(seq_n, rows)[order]
    nblocks = seq_n * rows // BLOCK
    flip = me.astype(jnp.int32) * (nblocks // seq_n)
    tab = pair_table(random_blocks[0], global_blocks[0], flip, nblocks)
    gl = global_blocks[0] ^ flip
    pack, rest = packed_weights(
        w_query, w_key, w_value, w_output, w_up, w_down, b_up[None], vec, dp_n, seq_n, ffn_n
    )
    lanes = pack.shape[4]
    pack, seg, tab, gl = lax.optimization_barrier((pack, seg, tab, gl))
    pack = lax.all_to_all(
        pack.reshape(devices, own_pad + 8, lanes), ALL, split_axis=0, concat_axis=0, tiled=True
    )
    rest = lax.all_gather(rest, ALL, axis=0, tiled=False)
    w_own = pack[:, :own].reshape(width, lanes)
    share = devices // seq_n
    biases = lax.dynamic_slice(pack, (share * me, own_pad + 6, 0), (share, 2, own))
    biases = biases.transpose(1, 0, 2).reshape(2, group).astype(f32)
    by_head = biases[1].reshape(heads, 1, HEAD_DIM)
    b_kv = jnp.concatenate([jnp.zeros_like(by_head), by_head], axis=1).reshape(1, heads * PAIR)

    ctx, (lse, lseg, k_all, v_all, q_all, mask_all) = attention_forward(
        tab, gl, near, seg, w_own, b_kv, biases[0][:, None]
    )
    ctx_parts = [ctx[0]] + [flip_send(ctx[k], "seq", k) for k in range(1, seq_n)]

    up_rows = w_up.shape[0]
    at = 2 * up_rows
    rest = rest.reshape(outer, ffn_n, rest.shape[1], width)
    w_o = rest[:, :, at : at + own].reshape(width, width)
    bias_up = rest[0, :, at + own_pad + 7].astype(f32)
    vecs = rest[:, :, at + own_pad :, :own].transpose(2, 0, 1, 3).reshape(8, width).astype(f32)
    direct = up_rows % 16 == 0 and own % 8 == 0 and outer % seq_n == 0 and (outer // seq_n) * ffn_n * own == group
    if not direct:
        rest = rest[:, :, :at].reshape(outer, ffn_n, 2, up_rows, width).transpose(1, 2, 0, 3, 4)
        rest = rest.reshape(1, ffn_n, 2 * outer * up_rows, width)
    slabs, slab_rows = (outer, up_rows) if direct else (1, outer * up_rows)

    got = rows_chain(me_ref, ctx_parts, features, cotangent[0], rest, slab_rows, w_o, vecs, bias_up)
    out, grad_resid_one, hidden, grad_pre, normed_t, grad_ffn_t, grad_branch = got[:7]
    grad_ctx, (sums, grad_bias_up) = got[7 : 7 + seq_n], got[7 + seq_n :]
    do = [grad_ctx[0]] + [flip_send(grad_ctx[k], "seq", k) for k in range(1, seq_n)]

    vec_grads = sums[:6].astype(bf16).reshape(6, outer, ffn_n, own).transpose(1, 2, 0, 3)
    vec_grads = jnp.pad(vec_grads, ((0, 0), (0, 0), (0, 1), (0, width - own)))
    top = jnp.broadcast_to(grad_bias_up[None, :ffn_n, None].astype(bf16), (outer, ffn_n, 1, width))
    small = jnp.concatenate([top, vec_grads], axis=2)
    payload = outer_products(
        me_ref, ctx_parts, normed_t, grad_ffn_t, grad_branch, grad_pre, hidden, small, slabs, slab_rows,
        own if direct else 0, APART if direct else 0,
    )
    payload, apart = payload if direct else (payload[0], None)
    if not direct:
        grad_out = dot_nn(jnp.concatenate(ctx_parts, axis=0), grad_branch).astype(bf16)
        grad_out = grad_out.reshape(seq_n, group, width)[order].reshape(outer, ffn_n, own, width)
        payload = payload.reshape(ffn_n, 2, outer, up_rows, width).transpose(2, 0, 1, 3, 4)
        payload = jnp.concatenate([payload.reshape(outer, ffn_n, at, width), grad_out, small], axis=2)
        payload = jnp.pad(payload, ((0, 0), (0, 0), (0, -payload.shape[2] % 32), (0, 0)))
    payload, apart, do = lax.optimization_barrier((payload, apart, do))
    total = lax.psum_scatter(payload.reshape(-1, width), ALL, scatter_dimension=0, tiled=True)
    if direct:
        apart = lax.all_to_all(
            apart.reshape(devices, APART, width), ALL, split_axis=0, concat_axis=0, tiled=True
        )

    got = attention_backward(tab, gl, do, k_all, v_all, q_all, mask_all, seg, lse, lseg, w_own, grad_resid_one)
    dq, dkv, grad_features = got[:3]
    part = [None] + list(got[3:])
    bit = 1
    while bit < seq_n:
        for k in range(seq_n):
            if k & -k == bit and k != bit:
                came = flip_send(part[k], "seq", bit).astype(f32)
                part[k ^ bit] = (part[k ^ bit].astype(f32) + came).astype(bf16)
        bit *= 2
    grad_w = projection_gradients(near, dq, dkv, own, devices)
    grad_w, part = lax.optimization_barrier((grad_w, part[1:]))
    grad_w, apart = lax.optimization_barrier((grad_w, apart))
    part = [None] + part
    bit = seq_n // 2
    while bit:
        grad_features = grad_features + flip_send(part[bit], "seq", bit).astype(f32)
        bit //= 2
    grad_w = lax.all_to_all(grad_w, ALL, split_axis=0, concat_axis=0, tiled=True)
    if direct:
        out_up, out_down, out_output, notes = finished(apart, total, up_rows, own)
    else:
        total = total.astype(f32)
        out_up, out_down, out_output = total[:up_rows], total[up_rows:at], total[at : at + own]
        notes = total[at + own : at + own + 8]
    out_bias_up = notes[0]
    out_vecs = notes[1:7, :own]
    out_query, out_key, out_value, col_sums = unpacked_gradients(
        grad_w.reshape(dp_n, seq_n, ffn_n, own_pad + 8, lanes), own, width
    )
    row = lax.dynamic_index_in_dim(col_sums, here // share, keepdims=False)
    row = jnp.stack([row[heads * PAIR : heads * PAIR + group], row[: heads * PAIR].reshape(heads, 2, HEAD_DIM)[:, 1].reshape(group)])
    out_b = lax.dynamic_slice(row, (0, here % share * own), (2, own))
    return (
        out[None],
        grad_features[None],
        out_query,
        out_key,
        out_value,
        out_output,
        out_b[0],
        out_b[1],
        out_vecs[0],
        out_up,
        out_bias_up,
        out_down,
        out_vecs[1],
        out_vecs[2],
        out_vecs[3],
        out_vecs[4],
        out_vecs[5],
    )


def solution(mesh):
    return jax.shard_map(
        shards,
        mesh=mesh,
        in_specs=(
            P(("dp", "ffn"), "seq", None),
            P(("dp", "seq", "ffn"), None),
            P(("dp", "seq", "ffn"), None),
            P(("dp", "seq", "ffn"), None),
            P(("dp", "seq", "ffn"), None),
            P(("dp", "seq", "ffn")),
            P(("dp", "seq", "ffn")),
            P(("dp", "seq", "ffn")),
            P(("dp", "seq"), "ffn"),
            P("ffn"),
            P(("dp", "seq"), "ffn"),
            P(("dp", "seq", "ffn")),
            P(("dp", "seq", "ffn")),
            P(("dp", "seq", "ffn")),
            P(("dp", "seq", "ffn")),
            P(("dp", "seq", "ffn")),
            P(("dp", "ffn"), None),
            P(("dp", "ffn"), "seq", None, None),
            P(("dp", "ffn"), None),
            P(("dp", "ffn"), "seq", None),
        ),
        out_specs=(
            P(("dp", "ffn"), "seq", None),
            P(("dp", "ffn"), "seq", None),
            P(("dp", "seq", "ffn"), None),
            P(("dp", "seq", "ffn"), None),
            P(("dp", "seq", "ffn"), None),
            P(("dp", "seq", "ffn"), None),
            P(("dp", "seq", "ffn")),
            P(("dp", "seq", "ffn")),
            P(("dp", "seq", "ffn")),
            P(("dp", "seq"), "ffn"),
            P("ffn"),
            P(("dp", "seq"), "ffn"),
            P(("dp", "seq", "ffn")),
            P(("dp", "seq", "ffn")),
            P(("dp", "seq", "ffn")),
            P(("dp", "seq", "ffn")),
            P(("dp", "seq", "ffn")),
        ),
        check_vma=False,
    )
```

```python
import functools
import jax
import jax.numpy as jnp
from jax import lax
from jax.experimental import pallas as pl
from jax.sharding import PartitionSpec as P
from jax.experimental.pallas import tpu as pltpu

HEAD_DIM = 64
BLOCK = 64
PAIR = 2 * BLOCK
MASKED = -1e30
bf16 = jnp.bfloat16
f32 = jnp.float32


def dot_nn(a, b):
    return lax.dot_general(a, b, (((1,), (0,)), ((), ())), preferred_element_type=f32)


def dot_nt(a, b):
    return lax.dot_general(a, b, (((1,), (1,)), ((), ())), preferred_element_type=f32)


def dot_tn(a, b):
    return lax.dot_general(a, b, (((0,), (0,)), ((), ())), preferred_element_type=f32)


def slots(rand_ref, glob_ref, flip, head, pair, nblocks):
    first = (2 * pair) ^ flip

    def row(block):
        return pl.multiple_of(block * BLOCK, BLOCK)

    def near(block):
        bad = (block < 0) | (block >= nblocks) | (block == glob_ref[0, 0]) | (block == glob_ref[0, 1])
        return row(jnp.where(bad, nblocks, block ^ flip))

    def drawn(block):
        at = (head * nblocks + block) * 3
        return [row(rand_ref[at + j] ^ flip) for j in range(3)]

    shared = [near(first), near(first + 1)] + [row(glob_ref[0, j] ^ flip) for j in range(2)]
    return shared, [near(first - 1)] + drawn(first), [near(first + 2)] + drawn(first + 1)


def stack_rows(ref, offsets, lanes):
    return jnp.concatenate([ref[pl.ds(o, BLOCK), lanes] for o in offsets], axis=0)


def lane_halves(width, dtype):
    lane = lax.broadcasted_iota(jnp.int32, (1, width), 1) % PAIR
    first = (lane < BLOCK).astype(dtype)
    second = (lane >= BLOCK).astype(dtype)
    return first, second


UNROLL = 4
BACK_UNROLL = 2
APART = 32
VMEM_BYTES = 62 << 20


def head_lanes(h):
    return slice(h * PAIR, (h + 1) * PAIR)


def query_columns(q_ref, mask_ref, h, at):
    return jnp.concatenate([q_ref[h * BLOCK : (h + 1) * BLOCK, pl.ds(at, PAIR)], mask_ref[:, pl.ds(at, PAIR)]], axis=0)


def global_queries(q_ref, mask_ref, h, gl):
    return jnp.concatenate(
        [
            global_columns(q_ref, slice(h * BLOCK, (h + 1) * BLOCK), gl),
            global_columns(mask_ref, slice(0, BLOCK), gl),
        ],
        axis=0,
    ).astype(bf16)


def placed(me_ref, glob_ref, nblocks, chunks):
    flip = me_ref[0] * (nblocks // chunks)
    return flip, [glob_ref[0, j] ^ flip for j in range(2)]


def global_columns(src_ref, rows, gl):
    lane = lax.broadcasted_iota(jnp.int32, (1, PAIR), 1)
    parts = []
    for g in range(2):
        block = gl[g]
        at = pl.multiple_of((block // 2) * PAIR, PAIR)
        both = src_ref[rows, pl.ds(at, PAIR)].astype(f32)
        moved = pltpu.roll(both, BLOCK, 1)
        parts.append(jnp.where(block % 2 == g, both, moved))
    return jnp.where(lane < BLOCK, parts[0], parts[1])


def put_global_columns(dst_ref, rows, gl, value, per_chunk, low, high):
    lane = lax.broadcasted_iota(jnp.int32, (1, PAIR), 1)
    moved = pltpu.roll(value, BLOCK, 1)
    for g in range(2):
        pair = gl[g] // 2
        half = gl[g] % 2
        chunk = pair // per_chunk

        @pl.when((chunk >= low) & (chunk < high))
        def _():
            at = pl.multiple_of((pair % per_chunk) * PAIR, PAIR)
            src = jnp.where(half == g, value, moved)
            old = dst_ref[chunk - low, rows, pl.ds(at, PAIR)].astype(f32)
            new = jnp.where((lane >= BLOCK) == (half == 1), src, old)
            dst_ref[chunk - low, rows, pl.ds(at, PAIR)] = new.astype(dst_ref.dtype)


def project_rows(x, seg, w_ref, wq, bkv_ref, bq_ref, k_ref, v_ref, q_ref, mask_ref, at):
    n = x.shape[0]
    lanes = v_ref.shape[1]
    y = dot_nn(x, w_ref[:, 0:lanes]) + bkv_ref[...]
    spot = lax.broadcasted_iota(jnp.int32, (PAIR, n), 0) - BLOCK
    mark = jnp.transpose((spot == seg).astype(f32), (1, 0))
    lane = lax.broadcasted_iota(jnp.int32, (1, PAIR), 1)
    rows = pl.ds(at, n)
    v_ref[rows, :] = y.astype(bf16)
    for h in range(lanes // PAIR):
        k_ref[rows, head_lanes(h)] = jnp.where(lane < BLOCK, y[:, head_lanes(h)], mark).astype(bf16)
    z = (dot_nt(wq, x) + bq_ref[...]).astype(bf16)
    q_ref[:, rows] = (z.astype(f32) * HEAD_DIM ** -0.5).astype(bf16)
    row = lax.broadcasted_iota(jnp.int32, (BLOCK, n), 0)
    mask_ref[:, rows] = jnp.where((row <= 16) & (row != seg), MASKED, 0.0).astype(bf16)


def query_weights(w_ref, heads):
    at = heads * PAIR
    cols = w_ref[:, at : at + 2 * PAIR].astype(f32)
    return jnp.transpose(cols, (1, 0))[0 : heads * HEAD_DIM].astype(bf16)


def sparse_forward(heads, low, high, per_chunk, rand_ref, glob_ref, flip, k_ref, kv_ref, q_ref, mask_ref, out_ref, lse_ref):
    nblocks = (k_ref.shape[0] - BLOCK) // BLOCK
    first, second = lane_halves(PAIR, bf16)
    lane = lax.broadcasted_iota(jnp.int32, (1, PAIR), 1)

    def one_pair(spot):
        chunk = spot // per_chunk
        local = pl.multiple_of((spot % per_chunk) * PAIR, PAIR)
        pair = low * per_chunk + spot
        at = pl.multiple_of(pair * PAIR, PAIR)
        for h in range(heads):
            shared, mine, other = slots(rand_ref, glob_ref, flip, h, pair, nblocks)
            kl = head_lanes(h)
            q = query_columns(q_ref, mask_ref, h, at)
            s_sh = dot_nn(stack_rows(k_ref, shared, kl), q)
            k_pr = jnp.concatenate([stack_rows(k_ref, mine, kl), stack_rows(k_ref, other, kl)], axis=1)
            s_pr = dot_nn(k_pr, jnp.concatenate([q * first, q * second], axis=0))
            peak = jnp.maximum(jnp.max(s_sh, axis=0, keepdims=True), jnp.max(s_pr, axis=0, keepdims=True))
            e_sh = jnp.exp(s_sh - peak)
            e_pr = jnp.exp(s_pr - peak)
            total = jnp.sum(e_sh, axis=0, keepdims=True) + jnp.sum(e_pr, axis=0, keepdims=True)
            inv = 1.0 / total
            p_sh = (e_sh * inv).astype(bf16)
            p_pr = (e_pr * inv).astype(bf16)
            v_pr = jnp.concatenate([stack_rows(kv_ref, mine, kl), stack_rows(kv_ref, other, kl)], axis=1)
            o_sh = dot_tn(stack_rows(kv_ref, shared, kl), p_sh)
            o_pr = dot_tn(v_pr, p_pr)
            ctx = o_sh[BLOCK:PAIR] + jnp.where(lane < BLOCK, o_pr[BLOCK:PAIR], o_pr[PAIR + BLOCK : 2 * PAIR])
            out_ref[chunk, h * BLOCK : (h + 1) * BLOCK, pl.ds(local, PAIR)] = ctx.astype(bf16)
            lse_ref[h, pl.ds(spot, 1), :] = peak + jnp.log(total)

    @pl.loop(0, (high - low) * per_chunk // UNROLL)
    def _(some):
        for i in range(UNROLL):
            one_pair(UNROLL * some + i)


def forward_kernel(heads, chunks, me_ref, rand_ref, glob_ref, *refs):
    x_refs = refs[0:chunks]
    seg_ref, w_ref, bkv_ref, bq_ref = refs[chunks : chunks + 4]
    far = chunks // 2
    out_refs = refs[chunks + 4 : chunks + 4 + far]
    lse_ref, lseg_ref, glob_ctx_ref, k_sc, v_sc, q_sc, mask_sc, s_sc, out_ref, seg_sc = refs[chunks + 4 + far :]
    rows = x_refs[0].shape[0]
    length = rows * chunks
    per_chunk = length // PAIR // chunks
    flip, gl = placed(me_ref, glob_ref, length // BLOCK, chunks)
    tile = 256
    wq = query_weights(w_ref, heads)
    for c in range(chunks):
        seg_sc[c : c + 1, :] = seg_ref[pl.ds(me_ref[0] ^ c, 1), :]
    for c in range(chunks):

        @pl.loop(0, rows // tile)
        def _(t):
            at = pl.multiple_of(t * tile, tile)
            project_rows(
                x_refs[c][pl.ds(at, tile), :], seg_sc[c : c + 1, pl.ds(at, tile)], w_ref, wq, bkv_ref, bq_ref,
                k_sc, v_sc, q_sc, mask_sc, pl.multiple_of(c * rows + t * tile, tile),
            )

    null_lane = lax.broadcasted_iota(jnp.int32, (BLOCK, heads * PAIR), 1) % PAIR
    k_sc[pl.ds(length, BLOCK), :] = (null_lane == BLOCK + 16).astype(f32).astype(bf16)
    v_sc[pl.ds(length, BLOCK), :] = jnp.zeros((BLOCK, heads * PAIR), bf16)
    sparse_forward(heads, far, chunks, per_chunk, rand_ref, glob_ref, flip, k_sc, v_sc, q_sc, mask_sc, out_ref, lse_ref)

    step = 512
    queries = [global_queries(q_sc, mask_sc, h, gl) for h in range(heads)]

    def score(c, peaks):
        at = pl.multiple_of(c * step, step)
        new = []
        for h in range(heads):
            got = dot_nn(k_sc[pl.ds(at, step), head_lanes(h)], queries[h])
            s_sc[h, pl.ds(at, step), :] = got
            new.append(jnp.maximum(peaks[h], jnp.max(got, axis=0, keepdims=True)))
        return tuple(new)

    peaks = lax.fori_loop(0, length // step, score, (jnp.full((1, PAIR), MASKED, f32),) * heads)

    def gather(c, carry):
        at = pl.multiple_of(c * step, step)
        new = []
        for h in range(heads):
            total, ctx = carry[h]
            e = jnp.exp(s_sc[h, pl.ds(at, step), :] - peaks[h])
            ctx = ctx + dot_tn(v_sc[pl.ds(at, step), head_lanes(h)], e.astype(bf16))
            new.append((total + jnp.sum(e, axis=0, keepdims=True), ctx))
        return tuple(new)

    start = (jnp.zeros((1, PAIR), f32), jnp.zeros((PAIR, PAIR), f32))
    sums = lax.fori_loop(0, length // step, gather, (start,) * heads)
    for h in range(heads):
        total, ctx = sums[h]
        ctx = ctx[BLOCK:PAIR] * (1.0 / total)
        glob_ctx_ref[h] = ctx
        put_global_columns(out_ref, slice(h * BLOCK, (h + 1) * BLOCK), gl, ctx, per_chunk, far, chunks)
        lseg_ref[h : h + 1, :] = peaks[h] + jnp.log(total)
    for c in range(far):
        out_refs[c][...] = out_ref[c]


def attention_forward(me, rand, glob, x, seg, w, b_kv, b_q):
    chunks = len(x)
    far = chunks // 2
    rows = x[0].shape[0]
    length = rows * chunks
    heads = b_q.shape[0] // HEAD_DIM
    whole = lambda: pl.BlockSpec(memory_space=pltpu.VMEM)
    got = pl.pallas_call(
        functools.partial(forward_kernel, heads, chunks),
        out_shape=(jax.ShapeDtypeStruct((heads * HEAD_DIM, rows), bf16),) * far
        + (
            jax.ShapeDtypeStruct((heads, length // PAIR // 2, PAIR), f32),
            jax.ShapeDtypeStruct((heads, PAIR), f32),
            jax.ShapeDtypeStruct((heads, HEAD_DIM, PAIR), f32),
            jax.ShapeDtypeStruct((length + BLOCK, heads * PAIR), bf16),
            jax.ShapeDtypeStruct((length + BLOCK, heads * PAIR), bf16),
            jax.ShapeDtypeStruct((heads * HEAD_DIM, length), bf16),
            jax.ShapeDtypeStruct((BLOCK, length), bf16),
        ),
        in_specs=[pl.BlockSpec(memory_space=pltpu.SMEM)] * 3 + [whole() for _ in range(chunks + 4)],
        out_specs=tuple(whole() for _ in range(far + 7)),
        scratch_shapes=[
            pltpu.VMEM((heads, length, PAIR), f32),
            pltpu.VMEM((far, heads * HEAD_DIM, rows), bf16),
            pltpu.VMEM((chunks, rows), jnp.int32),
        ],
        compiler_params=pltpu.CompilerParams(vmem_limit_bytes=VMEM_BYTES),
        cost_estimate=pl.CostEstimate(flops=10_000_000_000, bytes_accessed=16_000_000, transcendentals=6_000_000),
        name="attention_forward",
    )(me, rand, glob, *x, seg, w, b_kv, b_q)
    return got[:far], got[far:]


def near_kernel(heads, chunks, me_ref, rand_ref, glob_ref, k_ref, kv_ref, q_ref, mask_ref, glob_ctx_ref, *refs):
    half = chunks // 2
    out_refs = refs[:half]
    lse_ref, out_ref = refs[half:]
    length = q_ref.shape[1]
    per_chunk = length // PAIR // chunks
    flip, gl = placed(me_ref, glob_ref, length // BLOCK, chunks)
    sparse_forward(heads, 0, half, per_chunk, rand_ref, glob_ref, flip, k_ref, kv_ref, q_ref, mask_ref, out_ref, lse_ref)
    for h in range(heads):
        put_global_columns(out_ref, slice(h * BLOCK, (h + 1) * BLOCK), gl, glob_ctx_ref[h], per_chunk, 0, half)
    for c in range(half):
        out_refs[c][...] = out_ref[c]


def attention_near(me, rand, glob, k, kv, q, mask, glob_ctx, chunks):
    heads = glob_ctx.shape[0]
    half = chunks // 2
    length = q.shape[1]
    rows = length // chunks
    whole = lambda: pl.BlockSpec(memory_space=pltpu.VMEM)
    got = pl.pallas_call(
        functools.partial(near_kernel, heads, chunks),
        out_shape=(jax.ShapeDtypeStruct((heads * HEAD_DIM, rows), bf16),) * half
        + (jax.ShapeDtypeStruct((heads, length // PAIR // 2, PAIR), f32),),
        in_specs=[pl.BlockSpec(memory_space=pltpu.SMEM)] * 3 + [whole() for _ in range(5)],
        out_specs=tuple(whole() for _ in range(half + 1)),
        scratch_shapes=[pltpu.VMEM((half, heads * HEAD_DIM, rows), bf16)],
        compiler_params=pltpu.CompilerParams(vmem_limit_bytes=VMEM_BYTES),
        cost_estimate=pl.CostEstimate(flops=6_000_000_000, bytes_accessed=9_000_000, transcendentals=3_000_000),
        name="attention_near",
    )(me, rand, glob, k, kv, q, mask, glob_ctx)
    return got[:half], got[half]


def backward_kernel(heads, chunks, me_ref, rand_ref, glob_ref, *refs):
    do_refs = refs[:chunks]
    (k_ref, kv_ref, q_ref, mask_ref, seg_ref, lse_near_ref, lse_far_ref, lseg_ref, w_ref, resid_ref, dq_ref, dkv_ref,
     first_ref) = refs[chunks : chunks + 13]
    part_refs = refs[chunks + 13 : 2 * chunks + 12]
    do_sc, acc, p_sc, d_sc, seg_sc, line_sc, lse_ref, row_sc = refs[2 * chunks + 12 :]
    rows = do_refs[0].shape[1]
    length = rows * chunks
    npairs = length // PAIR
    per_chunk = npairs // chunks
    scale = HEAD_DIM ** -0.5
    flip, gl = placed(me_ref, glob_ref, length // BLOCK, chunks)
    lse_ref[:, 0 : npairs // 2, :] = lse_near_ref[...]
    lse_ref[:, npairs // 2 :, :] = lse_far_ref[...]
    for c in range(chunks):
        do_sc[:, c * rows : (c + 1) * rows] = do_refs[c][...]
        row_sc[c : c + 1, :] = seg_ref[pl.ds(me_ref[0] ^ c, 1), :].astype(f32)

        @pl.loop(0, per_chunk // 4)
        def _(some):
            for i in range(4):
                t = 4 * some + i
                line = row_sc[c : c + 1, pl.ds(pl.multiple_of(t * PAIR, PAIR), PAIR)]
                line_sc[c * per_chunk + t] = line
                to = pl.multiple_of(c * rows + t * PAIR, PAIR)
                seg_sc[pl.ds(to, PAIR), :] = jnp.transpose(jnp.broadcast_to(line, (PAIR, PAIR)), (1, 0))

    seg_sc[length : length + BLOCK, :] = jnp.full((BLOCK, PAIR), -1.0, f32)
    first2, second2 = lane_halves(2 * PAIR, bf16)
    ffirst, fsecond = lane_halves(PAIR, f32)
    lane = lax.broadcasted_iota(jnp.int32, (1, PAIR), 1)
    line_row = lax.broadcasted_iota(jnp.int32, (PAIR, 1), 0)
    zeros = jnp.zeros((BLOCK, PAIR), bf16)
    blank = jnp.zeros((PAIR, PAIR), bf16)

    def head_rows(h):
        return slice(h * BLOCK, (h + 1) * BLOCK)

    def joint(q, mask, do):
        left = jnp.concatenate([q, mask, blank], axis=0)
        right = jnp.concatenate([blank, zeros, do], axis=0)
        return jnp.concatenate([left, right], axis=1)

    def sources(q, do):
        top = jnp.concatenate([q, zeros], axis=1)
        return jnp.concatenate([top, jnp.concatenate([zeros, do], axis=1)], axis=0)

    step = 512
    mask_glob = global_columns(mask_ref, slice(0, BLOCK), gl).astype(bf16)
    q_glob = [global_columns(q_ref, head_rows(h), gl).astype(bf16) for h in range(heads)]
    do_glob = [global_columns(do_sc, head_rows(h), gl).astype(bf16) for h in range(heads)]

    def weigh(c, deltas):
        at = pl.multiple_of(c * step, step)
        new = []
        for h in range(heads):
            left = jnp.concatenate([k_ref[pl.ds(at, step), head_lanes(h)], kv_ref[pl.ds(at, step), head_lanes(h)]], axis=1)
            both = dot_nn(left, joint(q_glob[h], mask_glob, do_glob[h]))
            p = jnp.exp(both[:, 0:PAIR] - lseg_ref[h : h + 1, :])
            dp = both[:, PAIR:]
            p_sc[h, pl.ds(at, step), :] = p
            d_sc[h, pl.ds(at, step), :] = dp
            new.append(deltas[h] + jnp.sum(p * dp, axis=0, keepdims=True))
        return tuple(new)

    deltas = lax.fori_loop(0, length // step, weigh, (jnp.zeros((1, PAIR), f32),) * heads)

    def spread(c, dqs):
        at = pl.multiple_of(c * step, step)
        new = []
        for h in range(heads):
            p = p_sc[h, pl.ds(at, step), :]
            ds = (p * (d_sc[h, pl.ds(at, step), :] - deltas[h])).astype(bf16)
            both = jnp.concatenate([ds, p.astype(bf16)], axis=1)
            acc[h, pl.ds(at, step), :] = dot_nt(both, sources(q_glob[h], do_glob[h]))
            new.append(dqs[h] + dot_tn(k_ref[pl.ds(at, step), head_lanes(h)], ds))
        return tuple(new)

    dqs = lax.fori_loop(0, length // step, spread, (jnp.zeros((PAIR, PAIR), f32),) * heads)
    for h in range(heads):
        acc[h, pl.ds(length, BLOCK), :] = jnp.zeros((BLOCK, PAIR), f32)

    def one_pair(pair):
        chunk = pair // per_chunk
        local = pl.multiple_of((pair % per_chunk) * PAIR, PAIR)
        at = pl.multiple_of(pair * PAIR, PAIR)
        hit_first = (gl[0] == 2 * pair) | (gl[1] == 2 * pair)
        hit_second = (gl[0] == 2 * pair + 1) | (gl[1] == 2 * pair + 1)
        shut = ffirst * jnp.where(hit_first, -MASKED, 0.0) + fsecond * jnp.where(hit_second, -MASKED, 0.0)
        every = slice(0, PAIR)
        for h in range(heads):
            kl = head_lanes(h)
            shared, mine, other = slots(rand_ref, glob_ref, flip, h, pair, length // BLOCK)
            q = q_ref[head_rows(h), pl.ds(at, PAIR)]
            do = do_sc[head_rows(h), pl.ds(at, PAIR)]
            lse = lse_ref[h, pl.ds(pair, 1), :] + shut
            src = sources(q, do)
            src2 = jnp.concatenate([src * first2, src * second2], axis=0)
            k_sh = stack_rows(k_ref, shared, kl)
            two_sh = dot_nn(
                jnp.concatenate([k_sh, stack_rows(kv_ref, shared, kl)], axis=1),
                joint(q, mask_ref[:, pl.ds(at, PAIR)], do),
            )
            kv_pr = jnp.concatenate([stack_rows(kv_ref, mine, kl), stack_rows(kv_ref, other, kl)], axis=1)
            two_pr = dot_nn(kv_pr, src2)
            seg_pr = jnp.where(lane < BLOCK, stack_rows(seg_sc, mine, every), stack_rows(seg_sc, other, every))
            agree = seg_pr == line_sc[pair]
            p_sh = jnp.exp(two_sh[:, 0:PAIR] - lse)
            p_pr = jnp.where(agree, jnp.exp(two_pr[:, 0:PAIR] - lse), 0.0)
            d_sh, d_pr = two_sh[:, PAIR:], two_pr[:, PAIR:]
            delta = jnp.sum(p_sh * d_sh, axis=0, keepdims=True) + jnp.sum(p_pr * d_pr, axis=0, keepdims=True)
            ds_sh = (p_sh * (d_sh - delta)).astype(bf16)
            ds_pr = (p_pr * (d_pr - delta)).astype(bf16)
            g_sh = dot_nt(jnp.concatenate([ds_sh, p_sh.astype(bf16)], axis=1), src)
            g_pr = dot_nt(jnp.concatenate([ds_pr, p_pr.astype(bf16)], axis=1), src2)
            for j, o in enumerate(shared):
                acc[h, pl.ds(o, BLOCK), :] += g_sh[j * BLOCK : (j + 1) * BLOCK]
            for j, o in enumerate(mine):
                acc[h, pl.ds(o, BLOCK), :] += g_pr[j * BLOCK : (j + 1) * BLOCK, 0:PAIR]
            for j, o in enumerate(other):
                acc[h, pl.ds(o, BLOCK), :] += g_pr[j * BLOCK : (j + 1) * BLOCK, PAIR:]
            t_pr = dot_tn(ds_pr, kv_pr)
            dq = dot_tn(ds_sh, k_sh) + jnp.where(line_row < BLOCK, t_pr[:, 0:PAIR], t_pr[:, PAIR:])
            dq = jnp.transpose(dq, (1, 0))[0:BLOCK]
            dq_ref[chunk, head_rows(h), pl.ds(local, PAIR)] = (dq * scale).astype(bf16)

    @pl.loop(0, npairs // BACK_UNROLL)
    def _(some):
        for i in range(BACK_UNROLL):
            one_pair(BACK_UNROLL * some + i)

    for h in range(heads):
        put_global_columns(dq_ref, head_rows(h), gl, dqs[h][0:BLOCK] * scale, per_chunk, 0, chunks)
        for c in range(chunks):
            dkv_ref[c, :, head_lanes(h)] = acc[h, pl.ds(c * rows, rows), :].astype(bf16)
    tile = 256
    wq = query_weights(w_ref, heads)
    for c in range(chunks):

        @pl.loop(0, rows // tile)
        def _(t):
            at = pl.multiple_of(t * tile, tile)
            got = dot_tn(dq_ref[c, :, pl.ds(at, tile)], wq)
            got = got + dot_nt(dkv_ref[c, pl.ds(at, tile), :], w_ref[:, 0 : heads * PAIR])
            if c == 0:
                first_ref[pl.ds(at, tile), :] = resid_ref[pl.ds(at, tile), :] + got
            else:
                part_refs[c - 1][pl.ds(at, tile), :] = got.astype(bf16)


def attention_backward(me, rand, glob, do, k, kv, q, mask, seg, lse_near, lse_far, lseg, w, resid):
    chunks = len(do)
    group, rows = do[0].shape
    heads = group // HEAD_DIM
    width = w.shape[0]
    length = rows * chunks
    whole = lambda: pl.BlockSpec(memory_space=pltpu.VMEM)
    return pl.pallas_call(
        functools.partial(backward_kernel, heads, chunks),
        out_shape=(
            jax.ShapeDtypeStruct((chunks, group, rows), bf16),
            jax.ShapeDtypeStruct((chunks, rows, heads * PAIR), bf16),
            jax.ShapeDtypeStruct((rows, width), f32),
        )
        + (jax.ShapeDtypeStruct((rows, width), bf16),) * (chunks - 1),
        in_specs=[pl.BlockSpec(memory_space=pltpu.SMEM)] * 3 + [whole() for _ in range(chunks + 10)],
        out_specs=tuple(whole() for _ in range(chunks + 2)),
        scratch_shapes=[
            pltpu.VMEM((group, length), bf16),
            pltpu.VMEM((heads, length + BLOCK, PAIR), f32),
            pltpu.VMEM((heads, length, PAIR), f32),
            pltpu.VMEM((heads, length, PAIR), f32),
            pltpu.VMEM((length + BLOCK, PAIR), f32),
            pltpu.VMEM((length // PAIR, 1, PAIR), f32),
            pltpu.VMEM((heads, length // PAIR, PAIR), f32),
            pltpu.VMEM((chunks, rows), f32),
        ],
        compiler_params=pltpu.CompilerParams(vmem_limit_bytes=VMEM_BYTES),
        cost_estimate=pl.CostEstimate(flops=30_000_000_000, bytes_accessed=24_000_000, transcendentals=8_000_000),
        name="attention_backward",
    )(me, rand, glob, *do, k, kv, q, mask, seg, lse_near, lse_far, lseg, w, resid)


def round_up(value, to):
    return -(-value // to) * to


def half_columns(ref, index, place):
    at = index // 2 * PAIR
    both = ref[:, at : at + PAIR].astype(f32)
    return both if index % 2 == place else pltpu.roll(both, BLOCK, 1)


def two_halves(first, second):
    lane = lax.broadcasted_iota(jnp.int32, (1, PAIR), 1)
    return jnp.where(lane < BLOCK, first, second)


def pack_kernel(seq_n, wq_ref, wk_ref, wv_ref, wo_ref, up_ref, down_ref, bup_ref, vec_ref, pack_ref, rest_ref):
    own, width = wq_ref.shape
    heads = width // HEAD_DIM // seq_n
    blocks, inner = pack_ref.shape[0], pack_ref.shape[2]
    for s in range(seq_n):
        pieces = [
            two_halves(half_columns(wk_ref, s * heads + h, 0), half_columns(wv_ref, s * heads + h, 1))
            for h in range(heads)
        ]
        for h in range(0, heads, 2):
            second = half_columns(wq_ref, s * heads + h + 1, 1) if h + 1 < heads else jnp.zeros((own, PAIR), f32)
            pieces.append(two_halves(half_columns(wq_ref, s * heads + h, 0), second))
        piece = jnp.concatenate(pieces, axis=1).astype(bf16)
        notes = jnp.concatenate([vec_ref[...], jnp.zeros((8, piece.shape[1] - width), bf16)], axis=1) if (
            piece.shape[1] > width
        ) else vec_ref[:, 0 : piece.shape[1]]
        for b in range(blocks):
            for i in range(inner):
                pack_ref[b, s, i, 0:own, :] = piece
                pack_ref[b, s, i, own : own + 8, :] = notes
    u = up_ref.shape[0]
    rest_ref[0:u, :] = up_ref[...]
    rest_ref[u : 2 * u, :] = down_ref[...]
    rest_ref[2 * u : 2 * u + own, :] = wo_ref[...]
    row = lax.broadcasted_iota(jnp.int32, (8, 1), 0)
    block = jnp.where(row == 7, bup_ref[...].astype(f32), vec_ref[...].astype(f32))
    rest_ref[2 * u + own : 2 * u + own + 8, :] = block.astype(bf16)


def packed_weights(w_q, w_k, w_v, w_o, w_up, w_down, b_up, vec, dp_n, seq_n, ffn_n):
    own, width = w_q.shape
    heads = width // HEAD_DIM // seq_n
    lanes = heads * PAIR + round_up(heads * HEAD_DIM, PAIR)
    u = w_up.shape[0]
    if own % 8 or u % 16:
        group = heads * HEAD_DIM
        cols = lambda w: w.reshape(own, seq_n, heads, HEAD_DIM).transpose(1, 0, 2, 3)
        kv = jnp.stack([cols(w_k), cols(w_v)], axis=3).reshape(seq_n, own, 2 * group)
        piece = jnp.concatenate([kv, cols(w_q).reshape(seq_n, own, group)], axis=2)
        piece = jnp.pad(piece, ((0, 0), (0, round_up(own, 8) - own), (0, lanes - 3 * group)))
        notes = jnp.broadcast_to(vec[None, :, :lanes], (seq_n, 8, lanes))
        piece = jnp.concatenate([piece, notes], axis=1)
        pack = jnp.broadcast_to(piece[None, :, None], (dp_n, seq_n, ffn_n) + piece.shape[1:])
        w_o = jnp.pad(w_o, ((0, round_up(own, 8) - own), (0, 0)))
        return pack, jnp.concatenate([w_up, w_down, w_o, vec[:7], b_up], axis=0)
    whole = lambda: pl.BlockSpec(memory_space=pltpu.VMEM)
    return pl.pallas_call(
        functools.partial(pack_kernel, seq_n),
        out_shape=(
            jax.ShapeDtypeStruct((dp_n, seq_n, ffn_n, own + 8, lanes), bf16),
            jax.ShapeDtypeStruct((2 * u + own + 8, width), bf16),
        ),
        in_specs=[whole() for _ in range(8)],
        out_specs=(whole(), whole()),
        name="packed_weights",
    )(w_q, w_k, w_v, w_o, w_up, w_down, b_up, vec)


def weights_kernel(chunks, direct, *refs):
    x_refs = refs[:chunks]
    dq_ref, dkv_ref, out_ref, sums_ref, acc = refs[chunks:]
    group, rows = dq_ref.shape[1], dq_ref.shape[2]
    lanes = dkv_ref.shape[2]
    ones = jnp.ones((8, rows), bf16)
    sum_q = jnp.zeros((8, group), f32)
    sum_kv = jnp.zeros((8, lanes), f32)
    acc[lanes + group :, :] = jnp.zeros((acc.shape[0] - lanes - group, acc.shape[1]), f32)
    for c in range(chunks):
        x = x_refs[c][...]
        got_kv = dot_tn(dkv_ref[c], x)
        got_q = dot_nn(dq_ref[c], x)
        if c == 0:
            acc[0:lanes, :] = got_kv
            acc[lanes : lanes + group, :] = got_q
        else:
            acc[0:lanes, :] += got_kv
            acc[lanes : lanes + group, :] += got_q
        sum_q = sum_q + dot_nt(ones, dq_ref[c])
        sum_kv = sum_kv + dot_nn(ones, dkv_ref[c])
    grad = jnp.transpose(acc[...], (1, 0))
    blank = jnp.zeros((8, acc.shape[0] - lanes - group), f32)
    sums = jnp.concatenate([sum_kv, sum_q, blank], axis=1)
    sums_ref[...] = sums
    if direct:
        blocks, per, _ = out_ref.shape
        own = per - 8
        grad = grad.astype(f32).reshape(blocks, own, acc.shape[0])
        for b in range(blocks):
            out_ref[b, 0:own, :] = grad[b].astype(bf16)
            out_ref[b, own:, :] = sums.astype(bf16)
    else:
        out_ref[...] = grad.astype(bf16)


def projection_gradients(x, dq, dkv, own, devices):
    chunks, group, rows = dq.shape
    width = x[0].shape[1]
    lanes = dkv.shape[2]
    full = lanes + round_up(group, PAIR)
    direct = own % 8 == 0
    whole = lambda: pl.BlockSpec(memory_space=pltpu.VMEM)
    out, sums = pl.pallas_call(
        functools.partial(weights_kernel, chunks, direct),
        out_shape=(
            jax.ShapeDtypeStruct((devices, own + 8, full) if direct else (width, full), bf16),
            jax.ShapeDtypeStruct((8, full), f32),
        ),
        in_specs=[whole() for _ in range(chunks + 2)],
        out_specs=(whole(), whole()),
        scratch_shapes=[pltpu.VMEM((full, width), f32)],
        compiler_params=pltpu.CompilerParams(vmem_limit_bytes=VMEM_BYTES),
        cost_estimate=pl.CostEstimate(flops=4_000_000_000, bytes_accessed=12_000_000, transcendentals=0),
        name="projection_gradients",
    )(*x, dq, dkv)
    if not direct:
        out = jnp.pad(out.reshape(devices, own, full), ((0, 0), (0, round_up(own, 8) - own), (0, 0)))
        out = jnp.concatenate([out, jnp.broadcast_to(sums[None].astype(bf16), (devices, 8, full))], axis=1)
    return out


def unpack_kernel(own, got_ref, q_ref, k_ref, v_ref, sums_ref, tot):
    dp_n, seq_n, ffn_n, per, full = got_ref.shape
    width = q_ref.shape[1]
    heads = width // HEAD_DIM // seq_n
    for s in range(seq_n):
        total = jnp.zeros((per, full), f32)
        for d in range(dp_n):
            for f in range(ffn_n):
                total = total + got_ref[d, s, f].astype(f32)
        tot[s] = total
        sums_ref[s : s + 1, :] = total[per - 8 : per - 7, :]
    for w in range(width // PAIR):
        spots = [((2 * w + i) // heads, (2 * w + i) % heads) for i in range(2)]
        cols = slice(w * PAIR, (w + 1) * PAIR)
        for ref, where in (
            (k_ref, lambda h: 2 * h),
            (v_ref, lambda h: 2 * h + 1),
            (q_ref, lambda h: 2 * heads + h),
        ):
            both = [half_columns(tot.at[g], where(h), i) for i, (g, h) in enumerate(spots)]
            ref[:, cols] = two_halves(*both)[0:own]


def unpacked_gradients(got, own, width):
    dp_n, seq_n, ffn_n, per, full = got.shape
    whole = lambda: pl.BlockSpec(memory_space=pltpu.VMEM)
    return pl.pallas_call(
        functools.partial(unpack_kernel, own),
        out_shape=(jax.ShapeDtypeStruct((own, width), f32),) * 3 + (jax.ShapeDtypeStruct((seq_n, full), f32),),
        in_specs=[whole()],
        out_specs=tuple(whole() for _ in range(4)),
        scratch_shapes=[pltpu.VMEM((seq_n, per, full), f32)],
        compiler_params=pltpu.CompilerParams(vmem_limit_bytes=VMEM_BYTES),
        name="unpacked_gradients",
    )(got)


NORM_EPS = 1e-12


def transposed(value):
    return jnp.transpose(value.astype(f32), (1, 0)).astype(bf16)


def unit_rows(value):
    center = value - jnp.mean(value, axis=-1, keepdims=True)
    scale = lax.rsqrt(jnp.mean(center * center, axis=-1, keepdims=True) + NORM_EPS)
    return center * scale, scale


def unit_rows_back(grad, unit, scale):
    return scale * (
        grad - jnp.mean(grad, axis=-1, keepdims=True) - unit * jnp.mean(grad * unit, axis=-1, keepdims=True)
    )


def rows_kernel(parts, blocks, up_rows, own, me_ref, *refs):
    ctx_refs = refs[:parts]
    (x_ref, cot_ref, rest_ref, wo_ref, vec_ref, bup_ref, out_ref, resid_ref, hid_ref, pre_ref, nlt_ref, gft_ref,
     gb_ref) = refs[parts : parts + 13]
    do_refs = refs[parts + 13 : 2 * parts + 13]
    sums_ref, gbup_ref, slope_sc, wo_sc, wide_sc = refs[2 * parts + 13 :]
    group = ctx_refs[0].shape[0]
    width = x_ref.shape[1]

    def up(f):
        return rest_ref[:, f, 0:up_rows, :].reshape(width, rest_ref.shape[3])

    def down(f):
        return rest_ref[:, f, up_rows : 2 * up_rows, :].reshape(width, rest_ref.shape[3])

    def own_rows(k):
        return pl.ds(pl.multiple_of((me_ref[0] ^ k) * group, group), group)

    @pl.when(pl.program_id(0) == 0)
    def _():
        sums_ref[...] = jnp.zeros_like(sums_ref)
        gbup_ref[...] = jnp.zeros_like(gbup_ref)
        if own:
            for o in range(rest_ref.shape[0]):
                for f in range(blocks):
                    to = (o * blocks + f) * own
                    wide_sc[to : to + own, :] = rest_ref[o, f, 2 * up_rows : 2 * up_rows + own, :].astype(f32)
            wo_sc[...] = wide_sc[...].astype(bf16)
        else:
            wo_sc[...] = wo_ref[...]

    def bias_up(f):
        if own:
            row = rest_ref[0, f, 2 * up_rows + own : 2 * up_rows + own + 8, :].astype(f32)
            return row[7:8, :]
        return bup_ref[f : f + 1, :]

    ctx = jnp.concatenate([r[...] for r in ctx_refs], axis=0)
    w_o = jnp.concatenate([wo_sc[own_rows(k), :] for k in range(parts)], axis=0)
    resid_one = x_ref[...].astype(f32) + (dot_tn(ctx, w_o) + vec_ref[0:1, :])
    unit_one, scale_one = unit_rows(resid_one)
    normed_one = unit_one * vec_ref[2:3, :] + vec_ref[3:4, :]
    low = normed_one.astype(bf16)
    nlt_ref[...] = transposed(normed_one)
    total = normed_one + vec_ref[1:2, :]
    pre = dot_nn(low, up(0)) + bias_up(0)
    for f in range(blocks):
        later = dot_nn(low, up(f + 1)) + bias_up(f + 1) if f + 1 < blocks else None
        phi = 0.5 + 0.5 * lax.erf(pre * (0.5 ** 0.5))
        slope_sc[f] = phi + pre * (jnp.exp(-0.5 * pre * pre) * 0.3989422804014327)
        hid = (pre * phi).astype(bf16)
        hid_ref[f] = hid
        total = total + dot_nt(hid, down(f))
        pre = later
    unit_two, scale_two = unit_rows(total)
    out_ref[...] = (unit_two * vec_ref[4:5, :] + vec_ref[5:6, :]).astype(bf16)
    cot = cot_ref[...].astype(f32)
    grad_two = unit_rows_back(cot * vec_ref[4:5, :], unit_two, scale_two)
    grad_ffn = grad_two.astype(bf16)
    gft_ref[...] = transposed(grad_two)
    grad_normed = grad_two
    back = dot_nn(grad_ffn, down(0))
    for f in range(blocks):
        later = dot_nn(grad_ffn, down(f + 1)) if f + 1 < blocks else None
        grad_pre = (back * slope_sc[f]).astype(bf16)
        pre_ref[f] = grad_pre
        gbup_ref[f : f + 1, :] += jnp.sum(grad_pre.astype(f32), axis=0, keepdims=True)
        grad_normed = grad_normed + dot_nt(grad_pre, up(f))
        back = later
    resid = unit_rows_back(grad_normed * vec_ref[2:3, :], unit_one, scale_one)
    resid_ref[...] = resid
    branch = resid.astype(bf16)
    gb_ref[...] = branch
    do = dot_nt(w_o, branch).astype(bf16)
    for k in range(parts):
        do_refs[k][...] = do[k * group : (k + 1) * group]
    for row, value in enumerate(
        (branch.astype(f32), grad_ffn.astype(f32), grad_normed * unit_one, grad_normed, cot * unit_two, cot)
    ):
        sums_ref[row : row + 1, :] += jnp.sum(value, axis=0, keepdims=True)


def rows_chain(me, ctx_parts, x, cot, rest, up_rows, own, w_o, vecs, bias_up):
    parts = len(ctx_parts)
    group, rows = ctx_parts[0].shape
    width = x.shape[1]
    outer, blocks, per, hidden = rest.shape
    tile = 256
    once = lambda shape: pl.BlockSpec(shape, lambda i: (0,) * len(shape), pipeline_mode=pl.Buffered(1))
    tall = pl.BlockSpec((tile, width), lambda i: (i, 0))
    wide = pl.BlockSpec((width, tile), lambda i: (0, i))
    cube = pl.BlockSpec((blocks, tile, hidden), lambda i: (0, i, 0))
    return pl.pallas_call(
        functools.partial(rows_kernel, parts, blocks, up_rows, own),
        grid=(rows // tile,),
        out_shape=(
            jax.ShapeDtypeStruct((rows, width), bf16),
            jax.ShapeDtypeStruct((rows, width), f32),
            jax.ShapeDtypeStruct((blocks, rows, hidden), bf16),
            jax.ShapeDtypeStruct((blocks, rows, hidden), bf16),
            jax.ShapeDtypeStruct((width, rows), bf16),
            jax.ShapeDtypeStruct((width, rows), bf16),
            jax.ShapeDtypeStruct((rows, width), bf16),
        )
        + (jax.ShapeDtypeStruct((group, rows), bf16),) * parts
        + (jax.ShapeDtypeStruct((8, width), f32), jax.ShapeDtypeStruct((8, hidden), f32)),
        in_specs=[pl.BlockSpec(memory_space=pltpu.SMEM)]
        + [pl.BlockSpec((group, tile), lambda i: (0, i))] * parts
        + [tall, tall, once(rest.shape), once(w_o.shape), once(vecs.shape), once(bias_up.shape)],
        out_specs=(
            tall, tall, cube, cube, wide, wide, tall,
        )
        + (pl.BlockSpec((group, tile), lambda i: (0, i)),) * parts
        + (pl.BlockSpec((8, width), lambda i: (0, 0)), pl.BlockSpec((8, hidden), lambda i: (0, 0))),
        scratch_shapes=[
            pltpu.VMEM((blocks, tile, hidden), f32),
            pltpu.VMEM((width, width), bf16),
            pltpu.VMEM((width, width), f32),
        ],
        compiler_params=pltpu.CompilerParams(vmem_limit_bytes=VMEM_BYTES),
        cost_estimate=pl.CostEstimate(flops=22_000_000_000, bytes_accessed=40_000_000, transcendentals=6_000_000),
        name="rows_chain",
    )(me, *ctx_parts, x, cot, rest, w_o, vecs, bias_up)


def outer_kernel(parts, up_rows, own, apart, me_ref, *refs):
    ctx_refs = refs[:parts]
    nlt_ref, gft_ref, gb_ref, pre_ref, hid_ref, sums_ref, gbup_ref, out_ref = refs[parts : parts + 8]
    wo_sc = refs[-1]
    slabs, hidden = out_ref.shape[0], out_ref.shape[3]
    group = ctx_refs[0].shape[0]
    f = pl.program_id(0)
    up = dot_nn(nlt_ref[...], pre_ref[0]).astype(bf16).reshape(slabs, up_rows, hidden)
    if apart:
        refs[parts + 8][:, 0, :, :] = up[:, 0:apart]
    out_ref[:, 0, 0 : up_rows - apart, :] = up[:, apart:]
    at = up_rows - apart
    down = dot_nn(gft_ref[...], hid_ref[0]).astype(bf16)
    out_ref[:, 0, at : at + up_rows, :] = down.reshape(slabs, up_rows, hidden)
    at += up_rows
    if not own:
        return

    @pl.when(f == 0)
    def _():
        for k in range(parts):
            wo_sc[k] = dot_nn(ctx_refs[k][...], gb_ref[...])

    share = slabs // parts
    stride = group // share
    for k in range(parts):
        for j in range(share):
            rows = pl.ds(pl.multiple_of(j * stride + f * own, 8), own)
            out_ref[(me_ref[0] ^ k) * share + j, 0, at : at + own, :] = wo_sc[k, rows, :].astype(bf16)
    small = jnp.concatenate([gbup_ref[pl.ds(f, 1), :], sums_ref[0:7, :]], axis=0).astype(bf16)
    for o in range(slabs):
        out_ref[o, 0, at + own :, :] = small


def outer_products(me, ctx_parts, nlt, gft, gb, pre, hid, sums, gbup, slabs, up_rows, own, apart):
    blocks, rows, hidden = pre.shape
    parts = len(ctx_parts)
    group = ctx_parts[0].shape[0]
    per = 2 * up_rows - apart + (own + 8 if own else 0)
    sizes = (per, apart) if apart else (per,)
    once = lambda shape: pl.BlockSpec(shape, lambda i: (0,) * len(shape), pipeline_mode=pl.Buffered(1))
    return pl.pallas_call(
        functools.partial(outer_kernel, parts, up_rows, own, apart),
        grid=(blocks,),
        out_shape=tuple(jax.ShapeDtypeStruct((slabs, blocks, r, hidden), bf16) for r in sizes),
        in_specs=[pl.BlockSpec(memory_space=pltpu.SMEM)]
        + [once(c.shape) for c in ctx_parts]
        + [
            once(nlt.shape),
            once(gft.shape),
            once(gb.shape),
            pl.BlockSpec((1, rows, hidden), lambda i: (i, 0, 0)),
            pl.BlockSpec((1, rows, hidden), lambda i: (i, 0, 0)),
            once(sums.shape),
            once(gbup.shape),
        ],
        out_specs=tuple(pl.BlockSpec((slabs, 1, r, hidden), lambda i: (0, i, 0, 0)) for r in sizes),
        scratch_shapes=[pltpu.VMEM((parts, group, gb.shape[1]), f32)],
        compiler_params=pltpu.CompilerParams(vmem_limit_bytes=VMEM_BYTES),
        cost_estimate=pl.CostEstimate(flops=11_000_000_000, bytes_accessed=28_000_000, transcendentals=0),
        name="outer_products",
    )(me, *ctx_parts, nlt, gft, gb, pre, hid, sums, gbup)


def finish_kernel(up_rows, own, apart_ref, total_ref, up_ref, down_ref, wo_ref, small_ref):
    apart = apart_ref.shape[1]
    total = jnp.zeros(apart_ref.shape[1:], f32)
    for d in range(apart_ref.shape[0]):
        total = total + apart_ref[d].astype(f32)
    up_ref[0:apart, :] = total
    rest = total_ref[...].astype(f32)
    at = up_rows - apart
    up_ref[apart:, :] = rest[0:at]
    down_ref[...] = rest[at : at + up_rows]
    at += up_rows
    wo_ref[...] = rest[at : at + own]
    small_ref[...] = rest[at + own : at + own + 8]


def finished(apart, total, up_rows, own):
    hidden = total.shape[1]
    whole = lambda: pl.BlockSpec(memory_space=pltpu.VMEM)
    return pl.pallas_call(
        functools.partial(finish_kernel, up_rows, own),
        out_shape=tuple(jax.ShapeDtypeStruct((r, hidden), f32) for r in (up_rows, up_rows, own, 8)),
        in_specs=[whole(), whole()],
        out_specs=tuple(whole() for _ in range(4)),
        name="finished",
    )(apart, total)


ALL = ("dp", "seq", "ffn")


def flip_send(array, axis, bits):
    count = lax.axis_size(axis)
    return lax.ppermute(array, axis, [(i, i ^ bits) for i in range(count)])


def shards(
    tokens, w_query, w_key, w_value, w_output, b_query, b_value, b_output, w_up, b_up, w_down, b_down,
    gain_attn, shift_attn, gain_ffn, shift_ffn, segment_ids, random_blocks, global_blocks, cotangent,
):
    seq_n, dp_n, ffn_n = lax.axis_size("seq"), lax.axis_size("dp"), lax.axis_size("ffn")
    outer, devices = dp_n * seq_n, dp_n * seq_n * ffn_n
    me = lax.axis_index("seq")
    here = (lax.axis_index("dp") * seq_n + me) * ffn_n + lax.axis_index("ffn")
    own, width = w_query.shape
    own_pad = round_up(own, 8)
    group = width // seq_n
    heads = group // HEAD_DIM
    features = tokens[0]
    rows = features.shape[0]
    order = jnp.stack([me ^ k for k in range(seq_n)])
    me_ref = me.astype(jnp.int32)[None]

    near = [features] + [None] * (seq_n - 1)
    for k in sorted(range(1, seq_n), key=lambda k: (k & (k - 1), -k)):
        bit = k & -k
        near[k] = flip_send(features if bit == k else near[k ^ bit], "seq", bit)

    vec = jnp.stack([b_output, b_down, gain_attn, shift_attn, gain_ffn, shift_ffn, b_query, b_value])
    vec = jnp.pad(vec, ((0, 0), (0, width - own)))
    seg = segment_ids[0].reshape(seq_n, rows)
    rand = random_blocks.reshape(-1)
    pack, rest = packed_weights(
        w_query, w_key, w_value, w_output, w_up, w_down, b_up[None], vec, dp_n, seq_n, ffn_n
    )
    lanes = pack.shape[4]
    pack, seg, rand = lax.optimization_barrier((pack, seg, rand))
    pack = lax.all_to_all(
        pack.reshape(devices, own_pad + 8, lanes), ALL, split_axis=0, concat_axis=0, tiled=True
    )
    rest = lax.all_gather(rest, ALL, axis=0, tiled=False)
    w_own = pack[:, :own].reshape(width, lanes)
    share = devices // seq_n
    biases = lax.dynamic_slice(pack, (share * me, own_pad + 6, 0), (share, 2, own))
    biases = biases.transpose(1, 0, 2).reshape(2, group).astype(f32)
    by_head = biases[1].reshape(heads, 1, HEAD_DIM)
    b_kv = jnp.concatenate([jnp.zeros_like(by_head), by_head], axis=1).reshape(1, heads * PAIR)

    far = seq_n // 2
    ctx_far, (lse_far, lseg, glob_ctx, k_all, v_all, q_all, mask_all) = attention_forward(
        me_ref, rand, global_blocks, near, seg, w_own, b_kv, biases[0][:, None]
    )
    ctx_parts = [None] * far + [flip_send(ctx_far[k - far], "seq", k) for k in range(far, seq_n)]
    ctx_near, lse_near = attention_near(
        me_ref, rand, global_blocks, k_all, v_all, q_all, mask_all, glob_ctx, seq_n
    )
    ctx_parts[far:], ctx_parts[0] = lax.optimization_barrier((ctx_parts[far:], ctx_near[0]))
    for k in range(1, far):
        ctx_parts[k] = flip_send(ctx_near[k], "seq", k)

    up_rows = w_up.shape[0]
    at = 2 * up_rows
    rest = rest.reshape(outer, ffn_n, rest.shape[1], width)
    w_o = rest[:, :, at : at + own].reshape(width, width)
    bias_up = rest[0, :, at + own_pad + 7].astype(f32)
    vecs = pack[:, own_pad:, :own].transpose(1, 0, 2).reshape(8, width).astype(f32)
    direct = up_rows % 16 == 0 and own % 8 == 0 and outer % seq_n == 0 and (outer // seq_n) * ffn_n * own == group
    if not direct:
        rest = rest[:, :, :at].reshape(outer, ffn_n, 2, up_rows, width).transpose(1, 2, 0, 3, 4)
        rest = rest.reshape(1, ffn_n, 2 * outer * up_rows, width)
    slabs, slab_rows = (outer, up_rows) if direct else (1, outer * up_rows)

    got = rows_chain(
        me_ref, ctx_parts, features, cotangent[0], rest, slab_rows, own if direct else 0,
        jnp.zeros((8, PAIR), bf16) if direct else w_o, vecs, jnp.zeros((8, PAIR), f32) if direct else bias_up,
    )
    out, grad_resid_one, hidden, grad_pre, normed_t, grad_ffn_t, grad_branch = got[:7]
    grad_ctx, (sums, grad_bias_up) = got[7 : 7 + seq_n], got[7 + seq_n :]
    do = [grad_ctx[0]] + [flip_send(grad_ctx[k], "seq", k) for k in range(1, seq_n)]

    payload = outer_products(
        me_ref, ctx_parts, normed_t, grad_ffn_t, grad_branch, grad_pre, hidden, sums, grad_bias_up, slabs, slab_rows,
        own if direct else 0, APART if direct else 0,
    )
    payload, apart = payload if direct else (payload[0], None)
    if not direct:
        grad_out = dot_nn(jnp.concatenate(ctx_parts, axis=0), grad_branch).astype(bf16)
        grad_out = grad_out.reshape(seq_n, group, width)[order].reshape(outer, ffn_n, own, width)
        top = jnp.broadcast_to(grad_bias_up[None, :ffn_n, None], (outer, ffn_n, 1, width))
        small = jnp.concatenate([top, jnp.broadcast_to(sums[None, None, :7], (outer, ffn_n, 7, width))], axis=2)
        small = small.astype(bf16)
        payload = payload.reshape(ffn_n, 2, outer, up_rows, width).transpose(2, 0, 1, 3, 4)
        payload = jnp.concatenate([payload.reshape(outer, ffn_n, at, width), grad_out, small], axis=2)
        payload = jnp.pad(payload, ((0, 0), (0, 0), (0, -payload.shape[2] % 32), (0, 0)))
    payload, apart, do = lax.optimization_barrier((payload, apart, do))
    total = lax.psum_scatter(payload.reshape(-1, width), ALL, scatter_dimension=0, tiled=True)
    if direct:
        apart = lax.all_to_all(
            apart.reshape(devices, APART, width), ALL, split_axis=0, concat_axis=0, tiled=True
        )

    got = attention_backward(
        me_ref, rand, global_blocks, do, k_all, v_all, q_all, mask_all, seg, lse_near, lse_far, lseg, w_own,
        grad_resid_one,
    )
    dq, dkv, grad_features = got[:3]
    part = [None] + list(got[3:])
    bit = 1
    while bit < seq_n:
        for k in range(seq_n):
            if k & -k == bit and k != bit:
                came = flip_send(part[k], "seq", bit).astype(f32)
                part[k ^ bit] = (part[k ^ bit].astype(f32) + came).astype(bf16)
        bit *= 2
    grad_w = projection_gradients(near, dq, dkv, own, devices)
    grad_w, part = lax.optimization_barrier((grad_w, part[1:]))
    grad_w, apart = lax.optimization_barrier((grad_w, apart))
    part = [None] + part
    bit = seq_n // 2
    while bit:
        grad_features = grad_features + flip_send(part[bit], "seq", bit).astype(f32)
        bit //= 2
    grad_w = lax.all_to_all(grad_w, ALL, split_axis=0, concat_axis=0, tiled=True)
    grad_w, grad_features = lax.optimization_barrier((grad_w, grad_features))
    if direct:
        out_up, out_down, out_output, notes = finished(apart, total, up_rows, own)
    else:
        total = total.astype(f32)
        out_up, out_down, out_output = total[:up_rows], total[up_rows:at], total[at : at + own]
        notes = total[at + own : at + own + 8]
    out_bias_up = notes[0]
    out_vecs = lax.dynamic_slice(notes, (1, here * own), (6, own))
    out_query, out_key, out_value, col_sums = unpacked_gradients(
        grad_w.reshape(dp_n, seq_n, ffn_n, own_pad + 8, lanes), own, width
    )
    row = lax.dynamic_index_in_dim(col_sums, here // share, keepdims=False)
    row = jnp.stack([row[heads * PAIR : heads * PAIR + group], row[: heads * PAIR].reshape(heads, 2, HEAD_DIM)[:, 1].reshape(group)])
    out_b = lax.dynamic_slice(row, (0, here % share * own), (2, own))
    return (
        out[None],
        grad_features[None],
        out_query,
        out_key,
        out_value,
        out_output,
        out_b[0],
        out_b[1],
        out_vecs[0],
        out_up,
        out_bias_up,
        out_down,
        out_vecs[1],
        out_vecs[2],
        out_vecs[3],
        out_vecs[4],
        out_vecs[5],
    )


def solution(mesh):
    return jax.shard_map(
        shards,
        mesh=mesh,
        in_specs=(
            P(("dp", "ffn"), "seq", None),
            P(("dp", "seq", "ffn"), None),
            P(("dp", "seq", "ffn"), None),
            P(("dp", "seq", "ffn"), None),
            P(("dp", "seq", "ffn"), None),
            P(("dp", "seq", "ffn")),
            P(("dp", "seq", "ffn")),
            P(("dp", "seq", "ffn")),
            P(("dp", "seq"), "ffn"),
            P("ffn"),
            P(("dp", "seq"), "ffn"),
            P(("dp", "seq", "ffn")),
            P(("dp", "seq", "ffn")),
            P(("dp", "seq", "ffn")),
            P(("dp", "seq", "ffn")),
            P(("dp", "seq", "ffn")),
            P(("dp", "ffn"), None),
            P(("dp", "ffn"), "seq", None, None),
            P(("dp", "ffn"), None),
            P(("dp", "ffn"), "seq", None),
        ),
        out_specs=(
            P(("dp", "ffn"), "seq", None),
            P(("dp", "ffn"), "seq", None),
            P(("dp", "seq", "ffn"), None),
            P(("dp", "seq", "ffn"), None),
            P(("dp", "seq", "ffn"), None),
            P(("dp", "seq", "ffn"), None),
            P(("dp", "seq", "ffn")),
            P(("dp", "seq", "ffn")),
            P(("dp", "seq", "ffn")),
            P(("dp", "seq"), "ffn"),
            P("ffn"),
            P(("dp", "seq"), "ffn"),
            P(("dp", "seq", "ffn")),
            P(("dp", "seq", "ffn")),
            P(("dp", "seq", "ffn")),
            P(("dp", "seq", "ffn")),
            P(("dp", "seq", "ffn")),
        ),
        check_vma=False,
    )
```

```python
import functools
import jax
import jax.numpy as jnp
from jax import lax
from jax.experimental import pallas as pl
from jax.sharding import PartitionSpec as P
from jax.experimental.pallas import tpu as pltpu

HEAD_DIM = 64
BLOCK = 64
PAIR = 2 * BLOCK
MASKED = -1e30
bf16 = jnp.bfloat16
f32 = jnp.float32


def dot_nn(a, b):
    return lax.dot_general(a, b, (((1,), (0,)), ((), ())), preferred_element_type=f32)


def dot_nt(a, b):
    return lax.dot_general(a, b, (((1,), (1,)), ((), ())), preferred_element_type=f32)


def dot_tn(a, b):
    return lax.dot_general(a, b, (((0,), (0,)), ((), ())), preferred_element_type=f32)


def slots(rand_ref, glob_ref, flip, head, pair, nblocks):
    first = (2 * pair) ^ flip

    def row(block):
        return pl.multiple_of(block * BLOCK, BLOCK)

    def near(block):
        bad = (block < 0) | (block >= nblocks) | (block == glob_ref[0, 0]) | (block == glob_ref[0, 1])
        return row(jnp.where(bad, nblocks, block ^ flip))

    def drawn(block):
        at = (head * nblocks + block) * 3
        return [row(rand_ref[at + j] ^ flip) for j in range(3)]

    shared = [near(first), near(first + 1)] + [row(glob_ref[0, j] ^ flip) for j in range(2)]
    return shared, [near(first - 1)] + drawn(first), [near(first + 2)] + drawn(first + 1)


def stack_rows(ref, offsets, lanes):
    return jnp.concatenate([ref[pl.ds(o, BLOCK), lanes] for o in offsets], axis=0)


def lane_halves(width, dtype):
    lane = lax.broadcasted_iota(jnp.int32, (1, width), 1) % PAIR
    first = (lane < BLOCK).astype(dtype)
    second = (lane >= BLOCK).astype(dtype)
    return first, second


UNROLL = 4
BACK_UNROLL = 2
APART = 48
VMEM_BYTES = 62 << 20


def head_lanes(h):
    return slice(h * PAIR, (h + 1) * PAIR)


def query_columns(q_ref, mask_ref, h, at):
    return jnp.concatenate([q_ref[h * BLOCK : (h + 1) * BLOCK, pl.ds(at, PAIR)], mask_ref[:, pl.ds(at, PAIR)]], axis=0)


def global_queries(q_ref, mask_ref, h, gl):
    return jnp.concatenate(
        [
            global_columns(q_ref, slice(h * BLOCK, (h + 1) * BLOCK), gl),
            global_columns(mask_ref, slice(0, BLOCK), gl),
        ],
        axis=0,
    ).astype(bf16)


def placed(me_ref, glob_ref, nblocks, chunks):
    flip = me_ref[0] * (nblocks // chunks)
    return flip, [glob_ref[0, j] ^ flip for j in range(2)]


def global_columns(src_ref, rows, gl):
    lane = lax.broadcasted_iota(jnp.int32, (1, PAIR), 1)
    parts = []
    for g in range(2):
        block = gl[g]
        at = pl.multiple_of((block // 2) * PAIR, PAIR)
        both = src_ref[rows, pl.ds(at, PAIR)].astype(f32)
        moved = pltpu.roll(both, BLOCK, 1)
        parts.append(jnp.where(block % 2 == g, both, moved))
    return jnp.where(lane < BLOCK, parts[0], parts[1])


def put_global_columns(dst_ref, rows, gl, value, per_chunk, low, high):
    lane = lax.broadcasted_iota(jnp.int32, (1, PAIR), 1)
    moved = pltpu.roll(value, BLOCK, 1)
    for g in range(2):
        pair = gl[g] // 2
        half = gl[g] % 2
        chunk = pair // per_chunk

        @pl.when((chunk >= low) & (chunk < high))
        def _():
            at = pl.multiple_of((pair % per_chunk) * PAIR, PAIR)
            src = jnp.where(half == g, value, moved)
            old = dst_ref[chunk - low, rows, pl.ds(at, PAIR)].astype(f32)
            new = jnp.where((lane >= BLOCK) == (half == 1), src, old)
            dst_ref[chunk - low, rows, pl.ds(at, PAIR)] = new.astype(dst_ref.dtype)


def project_rows(x, seg, w_ref, wq, bkv_ref, bq_ref, k_ref, v_ref, q_ref, mask_ref, at):
    n = x.shape[0]
    lanes = v_ref.shape[1]
    y = dot_nn(x, w_ref[:, 0:lanes]) + bkv_ref[...]
    spot = lax.broadcasted_iota(jnp.int32, (PAIR, n), 0) - BLOCK
    mark = jnp.transpose((spot == seg).astype(f32), (1, 0))
    lane = lax.broadcasted_iota(jnp.int32, (1, PAIR), 1)
    rows = pl.ds(at, n)
    v_ref[rows, :] = y.astype(bf16)
    for h in range(lanes // PAIR):
        k_ref[rows, head_lanes(h)] = jnp.where(lane < BLOCK, y[:, head_lanes(h)], mark).astype(bf16)
    z = (dot_nt(wq, x) + bq_ref[...]).astype(bf16)
    q_ref[:, rows] = (z.astype(f32) * HEAD_DIM ** -0.5).astype(bf16)
    row = lax.broadcasted_iota(jnp.int32, (BLOCK, n), 0)
    mask_ref[:, rows] = jnp.where((row <= 16) & (row != seg), MASKED, 0.0).astype(bf16)


def query_weights(w_ref, heads):
    at = heads * PAIR
    cols = w_ref[:, at : at + 2 * PAIR].astype(f32)
    return jnp.transpose(cols, (1, 0))[0 : heads * HEAD_DIM].astype(bf16)


def sparse_forward(heads, low, high, per_chunk, rand_ref, glob_ref, flip, k_ref, kv_ref, q_ref, mask_ref, out_ref, lse_ref):
    nblocks = (k_ref.shape[0] - BLOCK) // BLOCK
    first, second = lane_halves(PAIR, bf16)
    lane = lax.broadcasted_iota(jnp.int32, (1, PAIR), 1)

    def one_pair(spot):
        chunk = spot // per_chunk
        local = pl.multiple_of((spot % per_chunk) * PAIR, PAIR)
        pair = low * per_chunk + spot
        at = pl.multiple_of(pair * PAIR, PAIR)
        for h in range(heads):
            shared, mine, other = slots(rand_ref, glob_ref, flip, h, pair, nblocks)
            kl = head_lanes(h)
            q = query_columns(q_ref, mask_ref, h, at)
            s_sh = dot_nn(stack_rows(k_ref, shared, kl), q)
            k_pr = jnp.concatenate([stack_rows(k_ref, mine, kl), stack_rows(k_ref, other, kl)], axis=1)
            s_pr = dot_nn(k_pr, jnp.concatenate([q * first, q * second], axis=0))
            peak = jnp.maximum(jnp.max(s_sh, axis=0, keepdims=True), jnp.max(s_pr, axis=0, keepdims=True))
            e_sh = jnp.exp(s_sh - peak)
            e_pr = jnp.exp(s_pr - peak)
            total = jnp.sum(e_sh, axis=0, keepdims=True) + jnp.sum(e_pr, axis=0, keepdims=True)
            inv = 1.0 / total
            p_sh = (e_sh * inv).astype(bf16)
            p_pr = (e_pr * inv).astype(bf16)
            v_pr = jnp.concatenate([stack_rows(kv_ref, mine, kl), stack_rows(kv_ref, other, kl)], axis=1)
            o_sh = dot_tn(stack_rows(kv_ref, shared, kl), p_sh)
            o_pr = dot_tn(v_pr, p_pr)
            ctx = o_sh[BLOCK:PAIR] + jnp.where(lane < BLOCK, o_pr[BLOCK:PAIR], o_pr[PAIR + BLOCK : 2 * PAIR])
            out_ref[chunk, h * BLOCK : (h + 1) * BLOCK, pl.ds(local, PAIR)] = ctx.astype(bf16)
            lse_ref[h, pl.ds(spot, 1), :] = peak + jnp.log(total)

    @pl.loop(0, (high - low) * per_chunk // UNROLL)
    def _(some):
        for i in range(UNROLL):
            one_pair(UNROLL * some + i)


def forward_kernel(heads, chunks, me_ref, rand_ref, glob_ref, *refs):
    x_refs = refs[0:chunks]
    seg_ref, w_ref, bkv_ref, bq_ref = refs[chunks : chunks + 4]
    far = chunks // 2
    out_refs = refs[chunks + 4 : chunks + 4 + far]
    lse_ref, lseg_ref, glob_ctx_ref, k_sc, v_sc, q_sc, mask_sc, s_sc, out_ref, seg_sc = refs[chunks + 4 + far :]
    rows = x_refs[0].shape[0]
    length = rows * chunks
    per_chunk = length // PAIR // chunks
    flip, gl = placed(me_ref, glob_ref, length // BLOCK, chunks)
    tile = 256
    wq = query_weights(w_ref, heads)
    for c in range(chunks):
        seg_sc[c : c + 1, :] = seg_ref[pl.ds(me_ref[0] ^ c, 1), :]
    for c in range(chunks):

        @pl.loop(0, rows // tile)
        def _(t):
            at = pl.multiple_of(t * tile, tile)
            project_rows(
                x_refs[c][pl.ds(at, tile), :], seg_sc[c : c + 1, pl.ds(at, tile)], w_ref, wq, bkv_ref, bq_ref,
                k_sc, v_sc, q_sc, mask_sc, pl.multiple_of(c * rows + t * tile, tile),
            )

    null_lane = lax.broadcasted_iota(jnp.int32, (BLOCK, heads * PAIR), 1) % PAIR
    k_sc[pl.ds(length, BLOCK), :] = (null_lane == BLOCK + 16).astype(f32).astype(bf16)
    v_sc[pl.ds(length, BLOCK), :] = jnp.zeros((BLOCK, heads * PAIR), bf16)
    sparse_forward(heads, far, chunks, per_chunk, rand_ref, glob_ref, flip, k_sc, v_sc, q_sc, mask_sc, out_ref, lse_ref)

    step = 512
    queries = [global_queries(q_sc, mask_sc, h, gl) for h in range(heads)]

    def score(c, peaks):
        at = pl.multiple_of(c * step, step)
        new = []
        for h in range(heads):
            got = dot_nn(k_sc[pl.ds(at, step), head_lanes(h)], queries[h])
            s_sc[h, pl.ds(at, step), :] = got
            new.append(jnp.maximum(peaks[h], jnp.max(got, axis=0, keepdims=True)))
        return tuple(new)

    peaks = lax.fori_loop(0, length // step, score, (jnp.full((1, PAIR), MASKED, f32),) * heads)

    def gather(c, carry):
        at = pl.multiple_of(c * step, step)
        new = []
        for h in range(heads):
            total, ctx = carry[h]
            e = jnp.exp(s_sc[h, pl.ds(at, step), :] - peaks[h])
            ctx = ctx + dot_tn(v_sc[pl.ds(at, step), head_lanes(h)], e.astype(bf16))
            new.append((total + jnp.sum(e, axis=0, keepdims=True), ctx))
        return tuple(new)

    start = (jnp.zeros((1, PAIR), f32), jnp.zeros((PAIR, PAIR), f32))
    sums = lax.fori_loop(0, length // step, gather, (start,) * heads)
    for h in range(heads):
        total, ctx = sums[h]
        ctx = ctx[BLOCK:PAIR] * (1.0 / total)
        glob_ctx_ref[h] = ctx
        put_global_columns(out_ref, slice(h * BLOCK, (h + 1) * BLOCK), gl, ctx, per_chunk, far, chunks)
        lseg_ref[h : h + 1, :] = peaks[h] + jnp.log(total)
    for c in range(far):
        out_refs[c][...] = out_ref[c]


def attention_forward(me, rand, glob, x, seg, w, b_kv, b_q):
    chunks = len(x)
    far = chunks // 2
    rows = x[0].shape[0]
    length = rows * chunks
    heads = b_q.shape[0] // HEAD_DIM
    whole = lambda: pl.BlockSpec(memory_space=pltpu.VMEM)
    got = pl.pallas_call(
        functools.partial(forward_kernel, heads, chunks),
        out_shape=(jax.ShapeDtypeStruct((heads * HEAD_DIM, rows), bf16),) * far
        + (
            jax.ShapeDtypeStruct((heads, length // PAIR // 2, PAIR), f32),
            jax.ShapeDtypeStruct((heads, PAIR), f32),
            jax.ShapeDtypeStruct((heads, HEAD_DIM, PAIR), f32),
            jax.ShapeDtypeStruct((length + BLOCK, heads * PAIR), bf16),
            jax.ShapeDtypeStruct((length + BLOCK, heads * PAIR), bf16),
            jax.ShapeDtypeStruct((heads * HEAD_DIM, length), bf16),
            jax.ShapeDtypeStruct((BLOCK, length), bf16),
        ),
        in_specs=[pl.BlockSpec(memory_space=pltpu.SMEM)] * 3 + [whole() for _ in range(chunks + 4)],
        out_specs=tuple(whole() for _ in range(far + 7)),
        scratch_shapes=[
            pltpu.VMEM((heads, length, PAIR), f32),
            pltpu.VMEM((far, heads * HEAD_DIM, rows), bf16),
            pltpu.VMEM((chunks, rows), jnp.int32),
        ],
        compiler_params=pltpu.CompilerParams(vmem_limit_bytes=VMEM_BYTES),
        cost_estimate=pl.CostEstimate(flops=10_000_000_000, bytes_accessed=16_000_000, transcendentals=6_000_000),
        name="attention_forward",
    )(me, rand, glob, *x, seg, w, b_kv, b_q)
    return got[:far], got[far:]


def near_kernel(heads, chunks, me_ref, rand_ref, glob_ref, k_ref, kv_ref, q_ref, mask_ref, glob_ctx_ref, *refs):
    half = chunks // 2
    out_refs = refs[:half]
    lse_ref, out_ref = refs[half:]
    length = q_ref.shape[1]
    per_chunk = length // PAIR // chunks
    flip, gl = placed(me_ref, glob_ref, length // BLOCK, chunks)
    sparse_forward(heads, 0, half, per_chunk, rand_ref, glob_ref, flip, k_ref, kv_ref, q_ref, mask_ref, out_ref, lse_ref)
    for h in range(heads):
        put_global_columns(out_ref, slice(h * BLOCK, (h + 1) * BLOCK), gl, glob_ctx_ref[h], per_chunk, 0, half)
    for c in range(half):
        out_refs[c][...] = out_ref[c]


def attention_near(me, rand, glob, k, kv, q, mask, glob_ctx, chunks):
    heads = glob_ctx.shape[0]
    half = chunks // 2
    length = q.shape[1]
    rows = length // chunks
    whole = lambda: pl.BlockSpec(memory_space=pltpu.VMEM)
    got = pl.pallas_call(
        functools.partial(near_kernel, heads, chunks),
        out_shape=(jax.ShapeDtypeStruct((heads * HEAD_DIM, rows), bf16),) * half
        + (jax.ShapeDtypeStruct((heads, length // PAIR // 2, PAIR), f32),),
        in_specs=[pl.BlockSpec(memory_space=pltpu.SMEM)] * 3 + [whole() for _ in range(5)],
        out_specs=tuple(whole() for _ in range(half + 1)),
        scratch_shapes=[pltpu.VMEM((half, heads * HEAD_DIM, rows), bf16)],
        compiler_params=pltpu.CompilerParams(vmem_limit_bytes=VMEM_BYTES),
        cost_estimate=pl.CostEstimate(flops=6_000_000_000, bytes_accessed=9_000_000, transcendentals=3_000_000),
        name="attention_near",
    )(me, rand, glob, k, kv, q, mask, glob_ctx)
    return got[:half], got[half]


def backward_kernel(heads, chunks, me_ref, rand_ref, glob_ref, *refs):
    do_refs = refs[:chunks]
    (k_ref, kv_ref, q_ref, mask_ref, seg_ref, lse_near_ref, lse_far_ref, lseg_ref, w_ref, resid_ref, dq_ref, dkv_ref,
     first_ref) = refs[chunks : chunks + 13]
    part_refs = refs[chunks + 13 : 2 * chunks + 12]
    do_sc, acc, p_sc, d_sc, seg_sc, line_sc, lse_ref, row_sc = refs[2 * chunks + 12 :]
    rows = do_refs[0].shape[1]
    length = rows * chunks
    npairs = length // PAIR
    per_chunk = npairs // chunks
    scale = HEAD_DIM ** -0.5
    flip, gl = placed(me_ref, glob_ref, length // BLOCK, chunks)
    lse_ref[:, 0 : npairs // 2, :] = lse_near_ref[...]
    lse_ref[:, npairs // 2 :, :] = lse_far_ref[...]
    for c in range(chunks):
        do_sc[:, c * rows : (c + 1) * rows] = do_refs[c][...]
        row_sc[c : c + 1, :] = seg_ref[pl.ds(me_ref[0] ^ c, 1), :].astype(f32)

        @pl.loop(0, per_chunk // 4)
        def _(some):
            for i in range(4):
                t = 4 * some + i
                line = row_sc[c : c + 1, pl.ds(pl.multiple_of(t * PAIR, PAIR), PAIR)]
                line_sc[c * per_chunk + t] = line
                to = pl.multiple_of(c * rows + t * PAIR, PAIR)
                seg_sc[pl.ds(to, PAIR), :] = jnp.transpose(jnp.broadcast_to(line, (PAIR, PAIR)), (1, 0))

    seg_sc[length : length + BLOCK, :] = jnp.full((BLOCK, PAIR), -1.0, f32)
    first2, second2 = lane_halves(2 * PAIR, bf16)
    ffirst, fsecond = lane_halves(PAIR, f32)
    lane = lax.broadcasted_iota(jnp.int32, (1, PAIR), 1)
    line_row = lax.broadcasted_iota(jnp.int32, (PAIR, 1), 0)
    zeros = jnp.zeros((BLOCK, PAIR), bf16)
    blank = jnp.zeros((PAIR, PAIR), bf16)

    def head_rows(h):
        return slice(h * BLOCK, (h + 1) * BLOCK)

    def joint(q, mask, do):
        left = jnp.concatenate([q, mask, blank], axis=0)
        right = jnp.concatenate([blank, zeros, do], axis=0)
        return jnp.concatenate([left, right], axis=1)

    def sources(q, do):
        top = jnp.concatenate([q, zeros], axis=1)
        return jnp.concatenate([top, jnp.concatenate([zeros, do], axis=1)], axis=0)

    step = 512
    mask_glob = global_columns(mask_ref, slice(0, BLOCK), gl).astype(bf16)
    q_glob = [global_columns(q_ref, head_rows(h), gl).astype(bf16) for h in range(heads)]
    do_glob = [global_columns(do_sc, head_rows(h), gl).astype(bf16) for h in range(heads)]

    def weigh(c, deltas):
        at = pl.multiple_of(c * step, step)
        new = []
        for h in range(heads):
            left = jnp.concatenate([k_ref[pl.ds(at, step), head_lanes(h)], kv_ref[pl.ds(at, step), head_lanes(h)]], axis=1)
            both = dot_nn(left, joint(q_glob[h], mask_glob, do_glob[h]))
            p = jnp.exp(both[:, 0:PAIR] - lseg_ref[h : h + 1, :])
            dp = both[:, PAIR:]
            p_sc[h, pl.ds(at, step), :] = p
            d_sc[h, pl.ds(at, step), :] = dp
            new.append(deltas[h] + jnp.sum(p * dp, axis=0, keepdims=True))
        return tuple(new)

    deltas = lax.fori_loop(0, length // step, weigh, (jnp.zeros((1, PAIR), f32),) * heads)

    def spread(c, dqs):
        at = pl.multiple_of(c * step, step)
        new = []
        for h in range(heads):
            p = p_sc[h, pl.ds(at, step), :]
            ds = (p * (d_sc[h, pl.ds(at, step), :] - deltas[h])).astype(bf16)
            both = jnp.concatenate([ds, p.astype(bf16)], axis=1)
            acc[h, pl.ds(at, step), :] = dot_nt(both, sources(q_glob[h], do_glob[h]))
            new.append(dqs[h] + dot_tn(k_ref[pl.ds(at, step), head_lanes(h)], ds))
        return tuple(new)

    dqs = lax.fori_loop(0, length // step, spread, (jnp.zeros((PAIR, PAIR), f32),) * heads)
    for h in range(heads):
        acc[h, pl.ds(length, BLOCK), :] = jnp.zeros((BLOCK, PAIR), f32)

    def one_pair(pair):
        chunk = pair // per_chunk
        local = pl.multiple_of((pair % per_chunk) * PAIR, PAIR)
        at = pl.multiple_of(pair * PAIR, PAIR)
        hit_first = (gl[0] == 2 * pair) | (gl[1] == 2 * pair)
        hit_second = (gl[0] == 2 * pair + 1) | (gl[1] == 2 * pair + 1)
        shut = ffirst * jnp.where(hit_first, -MASKED, 0.0) + fsecond * jnp.where(hit_second, -MASKED, 0.0)
        every = slice(0, PAIR)
        for h in range(heads):
            kl = head_lanes(h)
            shared, mine, other = slots(rand_ref, glob_ref, flip, h, pair, length // BLOCK)
            q = q_ref[head_rows(h), pl.ds(at, PAIR)]
            do = do_sc[head_rows(h), pl.ds(at, PAIR)]
            lse = lse_ref[h, pl.ds(pair, 1), :] + shut
            src = sources(q, do)
            src2 = jnp.concatenate([src * first2, src * second2], axis=0)
            k_sh = stack_rows(k_ref, shared, kl)
            two_sh = dot_nn(
                jnp.concatenate([k_sh, stack_rows(kv_ref, shared, kl)], axis=1),
                joint(q, mask_ref[:, pl.ds(at, PAIR)], do),
            )
            kv_pr = jnp.concatenate([stack_rows(kv_ref, mine, kl), stack_rows(kv_ref, other, kl)], axis=1)
            two_pr = dot_nn(kv_pr, src2)
            seg_pr = jnp.where(lane < BLOCK, stack_rows(seg_sc, mine, every), stack_rows(seg_sc, other, every))
            agree = seg_pr == line_sc[pair]
            p_sh = jnp.exp(two_sh[:, 0:PAIR] - lse)
            p_pr = jnp.where(agree, jnp.exp(two_pr[:, 0:PAIR] - lse), 0.0)
            d_sh, d_pr = two_sh[:, PAIR:], two_pr[:, PAIR:]
            delta = jnp.sum(p_sh * d_sh, axis=0, keepdims=True) + jnp.sum(p_pr * d_pr, axis=0, keepdims=True)
            ds_sh = (p_sh * (d_sh - delta)).astype(bf16)
            ds_pr = (p_pr * (d_pr - delta)).astype(bf16)
            g_sh = dot_nt(jnp.concatenate([ds_sh, p_sh.astype(bf16)], axis=1), src)
            g_pr = dot_nt(jnp.concatenate([ds_pr, p_pr.astype(bf16)], axis=1), src2)
            for j, o in enumerate(shared):
                acc[h, pl.ds(o, BLOCK), :] += g_sh[j * BLOCK : (j + 1) * BLOCK]
            for j, o in enumerate(mine):
                acc[h, pl.ds(o, BLOCK), :] += g_pr[j * BLOCK : (j + 1) * BLOCK, 0:PAIR]
            for j, o in enumerate(other):
                acc[h, pl.ds(o, BLOCK), :] += g_pr[j * BLOCK : (j + 1) * BLOCK, PAIR:]
            t_pr = dot_tn(ds_pr, kv_pr)
            dq = dot_tn(ds_sh, k_sh) + jnp.where(line_row < BLOCK, t_pr[:, 0:PAIR], t_pr[:, PAIR:])
            dq = jnp.transpose(dq, (1, 0))[0:BLOCK]
            dq_ref[chunk, head_rows(h), pl.ds(local, PAIR)] = (dq * scale).astype(bf16)

    @pl.loop(0, npairs // BACK_UNROLL)
    def _(some):
        for i in range(BACK_UNROLL):
            one_pair(BACK_UNROLL * some + i)

    for h in range(heads):
        put_global_columns(dq_ref, head_rows(h), gl, dqs[h][0:BLOCK] * scale, per_chunk, 0, chunks)
        for c in range(chunks):
            dkv_ref[c, :, head_lanes(h)] = acc[h, pl.ds(c * rows, rows), :].astype(bf16)
    tile = 256
    wq = query_weights(w_ref, heads)
    for c in range(chunks):

        @pl.loop(0, rows // tile)
        def _(t):
            at = pl.multiple_of(t * tile, tile)
            got = dot_tn(dq_ref[c, :, pl.ds(at, tile)], wq)
            got = got + dot_nt(dkv_ref[c, pl.ds(at, tile), :], w_ref[:, 0 : heads * PAIR])
            if c == 0:
                first_ref[pl.ds(at, tile), :] = resid_ref[pl.ds(at, tile), :] + got
            else:
                part_refs[c - 1][pl.ds(at, tile), :] = got.astype(bf16)


def attention_backward(me, rand, glob, do, k, kv, q, mask, seg, lse_near, lse_far, lseg, w, resid):
    chunks = len(do)
    group, rows = do[0].shape
    heads = group // HEAD_DIM
    width = w.shape[0]
    length = rows * chunks
    whole = lambda: pl.BlockSpec(memory_space=pltpu.VMEM)
    return pl.pallas_call(
        functools.partial(backward_kernel, heads, chunks),
        out_shape=(
            jax.ShapeDtypeStruct((chunks, group, rows), bf16),
            jax.ShapeDtypeStruct((chunks, rows, heads * PAIR), bf16),
            jax.ShapeDtypeStruct((rows, width), f32),
        )
        + (jax.ShapeDtypeStruct((rows, width), bf16),) * (chunks - 1),
        in_specs=[pl.BlockSpec(memory_space=pltpu.SMEM)] * 3 + [whole() for _ in range(chunks + 10)],
        out_specs=tuple(whole() for _ in range(chunks + 2)),
        scratch_shapes=[
            pltpu.VMEM((group, length), bf16),
            pltpu.VMEM((heads, length + BLOCK, PAIR), f32),
            pltpu.VMEM((heads, length, PAIR), f32),
            pltpu.VMEM((heads, length, PAIR), f32),
            pltpu.VMEM((length + BLOCK, PAIR), f32),
            pltpu.VMEM((length // PAIR, 1, PAIR), f32),
            pltpu.VMEM((heads, length // PAIR, PAIR), f32),
            pltpu.VMEM((chunks, rows), f32),
        ],
        compiler_params=pltpu.CompilerParams(vmem_limit_bytes=VMEM_BYTES),
        cost_estimate=pl.CostEstimate(flops=30_000_000_000, bytes_accessed=24_000_000, transcendentals=8_000_000),
        name="attention_backward",
    )(me, rand, glob, *do, k, kv, q, mask, seg, lse_near, lse_far, lseg, w, resid)


def round_up(value, to):
    return -(-value // to) * to


def half_columns(ref, index, place):
    at = index // 2 * PAIR
    both = ref[:, at : at + PAIR].astype(f32)
    return both if index % 2 == place else pltpu.roll(both, BLOCK, 1)


def two_halves(first, second):
    lane = lax.broadcasted_iota(jnp.int32, (1, PAIR), 1)
    return jnp.where(lane < BLOCK, first, second)


def pack_kernel(seq_n, wq_ref, wk_ref, wv_ref, wo_ref, up_ref, down_ref, bup_ref, vec_ref, pack_ref, rest_ref):
    own, width = wq_ref.shape
    heads = width // HEAD_DIM // seq_n
    blocks, inner = pack_ref.shape[0], pack_ref.shape[2]
    for s in range(seq_n):
        pieces = [
            two_halves(half_columns(wk_ref, s * heads + h, 0), half_columns(wv_ref, s * heads + h, 1))
            for h in range(heads)
        ]
        for h in range(0, heads, 2):
            second = half_columns(wq_ref, s * heads + h + 1, 1) if h + 1 < heads else jnp.zeros((own, PAIR), f32)
            pieces.append(two_halves(half_columns(wq_ref, s * heads + h, 0), second))
        piece = jnp.concatenate(pieces, axis=1).astype(bf16)
        notes = jnp.concatenate([vec_ref[...], jnp.zeros((8, piece.shape[1] - width), bf16)], axis=1) if (
            piece.shape[1] > width
        ) else vec_ref[:, 0 : piece.shape[1]]
        for b in range(blocks):
            for i in range(inner):
                pack_ref[b, s, i, 0:own, :] = piece
                pack_ref[b, s, i, own : own + 8, :] = notes
    u = up_ref.shape[0]
    rest_ref[0:u, :] = up_ref[...]
    rest_ref[u : 2 * u, :] = down_ref[...]
    rest_ref[2 * u : 2 * u + own, :] = wo_ref[...]
    row = lax.broadcasted_iota(jnp.int32, (8, 1), 0)
    block = jnp.where(row == 7, bup_ref[...].astype(f32), vec_ref[...].astype(f32))
    rest_ref[2 * u + own : 2 * u + own + 8, :] = block.astype(bf16)


def packed_weights(w_q, w_k, w_v, w_o, w_up, w_down, b_up, vec, dp_n, seq_n, ffn_n):
    own, width = w_q.shape
    heads = width // HEAD_DIM // seq_n
    lanes = heads * PAIR + round_up(heads * HEAD_DIM, PAIR)
    u = w_up.shape[0]
    if own % 8 or u % 16:
        group = heads * HEAD_DIM
        cols = lambda w: w.reshape(own, seq_n, heads, HEAD_DIM).transpose(1, 0, 2, 3)
        kv = jnp.stack([cols(w_k), cols(w_v)], axis=3).reshape(seq_n, own, 2 * group)
        piece = jnp.concatenate([kv, cols(w_q).reshape(seq_n, own, group)], axis=2)
        piece = jnp.pad(piece, ((0, 0), (0, round_up(own, 8) - own), (0, lanes - 3 * group)))
        notes = jnp.broadcast_to(vec[None, :, :lanes], (seq_n, 8, lanes))
        piece = jnp.concatenate([piece, notes], axis=1)
        pack = jnp.broadcast_to(piece[None, :, None], (dp_n, seq_n, ffn_n) + piece.shape[1:])
        w_o = jnp.pad(w_o, ((0, round_up(own, 8) - own), (0, 0)))
        return pack, jnp.concatenate([w_up, w_down, w_o, vec[:7], b_up], axis=0)
    whole = lambda: pl.BlockSpec(memory_space=pltpu.VMEM)
    return pl.pallas_call(
        functools.partial(pack_kernel, seq_n),
        out_shape=(
            jax.ShapeDtypeStruct((dp_n, seq_n, ffn_n, own + 8, lanes), bf16),
            jax.ShapeDtypeStruct((2 * u + own + 8, width), bf16),
        ),
        in_specs=[whole() for _ in range(8)],
        out_specs=(whole(), whole()),
        name="packed_weights",
    )(w_q, w_k, w_v, w_o, w_up, w_down, b_up, vec)


def weights_kernel(chunks, direct, *refs):
    x_refs = refs[:chunks]
    dq_ref, dkv_ref, out_ref, sums_ref, acc, sum_sc = refs[chunks:]
    group = dq_ref.shape[1]
    lanes = dkv_ref.shape[2]
    full = acc.shape[0]
    x = jnp.concatenate([r[...] for r in x_refs], axis=0)
    dkv = jnp.concatenate([dkv_ref[c] for c in range(chunks)], axis=0)
    dq = jnp.concatenate([dq_ref[c] for c in range(chunks)], axis=1)
    ones = jnp.ones((8, x.shape[0]), bf16)

    @pl.when(pl.program_id(0) == 0)
    def _():
        acc[...] = jnp.zeros_like(acc)
        sum_sc[...] = jnp.zeros_like(sum_sc)

    acc[0:lanes, :] += dot_tn(dkv, x)
    acc[lanes : lanes + group, :] += dot_nn(dq, x)
    sum_sc[:, 0:lanes] += dot_nn(ones, dkv)
    sum_sc[:, lanes : lanes + group] += dot_nt(ones, dq)

    @pl.when(pl.program_id(0) == pl.num_programs(0) - 1)
    def _():
        grad = jnp.transpose(acc[...], (1, 0))
        sums_ref[...] = sum_sc[...]
        if direct:
            blocks, per, _ = out_ref.shape
            own = per - 8
            grad = grad.reshape(blocks, own, full)
            for b in range(blocks):
                out_ref[b, 0:own, :] = grad[b].astype(bf16)
                out_ref[b, own:, :] = sum_sc[...].astype(bf16)
        else:
            out_ref[...] = grad.astype(bf16)


def projection_gradients(x, dq, dkv, own, devices):
    chunks, group, rows = dq.shape
    width = x[0].shape[1]
    lanes = dkv.shape[2]
    full = lanes + round_up(group, PAIR)
    direct = own % 8 == 0
    tile = 256
    shape = (devices, own + 8, full) if direct else (width, full)
    out, sums = pl.pallas_call(
        functools.partial(weights_kernel, chunks, direct),
        grid=(rows // tile,),
        out_shape=(jax.ShapeDtypeStruct(shape, bf16), jax.ShapeDtypeStruct((8, full), f32)),
        in_specs=[pl.BlockSpec((tile, width), lambda i: (i, 0)) for _ in range(chunks)]
        + [
            pl.BlockSpec((chunks, group, tile), lambda i: (0, 0, i)),
            pl.BlockSpec((chunks, tile, lanes), lambda i: (0, i, 0)),
        ],
        out_specs=(
            pl.BlockSpec(shape, lambda i: (0,) * len(shape), pipeline_mode=pl.Buffered(1)),
            pl.BlockSpec((8, full), lambda i: (0, 0)),
        ),
        scratch_shapes=[pltpu.VMEM((full, width), f32), pltpu.VMEM((8, full), f32)],
        compiler_params=pltpu.CompilerParams(vmem_limit_bytes=VMEM_BYTES),
        cost_estimate=pl.CostEstimate(flops=4_000_000_000, bytes_accessed=12_000_000, transcendentals=0),
        name="projection_gradients",
    )(*x, dq, dkv)
    if not direct:
        out = jnp.pad(out.reshape(devices, own, full), ((0, 0), (0, round_up(own, 8) - own), (0, 0)))
        out = jnp.concatenate([out, jnp.broadcast_to(sums[None].astype(bf16), (devices, 8, full))], axis=1)
    return out


def unpack_kernel(own, got_ref, q_ref, k_ref, v_ref, sums_ref, tot):
    dp_n, seq_n, ffn_n, per, full = got_ref.shape
    width = q_ref.shape[1]
    heads = width // HEAD_DIM // seq_n
    for s in range(seq_n):
        total = jnp.zeros((per, full), f32)
        for d in range(dp_n):
            for f in range(ffn_n):
                total = total + got_ref[d, s, f].astype(f32)
        tot[s] = total
        sums_ref[s : s + 1, :] = total[per - 8 : per - 7, :]
    for w in range(width // PAIR):
        spots = [((2 * w + i) // heads, (2 * w + i) % heads) for i in range(2)]
        cols = slice(w * PAIR, (w + 1) * PAIR)
        for ref, where in (
            (k_ref, lambda h: 2 * h),
            (v_ref, lambda h: 2 * h + 1),
            (q_ref, lambda h: 2 * heads + h),
        ):
            both = [half_columns(tot.at[g], where(h), i) for i, (g, h) in enumerate(spots)]
            ref[:, cols] = two_halves(*both)[0:own]


def unpacked_gradients(got, own, width):
    dp_n, seq_n, ffn_n, per, full = got.shape
    whole = lambda: pl.BlockSpec(memory_space=pltpu.VMEM)
    return pl.pallas_call(
        functools.partial(unpack_kernel, own),
        out_shape=(jax.ShapeDtypeStruct((own, width), f32),) * 3 + (jax.ShapeDtypeStruct((seq_n, full), f32),),
        in_specs=[whole()],
        out_specs=tuple(whole() for _ in range(4)),
        scratch_shapes=[pltpu.VMEM((seq_n, per, full), f32)],
        compiler_params=pltpu.CompilerParams(vmem_limit_bytes=VMEM_BYTES),
        name="unpacked_gradients",
    )(got)


NORM_EPS = 1e-12


def transposed(value):
    return jnp.transpose(value.astype(f32), (1, 0)).astype(bf16)


def unit_rows(value):
    center = value - jnp.mean(value, axis=-1, keepdims=True)
    scale = lax.rsqrt(jnp.mean(center * center, axis=-1, keepdims=True) + NORM_EPS)
    return center * scale, scale


def unit_rows_back(grad, unit, scale):
    return scale * (
        grad - jnp.mean(grad, axis=-1, keepdims=True) - unit * jnp.mean(grad * unit, axis=-1, keepdims=True)
    )


def rows_kernel(parts, blocks, up_rows, own, me_ref, *refs):
    ctx_refs = refs[:parts]
    (x_ref, cot_ref, rest_ref, wo_ref, vec_ref, bup_ref, out_ref, resid_ref, hid_ref, pre_ref, nlt_ref, gft_ref,
     gb_ref) = refs[parts : parts + 13]
    do_refs = refs[parts + 13 : 2 * parts + 13]
    sums_ref, gbup_ref, slope_sc, wo_sc, wide_sc = refs[2 * parts + 13 :]
    group = ctx_refs[0].shape[0]
    width = x_ref.shape[1]

    def up(f):
        return rest_ref[:, f, 0:up_rows, :].reshape(width, rest_ref.shape[3])

    def down(f):
        return rest_ref[:, f, up_rows : 2 * up_rows, :].reshape(width, rest_ref.shape[3])

    def own_rows(k):
        return pl.ds(pl.multiple_of((me_ref[0] ^ k) * group, group), group)

    @pl.when(pl.program_id(0) == 0)
    def _():
        sums_ref[...] = jnp.zeros_like(sums_ref)
        gbup_ref[...] = jnp.zeros_like(gbup_ref)
        if own:
            for o in range(rest_ref.shape[0]):
                for f in range(blocks):
                    to = (o * blocks + f) * own
                    wide_sc[to : to + own, :] = rest_ref[o, f, 2 * up_rows : 2 * up_rows + own, :].astype(f32)
            wo_sc[...] = wide_sc[...].astype(bf16)
        else:
            wo_sc[...] = wo_ref[...]

    def bias_up(f):
        if own:
            row = rest_ref[0, f, 2 * up_rows + own : 2 * up_rows + own + 8, :].astype(f32)
            return row[7:8, :]
        return bup_ref[f : f + 1, :]

    ctx = jnp.concatenate([r[...] for r in ctx_refs], axis=0)
    w_o = jnp.concatenate([wo_sc[own_rows(k), :] for k in range(parts)], axis=0)
    resid_one = x_ref[...].astype(f32) + (dot_tn(ctx, w_o) + vec_ref[0:1, :])
    unit_one, scale_one = unit_rows(resid_one)
    normed_one = unit_one * vec_ref[2:3, :] + vec_ref[3:4, :]
    low = normed_one.astype(bf16)
    nlt_ref[...] = transposed(normed_one)
    total = normed_one + vec_ref[1:2, :]
    pre = dot_nn(low, up(0)) + bias_up(0)
    for f in range(blocks):
        later = dot_nn(low, up(f + 1)) + bias_up(f + 1) if f + 1 < blocks else None
        phi = 0.5 + 0.5 * lax.erf(pre * (0.5 ** 0.5))
        slope_sc[f] = phi + pre * (jnp.exp(-0.5 * pre * pre) * 0.3989422804014327)
        hid = (pre * phi).astype(bf16)
        hid_ref[f] = hid
        total = total + dot_nt(hid, down(f))
        pre = later
    unit_two, scale_two = unit_rows(total)
    out_ref[...] = (unit_two * vec_ref[4:5, :] + vec_ref[5:6, :]).astype(bf16)
    cot = cot_ref[...].astype(f32)
    grad_two = unit_rows_back(cot * vec_ref[4:5, :], unit_two, scale_two)
    grad_ffn = grad_two.astype(bf16)
    gft_ref[...] = transposed(grad_two)
    grad_normed = grad_two
    back = dot_nn(grad_ffn, down(0))
    for f in range(blocks):
        later = dot_nn(grad_ffn, down(f + 1)) if f + 1 < blocks else None
        grad_pre = (back * slope_sc[f]).astype(bf16)
        pre_ref[f] = grad_pre
        gbup_ref[f : f + 1, :] += jnp.sum(grad_pre.astype(f32), axis=0, keepdims=True)
        grad_normed = grad_normed + dot_nt(grad_pre, up(f))
        back = later
    resid = unit_rows_back(grad_normed * vec_ref[2:3, :], unit_one, scale_one)
    resid_ref[...] = resid
    branch = resid.astype(bf16)
    gb_ref[...] = branch
    do = dot_nt(w_o, branch).astype(bf16)
    for k in range(parts):
        do_refs[k][...] = do[k * group : (k + 1) * group]
    for row, value in enumerate(
        (branch.astype(f32), grad_ffn.astype(f32), grad_normed * unit_one, grad_normed, cot * unit_two, cot)
    ):
        sums_ref[row : row + 1, :] += jnp.sum(value, axis=0, keepdims=True)


def rows_chain(me, ctx_parts, x, cot, rest, up_rows, own, w_o, vecs, bias_up):
    parts = len(ctx_parts)
    group, rows = ctx_parts[0].shape
    width = x.shape[1]
    outer, blocks, per, hidden = rest.shape
    tile = 256
    once = lambda shape: pl.BlockSpec(shape, lambda i: (0,) * len(shape), pipeline_mode=pl.Buffered(1))
    tall = pl.BlockSpec((tile, width), lambda i: (i, 0))
    wide = pl.BlockSpec((width, tile), lambda i: (0, i))
    cube = pl.BlockSpec((blocks, tile, hidden), lambda i: (0, i, 0))
    return pl.pallas_call(
        functools.partial(rows_kernel, parts, blocks, up_rows, own),
        grid=(rows // tile,),
        out_shape=(
            jax.ShapeDtypeStruct((rows, width), bf16),
            jax.ShapeDtypeStruct((rows, width), f32),
            jax.ShapeDtypeStruct((blocks, rows, hidden), bf16),
            jax.ShapeDtypeStruct((blocks, rows, hidden), bf16),
            jax.ShapeDtypeStruct((width, rows), bf16),
            jax.ShapeDtypeStruct((width, rows), bf16),
            jax.ShapeDtypeStruct((rows, width), bf16),
        )
        + (jax.ShapeDtypeStruct((group, rows), bf16),) * parts
        + (jax.ShapeDtypeStruct((8, width), f32), jax.ShapeDtypeStruct((8, hidden), f32)),
        in_specs=[pl.BlockSpec(memory_space=pltpu.SMEM)]
        + [pl.BlockSpec((group, tile), lambda i: (0, i))] * parts
        + [tall, tall, once(rest.shape), once(w_o.shape), once(vecs.shape), once(bias_up.shape)],
        out_specs=(
            tall, tall, cube, cube, wide, wide, tall,
        )
        + (pl.BlockSpec((group, tile), lambda i: (0, i)),) * parts
        + (pl.BlockSpec((8, width), lambda i: (0, 0)), pl.BlockSpec((8, hidden), lambda i: (0, 0))),
        scratch_shapes=[
            pltpu.VMEM((blocks, tile, hidden), f32),
            pltpu.VMEM((width, width), bf16),
            pltpu.VMEM((width, width), f32),
        ],
        compiler_params=pltpu.CompilerParams(vmem_limit_bytes=VMEM_BYTES),
        cost_estimate=pl.CostEstimate(flops=22_000_000_000, bytes_accessed=40_000_000, transcendentals=6_000_000),
        name="rows_chain",
    )(me, *ctx_parts, x, cot, rest, w_o, vecs, bias_up)


def outer_kernel(parts, up_rows, own, apart, me_ref, *refs):
    ctx_refs = refs[:parts]
    nlt_ref, gft_ref, gb_ref, pre_ref, hid_ref, sums_ref, gbup_ref, out_ref = refs[parts : parts + 8]
    wo_sc = refs[-1]
    slabs, hidden = out_ref.shape[0], out_ref.shape[3]
    group = ctx_refs[0].shape[0]
    f = pl.program_id(0)
    up = dot_nn(nlt_ref[...], pre_ref[0]).astype(bf16).reshape(slabs, up_rows, hidden)
    if apart:
        refs[parts + 8][:, 0, :, :] = up[:, 0:apart]
    out_ref[:, 0, 0 : up_rows - apart, :] = up[:, apart:]
    at = up_rows - apart
    down = dot_nn(gft_ref[...], hid_ref[0]).astype(bf16)
    out_ref[:, 0, at : at + up_rows, :] = down.reshape(slabs, up_rows, hidden)
    at += up_rows
    if not own:
        return

    @pl.when(f == 0)
    def _():
        for k in range(parts):
            wo_sc[k] = dot_nn(ctx_refs[k][...], gb_ref[...])

    share = slabs // parts
    stride = group // share
    for k in range(parts):
        for j in range(share):
            rows = pl.ds(pl.multiple_of(j * stride + f * own, 8), own)
            out_ref[(me_ref[0] ^ k) * share + j, 0, at : at + own, :] = wo_sc[k, rows, :].astype(bf16)
    small = jnp.concatenate([gbup_ref[pl.ds(f, 1), :], sums_ref[0:7, :]], axis=0).astype(bf16)
    for o in range(slabs):
        out_ref[o, 0, at + own :, :] = small


def outer_products(me, ctx_parts, nlt, gft, gb, pre, hid, sums, gbup, slabs, up_rows, own, apart):
    blocks, rows, hidden = pre.shape
    parts = len(ctx_parts)
    group = ctx_parts[0].shape[0]
    per = 2 * up_rows - apart + (own + 8 if own else 0)
    sizes = (per, apart) if apart else (per,)
    once = lambda shape: pl.BlockSpec(shape, lambda i: (0,) * len(shape), pipeline_mode=pl.Buffered(1))
    return pl.pallas_call(
        functools.partial(outer_kernel, parts, up_rows, own, apart),
        grid=(blocks,),
        out_shape=tuple(jax.ShapeDtypeStruct((slabs, blocks, r, hidden), bf16) for r in sizes),
        in_specs=[pl.BlockSpec(memory_space=pltpu.SMEM)]
        + [once(c.shape) for c in ctx_parts]
        + [
            once(nlt.shape),
            once(gft.shape),
            once(gb.shape),
            pl.BlockSpec((1, rows, hidden), lambda i: (i, 0, 0)),
            pl.BlockSpec((1, rows, hidden), lambda i: (i, 0, 0)),
            once(sums.shape),
            once(gbup.shape),
        ],
        out_specs=tuple(pl.BlockSpec((slabs, 1, r, hidden), lambda i: (0, i, 0, 0)) for r in sizes),
        scratch_shapes=[pltpu.VMEM((parts, group, gb.shape[1]), f32)],
        compiler_params=pltpu.CompilerParams(vmem_limit_bytes=VMEM_BYTES),
        cost_estimate=pl.CostEstimate(flops=11_000_000_000, bytes_accessed=28_000_000, transcendentals=0),
        name="outer_products",
    )(me, *ctx_parts, nlt, gft, gb, pre, hid, sums, gbup)


def finish_kernel(up_rows, own, apart_ref, total_ref, up_ref, down_ref, wo_ref, small_ref):
    apart = apart_ref.shape[1]
    total = jnp.zeros(apart_ref.shape[1:], f32)
    for d in range(apart_ref.shape[0]):
        total = total + apart_ref[d].astype(f32)
    up_ref[0:apart, :] = total
    rest = total_ref[...].astype(f32)
    at = up_rows - apart
    up_ref[apart:, :] = rest[0:at]
    down_ref[...] = rest[at : at + up_rows]
    at += up_rows
    wo_ref[...] = rest[at : at + own]
    small_ref[...] = rest[at + own : at + own + 8]


def finished(apart, total, up_rows, own):
    hidden = total.shape[1]
    whole = lambda: pl.BlockSpec(memory_space=pltpu.VMEM)
    return pl.pallas_call(
        functools.partial(finish_kernel, up_rows, own),
        out_shape=tuple(jax.ShapeDtypeStruct((r, hidden), f32) for r in (up_rows, up_rows, own, 8)),
        in_specs=[whole(), whole()],
        out_specs=tuple(whole() for _ in range(4)),
        name="finished",
    )(apart, total)


ALL = ("dp", "seq", "ffn")


def flip_send(array, axis, bits):
    count = lax.axis_size(axis)
    return lax.ppermute(array, axis, [(i, i ^ bits) for i in range(count)])


def shards(
    tokens, w_query, w_key, w_value, w_output, b_query, b_value, b_output, w_up, b_up, w_down, b_down,
    gain_attn, shift_attn, gain_ffn, shift_ffn, segment_ids, random_blocks, global_blocks, cotangent,
):
    seq_n, dp_n, ffn_n = lax.axis_size("seq"), lax.axis_size("dp"), lax.axis_size("ffn")
    outer, devices = dp_n * seq_n, dp_n * seq_n * ffn_n
    me = lax.axis_index("seq")
    here = (lax.axis_index("dp") * seq_n + me) * ffn_n + lax.axis_index("ffn")
    own, width = w_query.shape
    own_pad = round_up(own, 8)
    group = width // seq_n
    heads = group // HEAD_DIM
    features = tokens[0]
    rows = features.shape[0]
    order = jnp.stack([me ^ k for k in range(seq_n)])
    me_ref = me.astype(jnp.int32)[None]

    near = [features] + [None] * (seq_n - 1)
    for k in sorted(range(1, seq_n), key=lambda k: (k & (k - 1), -k)):
        bit = k & -k
        near[k] = flip_send(features if bit == k else near[k ^ bit], "seq", bit)

    vec = jnp.stack([b_output, b_down, gain_attn, shift_attn, gain_ffn, shift_ffn, b_query, b_value])
    vec = jnp.pad(vec, ((0, 0), (0, width - own)))
    seg = segment_ids[0].reshape(seq_n, rows)
    rand = random_blocks.reshape(-1)
    pack, rest = packed_weights(
        w_query, w_key, w_value, w_output, w_up, w_down, b_up[None], vec, dp_n, seq_n, ffn_n
    )
    lanes = pack.shape[4]
    pack, seg, rand = lax.optimization_barrier((pack, seg, rand))
    pack = lax.all_to_all(
        pack.reshape(devices, own_pad + 8, lanes), ALL, split_axis=0, concat_axis=0, tiled=True
    )
    rest = lax.all_gather(rest, ALL, axis=0, tiled=False)
    w_own = pack[:, :own].reshape(width, lanes)
    share = devices // seq_n
    biases = lax.dynamic_slice(pack, (share * me, own_pad + 6, 0), (share, 2, own))
    biases = biases.transpose(1, 0, 2).reshape(2, group).astype(f32)
    by_head = biases[1].reshape(heads, 1, HEAD_DIM)
    b_kv = jnp.concatenate([jnp.zeros_like(by_head), by_head], axis=1).reshape(1, heads * PAIR)

    far = seq_n // 2
    ctx_far, (lse_far, lseg, glob_ctx, k_all, v_all, q_all, mask_all) = attention_forward(
        me_ref, rand, global_blocks, near, seg, w_own, b_kv, biases[0][:, None]
    )
    ctx_parts = [None] * far + [flip_send(ctx_far[k - far], "seq", k) for k in range(far, seq_n)]
    ctx_near, lse_near = attention_near(
        me_ref, rand, global_blocks, k_all, v_all, q_all, mask_all, glob_ctx, seq_n
    )
    ctx_parts[far:], ctx_parts[0] = lax.optimization_barrier((ctx_parts[far:], ctx_near[0]))
    for k in range(1, far):
        ctx_parts[k] = flip_send(ctx_near[k], "seq", k)

    up_rows = w_up.shape[0]
    at = 2 * up_rows
    rest = rest.reshape(outer, ffn_n, rest.shape[1], width)
    w_o = rest[:, :, at : at + own].reshape(width, width)
    bias_up = rest[0, :, at + own_pad + 7].astype(f32)
    vecs = pack[:, own_pad:, :own].transpose(1, 0, 2).reshape(8, width).astype(f32)
    direct = up_rows % 16 == 0 and own % 8 == 0 and outer % seq_n == 0 and (outer // seq_n) * ffn_n * own == group
    if not direct:
        rest = rest[:, :, :at].reshape(outer, ffn_n, 2, up_rows, width).transpose(1, 2, 0, 3, 4)
        rest = rest.reshape(1, ffn_n, 2 * outer * up_rows, width)
    slabs, slab_rows = (outer, up_rows) if direct else (1, outer * up_rows)

    got = rows_chain(
        me_ref, ctx_parts, features, cotangent[0], rest, slab_rows, own if direct else 0,
        jnp.zeros((8, PAIR), bf16) if direct else w_o, vecs, jnp.zeros((8, PAIR), f32) if direct else bias_up,
    )
    out, grad_resid_one, hidden, grad_pre, normed_t, grad_ffn_t, grad_branch = got[:7]
    grad_ctx, (sums, grad_bias_up) = got[7 : 7 + seq_n], got[7 + seq_n :]
    do = [grad_ctx[0]] + [flip_send(grad_ctx[k], "seq", k) for k in range(1, seq_n)]

    payload = outer_products(
        me_ref, ctx_parts, normed_t, grad_ffn_t, grad_branch, grad_pre, hidden, sums, grad_bias_up, slabs, slab_rows,
        own if direct else 0, APART if direct else 0,
    )
    payload, apart = payload if direct else (payload[0], None)
    if not direct:
        grad_out = dot_nn(jnp.concatenate(ctx_parts, axis=0), grad_branch).astype(bf16)
        grad_out = grad_out.reshape(seq_n, group, width)[order].reshape(outer, ffn_n, own, width)
        top = jnp.broadcast_to(grad_bias_up[None, :ffn_n, None], (outer, ffn_n, 1, width))
        small = jnp.concatenate([top, jnp.broadcast_to(sums[None, None, :7], (outer, ffn_n, 7, width))], axis=2)
        small = small.astype(bf16)
        payload = payload.reshape(ffn_n, 2, outer, up_rows, width).transpose(2, 0, 1, 3, 4)
        payload = jnp.concatenate([payload.reshape(outer, ffn_n, at, width), grad_out, small], axis=2)
        payload = jnp.pad(payload, ((0, 0), (0, 0), (0, -payload.shape[2] % 32), (0, 0)))
    payload, apart, do = lax.optimization_barrier((payload, apart, do))
    total = lax.psum_scatter(payload.reshape(-1, width), ("dp", "seq"), scatter_dimension=0, tiled=True)
    if direct:
        apart = lax.all_to_all(
            apart.reshape(devices, APART, width), ALL, split_axis=0, concat_axis=0, tiled=True
        )

    got = attention_backward(
        me_ref, rand, global_blocks, do, k_all, v_all, q_all, mask_all, seg, lse_near, lse_far, lseg, w_own,
        grad_resid_one,
    )
    dq, dkv, grad_features = got[:3]
    part = [None] + list(got[3:])
    bit = 1
    while bit < seq_n:
        for k in range(seq_n):
            if k & -k == bit and k != bit:
                came = flip_send(part[k], "seq", bit).astype(f32)
                part[k ^ bit] = (part[k ^ bit].astype(f32) + came).astype(bf16)
        bit *= 2
    grad_w = projection_gradients(near, dq, dkv, own, devices)
    grad_w, part = lax.optimization_barrier((grad_w, part[1:]))
    grad_w, apart = lax.optimization_barrier((grad_w, apart))
    part = [None] + part
    bit = seq_n // 2
    part[bit], total = lax.optimization_barrier((part[bit], total))
    total = lax.psum_scatter(total, "ffn", scatter_dimension=0, tiled=True)
    while bit:
        grad_features = grad_features + flip_send(part[bit], "seq", bit).astype(f32)
        bit //= 2
    grad_w = lax.all_to_all(grad_w, ALL, split_axis=0, concat_axis=0, tiled=True)
    if direct:
        out_up, out_down, out_output, notes = finished(apart, total, up_rows, own)
    else:
        total = total.astype(f32)
        out_up, out_down, out_output = total[:up_rows], total[up_rows:at], total[at : at + own]
        notes = total[at + own : at + own + 8]
    out_bias_up = notes[0]
    out_vecs = lax.dynamic_slice(notes, (1, here * own), (6, own))
    out_query, out_key, out_value, col_sums = unpacked_gradients(
        grad_w.reshape(dp_n, seq_n, ffn_n, own_pad + 8, lanes), own, width
    )
    row = lax.dynamic_index_in_dim(col_sums, here // share, keepdims=False)
    row = jnp.stack([row[heads * PAIR : heads * PAIR + group], row[: heads * PAIR].reshape(heads, 2, HEAD_DIM)[:, 1].reshape(group)])
    out_b = lax.dynamic_slice(row, (0, here % share * own), (2, own))
    return (
        out[None],
        grad_features[None],
        out_query,
        out_key,
        out_value,
        out_output,
        out_b[0],
        out_b[1],
        out_vecs[0],
        out_up,
        out_bias_up,
        out_down,
        out_vecs[1],
        out_vecs[2],
        out_vecs[3],
        out_vecs[4],
        out_vecs[5],
    )


def solution(mesh):
    return jax.shard_map(
        shards,
        mesh=mesh,
        in_specs=(
            P(("dp", "ffn"), "seq", None),
            P(("dp", "seq", "ffn"), None),
            P(("dp", "seq", "ffn"), None),
            P(("dp", "seq", "ffn"), None),
            P(("dp", "seq", "ffn"), None),
            P(("dp", "seq", "ffn")),
            P(("dp", "seq", "ffn")),
            P(("dp", "seq", "ffn")),
            P(("dp", "seq"), "ffn"),
            P("ffn"),
            P(("dp", "seq"), "ffn"),
            P(("dp", "seq", "ffn")),
            P(("dp", "seq", "ffn")),
            P(("dp", "seq", "ffn")),
            P(("dp", "seq", "ffn")),
            P(("dp", "seq", "ffn")),
            P(("dp", "ffn"), None),
            P(("dp", "ffn"), "seq", None, None),
            P(("dp", "ffn"), None),
            P(("dp", "ffn"), "seq", None),
        ),
        out_specs=(
            P(("dp", "ffn"), "seq", None),
            P(("dp", "ffn"), "seq", None),
            P(("dp", "seq", "ffn"), None),
            P(("dp", "seq", "ffn"), None),
            P(("dp", "seq", "ffn"), None),
            P(("dp", "seq", "ffn"), None),
            P(("dp", "seq", "ffn")),
            P(("dp", "seq", "ffn")),
            P(("dp", "seq", "ffn")),
            P(("dp", "seq"), "ffn"),
            P("ffn"),
            P(("dp", "seq"), "ffn"),
            P(("dp", "seq", "ffn")),
            P(("dp", "seq", "ffn")),
            P(("dp", "seq", "ffn")),
            P(("dp", "seq", "ffn")),
            P(("dp", "seq", "ffn")),
        ),
        check_vma=False,
    )
```

```python
import functools
import jax
import jax.numpy as jnp
from jax import lax
from jax.experimental import pallas as pl
from jax.sharding import PartitionSpec as P
from jax.experimental.pallas import tpu as pltpu

HEAD_DIM = 64
BLOCK = 64
PAIR = 2 * BLOCK
MASKED = -1e30
bf16 = jnp.bfloat16
f32 = jnp.float32


def dot_nn(a, b):
    return lax.dot_general(a, b, (((1,), (0,)), ((), ())), preferred_element_type=f32)


def dot_nt(a, b):
    return lax.dot_general(a, b, (((1,), (1,)), ((), ())), preferred_element_type=f32)


def dot_tn(a, b):
    return lax.dot_general(a, b, (((0,), (0,)), ((), ())), preferred_element_type=f32)


def slots(rand_ref, glob_ref, flip, head, pair, nblocks):
    first = (2 * pair) ^ flip

    def row(block):
        return pl.multiple_of(block * BLOCK, BLOCK)

    def near(block):
        bad = (block < 0) | (block >= nblocks) | (block == glob_ref[0, 0]) | (block == glob_ref[0, 1])
        return row(jnp.where(bad, nblocks, block ^ flip))

    def drawn(block):
        at = (head * nblocks + block) * 3
        return [row(rand_ref[at + j] ^ flip) for j in range(3)]

    shared = [near(first), near(first + 1)] + [row(glob_ref[0, j] ^ flip) for j in range(2)]
    return shared, [near(first - 1)] + drawn(first), [near(first + 2)] + drawn(first + 1)


def stack_rows(ref, offsets, lanes):
    return jnp.concatenate([ref[pl.ds(o, BLOCK), lanes] for o in offsets], axis=0)


def lane_halves(width, dtype):
    lane = lax.broadcasted_iota(jnp.int32, (1, width), 1) % PAIR
    first = (lane < BLOCK).astype(dtype)
    second = (lane >= BLOCK).astype(dtype)
    return first, second


UNROLL = 4
BACK_UNROLL = 4
APART = 0
VMEM_BYTES = 62 << 20


def head_lanes(h):
    return slice(h * PAIR, (h + 1) * PAIR)


def query_columns(q_ref, mask_ref, h, at):
    return jnp.concatenate([q_ref[h * BLOCK : (h + 1) * BLOCK, pl.ds(at, PAIR)], mask_ref[:, pl.ds(at, PAIR)]], axis=0)


def global_queries(q_ref, mask_ref, h, gl):
    return jnp.concatenate(
        [
            global_columns(q_ref, slice(h * BLOCK, (h + 1) * BLOCK), gl),
            global_columns(mask_ref, slice(0, BLOCK), gl),
        ],
        axis=0,
    ).astype(bf16)


def placed(me_ref, glob_ref, nblocks, chunks):
    flip = me_ref[0] * (nblocks // chunks)
    return flip, [glob_ref[0, j] ^ flip for j in range(2)]


def global_columns(src_ref, rows, gl):
    lane = lax.broadcasted_iota(jnp.int32, (1, PAIR), 1)
    parts = []
    for g in range(2):
        block = gl[g]
        at = pl.multiple_of((block // 2) * PAIR, PAIR)
        both = src_ref[rows, pl.ds(at, PAIR)].astype(f32)
        moved = pltpu.roll(both, BLOCK, 1)
        parts.append(jnp.where(block % 2 == g, both, moved))
    return jnp.where(lane < BLOCK, parts[0], parts[1])


def put_global_columns(dst_ref, rows, gl, value, per_chunk, low, high):
    lane = lax.broadcasted_iota(jnp.int32, (1, PAIR), 1)
    moved = pltpu.roll(value, BLOCK, 1)
    for g in range(2):
        pair = gl[g] // 2
        half = gl[g] % 2
        chunk = pair // per_chunk

        @pl.when((chunk >= low) & (chunk < high))
        def _():
            at = pl.multiple_of((pair % per_chunk) * PAIR, PAIR)
            src = jnp.where(half == g, value, moved)
            old = dst_ref[chunk - low, rows, pl.ds(at, PAIR)].astype(f32)
            new = jnp.where((lane >= BLOCK) == (half == 1), src, old)
            dst_ref[chunk - low, rows, pl.ds(at, PAIR)] = new.astype(dst_ref.dtype)


def project_rows(x, seg, w_ref, wq, bkv_ref, bq_ref, k_ref, v_ref, q_ref, mask_ref, at):
    n = x.shape[0]
    lanes = v_ref.shape[1]
    y = dot_nn(x, w_ref[:, 0:lanes]) + bkv_ref[...]
    spot = lax.broadcasted_iota(jnp.int32, (PAIR, n), 0) - BLOCK
    mark = jnp.transpose((spot == seg).astype(f32), (1, 0))
    lane = lax.broadcasted_iota(jnp.int32, (1, PAIR), 1)
    rows = pl.ds(at, n)
    v_ref[rows, :] = y.astype(bf16)
    for h in range(lanes // PAIR):
        k_ref[rows, head_lanes(h)] = jnp.where(lane < BLOCK, y[:, head_lanes(h)], mark).astype(bf16)
    z = (dot_nt(wq, x) + bq_ref[...]).astype(bf16)
    q_ref[:, rows] = (z.astype(f32) * HEAD_DIM ** -0.5).astype(bf16)
    row = lax.broadcasted_iota(jnp.int32, (BLOCK, n), 0)
    mask_ref[:, rows] = jnp.where((row <= 16) & (row != seg), MASKED, 0.0).astype(bf16)


def query_weights(w_ref, heads):
    at = heads * PAIR
    cols = w_ref[:, at : at + 2 * PAIR].astype(f32)
    return jnp.transpose(cols, (1, 0))[0 : heads * HEAD_DIM].astype(bf16)


def sparse_forward(heads, low, high, per_chunk, rand_ref, glob_ref, flip, k_ref, kv_ref, q_ref, mask_ref, out_ref, lse_ref):
    nblocks = (k_ref.shape[0] - BLOCK) // BLOCK
    first, second = lane_halves(PAIR, bf16)
    lane = lax.broadcasted_iota(jnp.int32, (1, PAIR), 1)

    def one_pair(spot):
        chunk = spot // per_chunk
        local = pl.multiple_of((spot % per_chunk) * PAIR, PAIR)
        pair = low * per_chunk + spot
        at = pl.multiple_of(pair * PAIR, PAIR)
        for h in range(heads):
            shared, mine, other = slots(rand_ref, glob_ref, flip, h, pair, nblocks)
            kl = head_lanes(h)
            q = query_columns(q_ref, mask_ref, h, at)
            s_sh = dot_nn(stack_rows(k_ref, shared, kl), q)
            k_pr = jnp.concatenate([stack_rows(k_ref, mine, kl), stack_rows(k_ref, other, kl)], axis=1)
            s_pr = dot_nn(k_pr, jnp.concatenate([q * first, q * second], axis=0))
            peak = jnp.maximum(jnp.max(s_sh, axis=0, keepdims=True), jnp.max(s_pr, axis=0, keepdims=True))
            e_sh = jnp.exp(s_sh - peak)
            e_pr = jnp.exp(s_pr - peak)
            total = jnp.sum(e_sh, axis=0, keepdims=True) + jnp.sum(e_pr, axis=0, keepdims=True)
            inv = 1.0 / total
            p_sh = (e_sh * inv).astype(bf16)
            p_pr = (e_pr * inv).astype(bf16)
            v_pr = jnp.concatenate([stack_rows(kv_ref, mine, kl), stack_rows(kv_ref, other, kl)], axis=1)
            o_sh = dot_tn(stack_rows(kv_ref, shared, kl), p_sh)
            o_pr = dot_tn(v_pr, p_pr)
            ctx = o_sh[BLOCK:PAIR] + jnp.where(lane < BLOCK, o_pr[BLOCK:PAIR], o_pr[PAIR + BLOCK : 2 * PAIR])
            out_ref[chunk, h * BLOCK : (h + 1) * BLOCK, pl.ds(local, PAIR)] = ctx.astype(bf16)
            lse_ref[h, pl.ds(spot, 1), :] = peak + jnp.log(total)

    @pl.loop(0, (high - low) * per_chunk // UNROLL)
    def _(some):
        for i in range(UNROLL):
            one_pair(UNROLL * some + i)


def forward_kernel(heads, chunks, me_ref, rand_ref, glob_ref, *refs):
    x_refs = refs[0:chunks]
    seg_ref, w_ref, bkv_ref, bq_ref = refs[chunks : chunks + 4]
    far = chunks // 2
    out_refs = refs[chunks + 4 : chunks + 4 + far]
    lse_ref, lseg_ref, glob_ctx_ref, k_sc, v_sc, q_sc, mask_sc, s_sc, out_ref, seg_sc = refs[chunks + 4 + far :]
    rows = x_refs[0].shape[0]
    length = rows * chunks
    per_chunk = length // PAIR // chunks
    flip, gl = placed(me_ref, glob_ref, length // BLOCK, chunks)
    tile = 256
    wq = query_weights(w_ref, heads)
    for c in range(chunks):
        seg_sc[c : c + 1, :] = seg_ref[pl.ds(me_ref[0] ^ c, 1), :]
    for c in range(chunks):

        @pl.loop(0, rows // tile)
        def _(t):
            at = pl.multiple_of(t * tile, tile)
            project_rows(
                x_refs[c][pl.ds(at, tile), :], seg_sc[c : c + 1, pl.ds(at, tile)], w_ref, wq, bkv_ref, bq_ref,
                k_sc, v_sc, q_sc, mask_sc, pl.multiple_of(c * rows + t * tile, tile),
            )

    null_lane = lax.broadcasted_iota(jnp.int32, (BLOCK, heads * PAIR), 1) % PAIR
    k_sc[pl.ds(length, BLOCK), :] = (null_lane == BLOCK + 16).astype(f32).astype(bf16)
    v_sc[pl.ds(length, BLOCK), :] = jnp.zeros((BLOCK, heads * PAIR), bf16)
    sparse_forward(heads, far, chunks, per_chunk, rand_ref, glob_ref, flip, k_sc, v_sc, q_sc, mask_sc, out_ref, lse_ref)

    step = 512
    queries = [global_queries(q_sc, mask_sc, h, gl) for h in range(heads)]

    def score(c, peaks):
        at = pl.multiple_of(c * step, step)
        new = []
        for h in range(heads):
            got = dot_nn(k_sc[pl.ds(at, step), head_lanes(h)], queries[h])
            s_sc[h, pl.ds(at, step), :] = got
            new.append(jnp.maximum(peaks[h], jnp.max(got, axis=0, keepdims=True)))
        return tuple(new)

    peaks = lax.fori_loop(0, length // step, score, (jnp.full((1, PAIR), MASKED, f32),) * heads)

    def gather(c, carry):
        at = pl.multiple_of(c * step, step)
        new = []
        for h in range(heads):
            total, ctx = carry[h]
            e = jnp.exp(s_sc[h, pl.ds(at, step), :] - peaks[h])
            ctx = ctx + dot_tn(v_sc[pl.ds(at, step), head_lanes(h)], e.astype(bf16))
            new.append((total + jnp.sum(e, axis=0, keepdims=True), ctx))
        return tuple(new)

    start = (jnp.zeros((1, PAIR), f32), jnp.zeros((PAIR, PAIR), f32))
    sums = lax.fori_loop(0, length // step, gather, (start,) * heads)
    for h in range(heads):
        total, ctx = sums[h]
        ctx = ctx[BLOCK:PAIR] * (1.0 / total)
        glob_ctx_ref[h] = ctx
        put_global_columns(out_ref, slice(h * BLOCK, (h + 1) * BLOCK), gl, ctx, per_chunk, far, chunks)
        lseg_ref[h : h + 1, :] = peaks[h] + jnp.log(total)
    for c in range(far):
        out_refs[c][...] = out_ref[c]


def attention_forward(me, rand, glob, x, seg, w, b_kv, b_q):
    chunks = len(x)
    far = chunks // 2
    rows = x[0].shape[0]
    length = rows * chunks
    heads = b_q.shape[0] // HEAD_DIM
    whole = lambda: pl.BlockSpec(memory_space=pltpu.VMEM)
    got = pl.pallas_call(
        functools.partial(forward_kernel, heads, chunks),
        out_shape=(jax.ShapeDtypeStruct((heads * HEAD_DIM, rows), bf16),) * far
        + (
            jax.ShapeDtypeStruct((heads, length // PAIR // 2, PAIR), f32),
            jax.ShapeDtypeStruct((heads, PAIR), f32),
            jax.ShapeDtypeStruct((heads, HEAD_DIM, PAIR), f32),
            jax.ShapeDtypeStruct((length + BLOCK, heads * PAIR), bf16),
            jax.ShapeDtypeStruct((length + BLOCK, heads * PAIR), bf16),
            jax.ShapeDtypeStruct((heads * HEAD_DIM, length), bf16),
            jax.ShapeDtypeStruct((BLOCK, length), bf16),
        ),
        in_specs=[pl.BlockSpec(memory_space=pltpu.SMEM)] * 3 + [whole() for _ in range(chunks + 4)],
        out_specs=tuple(whole() for _ in range(far + 7)),
        scratch_shapes=[
            pltpu.VMEM((heads, length, PAIR), f32),
            pltpu.VMEM((far, heads * HEAD_DIM, rows), bf16),
            pltpu.VMEM((chunks, rows), jnp.int32),
        ],
        compiler_params=pltpu.CompilerParams(vmem_limit_bytes=VMEM_BYTES),
        cost_estimate=pl.CostEstimate(flops=10_000_000_000, bytes_accessed=16_000_000, transcendentals=6_000_000),
        name="attention_forward",
    )(me, rand, glob, *x, seg, w, b_kv, b_q)
    return got[:far], got[far:]


def near_kernel(heads, chunks, me_ref, rand_ref, glob_ref, k_ref, kv_ref, q_ref, mask_ref, glob_ctx_ref, *refs):
    half = chunks // 2
    out_refs = refs[:half]
    lse_ref, out_ref = refs[half:]
    length = q_ref.shape[1]
    per_chunk = length // PAIR // chunks
    flip, gl = placed(me_ref, glob_ref, length // BLOCK, chunks)
    sparse_forward(heads, 0, half, per_chunk, rand_ref, glob_ref, flip, k_ref, kv_ref, q_ref, mask_ref, out_ref, lse_ref)
    for h in range(heads):
        put_global_columns(out_ref, slice(h * BLOCK, (h + 1) * BLOCK), gl, glob_ctx_ref[h], per_chunk, 0, half)
    for c in range(half):
        out_refs[c][...] = out_ref[c]


def attention_near(me, rand, glob, k, kv, q, mask, glob_ctx, chunks):
    heads = glob_ctx.shape[0]
    half = chunks // 2
    length = q.shape[1]
    rows = length // chunks
    whole = lambda: pl.BlockSpec(memory_space=pltpu.VMEM)
    got = pl.pallas_call(
        functools.partial(near_kernel, heads, chunks),
        out_shape=(jax.ShapeDtypeStruct((heads * HEAD_DIM, rows), bf16),) * half
        + (jax.ShapeDtypeStruct((heads, length // PAIR // 2, PAIR), f32),),
        in_specs=[pl.BlockSpec(memory_space=pltpu.SMEM)] * 3 + [whole() for _ in range(5)],
        out_specs=tuple(whole() for _ in range(half + 1)),
        scratch_shapes=[pltpu.VMEM((half, heads * HEAD_DIM, rows), bf16)],
        compiler_params=pltpu.CompilerParams(vmem_limit_bytes=VMEM_BYTES),
        cost_estimate=pl.CostEstimate(flops=6_000_000_000, bytes_accessed=9_000_000, transcendentals=3_000_000),
        name="attention_near",
    )(me, rand, glob, k, kv, q, mask, glob_ctx)
    return got[:half], got[half]


def backward_kernel(heads, chunks, me_ref, rand_ref, glob_ref, *refs):
    do_refs = refs[:chunks]
    (k_ref, kv_ref, q_ref, mask_ref, seg_ref, lse_near_ref, lse_far_ref, lseg_ref, w_ref, resid_ref, dq_ref, dkv_ref,
     first_ref) = refs[chunks : chunks + 13]
    part_refs = refs[chunks + 13 : 2 * chunks + 12]
    do_sc, acc, p_sc, d_sc, seg_sc, line_sc, lse_ref, row_sc = refs[2 * chunks + 12 :]
    rows = do_refs[0].shape[1]
    length = rows * chunks
    npairs = length // PAIR
    per_chunk = npairs // chunks
    scale = HEAD_DIM ** -0.5
    flip, gl = placed(me_ref, glob_ref, length // BLOCK, chunks)
    lse_ref[:, 0 : npairs // 2, :] = lse_near_ref[...]
    lse_ref[:, npairs // 2 :, :] = lse_far_ref[...]
    for c in range(chunks):
        do_sc[:, c * rows : (c + 1) * rows] = do_refs[c][...]
        row_sc[c : c + 1, :] = seg_ref[pl.ds(me_ref[0] ^ c, 1), :].astype(f32)

        @pl.loop(0, per_chunk // 4)
        def _(some):
            for i in range(4):
                t = 4 * some + i
                line = row_sc[c : c + 1, pl.ds(pl.multiple_of(t * PAIR, PAIR), PAIR)]
                line_sc[c * per_chunk + t] = line
                to = pl.multiple_of(c * rows + t * PAIR, PAIR)
                seg_sc[pl.ds(to, PAIR), :] = jnp.transpose(jnp.broadcast_to(line, (PAIR, PAIR)), (1, 0))

    seg_sc[length : length + BLOCK, :] = jnp.full((BLOCK, PAIR), -1.0, f32)
    first2, second2 = lane_halves(2 * PAIR, bf16)
    ffirst, fsecond = lane_halves(PAIR, f32)
    lane = lax.broadcasted_iota(jnp.int32, (1, PAIR), 1)
    line_row = lax.broadcasted_iota(jnp.int32, (PAIR, 1), 0)
    zeros = jnp.zeros((BLOCK, PAIR), bf16)
    blank = jnp.zeros((PAIR, PAIR), bf16)

    def head_rows(h):
        return slice(h * BLOCK, (h + 1) * BLOCK)

    def joint(q, mask, do):
        left = jnp.concatenate([q, mask, blank], axis=0)
        right = jnp.concatenate([blank, zeros, do], axis=0)
        return jnp.concatenate([left, right], axis=1)

    def sources(q, do):
        top = jnp.concatenate([q, zeros], axis=1)
        return jnp.concatenate([top, jnp.concatenate([zeros, do], axis=1)], axis=0)

    step = 512
    mask_glob = global_columns(mask_ref, slice(0, BLOCK), gl).astype(bf16)
    q_glob = [global_columns(q_ref, head_rows(h), gl).astype(bf16) for h in range(heads)]
    do_glob = [global_columns(do_sc, head_rows(h), gl).astype(bf16) for h in range(heads)]

    def weigh(c, deltas):
        at = pl.multiple_of(c * step, step)
        new = []
        for h in range(heads):
            left = jnp.concatenate([k_ref[pl.ds(at, step), head_lanes(h)], kv_ref[pl.ds(at, step), head_lanes(h)]], axis=1)
            both = dot_nn(left, joint(q_glob[h], mask_glob, do_glob[h]))
            p = jnp.exp(both[:, 0:PAIR] - lseg_ref[h : h + 1, :])
            dp = both[:, PAIR:]
            p_sc[h, pl.ds(at, step), :] = p
            d_sc[h, pl.ds(at, step), :] = dp
            new.append(deltas[h] + jnp.sum(p * dp, axis=0, keepdims=True))
        return tuple(new)

    deltas = lax.fori_loop(0, length // step, weigh, (jnp.zeros((1, PAIR), f32),) * heads)

    def spread(c, dqs):
        at = pl.multiple_of(c * step, step)
        new = []
        for h in range(heads):
            p = p_sc[h, pl.ds(at, step), :]
            ds = (p * (d_sc[h, pl.ds(at, step), :] - deltas[h])).astype(bf16)
            both = jnp.concatenate([ds, p.astype(bf16)], axis=1)
            acc[h, pl.ds(at, step), :] = dot_nt(both, sources(q_glob[h], do_glob[h]))
            new.append(dqs[h] + dot_tn(k_ref[pl.ds(at, step), head_lanes(h)], ds))
        return tuple(new)

    dqs = lax.fori_loop(0, length // step, spread, (jnp.zeros((PAIR, PAIR), f32),) * heads)
    for h in range(heads):
        acc[h, pl.ds(length, BLOCK), :] = jnp.zeros((BLOCK, PAIR), f32)

    def one_pair(pair):
        chunk = pair // per_chunk
        local = pl.multiple_of((pair % per_chunk) * PAIR, PAIR)
        at = pl.multiple_of(pair * PAIR, PAIR)
        hit_first = (gl[0] == 2 * pair) | (gl[1] == 2 * pair)
        hit_second = (gl[0] == 2 * pair + 1) | (gl[1] == 2 * pair + 1)
        shut = ffirst * jnp.where(hit_first, -MASKED, 0.0) + fsecond * jnp.where(hit_second, -MASKED, 0.0)
        every = slice(0, PAIR)
        for h in range(heads):
            kl = head_lanes(h)
            shared, mine, other = slots(rand_ref, glob_ref, flip, h, pair, length // BLOCK)
            q = q_ref[head_rows(h), pl.ds(at, PAIR)]
            do = do_sc[head_rows(h), pl.ds(at, PAIR)]
            lse = lse_ref[h, pl.ds(pair, 1), :] + shut
            src = sources(q, do)
            src2 = jnp.concatenate([src * first2, src * second2], axis=0)
            k_sh = stack_rows(k_ref, shared, kl)
            two_sh = dot_nn(
                jnp.concatenate([k_sh, stack_rows(kv_ref, shared, kl)], axis=1),
                joint(q, mask_ref[:, pl.ds(at, PAIR)], do),
            )
            kv_pr = jnp.concatenate([stack_rows(kv_ref, mine, kl), stack_rows(kv_ref, other, kl)], axis=1)
            two_pr = dot_nn(kv_pr, src2)
            seg_pr = jnp.where(lane < BLOCK, stack_rows(seg_sc, mine, every), stack_rows(seg_sc, other, every))
            agree = seg_pr == line_sc[pair]
            p_sh = jnp.exp(two_sh[:, 0:PAIR] - lse)
            p_pr = jnp.where(agree, jnp.exp(two_pr[:, 0:PAIR] - lse), 0.0)
            d_sh, d_pr = two_sh[:, PAIR:], two_pr[:, PAIR:]
            delta = jnp.sum(p_sh * d_sh, axis=0, keepdims=True) + jnp.sum(p_pr * d_pr, axis=0, keepdims=True)
            ds_sh = (p_sh * (d_sh - delta)).astype(bf16)
            ds_pr = (p_pr * (d_pr - delta)).astype(bf16)
            g_sh = dot_nt(jnp.concatenate([ds_sh, p_sh.astype(bf16)], axis=1), src)
            g_pr = dot_nt(jnp.concatenate([ds_pr, p_pr.astype(bf16)], axis=1), src2)
            for j, o in enumerate(shared):
                acc[h, pl.ds(o, BLOCK), :] += g_sh[j * BLOCK : (j + 1) * BLOCK]
            for j, o in enumerate(mine):
                acc[h, pl.ds(o, BLOCK), :] += g_pr[j * BLOCK : (j + 1) * BLOCK, 0:PAIR]
            for j, o in enumerate(other):
                acc[h, pl.ds(o, BLOCK), :] += g_pr[j * BLOCK : (j + 1) * BLOCK, PAIR:]
            t_pr = dot_tn(ds_pr, kv_pr)
            dq = dot_tn(ds_sh, k_sh) + jnp.where(line_row < BLOCK, t_pr[:, 0:PAIR], t_pr[:, PAIR:])
            dq = jnp.transpose(dq, (1, 0))[0:BLOCK]
            dq_ref[chunk, head_rows(h), pl.ds(local, PAIR)] = (dq * scale).astype(bf16)

    @pl.loop(0, npairs // BACK_UNROLL)
    def _(some):
        for i in range(BACK_UNROLL):
            one_pair(BACK_UNROLL * some + i)

    for h in range(heads):
        put_global_columns(dq_ref, head_rows(h), gl, dqs[h][0:BLOCK] * scale, per_chunk, 0, chunks)
        for c in range(chunks):
            dkv_ref[c, :, head_lanes(h)] = acc[h, pl.ds(c * rows, rows), :].astype(bf16)
    tile = 256
    wq = query_weights(w_ref, heads)
    for c in range(chunks):

        @pl.loop(0, rows // tile)
        def _(t):
            at = pl.multiple_of(t * tile, tile)
            got = dot_tn(dq_ref[c, :, pl.ds(at, tile)], wq)
            got = got + dot_nt(dkv_ref[c, pl.ds(at, tile), :], w_ref[:, 0 : heads * PAIR])
            if c == 0:
                first_ref[pl.ds(at, tile), :] = resid_ref[pl.ds(at, tile), :] + got
            else:
                part_refs[c - 1][pl.ds(at, tile), :] = got.astype(bf16)


def attention_backward(me, rand, glob, do, k, kv, q, mask, seg, lse_near, lse_far, lseg, w, resid):
    chunks = len(do)
    group, rows = do[0].shape
    heads = group // HEAD_DIM
    width = w.shape[0]
    length = rows * chunks
    whole = lambda: pl.BlockSpec(memory_space=pltpu.VMEM)
    return pl.pallas_call(
        functools.partial(backward_kernel, heads, chunks),
        out_shape=(
            jax.ShapeDtypeStruct((chunks, group, rows), bf16),
            jax.ShapeDtypeStruct((chunks, rows, heads * PAIR), bf16),
            jax.ShapeDtypeStruct((rows, width), f32),
        )
        + (jax.ShapeDtypeStruct((rows, width), bf16),) * (chunks - 1),
        in_specs=[pl.BlockSpec(memory_space=pltpu.SMEM)] * 3 + [whole() for _ in range(chunks + 10)],
        out_specs=tuple(whole() for _ in range(chunks + 2)),
        scratch_shapes=[
            pltpu.VMEM((group, length), bf16),
            pltpu.VMEM((heads, length + BLOCK, PAIR), f32),
            pltpu.VMEM((heads, length, PAIR), f32),
            pltpu.VMEM((heads, length, PAIR), f32),
            pltpu.VMEM((length + BLOCK, PAIR), f32),
            pltpu.VMEM((length // PAIR, 1, PAIR), f32),
            pltpu.VMEM((heads, length // PAIR, PAIR), f32),
            pltpu.VMEM((chunks, rows), f32),
        ],
        compiler_params=pltpu.CompilerParams(vmem_limit_bytes=VMEM_BYTES),
        cost_estimate=pl.CostEstimate(flops=30_000_000_000, bytes_accessed=24_000_000, transcendentals=8_000_000),
        name="attention_backward",
    )(me, rand, glob, *do, k, kv, q, mask, seg, lse_near, lse_far, lseg, w, resid)


def round_up(value, to):
    return -(-value // to) * to


def half_columns(ref, index, place):
    at = index // 2 * PAIR
    both = ref[:, at : at + PAIR].astype(f32)
    return both if index % 2 == place else pltpu.roll(both, BLOCK, 1)


def two_halves(first, second):
    lane = lax.broadcasted_iota(jnp.int32, (1, PAIR), 1)
    return jnp.where(lane < BLOCK, first, second)


def pack_kernel(seq_n, wq_ref, wk_ref, wv_ref, wo_ref, up_ref, down_ref, bup_ref, vec_ref, pack_ref, rest_ref):
    own, width = wq_ref.shape
    heads = width // HEAD_DIM // seq_n
    blocks, inner = pack_ref.shape[0], pack_ref.shape[2]
    for s in range(seq_n):
        pieces = [
            two_halves(half_columns(wk_ref, s * heads + h, 0), half_columns(wv_ref, s * heads + h, 1))
            for h in range(heads)
        ]
        for h in range(0, heads, 2):
            second = half_columns(wq_ref, s * heads + h + 1, 1) if h + 1 < heads else jnp.zeros((own, PAIR), f32)
            pieces.append(two_halves(half_columns(wq_ref, s * heads + h, 0), second))
        piece = jnp.concatenate(pieces, axis=1).astype(bf16)
        notes = jnp.concatenate([vec_ref[...], jnp.zeros((8, piece.shape[1] - width), bf16)], axis=1) if (
            piece.shape[1] > width
        ) else vec_ref[:, 0 : piece.shape[1]]
        for b in range(blocks):
            for i in range(inner):
                pack_ref[b, s, i, 0:own, :] = piece
                pack_ref[b, s, i, own : own + 8, :] = notes
    u = up_ref.shape[0]
    rest_ref[0:u, :] = up_ref[...]
    rest_ref[u : 2 * u, :] = down_ref[...]
    rest_ref[2 * u : 2 * u + own, :] = wo_ref[...]
    row = lax.broadcasted_iota(jnp.int32, (8, 1), 0)
    block = jnp.where(row == 7, bup_ref[...].astype(f32), vec_ref[...].astype(f32))
    rest_ref[2 * u + own : 2 * u + own + 8, :] = block.astype(bf16)


def packed_weights(w_q, w_k, w_v, w_o, w_up, w_down, b_up, vec, dp_n, seq_n, ffn_n):
    own, width = w_q.shape
    heads = width // HEAD_DIM // seq_n
    lanes = heads * PAIR + round_up(heads * HEAD_DIM, PAIR)
    u = w_up.shape[0]
    if own % 8 or u % 16:
        group = heads * HEAD_DIM
        cols = lambda w: w.reshape(own, seq_n, heads, HEAD_DIM).transpose(1, 0, 2, 3)
        kv = jnp.stack([cols(w_k), cols(w_v)], axis=3).reshape(seq_n, own, 2 * group)
        piece = jnp.concatenate([kv, cols(w_q).reshape(seq_n, own, group)], axis=2)
        piece = jnp.pad(piece, ((0, 0), (0, round_up(own, 8) - own), (0, lanes - 3 * group)))
        notes = jnp.broadcast_to(vec[None, :, :lanes], (seq_n, 8, lanes))
        piece = jnp.concatenate([piece, notes], axis=1)
        pack = jnp.broadcast_to(piece[None, :, None], (dp_n, seq_n, ffn_n) + piece.shape[1:])
        w_o = jnp.pad(w_o, ((0, round_up(own, 8) - own), (0, 0)))
        return pack, jnp.concatenate([w_up, w_down, w_o, vec[:7], b_up], axis=0)
    whole = lambda: pl.BlockSpec(memory_space=pltpu.VMEM)
    return pl.pallas_call(
        functools.partial(pack_kernel, seq_n),
        out_shape=(
            jax.ShapeDtypeStruct((dp_n, seq_n, ffn_n, own + 8, lanes), bf16),
            jax.ShapeDtypeStruct((2 * u + own + 8, width), bf16),
        ),
        in_specs=[whole() for _ in range(8)],
        out_specs=(whole(), whole()),
        name="packed_weights",
    )(w_q, w_k, w_v, w_o, w_up, w_down, b_up, vec)


def weights_kernel(chunks, direct, *refs):
    x_refs = refs[:chunks]
    dq_ref, dkv_ref, out_ref, sums_ref, acc, sum_sc = refs[chunks:]
    group = dq_ref.shape[1]
    lanes = dkv_ref.shape[2]
    full = acc.shape[0]
    x = jnp.concatenate([r[...] for r in x_refs], axis=0)
    dkv = jnp.concatenate([dkv_ref[c] for c in range(chunks)], axis=0)
    dq = jnp.concatenate([dq_ref[c] for c in range(chunks)], axis=1)
    ones = jnp.ones((8, x.shape[0]), bf16)

    @pl.when(pl.program_id(0) == 0)
    def _():
        acc[...] = jnp.zeros_like(acc)
        sum_sc[...] = jnp.zeros_like(sum_sc)

    acc[0:lanes, :] += dot_tn(dkv, x)
    acc[lanes : lanes + group, :] += dot_nn(dq, x)
    sum_sc[:, 0:lanes] += dot_nn(ones, dkv)
    sum_sc[:, lanes : lanes + group] += dot_nt(ones, dq)

    @pl.when(pl.program_id(0) == pl.num_programs(0) - 1)
    def _():
        grad = jnp.transpose(acc[...], (1, 0))
        sums_ref[...] = sum_sc[...]
        if direct:
            blocks, per, _ = out_ref.shape
            own = per - 8
            grad = grad.reshape(blocks, own, full)
            for b in range(blocks):
                out_ref[b, 0:own, :] = grad[b].astype(bf16)
                out_ref[b, own:, :] = sum_sc[...].astype(bf16)
        else:
            out_ref[...] = grad.astype(bf16)


def projection_gradients(x, dq, dkv, own, devices):
    chunks, group, rows = dq.shape
    width = x[0].shape[1]
    lanes = dkv.shape[2]
    full = lanes + round_up(group, PAIR)
    direct = own % 8 == 0
    tile = 256
    shape = (devices, own + 8, full) if direct else (width, full)
    out, sums = pl.pallas_call(
        functools.partial(weights_kernel, chunks, direct),
        grid=(rows // tile,),
        out_shape=(jax.ShapeDtypeStruct(shape, bf16), jax.ShapeDtypeStruct((8, full), f32)),
        in_specs=[pl.BlockSpec((tile, width), lambda i: (i, 0)) for _ in range(chunks)]
        + [
            pl.BlockSpec((chunks, group, tile), lambda i: (0, 0, i)),
            pl.BlockSpec((chunks, tile, lanes), lambda i: (0, i, 0)),
        ],
        out_specs=(
            pl.BlockSpec(shape, lambda i: (0,) * len(shape), pipeline_mode=pl.Buffered(1)),
            pl.BlockSpec((8, full), lambda i: (0, 0)),
        ),
        scratch_shapes=[pltpu.VMEM((full, width), f32), pltpu.VMEM((8, full), f32)],
        compiler_params=pltpu.CompilerParams(vmem_limit_bytes=VMEM_BYTES),
        cost_estimate=pl.CostEstimate(flops=4_000_000_000, bytes_accessed=12_000_000, transcendentals=0),
        name="projection_gradients",
    )(*x, dq, dkv)
    if not direct:
        out = jnp.pad(out.reshape(devices, own, full), ((0, 0), (0, round_up(own, 8) - own), (0, 0)))
        out = jnp.concatenate([out, jnp.broadcast_to(sums[None].astype(bf16), (devices, 8, full))], axis=1)
    return out


def unpack_kernel(own, got_ref, q_ref, k_ref, v_ref, sums_ref, tot):
    dp_n, seq_n, ffn_n, per, full = got_ref.shape
    width = q_ref.shape[1]
    heads = width // HEAD_DIM // seq_n
    for s in range(seq_n):
        total = jnp.zeros((per, full), f32)
        for d in range(dp_n):
            for f in range(ffn_n):
                total = total + got_ref[d, s, f].astype(f32)
        tot[s] = total
        sums_ref[s : s + 1, :] = total[per - 8 : per - 7, :]
    for w in range(width // PAIR):
        spots = [((2 * w + i) // heads, (2 * w + i) % heads) for i in range(2)]
        cols = slice(w * PAIR, (w + 1) * PAIR)
        for ref, where in (
            (k_ref, lambda h: 2 * h),
            (v_ref, lambda h: 2 * h + 1),
            (q_ref, lambda h: 2 * heads + h),
        ):
            both = [half_columns(tot.at[g], where(h), i) for i, (g, h) in enumerate(spots)]
            ref[:, cols] = two_halves(*both)[0:own]


def unpacked_gradients(got, own, width):
    dp_n, seq_n, ffn_n, per, full = got.shape
    whole = lambda: pl.BlockSpec(memory_space=pltpu.VMEM)
    return pl.pallas_call(
        functools.partial(unpack_kernel, own),
        out_shape=(jax.ShapeDtypeStruct((own, width), f32),) * 3 + (jax.ShapeDtypeStruct((seq_n, full), f32),),
        in_specs=[whole()],
        out_specs=tuple(whole() for _ in range(4)),
        scratch_shapes=[pltpu.VMEM((seq_n, per, full), f32)],
        compiler_params=pltpu.CompilerParams(vmem_limit_bytes=VMEM_BYTES),
        name="unpacked_gradients",
    )(got)


NORM_EPS = 1e-12


def transposed(value):
    return jnp.transpose(value.astype(f32), (1, 0)).astype(bf16)


def unit_rows(value):
    center = value - jnp.mean(value, axis=-1, keepdims=True)
    scale = lax.rsqrt(jnp.mean(center * center, axis=-1, keepdims=True) + NORM_EPS)
    return center * scale, scale


def unit_rows_back(grad, unit, scale):
    return scale * (
        grad - jnp.mean(grad, axis=-1, keepdims=True) - unit * jnp.mean(grad * unit, axis=-1, keepdims=True)
    )


def rows_kernel(parts, blocks, up_rows, own, me_ref, *refs):
    ctx_refs = refs[:parts]
    (x_ref, cot_ref, rest_ref, wo_ref, vec_ref, bup_ref, out_ref, resid_ref, hid_ref, pre_ref, nlt_ref, gft_ref,
     gb_ref) = refs[parts : parts + 13]
    do_refs = refs[parts + 13 : 2 * parts + 13]
    sums_ref, gbup_ref, slope_sc, wo_sc, wide_sc = refs[2 * parts + 13 :]
    group = ctx_refs[0].shape[0]
    width = x_ref.shape[1]

    def up(f):
        return rest_ref[:, f, 0:up_rows, :].reshape(width, rest_ref.shape[3])

    def down(f):
        return rest_ref[:, f, up_rows : 2 * up_rows, :].reshape(width, rest_ref.shape[3])

    def own_rows(k):
        return pl.ds(pl.multiple_of((me_ref[0] ^ k) * group, group), group)

    @pl.when(pl.program_id(0) == 0)
    def _():
        sums_ref[...] = jnp.zeros_like(sums_ref)
        gbup_ref[...] = jnp.zeros_like(gbup_ref)
        if own:
            for o in range(rest_ref.shape[0]):
                for f in range(blocks):
                    to = (o * blocks + f) * own
                    wide_sc[to : to + own, :] = rest_ref[o, f, 2 * up_rows : 2 * up_rows + own, :].astype(f32)
            wo_sc[...] = wide_sc[...].astype(bf16)
        else:
            wo_sc[...] = wo_ref[...]

    def bias_up(f):
        if own:
            row = rest_ref[0, f, 2 * up_rows + own : 2 * up_rows + own + 8, :].astype(f32)
            return row[7:8, :]
        return bup_ref[f : f + 1, :]

    ctx = jnp.concatenate([r[...] for r in ctx_refs], axis=0)
    w_o = jnp.concatenate([wo_sc[own_rows(k), :] for k in range(parts)], axis=0)
    resid_one = x_ref[...].astype(f32) + (dot_tn(ctx, w_o) + vec_ref[0:1, :])
    unit_one, scale_one = unit_rows(resid_one)
    normed_one = unit_one * vec_ref[2:3, :] + vec_ref[3:4, :]
    low = normed_one.astype(bf16)
    nlt_ref[...] = transposed(normed_one)
    total = normed_one + vec_ref[1:2, :]
    pre = dot_nn(low, up(0)) + bias_up(0)
    for f in range(blocks):
        later = dot_nn(low, up(f + 1)) + bias_up(f + 1) if f + 1 < blocks else None
        phi = 0.5 + 0.5 * lax.erf(pre * (0.5 ** 0.5))
        slope_sc[f] = phi + pre * (jnp.exp(-0.5 * pre * pre) * 0.3989422804014327)
        hid = (pre * phi).astype(bf16)
        hid_ref[f] = hid
        total = total + dot_nt(hid, down(f))
        pre = later
    unit_two, scale_two = unit_rows(total)
    out_ref[...] = (unit_two * vec_ref[4:5, :] + vec_ref[5:6, :]).astype(bf16)
    cot = cot_ref[...].astype(f32)
    grad_two = unit_rows_back(cot * vec_ref[4:5, :], unit_two, scale_two)
    grad_ffn = grad_two.astype(bf16)
    gft_ref[...] = transposed(grad_two)
    grad_normed = grad_two
    back = dot_nn(grad_ffn, down(0))
    for f in range(blocks):
        later = dot_nn(grad_ffn, down(f + 1)) if f + 1 < blocks else None
        grad_pre = (back * slope_sc[f]).astype(bf16)
        pre_ref[f] = grad_pre
        gbup_ref[f : f + 1, :] += jnp.sum(grad_pre.astype(f32), axis=0, keepdims=True)
        grad_normed = grad_normed + dot_nt(grad_pre, up(f))
        back = later
    resid = unit_rows_back(grad_normed * vec_ref[2:3, :], unit_one, scale_one)
    resid_ref[...] = resid
    branch = resid.astype(bf16)
    gb_ref[...] = branch
    do = dot_nt(w_o, branch).astype(bf16)
    for k in range(parts):
        do_refs[k][...] = do[k * group : (k + 1) * group]
    for row, value in enumerate(
        (branch.astype(f32), grad_ffn.astype(f32), grad_normed * unit_one, grad_normed, cot * unit_two, cot)
    ):
        sums_ref[row : row + 1, :] += jnp.sum(value, axis=0, keepdims=True)


def rows_chain(me, ctx_parts, x, cot, rest, up_rows, own, w_o, vecs, bias_up):
    parts = len(ctx_parts)
    group, rows = ctx_parts[0].shape
    width = x.shape[1]
    outer, blocks, per, hidden = rest.shape
    tile = 256
    once = lambda shape: pl.BlockSpec(shape, lambda i: (0,) * len(shape), pipeline_mode=pl.Buffered(1))
    tall = pl.BlockSpec((tile, width), lambda i: (i, 0))
    wide = pl.BlockSpec((width, tile), lambda i: (0, i))
    cube = pl.BlockSpec((blocks, tile, hidden), lambda i: (0, i, 0))
    return pl.pallas_call(
        functools.partial(rows_kernel, parts, blocks, up_rows, own),
        grid=(rows // tile,),
        out_shape=(
            jax.ShapeDtypeStruct((rows, width), bf16),
            jax.ShapeDtypeStruct((rows, width), f32),
            jax.ShapeDtypeStruct((blocks, rows, hidden), bf16),
            jax.ShapeDtypeStruct((blocks, rows, hidden), bf16),
            jax.ShapeDtypeStruct((width, rows), bf16),
            jax.ShapeDtypeStruct((width, rows), bf16),
            jax.ShapeDtypeStruct((rows, width), bf16),
        )
        + (jax.ShapeDtypeStruct((group, rows), bf16),) * parts
        + (jax.ShapeDtypeStruct((8, width), f32), jax.ShapeDtypeStruct((8, hidden), f32)),
        in_specs=[pl.BlockSpec(memory_space=pltpu.SMEM)]
        + [pl.BlockSpec((group, tile), lambda i: (0, i))] * parts
        + [tall, tall, once(rest.shape), once(w_o.shape), once(vecs.shape), once(bias_up.shape)],
        out_specs=(
            tall, tall, cube, cube, wide, wide, tall,
        )
        + (pl.BlockSpec((group, tile), lambda i: (0, i)),) * parts
        + (pl.BlockSpec((8, width), lambda i: (0, 0)), pl.BlockSpec((8, hidden), lambda i: (0, 0))),
        scratch_shapes=[
            pltpu.VMEM((blocks, tile, hidden), f32),
            pltpu.VMEM((width, width), bf16),
            pltpu.VMEM((width, width), f32),
        ],
        compiler_params=pltpu.CompilerParams(vmem_limit_bytes=VMEM_BYTES),
        cost_estimate=pl.CostEstimate(flops=22_000_000_000, bytes_accessed=40_000_000, transcendentals=6_000_000),
        name="rows_chain",
    )(me, *ctx_parts, x, cot, rest, w_o, vecs, bias_up)


def outer_kernel(parts, up_rows, own, apart, me_ref, *refs):
    ctx_refs = refs[:parts]
    nlt_ref, gft_ref, gb_ref, pre_ref, hid_ref, sums_ref, gbup_ref, out_ref = refs[parts : parts + 8]
    wo_sc = refs[-1]
    slabs, hidden = out_ref.shape[0], out_ref.shape[3]
    group = ctx_refs[0].shape[0]
    f = pl.program_id(0)
    up = dot_nn(nlt_ref[...], pre_ref[0]).astype(bf16).reshape(slabs, up_rows, hidden)
    if apart:
        refs[parts + 8][:, 0, :, :] = up[:, 0:apart]
    out_ref[:, 0, 0 : up_rows - apart, :] = up[:, apart:]
    at = up_rows - apart
    down = dot_nn(gft_ref[...], hid_ref[0]).astype(bf16)
    out_ref[:, 0, at : at + up_rows, :] = down.reshape(slabs, up_rows, hidden)
    at += up_rows
    if not own:
        return

    @pl.when(f == 0)
    def _():
        for k in range(parts):
            wo_sc[k] = dot_nn(ctx_refs[k][...], gb_ref[...])

    share = slabs // parts
    stride = group // share
    for k in range(parts):
        for j in range(share):
            rows = pl.ds(pl.multiple_of(j * stride + f * own, 8), own)
            out_ref[(me_ref[0] ^ k) * share + j, 0, at : at + own, :] = wo_sc[k, rows, :].astype(bf16)
    small = jnp.concatenate([gbup_ref[pl.ds(f, 1), :], sums_ref[0:7, :]], axis=0).astype(bf16)
    for o in range(slabs):
        out_ref[o, 0, at + own :, :] = small


def outer_products(me, ctx_parts, nlt, gft, gb, pre, hid, sums, gbup, slabs, up_rows, own, apart):
    blocks, rows, hidden = pre.shape
    parts = len(ctx_parts)
    group = ctx_parts[0].shape[0]
    per = 2 * up_rows - apart + (own + 8 if own else 0)
    sizes = (per, apart) if apart else (per,)
    once = lambda shape: pl.BlockSpec(shape, lambda i: (0,) * len(shape), pipeline_mode=pl.Buffered(1))
    return pl.pallas_call(
        functools.partial(outer_kernel, parts, up_rows, own, apart),
        grid=(blocks,),
        out_shape=tuple(jax.ShapeDtypeStruct((slabs, blocks, r, hidden), bf16) for r in sizes),
        in_specs=[pl.BlockSpec(memory_space=pltpu.SMEM)]
        + [once(c.shape) for c in ctx_parts]
        + [
            once(nlt.shape),
            once(gft.shape),
            once(gb.shape),
            pl.BlockSpec((1, rows, hidden), lambda i: (i, 0, 0)),
            pl.BlockSpec((1, rows, hidden), lambda i: (i, 0, 0)),
            once(sums.shape),
            once(gbup.shape),
        ],
        out_specs=tuple(pl.BlockSpec((slabs, 1, r, hidden), lambda i: (0, i, 0, 0)) for r in sizes),
        scratch_shapes=[pltpu.VMEM((parts, group, gb.shape[1]), f32)],
        compiler_params=pltpu.CompilerParams(vmem_limit_bytes=VMEM_BYTES),
        cost_estimate=pl.CostEstimate(flops=11_000_000_000, bytes_accessed=28_000_000, transcendentals=0),
        name="outer_products",
    )(me, *ctx_parts, nlt, gft, gb, pre, hid, sums, gbup)


def finish_kernel(up_rows, own, total_ref, up_ref, down_ref, wo_ref, small_ref):
    rest = total_ref[...].astype(f32)
    up_ref[...] = rest[0:up_rows]
    down_ref[...] = rest[up_rows : 2 * up_rows]
    at = 2 * up_rows
    wo_ref[...] = rest[at : at + own]
    small_ref[...] = rest[at + own : at + own + 8]


def finished(total, up_rows, own):
    hidden = total.shape[1]
    whole = lambda: pl.BlockSpec(memory_space=pltpu.VMEM)
    return pl.pallas_call(
        functools.partial(finish_kernel, up_rows, own),
        out_shape=tuple(jax.ShapeDtypeStruct((r, hidden), f32) for r in (up_rows, up_rows, own, 8)),
        in_specs=[whole()],
        out_specs=tuple(whole() for _ in range(4)),
        name="finished",
    )(total)


ALL = ("dp", "seq", "ffn")


def flip_send(array, axis, bits):
    count = lax.axis_size(axis)
    return lax.ppermute(array, axis, [(i, i ^ bits) for i in range(count)])


def shards(
    tokens, w_query, w_key, w_value, w_output, b_query, b_value, b_output, w_up, b_up, w_down, b_down,
    gain_attn, shift_attn, gain_ffn, shift_ffn, segment_ids, random_blocks, global_blocks, cotangent,
):
    seq_n, dp_n, ffn_n = lax.axis_size("seq"), lax.axis_size("dp"), lax.axis_size("ffn")
    outer, devices = dp_n * seq_n, dp_n * seq_n * ffn_n
    me = lax.axis_index("seq")
    here = (lax.axis_index("dp") * seq_n + me) * ffn_n + lax.axis_index("ffn")
    own, width = w_query.shape
    own_pad = round_up(own, 8)
    group = width // seq_n
    heads = group // HEAD_DIM
    features = tokens[0]
    rows = features.shape[0]
    order = jnp.stack([me ^ k for k in range(seq_n)])
    me_ref = me.astype(jnp.int32)[None]

    near = [features] + [None] * (seq_n - 1)
    for k in sorted(range(1, seq_n), key=lambda k: (k & (k - 1), -k)):
        bit = k & -k
        near[k] = flip_send(features if bit == k else near[k ^ bit], "seq", bit)

    vec = jnp.stack([b_output, b_down, gain_attn, shift_attn, gain_ffn, shift_ffn, b_query, b_value])
    vec = jnp.pad(vec, ((0, 0), (0, width - own)))
    seg = segment_ids[0].reshape(seq_n, rows)
    rand = random_blocks.reshape(-1)
    pack, rest = packed_weights(
        w_query, w_key, w_value, w_output, w_up, w_down, b_up[None], vec, dp_n, seq_n, ffn_n
    )
    lanes = pack.shape[4]
    pack, seg, rand = lax.optimization_barrier((pack, seg, rand))
    pack = lax.all_to_all(
        pack.reshape(devices, own_pad + 8, lanes), ALL, split_axis=0, concat_axis=0, tiled=True
    )
    rest = lax.all_gather(rest, ALL, axis=0, tiled=False)
    w_own = pack[:, :own].reshape(width, lanes)
    share = devices // seq_n
    biases = lax.dynamic_slice(pack, (share * me, own_pad + 6, 0), (share, 2, own))
    biases = biases.transpose(1, 0, 2).reshape(2, group).astype(f32)
    by_head = biases[1].reshape(heads, 1, HEAD_DIM)
    b_kv = jnp.concatenate([jnp.zeros_like(by_head), by_head], axis=1).reshape(1, heads * PAIR)

    far = seq_n // 2
    ctx_far, (lse_far, lseg, glob_ctx, k_all, v_all, q_all, mask_all) = attention_forward(
        me_ref, rand, global_blocks, near, seg, w_own, b_kv, biases[0][:, None]
    )
    ctx_parts = [None] * far + [flip_send(ctx_far[k - far], "seq", k) for k in range(far, seq_n)]
    ctx_near, lse_near = attention_near(
        me_ref, rand, global_blocks, k_all, v_all, q_all, mask_all, glob_ctx, seq_n
    )
    ctx_parts[far:], ctx_parts[0] = lax.optimization_barrier((ctx_parts[far:], ctx_near[0]))
    for k in range(1, far):
        ctx_parts[k] = flip_send(ctx_near[k], "seq", k)

    up_rows = w_up.shape[0]
    at = 2 * up_rows
    rest = rest.reshape(outer, ffn_n, rest.shape[1], width)
    w_o = rest[:, :, at : at + own].reshape(width, width)
    bias_up = rest[0, :, at + own_pad + 7].astype(f32)
    vecs = pack[:, own_pad:, :own].transpose(1, 0, 2).reshape(8, width).astype(f32)
    direct = up_rows % 16 == 0 and own % 8 == 0 and outer % seq_n == 0 and (outer // seq_n) * ffn_n * own == group
    if not direct:
        rest = rest[:, :, :at].reshape(outer, ffn_n, 2, up_rows, width).transpose(1, 2, 0, 3, 4)
        rest = rest.reshape(1, ffn_n, 2 * outer * up_rows, width)
    slabs, slab_rows = (outer, up_rows) if direct else (1, outer * up_rows)

    got = rows_chain(
        me_ref, ctx_parts, features, cotangent[0], rest, slab_rows, own if direct else 0,
        jnp.zeros((8, PAIR), bf16) if direct else w_o, vecs, jnp.zeros((8, PAIR), f32) if direct else bias_up,
    )
    out, grad_resid_one, hidden, grad_pre, normed_t, grad_ffn_t, grad_branch = got[:7]
    grad_ctx, (sums, grad_bias_up) = got[7 : 7 + seq_n], got[7 + seq_n :]
    do = [grad_ctx[0]] + [flip_send(grad_ctx[k], "seq", k) for k in range(1, seq_n)]

    payload = outer_products(
        me_ref, ctx_parts, normed_t, grad_ffn_t, grad_branch, grad_pre, hidden, sums, grad_bias_up, slabs, slab_rows,
        own if direct else 0, APART if direct else 0,
    )
    payload, apart = payload if direct and APART else (payload[0], None)
    if not direct:
        grad_out = dot_nn(jnp.concatenate(ctx_parts, axis=0), grad_branch).astype(bf16)
        grad_out = grad_out.reshape(seq_n, group, width)[order].reshape(outer, ffn_n, own, width)
        top = jnp.broadcast_to(grad_bias_up[None, :ffn_n, None], (outer, ffn_n, 1, width))
        small = jnp.concatenate([top, jnp.broadcast_to(sums[None, None, :7], (outer, ffn_n, 7, width))], axis=2)
        small = small.astype(bf16)
        payload = payload.reshape(ffn_n, 2, outer, up_rows, width).transpose(2, 0, 1, 3, 4)
        payload = jnp.concatenate([payload.reshape(outer, ffn_n, at, width), grad_out, small], axis=2)
        payload = jnp.pad(payload, ((0, 0), (0, 0), (0, -payload.shape[2] % 32), (0, 0)))
    payload, apart, do = lax.optimization_barrier((payload, apart, do))
    total = lax.psum_scatter(payload.reshape(-1, width), ("dp", "seq"), scatter_dimension=0, tiled=True)
    if apart is not None:
        apart = lax.all_to_all(
            apart.reshape(devices, APART, width), ALL, split_axis=0, concat_axis=0, tiled=True
        )

    got = attention_backward(
        me_ref, rand, global_blocks, do, k_all, v_all, q_all, mask_all, seg, lse_near, lse_far, lseg, w_own,
        grad_resid_one,
    )
    dq, dkv, grad_features = got[:3]
    part = [None] + list(got[3:])
    bit = 1
    while bit < seq_n:
        for k in range(seq_n):
            if k & -k == bit and k != bit:
                came = flip_send(part[k], "seq", bit).astype(f32)
                part[k ^ bit] = (part[k ^ bit].astype(f32) + came).astype(bf16)
        bit *= 2
    grad_w = projection_gradients(near, dq, dkv, own, devices)
    grad_w, part = lax.optimization_barrier((grad_w, part[1:]))
    grad_w, apart = lax.optimization_barrier((grad_w, apart))
    part = [None] + part
    bit = seq_n // 2
    first = flip_send(part[bit][: rows // 8], "seq", bit)
    first, total = lax.optimization_barrier((first, total))
    total = lax.psum_scatter(total, "ffn", scatter_dimension=0, tiled=True)
    second = flip_send(part[bit][rows // 8 :], "seq", bit)
    grad_features = grad_features + jnp.concatenate([first, second], axis=0).astype(f32)
    bit //= 2
    while bit:
        grad_features = grad_features + flip_send(part[bit], "seq", bit).astype(f32)
        bit //= 2
    grad_w = lax.all_to_all(grad_w, ALL, split_axis=0, concat_axis=0, tiled=True)
    if direct:
        out_up, out_down, out_output, notes = finished(total, up_rows, own)
    else:
        total = total.astype(f32)
        out_up, out_down, out_output = total[:up_rows], total[up_rows:at], total[at : at + own]
        notes = total[at + own : at + own + 8]
    out_bias_up = notes[0]
    out_vecs = lax.dynamic_slice(notes, (1, here * own), (6, own))
    out_query, out_key, out_value, col_sums = unpacked_gradients(
        grad_w.reshape(dp_n, seq_n, ffn_n, own_pad + 8, lanes), own, width
    )
    row = lax.dynamic_index_in_dim(col_sums, here // share, keepdims=False)
    row = jnp.stack([row[heads * PAIR : heads * PAIR + group], row[: heads * PAIR].reshape(heads, 2, HEAD_DIM)[:, 1].reshape(group)])
    out_b = lax.dynamic_slice(row, (0, here % share * own), (2, own))
    return (
        out[None],
        grad_features[None],
        out_query,
        out_key,
        out_value,
        out_output,
        out_b[0],
        out_b[1],
        out_vecs[0],
        out_up,
        out_bias_up,
        out_down,
        out_vecs[1],
        out_vecs[2],
        out_vecs[3],
        out_vecs[4],
        out_vecs[5],
    )


def solution(mesh):
    return jax.shard_map(
        shards,
        mesh=mesh,
        in_specs=(
            P(("dp", "ffn"), "seq", None),
            P(("dp", "seq", "ffn"), None),
            P(("dp", "seq", "ffn"), None),
            P(("dp", "seq", "ffn"), None),
            P(("dp", "seq", "ffn"), None),
            P(("dp", "seq", "ffn")),
            P(("dp", "seq", "ffn")),
            P(("dp", "seq", "ffn")),
            P(("dp", "seq"), "ffn"),
            P("ffn"),
            P(("dp", "seq"), "ffn"),
            P(("dp", "seq", "ffn")),
            P(("dp", "seq", "ffn")),
            P(("dp", "seq", "ffn")),
            P(("dp", "seq", "ffn")),
            P(("dp", "seq", "ffn")),
            P(("dp", "ffn"), None),
            P(("dp", "ffn"), "seq", None, None),
            P(("dp", "ffn"), None),
            P(("dp", "ffn"), "seq", None),
        ),
        out_specs=(
            P(("dp", "ffn"), "seq", None),
            P(("dp", "ffn"), "seq", None),
            P(("dp", "seq", "ffn"), None),
            P(("dp", "seq", "ffn"), None),
            P(("dp", "seq", "ffn"), None),
            P(("dp", "seq", "ffn"), None),
            P(("dp", "seq", "ffn")),
            P(("dp", "seq", "ffn")),
            P(("dp", "seq", "ffn")),
            P(("dp", "seq"), "ffn"),
            P("ffn"),
            P(("dp", "seq"), "ffn"),
            P(("dp", "seq", "ffn")),
            P(("dp", "seq", "ffn")),
            P(("dp", "seq", "ffn")),
            P(("dp", "seq", "ffn")),
            P(("dp", "seq", "ffn")),
        ),
        check_vma=False,
    )
```

```python
import functools
import jax
import jax.numpy as jnp
from jax import lax
from jax.experimental import pallas as pl
from jax.sharding import PartitionSpec as P
from jax.experimental.pallas import tpu as pltpu

HEAD_DIM = 64
BLOCK = 64
PAIR = 2 * BLOCK
MASKED = -1e30
bf16 = jnp.bfloat16
f32 = jnp.float32


def dot_nn(a, b):
    return lax.dot_general(a, b, (((1,), (0,)), ((), ())), preferred_element_type=f32)


def dot_nt(a, b):
    return lax.dot_general(a, b, (((1,), (1,)), ((), ())), preferred_element_type=f32)


def dot_tn(a, b):
    return lax.dot_general(a, b, (((0,), (0,)), ((), ())), preferred_element_type=f32)


def slots(rand_ref, glob_ref, flip, head, pair, nblocks):
    first = (2 * pair) ^ flip

    def row(block):
        return pl.multiple_of(block * BLOCK, BLOCK)

    def near(block):
        bad = (block < 0) | (block >= nblocks) | (block == glob_ref[0, 0]) | (block == glob_ref[0, 1])
        return row(jnp.where(bad, nblocks, block ^ flip))

    def drawn(block):
        at = (head * nblocks + block) * 3
        return [row(rand_ref[at + j] ^ flip) for j in range(3)]

    shared = [near(first), near(first + 1)] + [row(glob_ref[0, j] ^ flip) for j in range(2)]
    return shared, [near(first - 1)] + drawn(first), [near(first + 2)] + drawn(first + 1)


def stack_rows(ref, offsets, lanes):
    return jnp.concatenate([ref[pl.ds(o, BLOCK), lanes] for o in offsets], axis=0)


def lane_halves(width, dtype):
    lane = lax.broadcasted_iota(jnp.int32, (1, width), 1) % PAIR
    first = (lane < BLOCK).astype(dtype)
    second = (lane >= BLOCK).astype(dtype)
    return first, second


UNROLL = 4
BACK_UNROLL = 4
APART = 0
VMEM_BYTES = 62 << 20


def head_lanes(h):
    return slice(h * PAIR, (h + 1) * PAIR)


def query_columns(q_ref, mask_ref, h, at):
    return jnp.concatenate([q_ref[h * BLOCK : (h + 1) * BLOCK, pl.ds(at, PAIR)], mask_ref[:, pl.ds(at, PAIR)]], axis=0)


def global_queries(q_ref, mask_ref, h, gl):
    return jnp.concatenate(
        [
            global_columns(q_ref, slice(h * BLOCK, (h + 1) * BLOCK), gl),
            global_columns(mask_ref, slice(0, BLOCK), gl),
        ],
        axis=0,
    ).astype(bf16)


def placed(me_ref, glob_ref, nblocks, chunks):
    flip = me_ref[0] * (nblocks // chunks)
    return flip, [glob_ref[0, j] ^ flip for j in range(2)]


def global_columns(src_ref, rows, gl):
    lane = lax.broadcasted_iota(jnp.int32, (1, PAIR), 1)
    parts = []
    for g in range(2):
        block = gl[g]
        at = pl.multiple_of((block // 2) * PAIR, PAIR)
        both = src_ref[rows, pl.ds(at, PAIR)].astype(f32)
        moved = pltpu.roll(both, BLOCK, 1)
        parts.append(jnp.where(block % 2 == g, both, moved))
    return jnp.where(lane < BLOCK, parts[0], parts[1])


def put_global_columns(dst_ref, rows, gl, value, per_chunk, low, high):
    lane = lax.broadcasted_iota(jnp.int32, (1, PAIR), 1)
    moved = pltpu.roll(value, BLOCK, 1)
    for g in range(2):
        pair = gl[g] // 2
        half = gl[g] % 2
        chunk = pair // per_chunk

        @pl.when((chunk >= low) & (chunk < high))
        def _():
            at = pl.multiple_of((pair % per_chunk) * PAIR, PAIR)
            src = jnp.where(half == g, value, moved)
            old = dst_ref[chunk - low, rows, pl.ds(at, PAIR)].astype(f32)
            new = jnp.where((lane >= BLOCK) == (half == 1), src, old)
            dst_ref[chunk - low, rows, pl.ds(at, PAIR)] = new.astype(dst_ref.dtype)


def project_rows(x, seg, w_ref, wq, bkv_ref, bq_ref, k_ref, v_ref, q_ref, mask_ref, at):
    n = x.shape[0]
    lanes = v_ref.shape[1]
    y = dot_nn(x, w_ref[:, 0:lanes]) + bkv_ref[...]
    spot = lax.broadcasted_iota(jnp.int32, (PAIR, n), 0) - BLOCK
    mark = jnp.transpose((spot == seg).astype(f32), (1, 0))
    lane = lax.broadcasted_iota(jnp.int32, (1, PAIR), 1)
    rows = pl.ds(at, n)
    v_ref[rows, :] = y.astype(bf16)
    for h in range(lanes // PAIR):
        k_ref[rows, head_lanes(h)] = jnp.where(lane < BLOCK, y[:, head_lanes(h)], mark).astype(bf16)
    z = (dot_nt(wq, x) + bq_ref[...]).astype(bf16)
    q_ref[:, rows] = (z.astype(f32) * HEAD_DIM ** -0.5).astype(bf16)
    row = lax.broadcasted_iota(jnp.int32, (BLOCK, n), 0)
    mask_ref[:, rows] = jnp.where((row <= 16) & (row != seg), MASKED, 0.0).astype(bf16)


def query_weights(w_ref, heads):
    at = heads * PAIR
    cols = w_ref[:, at : at + 2 * PAIR].astype(f32)
    return jnp.transpose(cols, (1, 0))[0 : heads * HEAD_DIM].astype(bf16)


def sparse_forward(heads, low, high, per_chunk, rand_ref, glob_ref, flip, k_ref, kv_ref, q_ref, mask_ref, out_ref, lse_ref):
    nblocks = (k_ref.shape[0] - BLOCK) // BLOCK
    first, second = lane_halves(PAIR, bf16)
    lane = lax.broadcasted_iota(jnp.int32, (1, PAIR), 1)

    def one_pair(spot):
        chunk = spot // per_chunk
        local = pl.multiple_of((spot % per_chunk) * PAIR, PAIR)
        pair = low * per_chunk + spot
        at = pl.multiple_of(pair * PAIR, PAIR)
        for h in range(heads):
            shared, mine, other = slots(rand_ref, glob_ref, flip, h, pair, nblocks)
            kl = head_lanes(h)
            q = query_columns(q_ref, mask_ref, h, at)
            s_sh = dot_nn(stack_rows(k_ref, shared, kl), q)
            k_pr = jnp.concatenate([stack_rows(k_ref, mine, kl), stack_rows(k_ref, other, kl)], axis=1)
            s_pr = dot_nn(k_pr, jnp.concatenate([q * first, q * second], axis=0))
            peak = jnp.maximum(jnp.max(s_sh, axis=0, keepdims=True), jnp.max(s_pr, axis=0, keepdims=True))
            e_sh = jnp.exp(s_sh - peak)
            e_pr = jnp.exp(s_pr - peak)
            total = jnp.sum(e_sh, axis=0, keepdims=True) + jnp.sum(e_pr, axis=0, keepdims=True)
            inv = 1.0 / total
            p_sh = (e_sh * inv).astype(bf16)
            p_pr = (e_pr * inv).astype(bf16)
            v_pr = jnp.concatenate([stack_rows(kv_ref, mine, kl), stack_rows(kv_ref, other, kl)], axis=1)
            o_sh = dot_tn(stack_rows(kv_ref, shared, kl), p_sh)
            o_pr = dot_tn(v_pr, p_pr)
            ctx = o_sh[BLOCK:PAIR] + jnp.where(lane < BLOCK, o_pr[BLOCK:PAIR], o_pr[PAIR + BLOCK : 2 * PAIR])
            out_ref[chunk, h * BLOCK : (h + 1) * BLOCK, pl.ds(local, PAIR)] = ctx.astype(bf16)
            lse_ref[h, pl.ds(spot, 1), :] = peak + jnp.log(total)

    @pl.loop(0, (high - low) * per_chunk // UNROLL)
    def _(some):
        for i in range(UNROLL):
            one_pair(UNROLL * some + i)


def forward_kernel(heads, chunks, me_ref, rand_ref, glob_ref, *refs):
    x_refs = refs[0:chunks]
    seg_ref, w_ref, bkv_ref, bq_ref = refs[chunks : chunks + 4]
    far = chunks // 2
    out_refs = refs[chunks + 4 : chunks + 4 + far]
    lse_ref, lseg_ref, glob_ctx_ref, k_sc, v_sc, q_sc, mask_sc, s_sc, out_ref, seg_sc = refs[chunks + 4 + far :]
    rows = x_refs[0].shape[0]
    length = rows * chunks
    per_chunk = length // PAIR // chunks
    flip, gl = placed(me_ref, glob_ref, length // BLOCK, chunks)
    tile = 256
    wq = query_weights(w_ref, heads)
    for c in range(chunks):
        seg_sc[c : c + 1, :] = seg_ref[pl.ds(me_ref[0] ^ c, 1), :]
    for c in range(chunks):

        @pl.loop(0, rows // tile)
        def _(t):
            at = pl.multiple_of(t * tile, tile)
            project_rows(
                x_refs[c][pl.ds(at, tile), :], seg_sc[c : c + 1, pl.ds(at, tile)], w_ref, wq, bkv_ref, bq_ref,
                k_sc, v_sc, q_sc, mask_sc, pl.multiple_of(c * rows + t * tile, tile),
            )

    null_lane = lax.broadcasted_iota(jnp.int32, (BLOCK, heads * PAIR), 1) % PAIR
    k_sc[pl.ds(length, BLOCK), :] = (null_lane == BLOCK + 16).astype(f32).astype(bf16)
    v_sc[pl.ds(length, BLOCK), :] = jnp.zeros((BLOCK, heads * PAIR), bf16)
    sparse_forward(heads, far, chunks, per_chunk, rand_ref, glob_ref, flip, k_sc, v_sc, q_sc, mask_sc, out_ref, lse_ref)

    step = 512
    queries = [global_queries(q_sc, mask_sc, h, gl) for h in range(heads)]

    def score(c, peaks):
        at = pl.multiple_of(c * step, step)
        new = []
        for h in range(heads):
            got = dot_nn(k_sc[pl.ds(at, step), head_lanes(h)], queries[h])
            s_sc[h, pl.ds(at, step), :] = got
            new.append(jnp.maximum(peaks[h], jnp.max(got, axis=0, keepdims=True)))
        return tuple(new)

    peaks = lax.fori_loop(0, length // step, score, (jnp.full((1, PAIR), MASKED, f32),) * heads)

    def gather(c, carry):
        at = pl.multiple_of(c * step, step)
        new = []
        for h in range(heads):
            total, ctx = carry[h]
            e = jnp.exp(s_sc[h, pl.ds(at, step), :] - peaks[h])
            ctx = ctx + dot_tn(v_sc[pl.ds(at, step), head_lanes(h)], e.astype(bf16))
            new.append((total + jnp.sum(e, axis=0, keepdims=True), ctx))
        return tuple(new)

    start = (jnp.zeros((1, PAIR), f32), jnp.zeros((PAIR, PAIR), f32))
    sums = lax.fori_loop(0, length // step, gather, (start,) * heads)
    for h in range(heads):
        total, ctx = sums[h]
        ctx = ctx[BLOCK:PAIR] * (1.0 / total)
        glob_ctx_ref[h] = ctx
        put_global_columns(out_ref, slice(h * BLOCK, (h + 1) * BLOCK), gl, ctx, per_chunk, far, chunks)
        lseg_ref[h : h + 1, :] = peaks[h] + jnp.log(total)
    for c in range(far):
        out_refs[c][...] = out_ref[c]


def attention_forward(me, rand, glob, x, seg, w, b_kv, b_q):
    chunks = len(x)
    far = chunks // 2
    rows = x[0].shape[0]
    length = rows * chunks
    heads = b_q.shape[0] // HEAD_DIM
    whole = lambda: pl.BlockSpec(memory_space=pltpu.VMEM)
    got = pl.pallas_call(
        functools.partial(forward_kernel, heads, chunks),
        out_shape=(jax.ShapeDtypeStruct((heads * HEAD_DIM, rows), bf16),) * far
        + (
            jax.ShapeDtypeStruct((heads, length // PAIR // 2, PAIR), f32),
            jax.ShapeDtypeStruct((heads, PAIR), f32),
            jax.ShapeDtypeStruct((heads, HEAD_DIM, PAIR), f32),
            jax.ShapeDtypeStruct((length + BLOCK, heads * PAIR), bf16),
            jax.ShapeDtypeStruct((length + BLOCK, heads * PAIR), bf16),
            jax.ShapeDtypeStruct((heads * HEAD_DIM, length), bf16),
            jax.ShapeDtypeStruct((BLOCK, length), bf16),
        ),
        in_specs=[pl.BlockSpec(memory_space=pltpu.SMEM)] * 3 + [whole() for _ in range(chunks + 4)],
        out_specs=tuple(whole() for _ in range(far + 7)),
        scratch_shapes=[
            pltpu.VMEM((heads, length, PAIR), f32),
            pltpu.VMEM((far, heads * HEAD_DIM, rows), bf16),
            pltpu.VMEM((chunks, rows), jnp.int32),
        ],
        compiler_params=pltpu.CompilerParams(vmem_limit_bytes=VMEM_BYTES),
        cost_estimate=pl.CostEstimate(flops=10_000_000_000, bytes_accessed=16_000_000, transcendentals=6_000_000),
        name="attention_forward",
    )(me, rand, glob, *x, seg, w, b_kv, b_q)
    return got[:far], got[far:]


def near_kernel(heads, chunks, me_ref, rand_ref, glob_ref, k_ref, kv_ref, q_ref, mask_ref, glob_ctx_ref, *refs):
    half = chunks // 2
    out_refs = refs[:half]
    lse_ref, out_ref = refs[half:]
    length = q_ref.shape[1]
    per_chunk = length // PAIR // chunks
    flip, gl = placed(me_ref, glob_ref, length // BLOCK, chunks)
    sparse_forward(heads, 0, half, per_chunk, rand_ref, glob_ref, flip, k_ref, kv_ref, q_ref, mask_ref, out_ref, lse_ref)
    for h in range(heads):
        put_global_columns(out_ref, slice(h * BLOCK, (h + 1) * BLOCK), gl, glob_ctx_ref[h], per_chunk, 0, half)
    for c in range(half):
        out_refs[c][...] = out_ref[c]


def attention_near(me, rand, glob, k, kv, q, mask, glob_ctx, chunks):
    heads = glob_ctx.shape[0]
    half = chunks // 2
    length = q.shape[1]
    rows = length // chunks
    whole = lambda: pl.BlockSpec(memory_space=pltpu.VMEM)
    got = pl.pallas_call(
        functools.partial(near_kernel, heads, chunks),
        out_shape=(jax.ShapeDtypeStruct((heads * HEAD_DIM, rows), bf16),) * half
        + (jax.ShapeDtypeStruct((heads, length // PAIR // 2, PAIR), f32),),
        in_specs=[pl.BlockSpec(memory_space=pltpu.SMEM)] * 3 + [whole() for _ in range(5)],
        out_specs=tuple(whole() for _ in range(half + 1)),
        scratch_shapes=[pltpu.VMEM((half, heads * HEAD_DIM, rows), bf16)],
        compiler_params=pltpu.CompilerParams(vmem_limit_bytes=VMEM_BYTES),
        cost_estimate=pl.CostEstimate(flops=6_000_000_000, bytes_accessed=9_000_000, transcendentals=3_000_000),
        name="attention_near",
    )(me, rand, glob, k, kv, q, mask, glob_ctx)
    return got[:half], got[half]


def backward_kernel(heads, chunks, me_ref, rand_ref, glob_ref, *refs):
    do_refs = refs[:chunks]
    (k_ref, kv_ref, q_ref, mask_ref, seg_ref, lse_near_ref, lse_far_ref, lseg_ref, w_ref, resid_ref, dq_ref, dkv_ref,
     first_ref) = refs[chunks : chunks + 13]
    part_refs = refs[chunks + 13 : 2 * chunks + 12]
    do_sc, acc, p_sc, d_sc, seg_sc, line_sc, lse_ref, row_sc = refs[2 * chunks + 12 :]
    rows = do_refs[0].shape[1]
    length = rows * chunks
    npairs = length // PAIR
    per_chunk = npairs // chunks
    scale = HEAD_DIM ** -0.5
    flip, gl = placed(me_ref, glob_ref, length // BLOCK, chunks)
    lse_ref[:, 0 : npairs // 2, :] = lse_near_ref[...]
    lse_ref[:, npairs // 2 :, :] = lse_far_ref[...]
    for c in range(chunks):
        do_sc[:, c * rows : (c + 1) * rows] = do_refs[c][...]
        row_sc[c : c + 1, :] = seg_ref[pl.ds(me_ref[0] ^ c, 1), :].astype(f32)

        @pl.loop(0, per_chunk // 4)
        def _(some):
            for i in range(4):
                t = 4 * some + i
                line = row_sc[c : c + 1, pl.ds(pl.multiple_of(t * PAIR, PAIR), PAIR)]
                line_sc[c * per_chunk + t] = line
                to = pl.multiple_of(c * rows + t * PAIR, PAIR)
                seg_sc[pl.ds(to, PAIR), :] = jnp.transpose(jnp.broadcast_to(line, (PAIR, PAIR)), (1, 0))

    seg_sc[length : length + BLOCK, :] = jnp.full((BLOCK, PAIR), -1.0, f32)
    first2, second2 = lane_halves(2 * PAIR, bf16)
    ffirst, fsecond = lane_halves(PAIR, f32)
    lane = lax.broadcasted_iota(jnp.int32, (1, PAIR), 1)
    line_row = lax.broadcasted_iota(jnp.int32, (PAIR, 1), 0)
    zeros = jnp.zeros((BLOCK, PAIR), bf16)
    blank = jnp.zeros((PAIR, PAIR), bf16)

    def head_rows(h):
        return slice(h * BLOCK, (h + 1) * BLOCK)

    def joint(q, mask, do):
        left = jnp.concatenate([q, mask, blank], axis=0)
        right = jnp.concatenate([blank, zeros, do], axis=0)
        return jnp.concatenate([left, right], axis=1)

    def sources(q, do):
        top = jnp.concatenate([q, zeros], axis=1)
        return jnp.concatenate([top, jnp.concatenate([zeros, do], axis=1)], axis=0)

    step = 512
    mask_glob = global_columns(mask_ref, slice(0, BLOCK), gl).astype(bf16)
    q_glob = [global_columns(q_ref, head_rows(h), gl).astype(bf16) for h in range(heads)]
    do_glob = [global_columns(do_sc, head_rows(h), gl).astype(bf16) for h in range(heads)]

    def weigh(c, deltas):
        at = pl.multiple_of(c * step, step)
        new = []
        for h in range(heads):
            left = jnp.concatenate([k_ref[pl.ds(at, step), head_lanes(h)], kv_ref[pl.ds(at, step), head_lanes(h)]], axis=1)
            both = dot_nn(left, joint(q_glob[h], mask_glob, do_glob[h]))
            p = jnp.exp(both[:, 0:PAIR] - lseg_ref[h : h + 1, :])
            dp = both[:, PAIR:]
            p_sc[h, pl.ds(at, step), :] = p
            d_sc[h, pl.ds(at, step), :] = dp
            new.append(deltas[h] + jnp.sum(p * dp, axis=0, keepdims=True))
        return tuple(new)

    deltas = lax.fori_loop(0, length // step, weigh, (jnp.zeros((1, PAIR), f32),) * heads)

    def spread(c, dqs):
        at = pl.multiple_of(c * step, step)
        new = []
        for h in range(heads):
            p = p_sc[h, pl.ds(at, step), :]
            ds = (p * (d_sc[h, pl.ds(at, step), :] - deltas[h])).astype(bf16)
            both = jnp.concatenate([ds, p.astype(bf16)], axis=1)
            acc[h, pl.ds(at, step), :] = dot_nt(both, sources(q_glob[h], do_glob[h]))
            new.append(dqs[h] + dot_tn(k_ref[pl.ds(at, step), head_lanes(h)], ds))
        return tuple(new)

    dqs = lax.fori_loop(0, length // step, spread, (jnp.zeros((PAIR, PAIR), f32),) * heads)
    for h in range(heads):
        acc[h, pl.ds(length, BLOCK), :] = jnp.zeros((BLOCK, PAIR), f32)

    def one_pair(pair):
        chunk = pair // per_chunk
        local = pl.multiple_of((pair % per_chunk) * PAIR, PAIR)
        at = pl.multiple_of(pair * PAIR, PAIR)
        hit_first = (gl[0] == 2 * pair) | (gl[1] == 2 * pair)
        hit_second = (gl[0] == 2 * pair + 1) | (gl[1] == 2 * pair + 1)
        shut = ffirst * jnp.where(hit_first, -MASKED, 0.0) + fsecond * jnp.where(hit_second, -MASKED, 0.0)
        every = slice(0, PAIR)
        for h in range(heads):
            kl = head_lanes(h)
            shared, mine, other = slots(rand_ref, glob_ref, flip, h, pair, length // BLOCK)
            q = q_ref[head_rows(h), pl.ds(at, PAIR)]
            do = do_sc[head_rows(h), pl.ds(at, PAIR)]
            lse = lse_ref[h, pl.ds(pair, 1), :] + shut
            src = sources(q, do)
            src2 = jnp.concatenate([src * first2, src * second2], axis=0)
            k_sh = stack_rows(k_ref, shared, kl)
            two_sh = dot_nn(
                jnp.concatenate([k_sh, stack_rows(kv_ref, shared, kl)], axis=1),
                joint(q, mask_ref[:, pl.ds(at, PAIR)], do),
            )
            kv_pr = jnp.concatenate([stack_rows(kv_ref, mine, kl), stack_rows(kv_ref, other, kl)], axis=1)
            two_pr = dot_nn(kv_pr, src2)
            seg_pr = jnp.where(lane < BLOCK, stack_rows(seg_sc, mine, every), stack_rows(seg_sc, other, every))
            agree = seg_pr == line_sc[pair]
            p_sh = jnp.exp(two_sh[:, 0:PAIR] - lse)
            p_pr = jnp.where(agree, jnp.exp(two_pr[:, 0:PAIR] - lse), 0.0)
            d_sh, d_pr = two_sh[:, PAIR:], two_pr[:, PAIR:]
            delta = jnp.sum(p_sh * d_sh, axis=0, keepdims=True) + jnp.sum(p_pr * d_pr, axis=0, keepdims=True)
            ds_sh = (p_sh * (d_sh - delta)).astype(bf16)
            ds_pr = (p_pr * (d_pr - delta)).astype(bf16)
            g_sh = dot_nt(jnp.concatenate([ds_sh, p_sh.astype(bf16)], axis=1), src)
            g_pr = dot_nt(jnp.concatenate([ds_pr, p_pr.astype(bf16)], axis=1), src2)
            for j, o in enumerate(shared):
                acc[h, pl.ds(o, BLOCK), :] += g_sh[j * BLOCK : (j + 1) * BLOCK]
            for j, o in enumerate(mine):
                acc[h, pl.ds(o, BLOCK), :] += g_pr[j * BLOCK : (j + 1) * BLOCK, 0:PAIR]
            for j, o in enumerate(other):
                acc[h, pl.ds(o, BLOCK), :] += g_pr[j * BLOCK : (j + 1) * BLOCK, PAIR:]
            t_pr = dot_tn(ds_pr, kv_pr)
            dq = dot_tn(ds_sh, k_sh) + jnp.where(line_row < BLOCK, t_pr[:, 0:PAIR], t_pr[:, PAIR:])
            dq = jnp.transpose(dq, (1, 0))[0:BLOCK]
            dq_ref[chunk, head_rows(h), pl.ds(local, PAIR)] = (dq * scale).astype(bf16)

    @pl.loop(0, npairs // BACK_UNROLL)
    def _(some):
        for i in range(BACK_UNROLL):
            one_pair(BACK_UNROLL * some + i)

    for h in range(heads):
        put_global_columns(dq_ref, head_rows(h), gl, dqs[h][0:BLOCK] * scale, per_chunk, 0, chunks)
        for c in range(chunks):
            dkv_ref[c, :, head_lanes(h)] = acc[h, pl.ds(c * rows, rows), :].astype(bf16)
    tile = 256
    wq = query_weights(w_ref, heads)
    for c in range(chunks):

        @pl.loop(0, rows // tile)
        def _(t):
            at = pl.multiple_of(t * tile, tile)
            got = dot_tn(dq_ref[c, :, pl.ds(at, tile)], wq)
            got = got + dot_nt(dkv_ref[c, pl.ds(at, tile), :], w_ref[:, 0 : heads * PAIR])
            if c == 0:
                first_ref[pl.ds(at, tile), :] = resid_ref[pl.ds(at, tile), :] + got
            else:
                part_refs[c - 1][pl.ds(at, tile), :] = got.astype(bf16)


def attention_backward(me, rand, glob, do, k, kv, q, mask, seg, lse_near, lse_far, lseg, w, resid):
    chunks = len(do)
    group, rows = do[0].shape
    heads = group // HEAD_DIM
    width = w.shape[0]
    length = rows * chunks
    whole = lambda: pl.BlockSpec(memory_space=pltpu.VMEM)
    return pl.pallas_call(
        functools.partial(backward_kernel, heads, chunks),
        out_shape=(
            jax.ShapeDtypeStruct((chunks, group, rows), bf16),
            jax.ShapeDtypeStruct((chunks, rows, heads * PAIR), bf16),
            jax.ShapeDtypeStruct((rows, width), f32),
        )
        + (jax.ShapeDtypeStruct((rows, width), bf16),) * (chunks - 1),
        in_specs=[pl.BlockSpec(memory_space=pltpu.SMEM)] * 3 + [whole() for _ in range(chunks + 10)],
        out_specs=tuple(whole() for _ in range(chunks + 2)),
        scratch_shapes=[
            pltpu.VMEM((group, length), bf16),
            pltpu.VMEM((heads, length + BLOCK, PAIR), f32),
            pltpu.VMEM((heads, length, PAIR), f32),
            pltpu.VMEM((heads, length, PAIR), f32),
            pltpu.VMEM((length + BLOCK, PAIR), f32),
            pltpu.VMEM((length // PAIR, 1, PAIR), f32),
            pltpu.VMEM((heads, length // PAIR, PAIR), f32),
            pltpu.VMEM((chunks, rows), f32),
        ],
        compiler_params=pltpu.CompilerParams(vmem_limit_bytes=VMEM_BYTES),
        cost_estimate=pl.CostEstimate(flops=30_000_000_000, bytes_accessed=24_000_000, transcendentals=8_000_000),
        name="attention_backward",
    )(me, rand, glob, *do, k, kv, q, mask, seg, lse_near, lse_far, lseg, w, resid)


def round_up(value, to):
    return -(-value // to) * to


def half_columns(ref, index, place):
    at = index // 2 * PAIR
    both = ref[:, at : at + PAIR].astype(f32)
    return both if index % 2 == place else pltpu.roll(both, BLOCK, 1)


def two_halves(first, second):
    lane = lax.broadcasted_iota(jnp.int32, (1, PAIR), 1)
    return jnp.where(lane < BLOCK, first, second)


def pack_kernel(seq_n, wq_ref, wk_ref, wv_ref, wo_ref, up_ref, down_ref, bup_ref, vec_ref, pack_ref, rest_ref):
    own, width = wq_ref.shape
    heads = width // HEAD_DIM // seq_n
    blocks, inner = pack_ref.shape[0], pack_ref.shape[2]
    for s in range(seq_n):
        pieces = [
            two_halves(half_columns(wk_ref, s * heads + h, 0), half_columns(wv_ref, s * heads + h, 1))
            for h in range(heads)
        ]
        for h in range(0, heads, 2):
            second = half_columns(wq_ref, s * heads + h + 1, 1) if h + 1 < heads else jnp.zeros((own, PAIR), f32)
            pieces.append(two_halves(half_columns(wq_ref, s * heads + h, 0), second))
        piece = jnp.concatenate(pieces, axis=1).astype(bf16)
        notes = jnp.concatenate([vec_ref[...], jnp.zeros((8, piece.shape[1] - width), bf16)], axis=1) if (
            piece.shape[1] > width
        ) else vec_ref[:, 0 : piece.shape[1]]
        for b in range(blocks):
            for i in range(inner):
                pack_ref[b, s, i, 0:own, :] = piece
                pack_ref[b, s, i, own : own + 8, :] = notes
    u = up_ref.shape[0]
    rest_ref[0:u, :] = up_ref[...]
    rest_ref[u : 2 * u, :] = down_ref[...]
    rest_ref[2 * u : 2 * u + own, :] = wo_ref[...]
    row = lax.broadcasted_iota(jnp.int32, (8, 1), 0)
    block = jnp.where(row == 7, bup_ref[...].astype(f32), vec_ref[...].astype(f32))
    rest_ref[2 * u + own : 2 * u + own + 8, :] = block.astype(bf16)


def packed_weights(w_q, w_k, w_v, w_o, w_up, w_down, b_up, vec, dp_n, seq_n, ffn_n):
    own, width = w_q.shape
    heads = width // HEAD_DIM // seq_n
    lanes = heads * PAIR + round_up(heads * HEAD_DIM, PAIR)
    u = w_up.shape[0]
    if own % 8 or u % 16:
        group = heads * HEAD_DIM
        cols = lambda w: w.reshape(own, seq_n, heads, HEAD_DIM).transpose(1, 0, 2, 3)
        kv = jnp.stack([cols(w_k), cols(w_v)], axis=3).reshape(seq_n, own, 2 * group)
        piece = jnp.concatenate([kv, cols(w_q).reshape(seq_n, own, group)], axis=2)
        piece = jnp.pad(piece, ((0, 0), (0, round_up(own, 8) - own), (0, lanes - 3 * group)))
        notes = jnp.broadcast_to(vec[None, :, :lanes], (seq_n, 8, lanes))
        piece = jnp.concatenate([piece, notes], axis=1)
        pack = jnp.broadcast_to(piece[None, :, None], (dp_n, seq_n, ffn_n) + piece.shape[1:])
        w_o = jnp.pad(w_o, ((0, round_up(own, 8) - own), (0, 0)))
        return pack, jnp.concatenate([w_up, w_down, w_o, vec[:7], b_up], axis=0)
    whole = lambda: pl.BlockSpec(memory_space=pltpu.VMEM)
    return pl.pallas_call(
        functools.partial(pack_kernel, seq_n),
        out_shape=(
            jax.ShapeDtypeStruct((dp_n, seq_n, ffn_n, own + 8, lanes), bf16),
            jax.ShapeDtypeStruct((2 * u + own + 8, width), bf16),
        ),
        in_specs=[whole() for _ in range(8)],
        out_specs=(whole(), whole()),
        name="packed_weights",
    )(w_q, w_k, w_v, w_o, w_up, w_down, b_up, vec)


def weights_kernel(chunks, direct, *refs):
    x_refs = refs[:chunks]
    dq_ref, dkv_ref, out_ref, sums_ref, acc, sum_sc = refs[chunks:]
    group = dq_ref.shape[1]
    lanes = dkv_ref.shape[2]
    full = acc.shape[0]
    x = jnp.concatenate([r[...] for r in x_refs], axis=0)
    dkv = jnp.concatenate([dkv_ref[c] for c in range(chunks)], axis=0)
    dq = jnp.concatenate([dq_ref[c] for c in range(chunks)], axis=1)
    ones = jnp.ones((8, x.shape[0]), bf16)

    @pl.when(pl.program_id(0) == 0)
    def _():
        acc[...] = jnp.zeros_like(acc)
        sum_sc[...] = jnp.zeros_like(sum_sc)

    acc[0:lanes, :] += dot_tn(dkv, x)
    acc[lanes : lanes + group, :] += dot_nn(dq, x)
    sum_sc[:, 0:lanes] += dot_nn(ones, dkv)
    sum_sc[:, lanes : lanes + group] += dot_nt(ones, dq)

    @pl.when(pl.program_id(0) == pl.num_programs(0) - 1)
    def _():
        grad = jnp.transpose(acc[...], (1, 0))
        sums_ref[...] = sum_sc[...]
        if direct:
            blocks, per, _ = out_ref.shape
            own = per - 8
            grad = grad.reshape(blocks, own, full)
            for b in range(blocks):
                out_ref[b, 0:own, :] = grad[b].astype(bf16)
                out_ref[b, own:, :] = sum_sc[...].astype(bf16)
        else:
            out_ref[...] = grad.astype(bf16)


def projection_gradients(x, dq, dkv, own, devices):
    chunks, group, rows = dq.shape
    width = x[0].shape[1]
    lanes = dkv.shape[2]
    full = lanes + round_up(group, PAIR)
    direct = own % 8 == 0
    tile = 256
    shape = (devices, own + 8, full) if direct else (width, full)
    out, sums = pl.pallas_call(
        functools.partial(weights_kernel, chunks, direct),
        grid=(rows // tile,),
        out_shape=(jax.ShapeDtypeStruct(shape, bf16), jax.ShapeDtypeStruct((8, full), f32)),
        in_specs=[pl.BlockSpec((tile, width), lambda i: (i, 0)) for _ in range(chunks)]
        + [
            pl.BlockSpec((chunks, group, tile), lambda i: (0, 0, i)),
            pl.BlockSpec((chunks, tile, lanes), lambda i: (0, i, 0)),
        ],
        out_specs=(
            pl.BlockSpec(shape, lambda i: (0,) * len(shape), pipeline_mode=pl.Buffered(1)),
            pl.BlockSpec((8, full), lambda i: (0, 0)),
        ),
        scratch_shapes=[pltpu.VMEM((full, width), f32), pltpu.VMEM((8, full), f32)],
        compiler_params=pltpu.CompilerParams(vmem_limit_bytes=VMEM_BYTES),
        cost_estimate=pl.CostEstimate(flops=4_000_000_000, bytes_accessed=12_000_000, transcendentals=0),
        name="projection_gradients",
    )(*x, dq, dkv)
    if not direct:
        out = jnp.pad(out.reshape(devices, own, full), ((0, 0), (0, round_up(own, 8) - own), (0, 0)))
        out = jnp.concatenate([out, jnp.broadcast_to(sums[None].astype(bf16), (devices, 8, full))], axis=1)
    return out


def unpack_kernel(own, got_ref, q_ref, k_ref, v_ref, sums_ref, tot):
    dp_n, seq_n, ffn_n, per, full = got_ref.shape
    width = q_ref.shape[1]
    heads = width // HEAD_DIM // seq_n
    for s in range(seq_n):
        total = jnp.zeros((per, full), f32)
        for d in range(dp_n):
            for f in range(ffn_n):
                total = total + got_ref[d, s, f].astype(f32)
        tot[s] = total
        sums_ref[s : s + 1, :] = total[per - 8 : per - 7, :]
    for w in range(width // PAIR):
        spots = [((2 * w + i) // heads, (2 * w + i) % heads) for i in range(2)]
        cols = slice(w * PAIR, (w + 1) * PAIR)
        for ref, where in (
            (k_ref, lambda h: 2 * h),
            (v_ref, lambda h: 2 * h + 1),
            (q_ref, lambda h: 2 * heads + h),
        ):
            both = [half_columns(tot.at[g], where(h), i) for i, (g, h) in enumerate(spots)]
            ref[:, cols] = two_halves(*both)[0:own]


def unpacked_gradients(got, own, width):
    dp_n, seq_n, ffn_n, per, full = got.shape
    whole = lambda: pl.BlockSpec(memory_space=pltpu.VMEM)
    return pl.pallas_call(
        functools.partial(unpack_kernel, own),
        out_shape=(jax.ShapeDtypeStruct((own, width), f32),) * 3 + (jax.ShapeDtypeStruct((seq_n, full), f32),),
        in_specs=[whole()],
        out_specs=tuple(whole() for _ in range(4)),
        scratch_shapes=[pltpu.VMEM((seq_n, per, full), f32)],
        compiler_params=pltpu.CompilerParams(vmem_limit_bytes=VMEM_BYTES),
        name="unpacked_gradients",
    )(got)


NORM_EPS = 1e-12


def transposed(value):
    return jnp.transpose(value.astype(f32), (1, 0)).astype(bf16)


def unit_rows(value):
    center = value - jnp.mean(value, axis=-1, keepdims=True)
    scale = lax.rsqrt(jnp.mean(center * center, axis=-1, keepdims=True) + NORM_EPS)
    return center * scale, scale


def unit_rows_back(grad, unit, scale):
    return scale * (
        grad - jnp.mean(grad, axis=-1, keepdims=True) - unit * jnp.mean(grad * unit, axis=-1, keepdims=True)
    )


def rows_kernel(parts, blocks, up_rows, own, me_ref, *refs):
    ctx_refs = refs[:parts]
    (x_ref, cot_ref, rest_ref, wo_ref, vec_ref, bup_ref, out_ref, resid_ref, hid_ref, pre_ref, nlt_ref, gft_ref,
     gb_ref) = refs[parts : parts + 13]
    do_refs = refs[parts + 13 : 2 * parts + 13]
    sums_ref, gbup_ref, slope_sc, wo_sc, wide_sc = refs[2 * parts + 13 :]
    group = ctx_refs[0].shape[0]
    width = x_ref.shape[1]

    def up(f):
        return rest_ref[:, f, 0:up_rows, :].reshape(width, rest_ref.shape[3])

    def down(f):
        return rest_ref[:, f, up_rows : 2 * up_rows, :].reshape(width, rest_ref.shape[3])

    def own_rows(k):
        return pl.ds(pl.multiple_of((me_ref[0] ^ k) * group, group), group)

    @pl.when(pl.program_id(0) == 0)
    def _():
        sums_ref[...] = jnp.zeros_like(sums_ref)
        gbup_ref[...] = jnp.zeros_like(gbup_ref)
        if own:
            for o in range(rest_ref.shape[0]):
                for f in range(blocks):
                    to = (o * blocks + f) * own
                    wide_sc[to : to + own, :] = rest_ref[o, f, 2 * up_rows : 2 * up_rows + own, :].astype(f32)
            wo_sc[...] = wide_sc[...].astype(bf16)
        else:
            wo_sc[...] = wo_ref[...]

    def bias_up(f):
        if own:
            row = rest_ref[0, f, 2 * up_rows + own : 2 * up_rows + own + 8, :].astype(f32)
            return row[7:8, :]
        return bup_ref[f : f + 1, :]

    ctx = jnp.concatenate([r[...] for r in ctx_refs], axis=0)
    w_o = jnp.concatenate([wo_sc[own_rows(k), :] for k in range(parts)], axis=0)
    resid_one = x_ref[...].astype(f32) + (dot_tn(ctx, w_o) + vec_ref[0:1, :])
    unit_one, scale_one = unit_rows(resid_one)
    normed_one = unit_one * vec_ref[2:3, :] + vec_ref[3:4, :]
    low = normed_one.astype(bf16)
    nlt_ref[...] = transposed(normed_one)
    total = normed_one + vec_ref[1:2, :]
    pre = dot_nn(low, up(0)) + bias_up(0)
    for f in range(blocks):
        later = dot_nn(low, up(f + 1)) + bias_up(f + 1) if f + 1 < blocks else None
        phi = 0.5 + 0.5 * lax.erf(pre * (0.5 ** 0.5))
        slope_sc[f] = phi + pre * (jnp.exp(-0.5 * pre * pre) * 0.3989422804014327)
        hid = (pre * phi).astype(bf16)
        hid_ref[f] = hid
        total = total + dot_nt(hid, down(f))
        pre = later
    unit_two, scale_two = unit_rows(total)
    out_ref[...] = (unit_two * vec_ref[4:5, :] + vec_ref[5:6, :]).astype(bf16)
    cot = cot_ref[...].astype(f32)
    grad_two = unit_rows_back(cot * vec_ref[4:5, :], unit_two, scale_two)
    grad_ffn = grad_two.astype(bf16)
    gft_ref[...] = transposed(grad_two)
    grad_normed = grad_two
    back = dot_nn(grad_ffn, down(0))
    for f in range(blocks):
        later = dot_nn(grad_ffn, down(f + 1)) if f + 1 < blocks else None
        grad_pre = (back * slope_sc[f]).astype(bf16)
        pre_ref[f] = grad_pre
        gbup_ref[f : f + 1, :] += jnp.sum(grad_pre.astype(f32), axis=0, keepdims=True)
        grad_normed = grad_normed + dot_nt(grad_pre, up(f))
        back = later
    resid = unit_rows_back(grad_normed * vec_ref[2:3, :], unit_one, scale_one)
    resid_ref[...] = resid
    branch = resid.astype(bf16)
    gb_ref[...] = branch
    do = dot_nt(w_o, branch).astype(bf16)
    for k in range(parts):
        do_refs[k][...] = do[k * group : (k + 1) * group]
    for row, value in enumerate(
        (branch.astype(f32), grad_ffn.astype(f32), grad_normed * unit_one, grad_normed, cot * unit_two, cot)
    ):
        sums_ref[row : row + 1, :] += jnp.sum(value, axis=0, keepdims=True)


def rows_chain(me, ctx_parts, x, cot, rest, up_rows, own, w_o, vecs, bias_up):
    parts = len(ctx_parts)
    group, rows = ctx_parts[0].shape
    width = x.shape[1]
    outer, blocks, per, hidden = rest.shape
    tile = 256
    once = lambda shape: pl.BlockSpec(shape, lambda i: (0,) * len(shape), pipeline_mode=pl.Buffered(1))
    tall = pl.BlockSpec((tile, width), lambda i: (i, 0))
    wide = pl.BlockSpec((width, tile), lambda i: (0, i))
    cube = pl.BlockSpec((blocks, tile, hidden), lambda i: (0, i, 0))
    return pl.pallas_call(
        functools.partial(rows_kernel, parts, blocks, up_rows, own),
        grid=(rows // tile,),
        out_shape=(
            jax.ShapeDtypeStruct((rows, width), bf16),
            jax.ShapeDtypeStruct((rows, width), f32),
            jax.ShapeDtypeStruct((blocks, rows, hidden), bf16),
            jax.ShapeDtypeStruct((blocks, rows, hidden), bf16),
            jax.ShapeDtypeStruct((width, rows), bf16),
            jax.ShapeDtypeStruct((width, rows), bf16),
            jax.ShapeDtypeStruct((rows, width), bf16),
        )
        + (jax.ShapeDtypeStruct((group, rows), bf16),) * parts
        + (jax.ShapeDtypeStruct((8, width), f32), jax.ShapeDtypeStruct((8, hidden), f32)),
        in_specs=[pl.BlockSpec(memory_space=pltpu.SMEM)]
        + [pl.BlockSpec((group, tile), lambda i: (0, i))] * parts
        + [tall, tall, once(rest.shape), once(w_o.shape), once(vecs.shape), once(bias_up.shape)],
        out_specs=(
            tall, tall, cube, cube, wide, wide, tall,
        )
        + (pl.BlockSpec((group, tile), lambda i: (0, i)),) * parts
        + (pl.BlockSpec((8, width), lambda i: (0, 0)), pl.BlockSpec((8, hidden), lambda i: (0, 0))),
        scratch_shapes=[
            pltpu.VMEM((blocks, tile, hidden), f32),
            pltpu.VMEM((width, width), bf16),
            pltpu.VMEM((width, width), f32),
        ],
        compiler_params=pltpu.CompilerParams(vmem_limit_bytes=VMEM_BYTES),
        cost_estimate=pl.CostEstimate(flops=22_000_000_000, bytes_accessed=40_000_000, transcendentals=6_000_000),
        name="rows_chain",
    )(me, *ctx_parts, x, cot, rest, w_o, vecs, bias_up)


def outer_kernel(parts, up_rows, own, apart, me_ref, *refs):
    ctx_refs = refs[:parts]
    nlt_ref, gft_ref, gb_ref, pre_ref, hid_ref, sums_ref, gbup_ref, out_ref = refs[parts : parts + 8]
    wo_sc = refs[-1]
    slabs, hidden = out_ref.shape[0], out_ref.shape[3]
    group = ctx_refs[0].shape[0]
    f = pl.program_id(0)
    up = dot_nn(nlt_ref[...], pre_ref[0]).astype(bf16).reshape(slabs, up_rows, hidden)
    if apart:
        refs[parts + 8][:, 0, :, :] = up[:, 0:apart]
    out_ref[:, 0, 0 : up_rows - apart, :] = up[:, apart:]
    at = up_rows - apart
    down = dot_nn(gft_ref[...], hid_ref[0]).astype(bf16)
    out_ref[:, 0, at : at + up_rows, :] = down.reshape(slabs, up_rows, hidden)
    at += up_rows
    if not own:
        return

    @pl.when(f == 0)
    def _():
        for k in range(parts):
            wo_sc[k] = dot_nn(ctx_refs[k][...], gb_ref[...])

    share = slabs // parts
    stride = group // share
    for k in range(parts):
        for j in range(share):
            rows = pl.ds(pl.multiple_of(j * stride + f * own, 8), own)
            out_ref[(me_ref[0] ^ k) * share + j, 0, at : at + own, :] = wo_sc[k, rows, :].astype(bf16)
    small = jnp.concatenate([gbup_ref[pl.ds(f, 1), :], sums_ref[0:7, :]], axis=0).astype(bf16)
    for o in range(slabs):
        out_ref[o, 0, at + own :, :] = small


def outer_products(me, ctx_parts, nlt, gft, gb, pre, hid, sums, gbup, slabs, up_rows, own, apart):
    blocks, rows, hidden = pre.shape
    parts = len(ctx_parts)
    group = ctx_parts[0].shape[0]
    per = 2 * up_rows - apart + (own + 8 if own else 0)
    sizes = (per, apart) if apart else (per,)
    once = lambda shape: pl.BlockSpec(shape, lambda i: (0,) * len(shape), pipeline_mode=pl.Buffered(1))
    return pl.pallas_call(
        functools.partial(outer_kernel, parts, up_rows, own, apart),
        grid=(blocks,),
        out_shape=tuple(jax.ShapeDtypeStruct((slabs, blocks, r, hidden), bf16) for r in sizes),
        in_specs=[pl.BlockSpec(memory_space=pltpu.SMEM)]
        + [once(c.shape) for c in ctx_parts]
        + [
            once(nlt.shape),
            once(gft.shape),
            once(gb.shape),
            pl.BlockSpec((1, rows, hidden), lambda i: (i, 0, 0)),
            pl.BlockSpec((1, rows, hidden), lambda i: (i, 0, 0)),
            once(sums.shape),
            once(gbup.shape),
        ],
        out_specs=tuple(pl.BlockSpec((slabs, 1, r, hidden), lambda i: (0, i, 0, 0)) for r in sizes),
        scratch_shapes=[pltpu.VMEM((parts, group, gb.shape[1]), f32)],
        compiler_params=pltpu.CompilerParams(vmem_limit_bytes=VMEM_BYTES),
        cost_estimate=pl.CostEstimate(flops=11_000_000_000, bytes_accessed=28_000_000, transcendentals=0),
        name="outer_products",
    )(me, *ctx_parts, nlt, gft, gb, pre, hid, sums, gbup)


def finish_kernel(up_rows, own, total_ref, up_ref, down_ref, wo_ref, small_ref):
    rest = total_ref[...].astype(f32)
    up_ref[...] = rest[0:up_rows]
    down_ref[...] = rest[up_rows : 2 * up_rows]
    at = 2 * up_rows
    wo_ref[...] = rest[at : at + own]
    small_ref[...] = rest[at + own : at + own + 8]


def finished(total, up_rows, own):
    hidden = total.shape[1]
    whole = lambda: pl.BlockSpec(memory_space=pltpu.VMEM)
    return pl.pallas_call(
        functools.partial(finish_kernel, up_rows, own),
        out_shape=tuple(jax.ShapeDtypeStruct((r, hidden), f32) for r in (up_rows, up_rows, own, 8)),
        in_specs=[whole()],
        out_specs=tuple(whole() for _ in range(4)),
        name="finished",
    )(total)


ALL = ("dp", "seq", "ffn")


def flip_send(array, axis, bits):
    count = lax.axis_size(axis)
    return lax.ppermute(array, axis, [(i, i ^ bits) for i in range(count)])


def shards(
    tokens, w_query, w_key, w_value, w_output, b_query, b_value, b_output, w_up, b_up, w_down, b_down,
    gain_attn, shift_attn, gain_ffn, shift_ffn, segment_ids, random_blocks, global_blocks, cotangent,
):
    seq_n, dp_n, ffn_n = lax.axis_size("seq"), lax.axis_size("dp"), lax.axis_size("ffn")
    outer, devices = dp_n * seq_n, dp_n * seq_n * ffn_n
    me = lax.axis_index("seq")
    here = (lax.axis_index("dp") * seq_n + me) * ffn_n + lax.axis_index("ffn")
    own, width = w_query.shape
    own_pad = round_up(own, 8)
    group = width // seq_n
    heads = group // HEAD_DIM
    features = tokens[0]
    rows = features.shape[0]
    order = jnp.stack([me ^ k for k in range(seq_n)])
    me_ref = me.astype(jnp.int32)[None]

    near = [features] + [None] * (seq_n - 1)
    for k in sorted(range(1, seq_n), key=lambda k: (k & (k - 1), -k)):
        bit = k & -k
        near[k] = flip_send(features if bit == k else near[k ^ bit], "seq", bit)

    vec = jnp.stack([b_output, b_down, gain_attn, shift_attn, gain_ffn, shift_ffn, b_query, b_value])
    vec = jnp.pad(vec, ((0, 0), (0, width - own)))
    seg = segment_ids[0].reshape(seq_n, rows)
    rand = random_blocks.reshape(-1)
    pack, rest = packed_weights(
        w_query, w_key, w_value, w_output, w_up, w_down, b_up[None], vec, dp_n, seq_n, ffn_n
    )
    lanes = pack.shape[4]
    pack, seg, rand = lax.optimization_barrier((pack, seg, rand))
    pack = lax.all_to_all(
        pack.reshape(devices, own_pad + 8, lanes), ALL, split_axis=0, concat_axis=0, tiled=True
    )
    rest = lax.all_gather(rest, ALL, axis=0, tiled=False)
    w_own = pack[:, :own].reshape(width, lanes)
    share = devices // seq_n
    biases = lax.dynamic_slice(pack, (share * me, own_pad + 6, 0), (share, 2, own))
    biases = biases.transpose(1, 0, 2).reshape(2, group).astype(f32)
    by_head = biases[1].reshape(heads, 1, HEAD_DIM)
    b_kv = jnp.concatenate([jnp.zeros_like(by_head), by_head], axis=1).reshape(1, heads * PAIR)

    far = seq_n // 2
    ctx_far, (lse_far, lseg, glob_ctx, k_all, v_all, q_all, mask_all) = attention_forward(
        me_ref, rand, global_blocks, near, seg, w_own, b_kv, biases[0][:, None]
    )
    ctx_parts = [None] * far + [flip_send(ctx_far[k - far], "seq", k) for k in range(far, seq_n)]
    ctx_near, lse_near = attention_near(
        me_ref, rand, global_blocks, k_all, v_all, q_all, mask_all, glob_ctx, seq_n
    )
    ctx_parts[far:], ctx_parts[0] = lax.optimization_barrier((ctx_parts[far:], ctx_near[0]))
    for k in range(1, far):
        ctx_parts[k] = flip_send(ctx_near[k], "seq", k)

    up_rows = w_up.shape[0]
    at = 2 * up_rows
    rest = rest.reshape(outer, ffn_n, rest.shape[1], width)
    w_o = rest[:, :, at : at + own].reshape(width, width)
    bias_up = rest[0, :, at + own_pad + 7].astype(f32)
    vecs = pack[:, own_pad:, :own].transpose(1, 0, 2).reshape(8, width).astype(f32)
    direct = up_rows % 16 == 0 and own % 8 == 0 and outer % seq_n == 0 and (outer // seq_n) * ffn_n * own == group
    if not direct:
        rest = rest[:, :, :at].reshape(outer, ffn_n, 2, up_rows, width).transpose(1, 2, 0, 3, 4)
        rest = rest.reshape(1, ffn_n, 2 * outer * up_rows, width)
    slabs, slab_rows = (outer, up_rows) if direct else (1, outer * up_rows)

    got = rows_chain(
        me_ref, ctx_parts, features, cotangent[0], rest, slab_rows, own if direct else 0,
        jnp.zeros((8, PAIR), bf16) if direct else w_o, vecs, jnp.zeros((8, PAIR), f32) if direct else bias_up,
    )
    out, grad_resid_one, hidden, grad_pre, normed_t, grad_ffn_t, grad_branch = got[:7]
    grad_ctx, (sums, grad_bias_up) = got[7 : 7 + seq_n], got[7 + seq_n :]
    do = [grad_ctx[0]] + [flip_send(grad_ctx[k], "seq", k) for k in range(1, seq_n)]

    payload = outer_products(
        me_ref, ctx_parts, normed_t, grad_ffn_t, grad_branch, grad_pre, hidden, sums, grad_bias_up, slabs, slab_rows,
        own if direct else 0, APART if direct else 0,
    )
    payload, apart = payload if direct and APART else (payload[0], None)
    if not direct:
        grad_out = dot_nn(jnp.concatenate(ctx_parts, axis=0), grad_branch).astype(bf16)
        grad_out = grad_out.reshape(seq_n, group, width)[order].reshape(outer, ffn_n, own, width)
        top = jnp.broadcast_to(grad_bias_up[None, :ffn_n, None], (outer, ffn_n, 1, width))
        small = jnp.concatenate([top, jnp.broadcast_to(sums[None, None, :7], (outer, ffn_n, 7, width))], axis=2)
        small = small.astype(bf16)
        payload = payload.reshape(ffn_n, 2, outer, up_rows, width).transpose(2, 0, 1, 3, 4)
        payload = jnp.concatenate([payload.reshape(outer, ffn_n, at, width), grad_out, small], axis=2)
        payload = jnp.pad(payload, ((0, 0), (0, 0), (0, -payload.shape[2] % 32), (0, 0)))
    payload, apart, do = lax.optimization_barrier((payload, apart, do))
    total = lax.psum_scatter(payload.reshape(-1, width), ("dp", "seq"), scatter_dimension=0, tiled=True)
    if apart is not None:
        apart = lax.all_to_all(
            apart.reshape(devices, APART, width), ALL, split_axis=0, concat_axis=0, tiled=True
        )

    got = attention_backward(
        me_ref, rand, global_blocks, do, k_all, v_all, q_all, mask_all, seg, lse_near, lse_far, lseg, w_own,
        grad_resid_one,
    )
    dq, dkv, grad_features = got[:3]
    part = [None] + list(got[3:])
    bit = 1
    while bit < seq_n:
        for k in range(seq_n):
            if k & -k == bit and k != bit:
                came = flip_send(part[k], "seq", bit).astype(f32)
                part[k ^ bit] = (part[k ^ bit].astype(f32) + came).astype(bf16)
        bit *= 2
    grad_w = projection_gradients(near, dq, dkv, own, devices)
    bit = seq_n // 2
    lead = 192
    first = flip_send(part[bit][:lead], "seq", bit)
    grad_w, first = lax.optimization_barrier((grad_w, first))
    second = flip_send(part[bit][lead:], "seq", bit)
    extra = [flip_send(part[k], "seq", k) for k in range(1, bit) if k & (k - 1) == 0]
    extra[0], total = lax.optimization_barrier((extra[0], total))
    total = lax.psum_scatter(total, "ffn", scatter_dimension=0, tiled=True)
    for piece in [jnp.concatenate([first, second], axis=0)] + extra:
        grad_features = grad_features + piece.astype(f32)
    grad_w = lax.all_to_all(grad_w, ALL, split_axis=0, concat_axis=0, tiled=True)
    if direct:
        out_up, out_down, out_output, notes = finished(total, up_rows, own)
    else:
        total = total.astype(f32)
        out_up, out_down, out_output = total[:up_rows], total[up_rows:at], total[at : at + own]
        notes = total[at + own : at + own + 8]
    out_bias_up = notes[0]
    out_vecs = lax.dynamic_slice(notes, (1, here * own), (6, own))
    out_query, out_key, out_value, col_sums = unpacked_gradients(
        grad_w.reshape(dp_n, seq_n, ffn_n, own_pad + 8, lanes), own, width
    )
    row = lax.dynamic_index_in_dim(col_sums, here // share, keepdims=False)
    row = jnp.stack([row[heads * PAIR : heads * PAIR + group], row[: heads * PAIR].reshape(heads, 2, HEAD_DIM)[:, 1].reshape(group)])
    out_b = lax.dynamic_slice(row, (0, here % share * own), (2, own))
    return (
        out[None],
        grad_features[None],
        out_query,
        out_key,
        out_value,
        out_output,
        out_b[0],
        out_b[1],
        out_vecs[0],
        out_up,
        out_bias_up,
        out_down,
        out_vecs[1],
        out_vecs[2],
        out_vecs[3],
        out_vecs[4],
        out_vecs[5],
    )


def solution(mesh):
    return jax.shard_map(
        shards,
        mesh=mesh,
        in_specs=(
            P(("dp", "ffn"), "seq", None),
            P(("dp", "seq", "ffn"), None),
            P(("dp", "seq", "ffn"), None),
            P(("dp", "seq", "ffn"), None),
            P(("dp", "seq", "ffn"), None),
            P(("dp", "seq", "ffn")),
            P(("dp", "seq", "ffn")),
            P(("dp", "seq", "ffn")),
            P(("dp", "seq"), "ffn"),
            P("ffn"),
            P(("dp", "seq"), "ffn"),
            P(("dp", "seq", "ffn")),
            P(("dp", "seq", "ffn")),
            P(("dp", "seq", "ffn")),
            P(("dp", "seq", "ffn")),
            P(("dp", "seq", "ffn")),
            P(("dp", "ffn"), None),
            P(("dp", "ffn"), "seq", None, None),
            P(("dp", "ffn"), None),
            P(("dp", "ffn"), "seq", None),
        ),
        out_specs=(
            P(("dp", "ffn"), "seq", None),
            P(("dp", "ffn"), "seq", None),
            P(("dp", "seq", "ffn"), None),
            P(("dp", "seq", "ffn"), None),
            P(("dp", "seq", "ffn"), None),
            P(("dp", "seq", "ffn"), None),
            P(("dp", "seq", "ffn")),
            P(("dp", "seq", "ffn")),
            P(("dp", "seq", "ffn")),
            P(("dp", "seq"), "ffn"),
            P("ffn"),
            P(("dp", "seq"), "ffn"),
            P(("dp", "seq", "ffn")),
            P(("dp", "seq", "ffn")),
            P(("dp", "seq", "ffn")),
            P(("dp", "seq", "ffn")),
            P(("dp", "seq", "ffn")),
        ),
        check_vma=False,
    )
```

```python
import functools
import jax
import jax.numpy as jnp
from jax import lax
from jax.experimental import pallas as pl
from jax.sharding import PartitionSpec as P
from jax.experimental.pallas import tpu as pltpu

HEAD_DIM = 64
BLOCK = 64
PAIR = 2 * BLOCK
MASKED = -1e30
bf16 = jnp.bfloat16
f32 = jnp.float32


def dot_nn(a, b):
    return lax.dot_general(a, b, (((1,), (0,)), ((), ())), preferred_element_type=f32)


def dot_nt(a, b):
    return lax.dot_general(a, b, (((1,), (1,)), ((), ())), preferred_element_type=f32)


def dot_tn(a, b):
    return lax.dot_general(a, b, (((0,), (0,)), ((), ())), preferred_element_type=f32)


def slots(rand_ref, glob_ref, flip, head, pair, nblocks):
    first = (2 * pair) ^ flip

    def row(block):
        return pl.multiple_of(block * BLOCK, BLOCK)

    def near(block):
        bad = (block < 0) | (block >= nblocks) | (block == glob_ref[0, 0]) | (block == glob_ref[0, 1])
        return row(jnp.where(bad, nblocks, block ^ flip))

    def drawn(block):
        at = (head * nblocks + block) * 3
        return [row(rand_ref[at + j] ^ flip) for j in range(3)]

    shared = [near(first), near(first + 1)] + [row(glob_ref[0, j] ^ flip) for j in range(2)]
    return shared, [near(first - 1)] + drawn(first), [near(first + 2)] + drawn(first + 1)


def stack_rows(ref, offsets, lanes):
    return jnp.concatenate([ref[pl.ds(o, BLOCK), lanes] for o in offsets], axis=0)


def lane_halves(width, dtype):
    lane = lax.broadcasted_iota(jnp.int32, (1, width), 1) % PAIR
    first = (lane < BLOCK).astype(dtype)
    second = (lane >= BLOCK).astype(dtype)
    return first, second


UNROLL = 4
BACK_UNROLL = 4
APART = 0
VMEM_BYTES = 62 << 20


def head_lanes(h):
    return slice(h * PAIR, (h + 1) * PAIR)


def query_columns(q_ref, mask_ref, h, at):
    return jnp.concatenate([q_ref[h * BLOCK : (h + 1) * BLOCK, pl.ds(at, PAIR)], mask_ref[:, pl.ds(at, PAIR)]], axis=0)


def global_queries(q_ref, mask_ref, h, gl):
    return jnp.concatenate(
        [
            global_columns(q_ref, slice(h * BLOCK, (h + 1) * BLOCK), gl),
            global_columns(mask_ref, slice(0, BLOCK), gl),
        ],
        axis=0,
    ).astype(bf16)


def placed(me_ref, glob_ref, nblocks, chunks):
    flip = me_ref[0] * (nblocks // chunks)
    return flip, [glob_ref[0, j] ^ flip for j in range(2)]


def global_columns(src_ref, rows, gl):
    lane = lax.broadcasted_iota(jnp.int32, (1, PAIR), 1)
    parts = []
    for g in range(2):
        block = gl[g]
        at = pl.multiple_of((block // 2) * PAIR, PAIR)
        both = src_ref[rows, pl.ds(at, PAIR)].astype(f32)
        moved = pltpu.roll(both, BLOCK, 1)
        parts.append(jnp.where(block % 2 == g, both, moved))
    return jnp.where(lane < BLOCK, parts[0], parts[1])


def put_global_columns(dst_ref, rows, gl, value, per_chunk, low, high):
    lane = lax.broadcasted_iota(jnp.int32, (1, PAIR), 1)
    moved = pltpu.roll(value, BLOCK, 1)
    for g in range(2):
        pair = gl[g] // 2
        half = gl[g] % 2
        chunk = pair // per_chunk

        @pl.when((chunk >= low) & (chunk < high))
        def _():
            at = pl.multiple_of((pair % per_chunk) * PAIR, PAIR)
            src = jnp.where(half == g, value, moved)
            old = dst_ref[chunk - low, rows, pl.ds(at, PAIR)].astype(f32)
            new = jnp.where((lane >= BLOCK) == (half == 1), src, old)
            dst_ref[chunk - low, rows, pl.ds(at, PAIR)] = new.astype(dst_ref.dtype)


def project_rows(x, seg, w_ref, wq, bkv_ref, bq_ref, k_ref, v_ref, q_ref, mask_ref, at):
    n = x.shape[0]
    lanes = v_ref.shape[1]
    y = dot_nn(x, w_ref[:, 0:lanes]) + bkv_ref[...]
    spot = lax.broadcasted_iota(jnp.int32, (PAIR, n), 0) - BLOCK
    mark = jnp.transpose((spot == seg).astype(f32), (1, 0))
    lane = lax.broadcasted_iota(jnp.int32, (1, PAIR), 1)
    rows = pl.ds(at, n)
    v_ref[rows, :] = y.astype(bf16)
    for h in range(lanes // PAIR):
        k_ref[rows, head_lanes(h)] = jnp.where(lane < BLOCK, y[:, head_lanes(h)], mark).astype(bf16)
    z = (dot_nt(wq, x) + bq_ref[...]).astype(bf16)
    q_ref[:, rows] = (z.astype(f32) * HEAD_DIM ** -0.5).astype(bf16)
    row = lax.broadcasted_iota(jnp.int32, (BLOCK, n), 0)
    mask_ref[:, rows] = jnp.where((row <= 16) & (row != seg), MASKED, 0.0).astype(bf16)


def query_weights(w_ref, heads):
    at = heads * PAIR
    cols = w_ref[:, at : at + 2 * PAIR].astype(f32)
    return jnp.transpose(cols, (1, 0))[0 : heads * HEAD_DIM].astype(bf16)


def sparse_forward(heads, low, high, per_chunk, rand_ref, glob_ref, flip, k_ref, kv_ref, q_ref, mask_ref, out_ref, lse_ref):
    nblocks = (k_ref.shape[0] - BLOCK) // BLOCK
    first, second = lane_halves(PAIR, bf16)
    lane = lax.broadcasted_iota(jnp.int32, (1, PAIR), 1)

    def one_pair(spot):
        chunk = spot // per_chunk
        local = pl.multiple_of((spot % per_chunk) * PAIR, PAIR)
        pair = low * per_chunk + spot
        at = pl.multiple_of(pair * PAIR, PAIR)
        for h in range(heads):
            shared, mine, other = slots(rand_ref, glob_ref, flip, h, pair, nblocks)
            kl = head_lanes(h)
            q = query_columns(q_ref, mask_ref, h, at)
            s_sh = dot_nn(stack_rows(k_ref, shared, kl), q)
            k_pr = jnp.concatenate([stack_rows(k_ref, mine, kl), stack_rows(k_ref, other, kl)], axis=1)
            s_pr = dot_nn(k_pr, jnp.concatenate([q * first, q * second], axis=0))
            peak = jnp.maximum(jnp.max(s_sh, axis=0, keepdims=True), jnp.max(s_pr, axis=0, keepdims=True))
            e_sh = jnp.exp(s_sh - peak)
            e_pr = jnp.exp(s_pr - peak)
            total = jnp.sum(e_sh, axis=0, keepdims=True) + jnp.sum(e_pr, axis=0, keepdims=True)
            inv = 1.0 / total
            p_sh = (e_sh * inv).astype(bf16)
            p_pr = (e_pr * inv).astype(bf16)
            v_pr = jnp.concatenate([stack_rows(kv_ref, mine, kl), stack_rows(kv_ref, other, kl)], axis=1)
            o_sh = dot_tn(stack_rows(kv_ref, shared, kl), p_sh)
            o_pr = dot_tn(v_pr, p_pr)
            ctx = o_sh[BLOCK:PAIR] + jnp.where(lane < BLOCK, o_pr[BLOCK:PAIR], o_pr[PAIR + BLOCK : 2 * PAIR])
            out_ref[chunk, h * BLOCK : (h + 1) * BLOCK, pl.ds(local, PAIR)] = ctx.astype(bf16)
            lse_ref[h, pl.ds(spot, 1), :] = peak + jnp.log(total)

    @pl.loop(0, (high - low) * per_chunk // UNROLL)
    def _(some):
        for i in range(UNROLL):
            one_pair(UNROLL * some + i)


def forward_kernel(heads, chunks, me_ref, rand_ref, glob_ref, *refs):
    x_refs = refs[0:chunks]
    seg_ref, w_ref, bkv_ref, bq_ref = refs[chunks : chunks + 4]
    far = chunks // 2
    out_refs = refs[chunks + 4 : chunks + 4 + far]
    lse_ref, lseg_ref, glob_ctx_ref, k_sc, v_sc, q_sc, mask_sc, s_sc, out_ref, seg_sc = refs[chunks + 4 + far :]
    rows = x_refs[0].shape[0]
    length = rows * chunks
    per_chunk = length // PAIR // chunks
    flip, gl = placed(me_ref, glob_ref, length // BLOCK, chunks)
    tile = 256
    wq = query_weights(w_ref, heads)
    for c in range(chunks):
        seg_sc[c : c + 1, :] = seg_ref[pl.ds(me_ref[0] ^ c, 1), :]
    for c in range(chunks):

        @pl.loop(0, rows // tile)
        def _(t):
            at = pl.multiple_of(t * tile, tile)
            project_rows(
                x_refs[c][pl.ds(at, tile), :], seg_sc[c : c + 1, pl.ds(at, tile)], w_ref, wq, bkv_ref, bq_ref,
                k_sc, v_sc, q_sc, mask_sc, pl.multiple_of(c * rows + t * tile, tile),
            )

    null_lane = lax.broadcasted_iota(jnp.int32, (BLOCK, heads * PAIR), 1) % PAIR
    k_sc[pl.ds(length, BLOCK), :] = (null_lane == BLOCK + 16).astype(f32).astype(bf16)
    v_sc[pl.ds(length, BLOCK), :] = jnp.zeros((BLOCK, heads * PAIR), bf16)
    sparse_forward(heads, far, chunks, per_chunk, rand_ref, glob_ref, flip, k_sc, v_sc, q_sc, mask_sc, out_ref, lse_ref)

    step = 512
    queries = [global_queries(q_sc, mask_sc, h, gl) for h in range(heads)]

    def score(c, peaks):
        at = pl.multiple_of(c * step, step)
        new = []
        for h in range(heads):
            got = dot_nn(k_sc[pl.ds(at, step), head_lanes(h)], queries[h])
            s_sc[h, pl.ds(at, step), :] = got
            new.append(jnp.maximum(peaks[h], jnp.max(got, axis=0, keepdims=True)))
        return tuple(new)

    peaks = lax.fori_loop(0, length // step, score, (jnp.full((1, PAIR), MASKED, f32),) * heads)

    def gather(c, carry):
        at = pl.multiple_of(c * step, step)
        new = []
        for h in range(heads):
            total, ctx = carry[h]
            e = jnp.exp(s_sc[h, pl.ds(at, step), :] - peaks[h])
            ctx = ctx + dot_tn(v_sc[pl.ds(at, step), head_lanes(h)], e.astype(bf16))
            new.append((total + jnp.sum(e, axis=0, keepdims=True), ctx))
        return tuple(new)

    start = (jnp.zeros((1, PAIR), f32), jnp.zeros((PAIR, PAIR), f32))
    sums = lax.fori_loop(0, length // step, gather, (start,) * heads)
    for h in range(heads):
        total, ctx = sums[h]
        ctx = ctx[BLOCK:PAIR] * (1.0 / total)
        glob_ctx_ref[h] = ctx
        put_global_columns(out_ref, slice(h * BLOCK, (h + 1) * BLOCK), gl, ctx, per_chunk, far, chunks)
        lseg_ref[h : h + 1, :] = peaks[h] + jnp.log(total)
    for c in range(far):
        out_refs[c][...] = out_ref[c]


def attention_forward(me, rand, glob, x, seg, w, b_kv, b_q):
    chunks = len(x)
    far = chunks // 2
    rows = x[0].shape[0]
    length = rows * chunks
    heads = b_q.shape[0] // HEAD_DIM
    whole = lambda: pl.BlockSpec(memory_space=pltpu.VMEM)
    got = pl.pallas_call(
        functools.partial(forward_kernel, heads, chunks),
        out_shape=(jax.ShapeDtypeStruct((heads * HEAD_DIM, rows), bf16),) * far
        + (
            jax.ShapeDtypeStruct((heads, length // PAIR // 2, PAIR), f32),
            jax.ShapeDtypeStruct((heads, PAIR), f32),
            jax.ShapeDtypeStruct((heads, HEAD_DIM, PAIR), f32),
            jax.ShapeDtypeStruct((length + BLOCK, heads * PAIR), bf16),
            jax.ShapeDtypeStruct((length + BLOCK, heads * PAIR), bf16),
            jax.ShapeDtypeStruct((heads * HEAD_DIM, length), bf16),
            jax.ShapeDtypeStruct((BLOCK, length), bf16),
        ),
        in_specs=[pl.BlockSpec(memory_space=pltpu.SMEM)] * 3 + [whole() for _ in range(chunks + 4)],
        out_specs=tuple(whole() for _ in range(far + 7)),
        scratch_shapes=[
            pltpu.VMEM((heads, length, PAIR), f32),
            pltpu.VMEM((far, heads * HEAD_DIM, rows), bf16),
            pltpu.VMEM((chunks, rows), jnp.int32),
        ],
        compiler_params=pltpu.CompilerParams(vmem_limit_bytes=VMEM_BYTES),
        cost_estimate=pl.CostEstimate(flops=10_000_000_000, bytes_accessed=16_000_000, transcendentals=6_000_000),
        name="attention_forward",
    )(me, rand, glob, *x, seg, w, b_kv, b_q)
    return got[:far], got[far:]


def near_kernel(heads, chunks, me_ref, rand_ref, glob_ref, k_ref, kv_ref, q_ref, mask_ref, glob_ctx_ref, *refs):
    half = chunks // 2
    out_refs = refs[:half]
    lse_ref, out_ref = refs[half:]
    length = q_ref.shape[1]
    per_chunk = length // PAIR // chunks
    flip, gl = placed(me_ref, glob_ref, length // BLOCK, chunks)
    sparse_forward(heads, 0, half, per_chunk, rand_ref, glob_ref, flip, k_ref, kv_ref, q_ref, mask_ref, out_ref, lse_ref)
    for h in range(heads):
        put_global_columns(out_ref, slice(h * BLOCK, (h + 1) * BLOCK), gl, glob_ctx_ref[h], per_chunk, 0, half)
    for c in range(half):
        out_refs[c][...] = out_ref[c]


def attention_near(me, rand, glob, k, kv, q, mask, glob_ctx, chunks):
    heads = glob_ctx.shape[0]
    half = chunks // 2
    length = q.shape[1]
    rows = length // chunks
    whole = lambda: pl.BlockSpec(memory_space=pltpu.VMEM)
    got = pl.pallas_call(
        functools.partial(near_kernel, heads, chunks),
        out_shape=(jax.ShapeDtypeStruct((heads * HEAD_DIM, rows), bf16),) * half
        + (jax.ShapeDtypeStruct((heads, length // PAIR // 2, PAIR), f32),),
        in_specs=[pl.BlockSpec(memory_space=pltpu.SMEM)] * 3 + [whole() for _ in range(5)],
        out_specs=tuple(whole() for _ in range(half + 1)),
        scratch_shapes=[pltpu.VMEM((half, heads * HEAD_DIM, rows), bf16)],
        compiler_params=pltpu.CompilerParams(vmem_limit_bytes=VMEM_BYTES),
        cost_estimate=pl.CostEstimate(flops=6_000_000_000, bytes_accessed=9_000_000, transcendentals=3_000_000),
        name="attention_near",
    )(me, rand, glob, k, kv, q, mask, glob_ctx)
    return got[:half], got[half]


def backward_kernel(heads, chunks, me_ref, rand_ref, glob_ref, *refs):
    do_refs = refs[:chunks]
    (k_ref, kv_ref, q_ref, mask_ref, seg_ref, lse_near_ref, lse_far_ref, lseg_ref, w_ref, resid_ref, dq_ref, dkv_ref,
     first_ref) = refs[chunks : chunks + 13]
    part_refs = refs[chunks + 13 : 2 * chunks + 12]
    do_sc, acc, p_sc, d_sc, seg_sc, line_sc, lse_ref, row_sc = refs[2 * chunks + 12 :]
    rows = do_refs[0].shape[1]
    length = rows * chunks
    npairs = length // PAIR
    per_chunk = npairs // chunks
    scale = HEAD_DIM ** -0.5
    flip, gl = placed(me_ref, glob_ref, length // BLOCK, chunks)
    lse_ref[:, 0 : npairs // 2, :] = lse_near_ref[...]
    lse_ref[:, npairs // 2 :, :] = lse_far_ref[...]
    for c in range(chunks):
        do_sc[:, c * rows : (c + 1) * rows] = do_refs[c][...]
        row_sc[c : c + 1, :] = seg_ref[pl.ds(me_ref[0] ^ c, 1), :].astype(f32)

        @pl.loop(0, per_chunk // 4)
        def _(some):
            for i in range(4):
                t = 4 * some + i
                line = row_sc[c : c + 1, pl.ds(pl.multiple_of(t * PAIR, PAIR), PAIR)]
                line_sc[c * per_chunk + t] = line
                to = pl.multiple_of(c * rows + t * PAIR, PAIR)
                seg_sc[pl.ds(to, PAIR), :] = jnp.transpose(jnp.broadcast_to(line, (PAIR, PAIR)), (1, 0))

    seg_sc[length : length + BLOCK, :] = jnp.full((BLOCK, PAIR), -1.0, f32)
    first2, second2 = lane_halves(2 * PAIR, bf16)
    ffirst, fsecond = lane_halves(PAIR, f32)
    lane = lax.broadcasted_iota(jnp.int32, (1, PAIR), 1)
    line_row = lax.broadcasted_iota(jnp.int32, (PAIR, 1), 0)
    zeros = jnp.zeros((BLOCK, PAIR), bf16)
    blank = jnp.zeros((PAIR, PAIR), bf16)

    def head_rows(h):
        return slice(h * BLOCK, (h + 1) * BLOCK)

    def joint(q, mask, do):
        left = jnp.concatenate([q, mask, blank], axis=0)
        right = jnp.concatenate([blank, zeros, do], axis=0)
        return jnp.concatenate([left, right], axis=1)

    def sources(q, do):
        top = jnp.concatenate([q, zeros], axis=1)
        return jnp.concatenate([top, jnp.concatenate([zeros, do], axis=1)], axis=0)

    step = 512
    mask_glob = global_columns(mask_ref, slice(0, BLOCK), gl).astype(bf16)
    q_glob = [global_columns(q_ref, head_rows(h), gl).astype(bf16) for h in range(heads)]
    do_glob = [global_columns(do_sc, head_rows(h), gl).astype(bf16) for h in range(heads)]

    def weigh(c, deltas):
        at = pl.multiple_of(c * step, step)
        new = []
        for h in range(heads):
            left = jnp.concatenate([k_ref[pl.ds(at, step), head_lanes(h)], kv_ref[pl.ds(at, step), head_lanes(h)]], axis=1)
            both = dot_nn(left, joint(q_glob[h], mask_glob, do_glob[h]))
            p = jnp.exp(both[:, 0:PAIR] - lseg_ref[h : h + 1, :])
            dp = both[:, PAIR:]
            p_sc[h, pl.ds(at, step), :] = p
            d_sc[h, pl.ds(at, step), :] = dp
            new.append(deltas[h] + jnp.sum(p * dp, axis=0, keepdims=True))
        return tuple(new)

    deltas = lax.fori_loop(0, length // step, weigh, (jnp.zeros((1, PAIR), f32),) * heads)

    def spread(c, dqs):
        at = pl.multiple_of(c * step, step)
        new = []
        for h in range(heads):
            p = p_sc[h, pl.ds(at, step), :]
            ds = (p * (d_sc[h, pl.ds(at, step), :] - deltas[h])).astype(bf16)
            both = jnp.concatenate([ds, p.astype(bf16)], axis=1)
            acc[h, pl.ds(at, step), :] = dot_nt(both, sources(q_glob[h], do_glob[h]))
            new.append(dqs[h] + dot_tn(k_ref[pl.ds(at, step), head_lanes(h)], ds))
        return tuple(new)

    dqs = lax.fori_loop(0, length // step, spread, (jnp.zeros((PAIR, PAIR), f32),) * heads)
    for h in range(heads):
        acc[h, pl.ds(length, BLOCK), :] = jnp.zeros((BLOCK, PAIR), f32)

    def one_pair(pair):
        chunk = pair // per_chunk
        local = pl.multiple_of((pair % per_chunk) * PAIR, PAIR)
        at = pl.multiple_of(pair * PAIR, PAIR)
        hit_first = (gl[0] == 2 * pair) | (gl[1] == 2 * pair)
        hit_second = (gl[0] == 2 * pair + 1) | (gl[1] == 2 * pair + 1)
        shut = ffirst * jnp.where(hit_first, -MASKED, 0.0) + fsecond * jnp.where(hit_second, -MASKED, 0.0)
        every = slice(0, PAIR)
        for h in range(heads):
            kl = head_lanes(h)
            shared, mine, other = slots(rand_ref, glob_ref, flip, h, pair, length // BLOCK)
            q = q_ref[head_rows(h), pl.ds(at, PAIR)]
            do = do_sc[head_rows(h), pl.ds(at, PAIR)]
            lse = lse_ref[h, pl.ds(pair, 1), :] + shut
            src = sources(q, do)
            src2 = jnp.concatenate([src * first2, src * second2], axis=0)
            k_sh = stack_rows(k_ref, shared, kl)
            two_sh = dot_nn(
                jnp.concatenate([k_sh, stack_rows(kv_ref, shared, kl)], axis=1),
                joint(q, mask_ref[:, pl.ds(at, PAIR)], do),
            )
            kv_pr = jnp.concatenate([stack_rows(kv_ref, mine, kl), stack_rows(kv_ref, other, kl)], axis=1)
            two_pr = dot_nn(kv_pr, src2)
            seg_pr = jnp.where(lane < BLOCK, stack_rows(seg_sc, mine, every), stack_rows(seg_sc, other, every))
            agree = seg_pr == line_sc[pair]
            p_sh = jnp.exp(two_sh[:, 0:PAIR] - lse)
            p_pr = jnp.where(agree, jnp.exp(two_pr[:, 0:PAIR] - lse), 0.0)
            d_sh, d_pr = two_sh[:, PAIR:], two_pr[:, PAIR:]
            delta = jnp.sum(p_sh * d_sh, axis=0, keepdims=True) + jnp.sum(p_pr * d_pr, axis=0, keepdims=True)
            ds_sh = (p_sh * (d_sh - delta)).astype(bf16)
            ds_pr = (p_pr * (d_pr - delta)).astype(bf16)
            g_sh = dot_nt(jnp.concatenate([ds_sh, p_sh.astype(bf16)], axis=1), src)
            g_pr = dot_nt(jnp.concatenate([ds_pr, p_pr.astype(bf16)], axis=1), src2)
            for j, o in enumerate(shared):
                acc[h, pl.ds(o, BLOCK), :] += g_sh[j * BLOCK : (j + 1) * BLOCK]
            for j, o in enumerate(mine):
                acc[h, pl.ds(o, BLOCK), :] += g_pr[j * BLOCK : (j + 1) * BLOCK, 0:PAIR]
            for j, o in enumerate(other):
                acc[h, pl.ds(o, BLOCK), :] += g_pr[j * BLOCK : (j + 1) * BLOCK, PAIR:]
            t_pr = dot_tn(ds_pr, kv_pr)
            dq = dot_tn(ds_sh, k_sh) + jnp.where(line_row < BLOCK, t_pr[:, 0:PAIR], t_pr[:, PAIR:])
            dq = jnp.transpose(dq, (1, 0))[0:BLOCK]
            dq_ref[chunk, head_rows(h), pl.ds(local, PAIR)] = (dq * scale).astype(bf16)

    @pl.loop(0, npairs // BACK_UNROLL)
    def _(some):
        for i in range(BACK_UNROLL):
            one_pair(BACK_UNROLL * some + i)

    for h in range(heads):
        put_global_columns(dq_ref, head_rows(h), gl, dqs[h][0:BLOCK] * scale, per_chunk, 0, chunks)
        for c in range(chunks):
            dkv_ref[c, :, head_lanes(h)] = acc[h, pl.ds(c * rows, rows), :].astype(bf16)
    tile = 256
    wq = query_weights(w_ref, heads)
    for c in range(chunks):

        @pl.loop(0, rows // tile)
        def _(t):
            at = pl.multiple_of(t * tile, tile)
            got = dot_tn(dq_ref[c, :, pl.ds(at, tile)], wq)
            got = got + dot_nt(dkv_ref[c, pl.ds(at, tile), :], w_ref[:, 0 : heads * PAIR])
            if c == 0:
                first_ref[pl.ds(at, tile), :] = resid_ref[pl.ds(at, tile), :] + got
            else:
                part_refs[c - 1][pl.ds(at, tile), :] = got.astype(bf16)


def attention_backward(me, rand, glob, do, k, kv, q, mask, seg, lse_near, lse_far, lseg, w, resid):
    chunks = len(do)
    group, rows = do[0].shape
    heads = group // HEAD_DIM
    width = w.shape[0]
    length = rows * chunks
    whole = lambda: pl.BlockSpec(memory_space=pltpu.VMEM)
    return pl.pallas_call(
        functools.partial(backward_kernel, heads, chunks),
        out_shape=(
            jax.ShapeDtypeStruct((chunks, group, rows), bf16),
            jax.ShapeDtypeStruct((chunks, rows, heads * PAIR), bf16),
            jax.ShapeDtypeStruct((rows, width), f32),
        )
        + (jax.ShapeDtypeStruct((rows, width), bf16),) * (chunks - 1),
        in_specs=[pl.BlockSpec(memory_space=pltpu.SMEM)] * 3 + [whole() for _ in range(chunks + 10)],
        out_specs=tuple(whole() for _ in range(chunks + 2)),
        scratch_shapes=[
            pltpu.VMEM((group, length), bf16),
            pltpu.VMEM((heads, length + BLOCK, PAIR), f32),
            pltpu.VMEM((heads, length, PAIR), f32),
            pltpu.VMEM((heads, length, PAIR), f32),
            pltpu.VMEM((length + BLOCK, PAIR), f32),
            pltpu.VMEM((length // PAIR, 1, PAIR), f32),
            pltpu.VMEM((heads, length // PAIR, PAIR), f32),
            pltpu.VMEM((chunks, rows), f32),
        ],
        compiler_params=pltpu.CompilerParams(vmem_limit_bytes=VMEM_BYTES),
        cost_estimate=pl.CostEstimate(flops=30_000_000_000, bytes_accessed=24_000_000, transcendentals=8_000_000),
        name="attention_backward",
    )(me, rand, glob, *do, k, kv, q, mask, seg, lse_near, lse_far, lseg, w, resid)


def round_up(value, to):
    return -(-value // to) * to


def half_columns(ref, index, place):
    at = index // 2 * PAIR
    both = ref[:, at : at + PAIR].astype(f32)
    return both if index % 2 == place else pltpu.roll(both, BLOCK, 1)


def two_halves(first, second):
    lane = lax.broadcasted_iota(jnp.int32, (1, PAIR), 1)
    return jnp.where(lane < BLOCK, first, second)


def pack_kernel(seq_n, wq_ref, wk_ref, wv_ref, wo_ref, up_ref, down_ref, bup_ref, vec_ref, pack_ref, rest_ref):
    own, width = wq_ref.shape
    heads = width // HEAD_DIM // seq_n
    blocks, inner = pack_ref.shape[0], pack_ref.shape[2]
    for s in range(seq_n):
        pieces = [
            two_halves(half_columns(wk_ref, s * heads + h, 0), half_columns(wv_ref, s * heads + h, 1))
            for h in range(heads)
        ]
        for h in range(0, heads, 2):
            second = half_columns(wq_ref, s * heads + h + 1, 1) if h + 1 < heads else vec_ref[...].astype(f32)
            pieces.append(two_halves(half_columns(wq_ref, s * heads + h, 0), second))
        piece = jnp.concatenate(pieces, axis=1).astype(bf16)
        for b in range(blocks):
            for i in range(inner):
                pack_ref[b, s, i] = piece
    u = up_ref.shape[0]
    rest_ref[0:u, :] = up_ref[...]
    rest_ref[u : 2 * u, :] = down_ref[...]
    rest_ref[2 * u : 2 * u + own, :] = wo_ref[...]
    rest_ref[2 * u + own : 2 * u + own + 8, :] = jnp.broadcast_to(bup_ref[...], (8, width))


def packed_weights(w_q, w_k, w_v, w_o, w_up, w_down, b_up, vec, dp_n, seq_n, ffn_n):
    own, width = w_q.shape
    heads = width // HEAD_DIM // seq_n
    lanes = heads * PAIR + round_up(heads * HEAD_DIM, PAIR)
    u = w_up.shape[0]
    if own % 8 or u % 16:
        group = heads * HEAD_DIM
        cols = lambda w: w.reshape(own, seq_n, heads, HEAD_DIM).transpose(1, 0, 2, 3)
        kv = jnp.stack([cols(w_k), cols(w_v)], axis=3).reshape(seq_n, own, 2 * group)
        notes = jnp.broadcast_to(vec[None, :, HEAD_DIM:], (seq_n, own, PAIR - HEAD_DIM))
        piece = jnp.concatenate([kv, cols(w_q).reshape(seq_n, own, group), notes], axis=2)
        piece = jnp.pad(piece, ((0, 0), (0, round_up(own, 8) - own), (0, 0)))
        pack = jnp.broadcast_to(piece[None, :, None], (dp_n, seq_n, ffn_n) + piece.shape[1:])
        w_o = jnp.pad(w_o, ((0, round_up(own, 8) - own), (0, 0)))
        return pack, jnp.concatenate([w_up, w_down, w_o, jnp.broadcast_to(b_up, (8, width))], axis=0)
    whole = lambda: pl.BlockSpec(memory_space=pltpu.VMEM)
    return pl.pallas_call(
        functools.partial(pack_kernel, seq_n),
        out_shape=(
            jax.ShapeDtypeStruct((dp_n, seq_n, ffn_n, own, lanes), bf16),
            jax.ShapeDtypeStruct((2 * u + own + 8, width), bf16),
        ),
        in_specs=[whole() for _ in range(8)],
        out_specs=(whole(), whole()),
        name="packed_weights",
    )(w_q, w_k, w_v, w_o, w_up, w_down, b_up, vec)


def weights_kernel(chunks, direct, *refs):
    x_refs = refs[:chunks]
    dq_ref, dkv_ref, out_ref, acc, sum_sc = refs[chunks:]
    group = dq_ref.shape[1]
    lanes = dkv_ref.shape[2]
    full, width = acc.shape
    x = jnp.concatenate([r[...] for r in x_refs], axis=0)
    dkv = jnp.concatenate([dkv_ref[c] for c in range(chunks)], axis=0)
    dq = jnp.concatenate([dq_ref[c] for c in range(chunks)], axis=1)
    ones = jnp.ones((8, x.shape[0]), bf16)

    @pl.when(pl.program_id(0) == 0)
    def _():
        acc[...] = jnp.zeros_like(acc)
        sum_sc[...] = jnp.zeros_like(sum_sc)

    acc[0:lanes, :] += dot_tn(dkv, x)
    acc[lanes : lanes + group, :] += dot_nn(dq, x)
    sum_sc[:, 0:lanes] += dot_nn(ones, dkv)
    sum_sc[:, lanes : lanes + group] += dot_nt(ones, dq)

    @pl.when(pl.program_id(0) == pl.num_programs(0) - 1)
    def _():
        lane = lax.broadcasted_iota(jnp.int32, (full, width), 0)
        spot = lax.broadcasted_iota(jnp.int32, (full, width), 1) % group
        pick_q = lane - lanes == spot
        pick_v = (lane < lanes) & (lane % PAIR >= BLOCK) & (lane // PAIR * BLOCK + lane % BLOCK == spot)
        sums = sum_sc[...].astype(bf16)
        row = lax.broadcasted_iota(jnp.int32, (8, width), 0)
        of_q = dot_nn(sums, pick_q.astype(f32).astype(bf16))
        of_v = dot_nn(sums, pick_v.astype(f32).astype(bf16))
        acc[lanes + group : lanes + group + 8, :] = jnp.where(row == 0, of_q, of_v)
        grad = jnp.transpose(acc[...], (1, 0))
        if direct:
            blocks, own, _ = out_ref.shape
            grad = grad.reshape(blocks, own, full)
            for b in range(blocks):
                out_ref[b] = grad[b].astype(bf16)
        else:
            out_ref[...] = grad.astype(bf16)


def projection_gradients(x, dq, dkv, own, devices):
    chunks, group, rows = dq.shape
    width = x[0].shape[1]
    lanes = dkv.shape[2]
    full = lanes + round_up(group, PAIR)
    direct = own % 8 == 0
    tile = 256
    shape = (devices, own, full) if direct else (width, full)
    out = pl.pallas_call(
        functools.partial(weights_kernel, chunks, direct),
        grid=(rows // tile,),
        out_shape=jax.ShapeDtypeStruct(shape, bf16),
        in_specs=[pl.BlockSpec((tile, width), lambda i: (i, 0)) for _ in range(chunks)]
        + [
            pl.BlockSpec((chunks, group, tile), lambda i: (0, 0, i)),
            pl.BlockSpec((chunks, tile, lanes), lambda i: (0, i, 0)),
        ],
        out_specs=pl.BlockSpec(shape, lambda i: (0,) * len(shape), pipeline_mode=pl.Buffered(1)),
        scratch_shapes=[pltpu.VMEM((full, width), f32), pltpu.VMEM((8, full), f32)],
        compiler_params=pltpu.CompilerParams(vmem_limit_bytes=VMEM_BYTES),
        cost_estimate=pl.CostEstimate(flops=4_000_000_000, bytes_accessed=12_000_000, transcendentals=0),
        name="projection_gradients",
    )(*x, dq, dkv)
    if not direct:
        out = jnp.pad(out.reshape(devices, own, full), ((0, 0), (0, round_up(own, 8) - own), (0, 0)))
    return out


def unpack_kernel(own, got_ref, q_ref, k_ref, v_ref, sums_ref, tot):
    dp_n, seq_n, ffn_n, per, full = got_ref.shape
    width = q_ref.shape[1]
    heads = width // HEAD_DIM // seq_n
    for s in range(seq_n):
        total = jnp.zeros((per, full), f32)
        for d in range(dp_n):
            for f in range(ffn_n):
                total = total + got_ref[d, s, f].astype(f32)
        tot[s] = total
        sums_ref[s] = total[:, full - PAIR :]
    for w in range(width // PAIR):
        spots = [((2 * w + i) // heads, (2 * w + i) % heads) for i in range(2)]
        cols = slice(w * PAIR, (w + 1) * PAIR)
        for ref, where in (
            (k_ref, lambda h: 2 * h),
            (v_ref, lambda h: 2 * h + 1),
            (q_ref, lambda h: 2 * heads + h),
        ):
            both = [half_columns(tot.at[g], where(h), i) for i, (g, h) in enumerate(spots)]
            ref[:, cols] = two_halves(*both)[0:own]


def unpacked_gradients(got, own, width):
    dp_n, seq_n, ffn_n, per, full = got.shape
    whole = lambda: pl.BlockSpec(memory_space=pltpu.VMEM)
    return pl.pallas_call(
        functools.partial(unpack_kernel, own),
        out_shape=(jax.ShapeDtypeStruct((own, width), f32),) * 3 + (jax.ShapeDtypeStruct((seq_n, per, PAIR), f32),),
        in_specs=[whole()],
        out_specs=tuple(whole() for _ in range(4)),
        scratch_shapes=[pltpu.VMEM((seq_n, per, full), f32)],
        compiler_params=pltpu.CompilerParams(vmem_limit_bytes=VMEM_BYTES),
        name="unpacked_gradients",
    )(got)


NORM_EPS = 1e-12


def transposed(value):
    return jnp.transpose(value.astype(f32), (1, 0)).astype(bf16)


def unit_rows(value):
    center = value - jnp.mean(value, axis=-1, keepdims=True)
    scale = lax.rsqrt(jnp.mean(center * center, axis=-1, keepdims=True) + NORM_EPS)
    return center * scale, scale


def unit_rows_back(grad, unit, scale):
    return scale * (
        grad - jnp.mean(grad, axis=-1, keepdims=True) - unit * jnp.mean(grad * unit, axis=-1, keepdims=True)
    )


def rows_kernel(parts, blocks, up_rows, own, me_ref, *refs):
    ctx_refs = refs[:parts]
    (x_ref, cot_ref, rest_ref, wo_ref, vec_ref, bup_ref, out_ref, resid_ref, hid_ref, pre_ref, nlt_ref, gft_ref,
     gb_ref) = refs[parts : parts + 13]
    do_refs = refs[parts + 13 : 2 * parts + 13]
    sums_ref, gbup_ref, slope_sc, wo_sc, wide_sc = refs[2 * parts + 13 :]
    group = ctx_refs[0].shape[0]
    width = x_ref.shape[1]

    def up(f):
        return rest_ref[:, f, 0:up_rows, :].reshape(width, rest_ref.shape[3])

    def down(f):
        return rest_ref[:, f, up_rows : 2 * up_rows, :].reshape(width, rest_ref.shape[3])

    def own_rows(k):
        return pl.ds(pl.multiple_of((me_ref[0] ^ k) * group, group), group)

    @pl.when(pl.program_id(0) == 0)
    def _():
        sums_ref[...] = jnp.zeros_like(sums_ref)
        gbup_ref[...] = jnp.zeros_like(gbup_ref)
        if own:
            for o in range(rest_ref.shape[0]):
                for f in range(blocks):
                    to = (o * blocks + f) * own
                    wide_sc[to : to + own, :] = rest_ref[o, f, 2 * up_rows : 2 * up_rows + own, :].astype(f32)
            wo_sc[...] = wide_sc[...].astype(bf16)
        else:
            wo_sc[...] = wo_ref[...]

    def bias_up(f):
        if own:
            row = rest_ref[0, f, 2 * up_rows + own : 2 * up_rows + own + 8, :].astype(f32)
            return row[7:8, :]
        return bup_ref[f : f + 1, :]

    ctx = jnp.concatenate([r[...] for r in ctx_refs], axis=0)
    w_o = jnp.concatenate([wo_sc[own_rows(k), :] for k in range(parts)], axis=0)
    resid_one = x_ref[...].astype(f32) + (dot_tn(ctx, w_o) + vec_ref[0:1, :])
    unit_one, scale_one = unit_rows(resid_one)
    normed_one = unit_one * vec_ref[2:3, :] + vec_ref[3:4, :]
    low = normed_one.astype(bf16)
    nlt_ref[...] = transposed(normed_one)
    total = normed_one + vec_ref[1:2, :]
    pre = dot_nn(low, up(0)) + bias_up(0)
    for f in range(blocks):
        later = dot_nn(low, up(f + 1)) + bias_up(f + 1) if f + 1 < blocks else None
        phi = 0.5 + 0.5 * lax.erf(pre * (0.5 ** 0.5))
        slope_sc[f] = phi + pre * (jnp.exp(-0.5 * pre * pre) * 0.3989422804014327)
        hid = (pre * phi).astype(bf16)
        hid_ref[f] = hid
        total = total + dot_nt(hid, down(f))
        pre = later
    unit_two, scale_two = unit_rows(total)
    out_ref[...] = (unit_two * vec_ref[4:5, :] + vec_ref[5:6, :]).astype(bf16)
    cot = cot_ref[...].astype(f32)
    grad_two = unit_rows_back(cot * vec_ref[4:5, :], unit_two, scale_two)
    grad_ffn = grad_two.astype(bf16)
    gft_ref[...] = transposed(grad_two)
    grad_normed = grad_two
    back = dot_nn(grad_ffn, down(0))
    for f in range(blocks):
        later = dot_nn(grad_ffn, down(f + 1)) if f + 1 < blocks else None
        grad_pre = (back * slope_sc[f]).astype(bf16)
        pre_ref[f] = grad_pre
        gbup_ref[f : f + 1, :] += jnp.sum(grad_pre.astype(f32), axis=0, keepdims=True)
        grad_normed = grad_normed + dot_nt(grad_pre, up(f))
        back = later
    resid = unit_rows_back(grad_normed * vec_ref[2:3, :], unit_one, scale_one)
    resid_ref[...] = resid
    branch = resid.astype(bf16)
    gb_ref[...] = branch
    do = dot_nt(w_o, branch).astype(bf16)
    for k in range(parts):
        do_refs[k][...] = do[k * group : (k + 1) * group]
    for row, value in enumerate(
        (branch.astype(f32), grad_ffn.astype(f32), grad_normed * unit_one, grad_normed, cot * unit_two, cot)
    ):
        sums_ref[row : row + 1, :] += jnp.sum(value, axis=0, keepdims=True)


def rows_chain(me, ctx_parts, x, cot, rest, up_rows, own, w_o, vecs, bias_up):
    parts = len(ctx_parts)
    group, rows = ctx_parts[0].shape
    width = x.shape[1]
    outer, blocks, per, hidden = rest.shape
    tile = 256
    once = lambda shape: pl.BlockSpec(shape, lambda i: (0,) * len(shape), pipeline_mode=pl.Buffered(1))
    tall = pl.BlockSpec((tile, width), lambda i: (i, 0))
    wide = pl.BlockSpec((width, tile), lambda i: (0, i))
    cube = pl.BlockSpec((blocks, tile, hidden), lambda i: (0, i, 0))
    return pl.pallas_call(
        functools.partial(rows_kernel, parts, blocks, up_rows, own),
        grid=(rows // tile,),
        out_shape=(
            jax.ShapeDtypeStruct((rows, width), bf16),
            jax.ShapeDtypeStruct((rows, width), f32),
            jax.ShapeDtypeStruct((blocks, rows, hidden), bf16),
            jax.ShapeDtypeStruct((blocks, rows, hidden), bf16),
            jax.ShapeDtypeStruct((width, rows), bf16),
            jax.ShapeDtypeStruct((width, rows), bf16),
            jax.ShapeDtypeStruct((rows, width), bf16),
        )
        + (jax.ShapeDtypeStruct((group, rows), bf16),) * parts
        + (jax.ShapeDtypeStruct((8, width), f32), jax.ShapeDtypeStruct((8, hidden), f32)),
        in_specs=[pl.BlockSpec(memory_space=pltpu.SMEM)]
        + [pl.BlockSpec((group, tile), lambda i: (0, i))] * parts
        + [tall, tall, once(rest.shape), once(w_o.shape), once(vecs.shape), once(bias_up.shape)],
        out_specs=(
            tall, tall, cube, cube, wide, wide, tall,
        )
        + (pl.BlockSpec((group, tile), lambda i: (0, i)),) * parts
        + (pl.BlockSpec((8, width), lambda i: (0, 0)), pl.BlockSpec((8, hidden), lambda i: (0, 0))),
        scratch_shapes=[
            pltpu.VMEM((blocks, tile, hidden), f32),
            pltpu.VMEM((width, width), bf16),
            pltpu.VMEM((width, width), f32),
        ],
        compiler_params=pltpu.CompilerParams(vmem_limit_bytes=VMEM_BYTES),
        cost_estimate=pl.CostEstimate(flops=22_000_000_000, bytes_accessed=40_000_000, transcendentals=6_000_000),
        name="rows_chain",
    )(me, *ctx_parts, x, cot, rest, w_o, vecs, bias_up)


def outer_kernel(parts, up_rows, own, apart, me_ref, *refs):
    ctx_refs = refs[:parts]
    nlt_ref, gft_ref, gb_ref, pre_ref, hid_ref, sums_ref, gbup_ref, out_ref = refs[parts : parts + 8]
    wo_sc = refs[-1]
    slabs, hidden = out_ref.shape[0], out_ref.shape[3]
    group = ctx_refs[0].shape[0]
    f = pl.program_id(0)
    up = dot_nn(nlt_ref[...], pre_ref[0]).astype(bf16).reshape(slabs, up_rows, hidden)
    if apart:
        refs[parts + 8][:, 0, :, :] = up[:, 0:apart]
    out_ref[:, 0, 0 : up_rows - apart, :] = up[:, apart:]
    at = up_rows - apart
    down = dot_nn(gft_ref[...], hid_ref[0]).astype(bf16)
    out_ref[:, 0, at : at + up_rows, :] = down.reshape(slabs, up_rows, hidden)
    at += up_rows
    if not own:
        return

    @pl.when(f == 0)
    def _():
        for k in range(parts):
            wo_sc[k] = dot_nn(ctx_refs[k][...], gb_ref[...])

    share = slabs // parts
    stride = group // share
    for k in range(parts):
        for j in range(share):
            rows = pl.ds(pl.multiple_of(j * stride + f * own, 8), own)
            out_ref[(me_ref[0] ^ k) * share + j, 0, at : at + own, :] = wo_sc[k, rows, :].astype(bf16)
    small = jnp.concatenate([gbup_ref[pl.ds(f, 1), :], sums_ref[0:7, :]], axis=0).astype(bf16)
    for o in range(slabs):
        out_ref[o, 0, at + own :, :] = small


def outer_products(me, ctx_parts, nlt, gft, gb, pre, hid, sums, gbup, slabs, up_rows, own, apart):
    blocks, rows, hidden = pre.shape
    parts = len(ctx_parts)
    group = ctx_parts[0].shape[0]
    per = 2 * up_rows - apart + (own + 8 if own else 0)
    sizes = (per, apart) if apart else (per,)
    once = lambda shape: pl.BlockSpec(shape, lambda i: (0,) * len(shape), pipeline_mode=pl.Buffered(1))
    return pl.pallas_call(
        functools.partial(outer_kernel, parts, up_rows, own, apart),
        grid=(blocks,),
        out_shape=tuple(jax.ShapeDtypeStruct((slabs, blocks, r, hidden), bf16) for r in sizes),
        in_specs=[pl.BlockSpec(memory_space=pltpu.SMEM)]
        + [once(c.shape) for c in ctx_parts]
        + [
            once(nlt.shape),
            once(gft.shape),
            once(gb.shape),
            pl.BlockSpec((1, rows, hidden), lambda i: (i, 0, 0)),
            pl.BlockSpec((1, rows, hidden), lambda i: (i, 0, 0)),
            once(sums.shape),
            once(gbup.shape),
        ],
        out_specs=tuple(pl.BlockSpec((slabs, 1, r, hidden), lambda i: (0, i, 0, 0)) for r in sizes),
        scratch_shapes=[pltpu.VMEM((parts, group, gb.shape[1]), f32)],
        compiler_params=pltpu.CompilerParams(vmem_limit_bytes=VMEM_BYTES),
        cost_estimate=pl.CostEstimate(flops=11_000_000_000, bytes_accessed=28_000_000, transcendentals=0),
        name="outer_products",
    )(me, *ctx_parts, nlt, gft, gb, pre, hid, sums, gbup)


def finish_kernel(up_rows, own, total_ref, up_ref, down_ref, wo_ref, small_ref):
    rest = total_ref[...].astype(f32)
    up_ref[...] = rest[0:up_rows]
    down_ref[...] = rest[up_rows : 2 * up_rows]
    at = 2 * up_rows
    wo_ref[...] = rest[at : at + own]
    small_ref[...] = rest[at + own : at + own + 8]


def finished(total, up_rows, own):
    hidden = total.shape[1]
    whole = lambda: pl.BlockSpec(memory_space=pltpu.VMEM)
    return pl.pallas_call(
        functools.partial(finish_kernel, up_rows, own),
        out_shape=tuple(jax.ShapeDtypeStruct((r, hidden), f32) for r in (up_rows, up_rows, own, 8)),
        in_specs=[whole()],
        out_specs=tuple(whole() for _ in range(4)),
        name="finished",
    )(total)


ALL = ("dp", "seq", "ffn")


def flip_send(array, axis, bits):
    count = lax.axis_size(axis)
    return lax.ppermute(array, axis, [(i, i ^ bits) for i in range(count)])


def shards(
    tokens, w_query, w_key, w_value, w_output, b_query, b_value, b_output, w_up, b_up, w_down, b_down,
    gain_attn, shift_attn, gain_ffn, shift_ffn, segment_ids, random_blocks, global_blocks, cotangent,
):
    seq_n, dp_n, ffn_n = lax.axis_size("seq"), lax.axis_size("dp"), lax.axis_size("ffn")
    outer, devices = dp_n * seq_n, dp_n * seq_n * ffn_n
    me = lax.axis_index("seq")
    here = (lax.axis_index("dp") * seq_n + me) * ffn_n + lax.axis_index("ffn")
    own, width = w_query.shape
    own_pad = round_up(own, 8)
    group = width // seq_n
    heads = group // HEAD_DIM
    features = tokens[0]
    rows = features.shape[0]
    order = jnp.stack([me ^ k for k in range(seq_n)])
    me_ref = me.astype(jnp.int32)[None]

    near = [features] + [None] * (seq_n - 1)
    for k in sorted(range(1, seq_n), key=lambda k: (k & (k - 1), -k)):
        bit = k & -k
        near[k] = flip_send(features if bit == k else near[k ^ bit], "seq", bit)

    vec = jnp.stack([b_output, b_down, gain_attn, shift_attn, gain_ffn, shift_ffn, b_query, b_value], axis=1)
    vec = jnp.pad(vec, ((0, 0), (HEAD_DIM, PAIR - HEAD_DIM - 8)))
    seg = segment_ids[0].reshape(seq_n, rows)
    rand = random_blocks.reshape(-1)
    pack, rest = packed_weights(
        w_query, w_key, w_value, w_output, w_up, w_down, b_up[None], vec, dp_n, seq_n, ffn_n
    )
    lanes = pack.shape[4]
    pack, seg, rand = lax.optimization_barrier((pack, seg, rand))
    pack = lax.all_to_all(
        pack.reshape(devices, own_pad, lanes), ALL, split_axis=0, concat_axis=0, tiled=True
    )
    rest = lax.all_gather(rest, ALL, axis=0, tiled=False)
    w_own = pack[:, :own].reshape(width, lanes)
    share = devices // seq_n
    vecs = w_own[:, lanes - HEAD_DIM : lanes - HEAD_DIM + 8].astype(f32).T
    biases = lax.dynamic_slice(vecs, (6, me * group), (2, group))
    by_head = biases[1].reshape(heads, 1, HEAD_DIM)
    b_kv = jnp.concatenate([jnp.zeros_like(by_head), by_head], axis=1).reshape(1, heads * PAIR)

    far = seq_n // 2
    ctx_far, (lse_far, lseg, glob_ctx, k_all, v_all, q_all, mask_all) = attention_forward(
        me_ref, rand, global_blocks, near, seg, w_own, b_kv, biases[0][:, None]
    )
    ctx_parts = [None] * far + [flip_send(ctx_far[k - far], "seq", k) for k in range(far, seq_n)]
    ctx_near, lse_near = attention_near(
        me_ref, rand, global_blocks, k_all, v_all, q_all, mask_all, glob_ctx, seq_n
    )
    ctx_parts[far:], ctx_parts[0] = lax.optimization_barrier((ctx_parts[far:], ctx_near[0]))
    for k in range(1, far):
        ctx_parts[k] = flip_send(ctx_near[k], "seq", k)

    up_rows = w_up.shape[0]
    at = 2 * up_rows
    rest = rest.reshape(outer, ffn_n, rest.shape[1], width)
    w_o = rest[:, :, at : at + own].reshape(width, width)
    bias_up = rest[0, :, at + own_pad + 7].astype(f32)
    direct = up_rows % 16 == 0 and own % 8 == 0 and outer % seq_n == 0 and (outer // seq_n) * ffn_n * own == group
    if not direct:
        rest = rest[:, :, :at].reshape(outer, ffn_n, 2, up_rows, width).transpose(1, 2, 0, 3, 4)
        rest = rest.reshape(1, ffn_n, 2 * outer * up_rows, width)
    slabs, slab_rows = (outer, up_rows) if direct else (1, outer * up_rows)

    got = rows_chain(
        me_ref, ctx_parts, features, cotangent[0], rest, slab_rows, own if direct else 0,
        jnp.zeros((8, PAIR), bf16) if direct else w_o, vecs, jnp.zeros((8, PAIR), f32) if direct else bias_up,
    )
    out, grad_resid_one, hidden, grad_pre, normed_t, grad_ffn_t, grad_branch = got[:7]
    grad_ctx, (sums, grad_bias_up) = got[7 : 7 + seq_n], got[7 + seq_n :]
    do = [grad_ctx[0]] + [flip_send(grad_ctx[k], "seq", k) for k in range(1, seq_n)]

    payload = outer_products(
        me_ref, ctx_parts, normed_t, grad_ffn_t, grad_branch, grad_pre, hidden, sums, grad_bias_up, slabs, slab_rows,
        own if direct else 0, APART if direct else 0,
    )
    payload, apart = payload if direct and APART else (payload[0], None)
    if not direct:
        grad_out = dot_nn(jnp.concatenate(ctx_parts, axis=0), grad_branch).astype(bf16)
        grad_out = grad_out.reshape(seq_n, group, width)[order].reshape(outer, ffn_n, own, width)
        top = jnp.broadcast_to(grad_bias_up[None, :ffn_n, None], (outer, ffn_n, 1, width))
        small = jnp.concatenate([top, jnp.broadcast_to(sums[None, None, :7], (outer, ffn_n, 7, width))], axis=2)
        small = small.astype(bf16)
        payload = payload.reshape(ffn_n, 2, outer, up_rows, width).transpose(2, 0, 1, 3, 4)
        payload = jnp.concatenate([payload.reshape(outer, ffn_n, at, width), grad_out, small], axis=2)
        payload = jnp.pad(payload, ((0, 0), (0, 0), (0, -payload.shape[2] % 32), (0, 0)))
    payload, apart, do = lax.optimization_barrier((payload, apart, do))
    total = lax.psum_scatter(payload.reshape(-1, width), ("dp", "seq"), scatter_dimension=0, tiled=True)
    if apart is not None:
        apart = lax.all_to_all(
            apart.reshape(devices, APART, width), ALL, split_axis=0, concat_axis=0, tiled=True
        )

    got = attention_backward(
        me_ref, rand, global_blocks, do, k_all, v_all, q_all, mask_all, seg, lse_near, lse_far, lseg, w_own,
        grad_resid_one,
    )
    dq, dkv, grad_features = got[:3]
    part = [None] + list(got[3:])
    bit = 1
    while bit < seq_n:
        for k in range(seq_n):
            if k & -k == bit and k != bit:
                came = flip_send(part[k], "seq", bit).astype(f32)
                part[k ^ bit] = (part[k ^ bit].astype(f32) + came).astype(bf16)
        bit *= 2
    grad_w = projection_gradients(near, dq, dkv, own, devices)
    grad_w, part = lax.optimization_barrier((grad_w, part[1:]))
    grad_w, apart = lax.optimization_barrier((grad_w, apart))
    part = [None] + part
    bit = seq_n // 2
    first = flip_send(part[bit][: rows // 8], "seq", bit)
    first, total = lax.optimization_barrier((first, total))
    total = lax.psum_scatter(total, "ffn", scatter_dimension=0, tiled=True)
    second = flip_send(part[bit][rows // 8 :], "seq", bit)
    grad_features = grad_features + jnp.concatenate([first, second], axis=0).astype(f32)
    bit //= 2
    while bit:
        grad_features = grad_features + flip_send(part[bit], "seq", bit).astype(f32)
        bit //= 2
    grad_w = lax.all_to_all(grad_w, ALL, split_axis=0, concat_axis=0, tiled=True)
    if direct:
        out_up, out_down, out_output, notes = finished(total, up_rows, own)
    else:
        total = total.astype(f32)
        out_up, out_down, out_output = total[:up_rows], total[up_rows:at], total[at : at + own]
        notes = total[at + own : at + own + 8]
    out_bias_up = notes[0]
    out_vecs = lax.dynamic_slice(notes, (1, here * own), (6, own))
    out_query, out_key, out_value, col_sums = unpacked_gradients(
        grad_w.reshape(dp_n, seq_n, ffn_n, own_pad, lanes), own, width
    )
    col = lax.dynamic_index_in_dim(col_sums, here // share, keepdims=False)[:own, HEAD_DIM : HEAD_DIM + 2]
    out_b = [col[:, 0], col[:, 1]]
    return (
        out[None],
        grad_features[None],
        out_query,
        out_key,
        out_value,
        out_output,
        out_b[0],
        out_b[1],
        out_vecs[0],
        out_up,
        out_bias_up,
        out_down,
        out_vecs[1],
        out_vecs[2],
        out_vecs[3],
        out_vecs[4],
        out_vecs[5],
    )


def solution(mesh):
    return jax.shard_map(
        shards,
        mesh=mesh,
        in_specs=(
            P(("dp", "ffn"), "seq", None),
            P(("dp", "seq", "ffn"), None),
            P(("dp", "seq", "ffn"), None),
            P(("dp", "seq", "ffn"), None),
            P(("dp", "seq", "ffn"), None),
            P(("dp", "seq", "ffn")),
            P(("dp", "seq", "ffn")),
            P(("dp", "seq", "ffn")),
            P(("dp", "seq"), "ffn"),
            P("ffn"),
            P(("dp", "seq"), "ffn"),
            P(("dp", "seq", "ffn")),
            P(("dp", "seq", "ffn")),
            P(("dp", "seq", "ffn")),
            P(("dp", "seq", "ffn")),
            P(("dp", "seq", "ffn")),
            P(("dp", "ffn"), None),
            P(("dp", "ffn"), "seq", None, None),
            P(("dp", "ffn"), None),
            P(("dp", "ffn"), "seq", None),
        ),
        out_specs=(
            P(("dp", "ffn"), "seq", None),
            P(("dp", "ffn"), "seq", None),
            P(("dp", "seq", "ffn"), None),
            P(("dp", "seq", "ffn"), None),
            P(("dp", "seq", "ffn"), None),
            P(("dp", "seq", "ffn"), None),
            P(("dp", "seq", "ffn")),
            P(("dp", "seq", "ffn")),
            P(("dp", "seq", "ffn")),
            P(("dp", "seq"), "ffn"),
            P("ffn"),
            P(("dp", "seq"), "ffn"),
            P(("dp", "seq", "ffn")),
            P(("dp", "seq", "ffn")),
            P(("dp", "seq", "ffn")),
            P(("dp", "seq", "ffn")),
            P(("dp", "seq", "ffn")),
        ),
        check_vma=False,
    )
```

```python
import functools
import jax
import jax.numpy as jnp
from jax import lax
from jax.experimental import pallas as pl
from jax.sharding import PartitionSpec as P
from jax.experimental.pallas import tpu as pltpu

HEAD_DIM = 64
BLOCK = 64
PAIR = 2 * BLOCK
MASKED = -1e30
bf16 = jnp.bfloat16
f32 = jnp.float32


def dot_nn(a, b):
    return lax.dot_general(a, b, (((1,), (0,)), ((), ())), preferred_element_type=f32)


def dot_nt(a, b):
    return lax.dot_general(a, b, (((1,), (1,)), ((), ())), preferred_element_type=f32)


def dot_tn(a, b):
    return lax.dot_general(a, b, (((0,), (0,)), ((), ())), preferred_element_type=f32)


def slots(rand_ref, glob_ref, flip, head, pair, nblocks):
    first = (2 * pair) ^ flip

    def row(block):
        return pl.multiple_of(block * BLOCK, BLOCK)

    def near(block):
        bad = (block < 0) | (block >= nblocks) | (block == glob_ref[0, 0]) | (block == glob_ref[0, 1])
        return row(jnp.where(bad, nblocks, block ^ flip))

    def drawn(block):
        at = (head * nblocks + block) * 3
        return [row(rand_ref[at + j] ^ flip) for j in range(3)]

    shared = [near(first), near(first + 1)] + [row(glob_ref[0, j] ^ flip) for j in range(2)]
    return shared, [near(first - 1)] + drawn(first), [near(first + 2)] + drawn(first + 1)


def stack_rows(ref, offsets, lanes):
    return jnp.concatenate([ref[pl.ds(o, BLOCK), lanes] for o in offsets], axis=0)


def lane_halves(width, dtype):
    lane = lax.broadcasted_iota(jnp.int32, (1, width), 1) % PAIR
    first = (lane < BLOCK).astype(dtype)
    second = (lane >= BLOCK).astype(dtype)
    return first, second


UNROLL = 4
BACK_UNROLL = 4
APART = 0
VMEM_BYTES = 62 << 20


def head_lanes(h):
    return slice(h * PAIR, (h + 1) * PAIR)


def query_columns(q_ref, mask_ref, h, at):
    return jnp.concatenate([q_ref[h * BLOCK : (h + 1) * BLOCK, pl.ds(at, PAIR)], mask_ref[:, pl.ds(at, PAIR)]], axis=0)


def global_queries(q_ref, mask_ref, h, gl):
    return jnp.concatenate(
        [
            global_columns(q_ref, slice(h * BLOCK, (h + 1) * BLOCK), gl),
            global_columns(mask_ref, slice(0, BLOCK), gl),
        ],
        axis=0,
    ).astype(bf16)


def placed(me_ref, glob_ref, nblocks, chunks):
    flip = me_ref[0] * (nblocks // chunks)
    return flip, [glob_ref[0, j] ^ flip for j in range(2)]


def global_columns(src_ref, rows, gl):
    lane = lax.broadcasted_iota(jnp.int32, (1, PAIR), 1)
    parts = []
    for g in range(2):
        block = gl[g]
        at = pl.multiple_of((block // 2) * PAIR, PAIR)
        both = src_ref[rows, pl.ds(at, PAIR)].astype(f32)
        moved = pltpu.roll(both, BLOCK, 1)
        parts.append(jnp.where(block % 2 == g, both, moved))
    return jnp.where(lane < BLOCK, parts[0], parts[1])


def put_global_columns(dst_ref, rows, gl, value, per_chunk, low, high):
    lane = lax.broadcasted_iota(jnp.int32, (1, PAIR), 1)
    moved = pltpu.roll(value, BLOCK, 1)
    for g in range(2):
        pair = gl[g] // 2
        half = gl[g] % 2
        chunk = pair // per_chunk

        @pl.when((chunk >= low) & (chunk < high))
        def _():
            at = pl.multiple_of((pair % per_chunk) * PAIR, PAIR)
            src = jnp.where(half == g, value, moved)
            old = dst_ref[chunk - low, rows, pl.ds(at, PAIR)].astype(f32)
            new = jnp.where((lane >= BLOCK) == (half == 1), src, old)
            dst_ref[chunk - low, rows, pl.ds(at, PAIR)] = new.astype(dst_ref.dtype)


def project_rows(x, seg, w_ref, wq, bkv_ref, bq_ref, k_ref, v_ref, q_ref, mask_ref, at):
    n = x.shape[0]
    lanes = v_ref.shape[1]
    y = dot_nn(x, w_ref[:, 0:lanes]) + bkv_ref[...]
    spot = lax.broadcasted_iota(jnp.int32, (PAIR, n), 0) - BLOCK
    mark = jnp.transpose((spot == seg).astype(f32), (1, 0))
    lane = lax.broadcasted_iota(jnp.int32, (1, PAIR), 1)
    rows = pl.ds(at, n)
    v_ref[rows, :] = y.astype(bf16)
    for h in range(lanes // PAIR):
        k_ref[rows, head_lanes(h)] = jnp.where(lane < BLOCK, y[:, head_lanes(h)], mark).astype(bf16)
    z = (dot_nt(wq, x) + bq_ref[...]).astype(bf16)
    q_ref[:, rows] = (z.astype(f32) * HEAD_DIM ** -0.5).astype(bf16)
    row = lax.broadcasted_iota(jnp.int32, (BLOCK, n), 0)
    mask_ref[:, rows] = jnp.where((row <= 16) & (row != seg), MASKED, 0.0).astype(bf16)


def query_weights(w_ref, heads):
    at = heads * PAIR
    cols = w_ref[:, at : at + 2 * PAIR].astype(f32)
    return jnp.transpose(cols, (1, 0))[0 : heads * HEAD_DIM].astype(bf16)


def sparse_forward(heads, low, high, per_chunk, rand_ref, glob_ref, flip, k_ref, kv_ref, q_ref, mask_ref, out_ref, lse_ref):
    nblocks = (k_ref.shape[0] - BLOCK) // BLOCK
    first, second = lane_halves(PAIR, bf16)
    lane = lax.broadcasted_iota(jnp.int32, (1, PAIR), 1)

    def one_pair(spot):
        chunk = spot // per_chunk
        local = pl.multiple_of((spot % per_chunk) * PAIR, PAIR)
        pair = low * per_chunk + spot
        at = pl.multiple_of(pair * PAIR, PAIR)
        for h in range(heads):
            shared, mine, other = slots(rand_ref, glob_ref, flip, h, pair, nblocks)
            kl = head_lanes(h)
            q = query_columns(q_ref, mask_ref, h, at)
            s_sh = dot_nn(stack_rows(k_ref, shared, kl), q)
            k_pr = jnp.concatenate([stack_rows(k_ref, mine, kl), stack_rows(k_ref, other, kl)], axis=1)
            s_pr = dot_nn(k_pr, jnp.concatenate([q * first, q * second], axis=0))
            peak = jnp.maximum(jnp.max(s_sh, axis=0, keepdims=True), jnp.max(s_pr, axis=0, keepdims=True))
            e_sh = jnp.exp(s_sh - peak)
            e_pr = jnp.exp(s_pr - peak)
            total = jnp.sum(e_sh, axis=0, keepdims=True) + jnp.sum(e_pr, axis=0, keepdims=True)
            inv = 1.0 / total
            p_sh = (e_sh * inv).astype(bf16)
            p_pr = (e_pr * inv).astype(bf16)
            v_pr = jnp.concatenate([stack_rows(kv_ref, mine, kl), stack_rows(kv_ref, other, kl)], axis=1)
            o_sh = dot_tn(stack_rows(kv_ref, shared, kl), p_sh)
            o_pr = dot_tn(v_pr, p_pr)
            ctx = o_sh[BLOCK:PAIR] + jnp.where(lane < BLOCK, o_pr[BLOCK:PAIR], o_pr[PAIR + BLOCK : 2 * PAIR])
            out_ref[chunk, h * BLOCK : (h + 1) * BLOCK, pl.ds(local, PAIR)] = ctx.astype(bf16)
            lse_ref[h, pl.ds(spot, 1), :] = peak + jnp.log(total)

    @pl.loop(0, (high - low) * per_chunk // UNROLL)
    def _(some):
        for i in range(UNROLL):
            one_pair(UNROLL * some + i)


def forward_kernel(heads, chunks, me_ref, rand_ref, glob_ref, *refs):
    x_refs = refs[0:chunks]
    seg_ref, w_ref, bkv_ref, bq_ref = refs[chunks : chunks + 4]
    far = chunks // 2
    out_refs = refs[chunks + 4 : chunks + 4 + far]
    lse_ref, lseg_ref, glob_ctx_ref, k_sc, v_sc, q_sc, mask_sc, s_sc, out_ref, seg_sc = refs[chunks + 4 + far :]
    rows = x_refs[0].shape[0]
    length = rows * chunks
    per_chunk = length // PAIR // chunks
    flip, gl = placed(me_ref, glob_ref, length // BLOCK, chunks)
    tile = 256
    wq = query_weights(w_ref, heads)
    for c in range(chunks):
        seg_sc[c : c + 1, :] = seg_ref[pl.ds(me_ref[0] ^ c, 1), :]
    for c in range(chunks):

        @pl.loop(0, rows // tile)
        def _(t):
            at = pl.multiple_of(t * tile, tile)
            project_rows(
                x_refs[c][pl.ds(at, tile), :], seg_sc[c : c + 1, pl.ds(at, tile)], w_ref, wq, bkv_ref, bq_ref,
                k_sc, v_sc, q_sc, mask_sc, pl.multiple_of(c * rows + t * tile, tile),
            )

    null_lane = lax.broadcasted_iota(jnp.int32, (BLOCK, heads * PAIR), 1) % PAIR
    k_sc[pl.ds(length, BLOCK), :] = (null_lane == BLOCK + 16).astype(f32).astype(bf16)
    v_sc[pl.ds(length, BLOCK), :] = jnp.zeros((BLOCK, heads * PAIR), bf16)
    sparse_forward(heads, far, chunks, per_chunk, rand_ref, glob_ref, flip, k_sc, v_sc, q_sc, mask_sc, out_ref, lse_ref)

    step = 512
    queries = [global_queries(q_sc, mask_sc, h, gl) for h in range(heads)]

    def score(c, peaks):
        at = pl.multiple_of(c * step, step)
        new = []
        for h in range(heads):
            got = dot_nn(k_sc[pl.ds(at, step), head_lanes(h)], queries[h])
            s_sc[h, pl.ds(at, step), :] = got
            new.append(jnp.maximum(peaks[h], jnp.max(got, axis=0, keepdims=True)))
        return tuple(new)

    peaks = lax.fori_loop(0, length // step, score, (jnp.full((1, PAIR), MASKED, f32),) * heads)

    def gather(c, carry):
        at = pl.multiple_of(c * step, step)
        new = []
        for h in range(heads):
            total, ctx = carry[h]
            e = jnp.exp(s_sc[h, pl.ds(at, step), :] - peaks[h])
            ctx = ctx + dot_tn(v_sc[pl.ds(at, step), head_lanes(h)], e.astype(bf16))
            new.append((total + jnp.sum(e, axis=0, keepdims=True), ctx))
        return tuple(new)

    start = (jnp.zeros((1, PAIR), f32), jnp.zeros((PAIR, PAIR), f32))
    sums = lax.fori_loop(0, length // step, gather, (start,) * heads)
    for h in range(heads):
        total, ctx = sums[h]
        ctx = ctx[BLOCK:PAIR] * (1.0 / total)
        glob_ctx_ref[h] = ctx
        put_global_columns(out_ref, slice(h * BLOCK, (h + 1) * BLOCK), gl, ctx, per_chunk, far, chunks)
        lseg_ref[h : h + 1, :] = peaks[h] + jnp.log(total)
    for c in range(far):
        out_refs[c][...] = out_ref[c]


def attention_forward(me, rand, glob, x, seg, w, b_kv, b_q):
    chunks = len(x)
    far = chunks // 2
    rows = x[0].shape[0]
    length = rows * chunks
    heads = b_q.shape[0] // HEAD_DIM
    whole = lambda: pl.BlockSpec(memory_space=pltpu.VMEM)
    got = pl.pallas_call(
        functools.partial(forward_kernel, heads, chunks),
        out_shape=(jax.ShapeDtypeStruct((heads * HEAD_DIM, rows), bf16),) * far
        + (
            jax.ShapeDtypeStruct((heads, length // PAIR // 2, PAIR), f32),
            jax.ShapeDtypeStruct((heads, PAIR), f32),
            jax.ShapeDtypeStruct((heads, HEAD_DIM, PAIR), f32),
            jax.ShapeDtypeStruct((length + BLOCK, heads * PAIR), bf16),
            jax.ShapeDtypeStruct((length + BLOCK, heads * PAIR), bf16),
            jax.ShapeDtypeStruct((heads * HEAD_DIM, length), bf16),
            jax.ShapeDtypeStruct((BLOCK, length), bf16),
        ),
        in_specs=[pl.BlockSpec(memory_space=pltpu.SMEM)] * 3 + [whole() for _ in range(chunks + 4)],
        out_specs=tuple(whole() for _ in range(far + 7)),
        scratch_shapes=[
            pltpu.VMEM((heads, length, PAIR), f32),
            pltpu.VMEM((far, heads * HEAD_DIM, rows), bf16),
            pltpu.VMEM((chunks, rows), jnp.int32),
        ],
        compiler_params=pltpu.CompilerParams(vmem_limit_bytes=VMEM_BYTES),
        cost_estimate=pl.CostEstimate(flops=10_000_000_000, bytes_accessed=16_000_000, transcendentals=6_000_000),
        name="attention_forward",
    )(me, rand, glob, *x, seg, w, b_kv, b_q)
    return got[:far], got[far:]


def near_kernel(heads, chunks, me_ref, rand_ref, glob_ref, k_ref, kv_ref, q_ref, mask_ref, glob_ctx_ref, *refs):
    half = chunks // 2
    out_refs = refs[:half]
    lse_ref, out_ref = refs[half:]
    length = q_ref.shape[1]
    per_chunk = length // PAIR // chunks
    flip, gl = placed(me_ref, glob_ref, length // BLOCK, chunks)
    sparse_forward(heads, 0, half, per_chunk, rand_ref, glob_ref, flip, k_ref, kv_ref, q_ref, mask_ref, out_ref, lse_ref)
    for h in range(heads):
        put_global_columns(out_ref, slice(h * BLOCK, (h + 1) * BLOCK), gl, glob_ctx_ref[h], per_chunk, 0, half)
    for c in range(half):
        out_refs[c][...] = out_ref[c]


def attention_near(me, rand, glob, k, kv, q, mask, glob_ctx, chunks):
    heads = glob_ctx.shape[0]
    half = chunks // 2
    length = q.shape[1]
    rows = length // chunks
    whole = lambda: pl.BlockSpec(memory_space=pltpu.VMEM)
    got = pl.pallas_call(
        functools.partial(near_kernel, heads, chunks),
        out_shape=(jax.ShapeDtypeStruct((heads * HEAD_DIM, rows), bf16),) * half
        + (jax.ShapeDtypeStruct((heads, length // PAIR // 2, PAIR), f32),),
        in_specs=[pl.BlockSpec(memory_space=pltpu.SMEM)] * 3 + [whole() for _ in range(5)],
        out_specs=tuple(whole() for _ in range(half + 1)),
        scratch_shapes=[pltpu.VMEM((half, heads * HEAD_DIM, rows), bf16)],
        compiler_params=pltpu.CompilerParams(vmem_limit_bytes=VMEM_BYTES),
        cost_estimate=pl.CostEstimate(flops=6_000_000_000, bytes_accessed=9_000_000, transcendentals=3_000_000),
        name="attention_near",
    )(me, rand, glob, k, kv, q, mask, glob_ctx)
    return got[:half], got[half]


def backward_kernel(heads, chunks, me_ref, rand_ref, glob_ref, *refs):
    do_refs = refs[:chunks]
    (k_ref, kv_ref, q_ref, mask_ref, seg_ref, lse_near_ref, lse_far_ref, lseg_ref, w_ref, resid_ref, dq_ref, dkv_ref,
     first_ref) = refs[chunks : chunks + 13]
    part_refs = refs[chunks + 13 : 2 * chunks + 12]
    do_sc, acc, p_sc, d_sc, seg_sc, line_sc, lse_ref, row_sc = refs[2 * chunks + 12 :]
    rows = do_refs[0].shape[1]
    length = rows * chunks
    npairs = length // PAIR
    per_chunk = npairs // chunks
    scale = HEAD_DIM ** -0.5
    flip, gl = placed(me_ref, glob_ref, length // BLOCK, chunks)
    lse_ref[:, 0 : npairs // 2, :] = lse_near_ref[...]
    lse_ref[:, npairs // 2 :, :] = lse_far_ref[...]
    for c in range(chunks):
        do_sc[:, c * rows : (c + 1) * rows] = do_refs[c][...]
        row_sc[c : c + 1, :] = seg_ref[pl.ds(me_ref[0] ^ c, 1), :].astype(f32)

        @pl.loop(0, per_chunk // 4)
        def _(some):
            for i in range(4):
                t = 4 * some + i
                line = row_sc[c : c + 1, pl.ds(pl.multiple_of(t * PAIR, PAIR), PAIR)]
                line_sc[c * per_chunk + t] = line
                to = pl.multiple_of(c * rows + t * PAIR, PAIR)
                seg_sc[pl.ds(to, PAIR), :] = jnp.transpose(jnp.broadcast_to(line, (PAIR, PAIR)), (1, 0))

    seg_sc[length : length + BLOCK, :] = jnp.full((BLOCK, PAIR), -1.0, f32)
    first2, second2 = lane_halves(2 * PAIR, bf16)
    ffirst, fsecond = lane_halves(PAIR, f32)
    lane = lax.broadcasted_iota(jnp.int32, (1, PAIR), 1)
    line_row = lax.broadcasted_iota(jnp.int32, (PAIR, 1), 0)
    zeros = jnp.zeros((BLOCK, PAIR), bf16)
    blank = jnp.zeros((PAIR, PAIR), bf16)

    def head_rows(h):
        return slice(h * BLOCK, (h + 1) * BLOCK)

    def joint(q, mask, do):
        left = jnp.concatenate([q, mask, blank], axis=0)
        right = jnp.concatenate([blank, zeros, do], axis=0)
        return jnp.concatenate([left, right], axis=1)

    def sources(q, do):
        top = jnp.concatenate([q, zeros], axis=1)
        return jnp.concatenate([top, jnp.concatenate([zeros, do], axis=1)], axis=0)

    step = 512
    mask_glob = global_columns(mask_ref, slice(0, BLOCK), gl).astype(bf16)
    q_glob = [global_columns(q_ref, head_rows(h), gl).astype(bf16) for h in range(heads)]
    do_glob = [global_columns(do_sc, head_rows(h), gl).astype(bf16) for h in range(heads)]

    def weigh(c, deltas):
        at = pl.multiple_of(c * step, step)
        new = []
        for h in range(heads):
            left = jnp.concatenate([k_ref[pl.ds(at, step), head_lanes(h)], kv_ref[pl.ds(at, step), head_lanes(h)]], axis=1)
            both = dot_nn(left, joint(q_glob[h], mask_glob, do_glob[h]))
            p = jnp.exp(both[:, 0:PAIR] - lseg_ref[h : h + 1, :])
            dp = both[:, PAIR:]
            p_sc[h, pl.ds(at, step), :] = p
            d_sc[h, pl.ds(at, step), :] = dp
            new.append(deltas[h] + jnp.sum(p * dp, axis=0, keepdims=True))
        return tuple(new)

    deltas = lax.fori_loop(0, length // step, weigh, (jnp.zeros((1, PAIR), f32),) * heads)

    def spread(c, dqs):
        at = pl.multiple_of(c * step, step)
        new = []
        for h in range(heads):
            p = p_sc[h, pl.ds(at, step), :]
            ds = (p * (d_sc[h, pl.ds(at, step), :] - deltas[h])).astype(bf16)
            both = jnp.concatenate([ds, p.astype(bf16)], axis=1)
            acc[h, pl.ds(at, step), :] = dot_nt(both, sources(q_glob[h], do_glob[h]))
            new.append(dqs[h] + dot_tn(k_ref[pl.ds(at, step), head_lanes(h)], ds))
        return tuple(new)

    dqs = lax.fori_loop(0, length // step, spread, (jnp.zeros((PAIR, PAIR), f32),) * heads)
    for h in range(heads):
        acc[h, pl.ds(length, BLOCK), :] = jnp.zeros((BLOCK, PAIR), f32)

    def one_pair(pair):
        chunk = pair // per_chunk
        local = pl.multiple_of((pair % per_chunk) * PAIR, PAIR)
        at = pl.multiple_of(pair * PAIR, PAIR)
        hit_first = (gl[0] == 2 * pair) | (gl[1] == 2 * pair)
        hit_second = (gl[0] == 2 * pair + 1) | (gl[1] == 2 * pair + 1)
        shut = ffirst * jnp.where(hit_first, -MASKED, 0.0) + fsecond * jnp.where(hit_second, -MASKED, 0.0)
        every = slice(0, PAIR)
        for h in range(heads):
            kl = head_lanes(h)
            shared, mine, other = slots(rand_ref, glob_ref, flip, h, pair, length // BLOCK)
            q = q_ref[head_rows(h), pl.ds(at, PAIR)]
            do = do_sc[head_rows(h), pl.ds(at, PAIR)]
            lse = lse_ref[h, pl.ds(pair, 1), :] + shut
            src = sources(q, do)
            src2 = jnp.concatenate([src * first2, src * second2], axis=0)
            k_sh = stack_rows(k_ref, shared, kl)
            two_sh = dot_nn(
                jnp.concatenate([k_sh, stack_rows(kv_ref, shared, kl)], axis=1),
                joint(q, mask_ref[:, pl.ds(at, PAIR)], do),
            )
            kv_pr = jnp.concatenate([stack_rows(kv_ref, mine, kl), stack_rows(kv_ref, other, kl)], axis=1)
            two_pr = dot_nn(kv_pr, src2)
            seg_pr = jnp.where(lane < BLOCK, stack_rows(seg_sc, mine, every), stack_rows(seg_sc, other, every))
            agree = seg_pr == line_sc[pair]
            p_sh = jnp.exp(two_sh[:, 0:PAIR] - lse)
            p_pr = jnp.where(agree, jnp.exp(two_pr[:, 0:PAIR] - lse), 0.0)
            d_sh, d_pr = two_sh[:, PAIR:], two_pr[:, PAIR:]
            delta = jnp.sum(p_sh * d_sh, axis=0, keepdims=True) + jnp.sum(p_pr * d_pr, axis=0, keepdims=True)
            ds_sh = (p_sh * (d_sh - delta)).astype(bf16)
            ds_pr = (p_pr * (d_pr - delta)).astype(bf16)
            g_sh = dot_nt(jnp.concatenate([ds_sh, p_sh.astype(bf16)], axis=1), src)
            g_pr = dot_nt(jnp.concatenate([ds_pr, p_pr.astype(bf16)], axis=1), src2)
            for j, o in enumerate(shared):
                acc[h, pl.ds(o, BLOCK), :] += g_sh[j * BLOCK : (j + 1) * BLOCK]
            for j, o in enumerate(mine):
                acc[h, pl.ds(o, BLOCK), :] += g_pr[j * BLOCK : (j + 1) * BLOCK, 0:PAIR]
            for j, o in enumerate(other):
                acc[h, pl.ds(o, BLOCK), :] += g_pr[j * BLOCK : (j + 1) * BLOCK, PAIR:]
            t_pr = dot_tn(ds_pr, kv_pr)
            dq = dot_tn(ds_sh, k_sh) + jnp.where(line_row < BLOCK, t_pr[:, 0:PAIR], t_pr[:, PAIR:])
            dq = jnp.transpose(dq, (1, 0))[0:BLOCK]
            dq_ref[chunk, head_rows(h), pl.ds(local, PAIR)] = (dq * scale).astype(bf16)

    @pl.loop(0, npairs // BACK_UNROLL)
    def _(some):
        for i in range(BACK_UNROLL):
            one_pair(BACK_UNROLL * some + i)

    for h in range(heads):
        put_global_columns(dq_ref, head_rows(h), gl, dqs[h][0:BLOCK] * scale, per_chunk, 0, chunks)
        for c in range(chunks):
            dkv_ref[c, :, head_lanes(h)] = acc[h, pl.ds(c * rows, rows), :].astype(bf16)
    tile = 256
    wq = query_weights(w_ref, heads)
    for c in range(chunks):

        @pl.loop(0, rows // tile)
        def _(t):
            at = pl.multiple_of(t * tile, tile)
            got = dot_tn(dq_ref[c, :, pl.ds(at, tile)], wq)
            got = got + dot_nt(dkv_ref[c, pl.ds(at, tile), :], w_ref[:, 0 : heads * PAIR])
            if c == 0:
                first_ref[pl.ds(at, tile), :] = resid_ref[pl.ds(at, tile), :] + got
            else:
                part_refs[c - 1][pl.ds(at, tile), :] = got.astype(bf16)


def attention_backward(me, rand, glob, do, k, kv, q, mask, seg, lse_near, lse_far, lseg, w, resid):
    chunks = len(do)
    group, rows = do[0].shape
    heads = group // HEAD_DIM
    width = w.shape[0]
    length = rows * chunks
    whole = lambda: pl.BlockSpec(memory_space=pltpu.VMEM)
    return pl.pallas_call(
        functools.partial(backward_kernel, heads, chunks),
        out_shape=(
            jax.ShapeDtypeStruct((chunks, group, rows), bf16),
            jax.ShapeDtypeStruct((chunks, rows, heads * PAIR), bf16),
            jax.ShapeDtypeStruct((rows, width), f32),
        )
        + (jax.ShapeDtypeStruct((rows, width), bf16),) * (chunks - 1),
        in_specs=[pl.BlockSpec(memory_space=pltpu.SMEM)] * 3 + [whole() for _ in range(chunks + 10)],
        out_specs=tuple(whole() for _ in range(chunks + 2)),
        scratch_shapes=[
            pltpu.VMEM((group, length), bf16),
            pltpu.VMEM((heads, length + BLOCK, PAIR), f32),
            pltpu.VMEM((heads, length, PAIR), f32),
            pltpu.VMEM((heads, length, PAIR), f32),
            pltpu.VMEM((length + BLOCK, PAIR), f32),
            pltpu.VMEM((length // PAIR, 1, PAIR), f32),
            pltpu.VMEM((heads, length // PAIR, PAIR), f32),
            pltpu.VMEM((chunks, rows), f32),
        ],
        compiler_params=pltpu.CompilerParams(vmem_limit_bytes=VMEM_BYTES),
        cost_estimate=pl.CostEstimate(flops=30_000_000_000, bytes_accessed=24_000_000, transcendentals=8_000_000),
        name="attention_backward",
    )(me, rand, glob, *do, k, kv, q, mask, seg, lse_near, lse_far, lseg, w, resid)


def round_up(value, to):
    return -(-value // to) * to


def half_columns(ref, index, place):
    at = index // 2 * PAIR
    both = ref[:, at : at + PAIR].astype(f32)
    return both if index % 2 == place else pltpu.roll(both, BLOCK, 1)


def two_halves(first, second):
    lane = lax.broadcasted_iota(jnp.int32, (1, PAIR), 1)
    return jnp.where(lane < BLOCK, first, second)


def pack_kernel(seq_n, wq_ref, wk_ref, wv_ref, wo_ref, up_ref, down_ref, bup_ref, vec_ref, pack_ref, rest_ref):
    own, width = wq_ref.shape
    heads = width // HEAD_DIM // seq_n
    blocks, inner = pack_ref.shape[0], pack_ref.shape[2]
    for s in range(seq_n):
        pieces = [
            two_halves(half_columns(wk_ref, s * heads + h, 0), half_columns(wv_ref, s * heads + h, 1))
            for h in range(heads)
        ]
        for h in range(0, heads, 2):
            second = half_columns(wq_ref, s * heads + h + 1, 1) if h + 1 < heads else vec_ref[...].astype(f32)
            pieces.append(two_halves(half_columns(wq_ref, s * heads + h, 0), second))
        piece = jnp.concatenate(pieces, axis=1).astype(bf16)
        for b in range(blocks):
            for i in range(inner):
                pack_ref[b, s, i] = piece
    u = up_ref.shape[0]
    rest_ref[0:u, :] = up_ref[...]
    rest_ref[u : 2 * u, :] = down_ref[...]
    rest_ref[2 * u : 2 * u + own, :] = wo_ref[...]
    rest_ref[2 * u + own : 2 * u + own + 8, :] = jnp.broadcast_to(bup_ref[...], (8, width))


def packed_weights(w_q, w_k, w_v, w_o, w_up, w_down, b_up, vec, dp_n, seq_n, ffn_n):
    own, width = w_q.shape
    heads = width // HEAD_DIM // seq_n
    lanes = heads * PAIR + round_up(heads * HEAD_DIM, PAIR)
    u = w_up.shape[0]
    if own % 8 or u % 16:
        group = heads * HEAD_DIM
        cols = lambda w: w.reshape(own, seq_n, heads, HEAD_DIM).transpose(1, 0, 2, 3)
        kv = jnp.stack([cols(w_k), cols(w_v)], axis=3).reshape(seq_n, own, 2 * group)
        notes = jnp.broadcast_to(vec[None, :, HEAD_DIM:], (seq_n, own, PAIR - HEAD_DIM))
        piece = jnp.concatenate([kv, cols(w_q).reshape(seq_n, own, group), notes], axis=2)
        piece = jnp.pad(piece, ((0, 0), (0, round_up(own, 8) - own), (0, 0)))
        pack = jnp.broadcast_to(piece[None, :, None], (dp_n, seq_n, ffn_n) + piece.shape[1:])
        w_o = jnp.pad(w_o, ((0, round_up(own, 8) - own), (0, 0)))
        return pack, jnp.concatenate([w_up, w_down, w_o, jnp.broadcast_to(b_up, (8, width))], axis=0)
    whole = lambda: pl.BlockSpec(memory_space=pltpu.VMEM)
    return pl.pallas_call(
        functools.partial(pack_kernel, seq_n),
        out_shape=(
            jax.ShapeDtypeStruct((dp_n, seq_n, ffn_n, own, lanes), bf16),
            jax.ShapeDtypeStruct((2 * u + own + 8, width), bf16),
        ),
        in_specs=[whole() for _ in range(8)],
        out_specs=(whole(), whole()),
        name="packed_weights",
    )(w_q, w_k, w_v, w_o, w_up, w_down, b_up, vec)


def weights_kernel(chunks, direct, *refs):
    x_refs = refs[:chunks]
    dq_ref, dkv_ref, out_ref, acc, sum_sc = refs[chunks:]
    group = dq_ref.shape[1]
    lanes = dkv_ref.shape[2]
    full, width = acc.shape
    x = jnp.concatenate([r[...] for r in x_refs], axis=0)
    dkv = jnp.concatenate([dkv_ref[c] for c in range(chunks)], axis=0)
    dq = jnp.concatenate([dq_ref[c] for c in range(chunks)], axis=1)
    ones = jnp.ones((8, x.shape[0]), bf16)

    @pl.when(pl.program_id(0) == 0)
    def _():
        acc[...] = jnp.zeros_like(acc)
        sum_sc[...] = jnp.zeros_like(sum_sc)

    acc[0:lanes, :] += dot_tn(dkv, x)
    acc[lanes : lanes + group, :] += dot_nn(dq, x)
    sum_sc[:, 0:lanes] += dot_nn(ones, dkv)
    sum_sc[:, lanes : lanes + group] += dot_nt(ones, dq)

    @pl.when(pl.program_id(0) == pl.num_programs(0) - 1)
    def _():
        lane = lax.broadcasted_iota(jnp.int32, (full, width), 0)
        spot = lax.broadcasted_iota(jnp.int32, (full, width), 1) % group
        pick_q = lane - lanes == spot
        pick_v = (lane < lanes) & (lane % PAIR >= BLOCK) & (lane // PAIR * BLOCK + lane % BLOCK == spot)
        sums = sum_sc[...].astype(bf16)
        row = lax.broadcasted_iota(jnp.int32, (8, width), 0)
        of_q = dot_nn(sums, pick_q.astype(f32).astype(bf16))
        of_v = dot_nn(sums, pick_v.astype(f32).astype(bf16))
        acc[lanes + group : lanes + group + 8, :] = jnp.where(row == 0, of_q, of_v)
        grad = jnp.transpose(acc[...], (1, 0))
        if direct:
            blocks, own, _ = out_ref.shape
            grad = grad.reshape(blocks, own, full)
            for b in range(blocks):
                out_ref[b] = grad[b].astype(bf16)
        else:
            out_ref[...] = grad.astype(bf16)


def projection_gradients(x, dq, dkv, own, devices):
    chunks, group, rows = dq.shape
    width = x[0].shape[1]
    lanes = dkv.shape[2]
    full = lanes + round_up(group, PAIR)
    direct = own % 8 == 0
    tile = 256
    shape = (devices, own, full) if direct else (width, full)
    out = pl.pallas_call(
        functools.partial(weights_kernel, chunks, direct),
        grid=(rows // tile,),
        out_shape=jax.ShapeDtypeStruct(shape, bf16),
        in_specs=[pl.BlockSpec((tile, width), lambda i: (i, 0)) for _ in range(chunks)]
        + [
            pl.BlockSpec((chunks, group, tile), lambda i: (0, 0, i)),
            pl.BlockSpec((chunks, tile, lanes), lambda i: (0, i, 0)),
        ],
        out_specs=pl.BlockSpec(shape, lambda i: (0,) * len(shape), pipeline_mode=pl.Buffered(1)),
        scratch_shapes=[pltpu.VMEM((full, width), f32), pltpu.VMEM((8, full), f32)],
        compiler_params=pltpu.CompilerParams(vmem_limit_bytes=VMEM_BYTES),
        cost_estimate=pl.CostEstimate(flops=4_000_000_000, bytes_accessed=12_000_000, transcendentals=0),
        name="projection_gradients",
    )(*x, dq, dkv)
    if not direct:
        out = jnp.pad(out.reshape(devices, own, full), ((0, 0), (0, round_up(own, 8) - own), (0, 0)))
    return out


def unpack_kernel(own, got_ref, q_ref, k_ref, v_ref, sums_ref, tot):
    dp_n, seq_n, ffn_n, per, full = got_ref.shape
    width = q_ref.shape[1]
    heads = width // HEAD_DIM // seq_n
    for s in range(seq_n):
        total = jnp.zeros((per, full), f32)
        for d in range(dp_n):
            for f in range(ffn_n):
                total = total + got_ref[d, s, f].astype(f32)
        tot[s] = total
        sums_ref[s] = total[:, full - PAIR :]
    for w in range(width // PAIR):
        spots = [((2 * w + i) // heads, (2 * w + i) % heads) for i in range(2)]
        cols = slice(w * PAIR, (w + 1) * PAIR)
        for ref, where in (
            (k_ref, lambda h: 2 * h),
            (v_ref, lambda h: 2 * h + 1),
            (q_ref, lambda h: 2 * heads + h),
        ):
            both = [half_columns(tot.at[g], where(h), i) for i, (g, h) in enumerate(spots)]
            ref[:, cols] = two_halves(*both)[0:own]


def unpacked_gradients(got, own, width):
    dp_n, seq_n, ffn_n, per, full = got.shape
    whole = lambda: pl.BlockSpec(memory_space=pltpu.VMEM)
    return pl.pallas_call(
        functools.partial(unpack_kernel, own),
        out_shape=(jax.ShapeDtypeStruct((own, width), f32),) * 3 + (jax.ShapeDtypeStruct((seq_n, per, PAIR), f32),),
        in_specs=[whole()],
        out_specs=tuple(whole() for _ in range(4)),
        scratch_shapes=[pltpu.VMEM((seq_n, per, full), f32)],
        compiler_params=pltpu.CompilerParams(vmem_limit_bytes=VMEM_BYTES),
        cost_estimate=pl.CostEstimate(flops=40_000_000_000, bytes_accessed=3_000_000, transcendentals=0),
        name="unpacked_gradients",
    )(got)


NORM_EPS = 1e-12


def transposed(value):
    return jnp.transpose(value.astype(f32), (1, 0)).astype(bf16)


def unit_rows(value):
    center = value - jnp.mean(value, axis=-1, keepdims=True)
    scale = lax.rsqrt(jnp.mean(center * center, axis=-1, keepdims=True) + NORM_EPS)
    return center * scale, scale


def unit_rows_back(grad, unit, scale):
    return scale * (
        grad - jnp.mean(grad, axis=-1, keepdims=True) - unit * jnp.mean(grad * unit, axis=-1, keepdims=True)
    )


def rows_kernel(parts, blocks, up_rows, own, me_ref, *refs):
    ctx_refs = refs[:parts]
    (x_ref, cot_ref, rest_ref, wo_ref, vec_ref, bup_ref, out_ref, resid_ref, hid_ref, pre_ref, nlt_ref, gft_ref,
     gb_ref) = refs[parts : parts + 13]
    do_refs = refs[parts + 13 : 2 * parts + 13]
    sums_ref, gbup_ref, slope_sc, wo_sc, wide_sc = refs[2 * parts + 13 :]
    group = ctx_refs[0].shape[0]
    width = x_ref.shape[1]

    def up(f):
        return rest_ref[:, f, 0:up_rows, :].reshape(width, rest_ref.shape[3])

    def down(f):
        return rest_ref[:, f, up_rows : 2 * up_rows, :].reshape(width, rest_ref.shape[3])

    def own_rows(k):
        return pl.ds(pl.multiple_of((me_ref[0] ^ k) * group, group), group)

    @pl.when(pl.program_id(0) == 0)
    def _():
        sums_ref[...] = jnp.zeros_like(sums_ref)
        gbup_ref[...] = jnp.zeros_like(gbup_ref)
        if own:
            for o in range(rest_ref.shape[0]):
                for f in range(blocks):
                    to = (o * blocks + f) * own
                    wide_sc[to : to + own, :] = rest_ref[o, f, 2 * up_rows : 2 * up_rows + own, :].astype(f32)
            wo_sc[...] = wide_sc[...].astype(bf16)
        else:
            wo_sc[...] = wo_ref[...]

    def bias_up(f):
        if own:
            row = rest_ref[0, f, 2 * up_rows + own : 2 * up_rows + own + 8, :].astype(f32)
            return row[7:8, :]
        return bup_ref[f : f + 1, :]

    ctx = jnp.concatenate([r[...] for r in ctx_refs], axis=0)
    w_o = jnp.concatenate([wo_sc[own_rows(k), :] for k in range(parts)], axis=0)
    resid_one = x_ref[...].astype(f32) + (dot_tn(ctx, w_o) + vec_ref[0:1, :])
    unit_one, scale_one = unit_rows(resid_one)
    normed_one = unit_one * vec_ref[2:3, :] + vec_ref[3:4, :]
    low = normed_one.astype(bf16)
    nlt_ref[...] = transposed(normed_one)
    total = normed_one + vec_ref[1:2, :]
    pre = dot_nn(low, up(0)) + bias_up(0)
    for f in range(blocks):
        later = dot_nn(low, up(f + 1)) + bias_up(f + 1) if f + 1 < blocks else None
        phi = 0.5 + 0.5 * lax.erf(pre * (0.5 ** 0.5))
        slope_sc[f] = phi + pre * (jnp.exp(-0.5 * pre * pre) * 0.3989422804014327)
        hid = (pre * phi).astype(bf16)
        hid_ref[f] = hid
        total = total + dot_nt(hid, down(f))
        pre = later
    unit_two, scale_two = unit_rows(total)
    out_ref[...] = (unit_two * vec_ref[4:5, :] + vec_ref[5:6, :]).astype(bf16)
    cot = cot_ref[...].astype(f32)
    grad_two = unit_rows_back(cot * vec_ref[4:5, :], unit_two, scale_two)
    grad_ffn = grad_two.astype(bf16)
    gft_ref[...] = transposed(grad_two)
    grad_normed = grad_two
    back = dot_nn(grad_ffn, down(0))
    for f in range(blocks):
        later = dot_nn(grad_ffn, down(f + 1)) if f + 1 < blocks else None
        grad_pre = (back * slope_sc[f]).astype(bf16)
        pre_ref[f] = grad_pre
        gbup_ref[f : f + 1, :] += jnp.sum(grad_pre.astype(f32), axis=0, keepdims=True)
        grad_normed = grad_normed + dot_nt(grad_pre, up(f))
        back = later
    resid = unit_rows_back(grad_normed * vec_ref[2:3, :], unit_one, scale_one)
    resid_ref[...] = resid
    branch = resid.astype(bf16)
    gb_ref[...] = branch
    do = dot_nt(w_o, branch).astype(bf16)
    for k in range(parts):
        do_refs[k][...] = do[k * group : (k + 1) * group]
    for row, value in enumerate(
        (branch.astype(f32), grad_ffn.astype(f32), grad_normed * unit_one, grad_normed, cot * unit_two, cot)
    ):
        sums_ref[row : row + 1, :] += jnp.sum(value, axis=0, keepdims=True)


def rows_chain(me, ctx_parts, x, cot, rest, up_rows, own, w_o, vecs, bias_up):
    parts = len(ctx_parts)
    group, rows = ctx_parts[0].shape
    width = x.shape[1]
    outer, blocks, per, hidden = rest.shape
    tile = 256
    once = lambda shape: pl.BlockSpec(shape, lambda i: (0,) * len(shape), pipeline_mode=pl.Buffered(1))
    tall = pl.BlockSpec((tile, width), lambda i: (i, 0))
    wide = pl.BlockSpec((width, tile), lambda i: (0, i))
    cube = pl.BlockSpec((blocks, tile, hidden), lambda i: (0, i, 0))
    return pl.pallas_call(
        functools.partial(rows_kernel, parts, blocks, up_rows, own),
        grid=(rows // tile,),
        out_shape=(
            jax.ShapeDtypeStruct((rows, width), bf16),
            jax.ShapeDtypeStruct((rows, width), f32),
            jax.ShapeDtypeStruct((blocks, rows, hidden), bf16),
            jax.ShapeDtypeStruct((blocks, rows, hidden), bf16),
            jax.ShapeDtypeStruct((width, rows), bf16),
            jax.ShapeDtypeStruct((width, rows), bf16),
            jax.ShapeDtypeStruct((rows, width), bf16),
        )
        + (jax.ShapeDtypeStruct((group, rows), bf16),) * parts
        + (jax.ShapeDtypeStruct((8, width), f32), jax.ShapeDtypeStruct((8, hidden), f32)),
        in_specs=[pl.BlockSpec(memory_space=pltpu.SMEM)]
        + [pl.BlockSpec((group, tile), lambda i: (0, i))] * parts
        + [tall, tall, once(rest.shape), once(w_o.shape), once(vecs.shape), once(bias_up.shape)],
        out_specs=(
            tall, tall, cube, cube, wide, wide, tall,
        )
        + (pl.BlockSpec((group, tile), lambda i: (0, i)),) * parts
        + (pl.BlockSpec((8, width), lambda i: (0, 0)), pl.BlockSpec((8, hidden), lambda i: (0, 0))),
        scratch_shapes=[
            pltpu.VMEM((blocks, tile, hidden), f32),
            pltpu.VMEM((width, width), bf16),
            pltpu.VMEM((width, width), f32),
        ],
        compiler_params=pltpu.CompilerParams(vmem_limit_bytes=VMEM_BYTES),
        cost_estimate=pl.CostEstimate(flops=22_000_000_000, bytes_accessed=40_000_000, transcendentals=6_000_000),
        name="rows_chain",
    )(me, *ctx_parts, x, cot, rest, w_o, vecs, bias_up)


def outer_kernel(parts, up_rows, own, apart, me_ref, *refs):
    ctx_refs = refs[:parts]
    nlt_ref, gft_ref, gb_ref, pre_ref, hid_ref, sums_ref, gbup_ref, out_ref = refs[parts : parts + 8]
    wo_sc = refs[-1]
    slabs, hidden = out_ref.shape[0], out_ref.shape[3]
    group = ctx_refs[0].shape[0]
    f = pl.program_id(0)
    up = dot_nn(nlt_ref[...], pre_ref[0]).astype(bf16).reshape(slabs, up_rows, hidden)
    if apart:
        refs[parts + 8][:, 0, :, :] = up[:, 0:apart]
    out_ref[:, 0, 0 : up_rows - apart, :] = up[:, apart:]
    at = up_rows - apart
    down = dot_nn(gft_ref[...], hid_ref[0]).astype(bf16)
    out_ref[:, 0, at : at + up_rows, :] = down.reshape(slabs, up_rows, hidden)
    at += up_rows
    if not own:
        return

    @pl.when(f == 0)
    def _():
        for k in range(parts):
            wo_sc[k] = dot_nn(ctx_refs[k][...], gb_ref[...])

    share = slabs // parts
    stride = group // share
    for k in range(parts):
        for j in range(share):
            rows = pl.ds(pl.multiple_of(j * stride + f * own, 8), own)
            out_ref[(me_ref[0] ^ k) * share + j, 0, at : at + own, :] = wo_sc[k, rows, :].astype(bf16)
    small = jnp.concatenate([gbup_ref[pl.ds(f, 1), :], sums_ref[0:7, :]], axis=0).astype(bf16)
    for o in range(slabs):
        out_ref[o, 0, at + own :, :] = small


def outer_products(me, ctx_parts, nlt, gft, gb, pre, hid, sums, gbup, slabs, up_rows, own, apart):
    blocks, rows, hidden = pre.shape
    parts = len(ctx_parts)
    group = ctx_parts[0].shape[0]
    per = 2 * up_rows - apart + (own + 8 if own else 0)
    sizes = (per, apart) if apart else (per,)
    once = lambda shape: pl.BlockSpec(shape, lambda i: (0,) * len(shape), pipeline_mode=pl.Buffered(1))
    return pl.pallas_call(
        functools.partial(outer_kernel, parts, up_rows, own, apart),
        grid=(blocks,),
        out_shape=tuple(jax.ShapeDtypeStruct((slabs, blocks, r, hidden), bf16) for r in sizes),
        in_specs=[pl.BlockSpec(memory_space=pltpu.SMEM)]
        + [once(c.shape) for c in ctx_parts]
        + [
            once(nlt.shape),
            once(gft.shape),
            once(gb.shape),
            pl.BlockSpec((1, rows, hidden), lambda i: (i, 0, 0)),
            pl.BlockSpec((1, rows, hidden), lambda i: (i, 0, 0)),
            once(sums.shape),
            once(gbup.shape),
        ],
        out_specs=tuple(pl.BlockSpec((slabs, 1, r, hidden), lambda i: (0, i, 0, 0)) for r in sizes),
        scratch_shapes=[pltpu.VMEM((parts, group, gb.shape[1]), f32)],
        compiler_params=pltpu.CompilerParams(vmem_limit_bytes=VMEM_BYTES),
        cost_estimate=pl.CostEstimate(flops=11_000_000_000, bytes_accessed=28_000_000, transcendentals=0),
        name="outer_products",
    )(me, *ctx_parts, nlt, gft, gb, pre, hid, sums, gbup)


def finish_kernel(up_rows, own, total_ref, up_ref, down_ref, wo_ref, small_ref):
    rest = total_ref[...].astype(f32)
    up_ref[...] = rest[0:up_rows]
    down_ref[...] = rest[up_rows : 2 * up_rows]
    at = 2 * up_rows
    wo_ref[...] = rest[at : at + own]
    small_ref[...] = rest[at + own : at + own + 8]


def finished(total, up_rows, own):
    hidden = total.shape[1]
    whole = lambda: pl.BlockSpec(memory_space=pltpu.VMEM)
    return pl.pallas_call(
        functools.partial(finish_kernel, up_rows, own),
        out_shape=tuple(jax.ShapeDtypeStruct((r, hidden), f32) for r in (up_rows, up_rows, own, 8)),
        in_specs=[whole()],
        out_specs=tuple(whole() for _ in range(4)),
        name="finished",
    )(total)


ALL = ("dp", "seq", "ffn")


def flip_send(array, axis, bits):
    count = lax.axis_size(axis)
    return lax.ppermute(array, axis, [(i, i ^ bits) for i in range(count)])


def shards(
    tokens, w_query, w_key, w_value, w_output, b_query, b_value, b_output, w_up, b_up, w_down, b_down,
    gain_attn, shift_attn, gain_ffn, shift_ffn, segment_ids, random_blocks, global_blocks, cotangent,
):
    seq_n, dp_n, ffn_n = lax.axis_size("seq"), lax.axis_size("dp"), lax.axis_size("ffn")
    outer, devices = dp_n * seq_n, dp_n * seq_n * ffn_n
    me = lax.axis_index("seq")
    here = (lax.axis_index("dp") * seq_n + me) * ffn_n + lax.axis_index("ffn")
    own, width = w_query.shape
    own_pad = round_up(own, 8)
    group = width // seq_n
    heads = group // HEAD_DIM
    features = tokens[0]
    rows = features.shape[0]
    order = jnp.stack([me ^ k for k in range(seq_n)])
    me_ref = me.astype(jnp.int32)[None]

    near = [features] + [None] * (seq_n - 1)
    for k in sorted(range(1, seq_n), key=lambda k: (k & (k - 1), -k)):
        bit = k & -k
        near[k] = flip_send(features if bit == k else near[k ^ bit], "seq", bit)

    vec = jnp.stack([b_output, b_down, gain_attn, shift_attn, gain_ffn, shift_ffn, b_query, b_value], axis=1)
    vec = jnp.pad(vec, ((0, 0), (HEAD_DIM, PAIR - HEAD_DIM - 8)))
    seg = segment_ids[0].reshape(seq_n, rows)
    rand = random_blocks.reshape(-1)
    pack, rest = packed_weights(
        w_query, w_key, w_value, w_output, w_up, w_down, b_up[None], vec, dp_n, seq_n, ffn_n
    )
    lanes = pack.shape[4]
    pack, seg, rand = lax.optimization_barrier((pack, seg, rand))
    pack = lax.all_to_all(
        pack.reshape(devices, own_pad, lanes), ALL, split_axis=0, concat_axis=0, tiled=True
    )
    rest = lax.all_gather(rest, ALL, axis=0, tiled=False)
    w_own = pack[:, :own].reshape(width, lanes)
    share = devices // seq_n
    vecs = w_own[:, lanes - HEAD_DIM : lanes - HEAD_DIM + 8].astype(f32).T
    biases = lax.dynamic_slice(vecs, (6, me * group), (2, group))
    by_head = biases[1].reshape(heads, 1, HEAD_DIM)
    b_kv = jnp.concatenate([jnp.zeros_like(by_head), by_head], axis=1).reshape(1, heads * PAIR)

    far = seq_n // 2
    ctx_far, (lse_far, lseg, glob_ctx, k_all, v_all, q_all, mask_all) = attention_forward(
        me_ref, rand, global_blocks, near, seg, w_own, b_kv, biases[0][:, None]
    )
    ctx_parts = [None] * far + [flip_send(ctx_far[k - far], "seq", k) for k in range(far, seq_n)]
    ctx_near, lse_near = attention_near(
        me_ref, rand, global_blocks, k_all, v_all, q_all, mask_all, glob_ctx, seq_n
    )
    ctx_parts[far:], ctx_parts[0] = lax.optimization_barrier((ctx_parts[far:], ctx_near[0]))
    for k in range(1, far):
        ctx_parts[k] = flip_send(ctx_near[k], "seq", k)

    up_rows = w_up.shape[0]
    at = 2 * up_rows
    rest = rest.reshape(outer, ffn_n, rest.shape[1], width)
    w_o = rest[:, :, at : at + own].reshape(width, width)
    bias_up = rest[0, :, at + own_pad + 7].astype(f32)
    direct = up_rows % 16 == 0 and own % 8 == 0 and outer % seq_n == 0 and (outer // seq_n) * ffn_n * own == group
    if not direct:
        rest = rest[:, :, :at].reshape(outer, ffn_n, 2, up_rows, width).transpose(1, 2, 0, 3, 4)
        rest = rest.reshape(1, ffn_n, 2 * outer * up_rows, width)
    slabs, slab_rows = (outer, up_rows) if direct else (1, outer * up_rows)

    got = rows_chain(
        me_ref, ctx_parts, features, cotangent[0], rest, slab_rows, own if direct else 0,
        jnp.zeros((8, PAIR), bf16) if direct else w_o, vecs, jnp.zeros((8, PAIR), f32) if direct else bias_up,
    )
    out, grad_resid_one, hidden, grad_pre, normed_t, grad_ffn_t, grad_branch = got[:7]
    grad_ctx, (sums, grad_bias_up) = got[7 : 7 + seq_n], got[7 + seq_n :]
    do = [grad_ctx[0]] + [flip_send(grad_ctx[k], "seq", k) for k in range(1, seq_n)]

    payload = outer_products(
        me_ref, ctx_parts, normed_t, grad_ffn_t, grad_branch, grad_pre, hidden, sums, grad_bias_up, slabs, slab_rows,
        own if direct else 0, APART if direct else 0,
    )
    payload, apart = payload if direct and APART else (payload[0], None)
    if not direct:
        grad_out = dot_nn(jnp.concatenate(ctx_parts, axis=0), grad_branch).astype(bf16)
        grad_out = grad_out.reshape(seq_n, group, width)[order].reshape(outer, ffn_n, own, width)
        top = jnp.broadcast_to(grad_bias_up[None, :ffn_n, None], (outer, ffn_n, 1, width))
        small = jnp.concatenate([top, jnp.broadcast_to(sums[None, None, :7], (outer, ffn_n, 7, width))], axis=2)
        small = small.astype(bf16)
        payload = payload.reshape(ffn_n, 2, outer, up_rows, width).transpose(2, 0, 1, 3, 4)
        payload = jnp.concatenate([payload.reshape(outer, ffn_n, at, width), grad_out, small], axis=2)
        payload = jnp.pad(payload, ((0, 0), (0, 0), (0, -payload.shape[2] % 32), (0, 0)))
    payload, apart, do = lax.optimization_barrier((payload, apart, do))
    total = lax.psum_scatter(payload.reshape(-1, width), ("dp", "seq"), scatter_dimension=0, tiled=True)
    if apart is not None:
        apart = lax.all_to_all(
            apart.reshape(devices, APART, width), ALL, split_axis=0, concat_axis=0, tiled=True
        )

    got = attention_backward(
        me_ref, rand, global_blocks, do, k_all, v_all, q_all, mask_all, seg, lse_near, lse_far, lseg, w_own,
        grad_resid_one,
    )
    dq, dkv, grad_features = got[:3]
    part = [None] + list(got[3:])
    bit = 1
    while bit < seq_n:
        for k in range(seq_n):
            if k & -k == bit and k != bit:
                came = flip_send(part[k], "seq", bit).astype(f32)
                part[k ^ bit] = (part[k ^ bit].astype(f32) + came).astype(bf16)
        bit *= 2
    grad_w = projection_gradients(near, dq, dkv, own, devices)
    grad_w, part = lax.optimization_barrier((grad_w, part[1:]))
    grad_w, apart = lax.optimization_barrier((grad_w, apart))
    part = [None] + part
    bit = seq_n // 2
    part[bit], total = lax.optimization_barrier((part[bit], total))
    total = lax.psum_scatter(total, "ffn", scatter_dimension=0, tiled=True)
    while bit:
        grad_features = grad_features + flip_send(part[bit], "seq", bit).astype(f32)
        bit //= 2
    grad_w = lax.all_to_all(grad_w, ALL, split_axis=0, concat_axis=0, tiled=True)
    if direct:
        out_up, out_down, out_output, notes = finished(total, up_rows, own)
    else:
        total = total.astype(f32)
        out_up, out_down, out_output = total[:up_rows], total[up_rows:at], total[at : at + own]
        notes = total[at + own : at + own + 8]
    out_bias_up = notes[0]
    out_vecs = lax.dynamic_slice(notes, (1, here * own), (6, own))
    out_query, out_key, out_value, col_sums = unpacked_gradients(
        grad_w.reshape(dp_n, seq_n, ffn_n, own_pad, lanes), own, width
    )
    col = lax.dynamic_index_in_dim(col_sums, here // share, keepdims=False)[:own, HEAD_DIM : HEAD_DIM + 2]
    out_b = [col[:, 0], col[:, 1]]
    return (
        out[None],
        grad_features[None],
        out_query,
        out_key,
        out_value,
        out_output,
        out_b[0],
        out_b[1],
        out_vecs[0],
        out_up,
        out_bias_up,
        out_down,
        out_vecs[1],
        out_vecs[2],
        out_vecs[3],
        out_vecs[4],
        out_vecs[5],
    )


def solution(mesh):
    return jax.shard_map(
        shards,
        mesh=mesh,
        in_specs=(
            P(("dp", "ffn"), "seq", None),
            P(("dp", "seq", "ffn"), None),
            P(("dp", "seq", "ffn"), None),
            P(("dp", "seq", "ffn"), None),
            P(("dp", "seq", "ffn"), None),
            P(("dp", "seq", "ffn")),
            P(("dp", "seq", "ffn")),
            P(("dp", "seq", "ffn")),
            P(("dp", "seq"), "ffn"),
            P("ffn"),
            P(("dp", "seq"), "ffn"),
            P(("dp", "seq", "ffn")),
            P(("dp", "seq", "ffn")),
            P(("dp", "seq", "ffn")),
            P(("dp", "seq", "ffn")),
            P(("dp", "seq", "ffn")),
            P(("dp", "ffn"), None),
            P(("dp", "ffn"), "seq", None, None),
            P(("dp", "ffn"), None),
            P(("dp", "ffn"), "seq", None),
        ),
        out_specs=(
            P(("dp", "ffn"), "seq", None),
            P(("dp", "ffn"), "seq", None),
            P(("dp", "seq", "ffn"), None),
            P(("dp", "seq", "ffn"), None),
            P(("dp", "seq", "ffn"), None),
            P(("dp", "seq", "ffn"), None),
            P(("dp", "seq", "ffn")),
            P(("dp", "seq", "ffn")),
            P(("dp", "seq", "ffn")),
            P(("dp", "seq"), "ffn"),
            P("ffn"),
            P(("dp", "seq"), "ffn"),
            P(("dp", "seq", "ffn")),
            P(("dp", "seq", "ffn")),
            P(("dp", "seq", "ffn")),
            P(("dp", "seq", "ffn")),
            P(("dp", "seq", "ffn")),
        ),
        check_vma=False,
    )
```

```python
import functools
import jax
import jax.numpy as jnp
from jax import lax
from jax.experimental import pallas as pl
from jax.sharding import PartitionSpec as P
from jax.experimental.pallas import tpu as pltpu

HEAD_DIM = 64
BLOCK = 64
PAIR = 2 * BLOCK
MASKED = -1e30
bf16 = jnp.bfloat16
f32 = jnp.float32


def dot_nn(a, b):
    return lax.dot_general(a, b, (((1,), (0,)), ((), ())), preferred_element_type=f32)


def dot_nt(a, b):
    return lax.dot_general(a, b, (((1,), (1,)), ((), ())), preferred_element_type=f32)


def dot_tn(a, b):
    return lax.dot_general(a, b, (((0,), (0,)), ((), ())), preferred_element_type=f32)


def slots(rand_ref, glob_ref, flip, head, pair, nblocks):
    first = (2 * pair) ^ flip

    def row(block):
        return pl.multiple_of(block * BLOCK, BLOCK)

    def near(block):
        bad = (block < 0) | (block >= nblocks) | (block == glob_ref[0, 0]) | (block == glob_ref[0, 1])
        return row(jnp.where(bad, nblocks, block ^ flip))

    def drawn(block):
        at = (head * nblocks + block) * 3
        return [row(rand_ref[at + j] ^ flip) for j in range(3)]

    shared = [near(first), near(first + 1)] + [row(glob_ref[0, j] ^ flip) for j in range(2)]
    return shared, [near(first - 1)] + drawn(first), [near(first + 2)] + drawn(first + 1)


def stack_rows(ref, offsets, lanes):
    return jnp.concatenate([ref[pl.ds(o, BLOCK), lanes] for o in offsets], axis=0)


def lane_halves(width, dtype):
    lane = lax.broadcasted_iota(jnp.int32, (1, width), 1) % PAIR
    first = (lane < BLOCK).astype(dtype)
    second = (lane >= BLOCK).astype(dtype)
    return first, second


UNROLL = 4
BACK_UNROLL = 4
APART = 0
VMEM_BYTES = 62 << 20


def head_lanes(h):
    return slice(h * PAIR, (h + 1) * PAIR)


def query_columns(q_ref, mask_ref, h, at):
    return jnp.concatenate([q_ref[h * BLOCK : (h + 1) * BLOCK, pl.ds(at, PAIR)], mask_ref[:, pl.ds(at, PAIR)]], axis=0)


def global_queries(q_ref, mask_ref, h, gl):
    return jnp.concatenate(
        [
            global_columns(q_ref, slice(h * BLOCK, (h + 1) * BLOCK), gl),
            global_columns(mask_ref, slice(0, BLOCK), gl),
        ],
        axis=0,
    ).astype(bf16)


def placed(me_ref, glob_ref, nblocks, chunks):
    flip = me_ref[0] * (nblocks // chunks)
    return flip, [glob_ref[0, j] ^ flip for j in range(2)]


def global_columns(src_ref, rows, gl):
    lane = lax.broadcasted_iota(jnp.int32, (1, PAIR), 1)
    parts = []
    for g in range(2):
        block = gl[g]
        at = pl.multiple_of((block // 2) * PAIR, PAIR)
        both = src_ref[rows, pl.ds(at, PAIR)].astype(f32)
        moved = pltpu.roll(both, BLOCK, 1)
        parts.append(jnp.where(block % 2 == g, both, moved))
    return jnp.where(lane < BLOCK, parts[0], parts[1])


def put_global_columns(dst_ref, rows, gl, value, per_chunk, low, high):
    lane = lax.broadcasted_iota(jnp.int32, (1, PAIR), 1)
    moved = pltpu.roll(value, BLOCK, 1)
    for g in range(2):
        pair = gl[g] // 2
        half = gl[g] % 2
        chunk = pair // per_chunk

        @pl.when((chunk >= low) & (chunk < high))
        def _():
            at = pl.multiple_of((pair % per_chunk) * PAIR, PAIR)
            src = jnp.where(half == g, value, moved)
            old = dst_ref[chunk - low, rows, pl.ds(at, PAIR)].astype(f32)
            new = jnp.where((lane >= BLOCK) == (half == 1), src, old)
            dst_ref[chunk - low, rows, pl.ds(at, PAIR)] = new.astype(dst_ref.dtype)


def project_rows(x, seg, w_ref, wq, bkv_ref, bq_ref, k_ref, v_ref, q_ref, mask_ref, at):
    n = x.shape[0]
    lanes = v_ref.shape[1]
    y = dot_nn(x, w_ref[:, 0:lanes]) + bkv_ref[...]
    spot = lax.broadcasted_iota(jnp.int32, (PAIR, n), 0) - BLOCK
    mark = jnp.transpose((spot == seg).astype(f32), (1, 0))
    lane = lax.broadcasted_iota(jnp.int32, (1, PAIR), 1)
    rows = pl.ds(at, n)
    v_ref[rows, :] = y.astype(bf16)
    for h in range(lanes // PAIR):
        k_ref[rows, head_lanes(h)] = jnp.where(lane < BLOCK, y[:, head_lanes(h)], mark).astype(bf16)
    z = (dot_nt(wq, x) + bq_ref[...]).astype(bf16)
    q_ref[:, rows] = (z.astype(f32) * HEAD_DIM ** -0.5).astype(bf16)
    row = lax.broadcasted_iota(jnp.int32, (BLOCK, n), 0)
    mask_ref[:, rows] = jnp.where((row <= 16) & (row != seg), MASKED, 0.0).astype(bf16)


def query_weights(w_ref, heads):
    at = heads * PAIR
    cols = w_ref[:, at : at + 2 * PAIR].astype(f32)
    return jnp.transpose(cols, (1, 0))[0 : heads * HEAD_DIM].astype(bf16)


def sparse_forward(heads, low, high, per_chunk, rand_ref, glob_ref, flip, k_ref, kv_ref, q_ref, mask_ref, out_ref, lse_ref):
    nblocks = (k_ref.shape[0] - BLOCK) // BLOCK
    first, second = lane_halves(PAIR, bf16)
    lane = lax.broadcasted_iota(jnp.int32, (1, PAIR), 1)

    def one_pair(spot):
        chunk = spot // per_chunk
        local = pl.multiple_of((spot % per_chunk) * PAIR, PAIR)
        pair = low * per_chunk + spot
        at = pl.multiple_of(pair * PAIR, PAIR)
        for h in range(heads):
            shared, mine, other = slots(rand_ref, glob_ref, flip, h, pair, nblocks)
            kl = head_lanes(h)
            q = query_columns(q_ref, mask_ref, h, at)
            s_sh = dot_nn(stack_rows(k_ref, shared, kl), q)
            k_pr = jnp.concatenate([stack_rows(k_ref, mine, kl), stack_rows(k_ref, other, kl)], axis=1)
            s_pr = dot_nn(k_pr, jnp.concatenate([q * first, q * second], axis=0))
            peak = jnp.maximum(jnp.max(s_sh, axis=0, keepdims=True), jnp.max(s_pr, axis=0, keepdims=True))
            e_sh = jnp.exp(s_sh - peak)
            e_pr = jnp.exp(s_pr - peak)
            total = jnp.sum(e_sh, axis=0, keepdims=True) + jnp.sum(e_pr, axis=0, keepdims=True)
            inv = 1.0 / total
            p_sh = (e_sh * inv).astype(bf16)
            p_pr = (e_pr * inv).astype(bf16)
            v_pr = jnp.concatenate([stack_rows(kv_ref, mine, kl), stack_rows(kv_ref, other, kl)], axis=1)
            o_sh = dot_tn(stack_rows(kv_ref, shared, kl), p_sh)
            o_pr = dot_tn(v_pr, p_pr)
            ctx = o_sh[BLOCK:PAIR] + jnp.where(lane < BLOCK, o_pr[BLOCK:PAIR], o_pr[PAIR + BLOCK : 2 * PAIR])
            out_ref[chunk, h * BLOCK : (h + 1) * BLOCK, pl.ds(local, PAIR)] = ctx.astype(bf16)
            lse_ref[h, pl.ds(spot, 1), :] = peak + jnp.log(total)

    @pl.loop(0, (high - low) * per_chunk // UNROLL)
    def _(some):
        for i in range(UNROLL):
            one_pair(UNROLL * some + i)


def forward_kernel(heads, chunks, me_ref, rand_ref, glob_ref, *refs):
    x_refs = refs[0:chunks]
    seg_ref, w_ref, bkv_ref, bq_ref = refs[chunks : chunks + 4]
    far = chunks // 2
    out_refs = refs[chunks + 4 : chunks + 4 + far]
    lse_ref, lseg_ref, glob_ctx_ref = refs[chunks + 4 + far : chunks + 7 + far]
    saved_refs = refs[chunks + 7 + far : chunks + 11 + far]
    s_sc, out_ref, seg_sc, k_sc, v_sc, q_sc, mask_sc, sems = refs[chunks + 11 + far :]
    rows = x_refs[0].shape[0]
    length = rows * chunks
    per_chunk = length // PAIR // chunks
    flip, gl = placed(me_ref, glob_ref, length // BLOCK, chunks)
    tile = 256
    wq = query_weights(w_ref, heads)
    for c in range(chunks):
        seg_sc[c : c + 1, :] = seg_ref[pl.ds(me_ref[0] ^ c, 1), :]
    for c in range(chunks):

        @pl.loop(0, rows // tile)
        def _(t):
            at = pl.multiple_of(t * tile, tile)
            project_rows(
                x_refs[c][pl.ds(at, tile), :], seg_sc[c : c + 1, pl.ds(at, tile)], w_ref, wq, bkv_ref, bq_ref,
                k_sc, v_sc, q_sc, mask_sc, pl.multiple_of(c * rows + t * tile, tile),
            )

    null_lane = lax.broadcasted_iota(jnp.int32, (BLOCK, heads * PAIR), 1) % PAIR
    k_sc[pl.ds(length, BLOCK), :] = (null_lane == BLOCK + 16).astype(f32).astype(bf16)
    v_sc[pl.ds(length, BLOCK), :] = jnp.zeros((BLOCK, heads * PAIR), bf16)
    saves = [
        pltpu.make_async_copy(src, dst, sems.at[i])
        for i, (src, dst) in enumerate(zip((k_sc, v_sc, q_sc, mask_sc), saved_refs))
    ]
    for save in saves:
        save.start()
    sparse_forward(heads, far, chunks, per_chunk, rand_ref, glob_ref, flip, k_sc, v_sc, q_sc, mask_sc, out_ref, lse_ref)

    step = 512
    queries = [global_queries(q_sc, mask_sc, h, gl) for h in range(heads)]

    def score(c, peaks):
        at = pl.multiple_of(c * step, step)
        new = []
        for h in range(heads):
            got = dot_nn(k_sc[pl.ds(at, step), head_lanes(h)], queries[h])
            s_sc[h, pl.ds(at, step), :] = got
            new.append(jnp.maximum(peaks[h], jnp.max(got, axis=0, keepdims=True)))
        return tuple(new)

    peaks = lax.fori_loop(0, length // step, score, (jnp.full((1, PAIR), MASKED, f32),) * heads)

    def gather(c, carry):
        at = pl.multiple_of(c * step, step)
        new = []
        for h in range(heads):
            total, ctx = carry[h]
            e = jnp.exp(s_sc[h, pl.ds(at, step), :] - peaks[h])
            ctx = ctx + dot_tn(v_sc[pl.ds(at, step), head_lanes(h)], e.astype(bf16))
            new.append((total + jnp.sum(e, axis=0, keepdims=True), ctx))
        return tuple(new)

    start = (jnp.zeros((1, PAIR), f32), jnp.zeros((PAIR, PAIR), f32))
    sums = lax.fori_loop(0, length // step, gather, (start,) * heads)
    for h in range(heads):
        total, ctx = sums[h]
        ctx = ctx[BLOCK:PAIR] * (1.0 / total)
        glob_ctx_ref[h] = ctx
        put_global_columns(out_ref, slice(h * BLOCK, (h + 1) * BLOCK), gl, ctx, per_chunk, far, chunks)
        lseg_ref[h : h + 1, :] = peaks[h] + jnp.log(total)
    for c in range(far):
        out_refs[c][...] = out_ref[c]
    for save in saves:
        save.wait()


def attention_forward(me, rand, glob, x, seg, w, b_kv, b_q):
    chunks = len(x)
    far = chunks // 2
    rows = x[0].shape[0]
    length = rows * chunks
    heads = b_q.shape[0] // HEAD_DIM
    whole = lambda: pl.BlockSpec(memory_space=pltpu.VMEM)
    got = pl.pallas_call(
        functools.partial(forward_kernel, heads, chunks),
        out_shape=(jax.ShapeDtypeStruct((heads * HEAD_DIM, rows), bf16),) * far
        + (
            jax.ShapeDtypeStruct((heads, length // PAIR // 2, PAIR), f32),
            jax.ShapeDtypeStruct((heads, PAIR), f32),
            jax.ShapeDtypeStruct((heads, HEAD_DIM, PAIR), f32),
            jax.ShapeDtypeStruct((length + BLOCK, heads * PAIR), bf16),
            jax.ShapeDtypeStruct((length + BLOCK, heads * PAIR), bf16),
            jax.ShapeDtypeStruct((heads * HEAD_DIM, length), bf16),
            jax.ShapeDtypeStruct((BLOCK, length), bf16),
        ),
        in_specs=[pl.BlockSpec(memory_space=pltpu.SMEM)] * 3 + [whole() for _ in range(chunks + 4)],
        out_specs=tuple([whole() for _ in range(far + 3)] + [pl.BlockSpec(memory_space=pl.ANY)] * 4),
        scratch_shapes=[
            pltpu.VMEM((heads, length, PAIR), f32),
            pltpu.VMEM((far, heads * HEAD_DIM, rows), bf16),
            pltpu.VMEM((chunks, rows), jnp.int32),
            pltpu.VMEM((length + BLOCK, heads * PAIR), bf16),
            pltpu.VMEM((length + BLOCK, heads * PAIR), bf16),
            pltpu.VMEM((heads * HEAD_DIM, length), bf16),
            pltpu.VMEM((BLOCK, length), bf16),
            pltpu.SemaphoreType.DMA((4,)),
        ],
        compiler_params=pltpu.CompilerParams(vmem_limit_bytes=VMEM_BYTES),
        cost_estimate=pl.CostEstimate(flops=10_000_000_000, bytes_accessed=16_000_000, transcendentals=6_000_000),
        name="attention_forward",
    )(me, rand, glob, *x, seg, w, b_kv, b_q)
    return got[:far], got[far:]


def near_kernel(heads, chunks, me_ref, rand_ref, glob_ref, k_ref, kv_ref, q_ref, mask_ref, glob_ctx_ref, *refs):
    half = chunks // 2
    out_refs = refs[:half]
    lse_ref, out_ref = refs[half:]
    length = q_ref.shape[1]
    per_chunk = length // PAIR // chunks
    flip, gl = placed(me_ref, glob_ref, length // BLOCK, chunks)
    sparse_forward(heads, 0, half, per_chunk, rand_ref, glob_ref, flip, k_ref, kv_ref, q_ref, mask_ref, out_ref, lse_ref)
    for h in range(heads):
        put_global_columns(out_ref, slice(h * BLOCK, (h + 1) * BLOCK), gl, glob_ctx_ref[h], per_chunk, 0, half)
    for c in range(half):
        out_refs[c][...] = out_ref[c]


def attention_near(me, rand, glob, k, kv, q, mask, glob_ctx, chunks):
    heads = glob_ctx.shape[0]
    half = chunks // 2
    length = q.shape[1]
    rows = length // chunks
    whole = lambda: pl.BlockSpec(memory_space=pltpu.VMEM)
    got = pl.pallas_call(
        functools.partial(near_kernel, heads, chunks),
        out_shape=(jax.ShapeDtypeStruct((heads * HEAD_DIM, rows), bf16),) * half
        + (jax.ShapeDtypeStruct((heads, length // PAIR // 2, PAIR), f32),),
        in_specs=[pl.BlockSpec(memory_space=pltpu.SMEM)] * 3 + [whole() for _ in range(5)],
        out_specs=tuple(whole() for _ in range(half + 1)),
        scratch_shapes=[pltpu.VMEM((half, heads * HEAD_DIM, rows), bf16)],
        compiler_params=pltpu.CompilerParams(vmem_limit_bytes=VMEM_BYTES),
        cost_estimate=pl.CostEstimate(flops=6_000_000_000, bytes_accessed=9_000_000, transcendentals=3_000_000),
        name="attention_near",
    )(me, rand, glob, k, kv, q, mask, glob_ctx)
    return got[:half], got[half]


def backward_kernel(heads, chunks, me_ref, rand_ref, glob_ref, *refs):
    do_refs = refs[:chunks]
    (k_ref, kv_ref, q_ref, mask_ref, seg_ref, lse_near_ref, lse_far_ref, lseg_ref, w_ref, resid_hbm, dq_hbm, dkv_hbm,
     first_ref) = refs[chunks : chunks + 13]
    part_refs = refs[chunks + 13 : 2 * chunks + 12]
    (do_sc, acc, p_sc, d_sc, seg_sc, line_sc, lse_ref, row_sc, resid_ref, dq_ref, dkv_ref, sems) = refs[2 * chunks + 12 :]
    fetch = pltpu.make_async_copy(resid_hbm, resid_ref, sems.at[0])
    fetch.start()
    rows = do_refs[0].shape[1]
    length = rows * chunks
    npairs = length // PAIR
    per_chunk = npairs // chunks
    scale = HEAD_DIM ** -0.5
    flip, gl = placed(me_ref, glob_ref, length // BLOCK, chunks)
    lse_ref[:, 0 : npairs // 2, :] = lse_near_ref[...]
    lse_ref[:, npairs // 2 :, :] = lse_far_ref[...]
    for c in range(chunks):
        do_sc[:, c * rows : (c + 1) * rows] = do_refs[c][...]
        row_sc[c : c + 1, :] = seg_ref[pl.ds(me_ref[0] ^ c, 1), :].astype(f32)

        @pl.loop(0, per_chunk // 4)
        def _(some):
            for i in range(4):
                t = 4 * some + i
                line = row_sc[c : c + 1, pl.ds(pl.multiple_of(t * PAIR, PAIR), PAIR)]
                line_sc[c * per_chunk + t] = line
                to = pl.multiple_of(c * rows + t * PAIR, PAIR)
                seg_sc[pl.ds(to, PAIR), :] = jnp.transpose(jnp.broadcast_to(line, (PAIR, PAIR)), (1, 0))

    seg_sc[length : length + BLOCK, :] = jnp.full((BLOCK, PAIR), -1.0, f32)
    first2, second2 = lane_halves(2 * PAIR, bf16)
    ffirst, fsecond = lane_halves(PAIR, f32)
    lane = lax.broadcasted_iota(jnp.int32, (1, PAIR), 1)
    line_row = lax.broadcasted_iota(jnp.int32, (PAIR, 1), 0)
    zeros = jnp.zeros((BLOCK, PAIR), bf16)
    blank = jnp.zeros((PAIR, PAIR), bf16)

    def head_rows(h):
        return slice(h * BLOCK, (h + 1) * BLOCK)

    def joint(q, mask, do):
        left = jnp.concatenate([q, mask, blank], axis=0)
        right = jnp.concatenate([blank, zeros, do], axis=0)
        return jnp.concatenate([left, right], axis=1)

    def sources(q, do):
        top = jnp.concatenate([q, zeros], axis=1)
        return jnp.concatenate([top, jnp.concatenate([zeros, do], axis=1)], axis=0)

    step = 512
    mask_glob = global_columns(mask_ref, slice(0, BLOCK), gl).astype(bf16)
    q_glob = [global_columns(q_ref, head_rows(h), gl).astype(bf16) for h in range(heads)]
    do_glob = [global_columns(do_sc, head_rows(h), gl).astype(bf16) for h in range(heads)]

    def weigh(c, deltas):
        at = pl.multiple_of(c * step, step)
        new = []
        for h in range(heads):
            left = jnp.concatenate([k_ref[pl.ds(at, step), head_lanes(h)], kv_ref[pl.ds(at, step), head_lanes(h)]], axis=1)
            both = dot_nn(left, joint(q_glob[h], mask_glob, do_glob[h]))
            p = jnp.exp(both[:, 0:PAIR] - lseg_ref[h : h + 1, :])
            dp = both[:, PAIR:]
            p_sc[h, pl.ds(at, step), :] = p
            d_sc[h, pl.ds(at, step), :] = dp
            new.append(deltas[h] + jnp.sum(p * dp, axis=0, keepdims=True))
        return tuple(new)

    deltas = lax.fori_loop(0, length // step, weigh, (jnp.zeros((1, PAIR), f32),) * heads)

    def spread(c, dqs):
        at = pl.multiple_of(c * step, step)
        new = []
        for h in range(heads):
            p = p_sc[h, pl.ds(at, step), :]
            ds = (p * (d_sc[h, pl.ds(at, step), :] - deltas[h])).astype(bf16)
            both = jnp.concatenate([ds, p.astype(bf16)], axis=1)
            acc[h, pl.ds(at, step), :] = dot_nt(both, sources(q_glob[h], do_glob[h]))
            new.append(dqs[h] + dot_tn(k_ref[pl.ds(at, step), head_lanes(h)], ds))
        return tuple(new)

    dqs = lax.fori_loop(0, length // step, spread, (jnp.zeros((PAIR, PAIR), f32),) * heads)
    for h in range(heads):
        acc[h, pl.ds(length, BLOCK), :] = jnp.zeros((BLOCK, PAIR), f32)

    def one_pair(pair):
        chunk = pair // per_chunk
        local = pl.multiple_of((pair % per_chunk) * PAIR, PAIR)
        at = pl.multiple_of(pair * PAIR, PAIR)
        hit_first = (gl[0] == 2 * pair) | (gl[1] == 2 * pair)
        hit_second = (gl[0] == 2 * pair + 1) | (gl[1] == 2 * pair + 1)
        shut = ffirst * jnp.where(hit_first, -MASKED, 0.0) + fsecond * jnp.where(hit_second, -MASKED, 0.0)
        every = slice(0, PAIR)
        for h in range(heads):
            kl = head_lanes(h)
            shared, mine, other = slots(rand_ref, glob_ref, flip, h, pair, length // BLOCK)
            q = q_ref[head_rows(h), pl.ds(at, PAIR)]
            do = do_sc[head_rows(h), pl.ds(at, PAIR)]
            lse = lse_ref[h, pl.ds(pair, 1), :] + shut
            src = sources(q, do)
            src2 = jnp.concatenate([src * first2, src * second2], axis=0)
            k_sh = stack_rows(k_ref, shared, kl)
            two_sh = dot_nn(
                jnp.concatenate([k_sh, stack_rows(kv_ref, shared, kl)], axis=1),
                joint(q, mask_ref[:, pl.ds(at, PAIR)], do),
            )
            kv_pr = jnp.concatenate([stack_rows(kv_ref, mine, kl), stack_rows(kv_ref, other, kl)], axis=1)
            two_pr = dot_nn(kv_pr, src2)
            seg_pr = jnp.where(lane < BLOCK, stack_rows(seg_sc, mine, every), stack_rows(seg_sc, other, every))
            agree = seg_pr == line_sc[pair]
            p_sh = jnp.exp(two_sh[:, 0:PAIR] - lse)
            p_pr = jnp.where(agree, jnp.exp(two_pr[:, 0:PAIR] - lse), 0.0)
            d_sh, d_pr = two_sh[:, PAIR:], two_pr[:, PAIR:]
            delta = jnp.sum(p_sh * d_sh, axis=0, keepdims=True) + jnp.sum(p_pr * d_pr, axis=0, keepdims=True)
            ds_sh = (p_sh * (d_sh - delta)).astype(bf16)
            ds_pr = (p_pr * (d_pr - delta)).astype(bf16)
            g_sh = dot_nt(jnp.concatenate([ds_sh, p_sh.astype(bf16)], axis=1), src)
            g_pr = dot_nt(jnp.concatenate([ds_pr, p_pr.astype(bf16)], axis=1), src2)
            for j, o in enumerate(shared):
                acc[h, pl.ds(o, BLOCK), :] += g_sh[j * BLOCK : (j + 1) * BLOCK]
            for j, o in enumerate(mine):
                acc[h, pl.ds(o, BLOCK), :] += g_pr[j * BLOCK : (j + 1) * BLOCK, 0:PAIR]
            for j, o in enumerate(other):
                acc[h, pl.ds(o, BLOCK), :] += g_pr[j * BLOCK : (j + 1) * BLOCK, PAIR:]
            t_pr = dot_tn(ds_pr, kv_pr)
            dq = dot_tn(ds_sh, k_sh) + jnp.where(line_row < BLOCK, t_pr[:, 0:PAIR], t_pr[:, PAIR:])
            dq = jnp.transpose(dq, (1, 0))[0:BLOCK]
            dq_ref[chunk, head_rows(h), pl.ds(local, PAIR)] = (dq * scale).astype(bf16)

    @pl.loop(0, npairs // BACK_UNROLL)
    def _(some):
        for i in range(BACK_UNROLL):
            one_pair(BACK_UNROLL * some + i)

    for h in range(heads):
        put_global_columns(dq_ref, head_rows(h), gl, dqs[h][0:BLOCK] * scale, per_chunk, 0, chunks)
        for c in range(chunks):
            dkv_ref[c, :, head_lanes(h)] = acc[h, pl.ds(c * rows, rows), :].astype(bf16)
    saves = [
        pltpu.make_async_copy(dq_ref, dq_hbm, sems.at[1]),
        pltpu.make_async_copy(dkv_ref, dkv_hbm, sems.at[2]),
    ]
    for save in saves:
        save.start()
    fetch.wait()
    tile = 256
    wq = query_weights(w_ref, heads)
    for c in range(chunks):

        @pl.loop(0, rows // tile)
        def _(t):
            at = pl.multiple_of(t * tile, tile)
            got = dot_tn(dq_ref[c, :, pl.ds(at, tile)], wq)
            got = got + dot_nt(dkv_ref[c, pl.ds(at, tile), :], w_ref[:, 0 : heads * PAIR])
            if c == 0:
                first_ref[pl.ds(at, tile), :] = resid_ref[pl.ds(at, tile), :] + got
            else:
                part_refs[c - 1][pl.ds(at, tile), :] = got.astype(bf16)
    for save in saves:
        save.wait()


def attention_backward(me, rand, glob, do, k, kv, q, mask, seg, lse_near, lse_far, lseg, w, resid):
    chunks = len(do)
    group, rows = do[0].shape
    heads = group // HEAD_DIM
    width = w.shape[0]
    length = rows * chunks
    whole = lambda: pl.BlockSpec(memory_space=pltpu.VMEM)
    return pl.pallas_call(
        functools.partial(backward_kernel, heads, chunks),
        out_shape=(
            jax.ShapeDtypeStruct((chunks, group, rows), bf16),
            jax.ShapeDtypeStruct((chunks, rows, heads * PAIR), bf16),
            jax.ShapeDtypeStruct((rows, width), f32),
        )
        + (jax.ShapeDtypeStruct((rows, width), bf16),) * (chunks - 1),
        in_specs=[pl.BlockSpec(memory_space=pltpu.SMEM)] * 3
        + [whole() for _ in range(chunks + 9)]
        + [pl.BlockSpec(memory_space=pl.ANY)],
        out_specs=tuple([pl.BlockSpec(memory_space=pl.ANY)] * 2 + [whole() for _ in range(chunks)]),
        scratch_shapes=[
            pltpu.VMEM((group, length), bf16),
            pltpu.VMEM((heads, length + BLOCK, PAIR), f32),
            pltpu.VMEM((heads, length, PAIR), f32),
            pltpu.VMEM((heads, length, PAIR), f32),
            pltpu.VMEM((length + BLOCK, PAIR), f32),
            pltpu.VMEM((length // PAIR, 1, PAIR), f32),
            pltpu.VMEM((heads, length // PAIR, PAIR), f32),
            pltpu.VMEM((chunks, rows), f32),
            pltpu.VMEM((rows, width), f32),
            pltpu.VMEM((chunks, group, rows), bf16),
            pltpu.VMEM((chunks, rows, heads * PAIR), bf16),
            pltpu.SemaphoreType.DMA((3,)),
        ],
        compiler_params=pltpu.CompilerParams(vmem_limit_bytes=VMEM_BYTES),
        cost_estimate=pl.CostEstimate(flops=30_000_000_000, bytes_accessed=24_000_000, transcendentals=8_000_000),
        name="attention_backward",
    )(me, rand, glob, *do, k, kv, q, mask, seg, lse_near, lse_far, lseg, w, resid)


def round_up(value, to):
    return -(-value // to) * to


def half_columns(ref, index, place):
    at = index // 2 * PAIR
    both = ref[:, at : at + PAIR].astype(f32)
    return both if index % 2 == place else pltpu.roll(both, BLOCK, 1)


def two_halves(first, second):
    lane = lax.broadcasted_iota(jnp.int32, (1, PAIR), 1)
    return jnp.where(lane < BLOCK, first, second)


def pack_kernel(seq_n, wq_ref, wk_ref, wv_ref, vec_ref, pack_ref):
    own, width = wq_ref.shape
    heads = width // HEAD_DIM // seq_n
    blocks, inner = pack_ref.shape[0], pack_ref.shape[2]
    for s in range(seq_n):
        pieces = [
            two_halves(half_columns(wk_ref, s * heads + h, 0), half_columns(wv_ref, s * heads + h, 1))
            for h in range(heads)
        ]
        for h in range(0, heads, 2):
            second = half_columns(wq_ref, s * heads + h + 1, 1) if h + 1 < heads else vec_ref[...].astype(f32)
            pieces.append(two_halves(half_columns(wq_ref, s * heads + h, 0), second))
        piece = jnp.concatenate(pieces, axis=1).astype(bf16)
        for b in range(blocks):
            for i in range(inner):
                pack_ref[b, s, i] = piece


def rest_kernel(wo_ref, up_ref, down_ref, bup_ref, rest_ref):
    own, width = wo_ref.shape
    u = up_ref.shape[0]
    rest_ref[0:u, :] = up_ref[...]
    rest_ref[u : 2 * u, :] = down_ref[...]
    rest_ref[2 * u : 2 * u + own, :] = wo_ref[...]
    rest_ref[2 * u + own : 2 * u + own + 8, :] = jnp.broadcast_to(bup_ref[...], (8, width))


def packed_weights(w_q, w_k, w_v, w_o, w_up, w_down, b_up, vec, dp_n, seq_n, ffn_n):
    own, width = w_q.shape
    heads = width // HEAD_DIM // seq_n
    lanes = heads * PAIR + round_up(heads * HEAD_DIM, PAIR)
    u = w_up.shape[0]
    if own % 8 or u % 16:
        group = heads * HEAD_DIM
        cols = lambda w: w.reshape(own, seq_n, heads, HEAD_DIM).transpose(1, 0, 2, 3)
        kv = jnp.stack([cols(w_k), cols(w_v)], axis=3).reshape(seq_n, own, 2 * group)
        notes = jnp.broadcast_to(vec[None, :, HEAD_DIM:], (seq_n, own, PAIR - HEAD_DIM))
        piece = jnp.concatenate([kv, cols(w_q).reshape(seq_n, own, group), notes], axis=2)
        piece = jnp.pad(piece, ((0, 0), (0, round_up(own, 8) - own), (0, 0)))
        pack = jnp.broadcast_to(piece[None, :, None], (dp_n, seq_n, ffn_n) + piece.shape[1:])
        w_o = jnp.pad(w_o, ((0, round_up(own, 8) - own), (0, 0)))
        return pack, jnp.concatenate([w_up, w_down, w_o, jnp.broadcast_to(b_up, (8, width))], axis=0)
    whole = lambda: pl.BlockSpec(memory_space=pltpu.VMEM)
    rest = pl.pallas_call(
        rest_kernel,
        out_shape=jax.ShapeDtypeStruct((2 * u + own + 8, width), bf16),
        in_specs=[whole() for _ in range(4)],
        out_specs=whole(),
        name="rest_weights",
    )(w_o, w_up, w_down, b_up)
    pack = pl.pallas_call(
        functools.partial(pack_kernel, seq_n),
        out_shape=jax.ShapeDtypeStruct((dp_n, seq_n, ffn_n, own, lanes), bf16),
        in_specs=[whole() for _ in range(4)],
        out_specs=whole(),
        name="packed_weights",
    )(w_q, w_k, w_v, vec)
    return pack, rest


def weights_kernel(chunks, direct, *refs):
    x_refs = refs[:chunks]
    dq_ref, dkv_ref, out_ref, acc, sum_sc = refs[chunks:]
    group = dq_ref.shape[1]
    lanes = dkv_ref.shape[2]
    full, width = acc.shape
    x = jnp.concatenate([r[...] for r in x_refs], axis=0)
    dkv = jnp.concatenate([dkv_ref[c] for c in range(chunks)], axis=0)
    dq = jnp.concatenate([dq_ref[c] for c in range(chunks)], axis=1)
    ones = jnp.ones((8, x.shape[0]), bf16)

    @pl.when(pl.program_id(0) == 0)
    def _():
        acc[...] = jnp.zeros_like(acc)
        sum_sc[...] = jnp.zeros_like(sum_sc)

    acc[0:lanes, :] += dot_tn(dkv, x)
    acc[lanes : lanes + group, :] += dot_nn(dq, x)
    sum_sc[:, 0:lanes] += dot_nn(ones, dkv)
    sum_sc[:, lanes : lanes + group] += dot_nt(ones, dq)

    @pl.when(pl.program_id(0) == pl.num_programs(0) - 1)
    def _():
        lane = lax.broadcasted_iota(jnp.int32, (full, width), 0)
        spot = lax.broadcasted_iota(jnp.int32, (full, width), 1) % group
        pick_q = lane - lanes == spot
        pick_v = (lane < lanes) & (lane % PAIR >= BLOCK) & (lane // PAIR * BLOCK + lane % BLOCK == spot)
        sums = sum_sc[...].astype(bf16)
        row = lax.broadcasted_iota(jnp.int32, (8, width), 0)
        of_q = dot_nn(sums, pick_q.astype(f32).astype(bf16))
        of_v = dot_nn(sums, pick_v.astype(f32).astype(bf16))
        acc[lanes + group : lanes + group + 8, :] = jnp.where(row == 0, of_q, of_v)
        grad = jnp.transpose(acc[...], (1, 0))
        if direct:
            blocks, own, _ = out_ref.shape
            grad = grad.reshape(blocks, own, full)
            for b in range(blocks):
                out_ref[b] = grad[b].astype(bf16)
        else:
            out_ref[...] = grad.astype(bf16)


def projection_gradients(x, dq, dkv, own, devices):
    chunks, group, rows = dq.shape
    width = x[0].shape[1]
    lanes = dkv.shape[2]
    full = lanes + round_up(group, PAIR)
    direct = own % 8 == 0
    tile = 256
    shape = (devices, own, full) if direct else (width, full)
    out = pl.pallas_call(
        functools.partial(weights_kernel, chunks, direct),
        grid=(rows // tile,),
        out_shape=jax.ShapeDtypeStruct(shape, bf16),
        in_specs=[pl.BlockSpec((tile, width), lambda i: (i, 0)) for _ in range(chunks)]
        + [
            pl.BlockSpec((chunks, group, tile), lambda i: (0, 0, i)),
            pl.BlockSpec((chunks, tile, lanes), lambda i: (0, i, 0)),
        ],
        out_specs=pl.BlockSpec(shape, lambda i: (0,) * len(shape), pipeline_mode=pl.Buffered(1)),
        scratch_shapes=[pltpu.VMEM((full, width), f32), pltpu.VMEM((8, full), f32)],
        compiler_params=pltpu.CompilerParams(vmem_limit_bytes=VMEM_BYTES),
        cost_estimate=pl.CostEstimate(flops=4_000_000_000, bytes_accessed=12_000_000, transcendentals=0),
        name="projection_gradients",
    )(*x, dq, dkv)
    if not direct:
        out = jnp.pad(out.reshape(devices, own, full), ((0, 0), (0, round_up(own, 8) - own), (0, 0)))
    return out


def unpack_kernel(own, got_ref, q_ref, k_ref, v_ref, sums_ref, tot):
    dp_n, seq_n, ffn_n, per, full = got_ref.shape
    width = q_ref.shape[1]
    heads = width // HEAD_DIM // seq_n
    for s in range(seq_n):
        total = jnp.zeros((per, full), f32)
        for d in range(dp_n):
            for f in range(ffn_n):
                total = total + got_ref[d, s, f].astype(f32)
        tot[s] = total
        sums_ref[s] = total[:, full - PAIR :]
    for w in range(width // PAIR):
        spots = [((2 * w + i) // heads, (2 * w + i) % heads) for i in range(2)]
        cols = slice(w * PAIR, (w + 1) * PAIR)
        for ref, where in (
            (k_ref, lambda h: 2 * h),
            (v_ref, lambda h: 2 * h + 1),
            (q_ref, lambda h: 2 * heads + h),
        ):
            both = [half_columns(tot.at[g], where(h), i) for i, (g, h) in enumerate(spots)]
            ref[:, cols] = two_halves(*both)[0:own]


def unpacked_gradients(got, own, width):
    dp_n, seq_n, ffn_n, per, full = got.shape
    whole = lambda: pl.BlockSpec(memory_space=pltpu.VMEM)
    return pl.pallas_call(
        functools.partial(unpack_kernel, own),
        out_shape=(jax.ShapeDtypeStruct((own, width), f32),) * 3 + (jax.ShapeDtypeStruct((seq_n, per, PAIR), f32),),
        in_specs=[whole()],
        out_specs=tuple(whole() for _ in range(4)),
        scratch_shapes=[pltpu.VMEM((seq_n, per, full), f32)],
        compiler_params=pltpu.CompilerParams(vmem_limit_bytes=VMEM_BYTES),
        cost_estimate=pl.CostEstimate(flops=40_000_000_000, bytes_accessed=3_000_000, transcendentals=0),
        name="unpacked_gradients",
    )(got)


NORM_EPS = 1e-12


def transposed(value):
    return jnp.transpose(value.astype(f32), (1, 0)).astype(bf16)


def unit_rows(value):
    center = value - jnp.mean(value, axis=-1, keepdims=True)
    scale = lax.rsqrt(jnp.mean(center * center, axis=-1, keepdims=True) + NORM_EPS)
    return center * scale, scale


def unit_rows_back(grad, unit, scale):
    return scale * (
        grad - jnp.mean(grad, axis=-1, keepdims=True) - unit * jnp.mean(grad * unit, axis=-1, keepdims=True)
    )


def rows_kernel(parts, blocks, up_rows, own, me_ref, *refs):
    ctx_refs = refs[:parts]
    (x_ref, cot_ref, rest_ref, wo_ref, vec_ref, bup_ref, out_ref, resid_ref, hid_ref, pre_ref, nlt_ref, gft_ref,
     gb_ref) = refs[parts : parts + 13]
    do_refs = refs[parts + 13 : 2 * parts + 13]
    sums_ref, gbup_ref, slope_sc, wo_sc, wide_sc = refs[2 * parts + 13 :]
    group = ctx_refs[0].shape[0]
    width = x_ref.shape[1]

    def up(f):
        return rest_ref[:, f, 0:up_rows, :].reshape(width, rest_ref.shape[3])

    def down(f):
        return rest_ref[:, f, up_rows : 2 * up_rows, :].reshape(width, rest_ref.shape[3])

    def own_rows(k):
        return pl.ds(pl.multiple_of((me_ref[0] ^ k) * group, group), group)

    @pl.when(pl.program_id(0) == 0)
    def _():
        sums_ref[...] = jnp.zeros_like(sums_ref)
        gbup_ref[...] = jnp.zeros_like(gbup_ref)
        if own:
            for o in range(rest_ref.shape[0]):
                for f in range(blocks):
                    to = (o * blocks + f) * own
                    wide_sc[to : to + own, :] = rest_ref[o, f, 2 * up_rows : 2 * up_rows + own, :].astype(f32)
            wo_sc[...] = wide_sc[...].astype(bf16)
        else:
            wo_sc[...] = wo_ref[...]

    def bias_up(f):
        if own:
            row = rest_ref[0, f, 2 * up_rows + own : 2 * up_rows + own + 8, :].astype(f32)
            return row[7:8, :]
        return bup_ref[f : f + 1, :]

    ctx = jnp.concatenate([r[...] for r in ctx_refs], axis=0)
    w_o = jnp.concatenate([wo_sc[own_rows(k), :] for k in range(parts)], axis=0)
    resid_one = x_ref[...].astype(f32) + (dot_tn(ctx, w_o) + vec_ref[0:1, :])
    unit_one, scale_one = unit_rows(resid_one)
    normed_one = unit_one * vec_ref[2:3, :] + vec_ref[3:4, :]
    low = normed_one.astype(bf16)
    nlt_ref[...] = transposed(normed_one)
    total = normed_one + vec_ref[1:2, :]
    pre = dot_nn(low, up(0)) + bias_up(0)
    for f in range(blocks):
        later = dot_nn(low, up(f + 1)) + bias_up(f + 1) if f + 1 < blocks else None
        phi = 0.5 + 0.5 * lax.erf(pre * (0.5 ** 0.5))
        slope_sc[f] = phi + pre * (jnp.exp(-0.5 * pre * pre) * 0.3989422804014327)
        hid = (pre * phi).astype(bf16)
        hid_ref[f] = hid
        total = total + dot_nt(hid, down(f))
        pre = later
    unit_two, scale_two = unit_rows(total)
    out_ref[...] = (unit_two * vec_ref[4:5, :] + vec_ref[5:6, :]).astype(bf16)
    cot = cot_ref[...].astype(f32)
    grad_two = unit_rows_back(cot * vec_ref[4:5, :], unit_two, scale_two)
    grad_ffn = grad_two.astype(bf16)
    gft_ref[...] = transposed(grad_two)
    grad_normed = grad_two
    back = dot_nn(grad_ffn, down(0))
    for f in range(blocks):
        later = dot_nn(grad_ffn, down(f + 1)) if f + 1 < blocks else None
        grad_pre = (back * slope_sc[f]).astype(bf16)
        pre_ref[f] = grad_pre
        gbup_ref[f : f + 1, :] += jnp.sum(grad_pre.astype(f32), axis=0, keepdims=True)
        grad_normed = grad_normed + dot_nt(grad_pre, up(f))
        back = later
    resid = unit_rows_back(grad_normed * vec_ref[2:3, :], unit_one, scale_one)
    resid_ref[...] = resid
    branch = resid.astype(bf16)
    gb_ref[...] = branch
    do = dot_nt(w_o, branch).astype(bf16)
    for k in range(parts):
        do_refs[k][...] = do[k * group : (k + 1) * group]
    for row, value in enumerate(
        (branch.astype(f32), grad_ffn.astype(f32), grad_normed * unit_one, grad_normed, cot * unit_two, cot)
    ):
        sums_ref[row : row + 1, :] += jnp.sum(value, axis=0, keepdims=True)


def rows_chain(me, ctx_parts, x, cot, rest, up_rows, own, w_o, vecs, bias_up):
    parts = len(ctx_parts)
    group, rows = ctx_parts[0].shape
    width = x.shape[1]
    outer, blocks, per, hidden = rest.shape
    tile = 256
    once = lambda shape: pl.BlockSpec(shape, lambda i: (0,) * len(shape), pipeline_mode=pl.Buffered(1))
    tall = pl.BlockSpec((tile, width), lambda i: (i, 0))
    wide = pl.BlockSpec((width, tile), lambda i: (0, i))
    cube = pl.BlockSpec((blocks, tile, hidden), lambda i: (0, i, 0))
    return pl.pallas_call(
        functools.partial(rows_kernel, parts, blocks, up_rows, own),
        grid=(rows // tile,),
        out_shape=(
            jax.ShapeDtypeStruct((rows, width), bf16),
            jax.ShapeDtypeStruct((rows, width), f32),
            jax.ShapeDtypeStruct((blocks, rows, hidden), bf16),
            jax.ShapeDtypeStruct((blocks, rows, hidden), bf16),
            jax.ShapeDtypeStruct((width, rows), bf16),
            jax.ShapeDtypeStruct((width, rows), bf16),
            jax.ShapeDtypeStruct((rows, width), bf16),
        )
        + (jax.ShapeDtypeStruct((group, rows), bf16),) * parts
        + (jax.ShapeDtypeStruct((8, width), f32), jax.ShapeDtypeStruct((8, hidden), f32)),
        in_specs=[pl.BlockSpec(memory_space=pltpu.SMEM)]
        + [pl.BlockSpec((group, tile), lambda i: (0, i))] * parts
        + [tall, tall, once(rest.shape), once(w_o.shape), once(vecs.shape), once(bias_up.shape)],
        out_specs=(
            tall, tall, cube, cube, wide, wide, tall,
        )
        + (pl.BlockSpec((group, tile), lambda i: (0, i)),) * parts
        + (pl.BlockSpec((8, width), lambda i: (0, 0)), pl.BlockSpec((8, hidden), lambda i: (0, 0))),
        scratch_shapes=[
            pltpu.VMEM((blocks, tile, hidden), f32),
            pltpu.VMEM((width, width), bf16),
            pltpu.VMEM((width, width), f32),
        ],
        compiler_params=pltpu.CompilerParams(vmem_limit_bytes=VMEM_BYTES),
        cost_estimate=pl.CostEstimate(flops=22_000_000_000, bytes_accessed=40_000_000, transcendentals=6_000_000),
        name="rows_chain",
    )(me, *ctx_parts, x, cot, rest, w_o, vecs, bias_up)


def outer_kernel(parts, up_rows, own, apart, me_ref, *refs):
    ctx_refs = refs[:parts]
    nlt_ref, gft_ref, gb_ref, pre_ref, hid_ref, sums_ref, gbup_ref, out_ref = refs[parts : parts + 8]
    wo_sc = refs[-1]
    slabs, hidden = out_ref.shape[0], out_ref.shape[3]
    group = ctx_refs[0].shape[0]
    f = pl.program_id(0)
    up = dot_nn(nlt_ref[...], pre_ref[0]).astype(bf16).reshape(slabs, up_rows, hidden)
    if apart:
        refs[parts + 8][:, 0, :, :] = up[:, 0:apart]
    out_ref[:, 0, 0 : up_rows - apart, :] = up[:, apart:]
    at = up_rows - apart
    down = dot_nn(gft_ref[...], hid_ref[0]).astype(bf16)
    out_ref[:, 0, at : at + up_rows, :] = down.reshape(slabs, up_rows, hidden)
    at += up_rows
    if not own:
        return

    @pl.when(f == 0)
    def _():
        for k in range(parts):
            wo_sc[k] = dot_nn(ctx_refs[k][...], gb_ref[...])

    share = slabs // parts
    stride = group // share
    for k in range(parts):
        for j in range(share):
            rows = pl.ds(pl.multiple_of(j * stride + f * own, 8), own)
            out_ref[(me_ref[0] ^ k) * share + j, 0, at : at + own, :] = wo_sc[k, rows, :].astype(bf16)
    small = jnp.concatenate([gbup_ref[pl.ds(f, 1), :], sums_ref[0:7, :]], axis=0).astype(bf16)
    for o in range(slabs):
        out_ref[o, 0, at + own :, :] = small


def outer_products(me, ctx_parts, nlt, gft, gb, pre, hid, sums, gbup, slabs, up_rows, own, apart):
    blocks, rows, hidden = pre.shape
    parts = len(ctx_parts)
    group = ctx_parts[0].shape[0]
    per = 2 * up_rows - apart + (own + 8 if own else 0)
    sizes = (per, apart) if apart else (per,)
    once = lambda shape: pl.BlockSpec(shape, lambda i: (0,) * len(shape), pipeline_mode=pl.Buffered(1))
    return pl.pallas_call(
        functools.partial(outer_kernel, parts, up_rows, own, apart),
        grid=(blocks,),
        out_shape=tuple(jax.ShapeDtypeStruct((slabs, blocks, r, hidden), bf16) for r in sizes),
        in_specs=[pl.BlockSpec(memory_space=pltpu.SMEM)]
        + [once(c.shape) for c in ctx_parts]
        + [
            once(nlt.shape),
            once(gft.shape),
            once(gb.shape),
            pl.BlockSpec((1, rows, hidden), lambda i: (i, 0, 0)),
            pl.BlockSpec((1, rows, hidden), lambda i: (i, 0, 0)),
            once(sums.shape),
            once(gbup.shape),
        ],
        out_specs=tuple(pl.BlockSpec((slabs, 1, r, hidden), lambda i: (0, i, 0, 0)) for r in sizes),
        scratch_shapes=[pltpu.VMEM((parts, group, gb.shape[1]), f32)],
        compiler_params=pltpu.CompilerParams(vmem_limit_bytes=VMEM_BYTES),
        cost_estimate=pl.CostEstimate(flops=11_000_000_000, bytes_accessed=28_000_000, transcendentals=0),
        name="outer_products",
    )(me, *ctx_parts, nlt, gft, gb, pre, hid, sums, gbup)


def finish_kernel(up_rows, own, total_ref, up_ref, down_ref, wo_ref, small_ref):
    rest = total_ref[...].astype(f32)
    up_ref[...] = rest[0:up_rows]
    down_ref[...] = rest[up_rows : 2 * up_rows]
    at = 2 * up_rows
    wo_ref[...] = rest[at : at + own]
    small_ref[...] = rest[at + own : at + own + 8]


def finished(total, up_rows, own):
    hidden = total.shape[1]
    whole = lambda: pl.BlockSpec(memory_space=pltpu.VMEM)
    return pl.pallas_call(
        functools.partial(finish_kernel, up_rows, own),
        out_shape=tuple(jax.ShapeDtypeStruct((r, hidden), f32) for r in (up_rows, up_rows, own, 8)),
        in_specs=[whole()],
        out_specs=tuple(whole() for _ in range(4)),
        name="finished",
    )(total)


ALL = ("dp", "seq", "ffn")


def flip_send(array, axis, bits):
    count = lax.axis_size(axis)
    return lax.ppermute(array, axis, [(i, i ^ bits) for i in range(count)])


def shards(
    tokens, w_query, w_key, w_value, w_output, b_query, b_value, b_output, w_up, b_up, w_down, b_down,
    gain_attn, shift_attn, gain_ffn, shift_ffn, segment_ids, random_blocks, global_blocks, cotangent,
):
    seq_n, dp_n, ffn_n = lax.axis_size("seq"), lax.axis_size("dp"), lax.axis_size("ffn")
    outer, devices = dp_n * seq_n, dp_n * seq_n * ffn_n
    me = lax.axis_index("seq")
    here = (lax.axis_index("dp") * seq_n + me) * ffn_n + lax.axis_index("ffn")
    own, width = w_query.shape
    own_pad = round_up(own, 8)
    group = width // seq_n
    heads = group // HEAD_DIM
    features = tokens[0]
    rows = features.shape[0]
    order = jnp.stack([me ^ k for k in range(seq_n)])
    me_ref = me.astype(jnp.int32)[None]

    near = [features] + [None] * (seq_n - 1)
    for k in sorted(range(1, seq_n), key=lambda k: (k & (k - 1), -k)):
        bit = k & -k
        near[k] = flip_send(features if bit == k else near[k ^ bit], "seq", bit)

    vec = jnp.stack([b_output, b_down, gain_attn, shift_attn, gain_ffn, shift_ffn, b_query, b_value], axis=1)
    vec = jnp.pad(vec, ((0, 0), (HEAD_DIM, PAIR - HEAD_DIM - 8)))
    seg = segment_ids[0].reshape(seq_n, rows)
    rand = random_blocks.reshape(-1)
    pack, rest = packed_weights(
        w_query, w_key, w_value, w_output, w_up, w_down, b_up[None], vec, dp_n, seq_n, ffn_n
    )
    lanes = pack.shape[4]
    pack, seg, rand = lax.optimization_barrier((pack, seg, rand))
    pack = lax.all_to_all(
        pack.reshape(devices, own_pad, lanes), ALL, split_axis=0, concat_axis=0, tiled=True
    )
    rest = lax.all_gather(rest, ALL, axis=0, tiled=False)
    w_own = pack[:, :own].reshape(width, lanes)
    share = devices // seq_n
    vecs = w_own[:, lanes - HEAD_DIM : lanes - HEAD_DIM + 8].astype(f32).T
    biases = lax.dynamic_slice(vecs, (6, me * group), (2, group))
    by_head = biases[1].reshape(heads, 1, HEAD_DIM)
    b_kv = jnp.concatenate([jnp.zeros_like(by_head), by_head], axis=1).reshape(1, heads * PAIR)

    far = seq_n // 2
    ctx_far, (lse_far, lseg, glob_ctx, k_all, v_all, q_all, mask_all) = attention_forward(
        me_ref, rand, global_blocks, near, seg, w_own, b_kv, biases[0][:, None]
    )
    ctx_parts = [None] * far + [flip_send(ctx_far[k - far], "seq", k) for k in range(far, seq_n)]
    ctx_near, lse_near = attention_near(
        me_ref, rand, global_blocks, k_all, v_all, q_all, mask_all, glob_ctx, seq_n
    )
    ctx_parts[far:], ctx_parts[0] = lax.optimization_barrier((ctx_parts[far:], ctx_near[0]))
    for k in range(1, far):
        ctx_parts[k] = flip_send(ctx_near[k], "seq", k)

    up_rows = w_up.shape[0]
    at = 2 * up_rows
    rest = rest.reshape(outer, ffn_n, rest.shape[1], width)
    w_o = rest[:, :, at : at + own].reshape(width, width)
    bias_up = rest[0, :, at + own_pad + 7].astype(f32)
    direct = up_rows % 16 == 0 and own % 8 == 0 and outer % seq_n == 0 and (outer // seq_n) * ffn_n * own == group
    if not direct:
        rest = rest[:, :, :at].reshape(outer, ffn_n, 2, up_rows, width).transpose(1, 2, 0, 3, 4)
        rest = rest.reshape(1, ffn_n, 2 * outer * up_rows, width)
    slabs, slab_rows = (outer, up_rows) if direct else (1, outer * up_rows)

    got = rows_chain(
        me_ref, ctx_parts, features, cotangent[0], rest, slab_rows, own if direct else 0,
        vecs if direct else w_o, vecs, vecs if direct else bias_up,
    )
    out, grad_resid_one, hidden, grad_pre, normed_t, grad_ffn_t, grad_branch = got[:7]
    grad_ctx, (sums, grad_bias_up) = got[7 : 7 + seq_n], got[7 + seq_n :]
    do = [grad_ctx[0]] + [flip_send(grad_ctx[k], "seq", k) for k in range(1, seq_n)]

    payload = outer_products(
        me_ref, ctx_parts, normed_t, grad_ffn_t, grad_branch, grad_pre, hidden, sums, grad_bias_up, slabs, slab_rows,
        own if direct else 0, APART if direct else 0,
    )
    payload, apart = payload if direct and APART else (payload[0], None)
    if not direct:
        grad_out = dot_nn(jnp.concatenate(ctx_parts, axis=0), grad_branch).astype(bf16)
        grad_out = grad_out.reshape(seq_n, group, width)[order].reshape(outer, ffn_n, own, width)
        top = jnp.broadcast_to(grad_bias_up[None, :ffn_n, None], (outer, ffn_n, 1, width))
        small = jnp.concatenate([top, jnp.broadcast_to(sums[None, None, :7], (outer, ffn_n, 7, width))], axis=2)
        small = small.astype(bf16)
        payload = payload.reshape(ffn_n, 2, outer, up_rows, width).transpose(2, 0, 1, 3, 4)
        payload = jnp.concatenate([payload.reshape(outer, ffn_n, at, width), grad_out, small], axis=2)
        payload = jnp.pad(payload, ((0, 0), (0, 0), (0, -payload.shape[2] % 32), (0, 0)))
    payload, apart, do = lax.optimization_barrier((payload, apart, do))
    total = lax.psum_scatter(payload.reshape(-1, width), ("dp", "seq"), scatter_dimension=0, tiled=True)
    if apart is not None:
        apart = lax.all_to_all(
            apart.reshape(devices, APART, width), ALL, split_axis=0, concat_axis=0, tiled=True
        )

    got = attention_backward(
        me_ref, rand, global_blocks, do, k_all, v_all, q_all, mask_all, seg, lse_near, lse_far, lseg, w_own,
        grad_resid_one,
    )
    dq, dkv, grad_features = got[:3]
    part = [None] + list(got[3:])
    bit = 1
    while bit < seq_n:
        for k in range(seq_n):
            if k & -k == bit and k != bit:
                came = flip_send(part[k], "seq", bit).astype(f32)
                part[k ^ bit] = (part[k ^ bit].astype(f32) + came).astype(bf16)
        bit *= 2
    grad_w = projection_gradients(near, dq, dkv, own, devices)
    grad_w, part = lax.optimization_barrier((grad_w, part[1:]))
    grad_w, apart = lax.optimization_barrier((grad_w, apart))
    part = [None] + part
    bit = seq_n // 2
    part[bit], total = lax.optimization_barrier((part[bit], total))
    total = lax.psum_scatter(total, "ffn", scatter_dimension=0, tiled=True)
    while bit:
        grad_features = grad_features + flip_send(part[bit], "seq", bit).astype(f32)
        bit //= 2
    grad_w = lax.all_to_all(grad_w, ALL, split_axis=0, concat_axis=0, tiled=True)
    if direct:
        out_up, out_down, out_output, notes = finished(total, up_rows, own)
    else:
        total = total.astype(f32)
        out_up, out_down, out_output = total[:up_rows], total[up_rows:at], total[at : at + own]
        notes = total[at + own : at + own + 8]
    out_bias_up = notes[0]
    out_vecs = lax.dynamic_slice(notes, (1, here * own), (6, own))
    out_query, out_key, out_value, col_sums = unpacked_gradients(
        grad_w.reshape(dp_n, seq_n, ffn_n, own_pad, lanes), own, width
    )
    col = lax.dynamic_index_in_dim(col_sums, here // share, keepdims=False)[:own, HEAD_DIM : HEAD_DIM + 2]
    out_b = [col[:, 0], col[:, 1]]
    return (
        out[None],
        grad_features[None],
        out_query,
        out_key,
        out_value,
        out_output,
        out_b[0],
        out_b[1],
        out_vecs[0],
        out_up,
        out_bias_up,
        out_down,
        out_vecs[1],
        out_vecs[2],
        out_vecs[3],
        out_vecs[4],
        out_vecs[5],
    )


def solution(mesh):
    return jax.shard_map(
        shards,
        mesh=mesh,
        in_specs=(
            P(("dp", "ffn"), "seq", None),
            P(("dp", "seq", "ffn"), None),
            P(("dp", "seq", "ffn"), None),
            P(("dp", "seq", "ffn"), None),
            P(("dp", "seq", "ffn"), None),
            P(("dp", "seq", "ffn")),
            P(("dp", "seq", "ffn")),
            P(("dp", "seq", "ffn")),
            P(("dp", "seq"), "ffn"),
            P("ffn"),
            P(("dp", "seq"), "ffn"),
            P(("dp", "seq", "ffn")),
            P(("dp", "seq", "ffn")),
            P(("dp", "seq", "ffn")),
            P(("dp", "seq", "ffn")),
            P(("dp", "seq", "ffn")),
            P(("dp", "ffn"), None),
            P(("dp", "ffn"), "seq", None, None),
            P(("dp", "ffn"), None),
            P(("dp", "ffn"), "seq", None),
        ),
        out_specs=(
            P(("dp", "ffn"), "seq", None),
            P(("dp", "ffn"), "seq", None),
            P(("dp", "seq", "ffn"), None),
            P(("dp", "seq", "ffn"), None),
            P(("dp", "seq", "ffn"), None),
            P(("dp", "seq", "ffn"), None),
            P(("dp", "seq", "ffn")),
            P(("dp", "seq", "ffn")),
            P(("dp", "seq", "ffn")),
            P(("dp", "seq"), "ffn"),
            P("ffn"),
            P(("dp", "seq"), "ffn"),
            P(("dp", "seq", "ffn")),
            P(("dp", "seq", "ffn")),
            P(("dp", "seq", "ffn")),
            P(("dp", "seq", "ffn")),
            P(("dp", "seq", "ffn")),
        ),
        check_vma=False,
    )
```

```python
import functools
import jax
import jax.numpy as jnp
from jax import lax
from jax.experimental import pallas as pl
from jax.sharding import PartitionSpec as P
from jax.experimental.pallas import tpu as pltpu

HEAD_DIM = 64
BLOCK = 64
PAIR = 2 * BLOCK
MASKED = -1e30
bf16 = jnp.bfloat16
f32 = jnp.float32


def dot_nn(a, b):
    return lax.dot_general(a, b, (((1,), (0,)), ((), ())), preferred_element_type=f32)


def dot_nt(a, b):
    return lax.dot_general(a, b, (((1,), (1,)), ((), ())), preferred_element_type=f32)


def dot_tn(a, b):
    return lax.dot_general(a, b, (((0,), (0,)), ((), ())), preferred_element_type=f32)


def slots(rand_ref, glob_ref, flip, head, pair, nblocks):
    first = (2 * pair) ^ flip

    def row(block):
        return pl.multiple_of(block * BLOCK, BLOCK)

    def near(block):
        bad = (block < 0) | (block >= nblocks) | (block == glob_ref[0, 0]) | (block == glob_ref[0, 1])
        return row(jnp.where(bad, nblocks, block ^ flip))

    def drawn(block):
        at = (head * nblocks + block) * 3
        return [row(rand_ref[at + j] ^ flip) for j in range(3)]

    shared = [near(first), near(first + 1)] + [row(glob_ref[0, j] ^ flip) for j in range(2)]
    return shared, [near(first - 1)] + drawn(first), [near(first + 2)] + drawn(first + 1)


def stack_rows(ref, offsets, lanes):
    return jnp.concatenate([ref[pl.ds(o, BLOCK), lanes] for o in offsets], axis=0)


def lane_halves(width, dtype):
    lane = lax.broadcasted_iota(jnp.int32, (1, width), 1) % PAIR
    first = (lane < BLOCK).astype(dtype)
    second = (lane >= BLOCK).astype(dtype)
    return first, second


UNROLL = 4
BACK_UNROLL = 4
APART = 0
VMEM_BYTES = 62 << 20


def head_lanes(h):
    return slice(h * PAIR, (h + 1) * PAIR)


def query_columns(q_ref, mask_ref, h, at):
    return jnp.concatenate([q_ref[h * BLOCK : (h + 1) * BLOCK, pl.ds(at, PAIR)], mask_ref[:, pl.ds(at, PAIR)]], axis=0)


def global_queries(q_ref, mask_ref, h, gl):
    return jnp.concatenate(
        [
            global_columns(q_ref, slice(h * BLOCK, (h + 1) * BLOCK), gl),
            global_columns(mask_ref, slice(0, BLOCK), gl),
        ],
        axis=0,
    ).astype(bf16)


def placed(me_ref, glob_ref, nblocks, chunks):
    flip = me_ref[0] * (nblocks // chunks)
    return flip, [glob_ref[0, j] ^ flip for j in range(2)]


def global_columns(src_ref, rows, gl):
    lane = lax.broadcasted_iota(jnp.int32, (1, PAIR), 1)
    parts = []
    for g in range(2):
        block = gl[g]
        at = pl.multiple_of((block // 2) * PAIR, PAIR)
        both = src_ref[rows, pl.ds(at, PAIR)].astype(f32)
        moved = pltpu.roll(both, BLOCK, 1)
        parts.append(jnp.where(block % 2 == g, both, moved))
    return jnp.where(lane < BLOCK, parts[0], parts[1])


def put_global_columns(dst_ref, rows, gl, value, per_chunk, low, high):
    lane = lax.broadcasted_iota(jnp.int32, (1, PAIR), 1)
    moved = pltpu.roll(value, BLOCK, 1)
    for g in range(2):
        pair = gl[g] // 2
        half = gl[g] % 2
        chunk = pair // per_chunk

        @pl.when((chunk >= low) & (chunk < high))
        def _():
            at = pl.multiple_of((pair % per_chunk) * PAIR, PAIR)
            src = jnp.where(half == g, value, moved)
            old = dst_ref[chunk - low, rows, pl.ds(at, PAIR)].astype(f32)
            new = jnp.where((lane >= BLOCK) == (half == 1), src, old)
            dst_ref[chunk - low, rows, pl.ds(at, PAIR)] = new.astype(dst_ref.dtype)


def project_rows(x, seg, w_ref, wq, bkv_ref, bq_ref, k_ref, v_ref, q_ref, mask_ref, at):
    n = x.shape[0]
    lanes = v_ref.shape[1]
    y = dot_nn(x, w_ref[:, 0:lanes]) + bkv_ref[...]
    spot = lax.broadcasted_iota(jnp.int32, (PAIR, n), 0) - BLOCK
    mark = jnp.transpose((spot == seg).astype(f32), (1, 0))
    lane = lax.broadcasted_iota(jnp.int32, (1, PAIR), 1)
    rows = pl.ds(at, n)
    v_ref[rows, :] = y.astype(bf16)
    for h in range(lanes // PAIR):
        k_ref[rows, head_lanes(h)] = jnp.where(lane < BLOCK, y[:, head_lanes(h)], mark).astype(bf16)
    z = (dot_nt(wq, x) + bq_ref[...]).astype(bf16)
    q_ref[:, rows] = (z.astype(f32) * HEAD_DIM ** -0.5).astype(bf16)
    row = lax.broadcasted_iota(jnp.int32, (BLOCK, n), 0)
    mask_ref[:, rows] = jnp.where((row <= 16) & (row != seg), MASKED, 0.0).astype(bf16)


def query_weights(w_ref, heads):
    at = heads * PAIR
    cols = w_ref[:, at : at + 2 * PAIR].astype(f32)
    return jnp.transpose(cols, (1, 0))[0 : heads * HEAD_DIM].astype(bf16)


def sparse_forward(heads, low, high, per_chunk, rand_ref, glob_ref, flip, k_ref, kv_ref, q_ref, mask_ref, out_ref, lse_ref):
    nblocks = (k_ref.shape[0] - BLOCK) // BLOCK
    first, second = lane_halves(PAIR, bf16)
    lane = lax.broadcasted_iota(jnp.int32, (1, PAIR), 1)

    def one_pair(spot):
        chunk = spot // per_chunk
        local = pl.multiple_of((spot % per_chunk) * PAIR, PAIR)
        pair = low * per_chunk + spot
        at = pl.multiple_of(pair * PAIR, PAIR)
        for h in range(heads):
            shared, mine, other = slots(rand_ref, glob_ref, flip, h, pair, nblocks)
            kl = head_lanes(h)
            q = query_columns(q_ref, mask_ref, h, at)
            s_sh = dot_nn(stack_rows(k_ref, shared, kl), q)
            k_pr = jnp.concatenate([stack_rows(k_ref, mine, kl), stack_rows(k_ref, other, kl)], axis=1)
            s_pr = dot_nn(k_pr, jnp.concatenate([q * first, q * second], axis=0))
            peak = jnp.maximum(jnp.max(s_sh, axis=0, keepdims=True), jnp.max(s_pr, axis=0, keepdims=True))
            e_sh = jnp.exp(s_sh - peak)
            e_pr = jnp.exp(s_pr - peak)
            total = jnp.sum(e_sh, axis=0, keepdims=True) + jnp.sum(e_pr, axis=0, keepdims=True)
            inv = 1.0 / total
            p_sh = (e_sh * inv).astype(bf16)
            p_pr = (e_pr * inv).astype(bf16)
            v_pr = jnp.concatenate([stack_rows(kv_ref, mine, kl), stack_rows(kv_ref, other, kl)], axis=1)
            o_sh = dot_tn(stack_rows(kv_ref, shared, kl), p_sh)
            o_pr = dot_tn(v_pr, p_pr)
            ctx = o_sh[BLOCK:PAIR] + jnp.where(lane < BLOCK, o_pr[BLOCK:PAIR], o_pr[PAIR + BLOCK : 2 * PAIR])
            out_ref[chunk, h * BLOCK : (h + 1) * BLOCK, pl.ds(local, PAIR)] = ctx.astype(bf16)
            lse_ref[h, pl.ds(spot, 1), :] = peak + jnp.log(total)

    @pl.loop(0, (high - low) * per_chunk // UNROLL)
    def _(some):
        for i in range(UNROLL):
            one_pair(UNROLL * some + i)


def forward_kernel(heads, chunks, me_ref, rand_ref, glob_ref, *refs):
    x_refs = refs[0:chunks]
    seg_ref, w_ref, bkv_ref, bq_ref = refs[chunks : chunks + 4]
    far = chunks // 2
    out_refs = refs[chunks + 4 : chunks + 4 + far]
    lse_ref, lseg_ref, glob_ctx_ref = refs[chunks + 4 + far : chunks + 7 + far]
    saved_refs = refs[chunks + 7 + far : chunks + 11 + far]
    s_sc, out_ref, seg_sc, k_sc, v_sc, q_sc, mask_sc, sems = refs[chunks + 11 + far :]
    rows = x_refs[0].shape[0]
    length = rows * chunks
    per_chunk = length // PAIR // chunks
    flip, gl = placed(me_ref, glob_ref, length // BLOCK, chunks)
    tile = 256
    wq = query_weights(w_ref, heads)
    for c in range(chunks):
        seg_sc[c : c + 1, :] = seg_ref[pl.ds(me_ref[0] ^ c, 1), :]
    for c in range(chunks):

        @pl.loop(0, rows // tile)
        def _(t):
            at = pl.multiple_of(t * tile, tile)
            project_rows(
                x_refs[c][pl.ds(at, tile), :], seg_sc[c : c + 1, pl.ds(at, tile)], w_ref, wq, bkv_ref, bq_ref,
                k_sc, v_sc, q_sc, mask_sc, pl.multiple_of(c * rows + t * tile, tile),
            )

    null_lane = lax.broadcasted_iota(jnp.int32, (BLOCK, heads * PAIR), 1) % PAIR
    k_sc[pl.ds(length, BLOCK), :] = (null_lane == BLOCK + 16).astype(f32).astype(bf16)
    v_sc[pl.ds(length, BLOCK), :] = jnp.zeros((BLOCK, heads * PAIR), bf16)
    saves = [
        pltpu.make_async_copy(src, dst, sems.at[i])
        for i, (src, dst) in enumerate(zip((k_sc, v_sc, q_sc, mask_sc), saved_refs))
    ]
    for save in saves:
        save.start()
    sparse_forward(heads, far, chunks, per_chunk, rand_ref, glob_ref, flip, k_sc, v_sc, q_sc, mask_sc, out_ref, lse_ref)

    step = 512
    queries = [global_queries(q_sc, mask_sc, h, gl) for h in range(heads)]

    def score(c, peaks):
        at = pl.multiple_of(c * step, step)
        new = []
        for h in range(heads):
            got = dot_nn(k_sc[pl.ds(at, step), head_lanes(h)], queries[h])
            s_sc[h, pl.ds(at, step), :] = got
            new.append(jnp.maximum(peaks[h], jnp.max(got, axis=0, keepdims=True)))
        return tuple(new)

    peaks = lax.fori_loop(0, length // step, score, (jnp.full((1, PAIR), MASKED, f32),) * heads)

    def gather(c, carry):
        at = pl.multiple_of(c * step, step)
        new = []
        for h in range(heads):
            total, ctx = carry[h]
            e = jnp.exp(s_sc[h, pl.ds(at, step), :] - peaks[h])
            ctx = ctx + dot_tn(v_sc[pl.ds(at, step), head_lanes(h)], e.astype(bf16))
            new.append((total + jnp.sum(e, axis=0, keepdims=True), ctx))
        return tuple(new)

    start = (jnp.zeros((1, PAIR), f32), jnp.zeros((PAIR, PAIR), f32))
    sums = lax.fori_loop(0, length // step, gather, (start,) * heads)
    for h in range(heads):
        total, ctx = sums[h]
        ctx = ctx[BLOCK:PAIR] * (1.0 / total)
        glob_ctx_ref[h] = ctx
        put_global_columns(out_ref, slice(h * BLOCK, (h + 1) * BLOCK), gl, ctx, per_chunk, far, chunks)
        lseg_ref[h : h + 1, :] = peaks[h] + jnp.log(total)
    for c in range(far):
        out_refs[c][...] = out_ref[c]
    for save in saves:
        save.wait()


def attention_forward(me, rand, glob, x, seg, w, b_kv, b_q):
    chunks = len(x)
    far = chunks // 2
    rows = x[0].shape[0]
    length = rows * chunks
    heads = b_q.shape[0] // HEAD_DIM
    whole = lambda: pl.BlockSpec(memory_space=pltpu.VMEM)
    got = pl.pallas_call(
        functools.partial(forward_kernel, heads, chunks),
        out_shape=(jax.ShapeDtypeStruct((heads * HEAD_DIM, rows), bf16),) * far
        + (
            jax.ShapeDtypeStruct((heads, length // PAIR // 2, PAIR), f32),
            jax.ShapeDtypeStruct((heads, PAIR), f32),
            jax.ShapeDtypeStruct((heads, HEAD_DIM, PAIR), f32),
            jax.ShapeDtypeStruct((length + BLOCK, heads * PAIR), bf16),
            jax.ShapeDtypeStruct((length + BLOCK, heads * PAIR), bf16),
            jax.ShapeDtypeStruct((heads * HEAD_DIM, length), bf16),
            jax.ShapeDtypeStruct((BLOCK, length), bf16),
        ),
        in_specs=[pl.BlockSpec(memory_space=pltpu.SMEM)] * 3 + [whole() for _ in range(chunks + 4)],
        out_specs=tuple([whole() for _ in range(far + 3)] + [pl.BlockSpec(memory_space=pl.ANY)] * 4),
        scratch_shapes=[
            pltpu.VMEM((heads, length, PAIR), f32),
            pltpu.VMEM((far, heads * HEAD_DIM, rows), bf16),
            pltpu.VMEM((chunks, rows), jnp.int32),
            pltpu.VMEM((length + BLOCK, heads * PAIR), bf16),
            pltpu.VMEM((length + BLOCK, heads * PAIR), bf16),
            pltpu.VMEM((heads * HEAD_DIM, length), bf16),
            pltpu.VMEM((BLOCK, length), bf16),
            pltpu.SemaphoreType.DMA((4,)),
        ],
        compiler_params=pltpu.CompilerParams(vmem_limit_bytes=VMEM_BYTES),
        cost_estimate=pl.CostEstimate(flops=10_000_000_000, bytes_accessed=16_000_000, transcendentals=6_000_000),
        name="attention_forward",
    )(me, rand, glob, *x, seg, w, b_kv, b_q)
    return got[:far], got[far:]


def near_kernel(heads, chunks, me_ref, rand_ref, glob_ref, k_ref, kv_ref, q_ref, mask_ref, glob_ctx_ref, *refs):
    half = chunks // 2
    out_refs = refs[:half]
    lse_ref, out_ref = refs[half:]
    length = q_ref.shape[1]
    per_chunk = length // PAIR // chunks
    flip, gl = placed(me_ref, glob_ref, length // BLOCK, chunks)
    sparse_forward(heads, 0, half, per_chunk, rand_ref, glob_ref, flip, k_ref, kv_ref, q_ref, mask_ref, out_ref, lse_ref)
    for h in range(heads):
        put_global_columns(out_ref, slice(h * BLOCK, (h + 1) * BLOCK), gl, glob_ctx_ref[h], per_chunk, 0, half)
    for c in range(half):
        out_refs[c][...] = out_ref[c]


def attention_near(me, rand, glob, k, kv, q, mask, glob_ctx, chunks):
    heads = glob_ctx.shape[0]
    half = chunks // 2
    length = q.shape[1]
    rows = length // chunks
    whole = lambda: pl.BlockSpec(memory_space=pltpu.VMEM)
    got = pl.pallas_call(
        functools.partial(near_kernel, heads, chunks),
        out_shape=(jax.ShapeDtypeStruct((heads * HEAD_DIM, rows), bf16),) * half
        + (jax.ShapeDtypeStruct((heads, length // PAIR // 2, PAIR), f32),),
        in_specs=[pl.BlockSpec(memory_space=pltpu.SMEM)] * 3 + [whole() for _ in range(5)],
        out_specs=tuple(whole() for _ in range(half + 1)),
        scratch_shapes=[pltpu.VMEM((half, heads * HEAD_DIM, rows), bf16)],
        compiler_params=pltpu.CompilerParams(vmem_limit_bytes=VMEM_BYTES),
        cost_estimate=pl.CostEstimate(flops=6_000_000_000, bytes_accessed=9_000_000, transcendentals=3_000_000),
        name="attention_near",
    )(me, rand, glob, k, kv, q, mask, glob_ctx)
    return got[:half], got[half]


def backward_kernel(heads, chunks, me_ref, rand_ref, glob_ref, *refs):
    do_refs = refs[:chunks]
    (k_ref, kv_ref, q_ref, mask_ref, seg_ref, lse_near_ref, lse_far_ref, lseg_ref, w_ref, resid_hbm, dq_hbm, dkv_hbm,
     first_ref) = refs[chunks : chunks + 13]
    part_refs = refs[chunks + 13 : 2 * chunks + 12]
    (do_sc, acc, p_sc, d_sc, seg_sc, line_sc, lse_ref, row_sc, resid_ref, dq_ref, dkv_ref, sems) = refs[2 * chunks + 12 :]
    fetch = pltpu.make_async_copy(resid_hbm, resid_ref, sems.at[0])
    fetch.start()
    rows = do_refs[0].shape[1]
    length = rows * chunks
    npairs = length // PAIR
    per_chunk = npairs // chunks
    scale = HEAD_DIM ** -0.5
    flip, gl = placed(me_ref, glob_ref, length // BLOCK, chunks)
    lse_ref[:, 0 : npairs // 2, :] = lse_near_ref[...]
    lse_ref[:, npairs // 2 :, :] = lse_far_ref[...]
    for c in range(chunks):
        do_sc[:, c * rows : (c + 1) * rows] = do_refs[c][...]
        row_sc[c : c + 1, :] = seg_ref[pl.ds(me_ref[0] ^ c, 1), :].astype(f32)

        @pl.loop(0, per_chunk // 4)
        def _(some):
            for i in range(4):
                t = 4 * some + i
                line = row_sc[c : c + 1, pl.ds(pl.multiple_of(t * PAIR, PAIR), PAIR)]
                line_sc[c * per_chunk + t] = line
                to = pl.multiple_of(c * rows + t * PAIR, PAIR)
                seg_sc[pl.ds(to, PAIR), :] = jnp.transpose(jnp.broadcast_to(line, (PAIR, PAIR)), (1, 0))

    seg_sc[length : length + BLOCK, :] = jnp.full((BLOCK, PAIR), -1.0, f32)
    first2, second2 = lane_halves(2 * PAIR, bf16)
    ffirst, fsecond = lane_halves(PAIR, f32)
    lane = lax.broadcasted_iota(jnp.int32, (1, PAIR), 1)
    line_row = lax.broadcasted_iota(jnp.int32, (PAIR, 1), 0)
    zeros = jnp.zeros((BLOCK, PAIR), bf16)
    blank = jnp.zeros((PAIR, PAIR), bf16)

    def head_rows(h):
        return slice(h * BLOCK, (h + 1) * BLOCK)

    def joint(q, mask, do):
        left = jnp.concatenate([q, mask, blank], axis=0)
        right = jnp.concatenate([blank, zeros, do], axis=0)
        return jnp.concatenate([left, right], axis=1)

    def sources(q, do):
        top = jnp.concatenate([q, zeros], axis=1)
        return jnp.concatenate([top, jnp.concatenate([zeros, do], axis=1)], axis=0)

    step = 512
    mask_glob = global_columns(mask_ref, slice(0, BLOCK), gl).astype(bf16)
    q_glob = [global_columns(q_ref, head_rows(h), gl).astype(bf16) for h in range(heads)]
    do_glob = [global_columns(do_sc, head_rows(h), gl).astype(bf16) for h in range(heads)]

    def weigh(c, deltas):
        at = pl.multiple_of(c * step, step)
        new = []
        for h in range(heads):
            left = jnp.concatenate([k_ref[pl.ds(at, step), head_lanes(h)], kv_ref[pl.ds(at, step), head_lanes(h)]], axis=1)
            both = dot_nn(left, joint(q_glob[h], mask_glob, do_glob[h]))
            p = jnp.exp(both[:, 0:PAIR] - lseg_ref[h : h + 1, :])
            dp = both[:, PAIR:]
            p_sc[h, pl.ds(at, step), :] = p
            d_sc[h, pl.ds(at, step), :] = dp
            new.append(deltas[h] + jnp.sum(p * dp, axis=0, keepdims=True))
        return tuple(new)

    deltas = lax.fori_loop(0, length // step, weigh, (jnp.zeros((1, PAIR), f32),) * heads)

    def spread(c, dqs):
        at = pl.multiple_of(c * step, step)
        new = []
        for h in range(heads):
            p = p_sc[h, pl.ds(at, step), :]
            ds = (p * (d_sc[h, pl.ds(at, step), :] - deltas[h])).astype(bf16)
            both = jnp.concatenate([ds, p.astype(bf16)], axis=1)
            acc[h, pl.ds(at, step), :] = dot_nt(both, sources(q_glob[h], do_glob[h]))
            new.append(dqs[h] + dot_tn(k_ref[pl.ds(at, step), head_lanes(h)], ds))
        return tuple(new)

    dqs = lax.fori_loop(0, length // step, spread, (jnp.zeros((PAIR, PAIR), f32),) * heads)
    for h in range(heads):
        acc[h, pl.ds(length, BLOCK), :] = jnp.zeros((BLOCK, PAIR), f32)

    def one_pair(pair):
        chunk = pair // per_chunk
        local = pl.multiple_of((pair % per_chunk) * PAIR, PAIR)
        at = pl.multiple_of(pair * PAIR, PAIR)
        hit_first = (gl[0] == 2 * pair) | (gl[1] == 2 * pair)
        hit_second = (gl[0] == 2 * pair + 1) | (gl[1] == 2 * pair + 1)
        shut = ffirst * jnp.where(hit_first, -MASKED, 0.0) + fsecond * jnp.where(hit_second, -MASKED, 0.0)
        every = slice(0, PAIR)
        for h in range(heads):
            kl = head_lanes(h)
            shared, mine, other = slots(rand_ref, glob_ref, flip, h, pair, length // BLOCK)
            q = q_ref[head_rows(h), pl.ds(at, PAIR)]
            do = do_sc[head_rows(h), pl.ds(at, PAIR)]
            lse = lse_ref[h, pl.ds(pair, 1), :] + shut
            src = sources(q, do)
            src2 = jnp.concatenate([src * first2, src * second2], axis=0)
            k_sh = stack_rows(k_ref, shared, kl)
            two_sh = dot_nn(
                jnp.concatenate([k_sh, stack_rows(kv_ref, shared, kl)], axis=1),
                joint(q, mask_ref[:, pl.ds(at, PAIR)], do),
            )
            kv_pr = jnp.concatenate([stack_rows(kv_ref, mine, kl), stack_rows(kv_ref, other, kl)], axis=1)
            two_pr = dot_nn(kv_pr, src2)
            seg_pr = jnp.where(lane < BLOCK, stack_rows(seg_sc, mine, every), stack_rows(seg_sc, other, every))
            agree = seg_pr == line_sc[pair]
            p_sh = jnp.exp(two_sh[:, 0:PAIR] - lse)
            p_pr = jnp.where(agree, jnp.exp(two_pr[:, 0:PAIR] - lse), 0.0)
            d_sh, d_pr = two_sh[:, PAIR:], two_pr[:, PAIR:]
            delta = jnp.sum(p_sh * d_sh, axis=0, keepdims=True) + jnp.sum(p_pr * d_pr, axis=0, keepdims=True)
            ds_sh = (p_sh * (d_sh - delta)).astype(bf16)
            ds_pr = (p_pr * (d_pr - delta)).astype(bf16)
            g_sh = dot_nt(jnp.concatenate([ds_sh, p_sh.astype(bf16)], axis=1), src)
            g_pr = dot_nt(jnp.concatenate([ds_pr, p_pr.astype(bf16)], axis=1), src2)
            for j, o in enumerate(shared):
                acc[h, pl.ds(o, BLOCK), :] += g_sh[j * BLOCK : (j + 1) * BLOCK]
            for j, o in enumerate(mine):
                acc[h, pl.ds(o, BLOCK), :] += g_pr[j * BLOCK : (j + 1) * BLOCK, 0:PAIR]
            for j, o in enumerate(other):
                acc[h, pl.ds(o, BLOCK), :] += g_pr[j * BLOCK : (j + 1) * BLOCK, PAIR:]
            t_pr = dot_tn(ds_pr, kv_pr)
            dq = dot_tn(ds_sh, k_sh) + jnp.where(line_row < BLOCK, t_pr[:, 0:PAIR], t_pr[:, PAIR:])
            dq = jnp.transpose(dq, (1, 0))[0:BLOCK]
            dq_ref[chunk, head_rows(h), pl.ds(local, PAIR)] = (dq * scale).astype(bf16)

    @pl.loop(0, npairs // BACK_UNROLL)
    def _(some):
        for i in range(BACK_UNROLL):
            one_pair(BACK_UNROLL * some + i)

    for h in range(heads):
        put_global_columns(dq_ref, head_rows(h), gl, dqs[h][0:BLOCK] * scale, per_chunk, 0, chunks)
        for c in range(chunks):
            dkv_ref[c, :, head_lanes(h)] = acc[h, pl.ds(c * rows, rows), :].astype(bf16)
    saves = [
        pltpu.make_async_copy(dq_ref, dq_hbm, sems.at[1]),
        pltpu.make_async_copy(dkv_ref, dkv_hbm, sems.at[2]),
    ]
    for save in saves:
        save.start()
    fetch.wait()
    tile = 256
    wq = query_weights(w_ref, heads)
    for c in range(chunks):

        @pl.loop(0, rows // tile)
        def _(t):
            at = pl.multiple_of(t * tile, tile)
            got = dot_tn(dq_ref[c, :, pl.ds(at, tile)], wq)
            got = got + dot_nt(dkv_ref[c, pl.ds(at, tile), :], w_ref[:, 0 : heads * PAIR])
            if c == 0:
                first_ref[pl.ds(at, tile), :] = resid_ref[pl.ds(at, tile), :] + got
            else:
                part_refs[c - 1][pl.ds(at, tile), :] = got.astype(bf16)
    for save in saves:
        save.wait()


def attention_backward(me, rand, glob, do, k, kv, q, mask, seg, lse_near, lse_far, lseg, w, resid):
    chunks = len(do)
    group, rows = do[0].shape
    heads = group // HEAD_DIM
    width = w.shape[0]
    length = rows * chunks
    whole = lambda: pl.BlockSpec(memory_space=pltpu.VMEM)
    return pl.pallas_call(
        functools.partial(backward_kernel, heads, chunks),
        out_shape=(
            jax.ShapeDtypeStruct((chunks, group, rows), bf16),
            jax.ShapeDtypeStruct((chunks, rows, heads * PAIR), bf16),
            jax.ShapeDtypeStruct((rows, width), f32),
        )
        + (jax.ShapeDtypeStruct((rows, width), bf16),) * (chunks - 1),
        in_specs=[pl.BlockSpec(memory_space=pltpu.SMEM)] * 3
        + [whole() for _ in range(chunks + 9)]
        + [pl.BlockSpec(memory_space=pl.ANY)],
        out_specs=tuple([pl.BlockSpec(memory_space=pl.ANY)] * 2 + [whole() for _ in range(chunks)]),
        scratch_shapes=[
            pltpu.VMEM((group, length), bf16),
            pltpu.VMEM((heads, length + BLOCK, PAIR), f32),
            pltpu.VMEM((heads, length, PAIR), f32),
            pltpu.VMEM((heads, length, PAIR), f32),
            pltpu.VMEM((length + BLOCK, PAIR), f32),
            pltpu.VMEM((length // PAIR, 1, PAIR), f32),
            pltpu.VMEM((heads, length // PAIR, PAIR), f32),
            pltpu.VMEM((chunks, rows), f32),
            pltpu.VMEM((rows, width), f32),
            pltpu.VMEM((chunks, group, rows), bf16),
            pltpu.VMEM((chunks, rows, heads * PAIR), bf16),
            pltpu.SemaphoreType.DMA((3,)),
        ],
        compiler_params=pltpu.CompilerParams(vmem_limit_bytes=VMEM_BYTES),
        cost_estimate=pl.CostEstimate(flops=30_000_000_000, bytes_accessed=24_000_000, transcendentals=8_000_000),
        name="attention_backward",
    )(me, rand, glob, *do, k, kv, q, mask, seg, lse_near, lse_far, lseg, w, resid)


def round_up(value, to):
    return -(-value // to) * to


def half_columns(ref, index, place):
    at = index // 2 * PAIR
    both = ref[:, at : at + PAIR].astype(f32)
    return both if index % 2 == place else pltpu.roll(both, BLOCK, 1)


def two_halves(first, second):
    lane = lax.broadcasted_iota(jnp.int32, (1, PAIR), 1)
    return jnp.where(lane < BLOCK, first, second)


def pack_kernel(seq_n, wq_ref, wk_ref, wv_ref, vec_ref, more_ref, pack_ref):
    own, width = wq_ref.shape
    heads = width // HEAD_DIM // seq_n
    blocks, inner = pack_ref.shape[0], pack_ref.shape[2]
    for s in range(seq_n):
        pieces = [
            two_halves(half_columns(wk_ref, s * heads + h, 0), half_columns(wv_ref, s * heads + h, 1))
            for h in range(heads)
        ]
        for h in range(0, heads, 2):
            second = half_columns(wq_ref, s * heads + h + 1, 1) if h + 1 < heads else (
                vec_ref[...].astype(f32) + more_ref[...].astype(f32)
            )
            pieces.append(two_halves(half_columns(wq_ref, s * heads + h, 0), second))
        piece = jnp.concatenate(pieces, axis=1).astype(bf16)
        for b in range(blocks):
            for i in range(inner):
                pack_ref[b, s, i] = piece


def rest_kernel(wo_ref, up_ref, down_ref, rest_ref):
    own = wo_ref.shape[0]
    u = up_ref.shape[0]
    rest_ref[0:u, :] = up_ref[...]
    rest_ref[u : 2 * u, :] = down_ref[...]
    rest_ref[2 * u : 2 * u + own, :] = wo_ref[...]


def packed_weights(w_q, w_k, w_v, w_o, w_up, w_down, vec, more, dp_n, seq_n, ffn_n):
    own, width = w_q.shape
    heads = width // HEAD_DIM // seq_n
    lanes = heads * PAIR + round_up(heads * HEAD_DIM, PAIR)
    u = w_up.shape[0]
    if own % 8 or u % 16:
        group = heads * HEAD_DIM
        cols = lambda w: w.reshape(own, seq_n, heads, HEAD_DIM).transpose(1, 0, 2, 3)
        kv = jnp.stack([cols(w_k), cols(w_v)], axis=3).reshape(seq_n, own, 2 * group)
        notes = jnp.broadcast_to((vec + more)[None, :, HEAD_DIM:], (seq_n, own, PAIR - HEAD_DIM))
        piece = jnp.concatenate([kv, cols(w_q).reshape(seq_n, own, group), notes], axis=2)
        piece = jnp.pad(piece, ((0, 0), (0, round_up(own, 8) - own), (0, 0)))
        pack = jnp.broadcast_to(piece[None, :, None], (dp_n, seq_n, ffn_n) + piece.shape[1:])
        w_o = jnp.pad(w_o, ((0, round_up(own, 8) - own), (0, 0)))
        return pack, jnp.concatenate([w_up, w_down, w_o], axis=0)
    whole = lambda: pl.BlockSpec(memory_space=pltpu.VMEM)
    rest = pl.pallas_call(
        rest_kernel,
        out_shape=jax.ShapeDtypeStruct((2 * u + own, width), bf16),
        in_specs=[whole() for _ in range(3)],
        out_specs=whole(),
        name="rest_weights",
    )(w_o, w_up, w_down)
    pack = pl.pallas_call(
        functools.partial(pack_kernel, seq_n),
        out_shape=jax.ShapeDtypeStruct((dp_n, seq_n, ffn_n, own, lanes), bf16),
        in_specs=[whole() for _ in range(5)],
        out_specs=whole(),
        name="packed_weights",
    )(w_q, w_k, w_v, vec, more)
    return pack, rest


def weights_kernel(chunks, direct, *refs):
    x_refs = refs[:chunks]
    dq_ref, dkv_ref, out_ref, acc, sum_sc = refs[chunks:]
    group = dq_ref.shape[1]
    lanes = dkv_ref.shape[2]
    full, width = acc.shape
    x = jnp.concatenate([r[...] for r in x_refs], axis=0)
    dkv = jnp.concatenate([dkv_ref[c] for c in range(chunks)], axis=0)
    dq = jnp.concatenate([dq_ref[c] for c in range(chunks)], axis=1)
    ones = jnp.ones((8, x.shape[0]), bf16)

    @pl.when(pl.program_id(0) == 0)
    def _():
        acc[...] = jnp.zeros_like(acc)
        sum_sc[...] = jnp.zeros_like(sum_sc)

    acc[0:lanes, :] += dot_tn(dkv, x)
    acc[lanes : lanes + group, :] += dot_nn(dq, x)
    sum_sc[:, 0:lanes] += dot_nn(ones, dkv)
    sum_sc[:, lanes : lanes + group] += dot_nt(ones, dq)

    @pl.when(pl.program_id(0) == pl.num_programs(0) - 1)
    def _():
        lane = lax.broadcasted_iota(jnp.int32, (full, width), 0)
        spot = lax.broadcasted_iota(jnp.int32, (full, width), 1) % group
        pick_q = lane - lanes == spot
        pick_v = (lane < lanes) & (lane % PAIR >= BLOCK) & (lane // PAIR * BLOCK + lane % BLOCK == spot)
        sums = sum_sc[...].astype(bf16)
        row = lax.broadcasted_iota(jnp.int32, (8, width), 0)
        of_q = dot_nn(sums, pick_q.astype(f32).astype(bf16))
        of_v = dot_nn(sums, pick_v.astype(f32).astype(bf16))
        acc[lanes + group : lanes + group + 8, :] = jnp.where(row == 0, of_q, of_v)
        grad = jnp.transpose(acc[...], (1, 0))
        if direct:
            blocks, own, _ = out_ref.shape
            grad = grad.reshape(blocks, own, full)
            for b in range(blocks):
                out_ref[b] = grad[b].astype(bf16)
        else:
            out_ref[...] = grad.astype(bf16)


def projection_gradients(x, dq, dkv, own, devices):
    chunks, group, rows = dq.shape
    width = x[0].shape[1]
    lanes = dkv.shape[2]
    full = lanes + round_up(group, PAIR)
    direct = own % 8 == 0
    tile = 256
    shape = (devices, own, full) if direct else (width, full)
    out = pl.pallas_call(
        functools.partial(weights_kernel, chunks, direct),
        grid=(rows // tile,),
        out_shape=jax.ShapeDtypeStruct(shape, bf16),
        in_specs=[pl.BlockSpec((tile, width), lambda i: (i, 0)) for _ in range(chunks)]
        + [
            pl.BlockSpec((chunks, group, tile), lambda i: (0, 0, i)),
            pl.BlockSpec((chunks, tile, lanes), lambda i: (0, i, 0)),
        ],
        out_specs=pl.BlockSpec(shape, lambda i: (0,) * len(shape), pipeline_mode=pl.Buffered(1)),
        scratch_shapes=[pltpu.VMEM((full, width), f32), pltpu.VMEM((8, full), f32)],
        compiler_params=pltpu.CompilerParams(vmem_limit_bytes=VMEM_BYTES),
        cost_estimate=pl.CostEstimate(flops=4_000_000_000, bytes_accessed=12_000_000, transcendentals=0),
        name="projection_gradients",
    )(*x, dq, dkv)
    if not direct:
        out = jnp.pad(out.reshape(devices, own, full), ((0, 0), (0, round_up(own, 8) - own), (0, 0)))
    return out


def unpack_kernel(own, got_ref, q_ref, k_ref, v_ref, sums_ref, tot):
    dp_n, seq_n, ffn_n, per, full = got_ref.shape
    width = q_ref.shape[1]
    heads = width // HEAD_DIM // seq_n
    for s in range(seq_n):
        total = jnp.zeros((per, full), f32)
        for d in range(dp_n):
            for f in range(ffn_n):
                total = total + got_ref[d, s, f].astype(f32)
        tot[s] = total
        sums_ref[s] = total[:, full - PAIR :]
    for w in range(width // PAIR):
        spots = [((2 * w + i) // heads, (2 * w + i) % heads) for i in range(2)]
        cols = slice(w * PAIR, (w + 1) * PAIR)
        for ref, where in (
            (k_ref, lambda h: 2 * h),
            (v_ref, lambda h: 2 * h + 1),
            (q_ref, lambda h: 2 * heads + h),
        ):
            both = [half_columns(tot.at[g], where(h), i) for i, (g, h) in enumerate(spots)]
            ref[:, cols] = two_halves(*both)[0:own]


def unpacked_gradients(got, own, width):
    dp_n, seq_n, ffn_n, per, full = got.shape
    whole = lambda: pl.BlockSpec(memory_space=pltpu.VMEM)
    return pl.pallas_call(
        functools.partial(unpack_kernel, own),
        out_shape=(jax.ShapeDtypeStruct((own, width), f32),) * 3 + (jax.ShapeDtypeStruct((seq_n, per, PAIR), f32),),
        in_specs=[whole()],
        out_specs=tuple(whole() for _ in range(4)),
        scratch_shapes=[pltpu.VMEM((seq_n, per, full), f32)],
        compiler_params=pltpu.CompilerParams(vmem_limit_bytes=VMEM_BYTES),
        cost_estimate=pl.CostEstimate(flops=40_000_000_000, bytes_accessed=3_000_000, transcendentals=0),
        name="unpacked_gradients",
    )(got)


NORM_EPS = 1e-12


def transposed(value):
    return jnp.transpose(value.astype(f32), (1, 0)).astype(bf16)


def unit_rows(value):
    center = value - jnp.mean(value, axis=-1, keepdims=True)
    scale = lax.rsqrt(jnp.mean(center * center, axis=-1, keepdims=True) + NORM_EPS)
    return center * scale, scale


def unit_rows_back(grad, unit, scale):
    return scale * (
        grad - jnp.mean(grad, axis=-1, keepdims=True) - unit * jnp.mean(grad * unit, axis=-1, keepdims=True)
    )


def rows_kernel(parts, blocks, up_rows, own, me_ref, *refs):
    ctx_refs = refs[:parts]
    (x_ref, cot_ref, rest_ref, wo_ref, vec_ref, bup_ref, out_ref, resid_ref, hid_ref, pre_ref, nlt_ref, gft_ref,
     gb_ref) = refs[parts : parts + 13]
    do_refs = refs[parts + 13 : 2 * parts + 13]
    sums_ref, gbup_ref, slope_sc, wo_sc, wide_sc = refs[2 * parts + 13 :]
    group = ctx_refs[0].shape[0]
    width = x_ref.shape[1]

    def up(f):
        return rest_ref[:, f, 0:up_rows, :].reshape(width, rest_ref.shape[3])

    def down(f):
        return rest_ref[:, f, up_rows : 2 * up_rows, :].reshape(width, rest_ref.shape[3])

    def own_rows(k):
        return pl.ds(pl.multiple_of((me_ref[0] ^ k) * group, group), group)

    @pl.when(pl.program_id(0) == 0)
    def _():
        sums_ref[...] = jnp.zeros_like(sums_ref)
        gbup_ref[...] = jnp.zeros_like(gbup_ref)
        if own:
            for o in range(rest_ref.shape[0]):
                for f in range(blocks):
                    to = (o * blocks + f) * own
                    wide_sc[to : to + own, :] = rest_ref[o, f, 2 * up_rows : 2 * up_rows + own, :].astype(f32)
            wo_sc[...] = wide_sc[...].astype(bf16)
        else:
            wo_sc[...] = wo_ref[...]

    def bias_up(f):
        return bup_ref[f : f + 1, :]

    ctx = jnp.concatenate([r[...] for r in ctx_refs], axis=0)
    w_o = jnp.concatenate([wo_sc[own_rows(k), :] for k in range(parts)], axis=0)
    resid_one = x_ref[...].astype(f32) + (dot_tn(ctx, w_o) + vec_ref[0:1, :])
    unit_one, scale_one = unit_rows(resid_one)
    normed_one = unit_one * vec_ref[2:3, :] + vec_ref[3:4, :]
    low = normed_one.astype(bf16)
    nlt_ref[...] = transposed(normed_one)
    total = normed_one + vec_ref[1:2, :]
    pre = dot_nn(low, up(0)) + bias_up(0)
    for f in range(blocks):
        later = dot_nn(low, up(f + 1)) + bias_up(f + 1) if f + 1 < blocks else None
        phi = 0.5 + 0.5 * lax.erf(pre * (0.5 ** 0.5))
        slope_sc[f] = phi + pre * (jnp.exp(-0.5 * pre * pre) * 0.3989422804014327)
        hid = (pre * phi).astype(bf16)
        hid_ref[f] = hid
        total = total + dot_nt(hid, down(f))
        pre = later
    unit_two, scale_two = unit_rows(total)
    out_ref[...] = (unit_two * vec_ref[4:5, :] + vec_ref[5:6, :]).astype(bf16)
    cot = cot_ref[...].astype(f32)
    grad_two = unit_rows_back(cot * vec_ref[4:5, :], unit_two, scale_two)
    grad_ffn = grad_two.astype(bf16)
    gft_ref[...] = transposed(grad_two)
    grad_normed = grad_two
    back = dot_nn(grad_ffn, down(0))
    for f in range(blocks):
        later = dot_nn(grad_ffn, down(f + 1)) if f + 1 < blocks else None
        grad_pre = (back * slope_sc[f]).astype(bf16)
        pre_ref[f] = grad_pre
        gbup_ref[f : f + 1, :] += jnp.sum(grad_pre.astype(f32), axis=0, keepdims=True)
        grad_normed = grad_normed + dot_nt(grad_pre, up(f))
        back = later
    resid = unit_rows_back(grad_normed * vec_ref[2:3, :], unit_one, scale_one)
    resid_ref[...] = resid
    branch = resid.astype(bf16)
    gb_ref[...] = branch
    do = dot_nt(w_o, branch).astype(bf16)
    for k in range(parts):
        do_refs[k][...] = do[k * group : (k + 1) * group]
    for row, value in enumerate(
        (branch.astype(f32), grad_ffn.astype(f32), grad_normed * unit_one, grad_normed, cot * unit_two, cot)
    ):
        sums_ref[row : row + 1, :] += jnp.sum(value, axis=0, keepdims=True)


def rows_chain(me, ctx_parts, x, cot, rest, up_rows, own, w_o, vecs, bias_up):
    parts = len(ctx_parts)
    group, rows = ctx_parts[0].shape
    width = x.shape[1]
    outer, blocks, per, hidden = rest.shape
    tile = 256
    once = lambda shape: pl.BlockSpec(shape, lambda i: (0,) * len(shape), pipeline_mode=pl.Buffered(1))
    tall = pl.BlockSpec((tile, width), lambda i: (i, 0))
    wide = pl.BlockSpec((width, tile), lambda i: (0, i))
    cube = pl.BlockSpec((blocks, tile, hidden), lambda i: (0, i, 0))
    return pl.pallas_call(
        functools.partial(rows_kernel, parts, blocks, up_rows, own),
        grid=(rows // tile,),
        out_shape=(
            jax.ShapeDtypeStruct((rows, width), bf16),
            jax.ShapeDtypeStruct((rows, width), f32),
            jax.ShapeDtypeStruct((blocks, rows, hidden), bf16),
            jax.ShapeDtypeStruct((blocks, rows, hidden), bf16),
            jax.ShapeDtypeStruct((width, rows), bf16),
            jax.ShapeDtypeStruct((width, rows), bf16),
            jax.ShapeDtypeStruct((rows, width), bf16),
        )
        + (jax.ShapeDtypeStruct((group, rows), bf16),) * parts
        + (jax.ShapeDtypeStruct((8, width), f32), jax.ShapeDtypeStruct((8, hidden), f32)),
        in_specs=[pl.BlockSpec(memory_space=pltpu.SMEM)]
        + [pl.BlockSpec((group, tile), lambda i: (0, i))] * parts
        + [tall, tall, once(rest.shape), once(w_o.shape), once(vecs.shape), once(bias_up.shape)],
        out_specs=(
            tall, tall, cube, cube, wide, wide, tall,
        )
        + (pl.BlockSpec((group, tile), lambda i: (0, i)),) * parts
        + (pl.BlockSpec((8, width), lambda i: (0, 0)), pl.BlockSpec((8, hidden), lambda i: (0, 0))),
        scratch_shapes=[
            pltpu.VMEM((blocks, tile, hidden), f32),
            pltpu.VMEM((width, width), bf16),
            pltpu.VMEM((width, width), f32),
        ],
        compiler_params=pltpu.CompilerParams(vmem_limit_bytes=VMEM_BYTES),
        cost_estimate=pl.CostEstimate(flops=22_000_000_000, bytes_accessed=40_000_000, transcendentals=6_000_000),
        name="rows_chain",
    )(me, *ctx_parts, x, cot, rest, w_o, vecs, bias_up)


def outer_kernel(parts, up_rows, own, apart, me_ref, *refs):
    ctx_refs = refs[:parts]
    nlt_ref, gft_ref, gb_ref, pre_ref, hid_ref, sums_ref, gbup_ref, out_ref = refs[parts : parts + 8]
    wo_sc = refs[-1]
    slabs, hidden = out_ref.shape[0], out_ref.shape[3]
    group = ctx_refs[0].shape[0]
    f = pl.program_id(0)
    up = dot_nn(nlt_ref[...], pre_ref[0]).astype(bf16).reshape(slabs, up_rows, hidden)
    if apart:
        refs[parts + 8][:, 0, :, :] = up[:, 0:apart]
    out_ref[:, 0, 0 : up_rows - apart, :] = up[:, apart:]
    at = up_rows - apart
    down = dot_nn(gft_ref[...], hid_ref[0]).astype(bf16)
    out_ref[:, 0, at : at + up_rows, :] = down.reshape(slabs, up_rows, hidden)
    at += up_rows
    if not own:
        return

    @pl.when(f == 0)
    def _():
        for k in range(parts):
            wo_sc[k] = dot_nn(ctx_refs[k][...], gb_ref[...])

    share = slabs // parts
    stride = group // share
    for k in range(parts):
        for j in range(share):
            rows = pl.ds(pl.multiple_of(j * stride + f * own, 8), own)
            out_ref[(me_ref[0] ^ k) * share + j, 0, at : at + own, :] = wo_sc[k, rows, :].astype(bf16)
    small = jnp.concatenate([gbup_ref[pl.ds(f, 1), :], sums_ref[0:7, :]], axis=0).astype(bf16)
    for o in range(slabs):
        out_ref[o, 0, at + own :, :] = small


def outer_products(me, ctx_parts, nlt, gft, gb, pre, hid, sums, gbup, slabs, up_rows, own, apart):
    blocks, rows, hidden = pre.shape
    parts = len(ctx_parts)
    group = ctx_parts[0].shape[0]
    per = 2 * up_rows - apart + (own + 8 if own else 0)
    sizes = (per, apart) if apart else (per,)
    once = lambda shape: pl.BlockSpec(shape, lambda i: (0,) * len(shape), pipeline_mode=pl.Buffered(1))
    return pl.pallas_call(
        functools.partial(outer_kernel, parts, up_rows, own, apart),
        grid=(blocks,),
        out_shape=tuple(jax.ShapeDtypeStruct((slabs, blocks, r, hidden), bf16) for r in sizes),
        in_specs=[pl.BlockSpec(memory_space=pltpu.SMEM)]
        + [once(c.shape) for c in ctx_parts]
        + [
            once(nlt.shape),
            once(gft.shape),
            once(gb.shape),
            pl.BlockSpec((1, rows, hidden), lambda i: (i, 0, 0)),
            pl.BlockSpec((1, rows, hidden), lambda i: (i, 0, 0)),
            once(sums.shape),
            once(gbup.shape),
        ],
        out_specs=tuple(pl.BlockSpec((slabs, 1, r, hidden), lambda i: (0, i, 0, 0)) for r in sizes),
        scratch_shapes=[pltpu.VMEM((parts, group, gb.shape[1]), f32)],
        compiler_params=pltpu.CompilerParams(vmem_limit_bytes=VMEM_BYTES),
        cost_estimate=pl.CostEstimate(flops=11_000_000_000, bytes_accessed=28_000_000, transcendentals=0),
        name="outer_products",
    )(me, *ctx_parts, nlt, gft, gb, pre, hid, sums, gbup)


def finish_kernel(up_rows, own, total_ref, up_ref, down_ref, wo_ref, small_ref):
    rest = total_ref[...].astype(f32)
    up_ref[...] = rest[0:up_rows]
    down_ref[...] = rest[up_rows : 2 * up_rows]
    at = 2 * up_rows
    wo_ref[...] = rest[at : at + own]
    small_ref[...] = rest[at + own : at + own + 8]


def finished(total, up_rows, own):
    hidden = total.shape[1]
    whole = lambda: pl.BlockSpec(memory_space=pltpu.VMEM)
    return pl.pallas_call(
        functools.partial(finish_kernel, up_rows, own),
        out_shape=tuple(jax.ShapeDtypeStruct((r, hidden), f32) for r in (up_rows, up_rows, own, 8)),
        in_specs=[whole()],
        out_specs=tuple(whole() for _ in range(4)),
        cost_estimate=pl.CostEstimate(flops=2_000_000_000, bytes_accessed=2_000_000, transcendentals=0),
        name="finished",
    )(total)


def total_kernel(base_ref, *refs):
    total = base_ref[...]
    for ref in refs[:-1]:
        total = total + ref[...].astype(f32)
    refs[-1][...] = total


def token_total(base, pieces):
    rows, width = base.shape
    tile = 256
    tall = pl.BlockSpec((tile, width), lambda i: (i, 0))
    return pl.pallas_call(
        total_kernel,
        grid=(rows // tile,),
        out_shape=jax.ShapeDtypeStruct(base.shape, f32),
        in_specs=[tall] * (1 + len(pieces)),
        out_specs=tall,
        compiler_params=pltpu.CompilerParams(vmem_limit_bytes=VMEM_BYTES),
        cost_estimate=pl.CostEstimate(flops=TOTAL_FLOPS, bytes_accessed=9_000_000, transcendentals=0),
        name="token_total",
    )(base, *pieces)


TOTAL_FLOPS = 1_000_000_000
ALL = ("dp", "seq", "ffn")


def flip_send(array, axis, bits):
    count = lax.axis_size(axis)
    return lax.ppermute(array, axis, [(i, i ^ bits) for i in range(count)])


def shards(
    tokens, w_query, w_key, w_value, w_output, b_query, b_value, b_output, w_up, b_up, w_down, b_down,
    gain_attn, shift_attn, gain_ffn, shift_ffn, segment_ids, random_blocks, global_blocks, cotangent,
):
    seq_n, dp_n, ffn_n = lax.axis_size("seq"), lax.axis_size("dp"), lax.axis_size("ffn")
    outer, devices = dp_n * seq_n, dp_n * seq_n * ffn_n
    me = lax.axis_index("seq")
    here = (lax.axis_index("dp") * seq_n + me) * ffn_n + lax.axis_index("ffn")
    own, width = w_query.shape
    own_pad = round_up(own, 8)
    group = width // seq_n
    heads = group // HEAD_DIM
    features = tokens[0]
    rows = features.shape[0]
    order = jnp.stack([me ^ k for k in range(seq_n)])
    me_ref = me.astype(jnp.int32)[None]

    near = [features] + [None] * (seq_n - 1)
    for k in sorted(range(1, seq_n), key=lambda k: (k & (k - 1), -k)):
        bit = k & -k
        near[k] = flip_send(features if bit == k else near[k ^ bit], "seq", bit)

    vec = jnp.stack([b_output, b_down, gain_attn, shift_attn, gain_ffn, shift_ffn, b_query, b_value], axis=1)
    up_rows = w_up.shape[0]
    share_up = lax.dynamic_slice(b_up, (here // ffn_n * up_rows,), (up_rows,)).reshape(ffn_n, own).T
    more = jnp.pad(share_up, ((0, 0), (HEAD_DIM + 8, PAIR - HEAD_DIM - 8 - ffn_n)))
    vec = jnp.pad(vec, ((0, 0), (HEAD_DIM, PAIR - HEAD_DIM - 8)))
    seg = segment_ids[0].reshape(seq_n, rows)
    rand = random_blocks.reshape(-1)
    pack, rest = packed_weights(
        w_query, w_key, w_value, w_output, w_up, w_down, vec, more, dp_n, seq_n, ffn_n
    )
    lanes = pack.shape[4]
    pack, seg, rand = lax.optimization_barrier((pack, seg, rand))
    pack = lax.all_to_all(
        pack.reshape(devices, own_pad, lanes), ALL, split_axis=0, concat_axis=0, tiled=True
    )
    rest = lax.all_gather(rest, ALL, axis=0, tiled=False)
    w_own = pack[:, :own].reshape(width, lanes)
    share = devices // seq_n
    vecs = w_own[:, lanes - HEAD_DIM : lanes - HEAD_DIM + 8].astype(f32).T
    biases = lax.dynamic_slice(vecs, (6, me * group), (2, group))
    bias_up = w_own[:, lanes - HEAD_DIM + 8 : lanes - HEAD_DIM + 8 + ffn_n].reshape(outer, ffn_n, own, ffn_n)
    bias_up = bias_up.transpose(1, 0, 3, 2).reshape(ffn_n, width).astype(f32)
    by_head = biases[1].reshape(heads, 1, HEAD_DIM)
    b_kv = jnp.concatenate([jnp.zeros_like(by_head), by_head], axis=1).reshape(1, heads * PAIR)

    far = seq_n // 2
    ctx_far, (lse_far, lseg, glob_ctx, k_all, v_all, q_all, mask_all) = attention_forward(
        me_ref, rand, global_blocks, near, seg, w_own, b_kv, biases[0][:, None]
    )
    ctx_parts = [None] * far + [flip_send(ctx_far[k - far], "seq", k) for k in range(far, seq_n)]
    ctx_near, lse_near = attention_near(
        me_ref, rand, global_blocks, k_all, v_all, q_all, mask_all, glob_ctx, seq_n
    )
    ctx_parts[far:], ctx_parts[0] = lax.optimization_barrier((ctx_parts[far:], ctx_near[0]))
    for k in range(1, far):
        ctx_parts[k] = flip_send(ctx_near[k], "seq", k)

    at = 2 * up_rows
    rest = rest.reshape(outer, ffn_n, rest.shape[1], width)
    w_o = rest[:, :, at : at + own].reshape(width, width)
    direct = up_rows % 16 == 0 and own % 8 == 0 and outer % seq_n == 0 and (outer // seq_n) * ffn_n * own == group
    if not direct:
        rest = rest[:, :, :at].reshape(outer, ffn_n, 2, up_rows, width).transpose(1, 2, 0, 3, 4)
        rest = rest.reshape(1, ffn_n, 2 * outer * up_rows, width)
    slabs, slab_rows = (outer, up_rows) if direct else (1, outer * up_rows)

    got = rows_chain(
        me_ref, ctx_parts, features, cotangent[0], rest, slab_rows, own if direct else 0,
        vecs if direct else w_o, vecs, bias_up,
    )
    out, grad_resid_one, hidden, grad_pre, normed_t, grad_ffn_t, grad_branch = got[:7]
    grad_ctx, (sums, grad_bias_up) = got[7 : 7 + seq_n], got[7 + seq_n :]
    do = [grad_ctx[0]] + [flip_send(grad_ctx[k], "seq", k) for k in range(1, seq_n)]

    payload = outer_products(
        me_ref, ctx_parts, normed_t, grad_ffn_t, grad_branch, grad_pre, hidden, sums, grad_bias_up, slabs, slab_rows,
        own if direct else 0, APART if direct else 0,
    )
    payload, apart = payload if direct and APART else (payload[0], None)
    if not direct:
        grad_out = dot_nn(jnp.concatenate(ctx_parts, axis=0), grad_branch).astype(bf16)
        grad_out = grad_out.reshape(seq_n, group, width)[order].reshape(outer, ffn_n, own, width)
        top = jnp.broadcast_to(grad_bias_up[None, :ffn_n, None], (outer, ffn_n, 1, width))
        small = jnp.concatenate([top, jnp.broadcast_to(sums[None, None, :7], (outer, ffn_n, 7, width))], axis=2)
        small = small.astype(bf16)
        payload = payload.reshape(ffn_n, 2, outer, up_rows, width).transpose(2, 0, 1, 3, 4)
        payload = jnp.concatenate([payload.reshape(outer, ffn_n, at, width), grad_out, small], axis=2)
        payload = jnp.pad(payload, ((0, 0), (0, 0), (0, -payload.shape[2] % 32), (0, 0)))
    payload, apart, do = lax.optimization_barrier((payload, apart, do))
    total = lax.psum_scatter(payload.reshape(-1, width), ("dp", "seq"), scatter_dimension=0, tiled=True)
    if apart is not None:
        apart = lax.all_to_all(
            apart.reshape(devices, APART, width), ALL, split_axis=0, concat_axis=0, tiled=True
        )

    got = attention_backward(
        me_ref, rand, global_blocks, do, k_all, v_all, q_all, mask_all, seg, lse_near, lse_far, lseg, w_own,
        grad_resid_one,
    )
    dq, dkv, grad_features = got[:3]
    part = [None] + list(got[3:])
    bit = 1
    while bit < seq_n:
        for k in range(seq_n):
            if k & -k == bit and k != bit:
                came = flip_send(part[k], "seq", bit).astype(f32)
                part[k ^ bit] = (part[k ^ bit].astype(f32) + came).astype(bf16)
        bit *= 2
    grad_w = projection_gradients(near, dq, dkv, own, devices)
    grad_w, part = lax.optimization_barrier((grad_w, part[1:]))
    grad_w, apart = lax.optimization_barrier((grad_w, apart))
    part = [None] + part
    bit = seq_n // 2
    staged = total
    total = lax.psum_scatter(total, "ffn", scatter_dimension=0, tiled=True)
    pieces = []
    while bit:
        pieces.append(flip_send(part[bit], "seq", bit))
        bit //= 2
    pieces = lax.optimization_barrier((pieces, staged))[0]
    grad_features = token_total(grad_features, pieces)
    grad_w = lax.all_to_all(grad_w, ALL, split_axis=0, concat_axis=0, tiled=True)
    if direct:
        out_up, out_down, out_output, notes = finished(total, up_rows, own)
    else:
        total = total.astype(f32)
        out_up, out_down, out_output = total[:up_rows], total[up_rows:at], total[at : at + own]
        notes = total[at + own : at + own + 8]
    out_bias_up = notes[0]
    out_vecs = lax.dynamic_slice(notes, (1, here * own), (6, own))
    out_query, out_key, out_value, col_sums = unpacked_gradients(
        grad_w.reshape(dp_n, seq_n, ffn_n, own_pad, lanes), own, width
    )
    col = lax.dynamic_index_in_dim(col_sums, here // share, keepdims=False)[:own, HEAD_DIM : HEAD_DIM + 2]
    out_b = [col[:, 0], col[:, 1]]
    return (
        out[None],
        grad_features[None],
        out_query,
        out_key,
        out_value,
        out_output,
        out_b[0],
        out_b[1],
        out_vecs[0],
        out_up,
        out_bias_up,
        out_down,
        out_vecs[1],
        out_vecs[2],
        out_vecs[3],
        out_vecs[4],
        out_vecs[5],
    )


def solution(mesh):
    return jax.shard_map(
        shards,
        mesh=mesh,
        in_specs=(
            P(("dp", "ffn"), "seq", None),
            P(("dp", "seq", "ffn"), None),
            P(("dp", "seq", "ffn"), None),
            P(("dp", "seq", "ffn"), None),
            P(("dp", "seq", "ffn"), None),
            P(("dp", "seq", "ffn")),
            P(("dp", "seq", "ffn")),
            P(("dp", "seq", "ffn")),
            P(("dp", "seq"), "ffn"),
            P("ffn"),
            P(("dp", "seq"), "ffn"),
            P(("dp", "seq", "ffn")),
            P(("dp", "seq", "ffn")),
            P(("dp", "seq", "ffn")),
            P(("dp", "seq", "ffn")),
            P(("dp", "seq", "ffn")),
            P(("dp", "ffn"), None),
            P(("dp", "ffn"), "seq", None, None),
            P(("dp", "ffn"), None),
            P(("dp", "ffn"), "seq", None),
        ),
        out_specs=(
            P(("dp", "ffn"), "seq", None),
            P(("dp", "ffn"), "seq", None),
            P(("dp", "seq", "ffn"), None),
            P(("dp", "seq", "ffn"), None),
            P(("dp", "seq", "ffn"), None),
            P(("dp", "seq", "ffn"), None),
            P(("dp", "seq", "ffn")),
            P(("dp", "seq", "ffn")),
            P(("dp", "seq", "ffn")),
            P(("dp", "seq"), "ffn"),
            P("ffn"),
            P(("dp", "seq"), "ffn"),
            P(("dp", "seq", "ffn")),
            P(("dp", "seq", "ffn")),
            P(("dp", "seq", "ffn")),
            P(("dp", "seq", "ffn")),
            P(("dp", "seq", "ffn")),
        ),
        check_vma=False,
    )
```

```python
import functools
import jax
import jax.numpy as jnp
from jax import lax
from jax.experimental import pallas as pl
from jax.sharding import PartitionSpec as P
from jax.experimental.pallas import tpu as pltpu

HEAD_DIM = 64
BLOCK = 64
PAIR = 2 * BLOCK
MASKED = -1e30
bf16 = jnp.bfloat16
f32 = jnp.float32


def dot_nn(a, b):
    return lax.dot_general(a, b, (((1,), (0,)), ((), ())), preferred_element_type=f32)


def dot_nt(a, b):
    return lax.dot_general(a, b, (((1,), (1,)), ((), ())), preferred_element_type=f32)


def dot_tn(a, b):
    return lax.dot_general(a, b, (((0,), (0,)), ((), ())), preferred_element_type=f32)


def slots(rand_ref, glob_ref, flip, head, pair, nblocks):
    first = (2 * pair) ^ flip

    def row(block):
        return pl.multiple_of(block * BLOCK, BLOCK)

    def near(block):
        bad = (block < 0) | (block >= nblocks) | (block == glob_ref[0, 0]) | (block == glob_ref[0, 1])
        return row(jnp.where(bad, nblocks, block ^ flip))

    def drawn(block):
        at = (head * nblocks + block) * 3
        return [row(rand_ref[at + j] ^ flip) for j in range(3)]

    shared = [near(first), near(first + 1)] + [row(glob_ref[0, j] ^ flip) for j in range(2)]
    return shared, [near(first - 1)] + drawn(first), [near(first + 2)] + drawn(first + 1)


def stack_rows(ref, offsets, lanes):
    return jnp.concatenate([ref[pl.ds(o, BLOCK), lanes] for o in offsets], axis=0)


def lane_halves(width, dtype):
    lane = lax.broadcasted_iota(jnp.int32, (1, width), 1) % PAIR
    first = (lane < BLOCK).astype(dtype)
    second = (lane >= BLOCK).astype(dtype)
    return first, second


UNROLL = 4
BACK_UNROLL = 4
APART = 0
VMEM_BYTES = 62 << 20


def head_lanes(h):
    return slice(h * PAIR, (h + 1) * PAIR)


def query_columns(q_ref, mask_ref, h, at):
    return jnp.concatenate([q_ref[h * BLOCK : (h + 1) * BLOCK, pl.ds(at, PAIR)], mask_ref[:, pl.ds(at, PAIR)]], axis=0)


def global_queries(q_ref, mask_ref, h, gl):
    return jnp.concatenate(
        [
            global_columns(q_ref, slice(h * BLOCK, (h + 1) * BLOCK), gl),
            global_columns(mask_ref, slice(0, BLOCK), gl),
        ],
        axis=0,
    ).astype(bf16)


def placed(me_ref, glob_ref, nblocks, chunks):
    flip = me_ref[0] * (nblocks // chunks)
    return flip, [glob_ref[0, j] ^ flip for j in range(2)]


def global_columns(src_ref, rows, gl):
    lane = lax.broadcasted_iota(jnp.int32, (1, PAIR), 1)
    parts = []
    for g in range(2):
        block = gl[g]
        at = pl.multiple_of((block // 2) * PAIR, PAIR)
        both = src_ref[rows, pl.ds(at, PAIR)].astype(f32)
        moved = pltpu.roll(both, BLOCK, 1)
        parts.append(jnp.where(block % 2 == g, both, moved))
    return jnp.where(lane < BLOCK, parts[0], parts[1])


def put_global_columns(dst_ref, rows, gl, value, per_chunk, low, high):
    lane = lax.broadcasted_iota(jnp.int32, (1, PAIR), 1)
    moved = pltpu.roll(value, BLOCK, 1)
    for g in range(2):
        pair = gl[g] // 2
        half = gl[g] % 2
        chunk = pair // per_chunk

        @pl.when((chunk >= low) & (chunk < high))
        def _():
            at = pl.multiple_of((pair % per_chunk) * PAIR, PAIR)
            src = jnp.where(half == g, value, moved)
            old = dst_ref[chunk - low, rows, pl.ds(at, PAIR)].astype(f32)
            new = jnp.where((lane >= BLOCK) == (half == 1), src, old)
            dst_ref[chunk - low, rows, pl.ds(at, PAIR)] = new.astype(dst_ref.dtype)


def project_rows(x, seg, w_ref, wq, bkv_ref, bq_ref, k_ref, v_ref, q_ref, mask_ref, at):
    n = x.shape[0]
    lanes = v_ref.shape[1]
    y = dot_nn(x, w_ref[:, 0:lanes]) + bkv_ref[...]
    spot = lax.broadcasted_iota(jnp.int32, (PAIR, n), 0) - BLOCK
    mark = jnp.transpose((spot == seg).astype(f32), (1, 0))
    lane = lax.broadcasted_iota(jnp.int32, (1, PAIR), 1)
    rows = pl.ds(at, n)
    v_ref[rows, :] = y.astype(bf16)
    for h in range(lanes // PAIR):
        k_ref[rows, head_lanes(h)] = jnp.where(lane < BLOCK, y[:, head_lanes(h)], mark).astype(bf16)
    z = (dot_nt(wq, x) + bq_ref[...]).astype(bf16)
    q_ref[:, rows] = (z.astype(f32) * HEAD_DIM ** -0.5).astype(bf16)
    row = lax.broadcasted_iota(jnp.int32, (BLOCK, n), 0)
    mask_ref[:, rows] = jnp.where((row <= 16) & (row != seg), MASKED, 0.0).astype(bf16)


def query_weights(w_ref, heads):
    at = heads * PAIR
    cols = w_ref[:, at : at + 2 * PAIR].astype(f32)
    return jnp.transpose(cols, (1, 0))[0 : heads * HEAD_DIM].astype(bf16)


def sparse_forward(heads, low, high, per_chunk, rand_ref, glob_ref, flip, k_ref, kv_ref, q_ref, mask_ref, out_ref, lse_ref):
    nblocks = (k_ref.shape[0] - BLOCK) // BLOCK
    first, second = lane_halves(PAIR, bf16)
    lane = lax.broadcasted_iota(jnp.int32, (1, PAIR), 1)

    def one_pair(spot):
        chunk = spot // per_chunk
        local = pl.multiple_of((spot % per_chunk) * PAIR, PAIR)
        pair = low * per_chunk + spot
        at = pl.multiple_of(pair * PAIR, PAIR)
        for h in range(heads):
            shared, mine, other = slots(rand_ref, glob_ref, flip, h, pair, nblocks)
            kl = head_lanes(h)
            q = query_columns(q_ref, mask_ref, h, at)
            s_sh = dot_nn(stack_rows(k_ref, shared, kl), q)
            k_pr = jnp.concatenate([stack_rows(k_ref, mine, kl), stack_rows(k_ref, other, kl)], axis=1)
            s_pr = dot_nn(k_pr, jnp.concatenate([q * first, q * second], axis=0))
            peak = jnp.maximum(jnp.max(s_sh, axis=0, keepdims=True), jnp.max(s_pr, axis=0, keepdims=True))
            e_sh = jnp.exp(s_sh - peak)
            e_pr = jnp.exp(s_pr - peak)
            total = jnp.sum(e_sh, axis=0, keepdims=True) + jnp.sum(e_pr, axis=0, keepdims=True)
            inv = 1.0 / total
            p_sh = (e_sh * inv).astype(bf16)
            p_pr = (e_pr * inv).astype(bf16)
            v_pr = jnp.concatenate([stack_rows(kv_ref, mine, kl), stack_rows(kv_ref, other, kl)], axis=1)
            o_sh = dot_tn(stack_rows(kv_ref, shared, kl), p_sh)
            o_pr = dot_tn(v_pr, p_pr)
            ctx = o_sh[BLOCK:PAIR] + jnp.where(lane < BLOCK, o_pr[BLOCK:PAIR], o_pr[PAIR + BLOCK : 2 * PAIR])
            out_ref[chunk, h * BLOCK : (h + 1) * BLOCK, pl.ds(local, PAIR)] = ctx.astype(bf16)
            lse_ref[h, pl.ds(spot, 1), :] = peak + jnp.log(total)

    @pl.loop(0, (high - low) * per_chunk // UNROLL)
    def _(some):
        for i in range(UNROLL):
            one_pair(UNROLL * some + i)


def forward_kernel(heads, chunks, me_ref, rand_ref, glob_ref, *refs):
    x_refs = refs[0:chunks]
    seg_ref, w_ref, bkv_ref, bq_ref = refs[chunks : chunks + 4]
    far = chunks // 2
    out_refs = refs[chunks + 4 : chunks + 4 + far]
    lse_ref, lseg_ref, glob_ctx_ref = refs[chunks + 4 + far : chunks + 7 + far]
    saved_refs = refs[chunks + 7 + far : chunks + 11 + far]
    s_sc, out_ref, seg_sc, k_sc, v_sc, q_sc, mask_sc, sems = refs[chunks + 11 + far :]
    rows = x_refs[0].shape[0]
    length = rows * chunks
    per_chunk = length // PAIR // chunks
    flip, gl = placed(me_ref, glob_ref, length // BLOCK, chunks)
    tile = 256
    wq = query_weights(w_ref, heads)
    for c in range(chunks):
        seg_sc[c : c + 1, :] = seg_ref[pl.ds(me_ref[0] ^ c, 1), :]
    for c in range(chunks):

        @pl.loop(0, rows // tile)
        def _(t):
            at = pl.multiple_of(t * tile, tile)
            project_rows(
                x_refs[c][pl.ds(at, tile), :], seg_sc[c : c + 1, pl.ds(at, tile)], w_ref, wq, bkv_ref, bq_ref,
                k_sc, v_sc, q_sc, mask_sc, pl.multiple_of(c * rows + t * tile, tile),
            )

    null_lane = lax.broadcasted_iota(jnp.int32, (BLOCK, heads * PAIR), 1) % PAIR
    k_sc[pl.ds(length, BLOCK), :] = (null_lane == BLOCK + 16).astype(f32).astype(bf16)
    v_sc[pl.ds(length, BLOCK), :] = jnp.zeros((BLOCK, heads * PAIR), bf16)
    saves = [
        pltpu.make_async_copy(src, dst, sems.at[i])
        for i, (src, dst) in enumerate(zip((k_sc, v_sc, q_sc, mask_sc), saved_refs))
    ]
    for save in saves:
        save.start()
    sparse_forward(heads, far, chunks, per_chunk, rand_ref, glob_ref, flip, k_sc, v_sc, q_sc, mask_sc, out_ref, lse_ref)

    step = 512
    queries = [global_queries(q_sc, mask_sc, h, gl) for h in range(heads)]

    def score(c, peaks):
        at = pl.multiple_of(c * step, step)
        new = []
        for h in range(heads):
            got = dot_nn(k_sc[pl.ds(at, step), head_lanes(h)], queries[h])
            s_sc[h, pl.ds(at, step), :] = got
            new.append(jnp.maximum(peaks[h], jnp.max(got, axis=0, keepdims=True)))
        return tuple(new)

    peaks = lax.fori_loop(0, length // step, score, (jnp.full((1, PAIR), MASKED, f32),) * heads)

    def gather(c, carry):
        at = pl.multiple_of(c * step, step)
        new = []
        for h in range(heads):
            total, ctx = carry[h]
            e = jnp.exp(s_sc[h, pl.ds(at, step), :] - peaks[h])
            ctx = ctx + dot_tn(v_sc[pl.ds(at, step), head_lanes(h)], e.astype(bf16))
            new.append((total + jnp.sum(e, axis=0, keepdims=True), ctx))
        return tuple(new)

    start = (jnp.zeros((1, PAIR), f32), jnp.zeros((PAIR, PAIR), f32))
    sums = lax.fori_loop(0, length // step, gather, (start,) * heads)
    for h in range(heads):
        total, ctx = sums[h]
        ctx = ctx[BLOCK:PAIR] * (1.0 / total)
        glob_ctx_ref[h] = ctx
        put_global_columns(out_ref, slice(h * BLOCK, (h + 1) * BLOCK), gl, ctx, per_chunk, far, chunks)
        lseg_ref[h : h + 1, :] = peaks[h] + jnp.log(total)
    for c in range(far):
        out_refs[c][...] = out_ref[c]
    for save in saves:
        save.wait()


def attention_forward(me, rand, glob, x, seg, w, b_kv, b_q):
    chunks = len(x)
    far = chunks // 2
    rows = x[0].shape[0]
    length = rows * chunks
    heads = b_q.shape[0] // HEAD_DIM
    whole = lambda: pl.BlockSpec(memory_space=pltpu.VMEM)
    got = pl.pallas_call(
        functools.partial(forward_kernel, heads, chunks),
        out_shape=(jax.ShapeDtypeStruct((heads * HEAD_DIM, rows), bf16),) * far
        + (
            jax.ShapeDtypeStruct((heads, length // PAIR // 2, PAIR), f32),
            jax.ShapeDtypeStruct((heads, PAIR), f32),
            jax.ShapeDtypeStruct((heads, HEAD_DIM, PAIR), f32),
            jax.ShapeDtypeStruct((length + BLOCK, heads * PAIR), bf16),
            jax.ShapeDtypeStruct((length + BLOCK, heads * PAIR), bf16),
            jax.ShapeDtypeStruct((heads * HEAD_DIM, length), bf16),
            jax.ShapeDtypeStruct((BLOCK, length), bf16),
        ),
        in_specs=[pl.BlockSpec(memory_space=pltpu.SMEM)] * 3 + [whole() for _ in range(chunks + 4)],
        out_specs=tuple([whole() for _ in range(far + 3)] + [pl.BlockSpec(memory_space=pl.ANY)] * 4),
        scratch_shapes=[
            pltpu.VMEM((heads, length, PAIR), f32),
            pltpu.VMEM((far, heads * HEAD_DIM, rows), bf16),
            pltpu.VMEM((chunks, rows), jnp.int32),
            pltpu.VMEM((length + BLOCK, heads * PAIR), bf16),
            pltpu.VMEM((length + BLOCK, heads * PAIR), bf16),
            pltpu.VMEM((heads * HEAD_DIM, length), bf16),
            pltpu.VMEM((BLOCK, length), bf16),
            pltpu.SemaphoreType.DMA((4,)),
        ],
        compiler_params=pltpu.CompilerParams(vmem_limit_bytes=VMEM_BYTES),
        cost_estimate=pl.CostEstimate(flops=10_000_000_000, bytes_accessed=16_000_000, transcendentals=6_000_000),
        name="attention_forward",
    )(me, rand, glob, *x, seg, w, b_kv, b_q)
    return got[:far], got[far:]


def near_kernel(heads, chunks, me_ref, rand_ref, glob_ref, k_ref, kv_ref, q_ref, mask_ref, glob_ctx_ref, *refs):
    half = chunks // 2
    out_refs = refs[:half]
    lse_ref, out_ref = refs[half:]
    length = q_ref.shape[1]
    per_chunk = length // PAIR // chunks
    flip, gl = placed(me_ref, glob_ref, length // BLOCK, chunks)
    sparse_forward(heads, 0, half, per_chunk, rand_ref, glob_ref, flip, k_ref, kv_ref, q_ref, mask_ref, out_ref, lse_ref)
    for h in range(heads):
        put_global_columns(out_ref, slice(h * BLOCK, (h + 1) * BLOCK), gl, glob_ctx_ref[h], per_chunk, 0, half)
    for c in range(half):
        out_refs[c][...] = out_ref[c]


def attention_near(me, rand, glob, k, kv, q, mask, glob_ctx, chunks):
    heads = glob_ctx.shape[0]
    half = chunks // 2
    length = q.shape[1]
    rows = length // chunks
    whole = lambda: pl.BlockSpec(memory_space=pltpu.VMEM)
    got = pl.pallas_call(
        functools.partial(near_kernel, heads, chunks),
        out_shape=(jax.ShapeDtypeStruct((heads * HEAD_DIM, rows), bf16),) * half
        + (jax.ShapeDtypeStruct((heads, length // PAIR // 2, PAIR), f32),),
        in_specs=[pl.BlockSpec(memory_space=pltpu.SMEM)] * 3 + [whole() for _ in range(5)],
        out_specs=tuple(whole() for _ in range(half + 1)),
        scratch_shapes=[pltpu.VMEM((half, heads * HEAD_DIM, rows), bf16)],
        compiler_params=pltpu.CompilerParams(vmem_limit_bytes=VMEM_BYTES),
        cost_estimate=pl.CostEstimate(flops=6_000_000_000, bytes_accessed=9_000_000, transcendentals=3_000_000),
        name="attention_near",
    )(me, rand, glob, k, kv, q, mask, glob_ctx)
    return got[:half], got[half]


def backward_kernel(heads, chunks, me_ref, rand_ref, glob_ref, *refs):
    do_refs = refs[:chunks]
    (k_ref, kv_ref, q_ref, mask_ref, seg_ref, lse_near_ref, lse_far_ref, lseg_ref, w_ref, resid_hbm, dq_hbm, dkv_hbm,
     first_ref) = refs[chunks : chunks + 13]
    part_refs = refs[chunks + 13 : 2 * chunks + 12]
    (do_sc, acc, p_sc, d_sc, seg_sc, line_sc, lse_ref, row_sc, resid_ref, dq_ref, dkv_ref, sems) = refs[2 * chunks + 12 :]
    fetch = pltpu.make_async_copy(resid_hbm, resid_ref, sems.at[0])
    fetch.start()
    rows = do_refs[0].shape[1]
    length = rows * chunks
    npairs = length // PAIR
    per_chunk = npairs // chunks
    scale = HEAD_DIM ** -0.5
    flip, gl = placed(me_ref, glob_ref, length // BLOCK, chunks)
    lse_ref[:, 0 : npairs // 2, :] = lse_near_ref[...]
    lse_ref[:, npairs // 2 :, :] = lse_far_ref[...]
    for c in range(chunks):
        do_sc[:, c * rows : (c + 1) * rows] = do_refs[c][...]
        row_sc[c : c + 1, :] = seg_ref[pl.ds(me_ref[0] ^ c, 1), :].astype(f32)

        @pl.loop(0, per_chunk // 4)
        def _(some):
            for i in range(4):
                t = 4 * some + i
                line = row_sc[c : c + 1, pl.ds(pl.multiple_of(t * PAIR, PAIR), PAIR)]
                line_sc[c * per_chunk + t] = line
                to = pl.multiple_of(c * rows + t * PAIR, PAIR)
                seg_sc[pl.ds(to, PAIR), :] = jnp.transpose(jnp.broadcast_to(line, (PAIR, PAIR)), (1, 0))

    seg_sc[length : length + BLOCK, :] = jnp.full((BLOCK, PAIR), -1.0, f32)
    first2, second2 = lane_halves(2 * PAIR, bf16)
    ffirst, fsecond = lane_halves(PAIR, f32)
    lane = lax.broadcasted_iota(jnp.int32, (1, PAIR), 1)
    line_row = lax.broadcasted_iota(jnp.int32, (PAIR, 1), 0)
    zeros = jnp.zeros((BLOCK, PAIR), bf16)
    blank = jnp.zeros((PAIR, PAIR), bf16)

    def head_rows(h):
        return slice(h * BLOCK, (h + 1) * BLOCK)

    def joint(q, mask, do):
        left = jnp.concatenate([q, mask, blank], axis=0)
        right = jnp.concatenate([blank, zeros, do], axis=0)
        return jnp.concatenate([left, right], axis=1)

    def sources(q, do):
        top = jnp.concatenate([q, zeros], axis=1)
        return jnp.concatenate([top, jnp.concatenate([zeros, do], axis=1)], axis=0)

    step = 512
    mask_glob = global_columns(mask_ref, slice(0, BLOCK), gl).astype(bf16)
    q_glob = [global_columns(q_ref, head_rows(h), gl).astype(bf16) for h in range(heads)]
    do_glob = [global_columns(do_sc, head_rows(h), gl).astype(bf16) for h in range(heads)]

    def weigh(c, deltas):
        at = pl.multiple_of(c * step, step)
        new = []
        for h in range(heads):
            left = jnp.concatenate([k_ref[pl.ds(at, step), head_lanes(h)], kv_ref[pl.ds(at, step), head_lanes(h)]], axis=1)
            both = dot_nn(left, joint(q_glob[h], mask_glob, do_glob[h]))
            p = jnp.exp(both[:, 0:PAIR] - lseg_ref[h : h + 1, :])
            dp = both[:, PAIR:]
            p_sc[h, pl.ds(at, step), :] = p
            d_sc[h, pl.ds(at, step), :] = dp
            new.append(deltas[h] + jnp.sum(p * dp, axis=0, keepdims=True))
        return tuple(new)

    deltas = lax.fori_loop(0, length // step, weigh, (jnp.zeros((1, PAIR), f32),) * heads)

    def spread(c, dqs):
        at = pl.multiple_of(c * step, step)
        new = []
        for h in range(heads):
            p = p_sc[h, pl.ds(at, step), :]
            ds = (p * (d_sc[h, pl.ds(at, step), :] - deltas[h])).astype(bf16)
            both = jnp.concatenate([ds, p.astype(bf16)], axis=1)
            acc[h, pl.ds(at, step), :] = dot_nt(both, sources(q_glob[h], do_glob[h]))
            new.append(dqs[h] + dot_tn(k_ref[pl.ds(at, step), head_lanes(h)], ds))
        return tuple(new)

    dqs = lax.fori_loop(0, length // step, spread, (jnp.zeros((PAIR, PAIR), f32),) * heads)
    for h in range(heads):
        acc[h, pl.ds(length, BLOCK), :] = jnp.zeros((BLOCK, PAIR), f32)

    def one_pair(pair):
        chunk = pair // per_chunk
        local = pl.multiple_of((pair % per_chunk) * PAIR, PAIR)
        at = pl.multiple_of(pair * PAIR, PAIR)
        hit_first = (gl[0] == 2 * pair) | (gl[1] == 2 * pair)
        hit_second = (gl[0] == 2 * pair + 1) | (gl[1] == 2 * pair + 1)
        shut = ffirst * jnp.where(hit_first, -MASKED, 0.0) + fsecond * jnp.where(hit_second, -MASKED, 0.0)
        every = slice(0, PAIR)
        for h in range(heads):
            kl = head_lanes(h)
            shared, mine, other = slots(rand_ref, glob_ref, flip, h, pair, length // BLOCK)
            q = q_ref[head_rows(h), pl.ds(at, PAIR)]
            do = do_sc[head_rows(h), pl.ds(at, PAIR)]
            lse = lse_ref[h, pl.ds(pair, 1), :] + shut
            src = sources(q, do)
            src2 = jnp.concatenate([src * first2, src * second2], axis=0)
            k_sh = stack_rows(k_ref, shared, kl)
            two_sh = dot_nn(
                jnp.concatenate([k_sh, stack_rows(kv_ref, shared, kl)], axis=1),
                joint(q, mask_ref[:, pl.ds(at, PAIR)], do),
            )
            kv_pr = jnp.concatenate([stack_rows(kv_ref, mine, kl), stack_rows(kv_ref, other, kl)], axis=1)
            two_pr = dot_nn(kv_pr, src2)
            seg_pr = jnp.where(lane < BLOCK, stack_rows(seg_sc, mine, every), stack_rows(seg_sc, other, every))
            agree = seg_pr == line_sc[pair]
            p_sh = jnp.exp(two_sh[:, 0:PAIR] - lse)
            p_pr = jnp.where(agree, jnp.exp(two_pr[:, 0:PAIR] - lse), 0.0)
            d_sh, d_pr = two_sh[:, PAIR:], two_pr[:, PAIR:]
            delta = jnp.sum(p_sh * d_sh, axis=0, keepdims=True) + jnp.sum(p_pr * d_pr, axis=0, keepdims=True)
            ds_sh = (p_sh * (d_sh - delta)).astype(bf16)
            ds_pr = (p_pr * (d_pr - delta)).astype(bf16)
            g_sh = dot_nt(jnp.concatenate([ds_sh, p_sh.astype(bf16)], axis=1), src)
            g_pr = dot_nt(jnp.concatenate([ds_pr, p_pr.astype(bf16)], axis=1), src2)
            for j, o in enumerate(shared):
                acc[h, pl.ds(o, BLOCK), :] += g_sh[j * BLOCK : (j + 1) * BLOCK]
            for j, o in enumerate(mine):
                acc[h, pl.ds(o, BLOCK), :] += g_pr[j * BLOCK : (j + 1) * BLOCK, 0:PAIR]
            for j, o in enumerate(other):
                acc[h, pl.ds(o, BLOCK), :] += g_pr[j * BLOCK : (j + 1) * BLOCK, PAIR:]
            t_pr = dot_tn(ds_pr, kv_pr)
            dq = dot_tn(ds_sh, k_sh) + jnp.where(line_row < BLOCK, t_pr[:, 0:PAIR], t_pr[:, PAIR:])
            dq = jnp.transpose(dq, (1, 0))[0:BLOCK]
            dq_ref[chunk, head_rows(h), pl.ds(local, PAIR)] = (dq * scale).astype(bf16)

    @pl.loop(0, npairs // BACK_UNROLL)
    def _(some):
        for i in range(BACK_UNROLL):
            one_pair(BACK_UNROLL * some + i)

    for h in range(heads):
        put_global_columns(dq_ref, head_rows(h), gl, dqs[h][0:BLOCK] * scale, per_chunk, 0, chunks)
        for c in range(chunks):
            dkv_ref[c, :, head_lanes(h)] = acc[h, pl.ds(c * rows, rows), :].astype(bf16)
    saves = [
        pltpu.make_async_copy(dq_ref, dq_hbm, sems.at[1]),
        pltpu.make_async_copy(dkv_ref, dkv_hbm, sems.at[2]),
    ]
    for save in saves:
        save.start()
    fetch.wait()
    tile = 256
    wq = query_weights(w_ref, heads)
    for c in range(chunks):

        @pl.loop(0, rows // tile)
        def _(t):
            at = pl.multiple_of(t * tile, tile)
            got = dot_tn(dq_ref[c, :, pl.ds(at, tile)], wq)
            got = got + dot_nt(dkv_ref[c, pl.ds(at, tile), :], w_ref[:, 0 : heads * PAIR])
            if c == 0:
                first_ref[pl.ds(at, tile), :] = resid_ref[pl.ds(at, tile), :] + got
            else:
                part_refs[c - 1][pl.ds(at, tile), :] = got.astype(bf16)
    for save in saves:
        save.wait()


def attention_backward(me, rand, glob, do, k, kv, q, mask, seg, lse_near, lse_far, lseg, w, resid):
    chunks = len(do)
    group, rows = do[0].shape
    heads = group // HEAD_DIM
    width = w.shape[0]
    length = rows * chunks
    whole = lambda: pl.BlockSpec(memory_space=pltpu.VMEM)
    return pl.pallas_call(
        functools.partial(backward_kernel, heads, chunks),
        out_shape=(
            jax.ShapeDtypeStruct((chunks, group, rows), bf16),
            jax.ShapeDtypeStruct((chunks, rows, heads * PAIR), bf16),
            jax.ShapeDtypeStruct((rows, width), f32),
        )
        + (jax.ShapeDtypeStruct((rows, width), bf16),) * (chunks - 1),
        in_specs=[pl.BlockSpec(memory_space=pltpu.SMEM)] * 3
        + [whole() for _ in range(chunks + 9)]
        + [pl.BlockSpec(memory_space=pl.ANY)],
        out_specs=tuple([pl.BlockSpec(memory_space=pl.ANY)] * 2 + [whole() for _ in range(chunks)]),
        scratch_shapes=[
            pltpu.VMEM((group, length), bf16),
            pltpu.VMEM((heads, length + BLOCK, PAIR), f32),
            pltpu.VMEM((heads, length, PAIR), f32),
            pltpu.VMEM((heads, length, PAIR), f32),
            pltpu.VMEM((length + BLOCK, PAIR), f32),
            pltpu.VMEM((length // PAIR, 1, PAIR), f32),
            pltpu.VMEM((heads, length // PAIR, PAIR), f32),
            pltpu.VMEM((chunks, rows), f32),
            pltpu.VMEM((rows, width), f32),
            pltpu.VMEM((chunks, group, rows), bf16),
            pltpu.VMEM((chunks, rows, heads * PAIR), bf16),
            pltpu.SemaphoreType.DMA((3,)),
        ],
        compiler_params=pltpu.CompilerParams(vmem_limit_bytes=VMEM_BYTES),
        cost_estimate=pl.CostEstimate(flops=30_000_000_000, bytes_accessed=24_000_000, transcendentals=8_000_000),
        name="attention_backward",
    )(me, rand, glob, *do, k, kv, q, mask, seg, lse_near, lse_far, lseg, w, resid)


def round_up(value, to):
    return -(-value // to) * to


def half_columns(ref, index, place):
    at = index // 2 * PAIR
    both = ref[:, at : at + PAIR].astype(f32)
    return both if index % 2 == place else pltpu.roll(both, BLOCK, 1)


def two_halves(first, second):
    lane = lax.broadcasted_iota(jnp.int32, (1, PAIR), 1)
    return jnp.where(lane < BLOCK, first, second)


def pack_kernel(seq_n, wq_ref, wk_ref, wv_ref, vec_ref, more_ref, pack_ref):
    own, width = wq_ref.shape
    heads = width // HEAD_DIM // seq_n
    blocks, inner = pack_ref.shape[0], pack_ref.shape[2]
    for s in range(seq_n):
        pieces = [
            two_halves(half_columns(wk_ref, s * heads + h, 0), half_columns(wv_ref, s * heads + h, 1))
            for h in range(heads)
        ]
        for h in range(0, heads, 2):
            second = half_columns(wq_ref, s * heads + h + 1, 1) if h + 1 < heads else (
                vec_ref[...].astype(f32) + more_ref[...].astype(f32)
            )
            pieces.append(two_halves(half_columns(wq_ref, s * heads + h, 0), second))
        piece = jnp.concatenate(pieces, axis=1).astype(bf16)
        for b in range(blocks):
            for i in range(inner):
                pack_ref[b, s, i] = piece


def rest_kernel(wo_ref, up_ref, down_ref, rest_ref):
    own = wo_ref.shape[0]
    u = up_ref.shape[0]
    rest_ref[0:u, :] = up_ref[...]
    rest_ref[u : 2 * u, :] = down_ref[...]
    rest_ref[2 * u : 2 * u + own, :] = wo_ref[...]


def packed_weights(w_q, w_k, w_v, w_o, w_up, w_down, vec, more, dp_n, seq_n, ffn_n):
    own, width = w_q.shape
    heads = width // HEAD_DIM // seq_n
    lanes = heads * PAIR + round_up(heads * HEAD_DIM, PAIR)
    u = w_up.shape[0]
    if own % 8 or u % 16:
        group = heads * HEAD_DIM
        cols = lambda w: w.reshape(own, seq_n, heads, HEAD_DIM).transpose(1, 0, 2, 3)
        kv = jnp.stack([cols(w_k), cols(w_v)], axis=3).reshape(seq_n, own, 2 * group)
        notes = jnp.broadcast_to((vec + more)[None, :, HEAD_DIM:], (seq_n, own, PAIR - HEAD_DIM))
        piece = jnp.concatenate([kv, cols(w_q).reshape(seq_n, own, group), notes], axis=2)
        piece = jnp.pad(piece, ((0, 0), (0, round_up(own, 8) - own), (0, 0)))
        pack = jnp.broadcast_to(piece[None, :, None], (dp_n, seq_n, ffn_n) + piece.shape[1:])
        w_o = jnp.pad(w_o, ((0, round_up(own, 8) - own), (0, 0)))
        return pack, jnp.concatenate([w_up, w_down, w_o], axis=0)
    whole = lambda: pl.BlockSpec(memory_space=pltpu.VMEM)
    rest = pl.pallas_call(
        rest_kernel,
        out_shape=jax.ShapeDtypeStruct((2 * u + own, width), bf16),
        in_specs=[whole() for _ in range(3)],
        out_specs=whole(),
        name="rest_weights",
    )(w_o, w_up, w_down)
    pack = pl.pallas_call(
        functools.partial(pack_kernel, seq_n),
        out_shape=jax.ShapeDtypeStruct((dp_n, seq_n, ffn_n, own, lanes), bf16),
        in_specs=[whole() for _ in range(5)],
        out_specs=whole(),
        name="packed_weights",
    )(w_q, w_k, w_v, vec, more)
    return pack, rest


def weights_kernel(chunks, direct, *refs):
    x_refs = refs[:chunks]
    dq_ref, dkv_ref, out_ref, acc, sum_sc = refs[chunks:]
    group = dq_ref.shape[1]
    lanes = dkv_ref.shape[2]
    full, width = acc.shape
    x = jnp.concatenate([r[...] for r in x_refs], axis=0)
    dkv = jnp.concatenate([dkv_ref[c] for c in range(chunks)], axis=0)
    dq = jnp.concatenate([dq_ref[c] for c in range(chunks)], axis=1)
    ones = jnp.ones((8, x.shape[0]), bf16)

    @pl.when(pl.program_id(0) == 0)
    def _():
        acc[...] = jnp.zeros_like(acc)
        sum_sc[...] = jnp.zeros_like(sum_sc)

    acc[0:lanes, :] += dot_tn(dkv, x)
    acc[lanes : lanes + group, :] += dot_nn(dq, x)
    sum_sc[:, 0:lanes] += dot_nn(ones, dkv)
    sum_sc[:, lanes : lanes + group] += dot_nt(ones, dq)

    @pl.when(pl.program_id(0) == pl.num_programs(0) - 1)
    def _():
        lane = lax.broadcasted_iota(jnp.int32, (full, width), 0)
        spot = lax.broadcasted_iota(jnp.int32, (full, width), 1) % group
        pick_q = lane - lanes == spot
        pick_v = (lane < lanes) & (lane % PAIR >= BLOCK) & (lane // PAIR * BLOCK + lane % BLOCK == spot)
        sums = sum_sc[...].astype(bf16)
        row = lax.broadcasted_iota(jnp.int32, (8, width), 0)
        of_q = dot_nn(sums, pick_q.astype(f32).astype(bf16))
        of_v = dot_nn(sums, pick_v.astype(f32).astype(bf16))
        acc[lanes + group : lanes + group + 8, :] = jnp.where(row == 0, of_q, of_v)
        grad = jnp.transpose(acc[...], (1, 0))
        if direct:
            blocks, own, _ = out_ref.shape
            grad = grad.reshape(blocks, own, full)
            for b in range(blocks):
                out_ref[b] = grad[b].astype(bf16)
        else:
            out_ref[...] = grad.astype(bf16)


def projection_gradients(x, dq, dkv, own, devices):
    chunks, group, rows = dq.shape
    width = x[0].shape[1]
    lanes = dkv.shape[2]
    full = lanes + round_up(group, PAIR)
    direct = own % 8 == 0
    tile = 256
    shape = (devices, own, full) if direct else (width, full)
    out = pl.pallas_call(
        functools.partial(weights_kernel, chunks, direct),
        grid=(rows // tile,),
        out_shape=jax.ShapeDtypeStruct(shape, bf16),
        in_specs=[pl.BlockSpec((tile, width), lambda i: (i, 0)) for _ in range(chunks)]
        + [
            pl.BlockSpec((chunks, group, tile), lambda i: (0, 0, i)),
            pl.BlockSpec((chunks, tile, lanes), lambda i: (0, i, 0)),
        ],
        out_specs=pl.BlockSpec(shape, lambda i: (0,) * len(shape), pipeline_mode=pl.Buffered(1)),
        scratch_shapes=[pltpu.VMEM((full, width), f32), pltpu.VMEM((8, full), f32)],
        compiler_params=pltpu.CompilerParams(vmem_limit_bytes=VMEM_BYTES),
        cost_estimate=pl.CostEstimate(flops=4_000_000_000, bytes_accessed=12_000_000, transcendentals=0),
        name="projection_gradients",
    )(*x, dq, dkv)
    if not direct:
        out = jnp.pad(out.reshape(devices, own, full), ((0, 0), (0, round_up(own, 8) - own), (0, 0)))
    return out


def unpack_kernel(own, got_ref, q_ref, k_ref, v_ref, sums_ref, tot):
    dp_n, seq_n, ffn_n, per, full = got_ref.shape
    width = q_ref.shape[1]
    heads = width // HEAD_DIM // seq_n
    for s in range(seq_n):
        total = jnp.zeros((per, full), f32)
        for d in range(dp_n):
            for f in range(ffn_n):
                total = total + got_ref[d, s, f].astype(f32)
        tot[s] = total
        sums_ref[s] = total[:, full - PAIR :]
    for w in range(width // PAIR):
        spots = [((2 * w + i) // heads, (2 * w + i) % heads) for i in range(2)]
        cols = slice(w * PAIR, (w + 1) * PAIR)
        for ref, where in (
            (k_ref, lambda h: 2 * h),
            (v_ref, lambda h: 2 * h + 1),
            (q_ref, lambda h: 2 * heads + h),
        ):
            both = [half_columns(tot.at[g], where(h), i) for i, (g, h) in enumerate(spots)]
            ref[:, cols] = two_halves(*both)[0:own]


def unpacked_gradients(got, own, width):
    dp_n, seq_n, ffn_n, per, full = got.shape
    whole = lambda: pl.BlockSpec(memory_space=pltpu.VMEM)
    return pl.pallas_call(
        functools.partial(unpack_kernel, own),
        out_shape=(jax.ShapeDtypeStruct((own, width), f32),) * 3 + (jax.ShapeDtypeStruct((seq_n, per, PAIR), f32),),
        in_specs=[whole()],
        out_specs=tuple(whole() for _ in range(4)),
        scratch_shapes=[pltpu.VMEM((seq_n, per, full), f32)],
        compiler_params=pltpu.CompilerParams(vmem_limit_bytes=VMEM_BYTES),
        cost_estimate=pl.CostEstimate(flops=40_000_000_000, bytes_accessed=3_000_000, transcendentals=0),
        name="unpacked_gradients",
    )(got)


NORM_EPS = 1e-12


def transposed(value):
    return jnp.transpose(value.astype(f32), (1, 0)).astype(bf16)


def unit_rows(value):
    center = value - jnp.mean(value, axis=-1, keepdims=True)
    scale = lax.rsqrt(jnp.mean(center * center, axis=-1, keepdims=True) + NORM_EPS)
    return center * scale, scale


def unit_rows_back(grad, unit, scale):
    return scale * (
        grad - jnp.mean(grad, axis=-1, keepdims=True) - unit * jnp.mean(grad * unit, axis=-1, keepdims=True)
    )


def rows_kernel(parts, blocks, up_rows, own, me_ref, *refs):
    ctx_refs = refs[:parts]
    (x_ref, cot_ref, rest_ref, wo_ref, vec_ref, bup_ref, out_ref, resid_ref, hid_ref, pre_ref, nlt_ref, gft_ref,
     gb_ref) = refs[parts : parts + 13]
    do_refs = refs[parts + 13 : 2 * parts + 13]
    sums_ref, gbup_ref, slope_sc, wo_sc, wide_sc = refs[2 * parts + 13 :]
    group = ctx_refs[0].shape[0]
    width = x_ref.shape[1]

    def up(f):
        return rest_ref[:, f, 0:up_rows, :].reshape(width, rest_ref.shape[3])

    def down(f):
        return rest_ref[:, f, up_rows : 2 * up_rows, :].reshape(width, rest_ref.shape[3])

    def own_rows(k):
        return pl.ds(pl.multiple_of((me_ref[0] ^ k) * group, group), group)

    @pl.when(pl.program_id(0) == 0)
    def _():
        sums_ref[...] = jnp.zeros_like(sums_ref)
        gbup_ref[...] = jnp.zeros_like(gbup_ref)
        if own:
            for o in range(rest_ref.shape[0]):
                for f in range(blocks):
                    to = (o * blocks + f) * own
                    wide_sc[to : to + own, :] = rest_ref[o, f, 2 * up_rows : 2 * up_rows + own, :].astype(f32)
            wo_sc[...] = wide_sc[...].astype(bf16)
        else:
            wo_sc[...] = wo_ref[...]

    def bias_up(f):
        return bup_ref[f : f + 1, :]

    ctx = jnp.concatenate([r[...] for r in ctx_refs], axis=0)
    w_o = jnp.concatenate([wo_sc[own_rows(k), :] for k in range(parts)], axis=0)
    resid_one = x_ref[...].astype(f32) + (dot_tn(ctx, w_o) + vec_ref[0:1, :])
    unit_one, scale_one = unit_rows(resid_one)
    normed_one = unit_one * vec_ref[2:3, :] + vec_ref[3:4, :]
    low = normed_one.astype(bf16)
    nlt_ref[...] = transposed(normed_one)
    total = normed_one + vec_ref[1:2, :]
    pre = dot_nn(low, up(0)) + bias_up(0)
    for f in range(blocks):
        later = dot_nn(low, up(f + 1)) + bias_up(f + 1) if f + 1 < blocks else None
        phi = 0.5 + 0.5 * lax.erf(pre * (0.5 ** 0.5))
        slope_sc[f] = phi + pre * (jnp.exp(-0.5 * pre * pre) * 0.3989422804014327)
        hid = (pre * phi).astype(bf16)
        hid_ref[f] = hid
        total = total + dot_nt(hid, down(f))
        pre = later
    unit_two, scale_two = unit_rows(total)
    out_ref[...] = (unit_two * vec_ref[4:5, :] + vec_ref[5:6, :]).astype(bf16)
    cot = cot_ref[...].astype(f32)
    grad_two = unit_rows_back(cot * vec_ref[4:5, :], unit_two, scale_two)
    grad_ffn = grad_two.astype(bf16)
    gft_ref[...] = transposed(grad_two)
    grad_normed = grad_two
    back = dot_nn(grad_ffn, down(0))
    for f in range(blocks):
        later = dot_nn(grad_ffn, down(f + 1)) if f + 1 < blocks else None
        grad_pre = (back * slope_sc[f]).astype(bf16)
        pre_ref[f] = grad_pre
        gbup_ref[f : f + 1, :] += jnp.sum(grad_pre.astype(f32), axis=0, keepdims=True)
        grad_normed = grad_normed + dot_nt(grad_pre, up(f))
        back = later
    resid = unit_rows_back(grad_normed * vec_ref[2:3, :], unit_one, scale_one)
    resid_ref[...] = resid
    branch = resid.astype(bf16)
    gb_ref[...] = branch
    do = dot_nt(w_o, branch).astype(bf16)
    for k in range(parts):
        do_refs[k][...] = do[k * group : (k + 1) * group]
    for row, value in enumerate(
        (branch.astype(f32), grad_ffn.astype(f32), grad_normed * unit_one, grad_normed, cot * unit_two, cot)
    ):
        sums_ref[row : row + 1, :] += jnp.sum(value, axis=0, keepdims=True)


def rows_chain(me, ctx_parts, x, cot, rest, up_rows, own, w_o, vecs, bias_up):
    parts = len(ctx_parts)
    group, rows = ctx_parts[0].shape
    width = x.shape[1]
    outer, blocks, per, hidden = rest.shape
    tile = 256
    once = lambda shape: pl.BlockSpec(shape, lambda i: (0,) * len(shape), pipeline_mode=pl.Buffered(1))
    tall = pl.BlockSpec((tile, width), lambda i: (i, 0))
    wide = pl.BlockSpec((width, tile), lambda i: (0, i))
    cube = pl.BlockSpec((blocks, tile, hidden), lambda i: (0, i, 0))
    return pl.pallas_call(
        functools.partial(rows_kernel, parts, blocks, up_rows, own),
        grid=(rows // tile,),
        out_shape=(
            jax.ShapeDtypeStruct((rows, width), bf16),
            jax.ShapeDtypeStruct((rows, width), f32),
            jax.ShapeDtypeStruct((blocks, rows, hidden), bf16),
            jax.ShapeDtypeStruct((blocks, rows, hidden), bf16),
            jax.ShapeDtypeStruct((width, rows), bf16),
            jax.ShapeDtypeStruct((width, rows), bf16),
            jax.ShapeDtypeStruct((rows, width), bf16),
        )
        + (jax.ShapeDtypeStruct((group, rows), bf16),) * parts
        + (jax.ShapeDtypeStruct((8, width), f32), jax.ShapeDtypeStruct((8, hidden), f32)),
        in_specs=[pl.BlockSpec(memory_space=pltpu.SMEM)]
        + [pl.BlockSpec((group, tile), lambda i: (0, i))] * parts
        + [tall, tall, once(rest.shape), once(w_o.shape), once(vecs.shape), once(bias_up.shape)],
        out_specs=(
            tall, tall, cube, cube, wide, wide, tall,
        )
        + (pl.BlockSpec((group, tile), lambda i: (0, i)),) * parts
        + (pl.BlockSpec((8, width), lambda i: (0, 0)), pl.BlockSpec((8, hidden), lambda i: (0, 0))),
        scratch_shapes=[
            pltpu.VMEM((blocks, tile, hidden), f32),
            pltpu.VMEM((width, width), bf16),
            pltpu.VMEM((width, width), f32),
        ],
        compiler_params=pltpu.CompilerParams(vmem_limit_bytes=VMEM_BYTES),
        cost_estimate=pl.CostEstimate(flops=22_000_000_000, bytes_accessed=40_000_000, transcendentals=6_000_000),
        name="rows_chain",
    )(me, *ctx_parts, x, cot, rest, w_o, vecs, bias_up)


def outer_kernel(parts, up_rows, own, apart, me_ref, *refs):
    ctx_refs = refs[:parts]
    nlt_ref, gft_ref, gb_ref, pre_ref, hid_ref, sums_ref, gbup_ref, out_ref = refs[parts : parts + 8]
    wo_sc = refs[-1]
    slabs, hidden = out_ref.shape[0], out_ref.shape[3]
    group = ctx_refs[0].shape[0]
    f = pl.program_id(0)
    up = dot_nn(nlt_ref[...], pre_ref[0]).astype(bf16).reshape(slabs, up_rows, hidden)
    if apart:
        refs[parts + 8][:, 0, :, :] = up[:, 0:apart]
    out_ref[:, 0, 0 : up_rows - apart, :] = up[:, apart:]
    at = up_rows - apart
    down = dot_nn(gft_ref[...], hid_ref[0]).astype(bf16)
    out_ref[:, 0, at : at + up_rows, :] = down.reshape(slabs, up_rows, hidden)
    at += up_rows
    if not own:
        return

    @pl.when(f == 0)
    def _():
        for k in range(parts):
            wo_sc[k] = dot_nn(ctx_refs[k][...], gb_ref[...])

    share = slabs // parts
    stride = group // share
    for k in range(parts):
        for j in range(share):
            rows = pl.ds(pl.multiple_of(j * stride + f * own, 8), own)
            out_ref[(me_ref[0] ^ k) * share + j, 0, at : at + own, :] = wo_sc[k, rows, :].astype(bf16)
    small = jnp.concatenate([gbup_ref[pl.ds(f, 1), :], sums_ref[0:7, :]], axis=0).astype(bf16)
    for o in range(slabs):
        out_ref[o, 0, at + own :, :] = small


def outer_products(me, ctx_parts, nlt, gft, gb, pre, hid, sums, gbup, slabs, up_rows, own, apart):
    blocks, rows, hidden = pre.shape
    parts = len(ctx_parts)
    group = ctx_parts[0].shape[0]
    per = 2 * up_rows - apart + (own + 8 if own else 0)
    sizes = (per, apart) if apart else (per,)
    once = lambda shape: pl.BlockSpec(shape, lambda i: (0,) * len(shape), pipeline_mode=pl.Buffered(1))
    return pl.pallas_call(
        functools.partial(outer_kernel, parts, up_rows, own, apart),
        grid=(blocks,),
        out_shape=tuple(jax.ShapeDtypeStruct((slabs, blocks, r, hidden), bf16) for r in sizes),
        in_specs=[pl.BlockSpec(memory_space=pltpu.SMEM)]
        + [once(c.shape) for c in ctx_parts]
        + [
            once(nlt.shape),
            once(gft.shape),
            once(gb.shape),
            pl.BlockSpec((1, rows, hidden), lambda i: (i, 0, 0)),
            pl.BlockSpec((1, rows, hidden), lambda i: (i, 0, 0)),
            once(sums.shape),
            once(gbup.shape),
        ],
        out_specs=tuple(pl.BlockSpec((slabs, 1, r, hidden), lambda i: (0, i, 0, 0)) for r in sizes),
        scratch_shapes=[pltpu.VMEM((parts, group, gb.shape[1]), f32)],
        compiler_params=pltpu.CompilerParams(vmem_limit_bytes=VMEM_BYTES),
        cost_estimate=pl.CostEstimate(flops=11_000_000_000, bytes_accessed=28_000_000, transcendentals=0),
        name="outer_products",
    )(me, *ctx_parts, nlt, gft, gb, pre, hid, sums, gbup)


def finish_kernel(up_rows, own, total_ref, up_ref, down_ref, wo_ref, small_ref):
    rest = total_ref[...].astype(f32)
    up_ref[...] = rest[0:up_rows]
    down_ref[...] = rest[up_rows : 2 * up_rows]
    at = 2 * up_rows
    wo_ref[...] = rest[at : at + own]
    small_ref[...] = rest[at + own : at + own + 8]


def finished(total, up_rows, own):
    hidden = total.shape[1]
    whole = lambda: pl.BlockSpec(memory_space=pltpu.VMEM)
    return pl.pallas_call(
        functools.partial(finish_kernel, up_rows, own),
        out_shape=tuple(jax.ShapeDtypeStruct((r, hidden), f32) for r in (up_rows, up_rows, own, 8)),
        in_specs=[whole()],
        out_specs=tuple(whole() for _ in range(4)),
        cost_estimate=pl.CostEstimate(flops=2_000_000_000, bytes_accessed=2_000_000, transcendentals=0),
        name="finished",
    )(total)


def total_kernel(pieces, base_ref, *refs):
    total = base_ref[...]
    for ref in refs[:pieces]:
        total = total + ref[...].astype(f32)
    refs[-1][...] = total


def token_total(base, whole_pieces, part, first, done=None):
    rows, width = base.shape
    tile = 128
    skip = first // tile
    here = pl.BlockSpec((tile, width), lambda i: (i + skip, 0))
    count = len(whole_pieces) + 1
    args = [base, *whole_pieces, part] + ([] if done is None else [done])
    return pl.pallas_call(
        functools.partial(total_kernel, count),
        grid=(part.shape[0] // tile,),
        out_shape=jax.ShapeDtypeStruct(base.shape, f32),
        in_specs=[here] * count
        + [pl.BlockSpec((tile, width), lambda i: (i, 0))]
        + ([] if done is None else [pl.BlockSpec(memory_space=pl.ANY)]),
        out_specs=here,
        input_output_aliases={} if done is None else {count + 1: 0},
        compiler_params=pltpu.CompilerParams(vmem_limit_bytes=VMEM_BYTES),
        cost_estimate=pl.CostEstimate(flops=TOTAL_FLOPS, bytes_accessed=5_000_000, transcendentals=0),
        name="token_total",
    )(*args)


TOTAL_FLOPS = 1_000_000_000
ALL = ("dp", "seq", "ffn")


def flip_send(array, axis, bits):
    count = lax.axis_size(axis)
    return lax.ppermute(array, axis, [(i, i ^ bits) for i in range(count)])


def shards(
    tokens, w_query, w_key, w_value, w_output, b_query, b_value, b_output, w_up, b_up, w_down, b_down,
    gain_attn, shift_attn, gain_ffn, shift_ffn, segment_ids, random_blocks, global_blocks, cotangent,
):
    seq_n, dp_n, ffn_n = lax.axis_size("seq"), lax.axis_size("dp"), lax.axis_size("ffn")
    outer, devices = dp_n * seq_n, dp_n * seq_n * ffn_n
    me = lax.axis_index("seq")
    here = (lax.axis_index("dp") * seq_n + me) * ffn_n + lax.axis_index("ffn")
    own, width = w_query.shape
    own_pad = round_up(own, 8)
    group = width // seq_n
    heads = group // HEAD_DIM
    features = tokens[0]
    rows = features.shape[0]
    order = jnp.stack([me ^ k for k in range(seq_n)])
    me_ref = me.astype(jnp.int32)[None]

    near = [features] + [None] * (seq_n - 1)
    for k in sorted(range(1, seq_n), key=lambda k: (k & (k - 1), -k)):
        bit = k & -k
        near[k] = flip_send(features if bit == k else near[k ^ bit], "seq", bit)

    vec = jnp.stack([b_output, b_down, gain_attn, shift_attn, gain_ffn, shift_ffn, b_query, b_value], axis=1)
    up_rows = w_up.shape[0]
    share_up = lax.dynamic_slice(b_up, (here // ffn_n * up_rows,), (up_rows,)).reshape(ffn_n, own).T
    more = jnp.pad(share_up, ((0, 0), (HEAD_DIM + 8, PAIR - HEAD_DIM - 8 - ffn_n)))
    vec = jnp.pad(vec, ((0, 0), (HEAD_DIM, PAIR - HEAD_DIM - 8)))
    seg = segment_ids[0].reshape(seq_n, rows)
    rand = random_blocks.reshape(-1)
    pack, rest = packed_weights(
        w_query, w_key, w_value, w_output, w_up, w_down, vec, more, dp_n, seq_n, ffn_n
    )
    lanes = pack.shape[4]
    pack, seg, rand = lax.optimization_barrier((pack, seg, rand))
    pack = lax.all_to_all(
        pack.reshape(devices, own_pad, lanes), ALL, split_axis=0, concat_axis=0, tiled=True
    )
    rest = lax.all_gather(rest, ALL, axis=0, tiled=False)
    w_own = pack[:, :own].reshape(width, lanes)
    share = devices // seq_n
    vecs = w_own[:, lanes - HEAD_DIM : lanes - HEAD_DIM + 8].astype(f32).T
    biases = lax.dynamic_slice(vecs, (6, me * group), (2, group))
    bias_up = w_own[:, lanes - HEAD_DIM + 8 : lanes - HEAD_DIM + 8 + ffn_n].reshape(outer, ffn_n, own, ffn_n)
    bias_up = bias_up.transpose(1, 0, 3, 2).reshape(ffn_n, width).astype(f32)
    by_head = biases[1].reshape(heads, 1, HEAD_DIM)
    b_kv = jnp.concatenate([jnp.zeros_like(by_head), by_head], axis=1).reshape(1, heads * PAIR)

    far = seq_n // 2
    ctx_far, (lse_far, lseg, glob_ctx, k_all, v_all, q_all, mask_all) = attention_forward(
        me_ref, rand, global_blocks, near, seg, w_own, b_kv, biases[0][:, None]
    )
    ctx_parts = [None] * far + [flip_send(ctx_far[k - far], "seq", k) for k in range(far, seq_n)]
    ctx_near, lse_near = attention_near(
        me_ref, rand, global_blocks, k_all, v_all, q_all, mask_all, glob_ctx, seq_n
    )
    ctx_parts[far:], ctx_parts[0] = lax.optimization_barrier((ctx_parts[far:], ctx_near[0]))
    for k in range(1, far):
        ctx_parts[k] = flip_send(ctx_near[k], "seq", k)

    at = 2 * up_rows
    rest = rest.reshape(outer, ffn_n, rest.shape[1], width)
    w_o = rest[:, :, at : at + own].reshape(width, width)
    direct = up_rows % 16 == 0 and own % 8 == 0 and outer % seq_n == 0 and (outer // seq_n) * ffn_n * own == group
    if not direct:
        rest = rest[:, :, :at].reshape(outer, ffn_n, 2, up_rows, width).transpose(1, 2, 0, 3, 4)
        rest = rest.reshape(1, ffn_n, 2 * outer * up_rows, width)
    slabs, slab_rows = (outer, up_rows) if direct else (1, outer * up_rows)

    got = rows_chain(
        me_ref, ctx_parts, features, cotangent[0], rest, slab_rows, own if direct else 0,
        vecs if direct else w_o, vecs, bias_up,
    )
    out, grad_resid_one, hidden, grad_pre, normed_t, grad_ffn_t, grad_branch = got[:7]
    grad_ctx, (sums, grad_bias_up) = got[7 : 7 + seq_n], got[7 + seq_n :]
    do = [grad_ctx[0]] + [flip_send(grad_ctx[k], "seq", k) for k in range(1, seq_n)]

    payload = outer_products(
        me_ref, ctx_parts, normed_t, grad_ffn_t, grad_branch, grad_pre, hidden, sums, grad_bias_up, slabs, slab_rows,
        own if direct else 0, APART if direct else 0,
    )
    payload, apart = payload if direct and APART else (payload[0], None)
    if not direct:
        grad_out = dot_nn(jnp.concatenate(ctx_parts, axis=0), grad_branch).astype(bf16)
        grad_out = grad_out.reshape(seq_n, group, width)[order].reshape(outer, ffn_n, own, width)
        top = jnp.broadcast_to(grad_bias_up[None, :ffn_n, None], (outer, ffn_n, 1, width))
        small = jnp.concatenate([top, jnp.broadcast_to(sums[None, None, :7], (outer, ffn_n, 7, width))], axis=2)
        small = small.astype(bf16)
        payload = payload.reshape(ffn_n, 2, outer, up_rows, width).transpose(2, 0, 1, 3, 4)
        payload = jnp.concatenate([payload.reshape(outer, ffn_n, at, width), grad_out, small], axis=2)
        payload = jnp.pad(payload, ((0, 0), (0, 0), (0, -payload.shape[2] % 32), (0, 0)))
    payload, apart, do = lax.optimization_barrier((payload, apart, do))
    total = lax.psum_scatter(payload.reshape(-1, width), ("dp", "seq"), scatter_dimension=0, tiled=True)
    if apart is not None:
        apart = lax.all_to_all(
            apart.reshape(devices, APART, width), ALL, split_axis=0, concat_axis=0, tiled=True
        )

    got = attention_backward(
        me_ref, rand, global_blocks, do, k_all, v_all, q_all, mask_all, seg, lse_near, lse_far, lseg, w_own,
        grad_resid_one,
    )
    dq, dkv, grad_features = got[:3]
    part = [None] + list(got[3:])
    bit = 1
    while bit < seq_n:
        for k in range(seq_n):
            if k & -k == bit and k != bit:
                came = flip_send(part[k], "seq", bit).astype(f32)
                part[k ^ bit] = (part[k ^ bit].astype(f32) + came).astype(bf16)
        bit *= 2
    grad_w = projection_gradients(near, dq, dkv, own, devices)
    grad_w, part = lax.optimization_barrier((grad_w, part[1:]))
    grad_w, apart = lax.optimization_barrier((grad_w, apart))
    part = [None] + part
    bit = seq_n // 2
    staged = total
    total = lax.psum_scatter(total, "ffn", scatter_dimension=0, tiled=True)
    half = rows // 2
    first, second = part[bit][:half], part[bit][half:]
    first, second = flip_send(first, "seq", bit), flip_send(second, "seq", bit)
    bit //= 2
    others = []
    while bit:
        others.append(flip_send(part[bit], "seq", bit))
        bit //= 2
    first = lax.optimization_barrier((first, staged))[0]
    base = grad_features
    grad_features = token_total(base, others, first, 0)
    grad_features = token_total(base, others, second, half, grad_features)
    grad_w = lax.all_to_all(grad_w, ALL, split_axis=0, concat_axis=0, tiled=True)
    if direct:
        out_up, out_down, out_output, notes = finished(total, up_rows, own)
    else:
        total = total.astype(f32)
        out_up, out_down, out_output = total[:up_rows], total[up_rows:at], total[at : at + own]
        notes = total[at + own : at + own + 8]
    out_bias_up = notes[0]
    out_vecs = lax.dynamic_slice(notes, (1, here * own), (6, own))
    out_query, out_key, out_value, col_sums = unpacked_gradients(
        grad_w.reshape(dp_n, seq_n, ffn_n, own_pad, lanes), own, width
    )
    col = lax.dynamic_index_in_dim(col_sums, here // share, keepdims=False)[:own, HEAD_DIM : HEAD_DIM + 2]
    out_b = [col[:, 0], col[:, 1]]
    return (
        out[None],
        grad_features[None],
        out_query,
        out_key,
        out_value,
        out_output,
        out_b[0],
        out_b[1],
        out_vecs[0],
        out_up,
        out_bias_up,
        out_down,
        out_vecs[1],
        out_vecs[2],
        out_vecs[3],
        out_vecs[4],
        out_vecs[5],
    )


def solution(mesh):
    return jax.shard_map(
        shards,
        mesh=mesh,
        in_specs=(
            P(("dp", "ffn"), "seq", None),
            P(("dp", "seq", "ffn"), None),
            P(("dp", "seq", "ffn"), None),
            P(("dp", "seq", "ffn"), None),
            P(("dp", "seq", "ffn"), None),
            P(("dp", "seq", "ffn")),
            P(("dp", "seq", "ffn")),
            P(("dp", "seq", "ffn")),
            P(("dp", "seq"), "ffn"),
            P("ffn"),
            P(("dp", "seq"), "ffn"),
            P(("dp", "seq", "ffn")),
            P(("dp", "seq", "ffn")),
            P(("dp", "seq", "ffn")),
            P(("dp", "seq", "ffn")),
            P(("dp", "seq", "ffn")),
            P(("dp", "ffn"), None),
            P(("dp", "ffn"), "seq", None, None),
            P(("dp", "ffn"), None),
            P(("dp", "ffn"), "seq", None),
        ),
        out_specs=(
            P(("dp", "ffn"), "seq", None),
            P(("dp", "ffn"), "seq", None),
            P(("dp", "seq", "ffn"), None),
            P(("dp", "seq", "ffn"), None),
            P(("dp", "seq", "ffn"), None),
            P(("dp", "seq", "ffn"), None),
            P(("dp", "seq", "ffn")),
            P(("dp", "seq", "ffn")),
            P(("dp", "seq", "ffn")),
            P(("dp", "seq"), "ffn"),
            P("ffn"),
            P(("dp", "seq"), "ffn"),
            P(("dp", "seq", "ffn")),
            P(("dp", "seq", "ffn")),
            P(("dp", "seq", "ffn")),
            P(("dp", "seq", "ffn")),
            P(("dp", "seq", "ffn")),
        ),
        check_vma=False,
    )
```

```python
import functools
import jax
import jax.numpy as jnp
from jax import lax
from jax.experimental import pallas as pl
from jax.sharding import PartitionSpec as P
from jax.experimental.pallas import tpu as pltpu

HEAD_DIM = 64
BLOCK = 64
PAIR = 2 * BLOCK
MASKED = -1e30
bf16 = jnp.bfloat16
f32 = jnp.float32


def dot_nn(a, b):
    return lax.dot_general(a, b, (((1,), (0,)), ((), ())), preferred_element_type=f32)


def dot_nt(a, b):
    return lax.dot_general(a, b, (((1,), (1,)), ((), ())), preferred_element_type=f32)


def dot_tn(a, b):
    return lax.dot_general(a, b, (((0,), (0,)), ((), ())), preferred_element_type=f32)


def slots(rand_ref, glob_ref, flip, head, pair, nblocks):
    first = (2 * pair) ^ flip

    def row(block):
        return pl.multiple_of(block * BLOCK, BLOCK)

    def near(block):
        bad = (block < 0) | (block >= nblocks) | (block == glob_ref[0, 0]) | (block == glob_ref[0, 1])
        return row(jnp.where(bad, nblocks, block ^ flip))

    def drawn(block):
        at = (head * nblocks + block) * 3
        return [row(rand_ref[at + j] ^ flip) for j in range(3)]

    shared = [near(first), near(first + 1)] + [row(glob_ref[0, j] ^ flip) for j in range(2)]
    return shared, [near(first - 1)] + drawn(first), [near(first + 2)] + drawn(first + 1)


def stack_rows(ref, offsets, lanes):
    return jnp.concatenate([ref[pl.ds(o, BLOCK), lanes] for o in offsets], axis=0)


def lane_halves(width, dtype):
    lane = lax.broadcasted_iota(jnp.int32, (1, width), 1) % PAIR
    first = (lane < BLOCK).astype(dtype)
    second = (lane >= BLOCK).astype(dtype)
    return first, second


UNROLL = 4
BACK_UNROLL = 4
APART = 0
VMEM_BYTES = 62 << 20


def head_lanes(h):
    return slice(h * PAIR, (h + 1) * PAIR)


def query_columns(q_ref, mask_ref, h, at):
    return jnp.concatenate([q_ref[h * BLOCK : (h + 1) * BLOCK, pl.ds(at, PAIR)], mask_ref[:, pl.ds(at, PAIR)]], axis=0)


def global_queries(q_ref, mask_ref, h, gl):
    return jnp.concatenate(
        [
            global_columns(q_ref, slice(h * BLOCK, (h + 1) * BLOCK), gl),
            global_columns(mask_ref, slice(0, BLOCK), gl),
        ],
        axis=0,
    ).astype(bf16)


def placed(me_ref, glob_ref, nblocks, chunks):
    flip = me_ref[0] * (nblocks // chunks)
    return flip, [glob_ref[0, j] ^ flip for j in range(2)]


def global_columns(src_ref, rows, gl):
    lane = lax.broadcasted_iota(jnp.int32, (1, PAIR), 1)
    parts = []
    for g in range(2):
        block = gl[g]
        at = pl.multiple_of((block // 2) * PAIR, PAIR)
        both = src_ref[rows, pl.ds(at, PAIR)].astype(f32)
        moved = pltpu.roll(both, BLOCK, 1)
        parts.append(jnp.where(block % 2 == g, both, moved))
    return jnp.where(lane < BLOCK, parts[0], parts[1])


def put_global_columns(dst_ref, rows, gl, value, per_chunk, low, high):
    lane = lax.broadcasted_iota(jnp.int32, (1, PAIR), 1)
    moved = pltpu.roll(value, BLOCK, 1)
    for g in range(2):
        pair = gl[g] // 2
        half = gl[g] % 2
        chunk = pair // per_chunk

        @pl.when((chunk >= low) & (chunk < high))
        def _():
            at = pl.multiple_of((pair % per_chunk) * PAIR, PAIR)
            src = jnp.where(half == g, value, moved)
            old = dst_ref[chunk - low, rows, pl.ds(at, PAIR)].astype(f32)
            new = jnp.where((lane >= BLOCK) == (half == 1), src, old)
            dst_ref[chunk - low, rows, pl.ds(at, PAIR)] = new.astype(dst_ref.dtype)


def project_rows(x, seg, w_ref, wq, bkv_ref, bq_ref, k_ref, v_ref, q_ref, mask_ref, at):
    n = x.shape[0]
    lanes = v_ref.shape[1]
    y = dot_nn(x, w_ref[:, 0:lanes]) + bkv_ref[...]
    spot = lax.broadcasted_iota(jnp.int32, (PAIR, n), 0) - BLOCK
    mark = jnp.transpose((spot == seg).astype(f32), (1, 0))
    lane = lax.broadcasted_iota(jnp.int32, (1, PAIR), 1)
    rows = pl.ds(at, n)
    v_ref[rows, :] = y.astype(bf16)
    for h in range(lanes // PAIR):
        k_ref[rows, head_lanes(h)] = jnp.where(lane < BLOCK, y[:, head_lanes(h)], mark).astype(bf16)
    z = (dot_nt(wq, x) + bq_ref[...]).astype(bf16)
    q_ref[:, rows] = (z.astype(f32) * HEAD_DIM ** -0.5).astype(bf16)
    row = lax.broadcasted_iota(jnp.int32, (BLOCK, n), 0)
    mask_ref[:, rows] = jnp.where((row <= 16) & (row != seg), MASKED, 0.0).astype(bf16)


def query_weights(w_ref, heads):
    at = heads * PAIR
    cols = w_ref[:, at : at + 2 * PAIR].astype(f32)
    return jnp.transpose(cols, (1, 0))[0 : heads * HEAD_DIM].astype(bf16)


def sparse_forward(heads, low, high, per_chunk, rand_ref, glob_ref, flip, k_ref, kv_ref, q_ref, mask_ref, out_ref, lse_ref):
    nblocks = (k_ref.shape[0] - BLOCK) // BLOCK
    first, second = lane_halves(PAIR, bf16)
    lane = lax.broadcasted_iota(jnp.int32, (1, PAIR), 1)

    def one_pair(spot):
        chunk = spot // per_chunk
        local = pl.multiple_of((spot % per_chunk) * PAIR, PAIR)
        pair = low * per_chunk + spot
        at = pl.multiple_of(pair * PAIR, PAIR)
        for h in range(heads):
            shared, mine, other = slots(rand_ref, glob_ref, flip, h, pair, nblocks)
            kl = head_lanes(h)
            q = query_columns(q_ref, mask_ref, h, at)
            s_sh = dot_nn(stack_rows(k_ref, shared, kl), q)
            k_pr = jnp.concatenate([stack_rows(k_ref, mine, kl), stack_rows(k_ref, other, kl)], axis=1)
            s_pr = dot_nn(k_pr, jnp.concatenate([q * first, q * second], axis=0))
            peak = jnp.maximum(jnp.max(s_sh, axis=0, keepdims=True), jnp.max(s_pr, axis=0, keepdims=True))
            e_sh = jnp.exp(s_sh - peak)
            e_pr = jnp.exp(s_pr - peak)
            total = jnp.sum(e_sh, axis=0, keepdims=True) + jnp.sum(e_pr, axis=0, keepdims=True)
            inv = 1.0 / total
            p_sh = (e_sh * inv).astype(bf16)
            p_pr = (e_pr * inv).astype(bf16)
            v_pr = jnp.concatenate([stack_rows(kv_ref, mine, kl), stack_rows(kv_ref, other, kl)], axis=1)
            o_sh = dot_tn(stack_rows(kv_ref, shared, kl), p_sh)
            o_pr = dot_tn(v_pr, p_pr)
            ctx = o_sh[BLOCK:PAIR] + jnp.where(lane < BLOCK, o_pr[BLOCK:PAIR], o_pr[PAIR + BLOCK : 2 * PAIR])
            out_ref[chunk, h * BLOCK : (h + 1) * BLOCK, pl.ds(local, PAIR)] = ctx.astype(bf16)
            lse_ref[h, pl.ds(spot, 1), :] = peak + jnp.log(total)

    @pl.loop(0, (high - low) * per_chunk // UNROLL)
    def _(some):
        for i in range(UNROLL):
            one_pair(UNROLL * some + i)


def forward_kernel(heads, chunks, me_ref, rand_ref, glob_ref, *refs):
    x_refs = refs[0:chunks]
    seg_ref, w_ref, bkv_ref, bq_ref = refs[chunks : chunks + 4]
    far = chunks // 2
    out_refs = refs[chunks + 4 : chunks + 4 + far]
    lse_ref, lseg_ref, glob_ctx_ref = refs[chunks + 4 + far : chunks + 7 + far]
    saved_refs = refs[chunks + 7 + far : chunks + 11 + far]
    s_sc, out_ref, seg_sc, k_sc, v_sc, q_sc, mask_sc, sems = refs[chunks + 11 + far :]
    rows = x_refs[0].shape[0]
    length = rows * chunks
    per_chunk = length // PAIR // chunks
    flip, gl = placed(me_ref, glob_ref, length // BLOCK, chunks)
    tile = 256
    wq = query_weights(w_ref, heads)
    for c in range(chunks):
        seg_sc[c : c + 1, :] = seg_ref[pl.ds(me_ref[0] ^ c, 1), :]
    for c in range(chunks):

        @pl.loop(0, rows // tile)
        def _(t):
            at = pl.multiple_of(t * tile, tile)
            project_rows(
                x_refs[c][pl.ds(at, tile), :], seg_sc[c : c + 1, pl.ds(at, tile)], w_ref, wq, bkv_ref, bq_ref,
                k_sc, v_sc, q_sc, mask_sc, pl.multiple_of(c * rows + t * tile, tile),
            )

    null_lane = lax.broadcasted_iota(jnp.int32, (BLOCK, heads * PAIR), 1) % PAIR
    k_sc[pl.ds(length, BLOCK), :] = (null_lane == BLOCK + 16).astype(f32).astype(bf16)
    v_sc[pl.ds(length, BLOCK), :] = jnp.zeros((BLOCK, heads * PAIR), bf16)
    saves = [
        pltpu.make_async_copy(src, dst, sems.at[i])
        for i, (src, dst) in enumerate(zip((k_sc, v_sc, q_sc, mask_sc), saved_refs))
    ]
    for save in saves:
        save.start()
    sparse_forward(heads, far, chunks, per_chunk, rand_ref, glob_ref, flip, k_sc, v_sc, q_sc, mask_sc, out_ref, lse_ref)

    step = 512
    queries = [global_queries(q_sc, mask_sc, h, gl) for h in range(heads)]

    def score(c, peaks):
        at = pl.multiple_of(c * step, step)
        new = []
        for h in range(heads):
            got = dot_nn(k_sc[pl.ds(at, step), head_lanes(h)], queries[h])
            s_sc[h, pl.ds(at, step), :] = got
            new.append(jnp.maximum(peaks[h], jnp.max(got, axis=0, keepdims=True)))
        return tuple(new)

    peaks = lax.fori_loop(0, length // step, score, (jnp.full((1, PAIR), MASKED, f32),) * heads)

    def gather(c, carry):
        at = pl.multiple_of(c * step, step)
        new = []
        for h in range(heads):
            total, ctx = carry[h]
            e = jnp.exp(s_sc[h, pl.ds(at, step), :] - peaks[h])
            ctx = ctx + dot_tn(v_sc[pl.ds(at, step), head_lanes(h)], e.astype(bf16))
            new.append((total + jnp.sum(e, axis=0, keepdims=True), ctx))
        return tuple(new)

    start = (jnp.zeros((1, PAIR), f32), jnp.zeros((PAIR, PAIR), f32))
    sums = lax.fori_loop(0, length // step, gather, (start,) * heads)
    for h in range(heads):
        total, ctx = sums[h]
        ctx = ctx[BLOCK:PAIR] * (1.0 / total)
        glob_ctx_ref[h] = ctx
        put_global_columns(out_ref, slice(h * BLOCK, (h + 1) * BLOCK), gl, ctx, per_chunk, far, chunks)
        lseg_ref[h : h + 1, :] = peaks[h] + jnp.log(total)
    for c in range(far):
        out_refs[c][...] = out_ref[c]
    for save in saves:
        save.wait()


def attention_forward(me, rand, glob, x, seg, w, b_kv, b_q):
    chunks = len(x)
    far = chunks // 2
    rows = x[0].shape[0]
    length = rows * chunks
    heads = b_q.shape[0] // HEAD_DIM
    whole = lambda: pl.BlockSpec(memory_space=pltpu.VMEM)
    got = pl.pallas_call(
        functools.partial(forward_kernel, heads, chunks),
        out_shape=(jax.ShapeDtypeStruct((heads * HEAD_DIM, rows), bf16),) * far
        + (
            jax.ShapeDtypeStruct((heads, length // PAIR // 2, PAIR), f32),
            jax.ShapeDtypeStruct((heads, PAIR), f32),
            jax.ShapeDtypeStruct((heads, HEAD_DIM, PAIR), f32),
            jax.ShapeDtypeStruct((length + BLOCK, heads * PAIR), bf16),
            jax.ShapeDtypeStruct((length + BLOCK, heads * PAIR), bf16),
            jax.ShapeDtypeStruct((heads * HEAD_DIM, length), bf16),
            jax.ShapeDtypeStruct((BLOCK, length), bf16),
        ),
        in_specs=[pl.BlockSpec(memory_space=pltpu.SMEM)] * 3 + [whole() for _ in range(chunks + 4)],
        out_specs=tuple([whole() for _ in range(far + 3)] + [pl.BlockSpec(memory_space=pl.ANY)] * 4),
        scratch_shapes=[
            pltpu.VMEM((heads, length, PAIR), f32),
            pltpu.VMEM((far, heads * HEAD_DIM, rows), bf16),
            pltpu.VMEM((chunks, rows), jnp.int32),
            pltpu.VMEM((length + BLOCK, heads * PAIR), bf16),
            pltpu.VMEM((length + BLOCK, heads * PAIR), bf16),
            pltpu.VMEM((heads * HEAD_DIM, length), bf16),
            pltpu.VMEM((BLOCK, length), bf16),
            pltpu.SemaphoreType.DMA((4,)),
        ],
        compiler_params=pltpu.CompilerParams(vmem_limit_bytes=VMEM_BYTES),
        cost_estimate=pl.CostEstimate(flops=10_000_000_000, bytes_accessed=16_000_000, transcendentals=6_000_000),
        name="attention_forward",
    )(me, rand, glob, *x, seg, w, b_kv, b_q)
    return got[:far], got[far:]


def near_kernel(heads, chunks, me_ref, rand_ref, glob_ref, k_ref, kv_ref, q_ref, mask_ref, glob_ctx_ref, *refs):
    half = chunks // 2
    out_refs = refs[:half]
    lse_ref, out_ref = refs[half:]
    length = q_ref.shape[1]
    per_chunk = length // PAIR // chunks
    flip, gl = placed(me_ref, glob_ref, length // BLOCK, chunks)
    sparse_forward(heads, 0, half, per_chunk, rand_ref, glob_ref, flip, k_ref, kv_ref, q_ref, mask_ref, out_ref, lse_ref)
    for h in range(heads):
        put_global_columns(out_ref, slice(h * BLOCK, (h + 1) * BLOCK), gl, glob_ctx_ref[h], per_chunk, 0, half)
    for c in range(half):
        out_refs[c][...] = out_ref[c]


def attention_near(me, rand, glob, k, kv, q, mask, glob_ctx, chunks):
    heads = glob_ctx.shape[0]
    half = chunks // 2
    length = q.shape[1]
    rows = length // chunks
    whole = lambda: pl.BlockSpec(memory_space=pltpu.VMEM)
    got = pl.pallas_call(
        functools.partial(near_kernel, heads, chunks),
        out_shape=(jax.ShapeDtypeStruct((heads * HEAD_DIM, rows), bf16),) * half
        + (jax.ShapeDtypeStruct((heads, length // PAIR // 2, PAIR), f32),),
        in_specs=[pl.BlockSpec(memory_space=pltpu.SMEM)] * 3 + [whole() for _ in range(5)],
        out_specs=tuple(whole() for _ in range(half + 1)),
        scratch_shapes=[pltpu.VMEM((half, heads * HEAD_DIM, rows), bf16)],
        compiler_params=pltpu.CompilerParams(vmem_limit_bytes=VMEM_BYTES),
        cost_estimate=pl.CostEstimate(flops=6_000_000_000, bytes_accessed=9_000_000, transcendentals=3_000_000),
        name="attention_near",
    )(me, rand, glob, k, kv, q, mask, glob_ctx)
    return got[:half], got[half]


def backward_kernel(heads, chunks, me_ref, rand_ref, glob_ref, *refs):
    do_refs = refs[:chunks]
    (k_ref, kv_ref, q_ref, mask_ref, seg_ref, lse_near_ref, lse_far_ref, lseg_ref, w_ref, resid_hbm, dq_hbm, dkv_hbm,
     first_ref) = refs[chunks : chunks + 13]
    part_refs = refs[chunks + 13 : 2 * chunks + 12]
    (do_sc, acc, p_sc, d_sc, seg_sc, line_sc, lse_ref, row_sc, resid_ref, dq_ref, dkv_ref, sems) = refs[2 * chunks + 12 :]
    fetch = pltpu.make_async_copy(resid_hbm, resid_ref, sems.at[0])
    fetch.start()
    rows = do_refs[0].shape[1]
    length = rows * chunks
    npairs = length // PAIR
    per_chunk = npairs // chunks
    scale = HEAD_DIM ** -0.5
    flip, gl = placed(me_ref, glob_ref, length // BLOCK, chunks)
    lse_ref[:, 0 : npairs // 2, :] = lse_near_ref[...]
    lse_ref[:, npairs // 2 :, :] = lse_far_ref[...]
    for c in range(chunks):
        do_sc[:, c * rows : (c + 1) * rows] = do_refs[c][...]
        row_sc[c : c + 1, :] = seg_ref[pl.ds(me_ref[0] ^ c, 1), :].astype(f32)

        @pl.loop(0, per_chunk // 4)
        def _(some):
            for i in range(4):
                t = 4 * some + i
                line = row_sc[c : c + 1, pl.ds(pl.multiple_of(t * PAIR, PAIR), PAIR)]
                line_sc[c * per_chunk + t] = line
                to = pl.multiple_of(c * rows + t * PAIR, PAIR)
                seg_sc[pl.ds(to, PAIR), :] = jnp.transpose(jnp.broadcast_to(line, (PAIR, PAIR)), (1, 0))

    seg_sc[length : length + BLOCK, :] = jnp.full((BLOCK, PAIR), -1.0, f32)
    first2, second2 = lane_halves(2 * PAIR, bf16)
    ffirst, fsecond = lane_halves(PAIR, f32)
    lane = lax.broadcasted_iota(jnp.int32, (1, PAIR), 1)
    line_row = lax.broadcasted_iota(jnp.int32, (PAIR, 1), 0)
    zeros = jnp.zeros((BLOCK, PAIR), bf16)
    blank = jnp.zeros((PAIR, PAIR), bf16)

    def head_rows(h):
        return slice(h * BLOCK, (h + 1) * BLOCK)

    def joint(q, mask, do):
        left = jnp.concatenate([q, mask, blank], axis=0)
        right = jnp.concatenate([blank, zeros, do], axis=0)
        return jnp.concatenate([left, right], axis=1)

    def sources(q, do):
        top = jnp.concatenate([q, zeros], axis=1)
        return jnp.concatenate([top, jnp.concatenate([zeros, do], axis=1)], axis=0)

    step = 512
    mask_glob = global_columns(mask_ref, slice(0, BLOCK), gl).astype(bf16)
    q_glob = [global_columns(q_ref, head_rows(h), gl).astype(bf16) for h in range(heads)]
    do_glob = [global_columns(do_sc, head_rows(h), gl).astype(bf16) for h in range(heads)]

    def weigh(c, deltas):
        at = pl.multiple_of(c * step, step)
        new = []
        for h in range(heads):
            left = jnp.concatenate([k_ref[pl.ds(at, step), head_lanes(h)], kv_ref[pl.ds(at, step), head_lanes(h)]], axis=1)
            both = dot_nn(left, joint(q_glob[h], mask_glob, do_glob[h]))
            p = jnp.exp(both[:, 0:PAIR] - lseg_ref[h : h + 1, :])
            dp = both[:, PAIR:]
            p_sc[h, pl.ds(at, step), :] = p
            d_sc[h, pl.ds(at, step), :] = dp
            new.append(deltas[h] + jnp.sum(p * dp, axis=0, keepdims=True))
        return tuple(new)

    deltas = lax.fori_loop(0, length // step, weigh, (jnp.zeros((1, PAIR), f32),) * heads)

    def spread(c, dqs):
        at = pl.multiple_of(c * step, step)
        new = []
        for h in range(heads):
            p = p_sc[h, pl.ds(at, step), :]
            ds = (p * (d_sc[h, pl.ds(at, step), :] - deltas[h])).astype(bf16)
            both = jnp.concatenate([ds, p.astype(bf16)], axis=1)
            acc[h, pl.ds(at, step), :] = dot_nt(both, sources(q_glob[h], do_glob[h]))
            new.append(dqs[h] + dot_tn(k_ref[pl.ds(at, step), head_lanes(h)], ds))
        return tuple(new)

    dqs = lax.fori_loop(0, length // step, spread, (jnp.zeros((PAIR, PAIR), f32),) * heads)
    for h in range(heads):
        acc[h, pl.ds(length, BLOCK), :] = jnp.zeros((BLOCK, PAIR), f32)

    def one_pair(pair):
        chunk = pair // per_chunk
        local = pl.multiple_of((pair % per_chunk) * PAIR, PAIR)
        at = pl.multiple_of(pair * PAIR, PAIR)
        hit_first = (gl[0] == 2 * pair) | (gl[1] == 2 * pair)
        hit_second = (gl[0] == 2 * pair + 1) | (gl[1] == 2 * pair + 1)
        shut = ffirst * jnp.where(hit_first, -MASKED, 0.0) + fsecond * jnp.where(hit_second, -MASKED, 0.0)
        every = slice(0, PAIR)
        for h in range(heads):
            kl = head_lanes(h)
            shared, mine, other = slots(rand_ref, glob_ref, flip, h, pair, length // BLOCK)
            q = q_ref[head_rows(h), pl.ds(at, PAIR)]
            do = do_sc[head_rows(h), pl.ds(at, PAIR)]
            lse = lse_ref[h, pl.ds(pair, 1), :] + shut
            src = sources(q, do)
            src2 = jnp.concatenate([src * first2, src * second2], axis=0)
            k_sh = stack_rows(k_ref, shared, kl)
            two_sh = dot_nn(
                jnp.concatenate([k_sh, stack_rows(kv_ref, shared, kl)], axis=1),
                joint(q, mask_ref[:, pl.ds(at, PAIR)], do),
            )
            kv_pr = jnp.concatenate([stack_rows(kv_ref, mine, kl), stack_rows(kv_ref, other, kl)], axis=1)
            two_pr = dot_nn(kv_pr, src2)
            seg_pr = jnp.where(lane < BLOCK, stack_rows(seg_sc, mine, every), stack_rows(seg_sc, other, every))
            agree = seg_pr == line_sc[pair]
            p_sh = jnp.exp(two_sh[:, 0:PAIR] - lse)
            p_pr = jnp.where(agree, jnp.exp(two_pr[:, 0:PAIR] - lse), 0.0)
            d_sh, d_pr = two_sh[:, PAIR:], two_pr[:, PAIR:]
            delta = jnp.sum(p_sh * d_sh, axis=0, keepdims=True) + jnp.sum(p_pr * d_pr, axis=0, keepdims=True)
            ds_sh = (p_sh * (d_sh - delta)).astype(bf16)
            ds_pr = (p_pr * (d_pr - delta)).astype(bf16)
            g_sh = dot_nt(jnp.concatenate([ds_sh, p_sh.astype(bf16)], axis=1), src)
            g_pr = dot_nt(jnp.concatenate([ds_pr, p_pr.astype(bf16)], axis=1), src2)
            for j, o in enumerate(shared):
                acc[h, pl.ds(o, BLOCK), :] += g_sh[j * BLOCK : (j + 1) * BLOCK]
            for j, o in enumerate(mine):
                acc[h, pl.ds(o, BLOCK), :] += g_pr[j * BLOCK : (j + 1) * BLOCK, 0:PAIR]
            for j, o in enumerate(other):
                acc[h, pl.ds(o, BLOCK), :] += g_pr[j * BLOCK : (j + 1) * BLOCK, PAIR:]
            t_pr = dot_tn(ds_pr, kv_pr)
            dq = dot_tn(ds_sh, k_sh) + jnp.where(line_row < BLOCK, t_pr[:, 0:PAIR], t_pr[:, PAIR:])
            dq = jnp.transpose(dq, (1, 0))[0:BLOCK]
            dq_ref[chunk, head_rows(h), pl.ds(local, PAIR)] = (dq * scale).astype(bf16)

    @pl.loop(0, npairs // BACK_UNROLL)
    def _(some):
        for i in range(BACK_UNROLL):
            one_pair(BACK_UNROLL * some + i)

    for h in range(heads):
        put_global_columns(dq_ref, head_rows(h), gl, dqs[h][0:BLOCK] * scale, per_chunk, 0, chunks)
        for c in range(chunks):
            dkv_ref[c, :, head_lanes(h)] = acc[h, pl.ds(c * rows, rows), :].astype(bf16)
    saves = [
        pltpu.make_async_copy(dq_ref, dq_hbm, sems.at[1]),
        pltpu.make_async_copy(dkv_ref, dkv_hbm, sems.at[2]),
    ]
    for save in saves:
        save.start()
    fetch.wait()
    tile = 256
    wq = query_weights(w_ref, heads)
    for c in range(chunks):

        @pl.loop(0, rows // tile)
        def _(t):
            at = pl.multiple_of(t * tile, tile)
            got = dot_tn(dq_ref[c, :, pl.ds(at, tile)], wq)
            got = got + dot_nt(dkv_ref[c, pl.ds(at, tile), :], w_ref[:, 0 : heads * PAIR])
            if c == 0:
                first_ref[pl.ds(at, tile), :] = resid_ref[pl.ds(at, tile), :] + got
            else:
                part_refs[c - 1][pl.ds(at, tile), :] = got.astype(bf16)
    for save in saves:
        save.wait()


def attention_backward(me, rand, glob, do, k, kv, q, mask, seg, lse_near, lse_far, lseg, w, resid):
    chunks = len(do)
    group, rows = do[0].shape
    heads = group // HEAD_DIM
    width = w.shape[0]
    length = rows * chunks
    whole = lambda: pl.BlockSpec(memory_space=pltpu.VMEM)
    return pl.pallas_call(
        functools.partial(backward_kernel, heads, chunks),
        out_shape=(
            jax.ShapeDtypeStruct((chunks, group, rows), bf16),
            jax.ShapeDtypeStruct((chunks, rows, heads * PAIR), bf16),
            jax.ShapeDtypeStruct((rows, width), f32),
        )
        + (jax.ShapeDtypeStruct((rows, width), bf16),) * (chunks - 1),
        in_specs=[pl.BlockSpec(memory_space=pltpu.SMEM)] * 3
        + [whole() for _ in range(chunks + 9)]
        + [pl.BlockSpec(memory_space=pl.ANY)],
        out_specs=tuple([pl.BlockSpec(memory_space=pl.ANY)] * 2 + [whole() for _ in range(chunks)]),
        scratch_shapes=[
            pltpu.VMEM((group, length), bf16),
            pltpu.VMEM((heads, length + BLOCK, PAIR), f32),
            pltpu.VMEM((heads, length, PAIR), f32),
            pltpu.VMEM((heads, length, PAIR), f32),
            pltpu.VMEM((length + BLOCK, PAIR), f32),
            pltpu.VMEM((length // PAIR, 1, PAIR), f32),
            pltpu.VMEM((heads, length // PAIR, PAIR), f32),
            pltpu.VMEM((chunks, rows), f32),
            pltpu.VMEM((rows, width), f32),
            pltpu.VMEM((chunks, group, rows), bf16),
            pltpu.VMEM((chunks, rows, heads * PAIR), bf16),
            pltpu.SemaphoreType.DMA((3,)),
        ],
        compiler_params=pltpu.CompilerParams(vmem_limit_bytes=VMEM_BYTES),
        cost_estimate=pl.CostEstimate(flops=30_000_000_000, bytes_accessed=24_000_000, transcendentals=8_000_000),
        name="attention_backward",
    )(me, rand, glob, *do, k, kv, q, mask, seg, lse_near, lse_far, lseg, w, resid)


def round_up(value, to):
    return -(-value // to) * to


def half_columns(ref, index, place):
    at = index // 2 * PAIR
    both = ref[:, at : at + PAIR].astype(f32)
    return both if index % 2 == place else pltpu.roll(both, BLOCK, 1)


def two_halves(first, second):
    lane = lax.broadcasted_iota(jnp.int32, (1, PAIR), 1)
    return jnp.where(lane < BLOCK, first, second)


def pack_kernel(seq_n, wq_ref, wk_ref, wv_ref, vec_ref, more_ref, pack_ref):
    own, width = wq_ref.shape
    heads = width // HEAD_DIM // seq_n
    blocks, inner = pack_ref.shape[0], pack_ref.shape[2]
    for s in range(seq_n):
        pieces = [
            two_halves(half_columns(wk_ref, s * heads + h, 0), half_columns(wv_ref, s * heads + h, 1))
            for h in range(heads)
        ]
        for h in range(0, heads, 2):
            second = half_columns(wq_ref, s * heads + h + 1, 1) if h + 1 < heads else (
                vec_ref[...].astype(f32) + more_ref[...].astype(f32)
            )
            pieces.append(two_halves(half_columns(wq_ref, s * heads + h, 0), second))
        piece = jnp.concatenate(pieces, axis=1).astype(bf16)
        for b in range(blocks):
            for i in range(inner):
                pack_ref[b, s, i] = piece


def rest_kernel(wo_ref, up_ref, down_ref, rest_ref):
    own = wo_ref.shape[0]
    u = up_ref.shape[0]
    rest_ref[0:u, :] = up_ref[...]
    rest_ref[u : 2 * u, :] = down_ref[...]
    rest_ref[2 * u : 2 * u + own, :] = wo_ref[...]


def packed_weights(w_q, w_k, w_v, w_o, w_up, w_down, vec, more, dp_n, seq_n, ffn_n):
    own, width = w_q.shape
    heads = width // HEAD_DIM // seq_n
    lanes = heads * PAIR + round_up(heads * HEAD_DIM, PAIR)
    u = w_up.shape[0]
    if own % 8 or u % 16:
        group = heads * HEAD_DIM
        cols = lambda w: w.reshape(own, seq_n, heads, HEAD_DIM).transpose(1, 0, 2, 3)
        kv = jnp.stack([cols(w_k), cols(w_v)], axis=3).reshape(seq_n, own, 2 * group)
        notes = jnp.broadcast_to((vec + more)[None, :, HEAD_DIM:], (seq_n, own, PAIR - HEAD_DIM))
        piece = jnp.concatenate([kv, cols(w_q).reshape(seq_n, own, group), notes], axis=2)
        piece = jnp.pad(piece, ((0, 0), (0, round_up(own, 8) - own), (0, 0)))
        pack = jnp.broadcast_to(piece[None, :, None], (dp_n, seq_n, ffn_n) + piece.shape[1:])
        w_o = jnp.pad(w_o, ((0, round_up(own, 8) - own), (0, 0)))
        return pack, jnp.concatenate([w_up, w_down, w_o], axis=0)
    whole = lambda: pl.BlockSpec(memory_space=pltpu.VMEM)
    rest = pl.pallas_call(
        rest_kernel,
        out_shape=jax.ShapeDtypeStruct((2 * u + own, width), bf16),
        in_specs=[whole() for _ in range(3)],
        out_specs=whole(),
        name="rest_weights",
    )(w_o, w_up, w_down)
    pack = pl.pallas_call(
        functools.partial(pack_kernel, seq_n),
        out_shape=jax.ShapeDtypeStruct((dp_n, seq_n, ffn_n, own, lanes), bf16),
        in_specs=[whole() for _ in range(5)],
        out_specs=whole(),
        name="packed_weights",
    )(w_q, w_k, w_v, vec, more)
    return pack, rest


def weights_kernel(chunks, direct, *refs):
    x_refs = refs[:chunks]
    dq_ref, dkv_ref, out_ref, acc, sum_sc = refs[chunks:]
    group = dq_ref.shape[1]
    lanes = dkv_ref.shape[2]
    full, width = acc.shape
    x = jnp.concatenate([r[...] for r in x_refs], axis=0)
    dkv = jnp.concatenate([dkv_ref[c] for c in range(chunks)], axis=0)
    dq = jnp.concatenate([dq_ref[c] for c in range(chunks)], axis=1)
    ones = jnp.ones((8, x.shape[0]), bf16)

    @pl.when(pl.program_id(0) == 0)
    def _():
        acc[...] = jnp.zeros_like(acc)
        sum_sc[...] = jnp.zeros_like(sum_sc)

    acc[0:lanes, :] += dot_tn(dkv, x)
    acc[lanes : lanes + group, :] += dot_nn(dq, x)
    sum_sc[:, 0:lanes] += dot_nn(ones, dkv)
    sum_sc[:, lanes : lanes + group] += dot_nt(ones, dq)

    @pl.when(pl.program_id(0) == pl.num_programs(0) - 1)
    def _():
        lane = lax.broadcasted_iota(jnp.int32, (full, width), 0)
        spot = lax.broadcasted_iota(jnp.int32, (full, width), 1) % group
        pick_q = lane - lanes == spot
        pick_v = (lane < lanes) & (lane % PAIR >= BLOCK) & (lane // PAIR * BLOCK + lane % BLOCK == spot)
        sums = sum_sc[...].astype(bf16)
        row = lax.broadcasted_iota(jnp.int32, (8, width), 0)
        of_q = dot_nn(sums, pick_q.astype(f32).astype(bf16))
        of_v = dot_nn(sums, pick_v.astype(f32).astype(bf16))
        acc[lanes + group : lanes + group + 8, :] = jnp.where(row == 0, of_q, of_v)
        grad = jnp.transpose(acc[...], (1, 0))
        if direct:
            blocks, own, _ = out_ref.shape
            grad = grad.reshape(blocks, own, full)
            for b in range(blocks):
                out_ref[b] = grad[b].astype(bf16)
        else:
            out_ref[...] = grad.astype(bf16)


def projection_gradients(x, dq, dkv, own, devices):
    chunks, group, rows = dq.shape
    width = x[0].shape[1]
    lanes = dkv.shape[2]
    full = lanes + round_up(group, PAIR)
    direct = own % 8 == 0
    tile = 256
    shape = (devices, own, full) if direct else (width, full)
    out = pl.pallas_call(
        functools.partial(weights_kernel, chunks, direct),
        grid=(rows // tile,),
        out_shape=jax.ShapeDtypeStruct(shape, bf16),
        in_specs=[pl.BlockSpec((tile, width), lambda i: (i, 0)) for _ in range(chunks)]
        + [
            pl.BlockSpec((chunks, group, tile), lambda i: (0, 0, i)),
            pl.BlockSpec((chunks, tile, lanes), lambda i: (0, i, 0)),
        ],
        out_specs=pl.BlockSpec(shape, lambda i: (0,) * len(shape), pipeline_mode=pl.Buffered(1)),
        scratch_shapes=[pltpu.VMEM((full, width), f32), pltpu.VMEM((8, full), f32)],
        compiler_params=pltpu.CompilerParams(vmem_limit_bytes=VMEM_BYTES),
        cost_estimate=pl.CostEstimate(flops=4_000_000_000, bytes_accessed=12_000_000, transcendentals=0),
        name="projection_gradients",
    )(*x, dq, dkv)
    if not direct:
        out = jnp.pad(out.reshape(devices, own, full), ((0, 0), (0, round_up(own, 8) - own), (0, 0)))
    return out


def unpack_kernel(own, got_ref, q_ref, k_ref, v_ref, sums_ref, tot):
    dp_n, seq_n, ffn_n, per, full = got_ref.shape
    width = q_ref.shape[1]
    heads = width // HEAD_DIM // seq_n
    for s in range(seq_n):
        total = jnp.zeros((per, full), f32)
        for d in range(dp_n):
            for f in range(ffn_n):
                total = total + got_ref[d, s, f].astype(f32)
        tot[s] = total
        sums_ref[s] = total[:, full - PAIR :]
    for w in range(width // PAIR):
        spots = [((2 * w + i) // heads, (2 * w + i) % heads) for i in range(2)]
        cols = slice(w * PAIR, (w + 1) * PAIR)
        for ref, where in (
            (k_ref, lambda h: 2 * h),
            (v_ref, lambda h: 2 * h + 1),
            (q_ref, lambda h: 2 * heads + h),
        ):
            both = [half_columns(tot.at[g], where(h), i) for i, (g, h) in enumerate(spots)]
            ref[:, cols] = two_halves(*both)[0:own]


def unpacked_gradients(got, own, width):
    dp_n, seq_n, ffn_n, per, full = got.shape
    whole = lambda: pl.BlockSpec(memory_space=pltpu.VMEM)
    return pl.pallas_call(
        functools.partial(unpack_kernel, own),
        out_shape=(jax.ShapeDtypeStruct((own, width), f32),) * 3 + (jax.ShapeDtypeStruct((seq_n, per, PAIR), f32),),
        in_specs=[whole()],
        out_specs=tuple(whole() for _ in range(4)),
        scratch_shapes=[pltpu.VMEM((seq_n, per, full), f32)],
        compiler_params=pltpu.CompilerParams(vmem_limit_bytes=VMEM_BYTES),
        cost_estimate=pl.CostEstimate(flops=40_000_000_000, bytes_accessed=3_000_000, transcendentals=0),
        name="unpacked_gradients",
    )(got)


NORM_EPS = 1e-12


def transposed(value):
    return jnp.transpose(value.astype(f32), (1, 0)).astype(bf16)


def unit_rows(value):
    center = value - jnp.mean(value, axis=-1, keepdims=True)
    scale = lax.rsqrt(jnp.mean(center * center, axis=-1, keepdims=True) + NORM_EPS)
    return center * scale, scale


def unit_rows_back(grad, unit, scale):
    return scale * (
        grad - jnp.mean(grad, axis=-1, keepdims=True) - unit * jnp.mean(grad * unit, axis=-1, keepdims=True)
    )


def rows_kernel(parts, blocks, up_rows, own, me_ref, *refs):
    ctx_refs = refs[:parts]
    (x_ref, cot_ref, rest_ref, wo_ref, vec_ref, bup_ref, out_ref, resid_ref, hid_ref, pre_ref, nlt_ref, gft_ref,
     gb_ref) = refs[parts : parts + 13]
    do_refs = refs[parts + 13 : 2 * parts + 13]
    sums_ref, gbup_ref, slope_sc, wo_sc, wide_sc = refs[2 * parts + 13 :]
    group = ctx_refs[0].shape[0]
    width = x_ref.shape[1]

    def up(f):
        return rest_ref[:, f, 0:up_rows, :].reshape(width, rest_ref.shape[3])

    def down(f):
        return rest_ref[:, f, up_rows : 2 * up_rows, :].reshape(width, rest_ref.shape[3])

    def own_rows(k):
        return pl.ds(pl.multiple_of((me_ref[0] ^ k) * group, group), group)

    @pl.when(pl.program_id(0) == 0)
    def _():
        sums_ref[...] = jnp.zeros_like(sums_ref)
        gbup_ref[...] = jnp.zeros_like(gbup_ref)
        if own:
            for o in range(rest_ref.shape[0]):
                for f in range(blocks):
                    to = (o * blocks + f) * own
                    wide_sc[to : to + own, :] = rest_ref[o, f, 2 * up_rows : 2 * up_rows + own, :].astype(f32)
            wo_sc[...] = wide_sc[...].astype(bf16)
        else:
            wo_sc[...] = wo_ref[...]

    def bias_up(f):
        return bup_ref[f : f + 1, :]

    ctx = jnp.concatenate([r[...] for r in ctx_refs], axis=0)
    w_o = jnp.concatenate([wo_sc[own_rows(k), :] for k in range(parts)], axis=0)
    resid_one = x_ref[...].astype(f32) + (dot_tn(ctx, w_o) + vec_ref[0:1, :])
    unit_one, scale_one = unit_rows(resid_one)
    normed_one = unit_one * vec_ref[2:3, :] + vec_ref[3:4, :]
    low = normed_one.astype(bf16)
    nlt_ref[...] = transposed(normed_one)
    total = normed_one + vec_ref[1:2, :]
    pre = dot_nn(low, up(0)) + bias_up(0)
    for f in range(blocks):
        later = dot_nn(low, up(f + 1)) + bias_up(f + 1) if f + 1 < blocks else None
        phi = 0.5 + 0.5 * lax.erf(pre * (0.5 ** 0.5))
        slope_sc[f] = phi + pre * (jnp.exp(-0.5 * pre * pre) * 0.3989422804014327)
        hid = (pre * phi).astype(bf16)
        hid_ref[f] = hid
        total = total + dot_nt(hid, down(f))
        pre = later
    unit_two, scale_two = unit_rows(total)
    out_ref[...] = (unit_two * vec_ref[4:5, :] + vec_ref[5:6, :]).astype(bf16)
    cot = cot_ref[...].astype(f32)
    grad_two = unit_rows_back(cot * vec_ref[4:5, :], unit_two, scale_two)
    grad_ffn = grad_two.astype(bf16)
    gft_ref[...] = transposed(grad_two)
    grad_normed = grad_two
    back = dot_nn(grad_ffn, down(0))
    for f in range(blocks):
        later = dot_nn(grad_ffn, down(f + 1)) if f + 1 < blocks else None
        grad_pre = (back * slope_sc[f]).astype(bf16)
        pre_ref[f] = grad_pre
        gbup_ref[f : f + 1, :] += jnp.sum(grad_pre.astype(f32), axis=0, keepdims=True)
        grad_normed = grad_normed + dot_nt(grad_pre, up(f))
        back = later
    resid = unit_rows_back(grad_normed * vec_ref[2:3, :], unit_one, scale_one)
    resid_ref[...] = resid
    branch = resid.astype(bf16)
    gb_ref[...] = branch
    do = dot_nt(w_o, branch).astype(bf16)
    for k in range(parts):
        do_refs[k][...] = do[k * group : (k + 1) * group]
    for row, value in enumerate(
        (branch.astype(f32), grad_ffn.astype(f32), grad_normed * unit_one, grad_normed, cot * unit_two, cot)
    ):
        sums_ref[row : row + 1, :] += jnp.sum(value, axis=0, keepdims=True)


def rows_chain(me, ctx_parts, x, cot, rest, up_rows, own, w_o, vecs, bias_up):
    parts = len(ctx_parts)
    group, rows = ctx_parts[0].shape
    width = x.shape[1]
    outer, blocks, per, hidden = rest.shape
    tile = 256
    once = lambda shape: pl.BlockSpec(shape, lambda i: (0,) * len(shape), pipeline_mode=pl.Buffered(1))
    tall = pl.BlockSpec((tile, width), lambda i: (i, 0))
    wide = pl.BlockSpec((width, tile), lambda i: (0, i))
    cube = pl.BlockSpec((blocks, tile, hidden), lambda i: (0, i, 0))
    return pl.pallas_call(
        functools.partial(rows_kernel, parts, blocks, up_rows, own),
        grid=(rows // tile,),
        out_shape=(
            jax.ShapeDtypeStruct((rows, width), bf16),
            jax.ShapeDtypeStruct((rows, width), f32),
            jax.ShapeDtypeStruct((blocks, rows, hidden), bf16),
            jax.ShapeDtypeStruct((blocks, rows, hidden), bf16),
            jax.ShapeDtypeStruct((width, rows), bf16),
            jax.ShapeDtypeStruct((width, rows), bf16),
            jax.ShapeDtypeStruct((rows, width), bf16),
        )
        + (jax.ShapeDtypeStruct((group, rows), bf16),) * parts
        + (jax.ShapeDtypeStruct((8, width), f32), jax.ShapeDtypeStruct((8, hidden), f32)),
        in_specs=[pl.BlockSpec(memory_space=pltpu.SMEM)]
        + [pl.BlockSpec((group, tile), lambda i: (0, i))] * parts
        + [tall, tall, once(rest.shape), once(w_o.shape), once(vecs.shape), once(bias_up.shape)],
        out_specs=(
            tall, tall, cube, cube, wide, wide, tall,
        )
        + (pl.BlockSpec((group, tile), lambda i: (0, i)),) * parts
        + (pl.BlockSpec((8, width), lambda i: (0, 0)), pl.BlockSpec((8, hidden), lambda i: (0, 0))),
        scratch_shapes=[
            pltpu.VMEM((blocks, tile, hidden), f32),
            pltpu.VMEM((width, width), bf16),
            pltpu.VMEM((width, width), f32),
        ],
        compiler_params=pltpu.CompilerParams(vmem_limit_bytes=VMEM_BYTES),
        cost_estimate=pl.CostEstimate(flops=22_000_000_000, bytes_accessed=40_000_000, transcendentals=6_000_000),
        name="rows_chain",
    )(me, *ctx_parts, x, cot, rest, w_o, vecs, bias_up)


def outer_kernel(parts, up_rows, own, apart, me_ref, *refs):
    ctx_refs = refs[:parts]
    nlt_ref, gft_ref, gb_ref, pre_ref, hid_ref, sums_ref, gbup_ref, out_ref = refs[parts : parts + 8]
    wo_sc = refs[-1]
    slabs, hidden = out_ref.shape[0], out_ref.shape[3]
    group = ctx_refs[0].shape[0]
    f = pl.program_id(0)
    up = dot_nn(nlt_ref[...], pre_ref[0]).astype(bf16).reshape(slabs, up_rows, hidden)
    if apart:
        refs[parts + 8][:, 0, :, :] = up[:, 0:apart]
    out_ref[:, 0, 0 : up_rows - apart, :] = up[:, apart:]
    at = up_rows - apart
    down = dot_nn(gft_ref[...], hid_ref[0]).astype(bf16)
    out_ref[:, 0, at : at + up_rows, :] = down.reshape(slabs, up_rows, hidden)
    at += up_rows
    if not own:
        return

    @pl.when(f == 0)
    def _():
        for k in range(parts):
            wo_sc[k] = dot_nn(ctx_refs[k][...], gb_ref[...])

    share = slabs // parts
    stride = group // share
    for k in range(parts):
        for j in range(share):
            rows = pl.ds(pl.multiple_of(j * stride + f * own, 8), own)
            out_ref[(me_ref[0] ^ k) * share + j, 0, at : at + own, :] = wo_sc[k, rows, :].astype(bf16)
    small = jnp.concatenate([gbup_ref[pl.ds(f, 1), :], sums_ref[0:7, :]], axis=0).astype(bf16)
    for o in range(slabs):
        out_ref[o, 0, at + own :, :] = small


def outer_products(me, ctx_parts, nlt, gft, gb, pre, hid, sums, gbup, slabs, up_rows, own, apart):
    blocks, rows, hidden = pre.shape
    parts = len(ctx_parts)
    group = ctx_parts[0].shape[0]
    per = 2 * up_rows - apart + (own + 8 if own else 0)
    sizes = (per, apart) if apart else (per,)
    once = lambda shape: pl.BlockSpec(shape, lambda i: (0,) * len(shape), pipeline_mode=pl.Buffered(1))
    return pl.pallas_call(
        functools.partial(outer_kernel, parts, up_rows, own, apart),
        grid=(blocks,),
        out_shape=tuple(jax.ShapeDtypeStruct((slabs, blocks, r, hidden), bf16) for r in sizes),
        in_specs=[pl.BlockSpec(memory_space=pltpu.SMEM)]
        + [once(c.shape) for c in ctx_parts]
        + [
            once(nlt.shape),
            once(gft.shape),
            once(gb.shape),
            pl.BlockSpec((1, rows, hidden), lambda i: (i, 0, 0)),
            pl.BlockSpec((1, rows, hidden), lambda i: (i, 0, 0)),
            once(sums.shape),
            once(gbup.shape),
        ],
        out_specs=tuple(pl.BlockSpec((slabs, 1, r, hidden), lambda i: (0, i, 0, 0)) for r in sizes),
        scratch_shapes=[pltpu.VMEM((parts, group, gb.shape[1]), f32)],
        compiler_params=pltpu.CompilerParams(vmem_limit_bytes=VMEM_BYTES),
        cost_estimate=pl.CostEstimate(flops=11_000_000_000, bytes_accessed=28_000_000, transcendentals=0),
        name="outer_products",
    )(me, *ctx_parts, nlt, gft, gb, pre, hid, sums, gbup)


def finish_kernel(up_rows, own, total_ref, up_ref, down_ref, wo_ref, small_ref):
    rest = total_ref[...].astype(f32)
    up_ref[...] = rest[0:up_rows]
    down_ref[...] = rest[up_rows : 2 * up_rows]
    at = 2 * up_rows
    wo_ref[...] = rest[at : at + own]
    small_ref[...] = rest[at + own : at + own + 8]


def finished(total, up_rows, own):
    hidden = total.shape[1]
    whole = lambda: pl.BlockSpec(memory_space=pltpu.VMEM)
    return pl.pallas_call(
        functools.partial(finish_kernel, up_rows, own),
        out_shape=tuple(jax.ShapeDtypeStruct((r, hidden), f32) for r in (up_rows, up_rows, own, 8)),
        in_specs=[whole()],
        out_specs=tuple(whole() for _ in range(4)),
        cost_estimate=pl.CostEstimate(flops=2_000_000_000, bytes_accessed=2_000_000, transcendentals=0),
        name="finished",
    )(total)


def total_kernel(pieces, base_ref, *refs):
    total = base_ref[...]
    for ref in refs[:pieces]:
        total = total + ref[...].astype(f32)
    refs[-1][...] = total


def token_total(base, whole_pieces, part, first, done=None):
    rows, width = base.shape
    tile = 128
    skip = first // tile
    here = pl.BlockSpec((tile, width), lambda i: (i + skip, 0))
    count = len(whole_pieces) + 1
    args = [base, *whole_pieces, part] + ([] if done is None else [done])
    return pl.pallas_call(
        functools.partial(total_kernel, count),
        grid=(part.shape[0] // tile,),
        out_shape=jax.ShapeDtypeStruct(base.shape, f32),
        in_specs=[here] * count
        + [pl.BlockSpec((tile, width), lambda i: (i, 0))]
        + ([] if done is None else [pl.BlockSpec(memory_space=pl.ANY)]),
        out_specs=here,
        input_output_aliases={} if done is None else {count + 1: 0},
        compiler_params=pltpu.CompilerParams(vmem_limit_bytes=VMEM_BYTES),
        cost_estimate=pl.CostEstimate(flops=TOTAL_FLOPS, bytes_accessed=5_000_000, transcendentals=0),
        name="token_total",
    )(*args)


TOTAL_FLOPS = 1_000_000_000
ALL = ("dp", "seq", "ffn")


def flip_send(array, axis, bits):
    count = lax.axis_size(axis)
    return lax.ppermute(array, axis, [(i, i ^ bits) for i in range(count)])


def shards(
    tokens, w_query, w_key, w_value, w_output, b_query, b_value, b_output, w_up, b_up, w_down, b_down,
    gain_attn, shift_attn, gain_ffn, shift_ffn, segment_ids, random_blocks, global_blocks, cotangent,
):
    seq_n, dp_n, ffn_n = lax.axis_size("seq"), lax.axis_size("dp"), lax.axis_size("ffn")
    outer, devices = dp_n * seq_n, dp_n * seq_n * ffn_n
    me = lax.axis_index("seq")
    here = (lax.axis_index("dp") * seq_n + me) * ffn_n + lax.axis_index("ffn")
    own, width = w_query.shape
    own_pad = round_up(own, 8)
    group = width // seq_n
    heads = group // HEAD_DIM
    features = tokens[0]
    rows = features.shape[0]
    order = jnp.stack([me ^ k for k in range(seq_n)])
    me_ref = me.astype(jnp.int32)[None]

    near = [features] + [None] * (seq_n - 1)
    for k in sorted(range(1, seq_n), key=lambda k: (k & (k - 1), -k)):
        bit = k & -k
        near[k] = flip_send(features if bit == k else near[k ^ bit], "seq", bit)

    vec = jnp.stack([b_output, b_down, gain_attn, shift_attn, gain_ffn, shift_ffn, b_query, b_value], axis=1)
    up_rows = w_up.shape[0]
    share_up = lax.dynamic_slice(b_up, (here // ffn_n * up_rows,), (up_rows,)).reshape(ffn_n, own).T
    more = jnp.pad(share_up, ((0, 0), (HEAD_DIM + 8, PAIR - HEAD_DIM - 8 - ffn_n)))
    vec = jnp.pad(vec, ((0, 0), (HEAD_DIM, PAIR - HEAD_DIM - 8)))
    seg = segment_ids[0].reshape(seq_n, rows)
    rand = random_blocks.reshape(-1)
    pack, rest = packed_weights(
        w_query, w_key, w_value, w_output, w_up, w_down, vec, more, dp_n, seq_n, ffn_n
    )
    lanes = pack.shape[4]
    pack, seg, rand = lax.optimization_barrier((pack, seg, rand))
    pack = lax.all_to_all(
        pack.reshape(devices, own_pad, lanes), ALL, split_axis=0, concat_axis=0, tiled=True
    )
    rest = lax.all_gather(rest, ALL, axis=0, tiled=False)
    w_own = pack[:, :own].reshape(width, lanes)
    share = devices // seq_n
    vecs = w_own[:, lanes - HEAD_DIM : lanes - HEAD_DIM + 8].astype(f32).T
    biases = lax.dynamic_slice(vecs, (6, me * group), (2, group))
    bias_up = w_own[:, lanes - HEAD_DIM + 8 : lanes - HEAD_DIM + 8 + ffn_n].reshape(outer, ffn_n, own, ffn_n)
    bias_up = bias_up.transpose(1, 0, 3, 2).reshape(ffn_n, width).astype(f32)
    by_head = biases[1].reshape(heads, 1, HEAD_DIM)
    b_kv = jnp.concatenate([jnp.zeros_like(by_head), by_head], axis=1).reshape(1, heads * PAIR)

    far = seq_n // 2
    ctx_far, (lse_far, lseg, glob_ctx, k_all, v_all, q_all, mask_all) = attention_forward(
        me_ref, rand, global_blocks, near, seg, w_own, b_kv, biases[0][:, None]
    )
    ctx_parts = [None] * far + [flip_send(ctx_far[k - far], "seq", k) for k in range(far, seq_n)]
    ctx_near, lse_near = attention_near(
        me_ref, rand, global_blocks, k_all, v_all, q_all, mask_all, glob_ctx, seq_n
    )
    ctx_parts[far:], ctx_parts[0] = lax.optimization_barrier((ctx_parts[far:], ctx_near[0]))
    for k in range(1, far):
        ctx_parts[k] = flip_send(ctx_near[k], "seq", k)

    at = 2 * up_rows
    rest = rest.reshape(outer, ffn_n, rest.shape[1], width)
    w_o = rest[:, :, at : at + own].reshape(width, width)
    direct = up_rows % 16 == 0 and own % 8 == 0 and outer % seq_n == 0 and (outer // seq_n) * ffn_n * own == group
    if not direct:
        rest = rest[:, :, :at].reshape(outer, ffn_n, 2, up_rows, width).transpose(1, 2, 0, 3, 4)
        rest = rest.reshape(1, ffn_n, 2 * outer * up_rows, width)
    slabs, slab_rows = (outer, up_rows) if direct else (1, outer * up_rows)

    got = rows_chain(
        me_ref, ctx_parts, features, cotangent[0], rest, slab_rows, own if direct else 0,
        vecs if direct else w_o, vecs, bias_up,
    )
    out, grad_resid_one, hidden, grad_pre, normed_t, grad_ffn_t, grad_branch = got[:7]
    grad_ctx, (sums, grad_bias_up) = got[7 : 7 + seq_n], got[7 + seq_n :]
    do = [grad_ctx[0]] + [flip_send(grad_ctx[k], "seq", k) for k in range(1, seq_n)]

    payload = outer_products(
        me_ref, ctx_parts, normed_t, grad_ffn_t, grad_branch, grad_pre, hidden, sums, grad_bias_up, slabs, slab_rows,
        own if direct else 0, APART if direct else 0,
    )
    payload, apart = payload if direct and APART else (payload[0], None)
    if not direct:
        grad_out = dot_nn(jnp.concatenate(ctx_parts, axis=0), grad_branch).astype(bf16)
        grad_out = grad_out.reshape(seq_n, group, width)[order].reshape(outer, ffn_n, own, width)
        top = jnp.broadcast_to(grad_bias_up[None, :ffn_n, None], (outer, ffn_n, 1, width))
        small = jnp.concatenate([top, jnp.broadcast_to(sums[None, None, :7], (outer, ffn_n, 7, width))], axis=2)
        small = small.astype(bf16)
        payload = payload.reshape(ffn_n, 2, outer, up_rows, width).transpose(2, 0, 1, 3, 4)
        payload = jnp.concatenate([payload.reshape(outer, ffn_n, at, width), grad_out, small], axis=2)
        payload = jnp.pad(payload, ((0, 0), (0, 0), (0, -payload.shape[2] % 32), (0, 0)))
    payload, apart, do = lax.optimization_barrier((payload, apart, do))
    total = lax.psum_scatter(payload.reshape(-1, width), ("dp", "seq"), scatter_dimension=0, tiled=True)
    if apart is not None:
        apart = lax.all_to_all(
            apart.reshape(devices, APART, width), ALL, split_axis=0, concat_axis=0, tiled=True
        )

    got = attention_backward(
        me_ref, rand, global_blocks, do, k_all, v_all, q_all, mask_all, seg, lse_near, lse_far, lseg, w_own,
        grad_resid_one,
    )
    dq, dkv, grad_features = got[:3]
    part = [None] + list(got[3:])
    bit = 1
    while bit < seq_n:
        for k in range(seq_n):
            if k & -k == bit and k != bit:
                came = flip_send(part[k], "seq", bit).astype(f32)
                part[k ^ bit] = (part[k ^ bit].astype(f32) + came).astype(bf16)
        bit *= 2
    grad_w = projection_gradients(near, dq, dkv, own, devices)
    grad_w, part = lax.optimization_barrier((grad_w, part[1:]))
    grad_w, apart = lax.optimization_barrier((grad_w, apart))
    part = [None] + part
    bit = seq_n // 2
    staged = total
    total = lax.psum_scatter(total, "ffn", scatter_dimension=0, tiled=True)
    half = rows * 3 // 4
    first, second = part[bit][:half], part[bit][half:]
    first, second = flip_send(first, "seq", bit), flip_send(second, "seq", bit)
    bit //= 2
    others = []
    while bit:
        others.append(flip_send(part[bit], "seq", bit))
        bit //= 2
    first = lax.optimization_barrier((first, staged))[0]
    base = grad_features
    grad_features = token_total(base, others, first, 0)
    grad_features = token_total(base, others, second, half, grad_features)
    grad_w = lax.all_to_all(grad_w, ALL, split_axis=0, concat_axis=0, tiled=True)
    if direct:
        out_up, out_down, out_output, notes = finished(total, up_rows, own)
    else:
        total = total.astype(f32)
        out_up, out_down, out_output = total[:up_rows], total[up_rows:at], total[at : at + own]
        notes = total[at + own : at + own + 8]
    out_bias_up = notes[0]
    out_vecs = lax.dynamic_slice(notes, (1, here * own), (6, own))
    out_query, out_key, out_value, col_sums = unpacked_gradients(
        grad_w.reshape(dp_n, seq_n, ffn_n, own_pad, lanes), own, width
    )
    col = lax.dynamic_index_in_dim(col_sums, here // share, keepdims=False)[:own, HEAD_DIM : HEAD_DIM + 2]
    out_b = [col[:, 0], col[:, 1]]
    return (
        out[None],
        grad_features[None],
        out_query,
        out_key,
        out_value,
        out_output,
        out_b[0],
        out_b[1],
        out_vecs[0],
        out_up,
        out_bias_up,
        out_down,
        out_vecs[1],
        out_vecs[2],
        out_vecs[3],
        out_vecs[4],
        out_vecs[5],
    )


def solution(mesh):
    return jax.shard_map(
        shards,
        mesh=mesh,
        in_specs=(
            P(("dp", "ffn"), "seq", None),
            P(("dp", "seq", "ffn"), None),
            P(("dp", "seq", "ffn"), None),
            P(("dp", "seq", "ffn"), None),
            P(("dp", "seq", "ffn"), None),
            P(("dp", "seq", "ffn")),
            P(("dp", "seq", "ffn")),
            P(("dp", "seq", "ffn")),
            P(("dp", "seq"), "ffn"),
            P("ffn"),
            P(("dp", "seq"), "ffn"),
            P(("dp", "seq", "ffn")),
            P(("dp", "seq", "ffn")),
            P(("dp", "seq", "ffn")),
            P(("dp", "seq", "ffn")),
            P(("dp", "seq", "ffn")),
            P(("dp", "ffn"), None),
            P(("dp", "ffn"), "seq", None, None),
            P(("dp", "ffn"), None),
            P(("dp", "ffn"), "seq", None),
        ),
        out_specs=(
            P(("dp", "ffn"), "seq", None),
            P(("dp", "ffn"), "seq", None),
            P(("dp", "seq", "ffn"), None),
            P(("dp", "seq", "ffn"), None),
            P(("dp", "seq", "ffn"), None),
            P(("dp", "seq", "ffn"), None),
            P(("dp", "seq", "ffn")),
            P(("dp", "seq", "ffn")),
            P(("dp", "seq", "ffn")),
            P(("dp", "seq"), "ffn"),
            P("ffn"),
            P(("dp", "seq"), "ffn"),
            P(("dp", "seq", "ffn")),
            P(("dp", "seq", "ffn")),
            P(("dp", "seq", "ffn")),
            P(("dp", "seq", "ffn")),
            P(("dp", "seq", "ffn")),
        ),
        check_vma=False,
    )
```
